32 devices in a mesh: dp: 8 (over z, y), rep: 4 (over x, core).
Axes of the slice: x: 2, y: 2, z: 4, core: 2. Of those that a mesh axis runs over, the one named last changes fastest.
Arguments:
- image_tokens: bfloat16 [256, 50, 768], P(('dp', 'rep')), may hold values from -6 to 6
- image_weights: bfloat16 [768, 9216], P('dp'), may hold values from -1 to 1
- image_vectors: float32 [9216], replicated, may hold values from -0.8 to 1.4
- text_tokens: bfloat16 [64, 64, 768], P(('dp', 'rep')), may hold values from -6 to 6
- segments: int32 [64, 64], P(('dp', 'rep')), may hold values from 0 to 3, never falling along the last dimension, each value on 1 to 28 neighbouring positions
- text_weights: float32 [768, 9216], P('dp'), may hold values from -1 to 1
- text_vectors: float32 [9216], replicated, may hold values from -0.8 to 1.4
- momentum: float32 [768, 9216], P('dp'), may hold values from -0.5 to 0.5
- vector_momentum: float32 [9216], replicated, may hold values from -2.5 to 2.5
- error_feedback: float32 [4, 768, 9216], P('rep', 'dp'), may hold values from -2.5 to 2.5
- start_factors: float32 [8, 9216], replicated, may hold values from -6 to 6
Outputs:
- contrast_loss: float32 [], replicated
- text_output: float32 [64, 64, 768], P(('dp', 'rep'))
- text_input_grad: float32 [64, 64, 768], P(('dp', 'rep'))
- new_weights: float32 [768, 9216], P('dp')
- new_momentum: float32 [768, 9216], P('dp')
- new_feedback: float32 [4, 768, 9216], P('rep', 'dp')
- new_vectors: float32 [9216], replicated
- new_vector_momentum: float32 [9216], replicated
- left_factors: float32 [32, 768], replicated
- right_factors: float32 [8, 9216], replicated
The draws below stay inside these ranges and needn't reach their ends.
Inputs may be any that keep to these rules, and one draw needn't show every extreme that they name: `segments`: each row holds 4 captions numbered in order, each of 1 to 28 tokens, some caption of exactly 28.
All inputs are finite; a program needn't handle non-finite values.
Results may differ from the reference program's by a relative error of at most 0.015.
The reference program's roundings to bfloat16 on the way count: a program that leaves them out, or rounds other values in their place, can miss the bound.
Values may be sent and summed in bfloat16 or wider, within the bound.
A program may use at most 192 MiB of HBM per device.

```python
import math
import jax
import jax.numpy as jnp
import numpy as np
from jax import lax

D = 768
FF = 3072
HEADS = 12
HEAD_DIM = 64
PATCHES = 50
SEQ = 64
PER_ROW = 4
MOST = 28
RANK = 8
PAIRS_DEV = 8
PAIRS = 256
CAP_ROWS = 64
PACKED = 9216
VECTORS = 9216
N_DP = 8
N_REP = 4


def base_noise(key, shape):
    return jnp.clip(jax.random.normal(key, shape, jnp.float32), -3.5, 3.5)


def packed_matrices(key):
    split_keys = jax.random.split(key, 4)
    mixing = base_noise(split_keys[0], (D, 3 * D)) * (1.0 / D) ** 0.5
    output = base_noise(split_keys[1], (D, D)) * 2.0 * (1.0 / D) ** 0.5
    expand = base_noise(split_keys[2], (D, FF)) * (1.0 / D) ** 0.5
    shrink = base_noise(split_keys[3], (D, FF)) * 1.5 * (1.0 / FF) ** 0.5
    return jnp.concatenate([mixing, output, expand, shrink], axis=1)


def packed_vectors(key):
    split_keys = jax.random.split(key, 2)
    gains = jax.random.uniform(split_keys[0], (2, D), jnp.float32, 0.6, 1.4)
    shifts = jnp.clip(jax.random.normal(split_keys[1], (6 * D + FF,), jnp.float32), -4.0, 4.0) * 0.2
    return jnp.concatenate([gains[0], shifts[:D], shifts[D:2 * D], shifts[2 * D:3 * D], shifts[3 * D:4 * D], gains[1], shifts[4 * D:5 * D], shifts[5 * D:6 * D], shifts[6 * D:]])


def draw_image_weights(key, part):
    return packed_matrices(jax.random.fold_in(key, 11)).astype(jnp.bfloat16)


def draw_text_weights(key, part):
    return packed_matrices(jax.random.fold_in(key, 12))


def draw_image_vectors(key, part):
    return packed_vectors(jax.random.fold_in(key, 13))


def draw_text_vectors(key, part):
    return packed_vectors(jax.random.fold_in(key, 14))


def level_of(own_key, extent, shards, low, high):
    factor_of, own = 1.0, jax.random.fold_in(own_key, 6)
    for dim, shards_of in shards:
        heights = jnp.exp(jax.random.uniform(jax.random.fold_in(own, dim), (shards_of,), jnp.float32, low / len(shards), high / len(shards)))
        factor_of = factor_of * jnp.repeat(heights, extent[dim] // shards_of).reshape([-1 if axis == dim else 1 for axis in range(len(extent))])
    return factor_of


def profile(amount, total, most, slope):
    portions = [(1 << 20) // math.isqrt(rank ** slope) + 1 for rank in range(2, amount + 1)]
    rest, holding = total - most - (amount - 1), [1] * (amount - 1)
    while rest > 0:
        candidates = [i for i in range(amount - 1) if holding[i] < most]
        pool, left = sum([portions[i] for i in candidates]), rest
        for i in candidates:
            addition = min(most - holding[i], max(1, left * portions[i] // pool), rest)
            holding[i] = holding[i] + addition
            rest = rest - addition
    return np.array([most] + holding)


def ragged(rng, number_of, total, most, slope):
    if number_of == 2:
        one = jax.random.randint(rng, (), max(1, total - most), min(most, total - 1) + 1)
        return jnp.stack([one, total - one])
    lengths = jnp.asarray(profile(number_of, total, most, slope), jnp.int32)
    twos = (number_of - 1) // 2
    source_of, sink = lengths[1:1 + 2 * twos:2], lengths[2:2 + 2 * twos:2]
    margin = jnp.minimum(source_of - 1, most - sink)
    moved = jax.random.randint(jax.random.fold_in(rng, 1), (twos,), 0, 1 << 20) % (margin + 1)
    lengths = lengths.at[1:1 + 2 * twos:2].set(source_of - moved).at[2:2 + 2 * twos:2].set(sink + moved)
    return lengths[jax.random.permutation(jax.random.fold_in(rng, 2), number_of)]


def normal_values(stream_key, extent, scale, limit, shards=(), kind=jnp.bfloat16):
    loudness = level_of(stream_key, extent, shards, -0.22, 0.18) if shards else 1.0
    drawn = jax.random.normal(stream_key, extent, jnp.float32) * scale * loudness
    return jnp.minimum(jnp.maximum(drawn, -limit), limit).astype(kind)


def setup_inputs(seed: int = 0) -> dict:
    keys = jax.random.split(jax.random.key(seed), 12)
    image_tokens = normal_values(keys[0], (PAIRS, PATCHES, D), 1.0, 6.0, ((0, 32),))
    image_weights = draw_image_weights(jax.random.fold_in(keys[11], 71), 0)
    image_vectors = draw_image_vectors(jax.random.fold_in(keys[11], 71), 0)
    text_tokens = normal_values(keys[3], (CAP_ROWS, SEQ, D), 1.0, 6.0, ((0, 32),))
    segments = jax.vmap(lambda own: jnp.searchsorted(jnp.cumsum(ragged(own, PER_ROW, SEQ, MOST, 1)), jnp.arange(SEQ), side="right"))(jax.random.split(keys[4], CAP_ROWS)).reshape((CAP_ROWS, SEQ)).astype(jnp.int32)
    text_weights = draw_text_weights(jax.random.fold_in(keys[11], 71), 0)
    text_vectors = draw_text_vectors(jax.random.fold_in(keys[11], 71), 0)
    momentum = normal_values(keys[7], (D, PACKED), (0.002 * PAIRS ** 0.5), 0.5, ((0, 8),), jnp.float32)
    vector_momentum = normal_values(keys[8], (VECTORS,), (0.01 * PAIRS ** 0.5), 2.5, (), jnp.float32)
    error_feedback = normal_values(keys[9], (N_REP, D, PACKED), (0.01 * PAIRS ** 0.5), 2.5, ((0, 4), (1, 8)), jnp.float32)
    start_factors = normal_values(keys[10], (RANK, PACKED), 1.0, 6.0, (), jnp.float32)
    return {"image_tokens": image_tokens, "image_weights": image_weights, "image_vectors": image_vectors, "text_tokens": text_tokens, "segments": segments, "text_weights": text_weights, "text_vectors": text_vectors, "momentum": momentum, "vector_momentum": vector_momentum, "error_feedback": error_feedback, "start_factors": start_factors}


PRECISE = lax.Precision.HIGHEST
LAYER_EPS = 1e-06
SCORE_SCALE = 0.125
LOGIT_SCALE = 50.0
MOMENTUM_DECAY = 0.9
STEP_RATE = 0.08
NORM_FLOOR = 1e-08
MASKED = -1e+30

@jax.custom_vjp
def low(v):
    return lax.optimization_barrier(v.astype(jnp.bfloat16)).astype(jnp.float32)

@jax.custom_vjp
def low_back(v):
    return v

def low_keep(v):
    return (low(v), None)

def low_pass(kept, grad):
    return (grad,)

def back_keep(v):
    return (v, None)

def back_low(kept, grad):
    return (low(grad),)
low.defvjp(low_keep, low_pass)
low_back.defvjp(back_keep, back_low)

def layer_norm(values, layer_gain, layer_shift):
    center = values - lax.optimization_barrier(jnp.mean(values, axis=-1, keepdims=True))
    spread = lax.optimization_barrier(jnp.mean(center * center, axis=-1, keepdims=True))
    return center * lax.rsqrt(spread + LAYER_EPS) * layer_gain + layer_shift

def unit_rows(values):
    return values * lax.rsqrt(lax.optimization_barrier(jnp.sum(values * values, axis=-1, keepdims=True)) + LAYER_EPS)

def vector_parts(vectors):
    pieces = [vectors[position * D:(position + 1) * D] for position in range(8)]
    return pieces + [vectors[8 * D:]]

def matrix_bounds():
    return ((0, 3 * D), (3 * D, 4 * D), (4 * D, 4 * D + FF), (4 * D + FF, 4 * D + 2 * FF))

def residual_block(inputs, allowed, weights, vectors):
    gain_one, shift_one, bias_query, bias_value, bias_out, gain_two, shift_two, bias_shrink, bias_expand = vector_parts(vectors)
    row_count, seq_tokens = (inputs.shape[0], inputs.shape[1])
    normed = low(layer_norm(inputs, gain_one, shift_one))
    mixing = jnp.einsum('rsd,dc->rsc', normed, weights[:, :3 * D], precision=PRECISE)
    mixing = low_back(mixing + jnp.concatenate([bias_query, jnp.zeros_like(bias_query), bias_value]))
    head_parts = mixing.reshape(row_count, seq_tokens, 3, HEADS, HEAD_DIM)
    query_heads = low(head_parts[:, :, 0])
    key_heads = low(head_parts[:, :, 1])
    value_heads = low(head_parts[:, :, 2])
    scores = low_back(jnp.einsum('rshd,rthd->rhst', query_heads, key_heads, precision=PRECISE) * SCORE_SCALE)
    scores = jnp.where(allowed[:, None], scores, MASKED)
    attention = low(jax.nn.softmax(scores, axis=-1))
    mixed_heads = jnp.einsum('rhst,rthd->rshd', attention, value_heads, precision=PRECISE).reshape(row_count, seq_tokens, D)
    mixed_heads = low_back(low(mixed_heads))
    attended = low_back(jnp.einsum('rsd,de->rse', mixed_heads, weights[:, 3 * D:4 * D], precision=PRECISE) + bias_out)
    middle = inputs + attended
    normed_two = low(layer_norm(middle, gain_two, shift_two))
    hidden = low_back(jnp.einsum('rsd,df->rsf', normed_two, weights[:, 4 * D:4 * D + FF], precision=PRECISE) + bias_expand)
    active = low(jax.nn.gelu(hidden, approximate=False))
    shrunk = low_back(jnp.einsum('rsf,df->rsd', active, weights[:, 4 * D + FF:], precision=PRECISE) + bias_shrink)
    return middle + shrunk

def caption_pool(outputs, segments):
    caption_marks = (segments[:, None, :] == jnp.arange(PER_ROW, dtype=jnp.int32)[None, :, None]).astype(jnp.float32)
    sums = jnp.einsum('rks,rsd->rkd', caption_marks, outputs, precision=PRECISE)
    counts = lax.optimization_barrier(jnp.sum(caption_marks, axis=-1, keepdims=True))
    return (sums / counts).reshape(-1, D)

def side_loss(query_side, other_side, block_rows):
    pair_total = query_side.shape[0]
    starts = jnp.arange(pair_total // block_rows, dtype=jnp.int32) * block_rows

    def one_block(first_row):
        rows_here = lax.dynamic_slice_in_dim(query_side, first_row, block_rows, 0)
        logits = low_back(LOGIT_SCALE * jnp.einsum('pd,bd->pb', rows_here, other_side, precision=PRECISE))
        diagonal_pick = (jnp.arange(pair_total, dtype=jnp.int32)[None, :] == (first_row + jnp.arange(block_rows, dtype=jnp.int32))[:, None]).astype(jnp.float32)
        return jnp.sum(jax.nn.logsumexp(logits, axis=1) - lax.optimization_barrier(jnp.sum(diagonal_pick * logits, axis=1)))
    return jnp.sum(lax.map(jax.checkpoint(one_block), starts))

def orthonormal(stacked):
    finished = []
    for column_id in range(stacked.shape[1]):
        vector = stacked[:, column_id]
        for earlier in finished:
            vector = vector - lax.optimization_barrier(jnp.sum(earlier * vector, axis=-1, keepdims=True)) * earlier
        vector = vector / (jnp.sqrt(lax.optimization_barrier(jnp.sum(vector * vector, axis=-1, keepdims=True))) + NORM_FLOOR)
        finished.append(vector)
    return jnp.stack(finished, axis=1)

def reference(image_tokens, image_weights, image_vectors, text_tokens, segments, text_weights, text_vectors, momentum, vector_momentum, error_feedback, start_factors):
    pair_total = PAIRS
    per_device = PAIRS_DEV
    image_blocks = image_tokens.astype(jnp.float32).reshape(pair_total // per_device, per_device, PATCHES, D)
    frozen = image_weights.astype(jnp.float32)
    full_mask = jnp.zeros((per_device, PATCHES, PATCHES), jnp.int32) == 0

    def image_block(inputs):
        return unit_rows(lax.optimization_barrier(jnp.mean(residual_block(inputs, full_mask, frozen, image_vectors), axis=1)))
    image_emb = low(lax.map(image_block, image_blocks).reshape(pair_total, D))
    rows_device = per_device // PER_ROW
    text_blocks = text_tokens.astype(jnp.float32).reshape(N_DP, N_REP, rows_device, SEQ, D)
    allowed = (segments[:, :, None] == segments[:, None, :]).reshape(N_DP, N_REP, rows_device, SEQ, SEQ)
    worker_weights = jnp.broadcast_to(text_weights, (N_REP, D, PACKED))
    worker_vectors = jnp.broadcast_to(text_vectors, (N_REP, VECTORS))
    block_rows = math.gcd(pair_total, 512)

    def forward(inputs, weights_all, vectors_all):
        rounded = low(weights_all)

        def one_group(pieces):
            return jax.vmap(residual_block)(pieces[0], pieces[1], rounded, vectors_all)
        outputs = lax.map(jax.checkpoint(one_group), (inputs, allowed)).reshape(CAP_ROWS, SEQ, D)
        text_emb = low(unit_rows(caption_pool(outputs, segments)))
        objective = (side_loss(image_emb, text_emb, block_rows) + side_loss(text_emb, image_emb, block_rows)) / 2.0
        return (objective, outputs)
    (objective, outputs), pullback = jax.vjp(forward, text_blocks, worker_weights, worker_vectors)
    grad_inputs, grad_workers, grad_vectors = pullback((jnp.ones_like(objective), jnp.zeros_like(outputs)))
    worker_rows = grad_workers + error_feedback
    bounds = matrix_bounds()
    factors = jnp.stack([jnp.einsum('kc,rdc->kd', start_factors[:, first_col:after_col], worker_rows[:, :, first_col:after_col], precision=PRECISE) for first_col, after_col in bounds])
    left_basis = orthonormal(factors)
    new_right = jnp.concatenate([jnp.einsum('kd,rdc->kc', left_basis[matrix_id], worker_rows[:, :, bounds[matrix_id][0]:bounds[matrix_id][1]], precision=PRECISE) for matrix_id in range(4)], axis=1)
    approximation = jnp.concatenate([jnp.einsum('kd,kc->dc', left_basis[matrix_id], new_right[:, bounds[matrix_id][0]:bounds[matrix_id][1]], precision=PRECISE) for matrix_id in range(4)], axis=1)
    new_feedback = worker_rows - approximation / N_REP
    new_momentum = MOMENTUM_DECAY * momentum + approximation
    new_weights = text_weights - STEP_RATE * new_momentum
    vector_grad = lax.optimization_barrier(jnp.sum(grad_vectors, axis=0))
    new_vector_momentum = MOMENTUM_DECAY * vector_momentum + vector_grad
    new_vectors = text_vectors - STEP_RATE * new_vector_momentum
    contrast_loss = objective / pair_total
    return (contrast_loss, outputs, grad_inputs.reshape(CAP_ROWS, SEQ, D), new_weights, new_momentum, new_feedback, new_vectors, new_vector_momentum, left_basis.reshape(4 * RANK, D), new_right)
```

```python
import functools

import jax
import jax.numpy as jnp
from jax import lax
from jax.experimental import pallas as pl
from jax.experimental.pallas import tpu as pltpu
from jax.sharding import PartitionSpec as P

D = 768
FF = 3072
HEADS = 12
HEAD_DIM = 64
PER_ROW = 4
GROUP = 4
SECTION = 3072
LANE_COLS = 512

PRECISE = lax.Precision.HIGHEST
LAYER_EPS = 1e-06
SCORE_SCALE = 0.125
LOGIT_SCALE = 50.0
MOMENTUM_DECAY = 0.9
STEP_RATE = 0.08
NORM_FLOOR = 1e-08
MASKED = -1e30
MESH = pl.DeviceIdType.MESH


def layer_norm(values, layer_gain, layer_shift):
    center = values - jnp.mean(values, axis=-1, keepdims=True)
    spread = jnp.mean(center * center, axis=-1, keepdims=True)
    return center * lax.rsqrt(spread + LAYER_EPS) * layer_gain + layer_shift


def unit_rows(values):
    return values * lax.rsqrt(jnp.sum(values * values, axis=-1, keepdims=True) + LAYER_EPS)


def vector_parts(vectors):
    pieces = [vectors[position * D : (position + 1) * D] for position in range(8)]
    return pieces + [vectors[8 * D :]]


def matrix_bounds():
    return ((0, 3 * D), (3 * D, 4 * D), (4 * D, 4 * D + FF), (4 * D + FF, 4 * D + 2 * FF))


def gather_kernel(
    n_dp, text_ref, image_ref, tok_ref, seg_ref, wt_ref, wi_ref, tok_out, seg_out,
    z_send, z_recv, y_send, y_recv, x_send, x_recv, c_send, c_recv, t_send, t_recv, t_own, own_sem,
):
    n_inner = n_dp // GROUP
    d_at, r_at = lax.axis_index("dp"), lax.axis_index("rep")
    z_at, y_at = d_at // n_inner, d_at % n_inner
    x_at, c_at = r_at // 2, r_at % 2
    z_peers = [(lax.rem(z_at + k, GROUP) * n_inner + y_at, r_at) for k in range(1, GROUP)]
    z_from = [lax.rem(z_at + GROUP - k, GROUP) for k in range(1, GROUP)]
    y_peers = [(z_at * n_inner + lax.rem(y_at + k, n_inner), r_at) for k in range(1, n_inner)]
    y_from = [lax.rem(y_at + n_inner - k, n_inner) for k in range(1, n_inner)]
    x_peer = (d_at, (1 - x_at) * 2 + c_at)
    c_peer = (d_at, x_at * 2 + 1 - c_at)

    barrier = pltpu.get_barrier_semaphore()
    everyone = z_peers + y_peers + [x_peer, c_peer]
    for peer in everyone:
        pl.semaphore_signal(barrier, inc=1, device_id=peer, device_id_type=MESH)
    pl.semaphore_wait(barrier, len(everyone))

    def shard_of(z, y):
        return z * n_inner + y

    sections = [(image_ref, wi_ref, 0), (text_ref, wt_ref, 0), (image_ref, wi_ref, 1),
                (text_ref, wt_ref, 1), (image_ref, wi_ref, 2), (text_ref, wt_ref, 2)]

    def cols(section, lane):
        start = sections[section][2] * SECTION + lane * LANE_COLS
        return pl.ds(pl.multiple_of(start, 128), LANE_COLS)

    lane_both = c_at
    lane_mine = 2 + x_at * 2 + c_at
    lane_theirs = 2 + (1 - x_at) * 2 + c_at
    lanes = (lane_both, lane_mine)

    locals_ = [
        pltpu.make_async_copy(tok_ref, tok_out.at[z_at], t_own.at[0]),
        pltpu.make_async_copy(seg_ref, seg_out.at[z_at], t_own.at[1]),
    ]
    for s, (src, full, _) in enumerate(sections):
        for j in range(2):
            column = cols(s, lanes[j])
            locals_.append(pltpu.make_async_copy(src.at[:, column], full.at[d_at, :, column], own_sem.at[s, j]))
    for copy in locals_:
        copy.start()

    def remote(src, dst, send, recv, peer):
        return pltpu.make_async_remote_copy(
            src_ref=src, dst_ref=dst, send_sem=send, recv_sem=recv, device_id=peer, device_id_type=MESH
        )

    def z_copy(s, k, j):
        src, full, _ = sections[s]
        return remote(
            src.at[:, cols(s, lanes[j])], full.at[d_at, :, cols(s, lanes[j])],
            z_send.at[s, k, j], z_recv.at[s, k, j], z_peers[k],
        )

    def y_copy(s, q, zi, j):
        src, full, _ = sections[s]
        column = cols(s, lanes[j])
        if zi == 0:
            shard, source = d_at, src.at[:, column]
        else:
            shard = shard_of(z_from[zi - 1], y_at)
            source = full.at[shard, :, column]
        return remote(source, full.at[shard, :, column], y_send.at[s, q, zi, j], y_recv.at[s, q, zi, j], y_peers[q])

    def x_copy(s):
        full = sections[s][1]
        block = full.at[:, :, cols(s, lane_mine)]
        return remote(block, block, x_send.at[s], x_recv.at[s], x_peer)

    def c_copy(s, j):
        full = sections[s][1]
        block = full.at[:, :, cols(s, (lane_both, lane_mine, lane_theirs)[j])]
        return remote(block, block, c_send.at[s, j], c_recv.at[s, j], c_peer)

    count = len(sections)
    tokens = []
    for k in range(GROUP - 1):
        tokens.append(remote(tok_ref, tok_out.at[z_at], t_send.at[0, k], t_recv.at[0, k], z_peers[k]))
        tokens.append(remote(seg_ref, seg_out.at[z_at], t_send.at[1, k], t_recv.at[1, k], z_peers[k]))

    def begin(s):
        for j in range(2):
            for k in range(GROUP - 1):
                z_copy(s, k, j).start()
            for q in range(n_inner - 1):
                y_copy(s, q, 0, j).start()

    begin(0)
    for copy in tokens:
        copy.start()
    for copy in locals_:
        copy.wait()
    begin(1)
    for step in range(count + 3):
        if step < count:
            for k in range(GROUP - 1):
                for j in range(2):
                    z_copy(step, k, j).wait_recv()
                    for q in range(n_inner - 1):
                        y_copy(step, q, k + 1, j).start()
            if step + 2 < count:
                begin(step + 2)
        s = step - 1
        if 0 <= s < count:
            for q in range(n_inner - 1):
                for zi in range(GROUP):
                    for j in range(2):
                        y_copy(s, q, zi, j).wait_recv()
            x_copy(s).start()
            for j in range(2):
                c_copy(s, j).start()
        s = step - 2
        if 0 <= s < count:
            x_copy(s).wait_recv()
            c_copy(s, 2).start()
        s = step - 3
        if 0 <= s < count:
            for j in range(3):
                c_copy(s, j).wait_recv()
    for copy in tokens:
        copy.wait()
    for s in range(count):
        for j in range(2):
            for k in range(GROUP - 1):
                z_copy(s, k, j).wait_send()
            for q in range(n_inner - 1):
                for zi in range(GROUP):
                    y_copy(s, q, zi, j).wait_send()
        x_copy(s).wait_send()
        for j in range(3):
            c_copy(s, j).wait_send()


def gather_weights(n_dp, text_low, image_low, tokens, segments):
    n_inner = n_dp // GROUP
    full = jax.ShapeDtypeStruct((n_dp,) + text_low.shape, jnp.bfloat16)
    hbm = pl.BlockSpec(memory_space=pltpu.HBM)
    dma = pltpu.SemaphoreType.DMA
    return pl.pallas_call(
        functools.partial(gather_kernel, n_dp),
        out_shape=(
            full,
            full,
            jax.ShapeDtypeStruct((GROUP,) + tokens.shape, jnp.bfloat16),
            jax.ShapeDtypeStruct((GROUP,) + segments.shape, jnp.int32),
        ),
        in_specs=[hbm] * 4,
        out_specs=(hbm,) * 4,
        scratch_shapes=[
            dma((6, GROUP - 1, 2)), dma((6, GROUP - 1, 2)),
            dma((6, n_inner - 1, GROUP, 2)), dma((6, n_inner - 1, GROUP, 2)),
            dma((6,)), dma((6,)), dma((6, 3)), dma((6, 3)),
            dma((2, GROUP - 1)), dma((2, GROUP - 1)), dma((2,)), dma((6, 2)),
        ],
        compiler_params=pltpu.CompilerParams(collective_id=1, has_side_effects=True),
        name="gather_weights",
    )(text_low, image_low, tokens, segments)


def peer_at(offset, n_dp, n_rep):
    me = lax.axis_index("dp") * n_rep + lax.axis_index("rep")
    other = lax.rem(me + offset, n_dp * n_rep)
    return other, (other // n_rep, lax.rem(other, n_rep))


def meet(n_dp, n_rep):
    total = n_dp * n_rep
    barrier = pltpu.get_barrier_semaphore()

    def hello(offset, carry):
        _, peer = peer_at(offset, n_dp, n_rep)
        pl.semaphore_signal(barrier, inc=1, device_id=peer, device_id_type=MESH)
        return carry

    lax.fori_loop(1, total, hello, 0)
    pl.semaphore_wait(barrier, total - 1)


def spread_kernel(n_dp, n_rep, mine_ref, all_ref, send, recv, own_sem):
    total = n_dp * n_rep
    me = lax.axis_index("dp") * n_rep + lax.axis_index("rep")
    own = pltpu.make_async_copy(mine_ref, all_ref.at[me], own_sem)
    own.start()
    meet(n_dp, n_rep)

    def copy(offset):
        _, peer = peer_at(offset, n_dp, n_rep)
        return pltpu.make_async_remote_copy(
            src_ref=mine_ref, dst_ref=all_ref.at[me], send_sem=send.at[offset - 1],
            recv_sem=recv.at[offset - 1], device_id=peer, device_id_type=MESH,
        )

    def begin(offset, carry):
        copy(offset).start()
        return carry

    def finish(offset, carry):
        copy(offset).wait()
        return carry

    lax.fori_loop(1, total, begin, 0)
    own.wait()
    lax.fori_loop(1, total, finish, 0)


def spread(mine, n_dp, n_rep, collective, name):
    total = n_dp * n_rep
    vmem = pl.BlockSpec(memory_space=pltpu.VMEM)
    dma = pltpu.SemaphoreType.DMA
    return pl.pallas_call(
        functools.partial(spread_kernel, n_dp, n_rep),
        out_shape=jax.ShapeDtypeStruct((total,) + mine.shape, mine.dtype),
        in_specs=[vmem],
        out_specs=vmem,
        scratch_shapes=[dma((total - 1,)), dma((total - 1,)), dma],
        compiler_params=pltpu.CompilerParams(
            collective_id=collective, has_side_effects=True, vmem_limit_bytes=48 << 20
        ),
        name=name,
    )(mine)


def total_kernel(n_dp, n_rep, mine_ref, out_ref, parts, sums, send, recv, send_two, recv_two):
    total = n_dp * n_rep
    me = lax.axis_index("dp") * n_rep + lax.axis_index("rep")
    meet(n_dp, n_rep)

    def scatter(offset):
        other, peer = peer_at(offset, n_dp, n_rep)
        return pltpu.make_async_remote_copy(
            src_ref=mine_ref.at[other], dst_ref=parts.at[offset - 1], send_sem=send.at[offset - 1],
            recv_sem=recv.at[offset - 1], device_id=peer, device_id_type=MESH,
        )

    def share(offset):
        _, peer = peer_at(offset, n_dp, n_rep)
        return pltpu.make_async_remote_copy(
            src_ref=sums, dst_ref=out_ref.at[me], send_sem=send_two.at[offset - 1],
            recv_sem=recv_two.at[offset - 1], device_id=peer, device_id_type=MESH,
        )

    def start_scatter(offset, carry):
        scatter(offset).start()
        return carry

    def add(offset, carry):
        scatter(offset).wait_recv()
        return carry + parts[offset - 1]

    def start_share(offset, carry):
        share(offset).start()
        return carry

    def finish(offset, carry):
        scatter(offset).wait_send()
        share(offset).wait()
        return carry

    lax.fori_loop(1, total, start_scatter, 0)
    result = lax.fori_loop(1, total, add, mine_ref[me])
    sums[...] = result
    lax.fori_loop(1, total, start_share, 0)
    out_ref[me] = result
    lax.fori_loop(1, total, finish, 0)


def total_over_all(flat, n_dp, n_rep, collective, name):
    total = n_dp * n_rep
    count = flat.shape[0]
    chunk = -(-count // (total * 1024)) * 1024
    padded = jnp.pad(flat, (0, total * chunk - count)).reshape(total, chunk // 128, 128)
    vmem = pl.BlockSpec(memory_space=pltpu.VMEM)
    dma = pltpu.SemaphoreType.DMA
    summed = pl.pallas_call(
        functools.partial(total_kernel, n_dp, n_rep),
        out_shape=jax.ShapeDtypeStruct(padded.shape, padded.dtype),
        in_specs=[vmem],
        out_specs=vmem,
        scratch_shapes=[
            pltpu.VMEM((total - 1,) + padded.shape[1:], padded.dtype),
            pltpu.VMEM(padded.shape[1:], padded.dtype),
            dma((total - 1,)), dma((total - 1,)), dma((total - 1,)), dma((total - 1,)),
        ],
        compiler_params=pltpu.CompilerParams(
            collective_id=collective, has_side_effects=True, vmem_limit_bytes=48 << 20
        ),
        name=name,
    )(padded)
    return summed.reshape(-1)[:count]


def masked_scores(query_heads, key_heads, allowed):
    scores = (
        jnp.einsum("rshd,rthd->rhst", query_heads, key_heads, preferred_element_type=jnp.float32)
        * SCORE_SCALE
    )
    return jnp.where(allowed[:, None], scores, MASKED)


def block_forward(inputs, allowed, weights, vector_pieces, pooled_only):
    (
        gain_one, shift_one, bias_query, bias_value, bias_out,
        gain_two, shift_two, bias_shrink, bias_expand,
    ) = vector_pieces
    row_count, seq_tokens = (inputs.shape[0], inputs.shape[1])
    normed = layer_norm(inputs, gain_one, shift_one).astype(jnp.bfloat16)
    mixing = jnp.einsum("rsd,dc->rsc", normed, weights[:, : 3 * D], preferred_element_type=jnp.float32)
    mixing = mixing + jnp.concatenate([bias_query, jnp.zeros_like(bias_query), bias_value])
    head_parts = mixing.astype(jnp.bfloat16).reshape(row_count, seq_tokens, 3, HEADS, HEAD_DIM)
    query_heads, key_heads, value_heads = (head_parts[:, :, 0], head_parts[:, :, 1], head_parts[:, :, 2])
    scores = masked_scores(query_heads, key_heads, allowed)
    highest = jnp.max(scores, axis=-1, keepdims=True)
    log_total = highest + jnp.log(jnp.sum(jnp.exp(scores - highest), axis=-1, keepdims=True))
    attention = jnp.exp(scores - log_total).astype(jnp.bfloat16)
    mixed_heads = jnp.einsum("rhst,rthd->rshd", attention, value_heads, preferred_element_type=jnp.float32)
    mixed_heads = mixed_heads.reshape(row_count, seq_tokens, D).astype(jnp.bfloat16)
    attended = (
        jnp.einsum("rsd,de->rse", mixed_heads, weights[:, 3 * D : 4 * D], preferred_element_type=jnp.float32)
        + bias_out
    )
    middle = inputs + attended
    normed_two = layer_norm(middle, gain_two, shift_two).astype(jnp.bfloat16)
    hidden = (
        jnp.einsum("rsd,df->rsf", normed_two, weights[:, 4 * D : 4 * D + FF], preferred_element_type=jnp.float32)
        + bias_expand
    )
    active = jax.nn.gelu(hidden, approximate=False).astype(jnp.bfloat16)
    shrink = weights[:, 4 * D + FF :]
    if pooled_only:
        mean_active = jnp.mean(active.astype(jnp.float32), axis=1)
        high = mean_active.astype(jnp.bfloat16)
        rest = mean_active - high.astype(jnp.float32)
        low = rest.astype(jnp.bfloat16)
        lower = (rest - low.astype(jnp.float32)).astype(jnp.bfloat16)
        stacked = jnp.concatenate([high, low, lower], axis=0)
        shrunk = jnp.einsum("pf,df->pd", stacked, shrink, preferred_element_type=jnp.float32)
        shrunk = jnp.sum(shrunk.reshape(3, row_count, D), axis=0)
        return jnp.mean(middle, axis=1) + shrunk + bias_shrink
    shrunk = jnp.einsum("rsf,df->rsd", active, shrink, preferred_element_type=jnp.float32) + bias_shrink
    kept = (normed, query_heads, key_heads, value_heads, log_total, mixed_heads, middle, normed_two, hidden, active)
    return (middle + shrunk, kept)


def token_sum(values_low):
    return jnp.sum(values_low.astype(jnp.float32).reshape(-1, values_low.shape[-1]), axis=0)


def block_backward(inputs, allowed, weights, vector_pieces, forward_kept, grad_out, own_group, own_count):
    (gain_one, shift_one, _, _, _, gain_two, shift_two, _, _) = vector_pieces
    (normed, query_heads, key_heads, value_heads, log_total, mixed_heads, middle, normed_two, hidden, active) = forward_kept
    row_count, seq_tokens = (inputs.shape[0], inputs.shape[1])
    grad_shrunk = grad_out.astype(jnp.bfloat16)
    grad_active = jnp.einsum("rsd,df->rsf", grad_shrunk, weights[:, 4 * D + FF :], preferred_element_type=jnp.float32)
    _, gelu_back = jax.vjp(lambda before_gelu: jax.nn.gelu(before_gelu, approximate=False), hidden)
    grad_hidden = gelu_back(grad_active)[0].astype(jnp.bfloat16)
    grad_normed_two = jnp.einsum(
        "rsf,df->rsd", grad_hidden, weights[:, 4 * D : 4 * D + FF], preferred_element_type=jnp.float32
    )
    _, norm_two_back = jax.vjp(layer_norm, middle, gain_two, shift_two)
    grad_middle, grad_gain_two, grad_shift_two = norm_two_back(grad_normed_two)
    grad_middle = grad_middle + grad_out
    grad_attended = grad_middle.astype(jnp.bfloat16)
    grad_mixed = jnp.einsum("rse,de->rsd", grad_attended, weights[:, 3 * D : 4 * D], preferred_element_type=jnp.float32)
    grad_mixed = grad_mixed.astype(jnp.bfloat16).reshape(row_count, seq_tokens, HEADS, HEAD_DIM)
    attention = jnp.exp(masked_scores(query_heads, key_heads, allowed) - log_total)
    grad_values = jnp.einsum("rhst,rshd->rthd", attention.astype(jnp.bfloat16), grad_mixed, preferred_element_type=jnp.float32)
    grad_attention = jnp.einsum("rshd,rthd->rhst", grad_mixed, value_heads, preferred_element_type=jnp.float32)
    grad_scores = attention * (grad_attention - jnp.sum(attention * grad_attention, axis=-1, keepdims=True))
    grad_scores = grad_scores.astype(jnp.bfloat16)
    grad_query = jnp.einsum("rhst,rthd->rshd", grad_scores, key_heads, preferred_element_type=jnp.float32) * SCORE_SCALE
    grad_keys = jnp.einsum("rhst,rshd->rthd", grad_scores, query_heads, preferred_element_type=jnp.float32) * SCORE_SCALE
    grad_mixing = (
        jnp.stack([grad_query, grad_keys, grad_values], axis=2).reshape(row_count, seq_tokens, 3 * D).astype(jnp.bfloat16)
    )

    def mine(values):
        return lax.dynamic_slice_in_dim(values, own_group * own_count, own_count, 0)

    grad_normed = jnp.einsum("rsc,dc->rsd", mine(grad_mixing), weights[:, : 3 * D], preferred_element_type=jnp.float32)
    _, norm_one_back = jax.vjp(layer_norm, mine(inputs), gain_one, shift_one)
    grad_inputs, grad_gain_one, grad_shift_one = norm_one_back(grad_normed)
    grad_inputs = grad_inputs + mine(grad_middle)
    share = 1.0 / GROUP
    vector_grad = jnp.concatenate(
        [
            grad_gain_one, grad_shift_one,
            share * token_sum(grad_mixing[..., :D]), share * token_sum(grad_mixing[..., 2 * D :]),
            share * token_sum(grad_attended), share * grad_gain_two, share * grad_shift_two,
            share * token_sum(grad_shrunk), share * token_sum(grad_hidden),
        ]
    )
    tokens = row_count * seq_tokens
    outer_terms = (
        (normed.reshape(tokens, D), grad_mixing.reshape(tokens, 3 * D)),
        (mixed_heads.reshape(tokens, D), grad_attended.reshape(tokens, D)),
        (normed_two.reshape(tokens, D), grad_hidden.reshape(tokens, FF)),
        (grad_shrunk.reshape(tokens, D), active.reshape(tokens, FF)),
    )
    return (grad_inputs, vector_grad, outer_terms)


def orthonormal(stacked):
    waiting = [stacked[:, column_id] for column_id in range(stacked.shape[1])]
    finished = []
    while waiting:
        vector = waiting.pop(0)
        vector = vector / (jnp.sqrt(jnp.sum(vector * vector, axis=-1, keepdims=True)) + NORM_FLOOR)
        finished.append(vector)
        if waiting:
            later = jnp.stack(waiting, axis=1)
            later = later - jnp.sum(vector[:, None] * later, axis=-1, keepdims=True) * vector[:, None]
            waiting = [later[:, i] for i in range(later.shape[1])]
    return jnp.stack(finished, axis=1)


def rows_factor(start_part, row_block):
    return jnp.einsum("kc,dc->kd", start_part, row_block, precision=PRECISE)


def per_device(
    image_tokens, image_weights, image_vectors, text_tokens, segments, text_weights,
    text_vectors, momentum, vector_momentum, error_feedback, start_factors,
):
    n_rep, n_dp = lax.axis_size("rep"), lax.axis_size("dp")
    n_inner = n_dp // GROUP
    total = n_rep * n_dp
    device_pairs, patches = image_tokens.shape[0], image_tokens.shape[1]
    text_rows, seq_tokens = text_tokens.shape[0], text_tokens.shape[1]
    pair_total = device_pairs * total
    own_rows = text_weights.shape[0]
    d_at, r_at = lax.axis_index("dp"), lax.axis_index("rep")
    z_at, y_at = d_at // n_inner, d_at % n_inner
    row_start = d_at * own_rows
    factor_rank = start_factors.shape[0]
    bounds = matrix_bounds()
    text_low, frozen, token_group, segment_group = gather_weights(
        n_dp, text_weights.astype(jnp.bfloat16), image_weights,
        text_tokens.reshape(text_rows * seq_tokens, D), segments,
    )
    text_low, frozen = text_low.reshape(D, -1), frozen.reshape(D, -1)
    full_mask = jnp.zeros((device_pairs, patches, patches), jnp.int32) == 0
    image_pooled = block_forward(
        image_tokens.astype(jnp.float32), full_mask, frozen, vector_parts(image_vectors), True
    )
    image_emb = unit_rows(image_pooled).astype(jnp.bfloat16)

    group_rows = GROUP * text_rows
    text_float = token_group.reshape(group_rows, seq_tokens, D).astype(jnp.float32)
    segment_all = segment_group.reshape(group_rows, seq_tokens)
    allowed = segment_all[:, :, None] == segment_all[:, None, :]
    vector_pieces = vector_parts(text_vectors)
    group_output, forward_kept = block_forward(text_float, allowed, text_low, vector_pieces, False)
    text_output = lax.dynamic_slice_in_dim(group_output, z_at * text_rows, text_rows, 0)
    caption_marks = (
        segment_all[:, None, :] == jnp.arange(PER_ROW, dtype=jnp.int32)[None, :, None]
    ).astype(jnp.float32)
    counts = jnp.sum(caption_marks, axis=-1, keepdims=True)
    pooled = (jnp.einsum("rks,rsd->rkd", caption_marks, group_output, precision=PRECISE) / counts).reshape(-1, D)
    text_norm, embed_back = jax.vjp(unit_rows, pooled)
    text_emb = text_norm.astype(jnp.bfloat16)
    own_emb = lax.dynamic_slice_in_dim(text_emb, z_at * device_pairs, device_pairs, 0)
    embeddings = spread(jnp.concatenate([image_emb, own_emb], axis=0), n_dp, n_rep, 2, "spread_embeddings")
    image_all = embeddings[:, :device_pairs].reshape(pair_total, D)
    text_all = embeddings[:, device_pairs:].reshape(pair_total, D)
    own_pairs = (
        ((jnp.arange(GROUP, dtype=jnp.int32) * n_inner + y_at) * n_rep + r_at)[:, None] * device_pairs
        + jnp.arange(device_pairs, dtype=jnp.int32)[None, :]
    ).reshape(-1)
    logits = LOGIT_SCALE * jnp.einsum("pd,bd->pb", image_all, text_all, preferred_element_type=jnp.float32)
    image_top = jnp.max(logits, axis=1)
    image_log_total = image_top + jnp.log(jnp.sum(jnp.exp(logits - image_top[:, None]), axis=1))
    caption_top = jnp.max(logits, axis=0)
    caption_log_total = caption_top + jnp.log(jnp.sum(jnp.exp(logits - caption_top[None, :]), axis=0))
    pair_ids = jnp.arange(pair_total, dtype=jnp.int32)
    matched = jnp.sum(jnp.where(pair_ids[:, None] == pair_ids[None, :], logits, 0.0), axis=1)
    loss_total = (jnp.sum(image_log_total - matched) + jnp.sum(caption_log_total - matched)) / (2.0 * pair_total)
    diagonal_pick = (pair_ids[None, :] == own_pairs[:, None]).astype(jnp.float32)
    text_logits = LOGIT_SCALE * jnp.einsum("pd,bd->pb", text_emb, image_all, preferred_element_type=jnp.float32)
    text_top = jnp.max(text_logits, axis=1, keepdims=True)
    text_log_total = text_top + jnp.log(jnp.sum(jnp.exp(text_logits - text_top), axis=1, keepdims=True))
    text_soft = ((jnp.exp(text_logits - text_log_total) - diagonal_pick) * 0.5).astype(jnp.bfloat16)
    column_soft = ((jnp.exp(text_logits - image_log_total[None, :]) - diagonal_pick) * 0.5).astype(jnp.bfloat16)
    grad_text = LOGIT_SCALE * (
        jnp.einsum("pb,bd->pd", text_soft, image_all, preferred_element_type=jnp.float32)
        + jnp.einsum("pb,bd->pd", column_soft, image_all, preferred_element_type=jnp.float32)
    )
    grad_pooled = embed_back(grad_text)[0].reshape(-1, PER_ROW, D) / counts
    grad_out = jnp.einsum("rks,rkd->rsd", caption_marks, grad_pooled, precision=PRECISE)
    grad_inputs, vector_grad, outer_terms = block_backward(
        text_float, allowed, text_low, vector_pieces, forward_kept, grad_out, z_at, text_rows
    )
    group_width = n_inner * own_rows
    worker_blocks = []
    feedback_rows = error_feedback[0]
    for (left_side, right_side), (first_col, after_col) in zip(outer_terms, bounds):
        left_cut = lax.dynamic_slice_in_dim(left_side, z_at * group_width, group_width, 1)
        block = jnp.einsum("tc,tk->ck", left_cut, right_side, preferred_element_type=jnp.float32)
        mine = lax.dynamic_slice_in_dim(block, y_at * own_rows, own_rows, 0)
        for k in range(1, n_inner):
            target = lax.rem(y_at + k, n_inner)
            outgoing = lax.dynamic_slice_in_dim(block, target * own_rows, own_rows, 0).astype(jnp.bfloat16)
            pairs = [
                (z * n_inner + y, z * n_inner + (y + k) % n_inner) for z in range(GROUP) for y in range(n_inner)
            ]
            mine = mine + lax.ppermute(outgoing, "dp", pairs).astype(jnp.float32)
        worker_blocks.append(mine + feedback_rows[:, first_col:after_col])
    factor_rows = jnp.concatenate(
        [
            rows_factor(start_factors[:, first_col:after_col], rows)
            for rows, (first_col, after_col) in zip(worker_blocks, bounds)
        ],
        axis=0,
    )
    gathered_rows = spread(factor_rows, n_dp, n_rep, 3, "spread_factors")
    factor = jnp.sum(gathered_rows.reshape(n_dp, n_rep, 4 * factor_rank, own_rows), axis=1)
    factor = jnp.swapaxes(factor, 0, 1).reshape(4, factor_rank, D)
    left_basis = orthonormal(factor).reshape(4 * factor_rank, D)
    basis_rows = lax.dynamic_slice_in_dim(left_basis, row_start, own_rows, 1)
    basis_parts = [basis_rows[i * factor_rank : (i + 1) * factor_rank] for i in range(4)]
    right_part = jnp.concatenate(
        [jnp.einsum("kd,dc->kc", part, rows, precision=PRECISE) for part, rows in zip(basis_parts, worker_blocks)],
        axis=1,
    )
    summed = total_over_all(
        jnp.concatenate([right_part.reshape(-1), vector_grad]), n_dp, n_rep, 4, "total_right"
    )
    new_right = summed[: right_part.size].reshape(right_part.shape)
    vector_total = summed[right_part.size :]
    approximation = jnp.concatenate(
        [
            jnp.einsum("kd,kc->dc", part, new_right[:, first_col:after_col], precision=PRECISE)
            for part, (first_col, after_col) in zip(basis_parts, bounds)
        ],
        axis=1,
    )
    worker_rows = jnp.concatenate(worker_blocks, axis=1)
    new_feedback = (worker_rows - approximation / n_rep)[None]
    new_momentum = MOMENTUM_DECAY * momentum + approximation
    new_weights = text_weights - STEP_RATE * new_momentum
    new_vector_momentum = MOMENTUM_DECAY * vector_momentum + vector_total
    new_vectors = text_vectors - STEP_RATE * new_vector_momentum
    return (
        loss_total, text_output, grad_inputs, new_weights, new_momentum, new_feedback,
        new_vectors, new_vector_momentum, left_basis, new_right,
    )


def solution(mesh):
    placed = (
        P(("dp", "rep"), None, None), P("dp", None), P(), P(("dp", "rep"), None, None), P(("dp", "rep"), None),
        P("dp", None), P(), P("dp", None), P(), P("rep", "dp", None), P(),
    )
    return jax.shard_map(
        per_device,
        mesh=mesh,
        in_specs=placed,
        out_specs=(
            P(), P(("dp", "rep"), None, None), P(("dp", "rep"), None, None), P("dp", None), P("dp", None),
            P("rep", "dp", None), P(), P(), P(), P(),
        ),
        check_vma=False,
    )
```

```python
import functools

import jax
import jax.numpy as jnp
from jax import lax
from jax.experimental import pallas as pl
from jax.experimental.pallas import tpu as pltpu
from jax.sharding import PartitionSpec as P

D = 768
FF = 3072
HEADS = 12
HEAD_DIM = 64
PER_ROW = 4
GROUP = 4
SECTION = 3072
LANE_COLS = 512

PRECISE = lax.Precision.HIGHEST
LAYER_EPS = 1e-06
SCORE_SCALE = 0.125
LOGIT_SCALE = 50.0
MOMENTUM_DECAY = 0.9
STEP_RATE = 0.08
NORM_FLOOR = 1e-08
MASKED = -1e30
MESH = pl.DeviceIdType.MESH


def layer_norm(values, layer_gain, layer_shift):
    center = values - jnp.mean(values, axis=-1, keepdims=True)
    spread = jnp.mean(center * center, axis=-1, keepdims=True)
    return center * lax.rsqrt(spread + LAYER_EPS) * layer_gain + layer_shift


def unit_rows(values):
    return values * lax.rsqrt(jnp.sum(values * values, axis=-1, keepdims=True) + LAYER_EPS)


def vector_parts(vectors):
    pieces = [vectors[position * D : (position + 1) * D] for position in range(8)]
    return pieces + [vectors[8 * D :]]


def matrix_bounds():
    return ((0, 3 * D), (3 * D, 4 * D), (4 * D, 4 * D + FF), (4 * D + FF, 4 * D + 2 * FF))


def gather_kernel(
    n_dp, text_ref, image_ref, tok_ref, seg_ref, wt_ref, wi_ref, tok_out, seg_out,
    z_send, z_recv, y_send, y_recv, x_send, x_recv, c_send, c_recv, t_send, t_recv, t_own, own_sem,
):
    n_inner = n_dp // GROUP
    d_at, r_at = lax.axis_index("dp"), lax.axis_index("rep")
    z_at, y_at = d_at // n_inner, d_at % n_inner
    x_at, c_at = r_at // 2, r_at % 2
    z_peers = [(lax.rem(z_at + k, GROUP) * n_inner + y_at, r_at) for k in range(1, GROUP)]
    z_from = [lax.rem(z_at + GROUP - k, GROUP) for k in range(1, GROUP)]
    y_peers = [(z_at * n_inner + lax.rem(y_at + k, n_inner), r_at) for k in range(1, n_inner)]
    y_from = [lax.rem(y_at + n_inner - k, n_inner) for k in range(1, n_inner)]
    x_peer = (d_at, (1 - x_at) * 2 + c_at)
    c_peer = (d_at, x_at * 2 + 1 - c_at)

    barrier = pltpu.get_barrier_semaphore()
    everyone = z_peers + y_peers + [x_peer, c_peer]
    for peer in everyone:
        pl.semaphore_signal(barrier, inc=1, device_id=peer, device_id_type=MESH)
    pl.semaphore_wait(barrier, len(everyone))

    def shard_of(z, y):
        return z * n_inner + y

    sections = [(image_ref, wi_ref, 0), (text_ref, wt_ref, 0), (image_ref, wi_ref, 1),
                (text_ref, wt_ref, 1), (image_ref, wi_ref, 2), (text_ref, wt_ref, 2)]

    def cols(section, lane):
        start = sections[section][2] * SECTION + lane * LANE_COLS
        return pl.ds(pl.multiple_of(start, 128), LANE_COLS)

    lane_both = c_at
    lane_mine = 2 + x_at * 2 + c_at
    lane_theirs = 2 + (1 - x_at) * 2 + c_at
    lanes = (lane_both, lane_mine)

    locals_ = [
        pltpu.make_async_copy(tok_ref, tok_out.at[z_at], t_own.at[0]),
        pltpu.make_async_copy(seg_ref, seg_out.at[z_at], t_own.at[1]),
    ]
    for s, (src, full, _) in enumerate(sections):
        for j in range(2):
            column = cols(s, lanes[j])
            locals_.append(pltpu.make_async_copy(src.at[:, column], full.at[d_at, :, column], own_sem.at[s, j]))
    for copy in locals_:
        copy.start()

    def remote(src, dst, send, recv, peer):
        return pltpu.make_async_remote_copy(
            src_ref=src, dst_ref=dst, send_sem=send, recv_sem=recv, device_id=peer, device_id_type=MESH
        )

    def z_copy(s, k, j):
        src, full, _ = sections[s]
        return remote(
            src.at[:, cols(s, lanes[j])], full.at[d_at, :, cols(s, lanes[j])],
            z_send.at[s, k, j], z_recv.at[s, k, j], z_peers[k],
        )

    def y_copy(s, q, zi, j):
        src, full, _ = sections[s]
        column = cols(s, lanes[j])
        if zi == 0:
            shard, source = d_at, src.at[:, column]
        else:
            shard = shard_of(z_from[zi - 1], y_at)
            source = full.at[shard, :, column]
        return remote(source, full.at[shard, :, column], y_send.at[s, q, zi, j], y_recv.at[s, q, zi, j], y_peers[q])

    def x_copy(s):
        full = sections[s][1]
        block = full.at[:, :, cols(s, lane_mine)]
        return remote(block, block, x_send.at[s], x_recv.at[s], x_peer)

    def c_copy(s, j):
        full = sections[s][1]
        block = full.at[:, :, cols(s, (lane_both, lane_mine, lane_theirs)[j])]
        return remote(block, block, c_send.at[s, j], c_recv.at[s, j], c_peer)

    count = len(sections)
    tokens = []
    for k in range(GROUP - 1):
        tokens.append(remote(tok_ref, tok_out.at[z_at], t_send.at[0, k], t_recv.at[0, k], z_peers[k]))
        tokens.append(remote(seg_ref, seg_out.at[z_at], t_send.at[1, k], t_recv.at[1, k], z_peers[k]))

    def begin(s):
        for j in range(2):
            for k in range(GROUP - 1):
                z_copy(s, k, j).start()
            for q in range(n_inner - 1):
                y_copy(s, q, 0, j).start()

    begin(0)
    for copy in tokens:
        copy.start()
    for copy in locals_:
        copy.wait()
    begin(1)
    for step in range(count + 3):
        if step < count:
            for k in range(GROUP - 1):
                for j in range(2):
                    z_copy(step, k, j).wait_recv()
                    for q in range(n_inner - 1):
                        y_copy(step, q, k + 1, j).start()
            if step + 2 < count:
                begin(step + 2)
        s = step - 1
        if 0 <= s < count:
            for q in range(n_inner - 1):
                for zi in range(GROUP):
                    for j in range(2):
                        y_copy(s, q, zi, j).wait_recv()
            x_copy(s).start()
            for j in range(2):
                c_copy(s, j).start()
        s = step - 2
        if 0 <= s < count:
            x_copy(s).wait_recv()
            c_copy(s, 2).start()
        s = step - 3
        if 0 <= s < count:
            for j in range(3):
                c_copy(s, j).wait_recv()
    for copy in tokens:
        copy.wait()
    for s in range(count):
        for j in range(2):
            for k in range(GROUP - 1):
                z_copy(s, k, j).wait_send()
            for q in range(n_inner - 1):
                for zi in range(GROUP):
                    y_copy(s, q, zi, j).wait_send()
        x_copy(s).wait_send()
        for j in range(3):
            c_copy(s, j).wait_send()


def gather_weights(n_dp, text_low, image_low, tokens, segments):
    n_inner = n_dp // GROUP
    full = jax.ShapeDtypeStruct((n_dp,) + text_low.shape, jnp.bfloat16)
    hbm = pl.BlockSpec(memory_space=pltpu.HBM)
    dma = pltpu.SemaphoreType.DMA
    return pl.pallas_call(
        functools.partial(gather_kernel, n_dp),
        out_shape=(
            full,
            full,
            jax.ShapeDtypeStruct((GROUP,) + tokens.shape, jnp.bfloat16),
            jax.ShapeDtypeStruct((GROUP,) + segments.shape, jnp.int32),
        ),
        in_specs=[hbm] * 4,
        out_specs=(hbm,) * 4,
        scratch_shapes=[
            dma((6, GROUP - 1, 2)), dma((6, GROUP - 1, 2)),
            dma((6, n_inner - 1, GROUP, 2)), dma((6, n_inner - 1, GROUP, 2)),
            dma((6,)), dma((6,)), dma((6, 3)), dma((6, 3)),
            dma((2, GROUP - 1)), dma((2, GROUP - 1)), dma((2,)), dma((6, 2)),
        ],
        compiler_params=pltpu.CompilerParams(collective_id=1, has_side_effects=True),
        name="gather_weights",
    )(text_low, image_low, tokens, segments)


TILE = 256
PAIR = 128
ROWS = 32
LANES = 6
PART = 768
PARTS = 12
DEPTH = 8
AHEAD = 2
LAG_Z = 1
LAG_Y = 1
LAG_X = 1
LAG_C = 1
AT_Y = 2 * LAG_Z + LAG_Y
AT_X = AT_Y + LAG_X
AT_C = AT_X + LAG_C
WORDS = (GROUP * PAIR)


def piece_of(vec_ref, index, width=D):
    return vec_ref[:, pl.ds(index * D, width)]


def loop(count, body, unroll=1):
    def step(i, carry):
        body(i)
        return carry

    lax.fori_loop(0, count, step, 0, unroll=unroll)


def aligned(i, size):
    return pl.ds(pl.multiple_of(i * size, size), size)


def norm_rows(values):
    center = values - jnp.mean(values, axis=-1, keepdims=True)
    spread_ = jnp.mean(center * center, axis=-1, keepdims=True)
    return center * lax.rsqrt(spread_ + LAYER_EPS)


def dot(left, right):
    return jnp.dot(left, right, preferred_element_type=jnp.float32)


def dot_nt(left, right):
    return lax.dot_general(left, right, (((1,), (1,)), ((), ())), preferred_element_type=jnp.float32)


def dot_tn(left, right):
    return lax.dot_general(left, right, (((0,), (0,)), ((), ())), preferred_element_type=jnp.float32)


def lane_is_first():
    return lax.broadcasted_iota(jnp.int32, (PAIR, PAIR), 1) < HEAD_DIM


def two_heads(block):
    first = lane_is_first()
    zero = jnp.zeros_like(block)
    return jnp.concatenate([jnp.where(first, block, zero), jnp.where(first, zero, block)], axis=0)


def attention_forward(qkv, mixed, chance, allowed_of):
    pairs = HEADS // 2

    def body(at):
        i, j = at // pairs, lax.rem(at, pairs)
        rows = aligned(i, PAIR)
        query = qkv[rows, aligned(j, PAIR)]
        key = qkv[rows, pl.ds(pl.multiple_of(D + j * PAIR, PAIR), PAIR)]
        value = qkv[rows, pl.ds(pl.multiple_of(2 * D + j * PAIR, PAIR), PAIR)]
        scores = dot_nt(two_heads(query), key) * SCORE_SCALE
        allowed = allowed_of(i)
        scores = jnp.where(jnp.concatenate([allowed, allowed], axis=0), scores, MASKED)
        scores = jnp.exp(scores - jnp.max(scores, axis=-1, keepdims=True))
        weight = scores / jnp.sum(scores, axis=-1, keepdims=True)
        if chance is not None:
            chance[at] = weight
        low = weight.astype(jnp.bfloat16)
        side = jnp.concatenate([low[:PAIR], low[PAIR:]], axis=1)
        mixed[rows, aligned(j, PAIR)] = dot(side, two_heads(value)).astype(jnp.bfloat16)

    loop(GROUP * pairs, body, unroll=2)


def forward_kernel(
    n_dp, patches,
    text_ref, image_ref, tok_ref, col_ref, row_ref, pic_ref, tvec_ref, ivec_ref,
    wt_out, words_out, text_pool_out, image_pool_out, marks_out, tok_out, qkv_out, chance_out, mid_out, slope_out,
    act_out, nt_out, at_out, mt_out,
    wi_ref, wt_vmem, tok, seg_col, seg_row, normed, qkv, mixed, middle, normed_two, active, slope, chance, total, hid, turned, apool,
    z_send, z_recv, y_send, y_recv, x_send, x_recv, c_send, c_recv, t_send, t_recv, t_own, own_sem, w_sem, out_sem,
):
    n_inner = n_dp // GROUP
    d_at, r_at = lax.axis_index("dp"), lax.axis_index("rep")
    z_at, y_at = d_at // n_inner, lax.rem(d_at, n_inner)
    x_at, c_at = r_at // 2, lax.rem(r_at, 2)
    z_peers = [(lax.rem(z_at + k, GROUP) * n_inner + y_at, r_at) for k in range(1, GROUP)]
    z_next = [((z_at - 1) * n_inner + y_at, r_at), ((z_at + 1) * n_inner + y_at, r_at)]
    y_peers = [(z_at * n_inner + 1 - y_at, r_at)]
    x_peer = (d_at, (1 - x_at) * 2 + c_at)
    c_peer = (d_at, x_at * 2 + 1 - c_at)

    barrier = pltpu.get_barrier_semaphore()
    everyone = z_peers + y_peers + [x_peer, c_peer]
    for peer in everyone:
        pl.semaphore_signal(barrier, inc=1, device_id=peer, device_id_type=MESH)
    pl.semaphore_wait(barrier, len(everyone))

    sections = [(text_ref, wt_vmem, k) for k in range(PARTS)] + [(image_ref, wi_ref, k) for k in range(PARTS)]
    count = len(sections)
    lane_both = c_at
    lane_mine = 2 + x_at * 2 + c_at
    lane_theirs = 2 + (1 - x_at) * 2 + c_at
    lanes = (lane_both, lane_mine)

    def remote(src, dst, send, recv, peer):
        return pltpu.make_async_remote_copy(
            src_ref=src, dst_ref=dst, send_sem=send, recv_sem=recv, device_id=peer, device_id_type=MESH
        )

    def cols(s):
        return pl.ds(sections[s][2] * PART, PART)

    def held(s, shard, lane):
        _, full, k = sections[s]
        return full.at[k, shard, lane]

    def z_copy(s, up, unit, j):
        shard = unit * n_inner + y_at
        return remote(
            held(s, shard, lanes[j]), held(s, shard, lanes[j]),
            z_send.at[s, up, unit, j], z_recv.at[s, unit, j], z_next[up],
        )

    def y_copy(s, q, unit, j):
        shard = unit * n_inner + y_at
        return remote(
            held(s, shard, lanes[j]), held(s, shard, lanes[j]),
            y_send.at[s, q, unit, j], y_recv.at[s, q, unit, j], y_peers[q],
        )

    def x_copy(s, unit):
        block = held(s, pl.ds(unit * n_inner, n_inner), lane_mine)
        return remote(block, block, x_send.at[s, unit], x_recv.at[s, unit], x_peer)

    def x_own_copy(s):
        block = held(s, z_at * n_inner + 1 - y_at, lane_mine)
        return remote(block, block, x_send.at[s, z_at], x_recv.at[s, z_at], x_peer)

    def c_copy(s, j):
        block = held(s, slice(None), (lane_both, lane_mine, lane_theirs)[j])
        return remote(block, block, c_send.at[s, j], c_recv.at[s, j], c_peer)

    def store(s):
        return pltpu.make_async_copy(wt_vmem.at[s], wt_out.at[:, :, :, cols(s)], w_sem.at[s])

    firsts = [
        pltpu.make_async_copy(tok_ref, tok.at[z_at], t_own.at[0]),
        pltpu.make_async_copy(col_ref, seg_col.at[z_at], t_own.at[1]),
        pltpu.make_async_copy(row_ref, seg_row.at[z_at], t_own.at[2]),
    ]
    z_open = (z_at > 0, z_at < GROUP - 1)

    def own_shard(s):
        src, _, _ = sections[s]
        return [
            pltpu.make_async_copy(src.at[lane, :, cols(s)], held(s, d_at, lane), own_sem.at[s, j])
            for j, lane in enumerate((lane_both, lane_mine, lane_theirs))
        ]

    tokens = []
    for k in range(GROUP - 1):
        for which, (src, dst) in enumerate(((tok_ref, tok), (col_ref, seg_col), (row_ref, seg_row))):
            tokens.append(remote(src, dst.at[z_at], t_send.at[which, k], t_recv.at[which, k], z_peers[k]))

    def begin(s):
        for copy in own_shard(s):
            copy.wait()
        for j in range(2):
            for up in range(2):
                pl.when(z_open[up])(z_copy(s, up, z_at, j).start)
            y_copy(s, 0, z_at, j).start()

    def arrive(s, hop):
        for up in range(2):
            unit = z_at - hop if up else z_at + hop

            @pl.when((unit >= 0) & (unit < GROUP))
            def _():
                for j in range(2):
                    z_copy(s, up, unit, j).wait_recv()
                    pl.when(z_open[up])(z_copy(s, up, unit, j).start)
                    y_copy(s, 0, unit, j).start()

    def over_units(unit_fn, own_fn):
        for unit in range(GROUP):
            pl.when(unit != z_at)(functools.partial(unit_fn, unit))
        own_fn()

    def carry_on(step):
        if step + AHEAD < count:
            begin(step + AHEAD)
        for hop in range(1, GROUP):
            s = step - (hop - 1) * LAG_Z
            if 0 <= s < count:
                arrive(s, hop)
        s = step - AT_Y
        if 0 <= s < count:
            for unit in range(GROUP):
                for j in range(2):
                    y_copy(s, 0, unit, j).wait_recv()
            over_units(lambda unit: x_copy(s, unit).start(), lambda: x_own_copy(s).start())
            for j in range(2):
                c_copy(s, j).start()
        s = step - AT_X
        if 0 <= s < count:
            over_units(lambda unit: x_copy(s, unit).wait_recv(), lambda: x_own_copy(s).wait_recv())
            c_copy(s, 2).start()
        s = step - AT_C
        if 0 <= s < count:
            for j in range(3):
                c_copy(s, j).wait_recv()
            if s < PARTS:
                store(s).start()


    def weight_tile(s, c):
        _, full, k = sections[s]
        return full[k, :, :, :, aligned(c, TILE)].reshape(D, TILE)

    def weight_rows(s, half):
        _, full, k = sections[s]
        return full[k, pl.ds(half * (n_dp // 2), n_dp // 2)].reshape(D // 2, PART)

    def first_norm(read, vec):
        def body(i):
            rows = aligned(i, ROWS)
            value = norm_rows(read(i).astype(jnp.float32))
            normed[rows, :] = (value * piece_of(vec, 0) + piece_of(vec, 1)).astype(jnp.bfloat16)

        loop(WORDS // ROWS, body)

    def project(slot, part, bias):
        def body(c):
            out = dot(normed[...], weight_tile(slot, c))
            if bias is not None:
                out = out + bias[0][:, pl.ds(pl.multiple_of(bias[1] * D + c * TILE, TILE), TILE)]
            qkv[:, pl.ds(pl.multiple_of(part * D + c * TILE, TILE), TILE)] = out.astype(jnp.bfloat16)

        loop(PART // TILE, body)

    def attend(slot, read, vec):
        def body(c):
            where = aligned(c, TILE)
            middle[:, where] = dot(mixed[...], weight_tile(slot, c)) + vec[
                :, pl.ds(pl.multiple_of(4 * D + c * TILE, TILE), TILE)
            ]

        loop(PART // TILE, body)

        def norm(i):
            rows = aligned(i, ROWS)
            value = middle[rows, :] + read(i).astype(jnp.float32)
            middle[rows, :] = value
            normed_two[rows, :] = (norm_rows(value) * piece_of(vec, 5) + piece_of(vec, 6)).astype(jnp.bfloat16)

        loop(WORDS // ROWS, norm)

    def expand(slot, part, vec, keep):
        def body(c):
            start = pl.multiple_of(part * PART + c * TILE, TILE)
            hid[...] = dot(normed_two[...], weight_tile(slot, c)) + vec[:, pl.ds(pl.multiple_of(8 * D + start, TILE), TILE)]

            def inner(i):
                rows = aligned(i, ROWS)
                value = hid[rows, :]
                phi = 0.5 + 0.5 * lax.erf(value * 0.7071067811865476)
                active[rows, pl.ds(start, TILE)] = (value * phi).astype(jnp.bfloat16)
                if keep:
                    slope[rows, pl.ds(start, TILE)] = phi + value * (
                        0.3989422804014327 * jnp.exp(-0.5 * value * value)
                    )

            loop(WORDS // ROWS, inner, unroll=2)

        loop(PART // TILE, body)

    def shrink(slot, part, vec):
        for half in range(2):
            where = pl.ds(half * (D // 2), D // 2)
            out = dot_nt(active[:, pl.ds(part * PART, PART)], weight_rows(slot, half))
            if part == 0:
                total[:, where] = out + middle[:, where] + vec[:, pl.ds(7 * D + half * (D // 2), D // 2)]
            else:
                total[:, where] += out

    def turn(source, slot, out):
        def body(c):
            turned[slot, aligned(c, PAIR), :] = source[:, aligned(c, PAIR)].T

        loop(D // PAIR, body)
        send_out(turned.at[slot, group_rows], out)

    outs, late = [], []

    def send_out(src, dst, kept=outs):
        copy = pltpu.make_async_copy(src, dst, out_sem.at[len(outs) + len(late)])
        copy.start()
        kept.append(copy)

    group_rows = pl.ds(pl.multiple_of(z_at * (D // GROUP), D // GROUP), D // GROUP)

    def text_read(i):
        per = PAIR // ROWS
        return tok[i // per, aligned(lax.rem(i, per), ROWS), :]

    def text_allowed(i):
        col = seg_col[i].astype(jnp.float32)
        row = seg_row[i].astype(jnp.float32)
        return col == row[0:1, :]

    def image_read(i):
        return pic_ref[aligned(i, ROWS), :]

    def picture(axis):
        at = lax.broadcasted_iota(jnp.int32, (PAIR, PAIR), axis)
        number = at // (PAIR // 2)
        return jnp.where(lax.rem(at, PAIR // 2) < patches, number, number + 2)

    def image_allowed(i):
        return picture(0) == picture(1)

    def keep_mark():
        image = lax.broadcasted_iota(jnp.int32, (GROUP * 2, WORDS), 0)
        at = lax.broadcasted_iota(jnp.int32, (GROUP * 2, WORDS), 1)
        inside = (at // (PAIR // 2) == image) & (lax.rem(at, PAIR // 2) < patches)
        return jnp.where(inside, 1.0, 0.0)

    def text_part(s):
        slot = s
        if s == 0:
            for copy in tokens:
                copy.wait()
            send_out(tok, tok_out)
            first_norm(text_read, tvec_ref)
            project(slot, 0, (tvec_ref, 2))
            turn(normed, 0, nt_out)
        elif s == 1:
            project(slot, 1, None)
        elif s == 2:
            project(slot, 2, (tvec_ref, 3))
            send_out(qkv, qkv_out)
            attention_forward(qkv, mixed, chance, text_allowed)
            send_out(chance, chance_out)
            turn(mixed, 1, at_out)
        elif s == 3:
            attend(slot, text_read, tvec_ref)
            send_out(middle, mid_out)
            turn(normed_two, 2, mt_out)
        elif s < 8:
            expand(slot, s - 4, tvec_ref, True)
        else:
            if s == 8:
                send_out(active, act_out)
                send_out(slope, slope_out)
            shrink(slot, s - 8, tvec_ref)
        if s == PARTS - 1:
            send_out(total.at[aligned(z_at, PAIR)], words_out, late)
            for i in range(GROUP):
                row = seg_row[i].astype(jnp.float32)[0:8, :]
                marks = jnp.where(row == lax.broadcasted_iota(jnp.int32, (8, PAIR), 0).astype(jnp.float32), 1.0, 0.0)
                marks_out[i] = marks
                sums = jnp.dot(
                    marks, total[pl.ds(i * PAIR, PAIR), :], precision=PRECISE, preferred_element_type=jnp.float32
                )
                text_pool_out[pl.ds(i * 8, 8), :] = sums / jnp.sum(marks, axis=1, keepdims=True)

    def image_part(s):
        slot, k = s, s - PARTS
        if k == 0:
            for copy in outs:
                copy.wait()
            first_norm(image_read, ivec_ref)
            project(slot, 0, (ivec_ref, 2))
        elif k == 1:
            project(slot, 1, None)
        elif k == 2:
            project(slot, 2, (ivec_ref, 3))
            attention_forward(qkv, mixed, None, image_allowed)
        elif k == 3:
            attend(slot, image_read, ivec_ref)
            apool[...] = jnp.zeros_like(apool)
        elif k < 8:
            expand(slot, k - 4, ivec_ref, False)
            mark = keep_mark().astype(jnp.bfloat16)
            where = pl.ds((k - 4) * PART, PART)
            mean = dot(mark, active[:, where]) * (1.0 / patches)
            high = mean.astype(jnp.bfloat16)
            rest = mean - high.astype(jnp.float32)
            low = rest.astype(jnp.bfloat16)
            apool[0:8, where] = high.astype(jnp.float32)
            apool[8:16, where] = low.astype(jnp.float32)
            apool[16:24, where] = rest - low.astype(jnp.float32)
        else:
            for half in range(2):
                where = pl.ds(half * (D // 2), D // 2)
                left = apool[:, pl.ds((k - 8) * PART, PART)].astype(jnp.bfloat16)
                out = dot_nt(left, weight_rows(slot, half))
                out = out[0:8] + out[8:16] + out[16:24]
                if k == 8:
                    held = jnp.concatenate(
                        [
                            jnp.sum(middle[pl.ds(i * (PAIR // 2), patches), where], axis=0, keepdims=True)
                            for i in range(GROUP * 2)
                        ],
                        axis=0,
                    )
                    image_pool_out[:, where] = (
                        held * (1.0 / patches) + ivec_ref[:, pl.ds(7 * D + half * (D // 2), D // 2)] + out
                    )
                else:
                    image_pool_out[:, where] += out

    for s in range(count):
        for copy in own_shard(s):
            copy.start()
        if s == 1:
            for copy in firsts:
                copy.start()
    begin(0)
    for copy in tokens:
        copy.start()
    for copy in firsts:
        copy.wait()
    for s in range(1, AHEAD):
        begin(s)
    for step in range(count + AT_C):
        carry_on(step)
        s = step - AT_C
        if 0 <= s < PARTS:
            text_part(s)
        elif PARTS <= s:
            image_part(s)
    for copy in late:
        copy.wait()
    for s in range(PARTS):
        store(s).wait()
    for s in range(count):
        for j in range(2):
            for up in range(2):
                for hop in range(GROUP - 1):
                    unit = z_at - hop if up else z_at + hop
                    inside = (unit >= 0) & (unit < GROUP) & z_open[up]
                    pl.when(inside)(z_copy(s, up, unit, j).wait_send)
            for unit in range(GROUP):
                y_copy(s, 0, unit, j).wait_send()
        over_units(lambda unit: x_copy(s, unit).wait_send(), lambda: x_own_copy(s).wait_send())
        for j in range(3):
            c_copy(s, j).wait_send()


def gather_and_forward(n_dp, text_low, image_low, tokens, segments, pictures, text_vectors, image_vectors):
    own, columns = text_low.shape
    images, patches = pictures.shape[0], pictures.shape[1]
    n_inner = n_dp // GROUP
    lane_rows = own // LANES
    count = 2 * PARTS
    numbers = (segments + jnp.arange(segments.shape[0], dtype=jnp.int32)[:, None] * PER_ROW).reshape(-1)
    numbers = numbers.astype(jnp.bfloat16)
    padded = jnp.pad(pictures, ((0, 0), (0, PAIR // 2 - patches), (0, 0))).reshape(WORDS, D)
    hbm, vmem = pl.BlockSpec(memory_space=pltpu.HBM), pl.BlockSpec(memory_space=pltpu.VMEM)
    low, full = jnp.bfloat16, jnp.float32
    shape = jax.ShapeDtypeStruct
    gathered = shape((n_dp, LANES, lane_rows, columns), low)
    turned = shape((D // GROUP, WORDS), low)
    pairs = GROUP * HEADS // 2
    dma = pltpu.SemaphoreType.DMA
    outs = pl.pallas_call(
        functools.partial(forward_kernel, n_dp, patches),
        out_shape=(
            gathered, shape((PAIR, D), full), shape((8 * GROUP, D), full), shape((images, D), full),
            shape((GROUP, 8, PAIR), full), shape((GROUP, PAIR, D), low), shape((WORDS, 3 * D), low), shape((pairs, 2 * PAIR, PAIR), full),
            shape((WORDS, D), full), shape((WORDS, FF), full), shape((WORDS, FF), low), turned, turned, turned,
        ),
        in_specs=[hbm] * 5 + [vmem] * 3,
        out_specs=(hbm, hbm, vmem, vmem, vmem) + (hbm,) * 9,
        scratch_shapes=[
            pltpu.VMEM((PARTS, n_dp, LANES, lane_rows, PART), low),
            pltpu.VMEM((PARTS, n_dp, LANES, lane_rows, PART), low),
            pltpu.VMEM((GROUP, PAIR, D), low),
            pltpu.VMEM((GROUP, PAIR, PAIR), low),
            pltpu.VMEM((GROUP, 16, PAIR), low),
            pltpu.VMEM((WORDS, D), low),
            pltpu.VMEM((WORDS, 3 * D), low),
            pltpu.VMEM((WORDS, D), low),
            pltpu.VMEM((WORDS, D), full),
            pltpu.VMEM((WORDS, D), low),
            pltpu.VMEM((WORDS, FF), low),
            pltpu.VMEM((WORDS, FF), full),
            pltpu.VMEM((pairs, 2 * PAIR, PAIR), full),
            pltpu.VMEM((WORDS, D), full),
            pltpu.VMEM((WORDS, TILE), full),
            pltpu.VMEM((3, D, WORDS), low),
            pltpu.VMEM((24, FF), full),
            dma((count, 2, GROUP, 2)), dma((count, GROUP, 2)),
            dma((count, n_inner - 1, GROUP, 2)), dma((count, n_inner - 1, GROUP, 2)),
            dma((count, GROUP)), dma((count, GROUP)), dma((count, 3)), dma((count, 3)),
            dma((3, GROUP - 1)), dma((3, GROUP - 1)), dma((3,)), dma((count, 3)), dma((PARTS,)), dma((12,)),
        ],
        compiler_params=pltpu.CompilerParams(collective_id=5, has_side_effects=True, vmem_limit_bytes=60 << 20),
        name="gather_and_forward",
    )(
        text_low.reshape(LANES, lane_rows, columns), image_low.reshape(LANES, lane_rows, columns), tokens,
        jnp.broadcast_to(numbers[:, None], (PAIR, PAIR)), jnp.broadcast_to(numbers[None, :], (16, PAIR)), padded,
        text_vectors.reshape(1, -1), image_vectors.reshape(1, -1),
    )
    return (outs[0].reshape(D, columns),) + tuple(outs[1:])


def peer_at(offset, n_dp, n_rep):
    me = lax.axis_index("dp") * n_rep + lax.axis_index("rep")
    other = lax.rem(me + offset, n_dp * n_rep)
    return other, (other // n_rep, lax.rem(other, n_rep))


def meet(n_dp, n_rep):
    total = n_dp * n_rep
    barrier = pltpu.get_barrier_semaphore()

    def hello(offset, carry):
        _, peer = peer_at(offset, n_dp, n_rep)
        pl.semaphore_signal(barrier, inc=1, device_id=peer, device_id_type=MESH)
        return carry

    lax.fori_loop(1, total, hello, 0)
    pl.semaphore_wait(barrier, total - 1)


def spread_kernel(n_dp, n_rep, mine_ref, all_ref, send, recv, own_sem):
    total = n_dp * n_rep
    me = lax.axis_index("dp") * n_rep + lax.axis_index("rep")
    own = pltpu.make_async_copy(mine_ref, all_ref.at[me], own_sem)
    own.start()
    meet(n_dp, n_rep)

    def copy(offset):
        _, peer = peer_at(offset, n_dp, n_rep)
        return pltpu.make_async_remote_copy(
            src_ref=mine_ref, dst_ref=all_ref.at[me], send_sem=send.at[offset - 1],
            recv_sem=recv.at[offset - 1], device_id=peer, device_id_type=MESH,
        )

    def begin(offset, carry):
        copy(offset).start()
        return carry

    def finish(offset, carry):
        copy(offset).wait()
        return carry

    lax.fori_loop(1, total, begin, 0)
    own.wait()
    lax.fori_loop(1, total, finish, 0)


def spread(mine, n_dp, n_rep, collective, name):
    total = n_dp * n_rep
    vmem = pl.BlockSpec(memory_space=pltpu.VMEM)
    dma = pltpu.SemaphoreType.DMA
    return pl.pallas_call(
        functools.partial(spread_kernel, n_dp, n_rep),
        out_shape=jax.ShapeDtypeStruct((total,) + mine.shape, mine.dtype),
        in_specs=[vmem],
        out_specs=vmem,
        scratch_shapes=[dma((total - 1,)), dma((total - 1,)), dma],
        compiler_params=pltpu.CompilerParams(
            collective_id=collective, has_side_effects=True, vmem_limit_bytes=48 << 20
        ),
        name=name,
    )(mine)


def total_kernel(n_dp, n_rep, mine_ref, out_ref, parts, sums, send, recv, send_two, recv_two):
    total = n_dp * n_rep
    me = lax.axis_index("dp") * n_rep + lax.axis_index("rep")
    meet(n_dp, n_rep)

    def scatter(offset):
        other, peer = peer_at(offset, n_dp, n_rep)
        return pltpu.make_async_remote_copy(
            src_ref=mine_ref.at[other], dst_ref=parts.at[offset - 1], send_sem=send.at[offset - 1],
            recv_sem=recv.at[offset - 1], device_id=peer, device_id_type=MESH,
        )

    def share(offset):
        _, peer = peer_at(offset, n_dp, n_rep)
        return pltpu.make_async_remote_copy(
            src_ref=sums, dst_ref=out_ref.at[me], send_sem=send_two.at[offset - 1],
            recv_sem=recv_two.at[offset - 1], device_id=peer, device_id_type=MESH,
        )

    def start_scatter(offset, carry):
        scatter(offset).start()
        return carry

    def add(offset, carry):
        scatter(offset).wait_recv()
        return carry + parts[offset - 1]

    def start_share(offset, carry):
        share(offset).start()
        return carry

    def finish(offset, carry):
        scatter(offset).wait_send()
        share(offset).wait()
        return carry

    lax.fori_loop(1, total, start_scatter, 0)
    result = lax.fori_loop(1, total, add, mine_ref[me])
    sums[...] = result
    lax.fori_loop(1, total, start_share, 0)
    out_ref[me] = result
    lax.fori_loop(1, total, finish, 0)


def total_over_all(flat, n_dp, n_rep, collective, name):
    total = n_dp * n_rep
    count = flat.shape[0]
    chunk = -(-count // (total * 1024)) * 1024
    padded = jnp.pad(flat, (0, total * chunk - count)).reshape(total, chunk // 128, 128)
    vmem = pl.BlockSpec(memory_space=pltpu.VMEM)
    dma = pltpu.SemaphoreType.DMA
    summed = pl.pallas_call(
        functools.partial(total_kernel, n_dp, n_rep),
        out_shape=jax.ShapeDtypeStruct(padded.shape, padded.dtype),
        in_specs=[vmem],
        out_specs=vmem,
        scratch_shapes=[
            pltpu.VMEM((total - 1,) + padded.shape[1:], padded.dtype),
            pltpu.VMEM(padded.shape[1:], padded.dtype),
            dma((total - 1,)), dma((total - 1,)), dma((total - 1,)), dma((total - 1,)),
        ],
        compiler_params=pltpu.CompilerParams(
            collective_id=collective, has_side_effects=True, vmem_limit_bytes=48 << 20
        ),
        name=name,
    )(padded)
    return summed.reshape(-1)[:count]


def masked_scores(query_heads, key_heads, allowed):
    scores = (
        jnp.einsum("rshd,rthd->rhst", query_heads, key_heads, preferred_element_type=jnp.float32)
        * SCORE_SCALE
    )
    return jnp.where(allowed[:, None], scores, MASKED)


def block_forward(inputs, allowed, weights, vector_pieces, pooled_only):
    (
        gain_one, shift_one, bias_query, bias_value, bias_out,
        gain_two, shift_two, bias_shrink, bias_expand,
    ) = vector_pieces
    row_count, seq_tokens = (inputs.shape[0], inputs.shape[1])
    normed = layer_norm(inputs, gain_one, shift_one).astype(jnp.bfloat16)
    mixing = jnp.einsum("rsd,dc->rsc", normed, weights[:, : 3 * D], preferred_element_type=jnp.float32)
    mixing = mixing + jnp.concatenate([bias_query, jnp.zeros_like(bias_query), bias_value])
    head_parts = mixing.astype(jnp.bfloat16).reshape(row_count, seq_tokens, 3, HEADS, HEAD_DIM)
    query_heads, key_heads, value_heads = (head_parts[:, :, 0], head_parts[:, :, 1], head_parts[:, :, 2])
    scores = masked_scores(query_heads, key_heads, allowed)
    highest = jnp.max(scores, axis=-1, keepdims=True)
    log_total = highest + jnp.log(jnp.sum(jnp.exp(scores - highest), axis=-1, keepdims=True))
    attention = jnp.exp(scores - log_total).astype(jnp.bfloat16)
    mixed_heads = jnp.einsum("rhst,rthd->rshd", attention, value_heads, preferred_element_type=jnp.float32)
    mixed_heads = mixed_heads.reshape(row_count, seq_tokens, D).astype(jnp.bfloat16)
    attended = (
        jnp.einsum("rsd,de->rse", mixed_heads, weights[:, 3 * D : 4 * D], preferred_element_type=jnp.float32)
        + bias_out
    )
    middle = inputs + attended
    normed_two = layer_norm(middle, gain_two, shift_two).astype(jnp.bfloat16)
    hidden = (
        jnp.einsum("rsd,df->rsf", normed_two, weights[:, 4 * D : 4 * D + FF], preferred_element_type=jnp.float32)
        + bias_expand
    )
    active = jax.nn.gelu(hidden, approximate=False).astype(jnp.bfloat16)
    shrink = weights[:, 4 * D + FF :]
    if pooled_only:
        mean_active = jnp.mean(active.astype(jnp.float32), axis=1)
        high = mean_active.astype(jnp.bfloat16)
        rest = mean_active - high.astype(jnp.float32)
        low = rest.astype(jnp.bfloat16)
        lower = (rest - low.astype(jnp.float32)).astype(jnp.bfloat16)
        stacked = jnp.concatenate([high, low, lower], axis=0)
        shrunk = jnp.einsum("pf,df->pd", stacked, shrink, preferred_element_type=jnp.float32)
        shrunk = jnp.sum(shrunk.reshape(3, row_count, D), axis=0)
        return jnp.mean(middle, axis=1) + shrunk + bias_shrink
    shrunk = jnp.einsum("rsf,df->rsd", active, shrink, preferred_element_type=jnp.float32) + bias_shrink
    kept = (normed, query_heads, key_heads, value_heads, log_total, mixed_heads, middle, normed_two, hidden, active)
    return (middle + shrunk, kept)


def token_sum(values_low):
    return jnp.sum(values_low.astype(jnp.float32).reshape(-1, values_low.shape[-1]), axis=0)


def block_backward(inputs, allowed, weights, vector_pieces, forward_kept, grad_out, own_group, own_count):
    (gain_one, shift_one, _, _, _, gain_two, shift_two, _, _) = vector_pieces
    (normed, query_heads, key_heads, value_heads, log_total, mixed_heads, middle, normed_two, hidden, active) = forward_kept
    row_count, seq_tokens = (inputs.shape[0], inputs.shape[1])
    grad_shrunk = grad_out.astype(jnp.bfloat16)
    grad_active = jnp.einsum("rsd,df->rsf", grad_shrunk, weights[:, 4 * D + FF :], preferred_element_type=jnp.float32)
    _, gelu_back = jax.vjp(lambda before_gelu: jax.nn.gelu(before_gelu, approximate=False), hidden)
    grad_hidden = gelu_back(grad_active)[0].astype(jnp.bfloat16)
    grad_normed_two = jnp.einsum(
        "rsf,df->rsd", grad_hidden, weights[:, 4 * D : 4 * D + FF], preferred_element_type=jnp.float32
    )
    _, norm_two_back = jax.vjp(layer_norm, middle, gain_two, shift_two)
    grad_middle, grad_gain_two, grad_shift_two = norm_two_back(grad_normed_two)
    grad_middle = grad_middle + grad_out
    grad_attended = grad_middle.astype(jnp.bfloat16)
    grad_mixed = jnp.einsum("rse,de->rsd", grad_attended, weights[:, 3 * D : 4 * D], preferred_element_type=jnp.float32)
    grad_mixed = grad_mixed.astype(jnp.bfloat16).reshape(row_count, seq_tokens, HEADS, HEAD_DIM)
    attention = jnp.exp(masked_scores(query_heads, key_heads, allowed) - log_total)
    grad_values = jnp.einsum("rhst,rshd->rthd", attention.astype(jnp.bfloat16), grad_mixed, preferred_element_type=jnp.float32)
    grad_attention = jnp.einsum("rshd,rthd->rhst", grad_mixed, value_heads, preferred_element_type=jnp.float32)
    grad_scores = attention * (grad_attention - jnp.sum(attention * grad_attention, axis=-1, keepdims=True))
    grad_scores = grad_scores.astype(jnp.bfloat16)
    grad_query = jnp.einsum("rhst,rthd->rshd", grad_scores, key_heads, preferred_element_type=jnp.float32) * SCORE_SCALE
    grad_keys = jnp.einsum("rhst,rshd->rthd", grad_scores, query_heads, preferred_element_type=jnp.float32) * SCORE_SCALE
    grad_mixing = (
        jnp.stack([grad_query, grad_keys, grad_values], axis=2).reshape(row_count, seq_tokens, 3 * D).astype(jnp.bfloat16)
    )

    def mine(values):
        return lax.dynamic_slice_in_dim(values, own_group * own_count, own_count, 0)

    grad_normed = jnp.einsum("rsc,dc->rsd", mine(grad_mixing), weights[:, : 3 * D], preferred_element_type=jnp.float32)
    _, norm_one_back = jax.vjp(layer_norm, mine(inputs), gain_one, shift_one)
    grad_inputs, grad_gain_one, grad_shift_one = norm_one_back(grad_normed)
    grad_inputs = grad_inputs + mine(grad_middle)
    share = 1.0 / GROUP
    vector_grad = jnp.concatenate(
        [
            grad_gain_one, grad_shift_one,
            share * token_sum(grad_mixing[..., :D]), share * token_sum(grad_mixing[..., 2 * D :]),
            share * token_sum(grad_attended), share * grad_gain_two, share * grad_shift_two,
            share * token_sum(grad_shrunk), share * token_sum(grad_hidden),
        ]
    )
    tokens = row_count * seq_tokens
    outer_terms = (
        (normed.reshape(tokens, D), grad_mixing.reshape(tokens, 3 * D)),
        (mixed_heads.reshape(tokens, D), grad_attended.reshape(tokens, D)),
        (normed_two.reshape(tokens, D), grad_hidden.reshape(tokens, FF)),
        (grad_shrunk.reshape(tokens, D), active.reshape(tokens, FF)),
    )
    return (grad_inputs, vector_grad, outer_terms)


def orthonormal(stacked):
    waiting = [stacked[:, column_id] for column_id in range(stacked.shape[1])]
    finished = []
    while waiting:
        vector = waiting.pop(0)
        vector = vector / (jnp.sqrt(jnp.sum(vector * vector, axis=-1, keepdims=True)) + NORM_FLOOR)
        finished.append(vector)
        if waiting:
            later = jnp.stack(waiting, axis=1)
            later = later - jnp.sum(vector[:, None] * later, axis=-1, keepdims=True) * vector[:, None]
            waiting = [later[:, i] for i in range(later.shape[1])]
    return jnp.stack(finished, axis=1)


def rows_factor(start_part, row_block):
    return jnp.einsum("kc,dc->kd", start_part, row_block, precision=PRECISE)


def per_device(
    image_tokens, image_weights, image_vectors, text_tokens, segments, text_weights,
    text_vectors, momentum, vector_momentum, error_feedback, start_factors,
):
    n_rep, n_dp = lax.axis_size("rep"), lax.axis_size("dp")
    n_inner = n_dp // GROUP
    total = n_rep * n_dp
    device_pairs, patches = image_tokens.shape[0], image_tokens.shape[1]
    text_rows, seq_tokens = text_tokens.shape[0], text_tokens.shape[1]
    pair_total = device_pairs * total
    own_rows = text_weights.shape[0]
    d_at, r_at = lax.axis_index("dp"), lax.axis_index("rep")
    z_at, y_at = d_at // n_inner, d_at % n_inner
    row_start = d_at * own_rows
    factor_rank = start_factors.shape[0]
    bounds = matrix_bounds()
    fused = own_rows % (16 * LANES) == 0 and n_inner == 2
    tokens = text_tokens.reshape(text_rows * seq_tokens, D)
    if fused:
        outs = gather_and_forward(
            n_dp, text_weights.astype(jnp.bfloat16), image_weights, tokens, segments, image_tokens,
            text_vectors, image_vectors,
        )
        text_low, image_pooled, marks, token_group = outs[0], outs[3], outs[4], outs[5]
        numbers = jnp.einsum("gct,c->gt", marks, jnp.arange(8, dtype=jnp.float32), precision=PRECISE)
        segment_group = numbers.astype(jnp.int32) % PER_ROW
    else:
        text_low, frozen, token_group, segment_group = gather_weights(
            n_dp, text_weights.astype(jnp.bfloat16), image_weights, tokens, segments
        )
        text_low, frozen = text_low.reshape(D, -1), frozen.reshape(D, -1)
        full_mask = jnp.zeros((device_pairs, patches, patches), jnp.int32) == 0
        image_pooled = block_forward(
            image_tokens.astype(jnp.float32), full_mask, frozen, vector_parts(image_vectors), True
        )
    image_emb = unit_rows(image_pooled).astype(jnp.bfloat16)

    group_rows = GROUP * text_rows
    text_float = token_group.reshape(group_rows, seq_tokens, D).astype(jnp.float32)
    segment_all = segment_group.reshape(group_rows, seq_tokens)
    allowed = segment_all[:, :, None] == segment_all[:, None, :]
    vector_pieces = vector_parts(text_vectors)
    group_output, forward_kept = block_forward(text_float, allowed, text_low, vector_pieces, False)
    text_output = lax.dynamic_slice_in_dim(group_output, z_at * text_rows, text_rows, 0)
    caption_marks = (
        segment_all[:, None, :] == jnp.arange(PER_ROW, dtype=jnp.int32)[None, :, None]
    ).astype(jnp.float32)
    counts = jnp.sum(caption_marks, axis=-1, keepdims=True)
    pooled = (jnp.einsum("rks,rsd->rkd", caption_marks, group_output, precision=PRECISE) / counts).reshape(-1, D)
    text_norm, embed_back = jax.vjp(unit_rows, pooled)
    text_emb = text_norm.astype(jnp.bfloat16)
    own_emb = lax.dynamic_slice_in_dim(text_emb, z_at * device_pairs, device_pairs, 0)
    embeddings = spread(jnp.concatenate([image_emb, own_emb], axis=0), n_dp, n_rep, 2, "spread_embeddings")
    image_all = embeddings[:, :device_pairs].reshape(pair_total, D)
    text_all = embeddings[:, device_pairs:].reshape(pair_total, D)
    own_pairs = (
        ((jnp.arange(GROUP, dtype=jnp.int32) * n_inner + y_at) * n_rep + r_at)[:, None] * device_pairs
        + jnp.arange(device_pairs, dtype=jnp.int32)[None, :]
    ).reshape(-1)
    logits = LOGIT_SCALE * jnp.einsum("pd,bd->pb", image_all, text_all, preferred_element_type=jnp.float32)
    image_top = jnp.max(logits, axis=1)
    image_log_total = image_top + jnp.log(jnp.sum(jnp.exp(logits - image_top[:, None]), axis=1))
    caption_top = jnp.max(logits, axis=0)
    caption_log_total = caption_top + jnp.log(jnp.sum(jnp.exp(logits - caption_top[None, :]), axis=0))
    pair_ids = jnp.arange(pair_total, dtype=jnp.int32)
    matched = jnp.sum(jnp.where(pair_ids[:, None] == pair_ids[None, :], logits, 0.0), axis=1)
    loss_total = (jnp.sum(image_log_total - matched) + jnp.sum(caption_log_total - matched)) / (2.0 * pair_total)
    diagonal_pick = (pair_ids[None, :] == own_pairs[:, None]).astype(jnp.float32)
    text_logits = LOGIT_SCALE * jnp.einsum("pd,bd->pb", text_emb, image_all, preferred_element_type=jnp.float32)
    text_top = jnp.max(text_logits, axis=1, keepdims=True)
    text_log_total = text_top + jnp.log(jnp.sum(jnp.exp(text_logits - text_top), axis=1, keepdims=True))
    text_soft = ((jnp.exp(text_logits - text_log_total) - diagonal_pick) * 0.5).astype(jnp.bfloat16)
    column_soft = ((jnp.exp(text_logits - image_log_total[None, :]) - diagonal_pick) * 0.5).astype(jnp.bfloat16)
    grad_text = LOGIT_SCALE * (
        jnp.einsum("pb,bd->pd", text_soft, image_all, preferred_element_type=jnp.float32)
        + jnp.einsum("pb,bd->pd", column_soft, image_all, preferred_element_type=jnp.float32)
    )
    grad_pooled = embed_back(grad_text)[0].reshape(-1, PER_ROW, D) / counts
    grad_out = jnp.einsum("rks,rkd->rsd", caption_marks, grad_pooled, precision=PRECISE)
    grad_inputs, vector_grad, outer_terms = block_backward(
        text_float, allowed, text_low, vector_pieces, forward_kept, grad_out, z_at, text_rows
    )
    group_width = n_inner * own_rows
    worker_blocks = []
    feedback_rows = error_feedback[0]
    for (left_side, right_side), (first_col, after_col) in zip(outer_terms, bounds):
        left_cut = lax.dynamic_slice_in_dim(left_side, z_at * group_width, group_width, 1)
        block = jnp.einsum("tc,tk->ck", left_cut, right_side, preferred_element_type=jnp.float32)
        mine = lax.dynamic_slice_in_dim(block, y_at * own_rows, own_rows, 0)
        for k in range(1, n_inner):
            target = lax.rem(y_at + k, n_inner)
            outgoing = lax.dynamic_slice_in_dim(block, target * own_rows, own_rows, 0).astype(jnp.bfloat16)
            pairs = [
                (z * n_inner + y, z * n_inner + (y + k) % n_inner) for z in range(GROUP) for y in range(n_inner)
            ]
            mine = mine + lax.ppermute(outgoing, "dp", pairs).astype(jnp.float32)
        worker_blocks.append(mine + feedback_rows[:, first_col:after_col])
    factor_rows = jnp.concatenate(
        [
            rows_factor(start_factors[:, first_col:after_col], rows)
            for rows, (first_col, after_col) in zip(worker_blocks, bounds)
        ],
        axis=0,
    )
    gathered_rows = spread(factor_rows, n_dp, n_rep, 3, "spread_factors")
    factor = jnp.sum(gathered_rows.reshape(n_dp, n_rep, 4 * factor_rank, own_rows), axis=1)
    factor = jnp.swapaxes(factor, 0, 1).reshape(4, factor_rank, D)
    left_basis = orthonormal(factor).reshape(4 * factor_rank, D)
    basis_rows = lax.dynamic_slice_in_dim(left_basis, row_start, own_rows, 1)
    basis_parts = [basis_rows[i * factor_rank : (i + 1) * factor_rank] for i in range(4)]
    right_part = jnp.concatenate(
        [jnp.einsum("kd,dc->kc", part, rows, precision=PRECISE) for part, rows in zip(basis_parts, worker_blocks)],
        axis=1,
    )
    summed = total_over_all(
        jnp.concatenate([right_part.reshape(-1), vector_grad]), n_dp, n_rep, 4, "total_right"
    )
    new_right = summed[: right_part.size].reshape(right_part.shape)
    vector_total = summed[right_part.size :]
    approximation = jnp.concatenate(
        [
            jnp.einsum("kd,kc->dc", part, new_right[:, first_col:after_col], precision=PRECISE)
            for part, (first_col, after_col) in zip(basis_parts, bounds)
        ],
        axis=1,
    )
    worker_rows = jnp.concatenate(worker_blocks, axis=1)
    new_feedback = (worker_rows - approximation / n_rep)[None]
    new_momentum = MOMENTUM_DECAY * momentum + approximation
    new_weights = text_weights - STEP_RATE * new_momentum
    new_vector_momentum = MOMENTUM_DECAY * vector_momentum + vector_total
    new_vectors = text_vectors - STEP_RATE * new_vector_momentum
    return (
        loss_total, text_output, grad_inputs, new_weights, new_momentum, new_feedback,
        new_vectors, new_vector_momentum, left_basis, new_right,
    )


def solution(mesh):
    placed = (
        P(("dp", "rep"), None, None), P("dp", None), P(), P(("dp", "rep"), None, None), P(("dp", "rep"), None),
        P("dp", None), P(), P("dp", None), P(), P("rep", "dp", None), P(),
    )
    return jax.shard_map(
        per_device,
        mesh=mesh,
        in_specs=placed,
        out_specs=(
            P(), P(("dp", "rep"), None, None), P(("dp", "rep"), None, None), P("dp", None), P("dp", None),
            P("rep", "dp", None), P(), P(), P(), P(),
        ),
        check_vma=False,
    )
```

```python
import functools

import jax
import jax.numpy as jnp
from jax import lax
from jax.experimental import pallas as pl
from jax.experimental.pallas import tpu as pltpu
from jax.sharding import PartitionSpec as P

D = 768
FF = 3072
HEADS = 12
HEAD_DIM = 64
PER_ROW = 4
GROUP = 4
SECTION = 3072
LANE_COLS = 512

PRECISE = lax.Precision.HIGHEST
LAYER_EPS = 1e-06
SCORE_SCALE = 0.125
LOGIT_SCALE = 50.0
MOMENTUM_DECAY = 0.9
STEP_RATE = 0.08
NORM_FLOOR = 1e-08
MASKED = -1e30
MESH = pl.DeviceIdType.MESH


def layer_norm(values, layer_gain, layer_shift):
    center = values - jnp.mean(values, axis=-1, keepdims=True)
    spread = jnp.mean(center * center, axis=-1, keepdims=True)
    return center * lax.rsqrt(spread + LAYER_EPS) * layer_gain + layer_shift


def unit_rows(values):
    return values * lax.rsqrt(jnp.sum(values * values, axis=-1, keepdims=True) + LAYER_EPS)


def vector_parts(vectors):
    pieces = [vectors[position * D : (position + 1) * D] for position in range(8)]
    return pieces + [vectors[8 * D :]]


def matrix_bounds():
    return ((0, 3 * D), (3 * D, 4 * D), (4 * D, 4 * D + FF), (4 * D + FF, 4 * D + 2 * FF))


def gather_kernel(
    n_dp, text_ref, image_ref, tok_ref, seg_ref, wt_ref, wi_ref, tok_out, seg_out,
    z_send, z_recv, y_send, y_recv, x_send, x_recv, c_send, c_recv, t_send, t_recv, t_own, own_sem,
):
    n_inner = n_dp // GROUP
    d_at, r_at = lax.axis_index("dp"), lax.axis_index("rep")
    z_at, y_at = d_at // n_inner, d_at % n_inner
    x_at, c_at = r_at // 2, r_at % 2
    z_peers = [(lax.rem(z_at + k, GROUP) * n_inner + y_at, r_at) for k in range(1, GROUP)]
    z_from = [lax.rem(z_at + GROUP - k, GROUP) for k in range(1, GROUP)]
    y_peers = [(z_at * n_inner + lax.rem(y_at + k, n_inner), r_at) for k in range(1, n_inner)]
    y_from = [lax.rem(y_at + n_inner - k, n_inner) for k in range(1, n_inner)]
    x_peer = (d_at, (1 - x_at) * 2 + c_at)
    c_peer = (d_at, x_at * 2 + 1 - c_at)

    barrier = pltpu.get_barrier_semaphore()
    everyone = z_peers + y_peers + [x_peer, c_peer]
    for peer in everyone:
        pl.semaphore_signal(barrier, inc=1, device_id=peer, device_id_type=MESH)
    pl.semaphore_wait(barrier, len(everyone))

    def shard_of(z, y):
        return z * n_inner + y

    sections = [(image_ref, wi_ref, 0), (text_ref, wt_ref, 0), (image_ref, wi_ref, 1),
                (text_ref, wt_ref, 1), (image_ref, wi_ref, 2), (text_ref, wt_ref, 2)]

    def cols(section, lane):
        start = sections[section][2] * SECTION + lane * LANE_COLS
        return pl.ds(pl.multiple_of(start, 128), LANE_COLS)

    lane_both = c_at
    lane_mine = 2 + x_at * 2 + c_at
    lane_theirs = 2 + (1 - x_at) * 2 + c_at
    lanes = (lane_both, lane_mine)

    locals_ = [
        pltpu.make_async_copy(tok_ref, tok_out.at[z_at], t_own.at[0]),
        pltpu.make_async_copy(seg_ref, seg_out.at[z_at], t_own.at[1]),
    ]
    for s, (src, full, _) in enumerate(sections):
        for j in range(2):
            column = cols(s, lanes[j])
            locals_.append(pltpu.make_async_copy(src.at[:, column], full.at[d_at, :, column], own_sem.at[s, j]))
    for copy in locals_:
        copy.start()

    def remote(src, dst, send, recv, peer):
        return pltpu.make_async_remote_copy(
            src_ref=src, dst_ref=dst, send_sem=send, recv_sem=recv, device_id=peer, device_id_type=MESH
        )

    def z_copy(s, k, j):
        src, full, _ = sections[s]
        return remote(
            src.at[:, cols(s, lanes[j])], full.at[d_at, :, cols(s, lanes[j])],
            z_send.at[s, k, j], z_recv.at[s, k, j], z_peers[k],
        )

    def y_copy(s, q, zi, j):
        src, full, _ = sections[s]
        column = cols(s, lanes[j])
        if zi == 0:
            shard, source = d_at, src.at[:, column]
        else:
            shard = shard_of(z_from[zi - 1], y_at)
            source = full.at[shard, :, column]
        return remote(source, full.at[shard, :, column], y_send.at[s, q, zi, j], y_recv.at[s, q, zi, j], y_peers[q])

    def x_copy(s):
        full = sections[s][1]
        block = full.at[:, :, cols(s, lane_mine)]
        return remote(block, block, x_send.at[s], x_recv.at[s], x_peer)

    def c_copy(s, j):
        full = sections[s][1]
        block = full.at[:, :, cols(s, (lane_both, lane_mine, lane_theirs)[j])]
        return remote(block, block, c_send.at[s, j], c_recv.at[s, j], c_peer)

    count = len(sections)
    tokens = []
    for k in range(GROUP - 1):
        tokens.append(remote(tok_ref, tok_out.at[z_at], t_send.at[0, k], t_recv.at[0, k], z_peers[k]))
        tokens.append(remote(seg_ref, seg_out.at[z_at], t_send.at[1, k], t_recv.at[1, k], z_peers[k]))

    def begin(s):
        for j in range(2):
            for k in range(GROUP - 1):
                z_copy(s, k, j).start()
            for q in range(n_inner - 1):
                y_copy(s, q, 0, j).start()

    begin(0)
    for copy in tokens:
        copy.start()
    for copy in locals_:
        copy.wait()
    begin(1)
    for step in range(count + 3):
        if step < count:
            for k in range(GROUP - 1):
                for j in range(2):
                    z_copy(step, k, j).wait_recv()
                    for q in range(n_inner - 1):
                        y_copy(step, q, k + 1, j).start()
            if step + 2 < count:
                begin(step + 2)
        s = step - 1
        if 0 <= s < count:
            for q in range(n_inner - 1):
                for zi in range(GROUP):
                    for j in range(2):
                        y_copy(s, q, zi, j).wait_recv()
            x_copy(s).start()
            for j in range(2):
                c_copy(s, j).start()
        s = step - 2
        if 0 <= s < count:
            x_copy(s).wait_recv()
            c_copy(s, 2).start()
        s = step - 3
        if 0 <= s < count:
            for j in range(3):
                c_copy(s, j).wait_recv()
    for copy in tokens:
        copy.wait()
    for s in range(count):
        for j in range(2):
            for k in range(GROUP - 1):
                z_copy(s, k, j).wait_send()
            for q in range(n_inner - 1):
                for zi in range(GROUP):
                    y_copy(s, q, zi, j).wait_send()
        x_copy(s).wait_send()
        for j in range(3):
            c_copy(s, j).wait_send()


def gather_weights(n_dp, text_low, image_low, tokens, segments):
    n_inner = n_dp // GROUP
    full = jax.ShapeDtypeStruct((n_dp,) + text_low.shape, jnp.bfloat16)
    hbm = pl.BlockSpec(memory_space=pltpu.HBM)
    dma = pltpu.SemaphoreType.DMA
    return pl.pallas_call(
        functools.partial(gather_kernel, n_dp),
        out_shape=(
            full,
            full,
            jax.ShapeDtypeStruct((GROUP,) + tokens.shape, jnp.bfloat16),
            jax.ShapeDtypeStruct((GROUP,) + segments.shape, jnp.int32),
        ),
        in_specs=[hbm] * 4,
        out_specs=(hbm,) * 4,
        scratch_shapes=[
            dma((6, GROUP - 1, 2)), dma((6, GROUP - 1, 2)),
            dma((6, n_inner - 1, GROUP, 2)), dma((6, n_inner - 1, GROUP, 2)),
            dma((6,)), dma((6,)), dma((6, 3)), dma((6, 3)),
            dma((2, GROUP - 1)), dma((2, GROUP - 1)), dma((2,)), dma((6, 2)),
        ],
        compiler_params=pltpu.CompilerParams(collective_id=1, has_side_effects=True),
        name="gather_weights",
    )(text_low, image_low, tokens, segments)


TILE = 256
PAIR = 128
ROWS = 32
LANES = 6
PART = 768
PARTS = 12
DEPTH = 8
AHEAD = 2
LAG_Z = 1
LAG_Y = 1
LAG_X = 1
LAG_C = 1
AT_Y = 2 * LAG_Z + LAG_Y
AT_X = AT_Y + LAG_X
AT_C = AT_X + LAG_C
WORDS = (GROUP * PAIR)


def piece_of(vec_ref, index, width=D):
    return vec_ref[:, pl.ds(index * D, width)]


def loop(count, body, unroll=1):
    def step(i, carry):
        body(i)
        return carry

    lax.fori_loop(0, count, step, 0, unroll=unroll)


def aligned(i, size):
    return pl.ds(pl.multiple_of(i * size, size), size)


def norm_rows(values):
    center = values - jnp.mean(values, axis=-1, keepdims=True)
    spread_ = jnp.mean(center * center, axis=-1, keepdims=True)
    return center * lax.rsqrt(spread_ + LAYER_EPS)


def dot(left, right):
    return jnp.dot(left, right, preferred_element_type=jnp.float32)


def dot_nt(left, right):
    return lax.dot_general(left, right, (((1,), (1,)), ((), ())), preferred_element_type=jnp.float32)


def dot_tn(left, right):
    return lax.dot_general(left, right, (((0,), (0,)), ((), ())), preferred_element_type=jnp.float32)


def lane_is_first():
    return lax.broadcasted_iota(jnp.int32, (PAIR, PAIR), 1) < HEAD_DIM


def two_heads(block):
    first = lane_is_first()
    zero = jnp.zeros_like(block)
    return jnp.concatenate([jnp.where(first, block, zero), jnp.where(first, zero, block)], axis=0)


def attention_forward(qkv, mixed, chance, allowed_of):
    pairs = HEADS // 2

    def body(at):
        i, j = at // pairs, lax.rem(at, pairs)
        rows = aligned(i, PAIR)
        query = qkv[rows, aligned(j, PAIR)]
        key = qkv[rows, pl.ds(pl.multiple_of(D + j * PAIR, PAIR), PAIR)]
        value = qkv[rows, pl.ds(pl.multiple_of(2 * D + j * PAIR, PAIR), PAIR)]
        scores = dot_nt(two_heads(query), key) * SCORE_SCALE
        allowed = allowed_of(i)
        scores = jnp.where(jnp.concatenate([allowed, allowed], axis=0), scores, MASKED)
        scores = jnp.exp(scores - jnp.max(scores, axis=-1, keepdims=True))
        weight = scores / jnp.sum(scores, axis=-1, keepdims=True)
        if chance is not None:
            chance[at] = weight
        low = weight.astype(jnp.bfloat16)
        side = jnp.concatenate([low[:PAIR], low[PAIR:]], axis=1)
        mixed[rows, aligned(j, PAIR)] = dot(side, two_heads(value)).astype(jnp.bfloat16)

    loop(GROUP * pairs, body, unroll=2)


def forward_kernel(
    n_dp, patches,
    text_ref, image_ref, tok_ref, col_ref, row_ref, pic_ref, tvec_ref, ivec_ref,
    wt_out, words_out, text_pool_out, image_pool_out, marks_out, qkv_out, chance_out, mid_out, slope_out,
    act_out, nt_out, at_out, mt_out,
    wi_ref, wt_vmem, tok, seg_col, seg_row, normed, qkv, mixed, middle, normed_two, active, slope, chance, total, hid, turned, apool,
    z_send, z_recv, y_send, y_recv, x_send, x_recv, c_send, c_recv, t_send, t_recv, t_own, own_sem, w_sem, out_sem,
):
    n_inner = n_dp // GROUP
    d_at, r_at = lax.axis_index("dp"), lax.axis_index("rep")
    z_at, y_at = d_at // n_inner, lax.rem(d_at, n_inner)
    x_at, c_at = r_at // 2, lax.rem(r_at, 2)
    z_peers = [(lax.rem(z_at + k, GROUP) * n_inner + y_at, r_at) for k in range(1, GROUP)]
    z_next = [((z_at - 1) * n_inner + y_at, r_at), ((z_at + 1) * n_inner + y_at, r_at)]
    y_peers = [(z_at * n_inner + 1 - y_at, r_at)]
    x_peer = (d_at, (1 - x_at) * 2 + c_at)
    c_peer = (d_at, x_at * 2 + 1 - c_at)

    barrier = pltpu.get_barrier_semaphore()
    everyone = z_peers + y_peers + [x_peer, c_peer]
    for peer in everyone:
        pl.semaphore_signal(barrier, inc=1, device_id=peer, device_id_type=MESH)
    pl.semaphore_wait(barrier, len(everyone))

    sections = [(text_ref, wt_vmem, k) for k in range(PARTS)] + [(image_ref, wi_ref, k) for k in range(PARTS)]
    count = len(sections)
    lane_both = c_at
    lane_mine = 2 + x_at * 2 + c_at
    lane_theirs = 2 + (1 - x_at) * 2 + c_at
    lanes = (lane_both, lane_mine)

    def remote(src, dst, send, recv, peer):
        return pltpu.make_async_remote_copy(
            src_ref=src, dst_ref=dst, send_sem=send, recv_sem=recv, device_id=peer, device_id_type=MESH
        )

    def cols(s):
        return pl.ds(sections[s][2] * PART, PART)

    def held(s, shard, lane):
        _, full, k = sections[s]
        return full.at[k, shard, lane]

    def z_copy(s, up, unit, j):
        shard = unit * n_inner + y_at
        return remote(
            held(s, shard, lanes[j]), held(s, shard, lanes[j]),
            z_send.at[s, up, unit, j], z_recv.at[s, unit, j], z_next[up],
        )

    def y_copy(s, q, unit, j):
        shard = unit * n_inner + y_at
        return remote(
            held(s, shard, lanes[j]), held(s, shard, lanes[j]),
            y_send.at[s, q, unit, j], y_recv.at[s, q, unit, j], y_peers[q],
        )

    def x_copy(s, unit):
        block = held(s, pl.ds(unit * n_inner, n_inner), lane_mine)
        return remote(block, block, x_send.at[s, unit], x_recv.at[s, unit], x_peer)

    def x_own_copy(s):
        block = held(s, z_at * n_inner + 1 - y_at, lane_mine)
        return remote(block, block, x_send.at[s, z_at], x_recv.at[s, z_at], x_peer)

    def c_copy(s, j):
        block = held(s, slice(None), (lane_both, lane_mine, lane_theirs)[j])
        return remote(block, block, c_send.at[s, j], c_recv.at[s, j], c_peer)

    def store(s):
        return pltpu.make_async_copy(wt_vmem.at[s], wt_out.at[s], w_sem.at[s])

    firsts = [
        pltpu.make_async_copy(tok_ref, tok.at[z_at], t_own.at[0]),
        pltpu.make_async_copy(col_ref, seg_col.at[z_at], t_own.at[1]),
        pltpu.make_async_copy(row_ref, seg_row.at[z_at], t_own.at[2]),
    ]
    z_open = (z_at > 0, z_at < GROUP - 1)

    def own_shard(s):
        src, _, _ = sections[s]
        return [
            pltpu.make_async_copy(src.at[lane, :, cols(s)], held(s, d_at, lane), own_sem.at[s, j])
            for j, lane in enumerate((lane_both, lane_mine, lane_theirs))
        ]

    tokens = []
    for k in range(GROUP - 1):
        for which, (src, dst) in enumerate(((tok_ref, tok), (col_ref, seg_col), (row_ref, seg_row))):
            tokens.append(remote(src, dst.at[z_at], t_send.at[which, k], t_recv.at[which, k], z_peers[k]))

    def begin(s):
        for copy in own_shard(s):
            copy.wait()
        for j in range(2):
            for up in range(2):
                pl.when(z_open[up])(z_copy(s, up, z_at, j).start)
            y_copy(s, 0, z_at, j).start()

    def arrive(s, hop):
        for up in range(2):
            unit = z_at - hop if up else z_at + hop

            @pl.when((unit >= 0) & (unit < GROUP))
            def _():
                for j in range(2):
                    z_copy(s, up, unit, j).wait_recv()
                    pl.when(z_open[up])(z_copy(s, up, unit, j).start)
                    y_copy(s, 0, unit, j).start()

    def over_units(unit_fn, own_fn):
        for unit in range(GROUP):
            pl.when(unit != z_at)(functools.partial(unit_fn, unit))
        own_fn()

    def carry_on(step):
        if step + AHEAD < count:
            begin(step + AHEAD)
        for hop in range(1, GROUP):
            s = step - (hop - 1) * LAG_Z
            if 0 <= s < count:
                arrive(s, hop)
        s = step - AT_Y
        if 0 <= s < count:
            for unit in range(GROUP):
                for j in range(2):
                    y_copy(s, 0, unit, j).wait_recv()
            over_units(lambda unit: x_copy(s, unit).start(), lambda: x_own_copy(s).start())
            for j in range(2):
                c_copy(s, j).start()
        s = step - AT_X
        if 0 <= s < count:
            over_units(lambda unit: x_copy(s, unit).wait_recv(), lambda: x_own_copy(s).wait_recv())
            c_copy(s, 2).start()
        s = step - AT_C
        if 0 <= s < count:
            for j in range(3):
                c_copy(s, j).wait_recv()
            if s < PARTS:
                store(s).start()


    def weight_tile(s, c):
        _, full, k = sections[s]
        return full[k, :, :, :, aligned(c, TILE)].reshape(D, TILE)

    def weight_rows(s, half):
        _, full, k = sections[s]
        return full[k, pl.ds(half * (n_dp // 2), n_dp // 2)].reshape(D // 2, PART)

    def first_norm(read, vec):
        def body(i):
            rows = aligned(i, ROWS)
            value = norm_rows(read(i).astype(jnp.float32))
            normed[rows, :] = (value * piece_of(vec, 0) + piece_of(vec, 1)).astype(jnp.bfloat16)

        loop(WORDS // ROWS, body)

    def project(slot, part, bias):
        def body(c):
            out = dot(normed[...], weight_tile(slot, c))
            if bias is not None:
                out = out + bias[0][:, pl.ds(pl.multiple_of(bias[1] * D + c * TILE, TILE), TILE)]
            qkv[:, pl.ds(pl.multiple_of(part * D + c * TILE, TILE), TILE)] = out.astype(jnp.bfloat16)

        loop(PART // TILE, body)

    def attend(slot, read, vec):
        def body(c):
            where = aligned(c, TILE)
            middle[:, where] = dot(mixed[...], weight_tile(slot, c)) + vec[
                :, pl.ds(pl.multiple_of(4 * D + c * TILE, TILE), TILE)
            ]

        loop(PART // TILE, body)

        def norm(i):
            rows = aligned(i, ROWS)
            value = middle[rows, :] + read(i).astype(jnp.float32)
            middle[rows, :] = value
            normed_two[rows, :] = (norm_rows(value) * piece_of(vec, 5) + piece_of(vec, 6)).astype(jnp.bfloat16)

        loop(WORDS // ROWS, norm)

    def expand(slot, part, vec, keep):
        def body(c):
            start = pl.multiple_of(part * PART + c * TILE, TILE)
            hid[...] = dot(normed_two[...], weight_tile(slot, c)) + vec[:, pl.ds(pl.multiple_of(8 * D + start, TILE), TILE)]

            def inner(i):
                rows = aligned(i, ROWS)
                value = hid[rows, :]
                phi = 0.5 + 0.5 * lax.erf(value * 0.7071067811865476)
                active[rows, pl.ds(start, TILE)] = (value * phi).astype(jnp.bfloat16)
                if keep:
                    slope[rows, pl.ds(start, TILE)] = phi + value * (
                        0.3989422804014327 * jnp.exp(-0.5 * value * value)
                    )

            loop(WORDS // ROWS, inner, unroll=2)

        loop(PART // TILE, body)

    def shrink(slot, part, vec):
        for half in range(2):
            where = pl.ds(half * (D // 2), D // 2)
            out = dot_nt(active[:, pl.ds(part * PART, PART)], weight_rows(slot, half))
            if part == 0:
                total[:, where] = out + middle[:, where] + vec[:, pl.ds(7 * D + half * (D // 2), D // 2)]
            else:
                total[:, where] += out

    def turn(source, slot, out):
        def body(c):
            turned[slot, aligned(c, PAIR), :] = source[:, aligned(c, PAIR)].T

        loop(D // PAIR, body)
        send_out(turned.at[slot, group_rows], out)

    outs, late = [], []

    def send_out(src, dst, kept=outs):
        copy = pltpu.make_async_copy(src, dst, out_sem.at[len(outs) + len(late)])
        copy.start()
        kept.append(copy)

    group_rows = pl.ds(pl.multiple_of(z_at * (D // GROUP), D // GROUP), D // GROUP)

    def text_read(i):
        per = PAIR // ROWS
        return tok[i // per, aligned(lax.rem(i, per), ROWS), :]

    def text_allowed(i):
        col = seg_col[i].astype(jnp.float32)
        row = seg_row[i].astype(jnp.float32)
        return col == row[0:1, :]

    def image_read(i):
        return pic_ref[aligned(i, ROWS), :]

    def picture(axis):
        at = lax.broadcasted_iota(jnp.int32, (PAIR, PAIR), axis)
        number = at // (PAIR // 2)
        return jnp.where(lax.rem(at, PAIR // 2) < patches, number, number + 2)

    def image_allowed(i):
        return picture(0) == picture(1)

    def keep_mark():
        image = lax.broadcasted_iota(jnp.int32, (GROUP * 2, WORDS), 0)
        at = lax.broadcasted_iota(jnp.int32, (GROUP * 2, WORDS), 1)
        inside = (at // (PAIR // 2) == image) & (lax.rem(at, PAIR // 2) < patches)
        return jnp.where(inside, 1.0, 0.0)

    def text_part(s):
        slot = s
        if s == 0:
            for copy in tokens:
                copy.wait()
            first_norm(text_read, tvec_ref)
            project(slot, 0, (tvec_ref, 2))
            turn(normed, 0, nt_out)
        elif s == 1:
            project(slot, 1, None)
        elif s == 2:
            project(slot, 2, (tvec_ref, 3))
            send_out(qkv, qkv_out)
            attention_forward(qkv, mixed, chance, text_allowed)
            send_out(chance, chance_out)
            turn(mixed, 1, at_out)
        elif s == 3:
            attend(slot, text_read, tvec_ref)
            send_out(middle, mid_out)
            turn(normed_two, 2, mt_out)
        elif s < 8:
            expand(slot, s - 4, tvec_ref, True)
        else:
            if s == 8:
                send_out(active, act_out)
                send_out(slope, slope_out)
            shrink(slot, s - 8, tvec_ref)
        if s == PARTS - 1:
            send_out(total.at[aligned(z_at, PAIR)], words_out, late)
            for i in range(GROUP):
                row = seg_row[i].astype(jnp.float32)[0:8, :]
                marks = jnp.where(row == lax.broadcasted_iota(jnp.int32, (8, PAIR), 0).astype(jnp.float32), 1.0, 0.0)
                marks_out[i] = marks
                sums = jnp.dot(
                    marks, total[pl.ds(i * PAIR, PAIR), :], precision=PRECISE, preferred_element_type=jnp.float32
                )
                text_pool_out[pl.ds(i * 8, 8), :] = sums / jnp.sum(marks, axis=1, keepdims=True)

    def image_part(s):
        slot, k = s, s - PARTS
        if k == 0:
            for copy in outs:
                copy.wait()
            first_norm(image_read, ivec_ref)
            project(slot, 0, (ivec_ref, 2))
        elif k == 1:
            project(slot, 1, None)
        elif k == 2:
            project(slot, 2, (ivec_ref, 3))
            attention_forward(qkv, mixed, None, image_allowed)
        elif k == 3:
            attend(slot, image_read, ivec_ref)
            apool[...] = jnp.zeros_like(apool)
        elif k < 8:
            expand(slot, k - 4, ivec_ref, False)
            mark = keep_mark().astype(jnp.bfloat16)
            where = pl.ds((k - 4) * PART, PART)
            mean = dot(mark, active[:, where]) * (1.0 / patches)
            high = mean.astype(jnp.bfloat16)
            rest = mean - high.astype(jnp.float32)
            low = rest.astype(jnp.bfloat16)
            apool[0:8, where] = high.astype(jnp.float32)
            apool[8:16, where] = low.astype(jnp.float32)
            apool[16:24, where] = rest - low.astype(jnp.float32)
        else:
            for half in range(2):
                where = pl.ds(half * (D // 2), D // 2)
                left = apool[:, pl.ds((k - 8) * PART, PART)].astype(jnp.bfloat16)
                out = dot_nt(left, weight_rows(slot, half))
                out = out[0:8] + out[8:16] + out[16:24]
                if k == 8:
                    held = jnp.concatenate(
                        [
                            jnp.sum(middle[pl.ds(i * (PAIR // 2), patches), where], axis=0, keepdims=True)
                            for i in range(GROUP * 2)
                        ],
                        axis=0,
                    )
                    image_pool_out[:, where] = (
                        held * (1.0 / patches) + ivec_ref[:, pl.ds(7 * D + half * (D // 2), D // 2)] + out
                    )
                else:
                    image_pool_out[:, where] += out

    for s in range(count):
        for copy in own_shard(s):
            copy.start()
        if s == 1:
            for copy in firsts:
                copy.start()
    begin(0)
    for copy in tokens:
        copy.start()
    for copy in firsts:
        copy.wait()
    for s in range(1, AHEAD):
        begin(s)
    for step in range(count + AT_C):
        carry_on(step)
        s = step - AT_C
        if 0 <= s < PARTS:
            text_part(s)
        elif PARTS <= s:
            image_part(s)
    for copy in late:
        copy.wait()
    for s in range(PARTS):
        store(s).wait()
    for s in range(count):
        for j in range(2):
            for up in range(2):
                for hop in range(GROUP - 1):
                    unit = z_at - hop if up else z_at + hop
                    inside = (unit >= 0) & (unit < GROUP) & z_open[up]
                    pl.when(inside)(z_copy(s, up, unit, j).wait_send)
            for unit in range(GROUP):
                y_copy(s, 0, unit, j).wait_send()
        over_units(lambda unit: x_copy(s, unit).wait_send(), lambda: x_own_copy(s).wait_send())
        for j in range(3):
            c_copy(s, j).wait_send()


def gather_and_forward(n_dp, text_low, image_low, tokens, segments, pictures, text_vectors, image_vectors):
    own, columns = text_low.shape
    images, patches = pictures.shape[0], pictures.shape[1]
    n_inner = n_dp // GROUP
    lane_rows = own // LANES
    count = 2 * PARTS
    numbers = (segments + jnp.arange(segments.shape[0], dtype=jnp.int32)[:, None] * PER_ROW).reshape(-1)
    numbers = numbers.astype(jnp.bfloat16)
    padded = jnp.pad(pictures, ((0, 0), (0, PAIR // 2 - patches), (0, 0))).reshape(WORDS, D)
    hbm, vmem = pl.BlockSpec(memory_space=pltpu.HBM), pl.BlockSpec(memory_space=pltpu.VMEM)
    low, full = jnp.bfloat16, jnp.float32
    shape = jax.ShapeDtypeStruct
    gathered = shape((PARTS, n_dp, LANES, lane_rows, PART), low)
    turned = shape((D // GROUP, WORDS), low)
    pairs = GROUP * HEADS // 2
    dma = pltpu.SemaphoreType.DMA
    outs = pl.pallas_call(
        functools.partial(forward_kernel, n_dp, patches),
        out_shape=(
            gathered, shape((PAIR, D), full), shape((8 * GROUP, D), full), shape((images, D), full),
            shape((GROUP, 8, PAIR), full), shape((WORDS, 3 * D), low), shape((pairs, 2 * PAIR, PAIR), full),
            shape((WORDS, D), full), shape((WORDS, FF), full), shape((WORDS, FF), low), turned, turned, turned,
        ),
        in_specs=[hbm] * 5 + [vmem] * 3,
        out_specs=(hbm, hbm, vmem, vmem, vmem) + (hbm,) * 8,
        scratch_shapes=[
            pltpu.VMEM((PARTS, n_dp, LANES, lane_rows, PART), low),
            pltpu.VMEM((PARTS, n_dp, LANES, lane_rows, PART), low),
            pltpu.VMEM((GROUP, PAIR, D), low),
            pltpu.VMEM((GROUP, PAIR, PAIR), low),
            pltpu.VMEM((GROUP, 16, PAIR), low),
            pltpu.VMEM((WORDS, D), low),
            pltpu.VMEM((WORDS, 3 * D), low),
            pltpu.VMEM((WORDS, D), low),
            pltpu.VMEM((WORDS, D), full),
            pltpu.VMEM((WORDS, D), low),
            pltpu.VMEM((WORDS, FF), low),
            pltpu.VMEM((WORDS, FF), full),
            pltpu.VMEM((pairs, 2 * PAIR, PAIR), full),
            pltpu.VMEM((WORDS, D), full),
            pltpu.VMEM((WORDS, TILE), full),
            pltpu.VMEM((3, D, WORDS), low),
            pltpu.VMEM((24, FF), full),
            dma((count, 2, GROUP, 2)), dma((count, GROUP, 2)),
            dma((count, n_inner - 1, GROUP, 2)), dma((count, n_inner - 1, GROUP, 2)),
            dma((count, GROUP)), dma((count, GROUP)), dma((count, 3)), dma((count, 3)),
            dma((3, GROUP - 1)), dma((3, GROUP - 1)), dma((3,)), dma((count, 3)), dma((PARTS,)), dma((12,)),
        ],
        compiler_params=pltpu.CompilerParams(collective_id=5, has_side_effects=True, vmem_limit_bytes=60 << 20),
        name="gather_and_forward",
    )(
        text_low.reshape(LANES, lane_rows, columns), image_low.reshape(LANES, lane_rows, columns), tokens,
        jnp.broadcast_to(numbers[:, None], (PAIR, PAIR)), jnp.broadcast_to(numbers[None, :], (16, PAIR)), padded,
        text_vectors.reshape(1, -1), image_vectors.reshape(1, -1),
    )
    return (outs[0].reshape(PARTS, D, PART),) + tuple(outs[1:])


def backward_kernel(
    n_dp,
    wt_ref, nt_ref, at_ref, mt_ref, qkv_ref, chance_ref, mid_ref, slope_ref, act_ref, feed_ref,
    e2t_ref, dy_ref, tok_ref, vec_ref,
    rows_out, input_out, vector_out,
    weight, turned, qkv, chance, middle, slope, active, grad_hidden, grad_mix, low, low_mixed, wide, block, sent, got, sums,
    load_sem, send, recv, out_sem,
):
    n_inner = n_dp // GROUP
    d_at, r_at = lax.axis_index("dp"), lax.axis_index("rep")
    z_at, y_at = d_at // n_inner, lax.rem(d_at, n_inner)
    peer = (z_at * n_inner + 1 - y_at, r_at)
    own = D // n_dp
    share = 1.0 / GROUP

    loads = {}

    def fetch(name, src, dst):
        copy = pltpu.make_async_copy(src, dst, load_sem.at[len(loads)])
        copy.start()
        loads[name] = copy

    def need(*names):
        for name in names:
            loads[name].wait()

    fetch("act", act_ref, active)
    for part in range(4):
        fetch(("w", 8 + part), wt_ref.at[8 + part], weight.at[8 + part])
    fetch("slope", slope_ref, slope)
    fetch("mt", mt_ref, turned.at[0])
    for part in range(4):
        fetch(("w", 4 + part), wt_ref.at[4 + part], weight.at[4 + part])
    fetch("mid", mid_ref, middle)
    fetch("at", at_ref, turned.at[1])
    fetch(("w", 3), wt_ref.at[3], weight.at[3])
    fetch("qkv", qkv_ref, qkv)
    fetch("chance", chance_ref, chance)
    fetch("nt", nt_ref, turned.at[2])
    for part in range(3):
        fetch(("w", part), wt_ref.at[part], weight.at[part])
    fetch("feed", feed_ref, rows_out)

    barrier = pltpu.get_barrier_semaphore()
    pl.semaphore_signal(barrier, inc=1, device_id=peer, device_id_type=MESH)
    pl.semaphore_wait(barrier, 1)

    def exchange(s):
        return pltpu.make_async_remote_copy(
            src_ref=sent.at[s], dst_ref=got.at[s], send_sem=send.at[s], recv_sem=recv.at[s],
            device_id=peer, device_id_type=MESH,
        )

    own_rows = pl.ds(pl.multiple_of(y_at * own, own), own)
    other_rows = pl.ds(pl.multiple_of((1 - y_at) * own, own), own)

    def outer(s, left, right_of):
        def body(c):
            block[...] = dot(left, right_of(c))
            where = pl.ds(pl.multiple_of(s * PART + c * TILE, TILE), TILE)
            rows_out[:, where] = rows_out[:, where] + block[own_rows, :]
            sent[s, :, aligned(c, TILE)] = block[other_rows, :].astype(jnp.bfloat16)

        loop(PART // TILE, body)
        exchange(s).start()

    ones = jnp.ones((16, WORDS), jnp.bfloat16)

    def column_sums(values, slot, scale):
        vector_out[:, pl.ds(slot, values.shape[1])] = dot(ones, values)[0:1, :] * scale

    def cast(i):
        rows = aligned(i, ROWS)
        low[rows, :] = dy_ref[rows, :].astype(jnp.bfloat16)

    loop(WORDS // ROWS, cast)
    column_sums(low[...], 7 * D, share)
    need("act", "feed")
    for part in range(4):
        outer(8 + part, e2t_ref[...], lambda c: active[:, pl.ds(pl.multiple_of(part * PART + c * TILE, TILE), TILE)])
    need("slope")
    for part in range(4):
        need(("w", 8 + part))

        def hidden_body(c):
            where = pl.ds(pl.multiple_of(part * PART + c * TILE, TILE), TILE)
            out = dot(low[...], weight[8 + part, :, aligned(c, TILE)])
            grad_hidden[:, where] = (out * slope[:, where]).astype(jnp.bfloat16)

        loop(PART // TILE, hidden_body)
        column_sums(grad_hidden[:, pl.ds(part * PART, PART)], 8 * D + part * PART, share)
    need("mt")
    for part in range(4):
        outer(
            4 + part, turned[0], lambda c: grad_hidden[:, pl.ds(pl.multiple_of(part * PART + c * TILE, TILE), TILE)]
        )
    for part in range(4):
        need(("w", 4 + part))
    for half in range(2):
        rows = pl.ds(half * (D // 2), D // 2)
        out = dot_nt(grad_hidden[:, pl.ds(0, PART)], weight[4, rows, :])
        for part in range(1, 4):
            out = out + dot_nt(grad_hidden[:, pl.ds(part * PART, PART)], weight[4 + part, rows, :])
        wide[:, rows] = out
    need("mid")

    def norm_back(value, grad, gain):
        center = value - jnp.mean(value, axis=-1, keepdims=True)
        scale = lax.rsqrt(jnp.mean(center * center, axis=-1, keepdims=True) + LAYER_EPS)
        unit = center * scale
        inner = grad * gain
        out = scale * (
            inner - jnp.mean(inner, axis=-1, keepdims=True) - unit * jnp.mean(inner * unit, axis=-1, keepdims=True)
        )
        return out, grad * unit

    def fold(values):
        return jnp.sum(values.reshape(ROWS // 8, 8, D), axis=0)

    sums[...] = jnp.zeros_like(sums)

    def second(i):
        rows = aligned(i, ROWS)
        grad = wide[rows, :]
        out, product = norm_back(middle[rows, :], grad, piece_of(vec_ref, 5))
        sums[0] += fold(product)
        sums[1] += fold(grad)
        out = out + dy_ref[rows, :]
        middle[rows, :] = out
        low[rows, :] = out.astype(jnp.bfloat16)

    loop(WORDS // ROWS, second)
    vector_out[:, pl.ds(5 * D, D)] = jnp.sum(sums[0], axis=0, keepdims=True) * share
    vector_out[:, pl.ds(6 * D, D)] = jnp.sum(sums[1], axis=0, keepdims=True) * share
    column_sums(low[...], 4 * D, share)
    need("at")
    outer(3, turned[1], lambda c: low[:, aligned(c, TILE)])
    need(("w", 3))
    for half in range(2):
        rows = pl.ds(half * (D // 2), D // 2)
        low_mixed[:, rows] = dot_nt(low[...], weight[3, rows, :]).astype(jnp.bfloat16)
    need("qkv", "chance")
    pairs = HEADS // 2

    def attention(at):
        i, j = at // pairs, lax.rem(at, pairs)
        rows = aligned(i, PAIR)
        q_cols = aligned(j, PAIR)
        k_cols = pl.ds(pl.multiple_of(D + j * PAIR, PAIR), PAIR)
        v_cols = pl.ds(pl.multiple_of(2 * D + j * PAIR, PAIR), PAIR)
        query, key, value = qkv[rows, q_cols], qkv[rows, k_cols], qkv[rows, v_cols]
        grad = two_heads(low_mixed[rows, q_cols])
        weight_ = chance[at]
        grad_mix[rows, v_cols] = dot_tn(weight_.astype(jnp.bfloat16), grad).astype(jnp.bfloat16)
        back = dot_nt(grad, value)
        back = weight_ * (back - jnp.sum(weight_ * back, axis=-1, keepdims=True))
        back = back.astype(jnp.bfloat16)
        side = jnp.concatenate([back[:PAIR], back[PAIR:]], axis=1)
        grad_mix[rows, q_cols] = (dot(side, two_heads(key)) * SCORE_SCALE).astype(jnp.bfloat16)
        grad_mix[rows, k_cols] = (dot_tn(back, two_heads(query)) * SCORE_SCALE).astype(jnp.bfloat16)

    loop(GROUP * pairs, attention, unroll=2)
    need("nt")
    for part in range(3):
        outer(part, turned[2], lambda c: grad_mix[:, pl.ds(pl.multiple_of(part * PART + c * TILE, TILE), TILE)])
    column_sums(grad_mix[:, pl.ds(0, D)], 2 * D, share)
    column_sums(grad_mix[:, pl.ds(2 * D, D)], 3 * D, share)
    for part in range(3):
        need(("w", part))
    mine = aligned(z_at, PAIR)
    for half in range(2):
        rows = pl.ds(half * (D // 2), D // 2)
        out = dot_nt(grad_mix[mine, pl.ds(0, PART)], weight[0, rows, :])
        for part in range(1, 3):
            out = out + dot_nt(grad_mix[mine, pl.ds(part * PART, PART)], weight[part, rows, :])
        wide[pl.ds(0, PAIR), rows] = out
    sums[...] = jnp.zeros_like(sums)

    def first(i):
        rows = aligned(i, ROWS)
        grad = wide[rows, :]
        out, product = norm_back(tok_ref[rows, :].astype(jnp.float32), grad, piece_of(vec_ref, 0))
        sums[0] += fold(product)
        sums[1] += fold(grad)
        input_out[rows, :] = out + middle[pl.ds(pl.multiple_of(z_at * PAIR + i * ROWS, ROWS), ROWS), :]

    loop(PAIR // ROWS, first)
    vector_out[:, pl.ds(0, D)] = jnp.sum(sums[0], axis=0, keepdims=True)
    vector_out[:, pl.ds(D, D)] = jnp.sum(sums[1], axis=0, keepdims=True)
    for s in (8, 9, 10, 11, 4, 5, 6, 7, 3, 0, 1, 2):
        exchange(s).wait_recv()

        def add(c):
            where = pl.ds(pl.multiple_of(s * PART + c * TILE, TILE), TILE)
            rows_out[:, where] = rows_out[:, where] + got[s, :, aligned(c, TILE)].astype(jnp.float32)

        loop(PART // TILE, add)
    for s in range(PARTS):
        exchange(s).wait_send()


def backward(n_dp, kept, turned_grad, grad_words, tokens, text_vectors, feedback_rows):
    weights, qkv, chance, middle, slope, active, n_turned, a_turned, m_turned = kept
    own = feedback_rows.shape[0]
    hbm, vmem = pl.BlockSpec(memory_space=pltpu.HBM), pl.BlockSpec(memory_space=pltpu.VMEM)
    low, full = jnp.bfloat16, jnp.float32
    shape = jax.ShapeDtypeStruct
    dma = pltpu.SemaphoreType.DMA
    pairs = GROUP * HEADS // 2
    return pl.pallas_call(
        functools.partial(backward_kernel, n_dp),
        out_shape=(shape(feedback_rows.shape, full), shape((PAIR, D), full), shape((1, 12 * D), full)),
        in_specs=[hbm] * 10 + [vmem] * 4,
        out_specs=(vmem, vmem, vmem),
        scratch_shapes=[
            pltpu.VMEM((PARTS, D, PART), low),
            pltpu.VMEM((3, D // GROUP, WORDS), low),
            pltpu.VMEM((WORDS, 3 * D), low),
            pltpu.VMEM((pairs, 2 * PAIR, PAIR), full),
            pltpu.VMEM((WORDS, D), full),
            pltpu.VMEM((WORDS, FF), full),
            pltpu.VMEM((WORDS, FF), low),
            pltpu.VMEM((WORDS, FF), low),
            pltpu.VMEM((WORDS, 3 * D), low),
            pltpu.VMEM((WORDS, D), low),
            pltpu.VMEM((WORDS, D), low),
            pltpu.VMEM((WORDS, D), full),
            pltpu.VMEM((D // GROUP, TILE), full),
            pltpu.VMEM((PARTS, own, PART), low),
            pltpu.VMEM((PARTS, own, PART), low),
            pltpu.VMEM((2, 8, D), full),
            dma((24,)), dma((PARTS,)), dma((PARTS,)), dma((4,)),
        ],
        compiler_params=pltpu.CompilerParams(collective_id=6, has_side_effects=True, vmem_limit_bytes=60 << 20),
        name="backward",
    )(
        weights, n_turned, a_turned, m_turned, qkv, chance, middle, slope, active, feedback_rows,
        turned_grad, grad_words, tokens, text_vectors.reshape(1, -1),
    )


def peer_at(offset, n_dp, n_rep):
    me = lax.axis_index("dp") * n_rep + lax.axis_index("rep")
    other = lax.rem(me + offset, n_dp * n_rep)
    return other, (other // n_rep, lax.rem(other, n_rep))


def meet(n_dp, n_rep):
    total = n_dp * n_rep
    barrier = pltpu.get_barrier_semaphore()

    def hello(offset, carry):
        _, peer = peer_at(offset, n_dp, n_rep)
        pl.semaphore_signal(barrier, inc=1, device_id=peer, device_id_type=MESH)
        return carry

    lax.fori_loop(1, total, hello, 0)
    pl.semaphore_wait(barrier, total - 1)


def spread_kernel(n_dp, n_rep, mine_ref, all_ref, send, recv, own_sem):
    total = n_dp * n_rep
    me = lax.axis_index("dp") * n_rep + lax.axis_index("rep")
    own = pltpu.make_async_copy(mine_ref, all_ref.at[me], own_sem)
    own.start()
    meet(n_dp, n_rep)

    def copy(offset):
        _, peer = peer_at(offset, n_dp, n_rep)
        return pltpu.make_async_remote_copy(
            src_ref=mine_ref, dst_ref=all_ref.at[me], send_sem=send.at[offset - 1],
            recv_sem=recv.at[offset - 1], device_id=peer, device_id_type=MESH,
        )

    def begin(offset, carry):
        copy(offset).start()
        return carry

    def finish(offset, carry):
        copy(offset).wait()
        return carry

    lax.fori_loop(1, total, begin, 0)
    own.wait()
    lax.fori_loop(1, total, finish, 0)


def spread(mine, n_dp, n_rep, collective, name):
    total = n_dp * n_rep
    vmem = pl.BlockSpec(memory_space=pltpu.VMEM)
    dma = pltpu.SemaphoreType.DMA
    return pl.pallas_call(
        functools.partial(spread_kernel, n_dp, n_rep),
        out_shape=jax.ShapeDtypeStruct((total,) + mine.shape, mine.dtype),
        in_specs=[vmem],
        out_specs=vmem,
        scratch_shapes=[dma((total - 1,)), dma((total - 1,)), dma],
        compiler_params=pltpu.CompilerParams(
            collective_id=collective, has_side_effects=True, vmem_limit_bytes=48 << 20
        ),
        name=name,
    )(mine)


def total_kernel(n_dp, n_rep, mine_ref, out_ref, parts, sums, send, recv, send_two, recv_two):
    total = n_dp * n_rep
    me = lax.axis_index("dp") * n_rep + lax.axis_index("rep")
    meet(n_dp, n_rep)

    def scatter(offset):
        other, peer = peer_at(offset, n_dp, n_rep)
        return pltpu.make_async_remote_copy(
            src_ref=mine_ref.at[other], dst_ref=parts.at[offset - 1], send_sem=send.at[offset - 1],
            recv_sem=recv.at[offset - 1], device_id=peer, device_id_type=MESH,
        )

    def share(offset):
        _, peer = peer_at(offset, n_dp, n_rep)
        return pltpu.make_async_remote_copy(
            src_ref=sums, dst_ref=out_ref.at[me], send_sem=send_two.at[offset - 1],
            recv_sem=recv_two.at[offset - 1], device_id=peer, device_id_type=MESH,
        )

    def start_scatter(offset, carry):
        scatter(offset).start()
        return carry

    def add(offset, carry):
        scatter(offset).wait_recv()
        return carry + parts[offset - 1]

    def start_share(offset, carry):
        share(offset).start()
        return carry

    def finish(offset, carry):
        scatter(offset).wait_send()
        share(offset).wait()
        return carry

    lax.fori_loop(1, total, start_scatter, 0)
    result = lax.fori_loop(1, total, add, mine_ref[me])
    sums[...] = result
    lax.fori_loop(1, total, start_share, 0)
    out_ref[me] = result
    lax.fori_loop(1, total, finish, 0)


def total_over_all(flat, n_dp, n_rep, collective, name):
    total = n_dp * n_rep
    count = flat.shape[0]
    chunk = -(-count // (total * 1024)) * 1024
    padded = jnp.pad(flat, (0, total * chunk - count)).reshape(total, chunk // 128, 128)
    vmem = pl.BlockSpec(memory_space=pltpu.VMEM)
    dma = pltpu.SemaphoreType.DMA
    summed = pl.pallas_call(
        functools.partial(total_kernel, n_dp, n_rep),
        out_shape=jax.ShapeDtypeStruct(padded.shape, padded.dtype),
        in_specs=[vmem],
        out_specs=vmem,
        scratch_shapes=[
            pltpu.VMEM((total - 1,) + padded.shape[1:], padded.dtype),
            pltpu.VMEM(padded.shape[1:], padded.dtype),
            dma((total - 1,)), dma((total - 1,)), dma((total - 1,)), dma((total - 1,)),
        ],
        compiler_params=pltpu.CompilerParams(
            collective_id=collective, has_side_effects=True, vmem_limit_bytes=48 << 20
        ),
        name=name,
    )(padded)
    return summed.reshape(-1)[:count]


def masked_scores(query_heads, key_heads, allowed):
    scores = (
        jnp.einsum("rshd,rthd->rhst", query_heads, key_heads, preferred_element_type=jnp.float32)
        * SCORE_SCALE
    )
    return jnp.where(allowed[:, None], scores, MASKED)


def block_forward(inputs, allowed, weights, vector_pieces, pooled_only):
    (
        gain_one, shift_one, bias_query, bias_value, bias_out,
        gain_two, shift_two, bias_shrink, bias_expand,
    ) = vector_pieces
    row_count, seq_tokens = (inputs.shape[0], inputs.shape[1])
    normed = layer_norm(inputs, gain_one, shift_one).astype(jnp.bfloat16)
    mixing = jnp.einsum("rsd,dc->rsc", normed, weights[:, : 3 * D], preferred_element_type=jnp.float32)
    mixing = mixing + jnp.concatenate([bias_query, jnp.zeros_like(bias_query), bias_value])
    head_parts = mixing.astype(jnp.bfloat16).reshape(row_count, seq_tokens, 3, HEADS, HEAD_DIM)
    query_heads, key_heads, value_heads = (head_parts[:, :, 0], head_parts[:, :, 1], head_parts[:, :, 2])
    scores = masked_scores(query_heads, key_heads, allowed)
    highest = jnp.max(scores, axis=-1, keepdims=True)
    log_total = highest + jnp.log(jnp.sum(jnp.exp(scores - highest), axis=-1, keepdims=True))
    attention = jnp.exp(scores - log_total).astype(jnp.bfloat16)
    mixed_heads = jnp.einsum("rhst,rthd->rshd", attention, value_heads, preferred_element_type=jnp.float32)
    mixed_heads = mixed_heads.reshape(row_count, seq_tokens, D).astype(jnp.bfloat16)
    attended = (
        jnp.einsum("rsd,de->rse", mixed_heads, weights[:, 3 * D : 4 * D], preferred_element_type=jnp.float32)
        + bias_out
    )
    middle = inputs + attended
    normed_two = layer_norm(middle, gain_two, shift_two).astype(jnp.bfloat16)
    hidden = (
        jnp.einsum("rsd,df->rsf", normed_two, weights[:, 4 * D : 4 * D + FF], preferred_element_type=jnp.float32)
        + bias_expand
    )
    active = jax.nn.gelu(hidden, approximate=False).astype(jnp.bfloat16)
    shrink = weights[:, 4 * D + FF :]
    if pooled_only:
        mean_active = jnp.mean(active.astype(jnp.float32), axis=1)
        high = mean_active.astype(jnp.bfloat16)
        rest = mean_active - high.astype(jnp.float32)
        low = rest.astype(jnp.bfloat16)
        lower = (rest - low.astype(jnp.float32)).astype(jnp.bfloat16)
        stacked = jnp.concatenate([high, low, lower], axis=0)
        shrunk = jnp.einsum("pf,df->pd", stacked, shrink, preferred_element_type=jnp.float32)
        shrunk = jnp.sum(shrunk.reshape(3, row_count, D), axis=0)
        return jnp.mean(middle, axis=1) + shrunk + bias_shrink
    shrunk = jnp.einsum("rsf,df->rsd", active, shrink, preferred_element_type=jnp.float32) + bias_shrink
    kept = (normed, query_heads, key_heads, value_heads, log_total, mixed_heads, middle, normed_two, hidden, active)
    return (middle + shrunk, kept)


def token_sum(values_low):
    return jnp.sum(values_low.astype(jnp.float32).reshape(-1, values_low.shape[-1]), axis=0)


def block_backward(inputs, allowed, weights, vector_pieces, forward_kept, grad_out, own_group, own_count):
    (gain_one, shift_one, _, _, _, gain_two, shift_two, _, _) = vector_pieces
    (normed, query_heads, key_heads, value_heads, log_total, mixed_heads, middle, normed_two, hidden, active) = forward_kept
    row_count, seq_tokens = (inputs.shape[0], inputs.shape[1])
    grad_shrunk = grad_out.astype(jnp.bfloat16)
    grad_active = jnp.einsum("rsd,df->rsf", grad_shrunk, weights[:, 4 * D + FF :], preferred_element_type=jnp.float32)
    _, gelu_back = jax.vjp(lambda before_gelu: jax.nn.gelu(before_gelu, approximate=False), hidden)
    grad_hidden = gelu_back(grad_active)[0].astype(jnp.bfloat16)
    grad_normed_two = jnp.einsum(
        "rsf,df->rsd", grad_hidden, weights[:, 4 * D : 4 * D + FF], preferred_element_type=jnp.float32
    )
    _, norm_two_back = jax.vjp(layer_norm, middle, gain_two, shift_two)
    grad_middle, grad_gain_two, grad_shift_two = norm_two_back(grad_normed_two)
    grad_middle = grad_middle + grad_out
    grad_attended = grad_middle.astype(jnp.bfloat16)
    grad_mixed = jnp.einsum("rse,de->rsd", grad_attended, weights[:, 3 * D : 4 * D], preferred_element_type=jnp.float32)
    grad_mixed = grad_mixed.astype(jnp.bfloat16).reshape(row_count, seq_tokens, HEADS, HEAD_DIM)
    attention = jnp.exp(masked_scores(query_heads, key_heads, allowed) - log_total)
    grad_values = jnp.einsum("rhst,rshd->rthd", attention.astype(jnp.bfloat16), grad_mixed, preferred_element_type=jnp.float32)
    grad_attention = jnp.einsum("rshd,rthd->rhst", grad_mixed, value_heads, preferred_element_type=jnp.float32)
    grad_scores = attention * (grad_attention - jnp.sum(attention * grad_attention, axis=-1, keepdims=True))
    grad_scores = grad_scores.astype(jnp.bfloat16)
    grad_query = jnp.einsum("rhst,rthd->rshd", grad_scores, key_heads, preferred_element_type=jnp.float32) * SCORE_SCALE
    grad_keys = jnp.einsum("rhst,rshd->rthd", grad_scores, query_heads, preferred_element_type=jnp.float32) * SCORE_SCALE
    grad_mixing = (
        jnp.stack([grad_query, grad_keys, grad_values], axis=2).reshape(row_count, seq_tokens, 3 * D).astype(jnp.bfloat16)
    )

    def mine(values):
        return lax.dynamic_slice_in_dim(values, own_group * own_count, own_count, 0)

    grad_normed = jnp.einsum("rsc,dc->rsd", mine(grad_mixing), weights[:, : 3 * D], preferred_element_type=jnp.float32)
    _, norm_one_back = jax.vjp(layer_norm, mine(inputs), gain_one, shift_one)
    grad_inputs, grad_gain_one, grad_shift_one = norm_one_back(grad_normed)
    grad_inputs = grad_inputs + mine(grad_middle)
    share = 1.0 / GROUP
    vector_grad = jnp.concatenate(
        [
            grad_gain_one, grad_shift_one,
            share * token_sum(grad_mixing[..., :D]), share * token_sum(grad_mixing[..., 2 * D :]),
            share * token_sum(grad_attended), share * grad_gain_two, share * grad_shift_two,
            share * token_sum(grad_shrunk), share * token_sum(grad_hidden),
        ]
    )
    tokens = row_count * seq_tokens
    outer_terms = (
        (normed.reshape(tokens, D), grad_mixing.reshape(tokens, 3 * D)),
        (mixed_heads.reshape(tokens, D), grad_attended.reshape(tokens, D)),
        (normed_two.reshape(tokens, D), grad_hidden.reshape(tokens, FF)),
        (grad_shrunk.reshape(tokens, D), active.reshape(tokens, FF)),
    )
    return (grad_inputs, vector_grad, outer_terms)


def orthonormal(stacked):
    waiting = [stacked[:, column_id] for column_id in range(stacked.shape[1])]
    finished = []
    while waiting:
        vector = waiting.pop(0)
        vector = vector / (jnp.sqrt(jnp.sum(vector * vector, axis=-1, keepdims=True)) + NORM_FLOOR)
        finished.append(vector)
        if waiting:
            later = jnp.stack(waiting, axis=1)
            later = later - jnp.sum(vector[:, None] * later, axis=-1, keepdims=True) * vector[:, None]
            waiting = [later[:, i] for i in range(later.shape[1])]
    return jnp.stack(finished, axis=1)


def rows_factor(start_part, row_block):
    return jnp.einsum("kc,dc->kd", start_part, row_block, precision=PRECISE)


def per_device(
    image_tokens, image_weights, image_vectors, text_tokens, segments, text_weights,
    text_vectors, momentum, vector_momentum, error_feedback, start_factors,
):
    n_rep, n_dp = lax.axis_size("rep"), lax.axis_size("dp")
    n_inner = n_dp // GROUP
    total = n_rep * n_dp
    device_pairs, patches = image_tokens.shape[0], image_tokens.shape[1]
    text_rows, seq_tokens = text_tokens.shape[0], text_tokens.shape[1]
    pair_total = device_pairs * total
    own_rows = text_weights.shape[0]
    d_at, r_at = lax.axis_index("dp"), lax.axis_index("rep")
    z_at, y_at = d_at // n_inner, d_at % n_inner
    row_start = d_at * own_rows
    factor_rank = start_factors.shape[0]
    bounds = matrix_bounds()
    tokens = text_tokens.reshape(text_rows * seq_tokens, D)
    words_low = text_weights.astype(jnp.bfloat16)
    feedback_rows = error_feedback[0]
    fused = (
        own_rows % (16 * LANES) == 0 and n_inner == 2 and n_rep == 4 and device_pairs == 8
        and text_rows * seq_tokens == PAIR and 2 * seq_tokens == PAIR and 2 * patches <= PAIR
    )
    if fused:
        outs = gather_and_forward(
            n_dp, words_low, image_weights, tokens, segments, image_tokens, text_vectors, image_vectors
        )
        text_output = outs[1].reshape(text_rows, seq_tokens, D)
        pooled, image_pooled, marks = outs[2], outs[3], outs[4]
        counts = jnp.sum(marks, axis=-1, keepdims=True)
    else:
        text_low, frozen, token_group, segment_group = gather_weights(
            n_dp, words_low, image_weights, tokens, segments
        )
        text_low, frozen = text_low.reshape(D, -1), frozen.reshape(D, -1)
        full_mask = jnp.zeros((device_pairs, patches, patches), jnp.int32) == 0
        image_pooled = block_forward(
            image_tokens.astype(jnp.float32), full_mask, frozen, vector_parts(image_vectors), True
        )
        group_rows = GROUP * text_rows
        text_float = token_group.reshape(group_rows, seq_tokens, D).astype(jnp.float32)
        segment_all = segment_group.reshape(group_rows, seq_tokens)
        allowed = segment_all[:, :, None] == segment_all[:, None, :]
        vector_pieces = vector_parts(text_vectors)
        group_output, forward_kept = block_forward(text_float, allowed, text_low, vector_pieces, False)
        text_output = lax.dynamic_slice_in_dim(group_output, z_at * text_rows, text_rows, 0)
        caption_marks = (
            segment_all[:, None, :] == jnp.arange(PER_ROW, dtype=jnp.int32)[None, :, None]
        ).astype(jnp.float32)
        counts = jnp.sum(caption_marks, axis=-1, keepdims=True)
        pooled = (jnp.einsum("rks,rsd->rkd", caption_marks, group_output, precision=PRECISE) / counts).reshape(-1, D)
    image_emb = unit_rows(image_pooled).astype(jnp.bfloat16)
    text_norm, embed_back = jax.vjp(unit_rows, pooled)
    text_emb = text_norm.astype(jnp.bfloat16)
    own_emb = lax.dynamic_slice_in_dim(text_emb, z_at * device_pairs, device_pairs, 0)
    embeddings = spread(jnp.concatenate([image_emb, own_emb], axis=0), n_dp, n_rep, 2, "spread_embeddings")
    image_all = embeddings[:, :device_pairs].reshape(pair_total, D)
    text_all = embeddings[:, device_pairs:].reshape(pair_total, D)
    own_pairs = (
        ((jnp.arange(GROUP, dtype=jnp.int32) * n_inner + y_at) * n_rep + r_at)[:, None] * device_pairs
        + jnp.arange(device_pairs, dtype=jnp.int32)[None, :]
    ).reshape(-1)
    logits = LOGIT_SCALE * jnp.einsum("pd,bd->pb", image_all, text_all, preferred_element_type=jnp.float32)
    image_top = jnp.max(logits, axis=1)
    image_log_total = image_top + jnp.log(jnp.sum(jnp.exp(logits - image_top[:, None]), axis=1))
    caption_top = jnp.max(logits, axis=0)
    caption_log_total = caption_top + jnp.log(jnp.sum(jnp.exp(logits - caption_top[None, :]), axis=0))
    pair_ids = jnp.arange(pair_total, dtype=jnp.int32)
    matched = jnp.sum(jnp.where(pair_ids[:, None] == pair_ids[None, :], logits, 0.0), axis=1)
    loss_total = (jnp.sum(image_log_total - matched) + jnp.sum(caption_log_total - matched)) / (2.0 * pair_total)
    diagonal_pick = (pair_ids[None, :] == own_pairs[:, None]).astype(jnp.float32)
    text_logits = LOGIT_SCALE * jnp.einsum("pd,bd->pb", text_emb, image_all, preferred_element_type=jnp.float32)
    text_top = jnp.max(text_logits, axis=1, keepdims=True)
    text_log_total = text_top + jnp.log(jnp.sum(jnp.exp(text_logits - text_top), axis=1, keepdims=True))
    text_soft = ((jnp.exp(text_logits - text_log_total) - diagonal_pick) * 0.5).astype(jnp.bfloat16)
    column_soft = ((jnp.exp(text_logits - image_log_total[None, :]) - diagonal_pick) * 0.5).astype(jnp.bfloat16)
    grad_text = LOGIT_SCALE * (
        jnp.einsum("pb,bd->pd", text_soft, image_all, preferred_element_type=jnp.float32)
        + jnp.einsum("pb,bd->pd", column_soft, image_all, preferred_element_type=jnp.float32)
    )
    grad_pooled = embed_back(grad_text)[0]
    if fused:
        grad_pooled = grad_pooled.reshape(GROUP, 8, D) / counts
        grad_words = jnp.einsum("gct,gcd->gtd", marks, grad_pooled, precision=PRECISE).reshape(WORDS, D)
        cut = lax.dynamic_slice_in_dim(grad_pooled, z_at * (D // GROUP), D // GROUP, 2)
        turned_grad = jnp.einsum("gct,gcd->dgt", marks, cut, precision=PRECISE).astype(jnp.bfloat16)
        kept = (outs[0],) + tuple(outs[5:])
        worker_rows, grad_inputs, vector_grad = backward(
            n_dp, kept, turned_grad.reshape(D // GROUP, WORDS), grad_words, tokens, text_vectors, feedback_rows
        )
        grad_inputs, vector_grad = grad_inputs.reshape(text_rows, seq_tokens, D), vector_grad.reshape(-1)
        worker_blocks = [worker_rows[:, first_col:after_col] for first_col, after_col in bounds]
    else:
        grad_pooled = grad_pooled.reshape(-1, PER_ROW, D) / counts
        grad_out = jnp.einsum("rks,rkd->rsd", caption_marks, grad_pooled, precision=PRECISE)
        grad_inputs, vector_grad, outer_terms = block_backward(
            text_float, allowed, text_low, vector_pieces, forward_kept, grad_out, z_at, text_rows
        )
        group_width = n_inner * own_rows
        worker_blocks = []
        for (left_side, right_side), (first_col, after_col) in zip(outer_terms, bounds):
            left_cut = lax.dynamic_slice_in_dim(left_side, z_at * group_width, group_width, 1)
            block = jnp.einsum("tc,tk->ck", left_cut, right_side, preferred_element_type=jnp.float32)
            mine = lax.dynamic_slice_in_dim(block, y_at * own_rows, own_rows, 0)
            for k in range(1, n_inner):
                target = lax.rem(y_at + k, n_inner)
                outgoing = lax.dynamic_slice_in_dim(block, target * own_rows, own_rows, 0).astype(jnp.bfloat16)
                pairs = [
                    (z * n_inner + y, z * n_inner + (y + k) % n_inner) for z in range(GROUP) for y in range(n_inner)
                ]
                mine = mine + lax.ppermute(outgoing, "dp", pairs).astype(jnp.float32)
            worker_blocks.append(mine + feedback_rows[:, first_col:after_col])
    factor_rows = jnp.concatenate(
        [
            rows_factor(start_factors[:, first_col:after_col], rows)
            for rows, (first_col, after_col) in zip(worker_blocks, bounds)
        ],
        axis=0,
    )
    gathered_rows = spread(factor_rows, n_dp, n_rep, 3, "spread_factors")
    factor = jnp.sum(gathered_rows.reshape(n_dp, n_rep, 4 * factor_rank, own_rows), axis=1)
    factor = jnp.swapaxes(factor, 0, 1).reshape(4, factor_rank, D)
    left_basis = orthonormal(factor).reshape(4 * factor_rank, D)
    basis_rows = lax.dynamic_slice_in_dim(left_basis, row_start, own_rows, 1)
    basis_parts = [basis_rows[i * factor_rank : (i + 1) * factor_rank] for i in range(4)]
    right_part = jnp.concatenate(
        [jnp.einsum("kd,dc->kc", part, rows, precision=PRECISE) for part, rows in zip(basis_parts, worker_blocks)],
        axis=1,
    )
    summed = total_over_all(
        jnp.concatenate([right_part.reshape(-1), vector_grad]), n_dp, n_rep, 4, "total_right"
    )
    new_right = summed[: right_part.size].reshape(right_part.shape)
    vector_total = summed[right_part.size :]
    approximation = jnp.concatenate(
        [
            jnp.einsum("kd,kc->dc", part, new_right[:, first_col:after_col], precision=PRECISE)
            for part, (first_col, after_col) in zip(basis_parts, bounds)
        ],
        axis=1,
    )
    worker_rows = jnp.concatenate(worker_blocks, axis=1)
    new_feedback = (worker_rows - approximation / n_rep)[None]
    new_momentum = MOMENTUM_DECAY * momentum + approximation
    new_weights = text_weights - STEP_RATE * new_momentum
    new_vector_momentum = MOMENTUM_DECAY * vector_momentum + vector_total
    new_vectors = text_vectors - STEP_RATE * new_vector_momentum
    return (
        loss_total, text_output, grad_inputs, new_weights, new_momentum, new_feedback,
        new_vectors, new_vector_momentum, left_basis, new_right,
    )


def solution(mesh):
    placed = (
        P(("dp", "rep"), None, None), P("dp", None), P(), P(("dp", "rep"), None, None), P(("dp", "rep"), None),
        P("dp", None), P(), P("dp", None), P(), P("rep", "dp", None), P(),
    )
    return jax.shard_map(
        per_device,
        mesh=mesh,
        in_specs=placed,
        out_specs=(
            P(), P(("dp", "rep"), None, None), P(("dp", "rep"), None, None), P("dp", None), P("dp", None),
            P("rep", "dp", None), P(), P(), P(), P(),
        ),
        check_vma=False,
    )
```

```python
import functools

import jax
import jax.numpy as jnp
from jax import lax
from jax.experimental import pallas as pl
from jax.experimental.pallas import tpu as pltpu
from jax.sharding import PartitionSpec as P

D = 768
FF = 3072
HEADS = 12
HEAD_DIM = 64
PER_ROW = 4
GROUP = 4
SECTION = 3072
LANE_COLS = 512

PRECISE = lax.Precision.HIGHEST
LAYER_EPS = 1e-06
SCORE_SCALE = 0.125
LOGIT_SCALE = 50.0
MOMENTUM_DECAY = 0.9
STEP_RATE = 0.08
NORM_FLOOR = 1e-08
MASKED = -1e30
MESH = pl.DeviceIdType.MESH


def layer_norm(values, layer_gain, layer_shift):
    center = values - jnp.mean(values, axis=-1, keepdims=True)
    spread = jnp.mean(center * center, axis=-1, keepdims=True)
    return center * lax.rsqrt(spread + LAYER_EPS) * layer_gain + layer_shift


def unit_rows(values):
    return values * lax.rsqrt(jnp.sum(values * values, axis=-1, keepdims=True) + LAYER_EPS)


def vector_parts(vectors):
    pieces = [vectors[position * D : (position + 1) * D] for position in range(8)]
    return pieces + [vectors[8 * D :]]


def matrix_bounds():
    return ((0, 3 * D), (3 * D, 4 * D), (4 * D, 4 * D + FF), (4 * D + FF, 4 * D + 2 * FF))


def gather_kernel(
    n_dp, text_ref, image_ref, tok_ref, seg_ref, wt_ref, wi_ref, tok_out, seg_out,
    z_send, z_recv, y_send, y_recv, x_send, x_recv, c_send, c_recv, t_send, t_recv, t_own, own_sem,
):
    n_inner = n_dp // GROUP
    d_at, r_at = lax.axis_index("dp"), lax.axis_index("rep")
    z_at, y_at = d_at // n_inner, d_at % n_inner
    x_at, c_at = r_at // 2, r_at % 2
    z_peers = [(lax.rem(z_at + k, GROUP) * n_inner + y_at, r_at) for k in range(1, GROUP)]
    z_from = [lax.rem(z_at + GROUP - k, GROUP) for k in range(1, GROUP)]
    y_peers = [(z_at * n_inner + lax.rem(y_at + k, n_inner), r_at) for k in range(1, n_inner)]
    y_from = [lax.rem(y_at + n_inner - k, n_inner) for k in range(1, n_inner)]
    x_peer = (d_at, (1 - x_at) * 2 + c_at)
    c_peer = (d_at, x_at * 2 + 1 - c_at)

    barrier = pltpu.get_barrier_semaphore()
    everyone = z_peers + y_peers + [x_peer, c_peer]
    for peer in everyone:
        pl.semaphore_signal(barrier, inc=1, device_id=peer, device_id_type=MESH)
    pl.semaphore_wait(barrier, len(everyone))

    def shard_of(z, y):
        return z * n_inner + y

    sections = [(image_ref, wi_ref, 0), (text_ref, wt_ref, 0), (image_ref, wi_ref, 1),
                (text_ref, wt_ref, 1), (image_ref, wi_ref, 2), (text_ref, wt_ref, 2)]

    def cols(section, lane):
        start = sections[section][2] * SECTION + lane * LANE_COLS
        return pl.ds(pl.multiple_of(start, 128), LANE_COLS)

    lane_both = c_at
    lane_mine = 2 + x_at * 2 + c_at
    lane_theirs = 2 + (1 - x_at) * 2 + c_at
    lanes = (lane_both, lane_mine)

    locals_ = [
        pltpu.make_async_copy(tok_ref, tok_out.at[z_at], t_own.at[0]),
        pltpu.make_async_copy(seg_ref, seg_out.at[z_at], t_own.at[1]),
    ]
    for s, (src, full, _) in enumerate(sections):
        for j in range(2):
            column = cols(s, lanes[j])
            locals_.append(pltpu.make_async_copy(src.at[:, column], full.at[d_at, :, column], own_sem.at[s, j]))
    for copy in locals_:
        copy.start()

    def remote(src, dst, send, recv, peer):
        return pltpu.make_async_remote_copy(
            src_ref=src, dst_ref=dst, send_sem=send, recv_sem=recv, device_id=peer, device_id_type=MESH
        )

    def z_copy(s, k, j):
        src, full, _ = sections[s]
        return remote(
            src.at[:, cols(s, lanes[j])], full.at[d_at, :, cols(s, lanes[j])],
            z_send.at[s, k, j], z_recv.at[s, k, j], z_peers[k],
        )

    def y_copy(s, q, zi, j):
        src, full, _ = sections[s]
        column = cols(s, lanes[j])
        if zi == 0:
            shard, source = d_at, src.at[:, column]
        else:
            shard = shard_of(z_from[zi - 1], y_at)
            source = full.at[shard, :, column]
        return remote(source, full.at[shard, :, column], y_send.at[s, q, zi, j], y_recv.at[s, q, zi, j], y_peers[q])

    def x_copy(s):
        full = sections[s][1]
        block = full.at[:, :, cols(s, lane_mine)]
        return remote(block, block, x_send.at[s], x_recv.at[s], x_peer)

    def c_copy(s, j):
        full = sections[s][1]
        block = full.at[:, :, cols(s, (lane_both, lane_mine, lane_theirs)[j])]
        return remote(block, block, c_send.at[s, j], c_recv.at[s, j], c_peer)

    count = len(sections)
    tokens = []
    for k in range(GROUP - 1):
        tokens.append(remote(tok_ref, tok_out.at[z_at], t_send.at[0, k], t_recv.at[0, k], z_peers[k]))
        tokens.append(remote(seg_ref, seg_out.at[z_at], t_send.at[1, k], t_recv.at[1, k], z_peers[k]))

    def begin(s):
        for j in range(2):
            for k in range(GROUP - 1):
                z_copy(s, k, j).start()
            for q in range(n_inner - 1):
                y_copy(s, q, 0, j).start()

    begin(0)
    for copy in tokens:
        copy.start()
    for copy in locals_:
        copy.wait()
    begin(1)
    for step in range(count + 3):
        if step < count:
            for k in range(GROUP - 1):
                for j in range(2):
                    z_copy(step, k, j).wait_recv()
                    for q in range(n_inner - 1):
                        y_copy(step, q, k + 1, j).start()
            if step + 2 < count:
                begin(step + 2)
        s = step - 1
        if 0 <= s < count:
            for q in range(n_inner - 1):
                for zi in range(GROUP):
                    for j in range(2):
                        y_copy(s, q, zi, j).wait_recv()
            x_copy(s).start()
            for j in range(2):
                c_copy(s, j).start()
        s = step - 2
        if 0 <= s < count:
            x_copy(s).wait_recv()
            c_copy(s, 2).start()
        s = step - 3
        if 0 <= s < count:
            for j in range(3):
                c_copy(s, j).wait_recv()
    for copy in tokens:
        copy.wait()
    for s in range(count):
        for j in range(2):
            for k in range(GROUP - 1):
                z_copy(s, k, j).wait_send()
            for q in range(n_inner - 1):
                for zi in range(GROUP):
                    y_copy(s, q, zi, j).wait_send()
        x_copy(s).wait_send()
        for j in range(3):
            c_copy(s, j).wait_send()


def gather_weights(n_dp, text_low, image_low, tokens, segments):
    n_inner = n_dp // GROUP
    full = jax.ShapeDtypeStruct((n_dp,) + text_low.shape, jnp.bfloat16)
    hbm = pl.BlockSpec(memory_space=pltpu.HBM)
    dma = pltpu.SemaphoreType.DMA
    return pl.pallas_call(
        functools.partial(gather_kernel, n_dp),
        out_shape=(
            full,
            full,
            jax.ShapeDtypeStruct((GROUP,) + tokens.shape, jnp.bfloat16),
            jax.ShapeDtypeStruct((GROUP,) + segments.shape, jnp.int32),
        ),
        in_specs=[hbm] * 4,
        out_specs=(hbm,) * 4,
        scratch_shapes=[
            dma((6, GROUP - 1, 2)), dma((6, GROUP - 1, 2)),
            dma((6, n_inner - 1, GROUP, 2)), dma((6, n_inner - 1, GROUP, 2)),
            dma((6,)), dma((6,)), dma((6, 3)), dma((6, 3)),
            dma((2, GROUP - 1)), dma((2, GROUP - 1)), dma((2,)), dma((6, 2)),
        ],
        compiler_params=pltpu.CompilerParams(collective_id=1, has_side_effects=True),
        name="gather_weights",
    )(text_low, image_low, tokens, segments)


TILE = 256
PAIR = 128
ROWS = 32
LANES = 6
PART = 768
PARTS = 12
DEPTH = 8
AHEAD = 2
LAG_Z = 1
LAG_Y = 1
LAG_X = 1
LAG_C = 1
AT_Y = 2 * LAG_Z + LAG_Y
AT_X = AT_Y + LAG_X
AT_C = AT_X + LAG_C
WORDS = (GROUP * PAIR)


def piece_of(vec_ref, index, width=D):
    return vec_ref[:, pl.ds(index * D, width)]


def loop(count, body, unroll=1):
    def step(i, carry):
        body(i)
        return carry

    lax.fori_loop(0, count, step, 0, unroll=unroll)


def aligned(i, size):
    return pl.ds(pl.multiple_of(i * size, size), size)


def norm_rows(values):
    center = values - jnp.mean(values, axis=-1, keepdims=True)
    spread_ = jnp.mean(center * center, axis=-1, keepdims=True)
    return center * lax.rsqrt(spread_ + LAYER_EPS)


def dot(left, right):
    return jnp.dot(left, right, preferred_element_type=jnp.float32)


def dot_nt(left, right):
    return lax.dot_general(left, right, (((1,), (1,)), ((), ())), preferred_element_type=jnp.float32)


def dot_tn(left, right):
    return lax.dot_general(left, right, (((0,), (0,)), ((), ())), preferred_element_type=jnp.float32)


def lane_is_first():
    return lax.broadcasted_iota(jnp.int32, (PAIR, PAIR), 1) < HEAD_DIM


def two_heads(block):
    first = lane_is_first()
    zero = jnp.zeros_like(block)
    return jnp.concatenate([jnp.where(first, block, zero), jnp.where(first, zero, block)], axis=0)


def attention_forward(qkv, mixed, chance, allowed_of):
    pairs = HEADS // 2

    def body(at):
        i, j = at // pairs, lax.rem(at, pairs)
        rows = aligned(i, PAIR)
        query = qkv[rows, aligned(j, PAIR)]
        key = qkv[rows, pl.ds(pl.multiple_of(D + j * PAIR, PAIR), PAIR)]
        value = qkv[rows, pl.ds(pl.multiple_of(2 * D + j * PAIR, PAIR), PAIR)]
        scores = dot_nt(two_heads(query), key) * SCORE_SCALE
        allowed = allowed_of(i)
        scores = jnp.where(jnp.concatenate([allowed, allowed], axis=0), scores, MASKED)
        scores = jnp.exp(scores - jnp.max(scores, axis=-1, keepdims=True))
        weight = scores / jnp.sum(scores, axis=-1, keepdims=True)
        if chance is not None:
            chance[at] = weight
        low = weight.astype(jnp.bfloat16)
        side = jnp.concatenate([low[:PAIR], low[PAIR:]], axis=1)
        mixed[rows, aligned(j, PAIR)] = dot(side, two_heads(value)).astype(jnp.bfloat16)

    loop(GROUP * pairs, body, unroll=2)


def forward_kernel(
    n_dp, patches,
    text_ref, image_ref, tok_ref, col_ref, row_ref, pic_ref, tvec_ref, ivec_ref,
    wt_out, words_out, text_pool_out, image_pool_out, marks_out, qkv_out, chance_out, mid_out, slope_out,
    act_out, nt_out, at_out, mt_out,
    wi_ref, wt_vmem, tok, seg_col, seg_row, normed, qkv, mixed, middle, normed_two, active, slope, chance, total, hid, turned, apool,
    z_send, z_recv, y_send, y_recv, x_send, x_recv, c_send, c_recv, t_send, t_recv, t_own, own_sem, w_sem, out_sem,
):
    n_inner = n_dp // GROUP
    d_at, r_at = lax.axis_index("dp"), lax.axis_index("rep")
    z_at, y_at = d_at // n_inner, lax.rem(d_at, n_inner)
    x_at, c_at = r_at // 2, lax.rem(r_at, 2)
    z_peers = [(lax.rem(z_at + k, GROUP) * n_inner + y_at, r_at) for k in range(1, GROUP)]
    z_next = [((z_at - 1) * n_inner + y_at, r_at), ((z_at + 1) * n_inner + y_at, r_at)]
    y_peers = [(z_at * n_inner + 1 - y_at, r_at)]
    x_peer = (d_at, (1 - x_at) * 2 + c_at)
    c_peer = (d_at, x_at * 2 + 1 - c_at)

    barrier = pltpu.get_barrier_semaphore()
    everyone = z_peers + y_peers + [x_peer, c_peer]
    for peer in everyone:
        pl.semaphore_signal(barrier, inc=1, device_id=peer, device_id_type=MESH)
    pl.semaphore_wait(barrier, len(everyone))

    sections = [(text_ref, wt_vmem, k) for k in range(PARTS)] + [(image_ref, wi_ref, k) for k in range(PARTS)]
    count = len(sections)
    lane_both = c_at
    lane_mine = 2 + x_at * 2 + c_at
    lane_theirs = 2 + (1 - x_at) * 2 + c_at
    lanes = (lane_both, lane_mine)

    def remote(src, dst, send, recv, peer):
        return pltpu.make_async_remote_copy(
            src_ref=src, dst_ref=dst, send_sem=send, recv_sem=recv, device_id=peer, device_id_type=MESH
        )

    def cols(s):
        return pl.ds(sections[s][2] * PART, PART)

    def held(s, shard, lane):
        _, full, k = sections[s]
        return full.at[k, shard, lane]

    def z_copy(s, up, unit, j):
        shard = unit * n_inner + y_at
        return remote(
            held(s, shard, lanes[j]), held(s, shard, lanes[j]),
            z_send.at[s, up, unit, j], z_recv.at[s, unit, j], z_next[up],
        )

    def y_copy(s, q, unit, j):
        shard = unit * n_inner + y_at
        return remote(
            held(s, shard, lanes[j]), held(s, shard, lanes[j]),
            y_send.at[s, q, unit, j], y_recv.at[s, q, unit, j], y_peers[q],
        )

    def x_copy(s, unit):
        block = held(s, pl.ds(unit * n_inner, n_inner), lane_mine)
        return remote(block, block, x_send.at[s, unit], x_recv.at[s, unit], x_peer)

    def x_own_copy(s):
        block = held(s, z_at * n_inner + 1 - y_at, lane_mine)
        return remote(block, block, x_send.at[s, z_at], x_recv.at[s, z_at], x_peer)

    def c_copy(s, j):
        block = held(s, slice(None), (lane_both, lane_mine, lane_theirs)[j])
        return remote(block, block, c_send.at[s, j], c_recv.at[s, j], c_peer)

    def store(s):
        return pltpu.make_async_copy(wt_vmem.at[s], wt_out.at[s], w_sem.at[s])

    firsts = [
        pltpu.make_async_copy(tok_ref, tok.at[z_at], t_own.at[0]),
        pltpu.make_async_copy(col_ref, seg_col.at[z_at], t_own.at[1]),
        pltpu.make_async_copy(row_ref, seg_row.at[z_at], t_own.at[2]),
    ]
    z_open = (z_at > 0, z_at < GROUP - 1)

    def own_shard(s):
        src, _, _ = sections[s]
        return [
            pltpu.make_async_copy(src.at[lane, :, cols(s)], held(s, d_at, lane), own_sem.at[s, j])
            for j, lane in enumerate((lane_both, lane_mine, lane_theirs))
        ]

    tokens = []
    for k in range(GROUP - 1):
        for which, (src, dst) in enumerate(((tok_ref, tok), (col_ref, seg_col), (row_ref, seg_row))):
            tokens.append(remote(src, dst.at[z_at], t_send.at[which, k], t_recv.at[which, k], z_peers[k]))

    def begin(s):
        for copy in own_shard(s):
            copy.wait()
        for j in range(2):
            for up in range(2):
                pl.when(z_open[up])(z_copy(s, up, z_at, j).start)
            y_copy(s, 0, z_at, j).start()

    def arrive(s, hop):
        for up in range(2):
            unit = z_at - hop if up else z_at + hop

            @pl.when((unit >= 0) & (unit < GROUP))
            def _():
                for j in range(2):
                    z_copy(s, up, unit, j).wait_recv()
                    pl.when(z_open[up])(z_copy(s, up, unit, j).start)
                    y_copy(s, 0, unit, j).start()

    def over_units(unit_fn, own_fn):
        for unit in range(GROUP):
            pl.when(unit != z_at)(functools.partial(unit_fn, unit))
        own_fn()

    def carry_on(step):
        if step + AHEAD < count:
            begin(step + AHEAD)
        for hop in range(1, GROUP):
            s = step - (hop - 1) * LAG_Z
            if 0 <= s < count:
                arrive(s, hop)
        s = step - AT_Y
        if 0 <= s < count:
            for unit in range(GROUP):
                for j in range(2):
                    y_copy(s, 0, unit, j).wait_recv()
            over_units(lambda unit: x_copy(s, unit).start(), lambda: x_own_copy(s).start())
            for j in range(2):
                c_copy(s, j).start()
        s = step - AT_X
        if 0 <= s < count:
            over_units(lambda unit: x_copy(s, unit).wait_recv(), lambda: x_own_copy(s).wait_recv())
            c_copy(s, 2).start()
        s = step - AT_C
        if 0 <= s < count:
            for j in range(3):
                c_copy(s, j).wait_recv()
            if s < PARTS:
                store(s).start()


    def weight_tile(s, c):
        _, full, k = sections[s]
        return full[k, :, :, :, aligned(c, TILE)].reshape(D, TILE)

    def weight_rows(s, half):
        _, full, k = sections[s]
        return full[k, pl.ds(half * (n_dp // 2), n_dp // 2)].reshape(D // 2, PART)

    def first_norm(read, vec):
        def body(i):
            rows = aligned(i, ROWS)
            value = norm_rows(read(i).astype(jnp.float32))
            normed[rows, :] = (value * piece_of(vec, 0) + piece_of(vec, 1)).astype(jnp.bfloat16)

        loop(WORDS // ROWS, body)

    def project(slot, part, bias):
        def body(c):
            out = dot(normed[...], weight_tile(slot, c))
            if bias is not None:
                out = out + bias[0][:, pl.ds(pl.multiple_of(bias[1] * D + c * TILE, TILE), TILE)]
            qkv[:, pl.ds(pl.multiple_of(part * D + c * TILE, TILE), TILE)] = out.astype(jnp.bfloat16)

        loop(PART // TILE, body)

    def attend(slot, read, vec):
        def body(c):
            where = aligned(c, TILE)
            middle[:, where] = dot(mixed[...], weight_tile(slot, c)) + vec[
                :, pl.ds(pl.multiple_of(4 * D + c * TILE, TILE), TILE)
            ]

        loop(PART // TILE, body)

        def norm(i):
            rows = aligned(i, ROWS)
            value = middle[rows, :] + read(i).astype(jnp.float32)
            middle[rows, :] = value
            normed_two[rows, :] = (norm_rows(value) * piece_of(vec, 5) + piece_of(vec, 6)).astype(jnp.bfloat16)

        loop(WORDS // ROWS, norm)

    def expand(slot, part, vec, keep):
        def body(c):
            start = pl.multiple_of(part * PART + c * TILE, TILE)
            hid[...] = dot(normed_two[...], weight_tile(slot, c)) + vec[:, pl.ds(pl.multiple_of(8 * D + start, TILE), TILE)]

            def inner(i):
                rows = aligned(i, ROWS)
                value = hid[rows, :]
                phi = 0.5 + 0.5 * lax.erf(value * 0.7071067811865476)
                active[rows, pl.ds(start, TILE)] = (value * phi).astype(jnp.bfloat16)
                if keep:
                    slope[rows, pl.ds(start, TILE)] = phi + value * (
                        0.3989422804014327 * jnp.exp(-0.5 * value * value)
                    )

            loop(WORDS // ROWS, inner, unroll=2)

        loop(PART // TILE, body)

    def shrink(slot, part, vec):
        for half in range(2):
            where = pl.ds(half * (D // 2), D // 2)
            out = dot_nt(active[:, pl.ds(part * PART, PART)], weight_rows(slot, half))
            if part == 0:
                total[:, where] = out + middle[:, where] + vec[:, pl.ds(7 * D + half * (D // 2), D // 2)]
            else:
                total[:, where] += out

    def turn(source, slot, out):
        def body(c):
            turned[slot, aligned(c, PAIR), :] = source[:, aligned(c, PAIR)].T

        loop(D // PAIR, body)
        send_out(turned.at[slot, group_rows], out)

    outs, late = [], []

    def send_out(src, dst, kept=outs):
        copy = pltpu.make_async_copy(src, dst, out_sem.at[len(outs) + len(late)])
        copy.start()
        kept.append(copy)

    group_rows = pl.ds(pl.multiple_of(z_at * (D // GROUP), D // GROUP), D // GROUP)

    def text_read(i):
        per = PAIR // ROWS
        return tok[i // per, aligned(lax.rem(i, per), ROWS), :]

    def text_allowed(i):
        col = seg_col[i].astype(jnp.float32)
        row = seg_row[i].astype(jnp.float32)
        return col == row[0:1, :]

    def image_read(i):
        return pic_ref[aligned(i, ROWS), :]

    def picture(axis):
        at = lax.broadcasted_iota(jnp.int32, (PAIR, PAIR), axis)
        number = at // (PAIR // 2)
        return jnp.where(lax.rem(at, PAIR // 2) < patches, number, number + 2)

    def image_allowed(i):
        return picture(0) == picture(1)

    def keep_mark():
        image = lax.broadcasted_iota(jnp.int32, (GROUP * 2, WORDS), 0)
        at = lax.broadcasted_iota(jnp.int32, (GROUP * 2, WORDS), 1)
        inside = (at // (PAIR // 2) == image) & (lax.rem(at, PAIR // 2) < patches)
        return jnp.where(inside, 1.0, 0.0)

    def text_part(s):
        slot = s
        if s == 0:
            for copy in tokens:
                copy.wait()
            first_norm(text_read, tvec_ref)
            project(slot, 0, (tvec_ref, 2))
            turn(normed, 0, nt_out)
        elif s == 1:
            project(slot, 1, None)
        elif s == 2:
            project(slot, 2, (tvec_ref, 3))
            send_out(qkv, qkv_out)
            attention_forward(qkv, mixed, chance, text_allowed)
            send_out(chance, chance_out)
            turn(mixed, 1, at_out)
        elif s == 3:
            attend(slot, text_read, tvec_ref)
            send_out(middle, mid_out)
            turn(normed_two, 2, mt_out)
        elif s < 8:
            expand(slot, s - 4, tvec_ref, True)
        else:
            if s == 8:
                send_out(active, act_out)
                send_out(slope, slope_out)
            shrink(slot, s - 8, tvec_ref)
        if s == PARTS - 1:
            send_out(total.at[aligned(z_at, PAIR)], words_out, late)
            for i in range(GROUP):
                row = seg_row[i].astype(jnp.float32)[0:8, :]
                marks = jnp.where(row == lax.broadcasted_iota(jnp.int32, (8, PAIR), 0).astype(jnp.float32), 1.0, 0.0)
                marks_out[i] = marks
                sums = jnp.dot(
                    marks, total[pl.ds(i * PAIR, PAIR), :], precision=PRECISE, preferred_element_type=jnp.float32
                )
                text_pool_out[pl.ds(i * 8, 8), :] = sums / jnp.sum(marks, axis=1, keepdims=True)

    def image_part(s):
        slot, k = s, s - PARTS
        if k == 0:
            for copy in outs:
                copy.wait()
            first_norm(image_read, ivec_ref)
            project(slot, 0, (ivec_ref, 2))
        elif k == 1:
            project(slot, 1, None)
        elif k == 2:
            project(slot, 2, (ivec_ref, 3))
            attention_forward(qkv, mixed, None, image_allowed)
        elif k == 3:
            attend(slot, image_read, ivec_ref)
            apool[...] = jnp.zeros_like(apool)
        elif k < 8:
            expand(slot, k - 4, ivec_ref, False)
            mark = keep_mark().astype(jnp.bfloat16)
            where = pl.ds((k - 4) * PART, PART)
            mean = dot(mark, active[:, where]) * (1.0 / patches)
            high = mean.astype(jnp.bfloat16)
            rest = mean - high.astype(jnp.float32)
            low = rest.astype(jnp.bfloat16)
            apool[0:8, where] = high.astype(jnp.float32)
            apool[8:16, where] = low.astype(jnp.float32)
            apool[16:24, where] = rest - low.astype(jnp.float32)
        else:
            for half in range(2):
                where = pl.ds(half * (D // 2), D // 2)
                left = apool[:, pl.ds((k - 8) * PART, PART)].astype(jnp.bfloat16)
                out = dot_nt(left, weight_rows(slot, half))
                out = out[0:8] + out[8:16] + out[16:24]
                if k == 8:
                    held = jnp.concatenate(
                        [
                            jnp.sum(middle[pl.ds(i * (PAIR // 2), patches), where], axis=0, keepdims=True)
                            for i in range(GROUP * 2)
                        ],
                        axis=0,
                    )
                    image_pool_out[:, where] = (
                        held * (1.0 / patches) + ivec_ref[:, pl.ds(7 * D + half * (D // 2), D // 2)] + out
                    )
                else:
                    image_pool_out[:, where] += out

    for s in range(count):
        for copy in own_shard(s):
            copy.start()
        if s == 1:
            for copy in firsts:
                copy.start()
    begin(0)
    for copy in tokens:
        copy.start()
    for copy in firsts:
        copy.wait()
    for s in range(1, AHEAD):
        begin(s)
    for step in range(count + AT_C):
        carry_on(step)
        s = step - AT_C
        if 0 <= s < PARTS:
            text_part(s)
        elif PARTS <= s:
            image_part(s)
    for copy in late:
        copy.wait()
    for s in range(PARTS):
        store(s).wait()
    for s in range(count):
        for j in range(2):
            for up in range(2):
                for hop in range(GROUP - 1):
                    unit = z_at - hop if up else z_at + hop
                    inside = (unit >= 0) & (unit < GROUP) & z_open[up]
                    pl.when(inside)(z_copy(s, up, unit, j).wait_send)
            for unit in range(GROUP):
                y_copy(s, 0, unit, j).wait_send()
        over_units(lambda unit: x_copy(s, unit).wait_send(), lambda: x_own_copy(s).wait_send())
        for j in range(3):
            c_copy(s, j).wait_send()


def gather_and_forward(n_dp, text_low, image_low, tokens, segments, pictures, text_vectors, image_vectors):
    own, columns = text_low.shape
    images, patches = pictures.shape[0], pictures.shape[1]
    n_inner = n_dp // GROUP
    lane_rows = own // LANES
    count = 2 * PARTS
    numbers = (segments + jnp.arange(segments.shape[0], dtype=jnp.int32)[:, None] * PER_ROW).reshape(-1)
    numbers = numbers.astype(jnp.bfloat16)
    padded = jnp.pad(pictures, ((0, 0), (0, PAIR // 2 - patches), (0, 0))).reshape(WORDS, D)
    hbm, vmem = pl.BlockSpec(memory_space=pltpu.HBM), pl.BlockSpec(memory_space=pltpu.VMEM)
    low, full = jnp.bfloat16, jnp.float32
    shape = jax.ShapeDtypeStruct
    gathered = shape((PARTS, n_dp, LANES, lane_rows, PART), low)
    turned = shape((D // GROUP, WORDS), low)
    pairs = GROUP * HEADS // 2
    dma = pltpu.SemaphoreType.DMA
    outs = pl.pallas_call(
        functools.partial(forward_kernel, n_dp, patches),
        out_shape=(
            gathered, shape((PAIR, D), full), shape((8 * GROUP, D), full), shape((images, D), full),
            shape((GROUP, 8, PAIR), full), shape((WORDS, 3 * D), low), shape((pairs, 2 * PAIR, PAIR), full),
            shape((WORDS, D), full), shape((WORDS, FF), full), shape((WORDS, FF), low), turned, turned, turned,
        ),
        in_specs=[hbm] * 5 + [vmem] * 3,
        out_specs=(hbm, hbm, vmem, vmem, vmem) + (hbm,) * 8,
        scratch_shapes=[
            pltpu.VMEM((PARTS, n_dp, LANES, lane_rows, PART), low),
            pltpu.VMEM((PARTS, n_dp, LANES, lane_rows, PART), low),
            pltpu.VMEM((GROUP, PAIR, D), low),
            pltpu.VMEM((GROUP, PAIR, PAIR), low),
            pltpu.VMEM((GROUP, 16, PAIR), low),
            pltpu.VMEM((WORDS, D), low),
            pltpu.VMEM((WORDS, 3 * D), low),
            pltpu.VMEM((WORDS, D), low),
            pltpu.VMEM((WORDS, D), full),
            pltpu.VMEM((WORDS, D), low),
            pltpu.VMEM((WORDS, FF), low),
            pltpu.VMEM((WORDS, FF), full),
            pltpu.VMEM((pairs, 2 * PAIR, PAIR), full),
            pltpu.VMEM((WORDS, D), full),
            pltpu.VMEM((WORDS, TILE), full),
            pltpu.VMEM((3, D, WORDS), low),
            pltpu.VMEM((24, FF), full),
            dma((count, 2, GROUP, 2)), dma((count, GROUP, 2)),
            dma((count, n_inner - 1, GROUP, 2)), dma((count, n_inner - 1, GROUP, 2)),
            dma((count, GROUP)), dma((count, GROUP)), dma((count, 3)), dma((count, 3)),
            dma((3, GROUP - 1)), dma((3, GROUP - 1)), dma((3,)), dma((count, 3)), dma((PARTS,)), dma((12,)),
        ],
        compiler_params=pltpu.CompilerParams(collective_id=5, has_side_effects=True, vmem_limit_bytes=60 << 20),
        name="gather_and_forward",
    )(
        text_low.reshape(LANES, lane_rows, columns), image_low.reshape(LANES, lane_rows, columns), tokens,
        jnp.broadcast_to(numbers[:, None], (PAIR, PAIR)), jnp.broadcast_to(numbers[None, :], (16, PAIR)), padded,
        text_vectors.reshape(1, -1), image_vectors.reshape(1, -1),
    )
    return (outs[0].reshape(PARTS, D, PART),) + tuple(outs[1:])


def backward_kernel(
    n_dp, n_rep,
    wt_ref, nt_ref, at_ref, mt_ref, qkv_ref, chance_ref, mid_ref, slope_ref, act_ref, feed_ref,
    tpool_ref, ipool_ref, marks_ref, tok_ref, vec_ref,
    rows_out, input_out, vector_out, loss_out,
    weight, turned, qkv, chance, middle, slope, active, grad_hidden, grad_mix, low, low_mixed, wide, block, sent, got, sums, dy_ref, e2t, pic_all, cap_all,
    load_sem, send, recv, p_send, p_recv, c_send, c_recv,
):
    n_inner = n_dp // GROUP
    d_at, r_at = lax.axis_index("dp"), lax.axis_index("rep")
    z_at, y_at = d_at // n_inner, lax.rem(d_at, n_inner)
    peer = (z_at * n_inner + 1 - y_at, r_at)
    own = D // n_dp
    share = 1.0 / GROUP

    barrier = pltpu.get_barrier_semaphore()
    devices = n_dp * n_rep
    me = d_at * n_rep + r_at

    def hello(offset, carry):
        _, other = peer_at(offset, n_dp, n_rep)
        pl.semaphore_signal(barrier, inc=1, device_id=other, device_id_type=MESH)
        return carry

    lax.fori_loop(1, devices, hello, 0)
    loads = {}

    def fetch(name, src, dst):
        copy = pltpu.make_async_copy(src, dst, load_sem.at[len(loads)])
        copy.start()
        loads[name] = copy

    def need(*names):
        for name in names:
            loads[name].wait()

    fetch("act", act_ref, active)
    for part in range(4):
        fetch(("w", 8 + part), wt_ref.at[8 + part], weight.at[8 + part])
    fetch("slope", slope_ref, slope)
    fetch("mt", mt_ref, turned.at[0])
    for part in range(4):
        fetch(("w", 4 + part), wt_ref.at[4 + part], weight.at[4 + part])
    fetch("mid", mid_ref, middle)
    fetch("at", at_ref, turned.at[1])
    fetch(("w", 3), wt_ref.at[3], weight.at[3])
    fetch("qkv", qkv_ref, qkv)
    fetch("chance", chance_ref, chance)
    fetch("nt", nt_ref, turned.at[2])
    for part in range(3):
        fetch(("w", part), wt_ref.at[part], weight.at[part])
    fetch("feed", feed_ref, rows_out)

    def exchange(s):
        return pltpu.make_async_remote_copy(
            src_ref=sent.at[s], dst_ref=got.at[s], send_sem=send.at[s], recv_sem=recv.at[s],
            device_id=peer, device_id_type=MESH,
        )

    own_rows = pl.ds(pl.multiple_of(y_at * own, own), own)
    other_rows = pl.ds(pl.multiple_of((1 - y_at) * own, own), own)

    def outer(s, left, right_of):
        def body(c):
            block[...] = dot(left, right_of(c))
            where = pl.ds(pl.multiple_of(s * PART + c * TILE, TILE), TILE)
            rows_out[:, where] = rows_out[:, where] + block[own_rows, :]
            sent[s, :, aligned(c, TILE)] = block[other_rows, :].astype(jnp.bfloat16)

        loop(PART // TILE, body)
        exchange(s).start()

    ones = jnp.ones((16, WORDS), jnp.bfloat16)

    def put(slot, values):
        for i in range(values.shape[1] // PAIR):
            vector_out[pl.ds(slot // PAIR + i, 1), :] = values[:, i * PAIR : (i + 1) * PAIR]

    def column_sums(values, slot, scale):
        put(slot, dot(ones, values)[0:1, :] * scale)


    near = n_inner * n_rep

    def near_peer(k):
        other = lax.rem(y_at * n_rep + r_at + k, near)
        return z_at * n_inner + other // n_rep, lax.rem(other, n_rep)

    def picture_copy(offset):
        _, other = peer_at(offset, n_dp, n_rep)
        return pltpu.make_async_remote_copy(
            src_ref=pic_all.at[me], dst_ref=pic_all.at[me], send_sem=p_send.at[offset - 1],
            recv_sem=p_recv.at[offset - 1], device_id=other, device_id_type=MESH,
        )

    def caption_copy(k):
        block_ = cap_all.at[:, y_at * n_rep + r_at]
        return pltpu.make_async_remote_copy(
            src_ref=block_, dst_ref=block_, send_sem=c_send.at[k - 1], recv_sem=c_recv.at[k - 1],
            device_id=near_peer(k), device_id_type=MESH,
        )

    def unit_of(values):
        return values * lax.rsqrt(jnp.sum(values * values, axis=-1, keepdims=True) + LAYER_EPS)

    def contrast():
        group_pairs = GROUP * 8
        pic_all[me] = unit_of(ipool_ref[...]).astype(jnp.bfloat16)
        for i in range(GROUP):
            cap_all[i, y_at * n_rep + r_at] = unit_of(tpool_ref[pl.ds(i * 8, 8), :]).astype(jnp.bfloat16)
        pl.semaphore_wait(barrier, devices - 1)

        def start_pictures(offset, carry):
            picture_copy(offset).start()
            return carry

        def end_pictures(offset, carry):
            picture_copy(offset).wait_recv()
            return carry

        lax.fori_loop(1, devices, start_pictures, 0)
        for k in range(1, near):
            caption_copy(k).start()
        for k in range(1, near):
            caption_copy(k).wait_recv()
        lax.fori_loop(1, devices, end_pictures, 0)
        pairs_ = devices * 8
        pics = pic_all[...].reshape(pairs_, D)
        caps = cap_all[...].reshape(pairs_, D)
        logits = dot_nt(caps, pics) * LOGIT_SCALE
        top = jnp.max(logits, axis=0, keepdims=True)
        image_log = top + jnp.log(jnp.sum(jnp.exp(logits - top), axis=0, keepdims=True))
        top = jnp.max(logits, axis=1, keepdims=True)
        caption_log = top + jnp.log(jnp.sum(jnp.exp(logits - top), axis=1, keepdims=True))
        row = lax.broadcasted_iota(jnp.int32, (pairs_, pairs_), 0)
        column = lax.broadcasted_iota(jnp.int32, (pairs_, pairs_), 1)
        matched = jnp.sum(jnp.where(row == column, logits, 0.0), axis=1, keepdims=True)
        loss = (jnp.sum(image_log) + jnp.sum(caption_log) - 2.0 * jnp.sum(matched)) / (2.0 * pairs_)
        loss_out[...] = jnp.full(loss_out.shape, loss, jnp.float32)
        pooled = tpool_ref[...]
        squares = lax.rsqrt(jnp.sum(pooled * pooled, axis=-1, keepdims=True) + LAYER_EPS)
        own_low = (pooled * squares).astype(jnp.bfloat16)
        own_logits = dot_nt(own_low, pics) * LOGIT_SCALE
        top = jnp.max(own_logits, axis=1, keepdims=True)
        own_log = top + jnp.log(jnp.sum(jnp.exp(own_logits - top), axis=1, keepdims=True))
        local = lax.broadcasted_iota(jnp.int32, (group_pairs, pairs_), 0)
        column = lax.broadcasted_iota(jnp.int32, (group_pairs, pairs_), 1)
        wanted = (local // 8) * (near * 8) + (y_at * n_rep + r_at) * 8 + lax.rem(local, 8)
        pick = jnp.where(wanted == column, 1.0, 0.0)
        soft = ((jnp.exp(own_logits - own_log) - pick) * 0.5).astype(jnp.bfloat16)
        across = ((jnp.exp(own_logits - image_log) - pick) * 0.5).astype(jnp.bfloat16)
        grad = LOGIT_SCALE * (dot(soft, pics) + dot(across, pics))
        grad = squares * (
            grad - pooled * (squares * squares) * jnp.sum(grad * pooled, axis=-1, keepdims=True)
        )
        for i in range(GROUP):
            marks = marks_ref[i]
            part = grad[i * 8 : (i + 1) * 8, :] / jnp.sum(marks, axis=1, keepdims=True)
            high, rest = split_two(part)
            rest_low = (part - high.astype(jnp.float32) - rest.astype(jnp.float32)).astype(jnp.bfloat16)
            stacked = jnp.concatenate([high, rest, rest_low], axis=0)
            marks_low = marks.astype(jnp.bfloat16)
            marks_low = jnp.concatenate([marks_low, marks_low, marks_low], axis=0)
            rows = pl.ds(i * PAIR, PAIR)
            words = dot_tn(marks_low, stacked)
            dy_ref[rows, :] = words
            low[rows, :] = words.astype(jnp.bfloat16)
            e2t[:, rows] = dot_tn(stacked, marks_low).astype(jnp.bfloat16)

    contrast()
    column_sums(low[...], 7 * D, share)
    need("act", "feed")
    for part in range(4):
        outer(8 + part, e2t[pl.ds(pl.multiple_of(z_at * (D // GROUP), D // GROUP), D // GROUP), :], lambda c: active[:, pl.ds(pl.multiple_of(part * PART + c * TILE, TILE), TILE)])
    need("slope")
    for part in range(4):
        need(("w", 8 + part))

        def hidden_body(c):
            where = pl.ds(pl.multiple_of(part * PART + c * TILE, TILE), TILE)
            out = dot(low[...], weight[8 + part, :, aligned(c, TILE)])
            grad_hidden[:, where] = (out * slope[:, where]).astype(jnp.bfloat16)

        loop(PART // TILE, hidden_body)
        column_sums(grad_hidden[:, pl.ds(part * PART, PART)], 8 * D + part * PART, share)
    need("mt")
    for part in range(4):
        outer(
            4 + part, turned[0], lambda c: grad_hidden[:, pl.ds(pl.multiple_of(part * PART + c * TILE, TILE), TILE)]
        )
    for part in range(4):
        need(("w", 4 + part))
    for half in range(2):
        rows = pl.ds(half * (D // 2), D // 2)
        out = dot_nt(grad_hidden[:, pl.ds(0, PART)], weight[4, rows, :])
        for part in range(1, 4):
            out = out + dot_nt(grad_hidden[:, pl.ds(part * PART, PART)], weight[4 + part, rows, :])
        wide[:, rows] = out
    need("mid")

    def norm_back(value, grad, gain):
        center = value - jnp.mean(value, axis=-1, keepdims=True)
        scale = lax.rsqrt(jnp.mean(center * center, axis=-1, keepdims=True) + LAYER_EPS)
        unit = center * scale
        inner = grad * gain
        out = scale * (
            inner - jnp.mean(inner, axis=-1, keepdims=True) - unit * jnp.mean(inner * unit, axis=-1, keepdims=True)
        )
        return out, grad * unit

    def fold(values):
        return jnp.sum(values.reshape(ROWS // 8, 8, D), axis=0)

    sums[...] = jnp.zeros_like(sums)

    def second(i):
        rows = aligned(i, ROWS)
        grad = wide[rows, :]
        out, product = norm_back(middle[rows, :], grad, piece_of(vec_ref, 5))
        sums[0] += fold(product)
        sums[1] += fold(grad)
        out = out + dy_ref[rows, :]
        middle[rows, :] = out
        low[rows, :] = out.astype(jnp.bfloat16)

    loop(WORDS // ROWS, second)
    put(5 * D, jnp.sum(sums[0], axis=0, keepdims=True) * share)
    put(6 * D, jnp.sum(sums[1], axis=0, keepdims=True) * share)
    column_sums(low[...], 4 * D, share)
    need("at")
    outer(3, turned[1], lambda c: low[:, aligned(c, TILE)])
    need(("w", 3))
    for half in range(2):
        rows = pl.ds(half * (D // 2), D // 2)
        low_mixed[:, rows] = dot_nt(low[...], weight[3, rows, :]).astype(jnp.bfloat16)
    need("qkv", "chance")
    pairs = HEADS // 2

    def attention(at):
        i, j = at // pairs, lax.rem(at, pairs)
        rows = aligned(i, PAIR)
        q_cols = aligned(j, PAIR)
        k_cols = pl.ds(pl.multiple_of(D + j * PAIR, PAIR), PAIR)
        v_cols = pl.ds(pl.multiple_of(2 * D + j * PAIR, PAIR), PAIR)
        query, key, value = qkv[rows, q_cols], qkv[rows, k_cols], qkv[rows, v_cols]
        grad = two_heads(low_mixed[rows, q_cols])
        weight_ = chance[at]
        grad_mix[rows, v_cols] = dot_tn(weight_.astype(jnp.bfloat16), grad).astype(jnp.bfloat16)
        back = dot_nt(grad, value)
        back = weight_ * (back - jnp.sum(weight_ * back, axis=-1, keepdims=True))
        back = back.astype(jnp.bfloat16)
        side = jnp.concatenate([back[:PAIR], back[PAIR:]], axis=1)
        grad_mix[rows, q_cols] = (dot(side, two_heads(key)) * SCORE_SCALE).astype(jnp.bfloat16)
        grad_mix[rows, k_cols] = (dot_tn(back, two_heads(query)) * SCORE_SCALE).astype(jnp.bfloat16)

    loop(GROUP * pairs, attention, unroll=2)
    need("nt")
    for part in range(3):
        outer(part, turned[2], lambda c: grad_mix[:, pl.ds(pl.multiple_of(part * PART + c * TILE, TILE), TILE)])
    column_sums(grad_mix[:, pl.ds(0, D)], 2 * D, share)
    column_sums(grad_mix[:, pl.ds(2 * D, D)], 3 * D, share)
    for part in range(3):
        need(("w", part))
    mine = aligned(z_at, PAIR)
    for half in range(2):
        rows = pl.ds(half * (D // 2), D // 2)
        out = dot_nt(grad_mix[mine, pl.ds(0, PART)], weight[0, rows, :])
        for part in range(1, 3):
            out = out + dot_nt(grad_mix[mine, pl.ds(part * PART, PART)], weight[part, rows, :])
        wide[pl.ds(0, PAIR), rows] = out
    sums[...] = jnp.zeros_like(sums)

    def first(i):
        rows = aligned(i, ROWS)
        grad = wide[rows, :]
        out, product = norm_back(tok_ref[rows, :].astype(jnp.float32), grad, piece_of(vec_ref, 0))
        sums[0] += fold(product)
        sums[1] += fold(grad)
        input_out[rows, :] = out + middle[pl.ds(pl.multiple_of(z_at * PAIR + i * ROWS, ROWS), ROWS), :]

    loop(PAIR // ROWS, first)
    put(0, jnp.sum(sums[0], axis=0, keepdims=True))
    put(D, jnp.sum(sums[1], axis=0, keepdims=True))
    for s in (8, 9, 10, 11, 4, 5, 6, 7, 3, 0, 1, 2):
        exchange(s).wait_recv()

        def add(c):
            where = pl.ds(pl.multiple_of(s * PART + c * TILE, TILE), TILE)
            rows_out[:, where] = rows_out[:, where] + got[s, :, aligned(c, TILE)].astype(jnp.float32)

        loop(PART // TILE, add)
    for s in range(PARTS):
        exchange(s).wait_send()
    for k in range(1, near):
        caption_copy(k).wait_send()

    def end_sends(offset, carry):
        picture_copy(offset).wait_send()
        return carry

    lax.fori_loop(1, devices, end_sends, 0)


def backward(n_dp, n_rep, kept, pooled, image_pooled, marks, tokens, text_vectors, feedback_rows):
    weights, qkv, chance, middle, slope, active, n_turned, a_turned, m_turned = kept
    own = feedback_rows.shape[0]
    hbm, vmem = pl.BlockSpec(memory_space=pltpu.HBM), pl.BlockSpec(memory_space=pltpu.VMEM)
    low, full = jnp.bfloat16, jnp.float32
    shape = jax.ShapeDtypeStruct
    dma = pltpu.SemaphoreType.DMA
    pairs = GROUP * HEADS // 2
    return pl.pallas_call(
        functools.partial(backward_kernel, n_dp, n_rep),
        out_shape=(shape(feedback_rows.shape, full), shape((PAIR, D), full), shape((12 * D // PAIR, PAIR), full), shape((8, PAIR), full)),
        in_specs=[hbm] * 10 + [vmem] * 5,
        out_specs=(vmem,) * 4,
        scratch_shapes=[
            pltpu.VMEM((PARTS, D, PART), low),
            pltpu.VMEM((3, D // GROUP, WORDS), low),
            pltpu.VMEM((WORDS, 3 * D), low),
            pltpu.VMEM((pairs, 2 * PAIR, PAIR), full),
            pltpu.VMEM((WORDS, D), full),
            pltpu.VMEM((WORDS, FF), full),
            pltpu.VMEM((WORDS, FF), low),
            pltpu.VMEM((WORDS, FF), low),
            pltpu.VMEM((WORDS, 3 * D), low),
            pltpu.VMEM((WORDS, D), low),
            pltpu.VMEM((WORDS, D), low),
            pltpu.VMEM((WORDS, D), full),
            pltpu.VMEM((D // GROUP, TILE), full),
            pltpu.VMEM((PARTS, own, PART), low),
            pltpu.VMEM((PARTS, own, PART), low),
            pltpu.VMEM((2, 8, D), full),
            pltpu.VMEM((WORDS, D), full),
            pltpu.VMEM((D, WORDS), low),
            pltpu.VMEM((n_dp * n_rep, 8, D), low),
            pltpu.VMEM((GROUP, n_dp * n_rep // GROUP, 8, D), low),
            dma((24,)), dma((PARTS,)), dma((PARTS,)),
            dma((n_dp * n_rep - 1,)), dma((n_dp * n_rep - 1,)), dma((8,)), dma((8,)),
        ],
        compiler_params=pltpu.CompilerParams(collective_id=6, has_side_effects=True, vmem_limit_bytes=60 << 20),
        name="backward",
    )(
        weights, n_turned, a_turned, m_turned, qkv, chance, middle, slope, active, feedback_rows,
        pooled, image_pooled, marks, tokens, text_vectors.reshape(1, -1),
    )


EXTRA = 9
OWN_TILES = 3


def split_two(values):
    high = values.astype(jnp.bfloat16)
    return high, (values - high.astype(jnp.float32)).astype(jnp.bfloat16)


def power_kernel(
    n_dp, n_rep,
    rows_ref, start_ref, vgrad_ref, vec_ref, vmom_ref,
    left_out, right_out, nvec_out, nvmom_out,
    rows, factor, factor_rep, factor_dp, basis, tiles, tiles_rep, quarter, tiles_dp, everything,
    load_sem, send, recv,
):
    d_at, r_at = lax.axis_index("dp"), lax.axis_index("rep")
    own = rows.shape[0]
    bounds = matrix_bounds()
    rank = start_ref.shape[0]
    strip = n_dp * OWN_TILES
    load = pltpu.make_async_copy(rows_ref, rows, load_sem)
    load.start()
    rep_peers = [(d_at, lax.rem(r_at + k, n_rep)) for k in range(1, n_rep)]
    dp_peers = [(lax.rem(d_at + k, n_dp), r_at) for k in range(1, n_dp)]
    barrier = pltpu.get_barrier_semaphore()
    for peer in rep_peers + dp_peers:
        pl.semaphore_signal(barrier, inc=1, device_id=peer, device_id_type=MESH)

    def remote(phase, k, src, dst, peer):
        return pltpu.make_async_remote_copy(
            src_ref=src, dst_ref=dst, send_sem=send.at[phase, k], recv_sem=recv.at[phase, k],
            device_id=peer, device_id_type=MESH,
        )

    phases = [
        [remote(0, k, factor, factor_rep.at[k], peer) for k, peer in enumerate(rep_peers)],
        [remote(1, k, factor_dp.at[d_at], factor_dp.at[d_at], peer) for k, peer in enumerate(dp_peers)],
        [
            remote(2, k, tiles.at[pl.ds(peer[1] * strip, strip)], tiles_rep.at[k], peer)
            for k, peer in enumerate(rep_peers)
        ],
        [
            remote(3, k, quarter.at[pl.ds(peer[0] * OWN_TILES, OWN_TILES)], tiles_dp.at[k], peer)
            for k, peer in enumerate(dp_peers)
        ],
    ]
    mine = pl.ds(r_at * strip + d_at * OWN_TILES, OWN_TILES)
    strip_mine = pl.ds(r_at * strip, strip)
    phases.append([remote(4, k, everything.at[mine], everything.at[mine], peer) for k, peer in enumerate(dp_peers)])
    phases.append(
        [remote(5, k, everything.at[strip_mine], everything.at[strip_mine], peer) for k, peer in enumerate(rep_peers)]
    )

    def begin(phase):
        for copy in phases[phase]:
            copy.start()

    def arrived(phase):
        for copy in phases[phase]:
            copy.wait_recv()

    factor[...] = jnp.zeros_like(factor)
    load.wait()
    for matrix, (first_col, after_col) in enumerate(bounds):
        total = jnp.zeros((2 * rank, own), jnp.float32)
        rest = jnp.zeros((2 * rank, own), jnp.float32)
        for at in range(first_col, after_col, PART):
            high, low = split_two(rows[:, pl.ds(at, PART)])
            start_high, start_low = split_two(start_ref[:, pl.ds(at, PART)])
            both = jnp.concatenate([start_high, start_low], axis=0)
            total = total + dot_nt(both, high)
            rest = rest + dot_nt(both, low)
        factor[pl.ds(matrix * rank, rank), pl.ds(0, own)] = total[:rank] + total[rank:] + rest[:rank]
    pl.semaphore_wait(barrier, len(rep_peers + dp_peers))
    begin(0)
    arrived(0)
    summed = factor[...]
    for k in range(n_rep - 1):
        summed = summed + factor_rep[k]
    factor_dp[d_at] = summed
    begin(1)
    arrived(1)
    vectors = jnp.concatenate([factor_dp[i] for i in range(n_dp)], axis=1).reshape(4, rank, n_dp * PAIR)
    place = lax.broadcasted_iota(jnp.int32, (4, rank, 1), 1)
    for k in range(rank):
        vector = vectors[:, k : k + 1, :]
        size = jnp.sqrt(jnp.sum(vector * vector, axis=-1, keepdims=True)) + NORM_FLOOR
        vector = vector / size
        along = jnp.sum(vector * vectors, axis=-1, keepdims=True)
        vectors = jnp.where(
            place == k, jnp.broadcast_to(vector, vectors.shape),
            vectors - jnp.where(place > k, along, 0.0) * vector,
        )
    vectors = vectors.reshape(4 * rank, n_dp * PAIR)
    basis[...] = vectors
    left_out[...] = vectors
    basis_high, basis_low = split_two(basis[:, aligned(d_at, PAIR)][:, :own])
    for matrix, (first_col, after_col) in enumerate(bounds):
        where = slice(matrix * rank, (matrix + 1) * rank)
        both = jnp.concatenate([basis_high[where], basis_low[where]], axis=0)

        def project(c):
            high, low = split_two(rows[:, pl.ds(pl.multiple_of(first_col + c * TILE, TILE), TILE)])
            out = dot(both, high)
            out = out[:rank] + out[rank:] + dot(both, low)[:rank]
            at = first_col // PAIR + c * (TILE // PAIR)
            for half in range(TILE // PAIR):
                tiles[at + half] = out[:, half * PAIR : (half + 1) * PAIR]

        loop((after_col - first_col) // TILE, project, unroll=3)
    columns = bounds[-1][1] // PAIR
    for i in range(EXTRA):
        tiles[columns + i] = vgrad_ref[pl.ds(i * 8, 8), :]
    for i in range(columns + EXTRA, n_rep * strip):
        tiles[i] = jnp.zeros((8, PAIR), jnp.float32)
    begin(2)
    arrived(2)
    value = tiles[strip_mine]
    for k in range(n_rep - 1):
        value = value + tiles_rep[k]
    quarter[...] = value
    begin(3)
    arrived(3)
    value = quarter[pl.ds(d_at * OWN_TILES, OWN_TILES)]
    for k in range(n_dp - 1):
        value = value + tiles_dp[k]
    everything[mine] = value
    begin(4)
    arrived(4)
    begin(5)
    arrived(5)
    for i in range(columns):
        right_out[:, pl.ds(i * PAIR, PAIR)] = everything[i]
    for i in range(EXTRA):
        at = pl.ds(i * 8, 8)
        moved = MOMENTUM_DECAY * vmom_ref[at, :] + everything[columns + i]
        nvmom_out[at, :] = moved
        nvec_out[at, :] = vec_ref[at, :] - STEP_RATE * moved
    for phase in phases:
        for copy in phase:
            copy.wait_send()


def power_step(n_dp, n_rep, rows, start, vector_grad, vectors, vector_momentum):
    own, columns = rows.shape
    rank = start.shape[0]
    hbm, vmem = pl.BlockSpec(memory_space=pltpu.HBM), pl.BlockSpec(memory_space=pltpu.VMEM)
    full = jnp.float32
    shape = jax.ShapeDtypeStruct
    dma = pltpu.SemaphoreType.DMA
    strip = n_dp * OWN_TILES
    flat = (columns // PAIR, PAIR)
    left, right, new_vectors, new_vector_momentum = pl.pallas_call(
        functools.partial(power_kernel, n_dp, n_rep),
        out_shape=(
            shape((4 * rank, n_dp * PAIR), full), shape(start.shape, full), shape(flat, full), shape(flat, full),
        ),
        in_specs=[hbm, vmem, vmem, vmem, vmem],
        out_specs=(vmem,) * 4,
        scratch_shapes=[
            pltpu.VMEM(rows.shape, full),
            pltpu.VMEM((4 * rank, PAIR), full),
            pltpu.VMEM((n_rep - 1, 4 * rank, PAIR), full),
            pltpu.VMEM((n_dp, 4 * rank, PAIR), full),
            pltpu.VMEM((4 * rank, n_dp * PAIR), full),
            pltpu.VMEM((n_rep * strip, 8, PAIR), full),
            pltpu.VMEM((n_rep - 1, strip, 8, PAIR), full),
            pltpu.VMEM((strip, 8, PAIR), full),
            pltpu.VMEM((n_dp - 1, OWN_TILES, 8, PAIR), full),
            pltpu.VMEM((n_rep * strip, 8, PAIR), full),
            dma, dma((6, n_dp - 1)), dma((6, n_dp - 1)),
        ],
        compiler_params=pltpu.CompilerParams(collective_id=7, has_side_effects=True, vmem_limit_bytes=60 << 20),
        name="power_step",
    )(rows, start, vector_grad, vectors.reshape(flat), vector_momentum.reshape(flat))
    return left, right, new_vectors.reshape(-1), new_vector_momentum.reshape(-1)


CHUNKS = 4


def finish_kernel(
    n_dp, n_rep,
    rows_ref, mom_ref, wts_ref, words_ref, input_ref, left_ref, right_ref,
    feed_out, mom_out, wts_out, words_out, input_out, left_out, right_out,
    rows, mom, wts, change, load_sem, store_sem, pass_sem,
):
    own = rows.shape[0]
    piece = own // CHUNKS
    rank = right_ref.shape[0]

    def load(i, j):
        src, dst = ((rows_ref, rows), (mom_ref, mom), (wts_ref, wts))[j]
        span = pl.ds(i * piece, piece)
        return pltpu.make_async_copy(src.at[span], dst.at[span], load_sem.at[i, j])

    def store(i, j):
        src, dst = ((rows, feed_out), (mom, mom_out), (wts, wts_out))[j]
        span = pl.ds(i * piece, piece)
        return pltpu.make_async_copy(src.at[span], dst.at[span], store_sem.at[i, j])

    for i in range(CHUNKS):
        for j in range(3):
            load(i, j).start()
    passed = [
        pltpu.make_async_copy(src, dst, pass_sem.at[i])
        for i, (src, dst) in enumerate(((words_ref, words_out), (input_ref, input_out), (right_ref, right_out)))
    ]
    for copy in passed:
        copy.start()
    left_out[...] = jnp.concatenate([left_ref[:, i * PAIR : i * PAIR + own] for i in range(n_dp)], axis=1)
    basis_high, basis_low = split_two(left_ref[:, aligned(lax.axis_index("dp"), PAIR)][:, :own])
    for matrix, (first_col, after_col) in enumerate(matrix_bounds()):
        where = slice(matrix * rank, (matrix + 1) * rank)
        left = jnp.concatenate([basis_high[where], basis_high[where], basis_low[where]], axis=0)

        def approximate(c):
            cols = pl.ds(pl.multiple_of(first_col + c * PART, PART), PART)
            high, low = split_two(right_ref[:, cols])
            change[:, cols] = dot_tn(left, jnp.concatenate([high, low, high], axis=0))

        loop((after_col - first_col) // PART, approximate)
    for i in range(CHUNKS):
        for j in range(3):
            load(i, j).wait()

        def update(c):
            span, cols = pl.ds(i * piece, piece), aligned(c, PART)
            delta = change[span, cols]
            rows[span, cols] = rows[span, cols] - delta * (1.0 / n_rep)
            moved = MOMENTUM_DECAY * mom[span, cols] + delta
            mom[span, cols] = moved
            wts[span, cols] = wts[span, cols] - STEP_RATE * moved

        loop(rows.shape[1] // PART, update)
        for j in range(3):
            store(i, j).start()
    for copy in passed:
        copy.wait()
    for i in range(CHUNKS):
        for j in range(3):
            store(i, j).wait()


def finish(n_dp, n_rep, rows, momentum, weights, left, right, words, grad_inputs):
    own, columns = rows.shape
    hbm, vmem = pl.BlockSpec(memory_space=pltpu.HBM), pl.BlockSpec(memory_space=pltpu.VMEM)
    full = jnp.float32
    shape = jax.ShapeDtypeStruct
    dma = pltpu.SemaphoreType.DMA
    big = shape(rows.shape, full)
    return pl.pallas_call(
        functools.partial(finish_kernel, n_dp, n_rep),
        out_shape=(
            big, big, big, shape(words.shape, full), shape(grad_inputs.shape, full),
            shape((left.shape[0], n_dp * own), full), shape(right.shape, full),
        ),
        in_specs=[hbm] * 5 + [vmem] * 2,
        out_specs=(hbm,) * 5 + (vmem, hbm),
        scratch_shapes=[pltpu.VMEM(rows.shape, full)] * 4 + [dma((CHUNKS, 3)), dma((CHUNKS, 3)), dma((3,))],
        compiler_params=pltpu.CompilerParams(vmem_limit_bytes=60 << 20),
        name="finish",
    )(rows, momentum, weights, words, grad_inputs, left, right)


def peer_at(offset, n_dp, n_rep):
    me = lax.axis_index("dp") * n_rep + lax.axis_index("rep")
    other = lax.rem(me + offset, n_dp * n_rep)
    return other, (other // n_rep, lax.rem(other, n_rep))


def meet(n_dp, n_rep):
    total = n_dp * n_rep
    barrier = pltpu.get_barrier_semaphore()

    def hello(offset, carry):
        _, peer = peer_at(offset, n_dp, n_rep)
        pl.semaphore_signal(barrier, inc=1, device_id=peer, device_id_type=MESH)
        return carry

    lax.fori_loop(1, total, hello, 0)
    pl.semaphore_wait(barrier, total - 1)


def spread_kernel(n_dp, n_rep, mine_ref, all_ref, send, recv, own_sem):
    total = n_dp * n_rep
    me = lax.axis_index("dp") * n_rep + lax.axis_index("rep")
    own = pltpu.make_async_copy(mine_ref, all_ref.at[me], own_sem)
    own.start()
    meet(n_dp, n_rep)

    def copy(offset):
        _, peer = peer_at(offset, n_dp, n_rep)
        return pltpu.make_async_remote_copy(
            src_ref=mine_ref, dst_ref=all_ref.at[me], send_sem=send.at[offset - 1],
            recv_sem=recv.at[offset - 1], device_id=peer, device_id_type=MESH,
        )

    def begin(offset, carry):
        copy(offset).start()
        return carry

    def finish(offset, carry):
        copy(offset).wait()
        return carry

    lax.fori_loop(1, total, begin, 0)
    own.wait()
    lax.fori_loop(1, total, finish, 0)


def spread(mine, n_dp, n_rep, collective, name):
    total = n_dp * n_rep
    vmem = pl.BlockSpec(memory_space=pltpu.VMEM)
    dma = pltpu.SemaphoreType.DMA
    return pl.pallas_call(
        functools.partial(spread_kernel, n_dp, n_rep),
        out_shape=jax.ShapeDtypeStruct((total,) + mine.shape, mine.dtype),
        in_specs=[vmem],
        out_specs=vmem,
        scratch_shapes=[dma((total - 1,)), dma((total - 1,)), dma],
        compiler_params=pltpu.CompilerParams(
            collective_id=collective, has_side_effects=True, vmem_limit_bytes=48 << 20
        ),
        name=name,
    )(mine)


def total_kernel(n_dp, n_rep, mine_ref, out_ref, parts, sums, send, recv, send_two, recv_two):
    total = n_dp * n_rep
    me = lax.axis_index("dp") * n_rep + lax.axis_index("rep")
    meet(n_dp, n_rep)

    def scatter(offset):
        other, peer = peer_at(offset, n_dp, n_rep)
        return pltpu.make_async_remote_copy(
            src_ref=mine_ref.at[other], dst_ref=parts.at[offset - 1], send_sem=send.at[offset - 1],
            recv_sem=recv.at[offset - 1], device_id=peer, device_id_type=MESH,
        )

    def share(offset):
        _, peer = peer_at(offset, n_dp, n_rep)
        return pltpu.make_async_remote_copy(
            src_ref=sums, dst_ref=out_ref.at[me], send_sem=send_two.at[offset - 1],
            recv_sem=recv_two.at[offset - 1], device_id=peer, device_id_type=MESH,
        )

    def start_scatter(offset, carry):
        scatter(offset).start()
        return carry

    def add(offset, carry):
        scatter(offset).wait_recv()
        return carry + parts[offset - 1]

    def start_share(offset, carry):
        share(offset).start()
        return carry

    def finish(offset, carry):
        scatter(offset).wait_send()
        share(offset).wait()
        return carry

    lax.fori_loop(1, total, start_scatter, 0)
    result = lax.fori_loop(1, total, add, mine_ref[me])
    sums[...] = result
    lax.fori_loop(1, total, start_share, 0)
    out_ref[me] = result
    lax.fori_loop(1, total, finish, 0)


def total_over_all(flat, n_dp, n_rep, collective, name):
    total = n_dp * n_rep
    count = flat.shape[0]
    chunk = -(-count // (total * 1024)) * 1024
    padded = jnp.pad(flat, (0, total * chunk - count)).reshape(total, chunk // 128, 128)
    vmem = pl.BlockSpec(memory_space=pltpu.VMEM)
    dma = pltpu.SemaphoreType.DMA
    summed = pl.pallas_call(
        functools.partial(total_kernel, n_dp, n_rep),
        out_shape=jax.ShapeDtypeStruct(padded.shape, padded.dtype),
        in_specs=[vmem],
        out_specs=vmem,
        scratch_shapes=[
            pltpu.VMEM((total - 1,) + padded.shape[1:], padded.dtype),
            pltpu.VMEM(padded.shape[1:], padded.dtype),
            dma((total - 1,)), dma((total - 1,)), dma((total - 1,)), dma((total - 1,)),
        ],
        compiler_params=pltpu.CompilerParams(
            collective_id=collective, has_side_effects=True, vmem_limit_bytes=48 << 20
        ),
        name=name,
    )(padded)
    return summed.reshape(-1)[:count]


def masked_scores(query_heads, key_heads, allowed):
    scores = (
        jnp.einsum("rshd,rthd->rhst", query_heads, key_heads, preferred_element_type=jnp.float32)
        * SCORE_SCALE
    )
    return jnp.where(allowed[:, None], scores, MASKED)


def block_forward(inputs, allowed, weights, vector_pieces, pooled_only):
    (
        gain_one, shift_one, bias_query, bias_value, bias_out,
        gain_two, shift_two, bias_shrink, bias_expand,
    ) = vector_pieces
    row_count, seq_tokens = (inputs.shape[0], inputs.shape[1])
    normed = layer_norm(inputs, gain_one, shift_one).astype(jnp.bfloat16)
    mixing = jnp.einsum("rsd,dc->rsc", normed, weights[:, : 3 * D], preferred_element_type=jnp.float32)
    mixing = mixing + jnp.concatenate([bias_query, jnp.zeros_like(bias_query), bias_value])
    head_parts = mixing.astype(jnp.bfloat16).reshape(row_count, seq_tokens, 3, HEADS, HEAD_DIM)
    query_heads, key_heads, value_heads = (head_parts[:, :, 0], head_parts[:, :, 1], head_parts[:, :, 2])
    scores = masked_scores(query_heads, key_heads, allowed)
    highest = jnp.max(scores, axis=-1, keepdims=True)
    log_total = highest + jnp.log(jnp.sum(jnp.exp(scores - highest), axis=-1, keepdims=True))
    attention = jnp.exp(scores - log_total).astype(jnp.bfloat16)
    mixed_heads = jnp.einsum("rhst,rthd->rshd", attention, value_heads, preferred_element_type=jnp.float32)
    mixed_heads = mixed_heads.reshape(row_count, seq_tokens, D).astype(jnp.bfloat16)
    attended = (
        jnp.einsum("rsd,de->rse", mixed_heads, weights[:, 3 * D : 4 * D], preferred_element_type=jnp.float32)
        + bias_out
    )
    middle = inputs + attended
    normed_two = layer_norm(middle, gain_two, shift_two).astype(jnp.bfloat16)
    hidden = (
        jnp.einsum("rsd,df->rsf", normed_two, weights[:, 4 * D : 4 * D + FF], preferred_element_type=jnp.float32)
        + bias_expand
    )
    active = jax.nn.gelu(hidden, approximate=False).astype(jnp.bfloat16)
    shrink = weights[:, 4 * D + FF :]
    if pooled_only:
        mean_active = jnp.mean(active.astype(jnp.float32), axis=1)
        high = mean_active.astype(jnp.bfloat16)
        rest = mean_active - high.astype(jnp.float32)
        low = rest.astype(jnp.bfloat16)
        lower = (rest - low.astype(jnp.float32)).astype(jnp.bfloat16)
        stacked = jnp.concatenate([high, low, lower], axis=0)
        shrunk = jnp.einsum("pf,df->pd", stacked, shrink, preferred_element_type=jnp.float32)
        shrunk = jnp.sum(shrunk.reshape(3, row_count, D), axis=0)
        return jnp.mean(middle, axis=1) + shrunk + bias_shrink
    shrunk = jnp.einsum("rsf,df->rsd", active, shrink, preferred_element_type=jnp.float32) + bias_shrink
    kept = (normed, query_heads, key_heads, value_heads, log_total, mixed_heads, middle, normed_two, hidden, active)
    return (middle + shrunk, kept)


def token_sum(values_low):
    return jnp.sum(values_low.astype(jnp.float32).reshape(-1, values_low.shape[-1]), axis=0)


def block_backward(inputs, allowed, weights, vector_pieces, forward_kept, grad_out, own_group, own_count):
    (gain_one, shift_one, _, _, _, gain_two, shift_two, _, _) = vector_pieces
    (normed, query_heads, key_heads, value_heads, log_total, mixed_heads, middle, normed_two, hidden, active) = forward_kept
    row_count, seq_tokens = (inputs.shape[0], inputs.shape[1])
    grad_shrunk = grad_out.astype(jnp.bfloat16)
    grad_active = jnp.einsum("rsd,df->rsf", grad_shrunk, weights[:, 4 * D + FF :], preferred_element_type=jnp.float32)
    _, gelu_back = jax.vjp(lambda before_gelu: jax.nn.gelu(before_gelu, approximate=False), hidden)
    grad_hidden = gelu_back(grad_active)[0].astype(jnp.bfloat16)
    grad_normed_two = jnp.einsum(
        "rsf,df->rsd", grad_hidden, weights[:, 4 * D : 4 * D + FF], preferred_element_type=jnp.float32
    )
    _, norm_two_back = jax.vjp(layer_norm, middle, gain_two, shift_two)
    grad_middle, grad_gain_two, grad_shift_two = norm_two_back(grad_normed_two)
    grad_middle = grad_middle + grad_out
    grad_attended = grad_middle.astype(jnp.bfloat16)
    grad_mixed = jnp.einsum("rse,de->rsd", grad_attended, weights[:, 3 * D : 4 * D], preferred_element_type=jnp.float32)
    grad_mixed = grad_mixed.astype(jnp.bfloat16).reshape(row_count, seq_tokens, HEADS, HEAD_DIM)
    attention = jnp.exp(masked_scores(query_heads, key_heads, allowed) - log_total)
    grad_values = jnp.einsum("rhst,rshd->rthd", attention.astype(jnp.bfloat16), grad_mixed, preferred_element_type=jnp.float32)
    grad_attention = jnp.einsum("rshd,rthd->rhst", grad_mixed, value_heads, preferred_element_type=jnp.float32)
    grad_scores = attention * (grad_attention - jnp.sum(attention * grad_attention, axis=-1, keepdims=True))
    grad_scores = grad_scores.astype(jnp.bfloat16)
    grad_query = jnp.einsum("rhst,rthd->rshd", grad_scores, key_heads, preferred_element_type=jnp.float32) * SCORE_SCALE
    grad_keys = jnp.einsum("rhst,rshd->rthd", grad_scores, query_heads, preferred_element_type=jnp.float32) * SCORE_SCALE
    grad_mixing = (
        jnp.stack([grad_query, grad_keys, grad_values], axis=2).reshape(row_count, seq_tokens, 3 * D).astype(jnp.bfloat16)
    )

    def mine(values):
        return lax.dynamic_slice_in_dim(values, own_group * own_count, own_count, 0)

    grad_normed = jnp.einsum("rsc,dc->rsd", mine(grad_mixing), weights[:, : 3 * D], preferred_element_type=jnp.float32)
    _, norm_one_back = jax.vjp(layer_norm, mine(inputs), gain_one, shift_one)
    grad_inputs, grad_gain_one, grad_shift_one = norm_one_back(grad_normed)
    grad_inputs = grad_inputs + mine(grad_middle)
    share = 1.0 / GROUP
    vector_grad = jnp.concatenate(
        [
            grad_gain_one, grad_shift_one,
            share * token_sum(grad_mixing[..., :D]), share * token_sum(grad_mixing[..., 2 * D :]),
            share * token_sum(grad_attended), share * grad_gain_two, share * grad_shift_two,
            share * token_sum(grad_shrunk), share * token_sum(grad_hidden),
        ]
    )
    tokens = row_count * seq_tokens
    outer_terms = (
        (normed.reshape(tokens, D), grad_mixing.reshape(tokens, 3 * D)),
        (mixed_heads.reshape(tokens, D), grad_attended.reshape(tokens, D)),
        (normed_two.reshape(tokens, D), grad_hidden.reshape(tokens, FF)),
        (grad_shrunk.reshape(tokens, D), active.reshape(tokens, FF)),
    )
    return (grad_inputs, vector_grad, outer_terms)


def orthonormal(stacked):
    waiting = [stacked[:, column_id] for column_id in range(stacked.shape[1])]
    finished = []
    while waiting:
        vector = waiting.pop(0)
        vector = vector / (jnp.sqrt(jnp.sum(vector * vector, axis=-1, keepdims=True)) + NORM_FLOOR)
        finished.append(vector)
        if waiting:
            later = jnp.stack(waiting, axis=1)
            later = later - jnp.sum(vector[:, None] * later, axis=-1, keepdims=True) * vector[:, None]
            waiting = [later[:, i] for i in range(later.shape[1])]
    return jnp.stack(finished, axis=1)


def rows_factor(start_part, row_block):
    return jnp.einsum("kc,dc->kd", start_part, row_block, precision=PRECISE)


def per_device(
    image_tokens, image_weights, image_vectors, text_tokens, segments, text_weights,
    text_vectors, momentum, vector_momentum, error_feedback, start_factors,
):
    n_rep, n_dp = lax.axis_size("rep"), lax.axis_size("dp")
    n_inner = n_dp // GROUP
    total = n_rep * n_dp
    device_pairs, patches = image_tokens.shape[0], image_tokens.shape[1]
    text_rows, seq_tokens = text_tokens.shape[0], text_tokens.shape[1]
    pair_total = device_pairs * total
    own_rows = text_weights.shape[0]
    d_at, r_at = lax.axis_index("dp"), lax.axis_index("rep")
    z_at, y_at = d_at // n_inner, d_at % n_inner
    row_start = d_at * own_rows
    factor_rank = start_factors.shape[0]
    bounds = matrix_bounds()
    tokens = text_tokens.reshape(text_rows * seq_tokens, D)
    words_low = text_weights.astype(jnp.bfloat16)
    feedback_rows = error_feedback[0]
    fused = (
        own_rows % (16 * LANES) == 0 and n_inner == 2 and n_rep == 4 and device_pairs == 8
        and text_rows * seq_tokens == PAIR and 2 * seq_tokens == PAIR and 2 * patches <= PAIR
        and n_dp == 8 and factor_rank == 8
    )
    if fused:
        outs = gather_and_forward(
            n_dp, words_low, image_weights, tokens, segments, image_tokens, text_vectors, image_vectors
        )
        words, pooled, image_pooled, marks = outs[1:5]
        kept = (outs[0],) + tuple(outs[5:])
        worker_rows, grad_inputs, vector_grad, loss = backward(
            n_dp, n_rep, kept, pooled, image_pooled, marks, tokens, text_vectors, feedback_rows
        )
        left_basis, new_right, new_vectors, new_vector_momentum = power_step(
            n_dp, n_rep, worker_rows, start_factors, vector_grad, text_vectors, vector_momentum
        )
        new_feedback, new_momentum, new_weights, words, grad_inputs, left_basis, new_right = finish(
            n_dp, n_rep, worker_rows, momentum, text_weights, left_basis, new_right, words, grad_inputs
        )
        return (
            loss[0, 0], words.reshape(text_rows, seq_tokens, D), grad_inputs.reshape(text_rows, seq_tokens, D),
            new_weights, new_momentum, new_feedback[None], new_vectors, new_vector_momentum, left_basis, new_right,
        )
    text_low, frozen, token_group, segment_group = gather_weights(
        n_dp, words_low, image_weights, tokens, segments
    )
    text_low, frozen = text_low.reshape(D, -1), frozen.reshape(D, -1)
    full_mask = jnp.zeros((device_pairs, patches, patches), jnp.int32) == 0
    image_pooled = block_forward(
        image_tokens.astype(jnp.float32), full_mask, frozen, vector_parts(image_vectors), True
    )
    group_rows = GROUP * text_rows
    text_float = token_group.reshape(group_rows, seq_tokens, D).astype(jnp.float32)
    segment_all = segment_group.reshape(group_rows, seq_tokens)
    allowed = segment_all[:, :, None] == segment_all[:, None, :]
    vector_pieces = vector_parts(text_vectors)
    group_output, forward_kept = block_forward(text_float, allowed, text_low, vector_pieces, False)
    text_output = lax.dynamic_slice_in_dim(group_output, z_at * text_rows, text_rows, 0)
    caption_marks = (
        segment_all[:, None, :] == jnp.arange(PER_ROW, dtype=jnp.int32)[None, :, None]
    ).astype(jnp.float32)
    counts = jnp.sum(caption_marks, axis=-1, keepdims=True)
    pooled = (jnp.einsum("rks,rsd->rkd", caption_marks, group_output, precision=PRECISE) / counts).reshape(-1, D)
    image_emb = unit_rows(image_pooled).astype(jnp.bfloat16)
    text_norm, embed_back = jax.vjp(unit_rows, pooled)
    text_emb = text_norm.astype(jnp.bfloat16)
    own_emb = lax.dynamic_slice_in_dim(text_emb, z_at * device_pairs, device_pairs, 0)
    embeddings = spread(jnp.concatenate([image_emb, own_emb], axis=0), n_dp, n_rep, 2, "spread_embeddings")
    image_all = embeddings[:, :device_pairs].reshape(pair_total, D)
    text_all = embeddings[:, device_pairs:].reshape(pair_total, D)
    own_pairs = (
        ((jnp.arange(GROUP, dtype=jnp.int32) * n_inner + y_at) * n_rep + r_at)[:, None] * device_pairs
        + jnp.arange(device_pairs, dtype=jnp.int32)[None, :]
    ).reshape(-1)
    logits = LOGIT_SCALE * jnp.einsum("pd,bd->pb", image_all, text_all, preferred_element_type=jnp.float32)
    image_top = jnp.max(logits, axis=1)
    image_log_total = image_top + jnp.log(jnp.sum(jnp.exp(logits - image_top[:, None]), axis=1))
    caption_top = jnp.max(logits, axis=0)
    caption_log_total = caption_top + jnp.log(jnp.sum(jnp.exp(logits - caption_top[None, :]), axis=0))
    pair_ids = jnp.arange(pair_total, dtype=jnp.int32)
    matched = jnp.sum(jnp.where(pair_ids[:, None] == pair_ids[None, :], logits, 0.0), axis=1)
    loss_total = (jnp.sum(image_log_total - matched) + jnp.sum(caption_log_total - matched)) / (2.0 * pair_total)
    diagonal_pick = (pair_ids[None, :] == own_pairs[:, None]).astype(jnp.float32)
    text_logits = LOGIT_SCALE * jnp.einsum("pd,bd->pb", text_emb, image_all, preferred_element_type=jnp.float32)
    text_top = jnp.max(text_logits, axis=1, keepdims=True)
    text_log_total = text_top + jnp.log(jnp.sum(jnp.exp(text_logits - text_top), axis=1, keepdims=True))
    text_soft = ((jnp.exp(text_logits - text_log_total) - diagonal_pick) * 0.5).astype(jnp.bfloat16)
    column_soft = ((jnp.exp(text_logits - image_log_total[None, :]) - diagonal_pick) * 0.5).astype(jnp.bfloat16)
    grad_text = LOGIT_SCALE * (
        jnp.einsum("pb,bd->pd", text_soft, image_all, preferred_element_type=jnp.float32)
        + jnp.einsum("pb,bd->pd", column_soft, image_all, preferred_element_type=jnp.float32)
    )
    grad_pooled = embed_back(grad_text)[0]
    grad_pooled = grad_pooled.reshape(-1, PER_ROW, D) / counts
    grad_out = jnp.einsum("rks,rkd->rsd", caption_marks, grad_pooled, precision=PRECISE)
    grad_inputs, vector_grad, outer_terms = block_backward(
        text_float, allowed, text_low, vector_pieces, forward_kept, grad_out, z_at, text_rows
    )
    group_width = n_inner * own_rows
    worker_blocks = []
    for (left_side, right_side), (first_col, after_col) in zip(outer_terms, bounds):
        left_cut = lax.dynamic_slice_in_dim(left_side, z_at * group_width, group_width, 1)
        block = jnp.einsum("tc,tk->ck", left_cut, right_side, preferred_element_type=jnp.float32)
        mine = lax.dynamic_slice_in_dim(block, y_at * own_rows, own_rows, 0)
        for k in range(1, n_inner):
            target = lax.rem(y_at + k, n_inner)
            outgoing = lax.dynamic_slice_in_dim(block, target * own_rows, own_rows, 0).astype(jnp.bfloat16)
            pairs = [
                (z * n_inner + y, z * n_inner + (y + k) % n_inner) for z in range(GROUP) for y in range(n_inner)
            ]
            mine = mine + lax.ppermute(outgoing, "dp", pairs).astype(jnp.float32)
        worker_blocks.append(mine + feedback_rows[:, first_col:after_col])
    factor_rows = jnp.concatenate(
        [
            rows_factor(start_factors[:, first_col:after_col], rows)
            for rows, (first_col, after_col) in zip(worker_blocks, bounds)
        ],
        axis=0,
    )
    gathered_rows = spread(factor_rows, n_dp, n_rep, 3, "spread_factors")
    factor = jnp.sum(gathered_rows.reshape(n_dp, n_rep, 4 * factor_rank, own_rows), axis=1)
    factor = jnp.swapaxes(factor, 0, 1).reshape(4, factor_rank, D)
    left_basis = orthonormal(factor).reshape(4 * factor_rank, D)
    basis_rows = lax.dynamic_slice_in_dim(left_basis, row_start, own_rows, 1)
    basis_parts = [basis_rows[i * factor_rank : (i + 1) * factor_rank] for i in range(4)]
    right_part = jnp.concatenate(
        [jnp.einsum("kd,dc->kc", part, rows, precision=PRECISE) for part, rows in zip(basis_parts, worker_blocks)],
        axis=1,
    )
    summed = total_over_all(
        jnp.concatenate([right_part.reshape(-1), vector_grad]), n_dp, n_rep, 4, "total_right"
    )
    new_right = summed[: right_part.size].reshape(right_part.shape)
    vector_total = summed[right_part.size :]
    approximation = jnp.concatenate(
        [
            jnp.einsum("kd,kc->dc", part, new_right[:, first_col:after_col], precision=PRECISE)
            for part, (first_col, after_col) in zip(basis_parts, bounds)
        ],
        axis=1,
    )
    worker_rows = jnp.concatenate(worker_blocks, axis=1)
    new_feedback = (worker_rows - approximation / n_rep)[None]
    new_momentum = MOMENTUM_DECAY * momentum + approximation
    new_weights = text_weights - STEP_RATE * new_momentum
    new_vector_momentum = MOMENTUM_DECAY * vector_momentum + vector_total
    new_vectors = text_vectors - STEP_RATE * new_vector_momentum
    return (
        loss_total, text_output, grad_inputs, new_weights, new_momentum, new_feedback,
        new_vectors, new_vector_momentum, left_basis, new_right,
    )


def solution(mesh):
    placed = (
        P(("dp", "rep"), None, None), P("dp", None), P(), P(("dp", "rep"), None, None), P(("dp", "rep"), None),
        P("dp", None), P(), P("dp", None), P(), P("rep", "dp", None), P(),
    )
    return jax.shard_map(
        per_device,
        mesh=mesh,
        in_specs=placed,
        out_specs=(
            P(), P(("dp", "rep"), None, None), P(("dp", "rep"), None, None), P("dp", None), P("dp", None),
            P("rep", "dp", None), P(), P(), P(), P(),
        ),
        check_vma=False,
    )
```

```python
import functools

import jax
import jax.numpy as jnp
from jax import lax
from jax.experimental import pallas as pl
from jax.experimental.pallas import tpu as pltpu
from jax.sharding import PartitionSpec as P

D = 768
FF = 3072
HEADS = 12
HEAD_DIM = 64
PER_ROW = 4
GROUP = 4
SECTION = 3072
LANE_COLS = 512

PRECISE = lax.Precision.HIGHEST
LAYER_EPS = 1e-06
SCORE_SCALE = 0.125
LOGIT_SCALE = 50.0
MOMENTUM_DECAY = 0.9
STEP_RATE = 0.08
NORM_FLOOR = 1e-08
MASKED = -1e30
MESH = pl.DeviceIdType.MESH


def layer_norm(values, layer_gain, layer_shift):
    center = values - jnp.mean(values, axis=-1, keepdims=True)
    spread = jnp.mean(center * center, axis=-1, keepdims=True)
    return center * lax.rsqrt(spread + LAYER_EPS) * layer_gain + layer_shift


def unit_rows(values):
    return values * lax.rsqrt(jnp.sum(values * values, axis=-1, keepdims=True) + LAYER_EPS)


def vector_parts(vectors):
    pieces = [vectors[position * D : (position + 1) * D] for position in range(8)]
    return pieces + [vectors[8 * D :]]


def matrix_bounds():
    return ((0, 3 * D), (3 * D, 4 * D), (4 * D, 4 * D + FF), (4 * D + FF, 4 * D + 2 * FF))


def gather_kernel(
    n_dp, text_ref, image_ref, tok_ref, seg_ref, wt_ref, wi_ref, tok_out, seg_out,
    z_send, z_recv, y_send, y_recv, x_send, x_recv, c_send, c_recv, t_send, t_recv, t_own, own_sem,
):
    n_inner = n_dp // GROUP
    d_at, r_at = lax.axis_index("dp"), lax.axis_index("rep")
    z_at, y_at = d_at // n_inner, d_at % n_inner
    x_at, c_at = r_at // 2, r_at % 2
    z_peers = [(lax.rem(z_at + k, GROUP) * n_inner + y_at, r_at) for k in range(1, GROUP)]
    z_from = [lax.rem(z_at + GROUP - k, GROUP) for k in range(1, GROUP)]
    y_peers = [(z_at * n_inner + lax.rem(y_at + k, n_inner), r_at) for k in range(1, n_inner)]
    y_from = [lax.rem(y_at + n_inner - k, n_inner) for k in range(1, n_inner)]
    x_peer = (d_at, (1 - x_at) * 2 + c_at)
    c_peer = (d_at, x_at * 2 + 1 - c_at)

    barrier = pltpu.get_barrier_semaphore()
    everyone = z_peers + y_peers + [x_peer, c_peer]
    for peer in everyone:
        pl.semaphore_signal(barrier, inc=1, device_id=peer, device_id_type=MESH)
    pl.semaphore_wait(barrier, len(everyone))

    def shard_of(z, y):
        return z * n_inner + y

    sections = [(image_ref, wi_ref, 0), (text_ref, wt_ref, 0), (image_ref, wi_ref, 1),
                (text_ref, wt_ref, 1), (image_ref, wi_ref, 2), (text_ref, wt_ref, 2)]

    def cols(section, lane):
        start = sections[section][2] * SECTION + lane * LANE_COLS
        return pl.ds(pl.multiple_of(start, 128), LANE_COLS)

    lane_both = c_at
    lane_mine = 2 + x_at * 2 + c_at
    lane_theirs = 2 + (1 - x_at) * 2 + c_at
    lanes = (lane_both, lane_mine)

    locals_ = [
        pltpu.make_async_copy(tok_ref, tok_out.at[z_at], t_own.at[0]),
        pltpu.make_async_copy(seg_ref, seg_out.at[z_at], t_own.at[1]),
    ]
    for s, (src, full, _) in enumerate(sections):
        for j in range(2):
            column = cols(s, lanes[j])
            locals_.append(pltpu.make_async_copy(src.at[:, column], full.at[d_at, :, column], own_sem.at[s, j]))
    for copy in locals_:
        copy.start()

    def remote(src, dst, send, recv, peer):
        return pltpu.make_async_remote_copy(
            src_ref=src, dst_ref=dst, send_sem=send, recv_sem=recv, device_id=peer, device_id_type=MESH
        )

    def z_copy(s, k, j):
        src, full, _ = sections[s]
        return remote(
            src.at[:, cols(s, lanes[j])], full.at[d_at, :, cols(s, lanes[j])],
            z_send.at[s, k, j], z_recv.at[s, k, j], z_peers[k],
        )

    def y_copy(s, q, zi, j):
        src, full, _ = sections[s]
        column = cols(s, lanes[j])
        if zi == 0:
            shard, source = d_at, src.at[:, column]
        else:
            shard = shard_of(z_from[zi - 1], y_at)
            source = full.at[shard, :, column]
        return remote(source, full.at[shard, :, column], y_send.at[s, q, zi, j], y_recv.at[s, q, zi, j], y_peers[q])

    def x_copy(s):
        full = sections[s][1]
        block = full.at[:, :, cols(s, lane_mine)]
        return remote(block, block, x_send.at[s], x_recv.at[s], x_peer)

    def c_copy(s, j):
        full = sections[s][1]
        block = full.at[:, :, cols(s, (lane_both, lane_mine, lane_theirs)[j])]
        return remote(block, block, c_send.at[s, j], c_recv.at[s, j], c_peer)

    count = len(sections)
    tokens = []
    for k in range(GROUP - 1):
        tokens.append(remote(tok_ref, tok_out.at[z_at], t_send.at[0, k], t_recv.at[0, k], z_peers[k]))
        tokens.append(remote(seg_ref, seg_out.at[z_at], t_send.at[1, k], t_recv.at[1, k], z_peers[k]))

    def begin(s):
        for j in range(2):
            for k in range(GROUP - 1):
                z_copy(s, k, j).start()
            for q in range(n_inner - 1):
                y_copy(s, q, 0, j).start()

    begin(0)
    for copy in tokens:
        copy.start()
    for copy in locals_:
        copy.wait()
    begin(1)
    for step in range(count + 3):
        if step < count:
            for k in range(GROUP - 1):
                for j in range(2):
                    z_copy(step, k, j).wait_recv()
                    for q in range(n_inner - 1):
                        y_copy(step, q, k + 1, j).start()
            if step + 2 < count:
                begin(step + 2)
        s = step - 1
        if 0 <= s < count:
            for q in range(n_inner - 1):
                for zi in range(GROUP):
                    for j in range(2):
                        y_copy(s, q, zi, j).wait_recv()
            x_copy(s).start()
            for j in range(2):
                c_copy(s, j).start()
        s = step - 2
        if 0 <= s < count:
            x_copy(s).wait_recv()
            c_copy(s, 2).start()
        s = step - 3
        if 0 <= s < count:
            for j in range(3):
                c_copy(s, j).wait_recv()
    for copy in tokens:
        copy.wait()
    for s in range(count):
        for j in range(2):
            for k in range(GROUP - 1):
                z_copy(s, k, j).wait_send()
            for q in range(n_inner - 1):
                for zi in range(GROUP):
                    y_copy(s, q, zi, j).wait_send()
        x_copy(s).wait_send()
        for j in range(3):
            c_copy(s, j).wait_send()


def gather_weights(n_dp, text_low, image_low, tokens, segments):
    n_inner = n_dp // GROUP
    full = jax.ShapeDtypeStruct((n_dp,) + text_low.shape, jnp.bfloat16)
    hbm = pl.BlockSpec(memory_space=pltpu.HBM)
    dma = pltpu.SemaphoreType.DMA
    return pl.pallas_call(
        functools.partial(gather_kernel, n_dp),
        out_shape=(
            full,
            full,
            jax.ShapeDtypeStruct((GROUP,) + tokens.shape, jnp.bfloat16),
            jax.ShapeDtypeStruct((GROUP,) + segments.shape, jnp.int32),
        ),
        in_specs=[hbm] * 4,
        out_specs=(hbm,) * 4,
        scratch_shapes=[
            dma((6, GROUP - 1, 2)), dma((6, GROUP - 1, 2)),
            dma((6, n_inner - 1, GROUP, 2)), dma((6, n_inner - 1, GROUP, 2)),
            dma((6,)), dma((6,)), dma((6, 3)), dma((6, 3)),
            dma((2, GROUP - 1)), dma((2, GROUP - 1)), dma((2,)), dma((6, 2)),
        ],
        compiler_params=pltpu.CompilerParams(collective_id=1, has_side_effects=True),
        name="gather_weights",
    )(text_low, image_low, tokens, segments)


TILE = 256
PAIR = 128
ROWS = 32
LANES = 6
PART = 768
PARTS = 12
DEPTH = 8
AHEAD = 2
OWN_AHEAD = 4
TOKENS_AT = 6
STEP_TIME = 4.0
LAG_Z = 1
LAG_Y = 1
LAG_X = 1
LAG_C = 1
AT_Y = 2 * LAG_Z + LAG_Y
AT_X = AT_Y + LAG_X
AT_C = AT_X + LAG_C
WORDS = (GROUP * PAIR)


def piece_of(vec_ref, index, width=D):
    return vec_ref[:, pl.ds(index * D, width)]


def loop(count, body, unroll=1):
    def step(i, carry):
        body(i)
        return carry

    lax.fori_loop(0, count, step, 0, unroll=unroll)


def aligned(i, size):
    return pl.ds(pl.multiple_of(i * size, size), size)


def norm_rows(values):
    center = values - jnp.mean(values, axis=-1, keepdims=True)
    spread_ = jnp.mean(center * center, axis=-1, keepdims=True)
    return center * lax.rsqrt(spread_ + LAYER_EPS)


def dot(left, right):
    return jnp.dot(left, right, preferred_element_type=jnp.float32)


def dot_nt(left, right):
    return lax.dot_general(left, right, (((1,), (1,)), ((), ())), preferred_element_type=jnp.float32)


def dot_tn(left, right):
    return lax.dot_general(left, right, (((0,), (0,)), ((), ())), preferred_element_type=jnp.float32)


def lane_is_first():
    return lax.broadcasted_iota(jnp.int32, (PAIR, PAIR), 1) < HEAD_DIM


def two_heads(block):
    first = lane_is_first()
    zero = jnp.zeros_like(block)
    return jnp.concatenate([jnp.where(first, block, zero), jnp.where(first, zero, block)], axis=0)


def attention_forward(qkv, mixed, chance, allowed_of, first, count):
    pairs = HEADS // 2

    def body(k):
        at = first + k
        i, j = at // pairs, lax.rem(at, pairs)
        rows = aligned(i, PAIR)
        query = qkv[rows, aligned(j, PAIR)]
        key = qkv[rows, pl.ds(pl.multiple_of(D + j * PAIR, PAIR), PAIR)]
        value = qkv[rows, pl.ds(pl.multiple_of(2 * D + j * PAIR, PAIR), PAIR)]
        scores = dot_nt(two_heads(query), key) * SCORE_SCALE
        allowed = allowed_of(i)
        scores = jnp.where(jnp.concatenate([allowed, allowed], axis=0), scores, MASKED)
        scores = jnp.exp(scores - jnp.max(scores, axis=-1, keepdims=True))
        weight = scores / jnp.sum(scores, axis=-1, keepdims=True)
        if chance is not None:
            chance[at] = weight
        low = weight.astype(jnp.bfloat16)
        side = jnp.concatenate([low[:PAIR], low[PAIR:]], axis=1)
        mixed[rows, aligned(j, PAIR)] = dot(side, two_heads(value)).astype(jnp.bfloat16)

    loop(count, body, unroll=2)


def forward_kernel(
    n_dp, n_rep, patches,
    text_ref, image_ref, tok_ref, row_ref, pic_ref, tvec_ref, ivec_ref,
    wt_out, pic_all, words_out, text_pool_out, marks_out, qkv_out, chance_out, mid_out, slope_out,
    act_out, nt_out, at_out, mt_out,
    wi_ref, wt_vmem, tok, seg_col, seg_row, normed, qkv, mixed, middle, normed_two, active, slope, chance, total, hid, turned, apool, image_pool_out,
    z_send, z_recv, y_send, y_recv, x_send, x_recv, c_send, c_recv, t_send, t_recv, t_own, own_sem, w_sem, out_sem, p_send, p_recv,
):
    n_inner = n_dp // GROUP
    d_at, r_at = lax.axis_index("dp"), lax.axis_index("rep")
    z_at, y_at = d_at // n_inner, lax.rem(d_at, n_inner)
    x_at, c_at = r_at // 2, lax.rem(r_at, 2)
    z_next = [((z_at - 1) * n_inner + y_at, r_at), ((z_at + 1) * n_inner + y_at, r_at)]
    y_peers = [(z_at * n_inner + 1 - y_at, r_at)]
    x_peer = (d_at, (1 - x_at) * 2 + c_at)
    c_peer = (d_at, x_at * 2 + 1 - c_at)

    devices = n_dp * n_rep
    me = d_at * n_rep + r_at
    barrier = pltpu.get_barrier_semaphore()

    def hello(offset, carry):
        _, other = peer_at(offset, n_dp, n_rep)
        pl.semaphore_signal(barrier, inc=1, device_id=other, device_id_type=MESH)
        return carry

    lax.fori_loop(1, devices, hello, 0)

    sections = [(image_ref, wi_ref, k) for k in range(PARTS)] + [(text_ref, wt_vmem, k) for k in range(PARTS)]
    count = len(sections)
    lane_both = c_at
    lane_mine = 2 + x_at * 2 + c_at
    lane_theirs = 2 + (1 - x_at) * 2 + c_at
    lanes = (lane_both, lane_mine)

    def remote(src, dst, send, recv, peer):
        return pltpu.make_async_remote_copy(
            src_ref=src, dst_ref=dst, send_sem=send, recv_sem=recv, device_id=peer, device_id_type=MESH
        )

    def cols(s):
        return pl.ds(sections[s][2] * PART, PART)

    def set_of(s):
        return s // PARTS

    def size_of(s, shards, lanes_):
        return sections[s][1].at[sections[s][2], pl.ds(0, shards), pl.ds(0, lanes_)]

    def all_size(group, shards, lanes_):
        return sections[group * PARTS][1].at[:, pl.ds(0, shards), pl.ds(0, lanes_)]

    def landed(block, recv, peer):
        remote(block, block, x_send.at[0], recv, peer).wait_recv()

    def gone(block, send, peer):
        remote(block, block, send, x_recv.at[0], peer).wait_send()

    def held(s, shard, lane):
        _, full, k = sections[s]
        return full.at[k, shard, lane]

    def z_copy(s, up, hop, j):
        unit = z_at - hop if up else z_at + hop
        shard = unit * n_inner + y_at
        return remote(
            held(s, shard, lanes[j]), held(s, shard, lanes[j]),
            z_send.at[set_of(s), up, hop], z_recv.at[s, unit], z_next[up],
        )

    def y_copy(s, q, unit, j):
        shard = unit * n_inner + y_at
        return remote(
            held(s, shard, lanes[j]), held(s, shard, lanes[j]),
            y_send.at[set_of(s)], y_recv.at[s], y_peers[q],
        )

    def x_copy(s, unit):
        block = held(s, pl.ds(unit * n_inner, n_inner), lane_mine)
        return remote(block, block, x_send.at[set_of(s)], x_recv.at[s], x_peer)

    def x_own_copy(s):
        block = held(s, z_at * n_inner + 1 - y_at, lane_mine)
        return remote(block, block, x_send.at[set_of(s)], x_recv.at[s], x_peer)

    def c_copy(s, j):
        block = held(s, slice(None), (lane_both, lane_mine, lane_theirs)[j])
        return remote(block, block, c_send.at[set_of(s)], c_recv.at[s], c_peer)

    def store(s):
        return pltpu.make_async_copy(wt_vmem.at[s - PARTS], wt_out.at[s - PARTS], w_sem.at[s - PARTS])

    z_open = (z_at > 0, z_at < GROUP - 1)

    def own_shard(s):
        src, _, _ = sections[s]
        return [
            pltpu.make_async_copy(src.at[lane, :, cols(s)], held(s, d_at, lane), own_sem.at[s])
            for lane in (lane_both, lane_mine, lane_theirs)
        ]

    gathered = ((tok_ref, tok), (row_ref, seg_row))
    firsts = [pltpu.make_async_copy(src, dst.at[z_at], t_own.at[i]) for i, (src, dst) in enumerate(gathered)]

    def token_copy(i, up, hop):
        unit = z_at - hop if up else z_at + hop
        block = gathered[i][1].at[unit]
        return remote(block, block, t_send.at[i, up, hop], t_recv.at[i, unit], z_next[up])

    def token_begin():
        for i in range(2):
            firsts[i].wait()
            for up in range(2):
                pl.when(z_open[up])(token_copy(i, up, 0).start)

    def token_arrive(hop):
        for up in range(2):
            unit = z_at - hop if up else z_at + hop

            @pl.when((unit >= 0) & (unit < GROUP))
            def _():
                for i in range(2):
                    block = gathered[i][1].at[0]
                    landed(block, t_recv.at[i, unit], z_next[up])
                    if hop < GROUP - 1:
                        pl.when(z_open[up])(token_copy(i, up, hop).start)

    def token_gone():
        for up in range(2):
            for hop in range(GROUP - 1):
                unit = z_at - hop if up else z_at + hop
                for i in range(2):
                    pl.when((unit >= 0) & (unit < GROUP) & z_open[up])(
                        functools.partial(gone, gathered[i][1].at[0], t_send.at[i, up, hop], z_next[up])
                    )

    def picture_copy(offset):
        _, other = peer_at(offset, n_dp, n_rep)
        return remote(pic_all.at[me], pic_all.at[me], p_send.at[offset - 1], p_recv.at[offset - 1], other)

    def send_pictures():
        values = image_pool_out[...]
        squares = jnp.sum(values * values, axis=-1, keepdims=True)
        pic_all[me] = (values * lax.rsqrt(squares + LAYER_EPS)).astype(jnp.bfloat16)

        def start(offset, carry):
            picture_copy(offset).start()
            return carry

        lax.fori_loop(1, devices, start, 0)

    def end_pictures():
        def end(offset, carry):
            picture_copy(offset).wait()
            return carry

        lax.fori_loop(1, devices, end, 0)

    def begin(s):
        block = size_of(s, 1, 3)
        pltpu.make_async_copy(block, block, own_sem.at[s]).wait()
        for j in range(2):
            for up in range(2):
                pl.when(z_open[up])(z_copy(s, up, 0, j).start)
            y_copy(s, 0, z_at, j).start()

    def arrive(s, hop):
        for up in range(2):
            unit = z_at - hop if up else z_at + hop

            @pl.when((unit >= 0) & (unit < GROUP))
            def _():
                landed(size_of(s, 1, 2), z_recv.at[s, unit], z_next[up])
                for j in range(2):
                    if hop < GROUP - 1:
                        pl.when(z_open[up])(z_copy(s, up, hop, j).start)
                    y_copy(s, 0, unit, j).start()

    def own_start(s):
        for copy in own_shard(s):
            copy.start()

    def stage_y(s):
        landed(size_of(s, GROUP, 2), y_recv.at[s], y_peers[0])
        for unit in range(GROUP):
            pl.when(unit != z_at)(x_copy(s, unit).start)
        x_own_copy(s).start()
        for j in range(2):
            c_copy(s, j).start()

    def stage_x(s):
        landed(size_of(s, n_dp - 1, 1), x_recv.at[s], x_peer)
        c_copy(s, 2).start()

    def stage_c(s):
        landed(size_of(s, n_dp, 3), c_recv.at[s], c_peer)
        if s >= PARTS:
            store(s).start()

    def carry_on(step):
        moves = []
        if step + OWN_AHEAD < count:
            moves.append(functools.partial(own_start, step + OWN_AHEAD))
        if step + AHEAD < count:
            moves.append(functools.partial(begin, step + AHEAD))
        for hop in range(1, GROUP):
            s = step - (hop - 1) * LAG_Z
            if 0 <= s < count:
                moves.append(functools.partial(arrive, s, hop))
        for lag, stage in ((AT_Y, stage_y), (AT_X, stage_x), (AT_C, stage_c)):
            if 0 <= step - lag < count:
                moves.append(functools.partial(stage, step - lag))
        if step == TOKENS_AT:
            moves.append(token_begin)
        for hop in range(1, GROUP):
            if step == TOKENS_AT + 2 * hop:
                moves.append(functools.partial(token_arrive, hop))
        return moves


    def weight_tile(s, c):
        _, full, k = sections[s]
        return full[k, :, :, :, aligned(c, TILE)].reshape(D, TILE)

    def weight_rows(s, half):
        _, full, k = sections[s]
        return full[k, pl.ds(half * (n_dp // 2), n_dp // 2)].reshape(D // 2, PART)

    def split_loop(total_, pieces, cost, body):
        size = total_ // pieces
        return [
            (cost, functools.partial(loop, size, functools.partial(lambda base, i: body(base + i), p * size)))
            for p in range(pieces)
        ]

    def first_norm(read, vec):
        def body(i):
            rows = aligned(i, ROWS)
            value = norm_rows(read(i).astype(jnp.float32))
            normed[rows, :] = (value * piece_of(vec, 0) + piece_of(vec, 1)).astype(jnp.bfloat16)

        return split_loop(WORDS // ROWS, 4, 0.5, body)

    def project(slot, part, bias):
        def body(c):
            out = dot(normed[...], weight_tile(slot, c))
            if bias is not None:
                out = out + bias[0][:, pl.ds(pl.multiple_of(bias[1] * D + c * TILE, TILE), TILE)]
            qkv[:, pl.ds(pl.multiple_of(part * D + c * TILE, TILE), TILE)] = out.astype(jnp.bfloat16)

        return split_loop(PART // TILE, 3, 0.6, body)

    def attend(slot, read, vec):
        def body(c):
            where = aligned(c, TILE)
            middle[:, where] = dot(mixed[...], weight_tile(slot, c)) + vec[
                :, pl.ds(pl.multiple_of(4 * D + c * TILE, TILE), TILE)
            ]

        def norm(i):
            rows = aligned(i, ROWS)
            value = middle[rows, :] + read(i).astype(jnp.float32)
            middle[rows, :] = value
            normed_two[rows, :] = (norm_rows(value) * piece_of(vec, 5) + piece_of(vec, 6)).astype(jnp.bfloat16)

        return split_loop(PART // TILE, 3, 0.6, body) + split_loop(WORDS // ROWS, 4, 0.6, norm)

    def expand(slot, part, vec, keep):
        def one(c, p):
            start = part * PART + c * TILE
            if p == 0:
                hid[...] = dot(normed_two[...], weight_tile(slot, c)) + vec[:, pl.ds(8 * D + start, TILE)]

            def inner(i):
                rows = aligned(i + p * (WORDS // ROWS // 2), ROWS)
                value = hid[rows, :]
                phi = 0.5 + 0.5 * lax.erf(value * 0.7071067811865476)
                active[rows, pl.ds(start, TILE)] = (value * phi).astype(jnp.bfloat16)
                if keep:
                    slope[rows, pl.ds(start, TILE)] = phi + value * (
                        0.3989422804014327 * jnp.exp(-0.5 * value * value)
                    )

            loop(WORDS // ROWS // 2, inner, unroll=2)

        return [
            (1.2 - 0.4 * p + 0.2 * keep, functools.partial(one, c, p)) for c in range(PART // TILE) for p in range(2)
        ]

    def shrink(slot, part, vec):
        def one(half):
            where = pl.ds(half * (D // 2), D // 2)
            out = dot_nt(active[:, pl.ds(part * PART, PART)], weight_rows(slot, half))
            if part == 0:
                total[:, where] = out + middle[:, where] + vec[:, pl.ds(7 * D + half * (D // 2), D // 2)]
            else:
                total[:, where] += out

        return [(0.8, functools.partial(one, half)) for half in range(2)]

    def attention(chance_, allowed_of):
        pairs_ = GROUP * HEADS // 2
        return [
            (1.2, functools.partial(attention_forward, qkv, mixed, chance_, allowed_of, first, 4))
            for first in range(0, pairs_, 4)
        ]

    def turn(source, slot, out):
        def body(c):
            turned[slot, aligned(c, PAIR), :] = source[:, aligned(c, PAIR)].T

        loop(D // PAIR, body)
        send_out(turned.at[slot, group_rows], out)

    outs = []

    def send_out(src, dst):
        copy = pltpu.make_async_copy(src, dst, out_sem.at[len(outs)])
        copy.start()
        outs.append(copy)

    group_rows = pl.ds(pl.multiple_of(z_at * (D // GROUP), D // GROUP), D // GROUP)

    def text_read(i):
        per = PAIR // ROWS
        return tok[i // per, aligned(lax.rem(i, per), ROWS), :]

    def text_allowed(i):
        row = seg_row[i].astype(jnp.float32)
        return seg_col[i] == row[0:1, :]

    def text_columns():
        for i in range(GROUP):
            row = seg_row[i].astype(jnp.float32)[0:1, :]
            seg_col[i] = jnp.broadcast_to(row, (PAIR, PAIR)).T

    def image_read(i):
        return pic_ref[aligned(i, ROWS), :]

    def picture(axis):
        at = lax.broadcasted_iota(jnp.int32, (PAIR, PAIR), axis)
        number = at // (PAIR // 2)
        return jnp.where(lax.rem(at, PAIR // 2) < patches, number, number + 2)

    def image_allowed(i):
        return picture(0) == picture(1)

    def keep_mark():
        image = lax.broadcasted_iota(jnp.int32, (GROUP * 2, WORDS), 0)
        at = lax.broadcasted_iota(jnp.int32, (GROUP * 2, WORDS), 1)
        inside = (at // (PAIR // 2) == image) & (lax.rem(at, PAIR // 2) < patches)
        return jnp.where(inside, 1.0, 0.0)

    def text_pool():
        send_out(total.at[aligned(z_at, PAIR)], words_out)
        for i in range(GROUP):
            row = seg_row[i].astype(jnp.float32)[0:8, :]
            marks = jnp.where(row == lax.broadcasted_iota(jnp.int32, (8, PAIR), 0).astype(jnp.float32), 1.0, 0.0)
            marks_out[i] = marks
            marks_low = marks.astype(jnp.bfloat16)
            value = total[pl.ds(i * PAIR, PAIR), :]
            high = value.astype(jnp.bfloat16)
            rest = value - high.astype(jnp.float32)
            low = rest.astype(jnp.bfloat16)
            lower = (rest - low.astype(jnp.float32)).astype(jnp.bfloat16)
            sums = dot(
                jnp.concatenate([marks_low] * 3, axis=1), jnp.concatenate([high, low, lower], axis=0)
            )
            text_pool_out[pl.ds(i * 8, 8), :] = sums / jnp.sum(marks, axis=1, keepdims=True)

    def text_part(k):
        slot = k + PARTS
        if k == 0:
            return (
                [(0.3, text_columns)] + first_norm(text_read, tvec_ref) + project(slot, 0, (tvec_ref, 2))
                + [(0.8, lambda: turn(normed, 0, nt_out))]
            )
        if k == 1:
            return project(slot, 1, None)
        if k == 2:
            return (
                project(slot, 2, (tvec_ref, 3)) + [(0.1, lambda: send_out(qkv, qkv_out))]
                + attention(chance, text_allowed)
                + [(0.1, lambda: send_out(chance, chance_out)), (0.8, lambda: turn(mixed, 1, at_out))]
            )
        if k == 3:
            return attend(slot, text_read, tvec_ref) + [
                (0.1, lambda: send_out(middle, mid_out)), (0.8, lambda: turn(normed_two, 2, mt_out))
            ]
        if k < 8:
            return expand(slot, k - 4, tvec_ref, True)
        pieces = shrink(slot, k - 8, tvec_ref)
        if k == 8:
            pieces = [(0.1, lambda: (send_out(active, act_out), send_out(slope, slope_out)))] + pieces
        if k == PARTS - 1:
            pieces = pieces + [(1.0, text_pool)]
        return pieces

    def pool_active(part):
        mark = keep_mark().astype(jnp.bfloat16)
        where = pl.ds(part * PART, PART)
        mean = dot(mark, active[:, where]) * (1.0 / patches)
        high = mean.astype(jnp.bfloat16)
        rest = mean - high.astype(jnp.float32)
        low = rest.astype(jnp.bfloat16)
        apool[0:8, where] = high.astype(jnp.float32)
        apool[8:16, where] = low.astype(jnp.float32)
        apool[16:24, where] = rest - low.astype(jnp.float32)

    def pool_shrink(slot, part):
        for half in range(2):
            where = pl.ds(half * (D // 2), D // 2)
            left = apool[:, pl.ds(part * PART, PART)].astype(jnp.bfloat16)
            out = dot_nt(left, weight_rows(slot, half))
            out = out[0:8] + out[8:16] + out[16:24]
            if part == 0:
                held_ = jnp.concatenate(
                    [
                        jnp.sum(middle[pl.ds(i * (PAIR // 2), patches), where], axis=0, keepdims=True)
                        for i in range(GROUP * 2)
                    ],
                    axis=0,
                )
                image_pool_out[:, where] = (
                    held_ * (1.0 / patches) + ivec_ref[:, pl.ds(7 * D + half * (D // 2), D // 2)] + out
                )
            else:
                image_pool_out[:, where] += out

    def image_part(k):
        slot = k
        if k == 0:
            return first_norm(image_read, ivec_ref) + project(slot, 0, (ivec_ref, 2))
        if k == 1:
            return project(slot, 1, None)
        if k == 2:
            return project(slot, 2, (ivec_ref, 3)) + attention(None, image_allowed)
        if k == 3:
            return attend(slot, image_read, ivec_ref)
        if k < 8:
            return expand(slot, k - 4, ivec_ref, False) + [(0.2, functools.partial(pool_active, k - 4))]
        pieces = [(0.5, functools.partial(pool_shrink, slot, k - 8))]
        if k == PARTS - 1:
            pieces.append((2.0, send_pictures))
        return pieces

    for s in range(min(OWN_AHEAD, count)):
        own_start(s)
    for copy in firsts:
        copy.start()
    pl.semaphore_wait(barrier, devices - 1)
    for s in range(AHEAD):
        begin(s)
    moves = [(step, move) for step in range(count + AT_C) for move in carry_on(step)]
    by_step = {}
    for step, move in moves:
        by_step.setdefault(step, []).append(move)
    timed = []
    for step in sorted(by_step):
        for i, move in enumerate(by_step[step]):
            timed.append((STEP_TIME * (step + i / len(by_step[step])), step, move))
    clock, done = 0.0, 0
    for s in range(count):
        pieces = image_part(s) if s < PARTS else text_part(s - PARTS)
        while done < len(timed) and timed[done][1] <= s + AT_C:
            clock = max(clock, timed[done][0])
            timed[done][2]()
            done += 1
        for cost, piece in pieces:
            piece()
            clock += cost
            while done < len(timed) and timed[done][0] <= clock:
                timed[done][2]()
                done += 1
    while done < len(timed):
        timed[done][2]()
        done += 1
    for copy in outs:
        copy.wait()
    for s in range(PARTS, count):
        store(s).wait()
    token_gone()
    end_pictures()
    for group in range(2):
        for up in range(2):
            for hop in range(GROUP - 1):
                unit = z_at - hop if up else z_at + hop
                pl.when((unit >= 0) & (unit < GROUP) & z_open[up])(
                    functools.partial(gone, all_size(group, 1, 2), z_send.at[group, up, hop], z_next[up])
                )
        gone(all_size(group, GROUP, 2), y_send.at[group], y_peers[0])
        gone(all_size(group, n_dp - 1, 1), x_send.at[group], x_peer)
        gone(all_size(group, n_dp, 3), c_send.at[group], c_peer)


def gather_and_forward(n_dp, n_rep, text_low, image_low, tokens, segments, pictures, text_vectors, image_vectors):
    own, columns = text_low.shape
    images, patches = pictures.shape[0], pictures.shape[1]
    lane_rows = own // LANES
    count = 2 * PARTS
    numbers = (segments + jnp.arange(segments.shape[0], dtype=jnp.int32)[:, None] * PER_ROW).reshape(-1)
    numbers = numbers.astype(jnp.bfloat16)
    padded = jnp.pad(pictures, ((0, 0), (0, PAIR // 2 - patches), (0, 0))).reshape(WORDS, D)
    hbm, vmem = pl.BlockSpec(memory_space=pltpu.HBM), pl.BlockSpec(memory_space=pltpu.VMEM)
    low, full = jnp.bfloat16, jnp.float32
    shape = jax.ShapeDtypeStruct
    gathered = shape((PARTS, n_dp, LANES, lane_rows, PART), low)
    turned = shape((D // GROUP, WORDS), low)
    pairs = GROUP * HEADS // 2
    dma = pltpu.SemaphoreType.DMA
    outs = pl.pallas_call(
        functools.partial(forward_kernel, n_dp, n_rep, patches),
        out_shape=(
            gathered, shape((n_dp * n_rep, images, D), low), shape((PAIR, D), full), shape((8 * GROUP, D), full),
            shape((GROUP, 8, PAIR), full), shape((WORDS, 3 * D), low), shape((pairs, 2 * PAIR, PAIR), full),
            shape((WORDS, D), full), shape((WORDS, FF), full), shape((WORDS, FF), low), turned, turned, turned,
        ),
        in_specs=[hbm] * 4 + [vmem] * 3,
        out_specs=(hbm, vmem, hbm, vmem, vmem) + (hbm,) * 8,
        scratch_shapes=[
            pltpu.VMEM((PARTS, n_dp, LANES, lane_rows, PART), low),
            pltpu.VMEM((PARTS, n_dp, LANES, lane_rows, PART), low),
            pltpu.VMEM((GROUP, PAIR, D), low),
            pltpu.VMEM((GROUP, PAIR, PAIR), full),
            pltpu.VMEM((GROUP, 16, PAIR), low),
            pltpu.VMEM((WORDS, D), low),
            pltpu.VMEM((WORDS, 3 * D), low),
            pltpu.VMEM((WORDS, D), low),
            pltpu.VMEM((WORDS, D), full),
            pltpu.VMEM((WORDS, D), low),
            pltpu.VMEM((WORDS, FF), low),
            pltpu.VMEM((WORDS, FF), full),
            pltpu.VMEM((pairs, 2 * PAIR, PAIR), full),
            pltpu.VMEM((WORDS, D), full),
            pltpu.VMEM((WORDS, TILE), full),
            pltpu.VMEM((3, D, WORDS), low),
            pltpu.VMEM((24, FF), full),
            pltpu.VMEM((images, D), full),
            dma((2, 2, GROUP - 1)), dma((count, GROUP)), dma((2,)), dma((count,)),
            dma((2,)), dma((count,)), dma((2,)), dma((count,)),
            dma((2, 2, GROUP - 1)), dma((2, GROUP)), dma((2,)), dma((count,)), dma((PARTS,)), dma((12,)),
            dma((n_dp * n_rep - 1,)), dma((n_dp * n_rep - 1,)),
        ],
        compiler_params=pltpu.CompilerParams(collective_id=5, has_side_effects=True, vmem_limit_bytes=60 << 20),
        name="gather_and_forward",
    )(
        text_low.reshape(LANES, lane_rows, columns), image_low.reshape(LANES, lane_rows, columns), tokens,
        jnp.broadcast_to(numbers[None, :], (16, PAIR)), padded,
        text_vectors.reshape(1, -1), image_vectors.reshape(1, -1),
    )
    return (outs[0].reshape(PARTS, D, PART),) + tuple(outs[1:])


def backward_kernel(
    n_dp, n_rep,
    wt_ref, nt_ref, at_ref, mt_ref, qkv_ref, chance_ref, mid_ref, slope_ref, act_ref, feed_ref,
    tpool_ref, pic_all, marks_ref, tok_ref, vec_ref,
    rows_out, input_out, vector_out, loss_out,
    weight, turned, qkv, chance, middle, slope, active, grad_hidden, grad_mix, low, low_mixed, wide, block, sent, got, sums, dy_ref, e2t, cap_all,
    load_sem, send, recv, c_send, c_recv,
):
    n_inner = n_dp // GROUP
    d_at, r_at = lax.axis_index("dp"), lax.axis_index("rep")
    z_at, y_at = d_at // n_inner, lax.rem(d_at, n_inner)
    peer = (z_at * n_inner + 1 - y_at, r_at)
    own = D // n_dp
    share = 1.0 / GROUP

    barrier = pltpu.get_barrier_semaphore()
    devices = n_dp * n_rep
    near = n_inner * n_rep

    def near_peer(k):
        other = lax.rem(y_at * n_rep + r_at + k, near)
        return z_at * n_inner + other // n_rep, lax.rem(other, n_rep)

    for k in range(1, near):
        pl.semaphore_signal(barrier, inc=1, device_id=near_peer(k), device_id_type=MESH)
    loads = {}

    def fetch(name, src, dst):
        copy = pltpu.make_async_copy(src, dst, load_sem.at[len(loads)])
        copy.start()
        loads[name] = copy

    def need(*names):
        for name in names:
            loads[name].wait()

    fetch("act", act_ref, active)
    for part in range(4):
        fetch(("w", 8 + part), wt_ref.at[8 + part], weight.at[8 + part])
    fetch("slope", slope_ref, slope)
    fetch("mt", mt_ref, turned.at[0])
    for part in range(4):
        fetch(("w", 4 + part), wt_ref.at[4 + part], weight.at[4 + part])
    fetch("mid", mid_ref, middle)
    fetch("at", at_ref, turned.at[1])
    fetch(("w", 3), wt_ref.at[3], weight.at[3])
    fetch("qkv", qkv_ref, qkv)
    fetch("chance", chance_ref, chance)
    fetch("nt", nt_ref, turned.at[2])
    for part in range(3):
        fetch(("w", part), wt_ref.at[part], weight.at[part])
    fetch("feed", feed_ref, rows_out)

    def exchange(s):
        return pltpu.make_async_remote_copy(
            src_ref=sent.at[s], dst_ref=got.at[s], send_sem=send.at[s], recv_sem=recv.at[s],
            device_id=peer, device_id_type=MESH,
        )

    own_rows = pl.ds(pl.multiple_of(y_at * own, own), own)
    other_rows = pl.ds(pl.multiple_of((1 - y_at) * own, own), own)

    def outer(s, left, right_of):
        def body(c):
            block[...] = dot(left, right_of(c))
            where = pl.ds(pl.multiple_of(s * PART + c * TILE, TILE), TILE)
            rows_out[:, where] = rows_out[:, where] + block[own_rows, :]
            sent[s, :, aligned(c, TILE)] = block[other_rows, :].astype(jnp.bfloat16)

        loop(PART // TILE, body)
        exchange(s).start()

    ones = jnp.ones((16, WORDS), jnp.bfloat16)

    def put(slot, values):
        for i in range(values.shape[1] // PAIR):
            vector_out[pl.ds(slot // PAIR + i, 1), :] = values[:, i * PAIR : (i + 1) * PAIR]

    def column_sums(values, slot, scale):
        put(slot, dot(ones, values)[0:1, :] * scale)


    def caption_copy(k):
        block_ = cap_all.at[:, y_at * n_rep + r_at]
        return pltpu.make_async_remote_copy(
            src_ref=block_, dst_ref=block_, send_sem=c_send.at[k - 1], recv_sem=c_recv.at[k - 1],
            device_id=near_peer(k), device_id_type=MESH,
        )

    def unit_of(values):
        return values * lax.rsqrt(jnp.sum(values * values, axis=-1, keepdims=True) + LAYER_EPS)

    def contrast():
        group_pairs = GROUP * 8
        for i in range(GROUP):
            cap_all[i, y_at * n_rep + r_at] = unit_of(tpool_ref[pl.ds(i * 8, 8), :]).astype(jnp.bfloat16)
        pl.semaphore_wait(barrier, near - 1)
        for k in range(1, near):
            caption_copy(k).start()
        for k in range(1, near):
            caption_copy(k).wait_recv()
        pairs_ = devices * 8
        pics = pic_all[...].reshape(pairs_, D)
        caps = cap_all[...].reshape(pairs_, D)
        logits = dot_nt(caps, pics) * LOGIT_SCALE
        top = jnp.max(logits, axis=0, keepdims=True)
        image_log = top + jnp.log(jnp.sum(jnp.exp(logits - top), axis=0, keepdims=True))
        top = jnp.max(logits, axis=1, keepdims=True)
        caption_log = top + jnp.log(jnp.sum(jnp.exp(logits - top), axis=1, keepdims=True))
        row = lax.broadcasted_iota(jnp.int32, (pairs_, pairs_), 0)
        column = lax.broadcasted_iota(jnp.int32, (pairs_, pairs_), 1)
        matched = jnp.sum(jnp.where(row == column, logits, 0.0), axis=1, keepdims=True)
        loss = (jnp.sum(image_log) + jnp.sum(caption_log) - 2.0 * jnp.sum(matched)) / (2.0 * pairs_)
        loss_out[...] = jnp.full(loss_out.shape, loss, jnp.float32)
        pooled = tpool_ref[...]
        squares = lax.rsqrt(jnp.sum(pooled * pooled, axis=-1, keepdims=True) + LAYER_EPS)
        own_low = (pooled * squares).astype(jnp.bfloat16)
        own_logits = dot_nt(own_low, pics) * LOGIT_SCALE
        top = jnp.max(own_logits, axis=1, keepdims=True)
        own_log = top + jnp.log(jnp.sum(jnp.exp(own_logits - top), axis=1, keepdims=True))
        local = lax.broadcasted_iota(jnp.int32, (group_pairs, pairs_), 0)
        column = lax.broadcasted_iota(jnp.int32, (group_pairs, pairs_), 1)
        wanted = (local // 8) * (near * 8) + (y_at * n_rep + r_at) * 8 + lax.rem(local, 8)
        pick = jnp.where(wanted == column, 1.0, 0.0)
        soft = ((jnp.exp(own_logits - own_log) - pick) * 0.5).astype(jnp.bfloat16)
        across = ((jnp.exp(own_logits - image_log) - pick) * 0.5).astype(jnp.bfloat16)
        grad = LOGIT_SCALE * (dot(soft, pics) + dot(across, pics))
        grad = squares * (
            grad - pooled * (squares * squares) * jnp.sum(grad * pooled, axis=-1, keepdims=True)
        )
        for i in range(GROUP):
            marks = marks_ref[i]
            part = grad[i * 8 : (i + 1) * 8, :] / jnp.sum(marks, axis=1, keepdims=True)
            high, rest = split_two(part)
            rest_low = (part - high.astype(jnp.float32) - rest.astype(jnp.float32)).astype(jnp.bfloat16)
            stacked = jnp.concatenate([high, rest, rest_low], axis=0)
            marks_low = marks.astype(jnp.bfloat16)
            marks_low = jnp.concatenate([marks_low, marks_low, marks_low], axis=0)
            rows = pl.ds(i * PAIR, PAIR)
            words = dot_tn(marks_low, stacked)
            dy_ref[rows, :] = words
            low[rows, :] = words.astype(jnp.bfloat16)
            e2t[:, rows] = dot_tn(stacked, marks_low).astype(jnp.bfloat16)

    contrast()
    column_sums(low[...], 7 * D, share)
    need("act", "feed")
    for part in range(4):
        outer(8 + part, e2t[pl.ds(pl.multiple_of(z_at * (D // GROUP), D // GROUP), D // GROUP), :], lambda c: active[:, pl.ds(pl.multiple_of(part * PART + c * TILE, TILE), TILE)])
    need("slope")
    for part in range(4):
        need(("w", 8 + part))

        def hidden_body(c):
            where = pl.ds(pl.multiple_of(part * PART + c * TILE, TILE), TILE)
            out = dot(low[...], weight[8 + part, :, aligned(c, TILE)])
            grad_hidden[:, where] = (out * slope[:, where]).astype(jnp.bfloat16)

        loop(PART // TILE, hidden_body)
        column_sums(grad_hidden[:, pl.ds(part * PART, PART)], 8 * D + part * PART, share)
    need("mt")
    for part in range(4):
        outer(
            4 + part, turned[0], lambda c: grad_hidden[:, pl.ds(pl.multiple_of(part * PART + c * TILE, TILE), TILE)]
        )
    for part in range(4):
        need(("w", 4 + part))
    for half in range(2):
        rows = pl.ds(half * (D // 2), D // 2)
        out = dot_nt(grad_hidden[:, pl.ds(0, PART)], weight[4, rows, :])
        for part in range(1, 4):
            out = out + dot_nt(grad_hidden[:, pl.ds(part * PART, PART)], weight[4 + part, rows, :])
        wide[:, rows] = out
    need("mid")

    def norm_back(value, grad, gain):
        center = value - jnp.mean(value, axis=-1, keepdims=True)
        scale = lax.rsqrt(jnp.mean(center * center, axis=-1, keepdims=True) + LAYER_EPS)
        unit = center * scale
        inner = grad * gain
        out = scale * (
            inner - jnp.mean(inner, axis=-1, keepdims=True) - unit * jnp.mean(inner * unit, axis=-1, keepdims=True)
        )
        return out, grad * unit

    def fold(values):
        return jnp.sum(values.reshape(ROWS // 8, 8, D), axis=0)

    sums[...] = jnp.zeros_like(sums)

    def second(i):
        rows = aligned(i, ROWS)
        grad = wide[rows, :]
        out, product = norm_back(middle[rows, :], grad, piece_of(vec_ref, 5))
        sums[0] += fold(product)
        sums[1] += fold(grad)
        out = out + dy_ref[rows, :]
        middle[rows, :] = out
        low[rows, :] = out.astype(jnp.bfloat16)

    loop(WORDS // ROWS, second)
    put(5 * D, jnp.sum(sums[0], axis=0, keepdims=True) * share)
    put(6 * D, jnp.sum(sums[1], axis=0, keepdims=True) * share)
    column_sums(low[...], 4 * D, share)
    need("at")
    outer(3, turned[1], lambda c: low[:, aligned(c, TILE)])
    need(("w", 3))
    for half in range(2):
        rows = pl.ds(half * (D // 2), D // 2)
        low_mixed[:, rows] = dot_nt(low[...], weight[3, rows, :]).astype(jnp.bfloat16)
    need("qkv", "chance")
    pairs = HEADS // 2

    def attention(at):
        i, j = at // pairs, lax.rem(at, pairs)
        rows = aligned(i, PAIR)
        q_cols = aligned(j, PAIR)
        k_cols = pl.ds(pl.multiple_of(D + j * PAIR, PAIR), PAIR)
        v_cols = pl.ds(pl.multiple_of(2 * D + j * PAIR, PAIR), PAIR)
        query, key, value = qkv[rows, q_cols], qkv[rows, k_cols], qkv[rows, v_cols]
        grad = two_heads(low_mixed[rows, q_cols])
        weight_ = chance[at]
        grad_mix[rows, v_cols] = dot_tn(weight_.astype(jnp.bfloat16), grad).astype(jnp.bfloat16)
        back = dot_nt(grad, value)
        back = weight_ * (back - jnp.sum(weight_ * back, axis=-1, keepdims=True))
        back = back.astype(jnp.bfloat16)
        side = jnp.concatenate([back[:PAIR], back[PAIR:]], axis=1)
        grad_mix[rows, q_cols] = (dot(side, two_heads(key)) * SCORE_SCALE).astype(jnp.bfloat16)
        grad_mix[rows, k_cols] = (dot_tn(back, two_heads(query)) * SCORE_SCALE).astype(jnp.bfloat16)

    loop(GROUP * pairs, attention, unroll=2)
    need("nt")
    for part in range(3):
        outer(part, turned[2], lambda c: grad_mix[:, pl.ds(pl.multiple_of(part * PART + c * TILE, TILE), TILE)])
    column_sums(grad_mix[:, pl.ds(0, D)], 2 * D, share)
    column_sums(grad_mix[:, pl.ds(2 * D, D)], 3 * D, share)
    for part in range(3):
        need(("w", part))
    mine = aligned(z_at, PAIR)
    for half in range(2):
        rows = pl.ds(half * (D // 2), D // 2)
        out = dot_nt(grad_mix[mine, pl.ds(0, PART)], weight[0, rows, :])
        for part in range(1, 3):
            out = out + dot_nt(grad_mix[mine, pl.ds(part * PART, PART)], weight[part, rows, :])
        wide[pl.ds(0, PAIR), rows] = out
    sums[...] = jnp.zeros_like(sums)

    def first(i):
        rows = aligned(i, ROWS)
        grad = wide[rows, :]
        out, product = norm_back(tok_ref[rows, :].astype(jnp.float32), grad, piece_of(vec_ref, 0))
        sums[0] += fold(product)
        sums[1] += fold(grad)
        input_out[rows, :] = out + middle[pl.ds(pl.multiple_of(z_at * PAIR + i * ROWS, ROWS), ROWS), :]

    loop(PAIR // ROWS, first)
    put(0, jnp.sum(sums[0], axis=0, keepdims=True))
    put(D, jnp.sum(sums[1], axis=0, keepdims=True))
    for s in (8, 9, 10, 11, 4, 5, 6, 7, 3, 0, 1, 2):
        exchange(s).wait_recv()

        def add(c):
            where = pl.ds(pl.multiple_of(s * PART + c * TILE, TILE), TILE)
            rows_out[:, where] = rows_out[:, where] + got[s, :, aligned(c, TILE)].astype(jnp.float32)

        loop(PART // TILE, add)
    for s in range(PARTS):
        exchange(s).wait_send()
    for k in range(1, near):
        caption_copy(k).wait_send()


def backward(n_dp, n_rep, kept, pooled, pictures, marks, tokens, text_vectors, feedback_rows):
    weights, qkv, chance, middle, slope, active, n_turned, a_turned, m_turned = kept
    own = feedback_rows.shape[0]
    hbm, vmem = pl.BlockSpec(memory_space=pltpu.HBM), pl.BlockSpec(memory_space=pltpu.VMEM)
    low, full = jnp.bfloat16, jnp.float32
    shape = jax.ShapeDtypeStruct
    dma = pltpu.SemaphoreType.DMA
    pairs = GROUP * HEADS // 2
    return pl.pallas_call(
        functools.partial(backward_kernel, n_dp, n_rep),
        out_shape=(shape(feedback_rows.shape, full), shape((PAIR, D), full), shape((12 * D // PAIR, PAIR), full), shape((8, PAIR), full)),
        in_specs=[hbm] * 10 + [vmem] * 5,
        out_specs=(vmem,) * 4,
        scratch_shapes=[
            pltpu.VMEM((PARTS, D, PART), low),
            pltpu.VMEM((3, D // GROUP, WORDS), low),
            pltpu.VMEM((WORDS, 3 * D), low),
            pltpu.VMEM((pairs, 2 * PAIR, PAIR), full),
            pltpu.VMEM((WORDS, D), full),
            pltpu.VMEM((WORDS, FF), full),
            pltpu.VMEM((WORDS, FF), low),
            pltpu.VMEM((WORDS, FF), low),
            pltpu.VMEM((WORDS, 3 * D), low),
            pltpu.VMEM((WORDS, D), low),
            pltpu.VMEM((WORDS, D), low),
            pltpu.VMEM((WORDS, D), full),
            pltpu.VMEM((D // GROUP, TILE), full),
            pltpu.VMEM((PARTS, own, PART), low),
            pltpu.VMEM((PARTS, own, PART), low),
            pltpu.VMEM((2, 8, D), full),
            pltpu.VMEM((WORDS, D), full),
            pltpu.VMEM((D, WORDS), low),
            pltpu.VMEM((GROUP, n_dp * n_rep // GROUP, 8, D), low),
            dma((24,)), dma((PARTS,)), dma((PARTS,)),
            dma((8,)), dma((8,)),
        ],
        compiler_params=pltpu.CompilerParams(collective_id=6, has_side_effects=True, vmem_limit_bytes=60 << 20),
        name="backward",
    )(
        weights, n_turned, a_turned, m_turned, qkv, chance, middle, slope, active, feedback_rows,
        pooled, pictures, marks, tokens, text_vectors.reshape(1, -1),
    )


EXTRA = 9
OWN_TILES = 3


def split_two(values):
    high = values.astype(jnp.bfloat16)
    return high, (values - high.astype(jnp.float32)).astype(jnp.bfloat16)


def power_kernel(
    n_dp, n_rep,
    rows_ref, start_ref, vgrad_ref, vec_ref, vmom_ref,
    left_out, right_out, nvec_out, nvmom_out,
    rows, factor, factor_rep, factor_dp, basis, tiles, tiles_rep, quarter, tiles_dp, everything,
    load_sem, send, recv,
):
    d_at, r_at = lax.axis_index("dp"), lax.axis_index("rep")
    own = rows.shape[0]
    bounds = matrix_bounds()
    rank = start_ref.shape[0]
    strip = n_dp * OWN_TILES
    load = pltpu.make_async_copy(rows_ref, rows, load_sem)
    load.start()
    rep_peers = [(d_at, lax.rem(r_at + k, n_rep)) for k in range(1, n_rep)]
    dp_peers = [(lax.rem(d_at + k, n_dp), r_at) for k in range(1, n_dp)]
    barrier = pltpu.get_barrier_semaphore()
    for peer in rep_peers + dp_peers:
        pl.semaphore_signal(barrier, inc=1, device_id=peer, device_id_type=MESH)

    def remote(phase, k, src, dst, peer):
        return pltpu.make_async_remote_copy(
            src_ref=src, dst_ref=dst, send_sem=send.at[phase, k], recv_sem=recv.at[phase, k],
            device_id=peer, device_id_type=MESH,
        )

    phases = [
        [remote(0, k, factor, factor_rep.at[k], peer) for k, peer in enumerate(rep_peers)],
        [remote(1, k, factor_dp.at[d_at], factor_dp.at[d_at], peer) for k, peer in enumerate(dp_peers)],
        [
            remote(2, k, tiles.at[pl.ds(peer[1] * strip, strip)], tiles_rep.at[k], peer)
            for k, peer in enumerate(rep_peers)
        ],
        [
            remote(3, k, quarter.at[pl.ds(peer[0] * OWN_TILES, OWN_TILES)], tiles_dp.at[k], peer)
            for k, peer in enumerate(dp_peers)
        ],
    ]
    mine = pl.ds(r_at * strip + d_at * OWN_TILES, OWN_TILES)
    strip_mine = pl.ds(r_at * strip, strip)
    phases.append([remote(4, k, everything.at[mine], everything.at[mine], peer) for k, peer in enumerate(dp_peers)])
    phases.append(
        [remote(5, k, everything.at[strip_mine], everything.at[strip_mine], peer) for k, peer in enumerate(rep_peers)]
    )

    def begin(phase):
        for copy in phases[phase]:
            copy.start()

    def arrived(phase):
        for copy in phases[phase]:
            copy.wait_recv()

    factor[...] = jnp.zeros_like(factor)
    load.wait()
    for matrix, (first_col, after_col) in enumerate(bounds):
        total = jnp.zeros((2 * rank, own), jnp.float32)
        rest = jnp.zeros((2 * rank, own), jnp.float32)
        for at in range(first_col, after_col, PART):
            high, low = split_two(rows[:, pl.ds(at, PART)])
            start_high, start_low = split_two(start_ref[:, pl.ds(at, PART)])
            both = jnp.concatenate([start_high, start_low], axis=0)
            total = total + dot_nt(both, high)
            rest = rest + dot_nt(both, low)
        factor[pl.ds(matrix * rank, rank), pl.ds(0, own)] = total[:rank] + total[rank:] + rest[:rank]
    pl.semaphore_wait(barrier, len(rep_peers + dp_peers))
    begin(0)
    arrived(0)
    summed = factor[...]
    for k in range(n_rep - 1):
        summed = summed + factor_rep[k]
    factor_dp[d_at] = summed
    begin(1)
    arrived(1)
    vectors = jnp.concatenate([factor_dp[i] for i in range(n_dp)], axis=1).reshape(4, rank, n_dp * PAIR)
    place = lax.broadcasted_iota(jnp.int32, (4, rank, 1), 1)
    for k in range(rank):
        vector = vectors[:, k : k + 1, :]
        size = jnp.sqrt(jnp.sum(vector * vector, axis=-1, keepdims=True)) + NORM_FLOOR
        vector = vector / size
        along = jnp.sum(vector * vectors, axis=-1, keepdims=True)
        vectors = jnp.where(
            place == k, jnp.broadcast_to(vector, vectors.shape),
            vectors - jnp.where(place > k, along, 0.0) * vector,
        )
    vectors = vectors.reshape(4 * rank, n_dp * PAIR)
    basis[...] = vectors
    left_out[...] = vectors
    basis_high, basis_low = split_two(basis[:, aligned(d_at, PAIR)][:, :own])
    for matrix, (first_col, after_col) in enumerate(bounds):
        where = slice(matrix * rank, (matrix + 1) * rank)
        both = jnp.concatenate([basis_high[where], basis_low[where]], axis=0)

        def project(c):
            high, low = split_two(rows[:, pl.ds(pl.multiple_of(first_col + c * TILE, TILE), TILE)])
            out = dot(both, high)
            out = out[:rank] + out[rank:] + dot(both, low)[:rank]
            at = first_col // PAIR + c * (TILE // PAIR)
            for half in range(TILE // PAIR):
                tiles[at + half] = out[:, half * PAIR : (half + 1) * PAIR]

        loop((after_col - first_col) // TILE, project, unroll=3)
    columns = bounds[-1][1] // PAIR
    for i in range(EXTRA):
        tiles[columns + i] = vgrad_ref[pl.ds(i * 8, 8), :]
    for i in range(columns + EXTRA, n_rep * strip):
        tiles[i] = jnp.zeros((8, PAIR), jnp.float32)
    begin(2)
    arrived(2)
    value = tiles[strip_mine]
    for k in range(n_rep - 1):
        value = value + tiles_rep[k]
    quarter[...] = value
    begin(3)
    arrived(3)
    value = quarter[pl.ds(d_at * OWN_TILES, OWN_TILES)]
    for k in range(n_dp - 1):
        value = value + tiles_dp[k]
    everything[mine] = value
    begin(4)
    arrived(4)
    begin(5)
    arrived(5)
    for i in range(columns):
        right_out[:, pl.ds(i * PAIR, PAIR)] = everything[i]
    for i in range(EXTRA):
        at = pl.ds(i * 8, 8)
        moved = MOMENTUM_DECAY * vmom_ref[at, :] + everything[columns + i]
        nvmom_out[at, :] = moved
        nvec_out[at, :] = vec_ref[at, :] - STEP_RATE * moved
    for phase in phases:
        for copy in phase:
            copy.wait_send()


def power_step(n_dp, n_rep, rows, start, vector_grad, vectors, vector_momentum):
    own, columns = rows.shape
    rank = start.shape[0]
    hbm, vmem = pl.BlockSpec(memory_space=pltpu.HBM), pl.BlockSpec(memory_space=pltpu.VMEM)
    full = jnp.float32
    shape = jax.ShapeDtypeStruct
    dma = pltpu.SemaphoreType.DMA
    strip = n_dp * OWN_TILES
    flat = (columns // PAIR, PAIR)
    left, right, new_vectors, new_vector_momentum = pl.pallas_call(
        functools.partial(power_kernel, n_dp, n_rep),
        out_shape=(
            shape((4 * rank, n_dp * PAIR), full), shape(start.shape, full), shape(flat, full), shape(flat, full),
        ),
        in_specs=[hbm, vmem, vmem, vmem, vmem],
        out_specs=(vmem,) * 4,
        scratch_shapes=[
            pltpu.VMEM(rows.shape, full),
            pltpu.VMEM((4 * rank, PAIR), full),
            pltpu.VMEM((n_rep - 1, 4 * rank, PAIR), full),
            pltpu.VMEM((n_dp, 4 * rank, PAIR), full),
            pltpu.VMEM((4 * rank, n_dp * PAIR), full),
            pltpu.VMEM((n_rep * strip, 8, PAIR), full),
            pltpu.VMEM((n_rep - 1, strip, 8, PAIR), full),
            pltpu.VMEM((strip, 8, PAIR), full),
            pltpu.VMEM((n_dp - 1, OWN_TILES, 8, PAIR), full),
            pltpu.VMEM((n_rep * strip, 8, PAIR), full),
            dma, dma((6, n_dp - 1)), dma((6, n_dp - 1)),
        ],
        compiler_params=pltpu.CompilerParams(collective_id=7, has_side_effects=True, vmem_limit_bytes=60 << 20),
        name="power_step",
    )(rows, start, vector_grad, vectors.reshape(flat), vector_momentum.reshape(flat))
    return left, right, new_vectors.reshape(-1), new_vector_momentum.reshape(-1)


CHUNKS = 4


def finish_kernel(
    n_dp, n_rep,
    rows_ref, mom_ref, wts_ref, words_ref, input_ref, left_ref, right_ref,
    feed_out, mom_out, wts_out, words_out, input_out, left_out, right_out,
    rows, mom, wts, change, through, load_sem, store_sem, pass_sem,
):
    own = rows.shape[0]
    piece = own // CHUNKS
    rank = right_ref.shape[0]

    def load(i, j):
        src, dst = ((rows_ref, rows), (mom_ref, mom), (wts_ref, wts))[j]
        span = pl.ds(i * piece, piece)
        return pltpu.make_async_copy(src.at[span], dst.at[span], load_sem.at[i, j])

    def store(i, j):
        src, dst = ((rows, feed_out), (mom, mom_out), (wts, wts_out))[j]
        span = pl.ds(i * piece, piece)
        return pltpu.make_async_copy(src.at[span], dst.at[span], store_sem.at[i, j])

    for i in range(CHUNKS):
        for j in range(3):
            load(i, j).start()
    taken = [
        pltpu.make_async_copy(src, through.at[i], pass_sem.at[i]) for i, src in enumerate((words_ref, input_ref))
    ]
    passed = [
        pltpu.make_async_copy(through.at[i], dst, pass_sem.at[2 + i]) for i, dst in enumerate((words_out, input_out))
    ]
    passed.append(pltpu.make_async_copy(right_ref, right_out, pass_sem.at[4]))
    for copy in taken:
        copy.start()
    passed[2].start()
    left_out[...] = jnp.concatenate([left_ref[:, i * PAIR : i * PAIR + own] for i in range(n_dp)], axis=1)
    basis_high, basis_low = split_two(left_ref[:, aligned(lax.axis_index("dp"), PAIR)][:, :own])
    for matrix, (first_col, after_col) in enumerate(matrix_bounds()):
        where = slice(matrix * rank, (matrix + 1) * rank)
        left = jnp.concatenate([basis_high[where], basis_high[where], basis_low[where]], axis=0)

        def approximate(c):
            cols = pl.ds(pl.multiple_of(first_col + c * PART, PART), PART)
            high, low = split_two(right_ref[:, cols])
            change[:, cols] = dot_tn(left, jnp.concatenate([high, low, high], axis=0))

        loop((after_col - first_col) // PART, approximate)
    for i in range(CHUNKS):
        for j in range(3):
            load(i, j).wait()

        def update(c):
            span, cols = pl.ds(i * piece, piece), aligned(c, PART)
            delta = change[span, cols]
            rows[span, cols] = rows[span, cols] - delta * (1.0 / n_rep)
            moved = MOMENTUM_DECAY * mom[span, cols] + delta
            mom[span, cols] = moved
            wts[span, cols] = wts[span, cols] - STEP_RATE * moved

        loop(rows.shape[1] // PART, update)
        for j in range(3):
            store(i, j).start()
        if i == 0:
            for k, copy in enumerate(taken):
                copy.wait()
                passed[k].start()
    for copy in passed:
        copy.wait()
    for i in range(CHUNKS):
        for j in range(3):
            store(i, j).wait()


def finish(n_dp, n_rep, rows, momentum, weights, left, right, words, grad_inputs):
    own, columns = rows.shape
    hbm, vmem = pl.BlockSpec(memory_space=pltpu.HBM), pl.BlockSpec(memory_space=pltpu.VMEM)
    full = jnp.float32
    shape = jax.ShapeDtypeStruct
    dma = pltpu.SemaphoreType.DMA
    big = shape(rows.shape, full)
    return pl.pallas_call(
        functools.partial(finish_kernel, n_dp, n_rep),
        out_shape=(
            big, big, big, shape(words.shape, full), shape(grad_inputs.shape, full),
            shape((left.shape[0], n_dp * own), full), shape(right.shape, full),
        ),
        in_specs=[hbm] * 5 + [vmem] * 2,
        out_specs=(hbm,) * 5 + (vmem, hbm),
        scratch_shapes=[pltpu.VMEM(rows.shape, full)] * 4
        + [pltpu.VMEM((2,) + words.shape, full), dma((CHUNKS, 3)), dma((CHUNKS, 3)), dma((5,))],
        compiler_params=pltpu.CompilerParams(vmem_limit_bytes=60 << 20),
        name="finish",
    )(rows, momentum, weights, words, grad_inputs, left, right)


def peer_at(offset, n_dp, n_rep):
    me = lax.axis_index("dp") * n_rep + lax.axis_index("rep")
    other = lax.rem(me + offset, n_dp * n_rep)
    return other, (other // n_rep, lax.rem(other, n_rep))


def meet(n_dp, n_rep):
    total = n_dp * n_rep
    barrier = pltpu.get_barrier_semaphore()

    def hello(offset, carry):
        _, peer = peer_at(offset, n_dp, n_rep)
        pl.semaphore_signal(barrier, inc=1, device_id=peer, device_id_type=MESH)
        return carry

    lax.fori_loop(1, total, hello, 0)
    pl.semaphore_wait(barrier, total - 1)


def spread_kernel(n_dp, n_rep, mine_ref, all_ref, send, recv, own_sem):
    total = n_dp * n_rep
    me = lax.axis_index("dp") * n_rep + lax.axis_index("rep")
    own = pltpu.make_async_copy(mine_ref, all_ref.at[me], own_sem)
    own.start()
    meet(n_dp, n_rep)

    def copy(offset):
        _, peer = peer_at(offset, n_dp, n_rep)
        return pltpu.make_async_remote_copy(
            src_ref=mine_ref, dst_ref=all_ref.at[me], send_sem=send.at[offset - 1],
            recv_sem=recv.at[offset - 1], device_id=peer, device_id_type=MESH,
        )

    def begin(offset, carry):
        copy(offset).start()
        return carry

    def finish(offset, carry):
        copy(offset).wait()
        return carry

    lax.fori_loop(1, total, begin, 0)
    own.wait()
    lax.fori_loop(1, total, finish, 0)


def spread(mine, n_dp, n_rep, collective, name):
    total = n_dp * n_rep
    vmem = pl.BlockSpec(memory_space=pltpu.VMEM)
    dma = pltpu.SemaphoreType.DMA
    return pl.pallas_call(
        functools.partial(spread_kernel, n_dp, n_rep),
        out_shape=jax.ShapeDtypeStruct((total,) + mine.shape, mine.dtype),
        in_specs=[vmem],
        out_specs=vmem,
        scratch_shapes=[dma((total - 1,)), dma((total - 1,)), dma],
        compiler_params=pltpu.CompilerParams(
            collective_id=collective, has_side_effects=True, vmem_limit_bytes=48 << 20
        ),
        name=name,
    )(mine)


def total_kernel(n_dp, n_rep, mine_ref, out_ref, parts, sums, send, recv, send_two, recv_two):
    total = n_dp * n_rep
    me = lax.axis_index("dp") * n_rep + lax.axis_index("rep")
    meet(n_dp, n_rep)

    def scatter(offset):
        other, peer = peer_at(offset, n_dp, n_rep)
        return pltpu.make_async_remote_copy(
            src_ref=mine_ref.at[other], dst_ref=parts.at[offset - 1], send_sem=send.at[offset - 1],
            recv_sem=recv.at[offset - 1], device_id=peer, device_id_type=MESH,
        )

    def share(offset):
        _, peer = peer_at(offset, n_dp, n_rep)
        return pltpu.make_async_remote_copy(
            src_ref=sums, dst_ref=out_ref.at[me], send_sem=send_two.at[offset - 1],
            recv_sem=recv_two.at[offset - 1], device_id=peer, device_id_type=MESH,
        )

    def start_scatter(offset, carry):
        scatter(offset).start()
        return carry

    def add(offset, carry):
        scatter(offset).wait_recv()
        return carry + parts[offset - 1]

    def start_share(offset, carry):
        share(offset).start()
        return carry

    def finish(offset, carry):
        scatter(offset).wait_send()
        share(offset).wait()
        return carry

    lax.fori_loop(1, total, start_scatter, 0)
    result = lax.fori_loop(1, total, add, mine_ref[me])
    sums[...] = result
    lax.fori_loop(1, total, start_share, 0)
    out_ref[me] = result
    lax.fori_loop(1, total, finish, 0)


def total_over_all(flat, n_dp, n_rep, collective, name):
    total = n_dp * n_rep
    count = flat.shape[0]
    chunk = -(-count // (total * 1024)) * 1024
    padded = jnp.pad(flat, (0, total * chunk - count)).reshape(total, chunk // 128, 128)
    vmem = pl.BlockSpec(memory_space=pltpu.VMEM)
    dma = pltpu.SemaphoreType.DMA
    summed = pl.pallas_call(
        functools.partial(total_kernel, n_dp, n_rep),
        out_shape=jax.ShapeDtypeStruct(padded.shape, padded.dtype),
        in_specs=[vmem],
        out_specs=vmem,
        scratch_shapes=[
            pltpu.VMEM((total - 1,) + padded.shape[1:], padded.dtype),
            pltpu.VMEM(padded.shape[1:], padded.dtype),
            dma((total - 1,)), dma((total - 1,)), dma((total - 1,)), dma((total - 1,)),
        ],
        compiler_params=pltpu.CompilerParams(
            collective_id=collective, has_side_effects=True, vmem_limit_bytes=48 << 20
        ),
        name=name,
    )(padded)
    return summed.reshape(-1)[:count]


def masked_scores(query_heads, key_heads, allowed):
    scores = (
        jnp.einsum("rshd,rthd->rhst", query_heads, key_heads, preferred_element_type=jnp.float32)
        * SCORE_SCALE
    )
    return jnp.where(allowed[:, None], scores, MASKED)


def block_forward(inputs, allowed, weights, vector_pieces, pooled_only):
    (
        gain_one, shift_one, bias_query, bias_value, bias_out,
        gain_two, shift_two, bias_shrink, bias_expand,
    ) = vector_pieces
    row_count, seq_tokens = (inputs.shape[0], inputs.shape[1])
    normed = layer_norm(inputs, gain_one, shift_one).astype(jnp.bfloat16)
    mixing = jnp.einsum("rsd,dc->rsc", normed, weights[:, : 3 * D], preferred_element_type=jnp.float32)
    mixing = mixing + jnp.concatenate([bias_query, jnp.zeros_like(bias_query), bias_value])
    head_parts = mixing.astype(jnp.bfloat16).reshape(row_count, seq_tokens, 3, HEADS, HEAD_DIM)
    query_heads, key_heads, value_heads = (head_parts[:, :, 0], head_parts[:, :, 1], head_parts[:, :, 2])
    scores = masked_scores(query_heads, key_heads, allowed)
    highest = jnp.max(scores, axis=-1, keepdims=True)
    log_total = highest + jnp.log(jnp.sum(jnp.exp(scores - highest), axis=-1, keepdims=True))
    attention = jnp.exp(scores - log_total).astype(jnp.bfloat16)
    mixed_heads = jnp.einsum("rhst,rthd->rshd", attention, value_heads, preferred_element_type=jnp.float32)
    mixed_heads = mixed_heads.reshape(row_count, seq_tokens, D).astype(jnp.bfloat16)
    attended = (
        jnp.einsum("rsd,de->rse", mixed_heads, weights[:, 3 * D : 4 * D], preferred_element_type=jnp.float32)
        + bias_out
    )
    middle = inputs + attended
    normed_two = layer_norm(middle, gain_two, shift_two).astype(jnp.bfloat16)
    hidden = (
        jnp.einsum("rsd,df->rsf", normed_two, weights[:, 4 * D : 4 * D + FF], preferred_element_type=jnp.float32)
        + bias_expand
    )
    active = jax.nn.gelu(hidden, approximate=False).astype(jnp.bfloat16)
    shrink = weights[:, 4 * D + FF :]
    if pooled_only:
        mean_active = jnp.mean(active.astype(jnp.float32), axis=1)
        high = mean_active.astype(jnp.bfloat16)
        rest = mean_active - high.astype(jnp.float32)
        low = rest.astype(jnp.bfloat16)
        lower = (rest - low.astype(jnp.float32)).astype(jnp.bfloat16)
        stacked = jnp.concatenate([high, low, lower], axis=0)
        shrunk = jnp.einsum("pf,df->pd", stacked, shrink, preferred_element_type=jnp.float32)
        shrunk = jnp.sum(shrunk.reshape(3, row_count, D), axis=0)
        return jnp.mean(middle, axis=1) + shrunk + bias_shrink
    shrunk = jnp.einsum("rsf,df->rsd", active, shrink, preferred_element_type=jnp.float32) + bias_shrink
    kept = (normed, query_heads, key_heads, value_heads, log_total, mixed_heads, middle, normed_two, hidden, active)
    return (middle + shrunk, kept)


def token_sum(values_low):
    return jnp.sum(values_low.astype(jnp.float32).reshape(-1, values_low.shape[-1]), axis=0)


def block_backward(inputs, allowed, weights, vector_pieces, forward_kept, grad_out, own_group, own_count):
    (gain_one, shift_one, _, _, _, gain_two, shift_two, _, _) = vector_pieces
    (normed, query_heads, key_heads, value_heads, log_total, mixed_heads, middle, normed_two, hidden, active) = forward_kept
    row_count, seq_tokens = (inputs.shape[0], inputs.shape[1])
    grad_shrunk = grad_out.astype(jnp.bfloat16)
    grad_active = jnp.einsum("rsd,df->rsf", grad_shrunk, weights[:, 4 * D + FF :], preferred_element_type=jnp.float32)
    _, gelu_back = jax.vjp(lambda before_gelu: jax.nn.gelu(before_gelu, approximate=False), hidden)
    grad_hidden = gelu_back(grad_active)[0].astype(jnp.bfloat16)
    grad_normed_two = jnp.einsum(
        "rsf,df->rsd", grad_hidden, weights[:, 4 * D : 4 * D + FF], preferred_element_type=jnp.float32
    )
    _, norm_two_back = jax.vjp(layer_norm, middle, gain_two, shift_two)
    grad_middle, grad_gain_two, grad_shift_two = norm_two_back(grad_normed_two)
    grad_middle = grad_middle + grad_out
    grad_attended = grad_middle.astype(jnp.bfloat16)
    grad_mixed = jnp.einsum("rse,de->rsd", grad_attended, weights[:, 3 * D : 4 * D], preferred_element_type=jnp.float32)
    grad_mixed = grad_mixed.astype(jnp.bfloat16).reshape(row_count, seq_tokens, HEADS, HEAD_DIM)
    attention = jnp.exp(masked_scores(query_heads, key_heads, allowed) - log_total)
    grad_values = jnp.einsum("rhst,rshd->rthd", attention.astype(jnp.bfloat16), grad_mixed, preferred_element_type=jnp.float32)
    grad_attention = jnp.einsum("rshd,rthd->rhst", grad_mixed, value_heads, preferred_element_type=jnp.float32)
    grad_scores = attention * (grad_attention - jnp.sum(attention * grad_attention, axis=-1, keepdims=True))
    grad_scores = grad_scores.astype(jnp.bfloat16)
    grad_query = jnp.einsum("rhst,rthd->rshd", grad_scores, key_heads, preferred_element_type=jnp.float32) * SCORE_SCALE
    grad_keys = jnp.einsum("rhst,rshd->rthd", grad_scores, query_heads, preferred_element_type=jnp.float32) * SCORE_SCALE
    grad_mixing = (
        jnp.stack([grad_query, grad_keys, grad_values], axis=2).reshape(row_count, seq_tokens, 3 * D).astype(jnp.bfloat16)
    )

    def mine(values):
        return lax.dynamic_slice_in_dim(values, own_group * own_count, own_count, 0)

    grad_normed = jnp.einsum("rsc,dc->rsd", mine(grad_mixing), weights[:, : 3 * D], preferred_element_type=jnp.float32)
    _, norm_one_back = jax.vjp(layer_norm, mine(inputs), gain_one, shift_one)
    grad_inputs, grad_gain_one, grad_shift_one = norm_one_back(grad_normed)
    grad_inputs = grad_inputs + mine(grad_middle)
    share = 1.0 / GROUP
    vector_grad = jnp.concatenate(
        [
            grad_gain_one, grad_shift_one,
            share * token_sum(grad_mixing[..., :D]), share * token_sum(grad_mixing[..., 2 * D :]),
            share * token_sum(grad_attended), share * grad_gain_two, share * grad_shift_two,
            share * token_sum(grad_shrunk), share * token_sum(grad_hidden),
        ]
    )
    tokens = row_count * seq_tokens
    outer_terms = (
        (normed.reshape(tokens, D), grad_mixing.reshape(tokens, 3 * D)),
        (mixed_heads.reshape(tokens, D), grad_attended.reshape(tokens, D)),
        (normed_two.reshape(tokens, D), grad_hidden.reshape(tokens, FF)),
        (grad_shrunk.reshape(tokens, D), active.reshape(tokens, FF)),
    )
    return (grad_inputs, vector_grad, outer_terms)


def orthonormal(stacked):
    waiting = [stacked[:, column_id] for column_id in range(stacked.shape[1])]
    finished = []
    while waiting:
        vector = waiting.pop(0)
        vector = vector / (jnp.sqrt(jnp.sum(vector * vector, axis=-1, keepdims=True)) + NORM_FLOOR)
        finished.append(vector)
        if waiting:
            later = jnp.stack(waiting, axis=1)
            later = later - jnp.sum(vector[:, None] * later, axis=-1, keepdims=True) * vector[:, None]
            waiting = [later[:, i] for i in range(later.shape[1])]
    return jnp.stack(finished, axis=1)


def rows_factor(start_part, row_block):
    return jnp.einsum("kc,dc->kd", start_part, row_block, precision=PRECISE)


def per_device(
    image_tokens, image_weights, image_vectors, text_tokens, segments, text_weights,
    text_vectors, momentum, vector_momentum, error_feedback, start_factors,
):
    n_rep, n_dp = lax.axis_size("rep"), lax.axis_size("dp")
    n_inner = n_dp // GROUP
    total = n_rep * n_dp
    device_pairs, patches = image_tokens.shape[0], image_tokens.shape[1]
    text_rows, seq_tokens = text_tokens.shape[0], text_tokens.shape[1]
    pair_total = device_pairs * total
    own_rows = text_weights.shape[0]
    d_at, r_at = lax.axis_index("dp"), lax.axis_index("rep")
    z_at, y_at = d_at // n_inner, d_at % n_inner
    row_start = d_at * own_rows
    factor_rank = start_factors.shape[0]
    bounds = matrix_bounds()
    tokens = text_tokens.reshape(text_rows * seq_tokens, D)
    words_low = text_weights.astype(jnp.bfloat16)
    feedback_rows = error_feedback[0]
    fused = (
        own_rows % (16 * LANES) == 0 and n_inner == 2 and n_rep == 4 and device_pairs == 8
        and text_rows * seq_tokens == PAIR and 2 * seq_tokens == PAIR and 2 * patches <= PAIR
        and n_dp == 8 and factor_rank == 8
    )
    if fused:
        outs = gather_and_forward(
            n_dp, n_rep, words_low, image_weights, tokens, segments, image_tokens, text_vectors, image_vectors
        )
        pictures, words, pooled, marks = outs[1:5]
        kept = (outs[0],) + tuple(outs[5:])
        worker_rows, grad_inputs, vector_grad, loss = backward(
            n_dp, n_rep, kept, pooled, pictures, marks, tokens, text_vectors, feedback_rows
        )
        left_basis, new_right, new_vectors, new_vector_momentum = power_step(
            n_dp, n_rep, worker_rows, start_factors, vector_grad, text_vectors, vector_momentum
        )
        new_feedback, new_momentum, new_weights, words, grad_inputs, left_basis, new_right = finish(
            n_dp, n_rep, worker_rows, momentum, text_weights, left_basis, new_right, words, grad_inputs
        )
        return (
            loss[0, 0], words.reshape(text_rows, seq_tokens, D), grad_inputs.reshape(text_rows, seq_tokens, D),
            new_weights, new_momentum, new_feedback[None], new_vectors, new_vector_momentum, left_basis, new_right,
        )
    text_low, frozen, token_group, segment_group = gather_weights(
        n_dp, words_low, image_weights, tokens, segments
    )
    text_low, frozen = text_low.reshape(D, -1), frozen.reshape(D, -1)
    full_mask = jnp.zeros((device_pairs, patches, patches), jnp.int32) == 0
    image_pooled = block_forward(
        image_tokens.astype(jnp.float32), full_mask, frozen, vector_parts(image_vectors), True
    )
    group_rows = GROUP * text_rows
    text_float = token_group.reshape(group_rows, seq_tokens, D).astype(jnp.float32)
    segment_all = segment_group.reshape(group_rows, seq_tokens)
    allowed = segment_all[:, :, None] == segment_all[:, None, :]
    vector_pieces = vector_parts(text_vectors)
    group_output, forward_kept = block_forward(text_float, allowed, text_low, vector_pieces, False)
    text_output = lax.dynamic_slice_in_dim(group_output, z_at * text_rows, text_rows, 0)
    caption_marks = (
        segment_all[:, None, :] == jnp.arange(PER_ROW, dtype=jnp.int32)[None, :, None]
    ).astype(jnp.float32)
    counts = jnp.sum(caption_marks, axis=-1, keepdims=True)
    pooled = (jnp.einsum("rks,rsd->rkd", caption_marks, group_output, precision=PRECISE) / counts).reshape(-1, D)
    image_emb = unit_rows(image_pooled).astype(jnp.bfloat16)
    text_norm, embed_back = jax.vjp(unit_rows, pooled)
    text_emb = text_norm.astype(jnp.bfloat16)
    own_emb = lax.dynamic_slice_in_dim(text_emb, z_at * device_pairs, device_pairs, 0)
    embeddings = spread(jnp.concatenate([image_emb, own_emb], axis=0), n_dp, n_rep, 2, "spread_embeddings")
    image_all = embeddings[:, :device_pairs].reshape(pair_total, D)
    text_all = embeddings[:, device_pairs:].reshape(pair_total, D)
    own_pairs = (
        ((jnp.arange(GROUP, dtype=jnp.int32) * n_inner + y_at) * n_rep + r_at)[:, None] * device_pairs
        + jnp.arange(device_pairs, dtype=jnp.int32)[None, :]
    ).reshape(-1)
    logits = LOGIT_SCALE * jnp.einsum("pd,bd->pb", image_all, text_all, preferred_element_type=jnp.float32)
    image_top = jnp.max(logits, axis=1)
    image_log_total = image_top + jnp.log(jnp.sum(jnp.exp(logits - image_top[:, None]), axis=1))
    caption_top = jnp.max(logits, axis=0)
    caption_log_total = caption_top + jnp.log(jnp.sum(jnp.exp(logits - caption_top[None, :]), axis=0))
    pair_ids = jnp.arange(pair_total, dtype=jnp.int32)
    matched = jnp.sum(jnp.where(pair_ids[:, None] == pair_ids[None, :], logits, 0.0), axis=1)
    loss_total = (jnp.sum(image_log_total - matched) + jnp.sum(caption_log_total - matched)) / (2.0 * pair_total)
    diagonal_pick = (pair_ids[None, :] == own_pairs[:, None]).astype(jnp.float32)
    text_logits = LOGIT_SCALE * jnp.einsum("pd,bd->pb", text_emb, image_all, preferred_element_type=jnp.float32)
    text_top = jnp.max(text_logits, axis=1, keepdims=True)
    text_log_total = text_top + jnp.log(jnp.sum(jnp.exp(text_logits - text_top), axis=1, keepdims=True))
    text_soft = ((jnp.exp(text_logits - text_log_total) - diagonal_pick) * 0.5).astype(jnp.bfloat16)
    column_soft = ((jnp.exp(text_logits - image_log_total[None, :]) - diagonal_pick) * 0.5).astype(jnp.bfloat16)
    grad_text = LOGIT_SCALE * (
        jnp.einsum("pb,bd->pd", text_soft, image_all, preferred_element_type=jnp.float32)
        + jnp.einsum("pb,bd->pd", column_soft, image_all, preferred_element_type=jnp.float32)
    )
    grad_pooled = embed_back(grad_text)[0]
    grad_pooled = grad_pooled.reshape(-1, PER_ROW, D) / counts
    grad_out = jnp.einsum("rks,rkd->rsd", caption_marks, grad_pooled, precision=PRECISE)
    grad_inputs, vector_grad, outer_terms = block_backward(
        text_float, allowed, text_low, vector_pieces, forward_kept, grad_out, z_at, text_rows
    )
    group_width = n_inner * own_rows
    worker_blocks = []
    for (left_side, right_side), (first_col, after_col) in zip(outer_terms, bounds):
        left_cut = lax.dynamic_slice_in_dim(left_side, z_at * group_width, group_width, 1)
        block = jnp.einsum("tc,tk->ck", left_cut, right_side, preferred_element_type=jnp.float32)
        mine = lax.dynamic_slice_in_dim(block, y_at * own_rows, own_rows, 0)
        for k in range(1, n_inner):
            target = lax.rem(y_at + k, n_inner)
            outgoing = lax.dynamic_slice_in_dim(block, target * own_rows, own_rows, 0).astype(jnp.bfloat16)
            pairs = [
                (z * n_inner + y, z * n_inner + (y + k) % n_inner) for z in range(GROUP) for y in range(n_inner)
            ]
            mine = mine + lax.ppermute(outgoing, "dp", pairs).astype(jnp.float32)
        worker_blocks.append(mine + feedback_rows[:, first_col:after_col])
    factor_rows = jnp.concatenate(
        [
            rows_factor(start_factors[:, first_col:after_col], rows)
            for rows, (first_col, after_col) in zip(worker_blocks, bounds)
        ],
        axis=0,
    )
    gathered_rows = spread(factor_rows, n_dp, n_rep, 3, "spread_factors")
    factor = jnp.sum(gathered_rows.reshape(n_dp, n_rep, 4 * factor_rank, own_rows), axis=1)
    factor = jnp.swapaxes(factor, 0, 1).reshape(4, factor_rank, D)
    left_basis = orthonormal(factor).reshape(4 * factor_rank, D)
    basis_rows = lax.dynamic_slice_in_dim(left_basis, row_start, own_rows, 1)
    basis_parts = [basis_rows[i * factor_rank : (i + 1) * factor_rank] for i in range(4)]
    right_part = jnp.concatenate(
        [jnp.einsum("kd,dc->kc", part, rows, precision=PRECISE) for part, rows in zip(basis_parts, worker_blocks)],
        axis=1,
    )
    summed = total_over_all(
        jnp.concatenate([right_part.reshape(-1), vector_grad]), n_dp, n_rep, 4, "total_right"
    )
    new_right = summed[: right_part.size].reshape(right_part.shape)
    vector_total = summed[right_part.size :]
    approximation = jnp.concatenate(
        [
            jnp.einsum("kd,kc->dc", part, new_right[:, first_col:after_col], precision=PRECISE)
            for part, (first_col, after_col) in zip(basis_parts, bounds)
        ],
        axis=1,
    )
    worker_rows = jnp.concatenate(worker_blocks, axis=1)
    new_feedback = (worker_rows - approximation / n_rep)[None]
    new_momentum = MOMENTUM_DECAY * momentum + approximation
    new_weights = text_weights - STEP_RATE * new_momentum
    new_vector_momentum = MOMENTUM_DECAY * vector_momentum + vector_total
    new_vectors = text_vectors - STEP_RATE * new_vector_momentum
    return (
        loss_total, text_output, grad_inputs, new_weights, new_momentum, new_feedback,
        new_vectors, new_vector_momentum, left_basis, new_right,
    )


def solution(mesh):
    placed = (
        P(("dp", "rep"), None, None), P("dp", None), P(), P(("dp", "rep"), None, None), P(("dp", "rep"), None),
        P("dp", None), P(), P("dp", None), P(), P("rep", "dp", None), P(),
    )
    return jax.shard_map(
        per_device,
        mesh=mesh,
        in_specs=placed,
        out_specs=(
            P(), P(("dp", "rep"), None, None), P(("dp", "rep"), None, None), P("dp", None), P("dp", None),
            P("rep", "dp", None), P(), P(), P(), P(),
        ),
        check_vma=False,
    )
```

```python
import functools

import jax
import jax.numpy as jnp
from jax import lax
from jax.experimental import pallas as pl
from jax.experimental.pallas import tpu as pltpu
from jax.sharding import PartitionSpec as P

D = 768
FF = 3072
HEADS = 12
HEAD_DIM = 64
PER_ROW = 4
GROUP = 4
SECTION = 3072
LANE_COLS = 512

PRECISE = lax.Precision.HIGHEST
LAYER_EPS = 1e-06
SCORE_SCALE = 0.125
LOGIT_SCALE = 50.0
MOMENTUM_DECAY = 0.9
STEP_RATE = 0.08
NORM_FLOOR = 1e-08
MASKED = -1e30
MESH = pl.DeviceIdType.MESH


def layer_norm(values, layer_gain, layer_shift):
    center = values - jnp.mean(values, axis=-1, keepdims=True)
    spread = jnp.mean(center * center, axis=-1, keepdims=True)
    return center * lax.rsqrt(spread + LAYER_EPS) * layer_gain + layer_shift


def unit_rows(values):
    return values * lax.rsqrt(jnp.sum(values * values, axis=-1, keepdims=True) + LAYER_EPS)


def vector_parts(vectors):
    pieces = [vectors[position * D : (position + 1) * D] for position in range(8)]
    return pieces + [vectors[8 * D :]]


def matrix_bounds():
    return ((0, 3 * D), (3 * D, 4 * D), (4 * D, 4 * D + FF), (4 * D + FF, 4 * D + 2 * FF))


def gather_kernel(
    n_dp, text_ref, image_ref, tok_ref, seg_ref, wt_ref, wi_ref, tok_out, seg_out,
    z_send, z_recv, y_send, y_recv, x_send, x_recv, c_send, c_recv, t_send, t_recv, t_own, own_sem,
):
    n_inner = n_dp // GROUP
    d_at, r_at = lax.axis_index("dp"), lax.axis_index("rep")
    z_at, y_at = d_at // n_inner, d_at % n_inner
    x_at, c_at = r_at // 2, r_at % 2
    z_peers = [(lax.rem(z_at + k, GROUP) * n_inner + y_at, r_at) for k in range(1, GROUP)]
    z_from = [lax.rem(z_at + GROUP - k, GROUP) for k in range(1, GROUP)]
    y_peers = [(z_at * n_inner + lax.rem(y_at + k, n_inner), r_at) for k in range(1, n_inner)]
    y_from = [lax.rem(y_at + n_inner - k, n_inner) for k in range(1, n_inner)]
    x_peer = (d_at, (1 - x_at) * 2 + c_at)
    c_peer = (d_at, x_at * 2 + 1 - c_at)

    barrier = pltpu.get_barrier_semaphore()
    everyone = z_peers + y_peers + [x_peer, c_peer]
    for peer in everyone:
        pl.semaphore_signal(barrier, inc=1, device_id=peer, device_id_type=MESH)
    pl.semaphore_wait(barrier, len(everyone))

    def shard_of(z, y):
        return z * n_inner + y

    sections = [(image_ref, wi_ref, 0), (text_ref, wt_ref, 0), (image_ref, wi_ref, 1),
                (text_ref, wt_ref, 1), (image_ref, wi_ref, 2), (text_ref, wt_ref, 2)]

    def cols(section, lane):
        start = sections[section][2] * SECTION + lane * LANE_COLS
        return pl.ds(pl.multiple_of(start, 128), LANE_COLS)

    lane_both = c_at
    lane_mine = 2 + x_at * 2 + c_at
    lane_theirs = 2 + (1 - x_at) * 2 + c_at
    lanes = (lane_both, lane_mine)

    locals_ = [
        pltpu.make_async_copy(tok_ref, tok_out.at[z_at], t_own.at[0]),
        pltpu.make_async_copy(seg_ref, seg_out.at[z_at], t_own.at[1]),
    ]
    for s, (src, full, _) in enumerate(sections):
        for j in range(2):
            column = cols(s, lanes[j])
            locals_.append(pltpu.make_async_copy(src.at[:, column], full.at[d_at, :, column], own_sem.at[s, j]))
    for copy in locals_:
        copy.start()

    def remote(src, dst, send, recv, peer):
        return pltpu.make_async_remote_copy(
            src_ref=src, dst_ref=dst, send_sem=send, recv_sem=recv, device_id=peer, device_id_type=MESH
        )

    def z_copy(s, k, j):
        src, full, _ = sections[s]
        return remote(
            src.at[:, cols(s, lanes[j])], full.at[d_at, :, cols(s, lanes[j])],
            z_send.at[s, k, j], z_recv.at[s, k, j], z_peers[k],
        )

    def y_copy(s, q, zi, j):
        src, full, _ = sections[s]
        column = cols(s, lanes[j])
        if zi == 0:
            shard, source = d_at, src.at[:, column]
        else:
            shard = shard_of(z_from[zi - 1], y_at)
            source = full.at[shard, :, column]
        return remote(source, full.at[shard, :, column], y_send.at[s, q, zi, j], y_recv.at[s, q, zi, j], y_peers[q])

    def x_copy(s):
        full = sections[s][1]
        block = full.at[:, :, cols(s, lane_mine)]
        return remote(block, block, x_send.at[s], x_recv.at[s], x_peer)

    def c_copy(s, j):
        full = sections[s][1]
        block = full.at[:, :, cols(s, (lane_both, lane_mine, lane_theirs)[j])]
        return remote(block, block, c_send.at[s, j], c_recv.at[s, j], c_peer)

    count = len(sections)
    tokens = []
    for k in range(GROUP - 1):
        tokens.append(remote(tok_ref, tok_out.at[z_at], t_send.at[0, k], t_recv.at[0, k], z_peers[k]))
        tokens.append(remote(seg_ref, seg_out.at[z_at], t_send.at[1, k], t_recv.at[1, k], z_peers[k]))

    def begin(s):
        for j in range(2):
            for k in range(GROUP - 1):
                z_copy(s, k, j).start()
            for q in range(n_inner - 1):
                y_copy(s, q, 0, j).start()

    begin(0)
    for copy in tokens:
        copy.start()
    for copy in locals_:
        copy.wait()
    begin(1)
    for step in range(count + 3):
        if step < count:
            for k in range(GROUP - 1):
                for j in range(2):
                    z_copy(step, k, j).wait_recv()
                    for q in range(n_inner - 1):
                        y_copy(step, q, k + 1, j).start()
            if step + 2 < count:
                begin(step + 2)
        s = step - 1
        if 0 <= s < count:
            for q in range(n_inner - 1):
                for zi in range(GROUP):
                    for j in range(2):
                        y_copy(s, q, zi, j).wait_recv()
            x_copy(s).start()
            for j in range(2):
                c_copy(s, j).start()
        s = step - 2
        if 0 <= s < count:
            x_copy(s).wait_recv()
            c_copy(s, 2).start()
        s = step - 3
        if 0 <= s < count:
            for j in range(3):
                c_copy(s, j).wait_recv()
    for copy in tokens:
        copy.wait()
    for s in range(count):
        for j in range(2):
            for k in range(GROUP - 1):
                z_copy(s, k, j).wait_send()
            for q in range(n_inner - 1):
                for zi in range(GROUP):
                    y_copy(s, q, zi, j).wait_send()
        x_copy(s).wait_send()
        for j in range(3):
            c_copy(s, j).wait_send()


def gather_weights(n_dp, text_low, image_low, tokens, segments):
    n_inner = n_dp // GROUP
    full = jax.ShapeDtypeStruct((n_dp,) + text_low.shape, jnp.bfloat16)
    hbm = pl.BlockSpec(memory_space=pltpu.HBM)
    dma = pltpu.SemaphoreType.DMA
    return pl.pallas_call(
        functools.partial(gather_kernel, n_dp),
        out_shape=(
            full,
            full,
            jax.ShapeDtypeStruct((GROUP,) + tokens.shape, jnp.bfloat16),
            jax.ShapeDtypeStruct((GROUP,) + segments.shape, jnp.int32),
        ),
        in_specs=[hbm] * 4,
        out_specs=(hbm,) * 4,
        scratch_shapes=[
            dma((6, GROUP - 1, 2)), dma((6, GROUP - 1, 2)),
            dma((6, n_inner - 1, GROUP, 2)), dma((6, n_inner - 1, GROUP, 2)),
            dma((6,)), dma((6,)), dma((6, 3)), dma((6, 3)),
            dma((2, GROUP - 1)), dma((2, GROUP - 1)), dma((2,)), dma((6, 2)),
        ],
        compiler_params=pltpu.CompilerParams(collective_id=1, has_side_effects=True),
        name="gather_weights",
    )(text_low, image_low, tokens, segments)


TILE = 256
PAIR = 128
ROWS = 32
LANES = 6
PART = 768
PARTS = 12
DEPTH = 8
AHEAD = 2
OWN_AHEAD = 4
TOKENS_AT = 6
STEP_TIME = 4.0
LAG_Z = 1
LAG_Y = 1
LAG_X = 1
LAG_C = 1
AT_Y = 2 * LAG_Z + LAG_Y
AT_X = AT_Y + LAG_X
AT_C = AT_X + LAG_C
WORDS = (GROUP * PAIR)


def piece_of(vec_ref, index, width=D):
    return vec_ref[:, pl.ds(index * D, width)]


def loop(count, body, unroll=1):
    def step(i, carry):
        body(i)
        return carry

    lax.fori_loop(0, count, step, 0, unroll=unroll)


def aligned(i, size):
    return pl.ds(pl.multiple_of(i * size, size), size)


def norm_rows(values):
    center = values - jnp.mean(values, axis=-1, keepdims=True)
    spread_ = jnp.mean(center * center, axis=-1, keepdims=True)
    return center * lax.rsqrt(spread_ + LAYER_EPS)


def dot(left, right):
    return jnp.dot(left, right, preferred_element_type=jnp.float32)


def dot_nt(left, right):
    return lax.dot_general(left, right, (((1,), (1,)), ((), ())), preferred_element_type=jnp.float32)


def dot_tn(left, right):
    return lax.dot_general(left, right, (((0,), (0,)), ((), ())), preferred_element_type=jnp.float32)


def lane_is_first():
    return lax.broadcasted_iota(jnp.int32, (PAIR, PAIR), 1) < HEAD_DIM


def two_heads(block):
    first = lane_is_first()
    zero = jnp.zeros_like(block)
    return jnp.concatenate([jnp.where(first, block, zero), jnp.where(first, zero, block)], axis=0)


def attention_forward(qkv, mixed, chance, allowed_of, first, count):
    pairs = HEADS // 2

    def body(k):
        at = first + k
        i, j = at // pairs, lax.rem(at, pairs)
        rows = aligned(i, PAIR)
        query = qkv[rows, aligned(j, PAIR)]
        key = qkv[rows, pl.ds(pl.multiple_of(D + j * PAIR, PAIR), PAIR)]
        value = qkv[rows, pl.ds(pl.multiple_of(2 * D + j * PAIR, PAIR), PAIR)]
        scores = dot_nt(two_heads(query), key) * SCORE_SCALE
        allowed = allowed_of(i)
        scores = jnp.where(jnp.concatenate([allowed, allowed], axis=0), scores, MASKED)
        scores = jnp.exp(scores - jnp.max(scores, axis=-1, keepdims=True))
        weight = scores / jnp.sum(scores, axis=-1, keepdims=True)
        if chance is not None:
            chance[at] = weight
        low = weight.astype(jnp.bfloat16)
        side = jnp.concatenate([low[:PAIR], low[PAIR:]], axis=1)
        mixed[rows, aligned(j, PAIR)] = dot(side, two_heads(value)).astype(jnp.bfloat16)

    loop(count, body, unroll=2)


def forward_kernel(
    n_dp, n_rep, patches,
    text_ref, image_ref, tok_ref, pic_ref, seg_ref, tvec_ref, ivec_ref,
    wt_out, pic_all, words_out, text_pool_out, marks_out, qkv_out, chance_out, mid_out, slope_out,
    act_out, nt_out, at_out, mt_out,
    wi_ref, wt_vmem, tok, seg_col, seg_row, normed, qkv, mixed, middle, normed_two, active, slope, chance, total, hid, turned, apool, image_pool_out, patches_in, padded, master,
    z_send, z_recv, y_send, y_recv, x_send, x_recv, c_send, c_recv, t_send, t_recv, t_own, own_sem, w_sem, out_sem, p_send, p_recv,
):
    n_inner = n_dp // GROUP
    d_at, r_at = lax.axis_index("dp"), lax.axis_index("rep")
    z_at, y_at = d_at // n_inner, lax.rem(d_at, n_inner)
    x_at, c_at = r_at // 2, lax.rem(r_at, 2)
    z_next = [((z_at - 1) * n_inner + y_at, r_at), ((z_at + 1) * n_inner + y_at, r_at)]
    y_peers = [(z_at * n_inner + 1 - y_at, r_at)]
    x_peer = (d_at, (1 - x_at) * 2 + c_at)
    c_peer = (d_at, x_at * 2 + 1 - c_at)

    devices = n_dp * n_rep
    me = d_at * n_rep + r_at
    z_open = (z_at > 0, z_at < GROUP - 1)
    barrier = pltpu.get_barrier_semaphore()

    def hello(peer):
        pl.semaphore_signal(barrier, inc=1, device_id=peer, device_id_type=MESH)

    for peer in (y_peers[0], x_peer, c_peer):
        hello(peer)
    for up in range(2):
        pl.when(z_open[up])(functools.partial(hello, z_next[up]))

    sections = [(image_ref, wi_ref, k) for k in range(PARTS)] + [(text_ref, wt_vmem, k) for k in range(PARTS)]
    count = len(sections)
    lane_mine = c_at * 3 + 2 * x_at
    lane_theirs = c_at * 3 + 2 * (1 - x_at)
    lanes_two = pl.ds(c_at * 3 + x_at, 2)
    lanes_three = pl.ds(c_at * 3, 3)

    def remote(src, dst, send, recv, peer):
        return pltpu.make_async_remote_copy(
            src_ref=src, dst_ref=dst, send_sem=send, recv_sem=recv, device_id=peer, device_id_type=MESH
        )

    def cols(s):
        return pl.ds(sections[s][2] * PART, PART)

    def set_of(s):
        return s // PARTS

    def size_of(s, shards, lanes_):
        return sections[s][1].at[sections[s][2], pl.ds(0, shards), pl.ds(0, lanes_)]

    def all_size(group, shards, lanes_):
        return sections[group * PARTS][1].at[:, pl.ds(0, shards), pl.ds(0, lanes_)]

    def landed(block, recv, peer):
        remote(block, block, x_send.at[0], recv, peer).wait_recv()

    def gone(block, send, peer):
        remote(block, block, send, x_recv.at[0], peer).wait_send()

    def held(s, shard, lane):
        _, full, k = sections[s]
        return full.at[k, shard, lane]

    def z_copy(s, up, hop):
        unit = z_at - hop if up else z_at + hop
        shard = unit * n_inner + y_at
        return remote(
            held(s, shard, lanes_two), held(s, shard, lanes_two),
            z_send.at[set_of(s), up, hop], z_recv.at[s, unit], z_next[up],
        )

    def y_copy(s, unit):
        shard = unit * n_inner + y_at
        return remote(
            held(s, shard, lanes_two), held(s, shard, lanes_two),
            y_send.at[set_of(s)], y_recv.at[s], y_peers[0],
        )

    def x_copy(s, unit):
        block = held(s, pl.ds(unit * n_inner, n_inner), lane_mine)
        return remote(block, block, x_send.at[set_of(s)], x_recv.at[s], x_peer)

    def x_own_copy(s):
        block = held(s, z_at * n_inner + 1 - y_at, lane_mine)
        return remote(block, block, x_send.at[set_of(s)], x_recv.at[s], x_peer)

    def c_copy(s, j):
        block = held(s, slice(None), (lanes_two, lane_theirs)[j])
        return remote(block, block, c_send.at[set_of(s)], c_recv.at[s], c_peer)

    def store(s):
        return pltpu.make_async_copy(wt_vmem.at[s - PARTS], wt_out.at[s - PARTS], w_sem.at[s - PARTS])

    def own_shard(s):
        src, _, _ = sections[s]
        return pltpu.make_async_copy(
            src.at[lanes_three, :, cols(s)], held(s, d_at, lanes_three) if s < PARTS else master.at[s % 4], own_sem.at[s]
        )

    def own_ready(s):
        own_shard(s).wait()
        if s >= PARTS:
            wt_vmem[s - PARTS, d_at, lanes_three] = master[s % 4].astype(jnp.bfloat16)

    gathered = ((tok_ref, tok), (None, seg_row))
    firsts = [
        pltpu.make_async_copy(tok_ref, tok.at[z_at], t_own.at[0]),
        pltpu.make_async_copy(pic_ref, patches_in, t_own.at[1]),
    ]

    def token_copy(i, up, hop):
        unit = z_at - hop if up else z_at + hop
        block = gathered[i][1].at[unit]
        return remote(block, block, t_send.at[i, up, hop], t_recv.at[i, unit], z_next[up])

    def token_begin():
        firsts[0].wait()
        number = seg_ref[...].astype(jnp.float32)
        number = jnp.concatenate([number[0:1, :], number[1:2, :] + PER_ROW], axis=1)
        seg_row[z_at] = jnp.broadcast_to(number, (16, PAIR)).astype(jnp.bfloat16)
        for i in range(2):
            for up in range(2):
                pl.when(z_open[up])(token_copy(i, up, 0).start)

    def token_arrive(hop):
        for up in range(2):
            unit = z_at - hop if up else z_at + hop

            @pl.when((unit >= 0) & (unit < GROUP))
            def _():
                for i in range(2):
                    block = gathered[i][1].at[0]
                    landed(block, t_recv.at[i, unit], z_next[up])
                    if hop < GROUP - 1:
                        pl.when(z_open[up])(token_copy(i, up, hop).start)

    def token_gone():
        for up in range(2):
            for hop in range(GROUP - 1):
                unit = z_at - hop if up else z_at + hop
                for i in range(2):
                    pl.when((unit >= 0) & (unit < GROUP) & z_open[up])(
                        functools.partial(gone, gathered[i][1].at[0], t_send.at[i, up, hop], z_next[up])
                    )

    def picture_copy(offset):
        _, other = peer_at(offset, n_dp, n_rep)
        return remote(pic_all.at[me], pic_all.at[me], p_send.at[offset - 1], p_recv.at[offset - 1], other)

    def send_pictures():
        values = image_pool_out[...]
        squares = jnp.sum(values * values, axis=-1, keepdims=True)
        pic_all[me] = (values * lax.rsqrt(squares + LAYER_EPS)).astype(jnp.bfloat16)

        def start(offset, carry):
            picture_copy(offset).start()
            return carry

        lax.fori_loop(1, devices, start, 0)

    def end_pictures():
        def end(offset, carry):
            picture_copy(offset).wait()
            return carry

        lax.fori_loop(1, devices, end, 0)

    def begin(s):
        own_ready(s)
        for up in range(2):
            pl.when(z_open[up])(z_copy(s, up, 0).start)
        y_copy(s, z_at).start()

    def arrive(s, hop):
        for up in range(2):
            unit = z_at - hop if up else z_at + hop

            @pl.when((unit >= 0) & (unit < GROUP))
            def _():
                landed(size_of(s, 1, 2), z_recv.at[s, unit], z_next[up])
                if hop < GROUP - 1:
                    pl.when(z_open[up])(z_copy(s, up, hop).start)
                y_copy(s, unit).start()

    def own_start(s):
        own_shard(s).start()

    def stage_y(s):
        landed(size_of(s, GROUP, 2), y_recv.at[s], y_peers[0])
        for unit in range(GROUP):
            pl.when(unit != z_at)(x_copy(s, unit).start)
        x_own_copy(s).start()
        c_copy(s, 0).start()

    def stage_x(s):
        landed(size_of(s, n_dp - 1, 1), x_recv.at[s], x_peer)
        c_copy(s, 1).start()

    def stage_c(s):
        landed(size_of(s, n_dp, 3), c_recv.at[s], c_peer)
        if s >= PARTS:
            store(s).start()

    def carry_on(step):
        moves = []
        if step + OWN_AHEAD < count:
            moves.append(functools.partial(own_start, step + OWN_AHEAD))
        if step + AHEAD < count:
            moves.append(functools.partial(begin, step + AHEAD))
        for hop in range(1, GROUP):
            s = step - (hop - 1) * LAG_Z
            if 0 <= s < count:
                moves.append(functools.partial(arrive, s, hop))
        for lag, stage in ((AT_Y, stage_y), (AT_X, stage_x), (AT_C, stage_c)):
            if 0 <= step - lag < count:
                moves.append(functools.partial(stage, step - lag))
        if step == TOKENS_AT:
            moves.append(token_begin)
        for hop in range(1, GROUP):
            if step == TOKENS_AT + 2 * hop:
                moves.append(functools.partial(token_arrive, hop))
        return moves


    def weight_tile(s, c):
        _, full, k = sections[s]
        return full[k, :, :, :, aligned(c, TILE)].reshape(D, TILE)

    def weight_rows(s, half):
        _, full, k = sections[s]
        return full[k, pl.ds(half * (n_dp // 2), n_dp // 2)].reshape(D // 2, PART)

    def split_loop(total_, pieces, cost, body):
        size = total_ // pieces
        return [
            (cost, functools.partial(loop, size, functools.partial(lambda base, i: body(base + i), p * size)))
            for p in range(pieces)
        ]

    def first_norm(read, vec):
        def body(i):
            rows = aligned(i, ROWS)
            value = norm_rows(read(i).astype(jnp.float32))
            normed[rows, :] = (value * piece_of(vec, 0) + piece_of(vec, 1)).astype(jnp.bfloat16)

        return split_loop(WORDS // ROWS, 4, 0.5, body)

    def project(slot, part, bias):
        def body(c):
            out = dot(normed[...], weight_tile(slot, c))
            if bias is not None:
                out = out + bias[0][:, pl.ds(pl.multiple_of(bias[1] * D + c * TILE, TILE), TILE)]
            qkv[:, pl.ds(pl.multiple_of(part * D + c * TILE, TILE), TILE)] = out.astype(jnp.bfloat16)

        return split_loop(PART // TILE, 3, 0.6, body)

    def attend(slot, read, vec):
        def body(c):
            where = aligned(c, TILE)
            middle[:, where] = dot(mixed[...], weight_tile(slot, c)) + vec[
                :, pl.ds(pl.multiple_of(4 * D + c * TILE, TILE), TILE)
            ]

        def norm(i):
            rows = aligned(i, ROWS)
            value = middle[rows, :] + read(i).astype(jnp.float32)
            middle[rows, :] = value
            normed_two[rows, :] = (norm_rows(value) * piece_of(vec, 5) + piece_of(vec, 6)).astype(jnp.bfloat16)

        return split_loop(PART // TILE, 3, 0.6, body) + split_loop(WORDS // ROWS, 4, 0.6, norm)

    def expand(slot, part, vec, keep):
        def one(c, p):
            start = part * PART + c * TILE
            if p == 0:
                hid[...] = dot(normed_two[...], weight_tile(slot, c)) + vec[:, pl.ds(8 * D + start, TILE)]

            def inner(i):
                rows = aligned(i + p * (WORDS // ROWS // 2), ROWS)
                value = hid[rows, :]
                phi = 0.5 + 0.5 * lax.erf(value * 0.7071067811865476)
                active[rows, pl.ds(start, TILE)] = (value * phi).astype(jnp.bfloat16)
                if keep:
                    slope[rows, pl.ds(start, TILE)] = phi + value * (
                        0.3989422804014327 * jnp.exp(-0.5 * value * value)
                    )

            loop(WORDS // ROWS // 2, inner, unroll=2)

        return [
            (1.2 - 0.4 * p + 0.2 * keep, functools.partial(one, c, p)) for c in range(PART // TILE) for p in range(2)
        ]

    def shrink(slot, part, vec):
        def one(half):
            where = pl.ds(half * (D // 2), D // 2)
            out = dot_nt(active[:, pl.ds(part * PART, PART)], weight_rows(slot, half))
            if part == 0:
                total[:, where] = out + middle[:, where] + vec[:, pl.ds(7 * D + half * (D // 2), D // 2)]
            else:
                total[:, where] += out

        return [(0.8, functools.partial(one, half)) for half in range(2)]

    def attention(chance_, allowed_of):
        pairs_ = GROUP * HEADS // 2
        return [
            (1.2, functools.partial(attention_forward, qkv, mixed, chance_, allowed_of, first, 4))
            for first in range(0, pairs_, 4)
        ]

    def turn(source, slot, out):
        def body(c):
            turned[slot, aligned(c, PAIR), :] = source[:, aligned(c, PAIR)].T

        loop(D // PAIR, body)
        send_out(turned.at[slot, group_rows], out)

    outs = []

    def send_out(src, dst):
        copy = pltpu.make_async_copy(src, dst, out_sem.at[len(outs)])
        copy.start()
        outs.append(copy)

    group_rows = pl.ds(pl.multiple_of(z_at * (D // GROUP), D // GROUP), D // GROUP)

    def text_read(i):
        per = PAIR // ROWS
        return tok[i // per, aligned(lax.rem(i, per), ROWS), :]

    def text_allowed(i):
        row = seg_row[i].astype(jnp.float32)
        return seg_col[i] == row[0:1, :]

    def text_columns():
        for i in range(GROUP):
            row = seg_row[i].astype(jnp.float32)[0:1, :]
            seg_col[i] = jnp.broadcast_to(row, (PAIR, PAIR)).T

    def image_read(i):
        return padded[i // 2, aligned(lax.rem(i, 2), ROWS), :]

    def picture(axis):
        at = lax.broadcasted_iota(jnp.int32, (PAIR, PAIR), axis)
        number = at // (PAIR // 2)
        return jnp.where(lax.rem(at, PAIR // 2) < patches, number, number + 2)

    def image_allowed(i):
        return picture(0) == picture(1)

    def keep_mark():
        image = lax.broadcasted_iota(jnp.int32, (GROUP * 2, WORDS), 0)
        at = lax.broadcasted_iota(jnp.int32, (GROUP * 2, WORDS), 1)
        inside = (at // (PAIR // 2) == image) & (lax.rem(at, PAIR // 2) < patches)
        return jnp.where(inside, 1.0, 0.0)

    def text_pool():
        send_out(total.at[aligned(z_at, PAIR)], words_out)
        for i in range(GROUP):
            row = seg_row[i].astype(jnp.float32)[0:8, :]
            marks = jnp.where(row == lax.broadcasted_iota(jnp.int32, (8, PAIR), 0).astype(jnp.float32), 1.0, 0.0)
            marks_out[i] = marks
            marks_low = marks.astype(jnp.bfloat16)
            value = total[pl.ds(i * PAIR, PAIR), :]
            high = value.astype(jnp.bfloat16)
            rest = value - high.astype(jnp.float32)
            low = rest.astype(jnp.bfloat16)
            lower = (rest - low.astype(jnp.float32)).astype(jnp.bfloat16)
            sums = dot(
                jnp.concatenate([marks_low] * 3, axis=1), jnp.concatenate([high, low, lower], axis=0)
            )
            text_pool_out[pl.ds(i * 8, 8), :] = sums / jnp.sum(marks, axis=1, keepdims=True)

    def text_part(k):
        slot = k + PARTS
        if k == 0:
            return (
                [(0.3, text_columns)] + first_norm(text_read, tvec_ref) + project(slot, 0, (tvec_ref, 2))
                + [(0.8, lambda: turn(normed, 0, nt_out))]
            )
        if k == 1:
            return project(slot, 1, None)
        if k == 2:
            return (
                project(slot, 2, (tvec_ref, 3)) + [(0.1, lambda: send_out(qkv, qkv_out))]
                + attention(chance, text_allowed)
                + [(0.1, lambda: send_out(chance, chance_out)), (0.8, lambda: turn(mixed, 1, at_out))]
            )
        if k == 3:
            return attend(slot, text_read, tvec_ref) + [
                (0.1, lambda: send_out(middle, mid_out)), (0.8, lambda: turn(normed_two, 2, mt_out))
            ]
        if k < 8:
            return expand(slot, k - 4, tvec_ref, True)
        pieces = shrink(slot, k - 8, tvec_ref)
        if k == 8:
            pieces = [(0.1, lambda: (send_out(active, act_out), send_out(slope, slope_out)))] + pieces
        if k == PARTS - 1:
            pieces = pieces + [(1.0, text_pool)]
        return pieces

    def pool_active(part):
        mark = keep_mark().astype(jnp.bfloat16)
        where = pl.ds(part * PART, PART)
        mean = dot(mark, active[:, where]) * (1.0 / patches)
        high = mean.astype(jnp.bfloat16)
        rest = mean - high.astype(jnp.float32)
        low = rest.astype(jnp.bfloat16)
        apool[0:8, where] = high.astype(jnp.float32)
        apool[8:16, where] = low.astype(jnp.float32)
        apool[16:24, where] = rest - low.astype(jnp.float32)

    def pool_shrink(slot, part):
        for half in range(2):
            where = pl.ds(half * (D // 2), D // 2)
            left = apool[:, pl.ds(part * PART, PART)].astype(jnp.bfloat16)
            out = dot_nt(left, weight_rows(slot, half))
            out = out[0:8] + out[8:16] + out[16:24]
            if part == 0:
                held_ = jnp.concatenate(
                    [
                        jnp.sum(middle[pl.ds(i * (PAIR // 2), patches), where], axis=0, keepdims=True)
                        for i in range(GROUP * 2)
                    ],
                    axis=0,
                )
                image_pool_out[:, where] = (
                    held_ * (1.0 / patches) + ivec_ref[:, pl.ds(7 * D + half * (D // 2), D // 2)] + out
                )
            else:
                image_pool_out[:, where] += out

    def image_part(k):
        slot = k
        if k == 0:
            return first_norm(image_read, ivec_ref) + project(slot, 0, (ivec_ref, 2))
        if k == 1:
            return project(slot, 1, None)
        if k == 2:
            return project(slot, 2, (ivec_ref, 3)) + attention(None, image_allowed)
        if k == 3:
            return attend(slot, image_read, ivec_ref)
        if k < 8:
            return expand(slot, k - 4, ivec_ref, False) + [(0.2, functools.partial(pool_active, k - 4))]
        pieces = [(0.5, functools.partial(pool_shrink, slot, k - 8))]
        if k == PARTS - 1:
            pieces.append((2.0, send_pictures))
        return pieces

    own_start(0)
    for copy in reversed(firsts):
        copy.start()
    for s in range(1, OWN_AHEAD):
        own_start(s)
    firsts[1].wait()
    for i in range(GROUP * 2):
        padded[i] = jnp.concatenate([patches_in[i], jnp.zeros((PAIR // 2 - patches, D), jnp.bfloat16)], axis=0)
    pl.semaphore_wait(barrier, 5 - jnp.where(z_at == 0, 1, 0) - jnp.where(z_at == GROUP - 1, 1, 0))
    for s in range(AHEAD):
        begin(s)
    moves = [(step, move) for step in range(count + AT_C) for move in carry_on(step)]
    by_step = {}
    for step, move in moves:
        by_step.setdefault(step, []).append(move)
    timed = []
    for step in sorted(by_step):
        for i, move in enumerate(by_step[step]):
            timed.append((STEP_TIME * (step + i / len(by_step[step])), step, move))
    clock, done = 0.0, 0
    for s in range(count):
        pieces = image_part(s) if s < PARTS else text_part(s - PARTS)
        while done < len(timed) and timed[done][1] <= s + AT_C:
            clock = max(clock, timed[done][0])
            timed[done][2]()
            done += 1
        for cost, piece in pieces:
            piece()
            clock += cost
            while done < len(timed) and timed[done][0] <= clock:
                timed[done][2]()
                done += 1
    while done < len(timed):
        timed[done][2]()
        done += 1
    for copy in outs:
        copy.wait()
    for s in range(PARTS, count):
        store(s).wait()
    token_gone()
    end_pictures()
    for group in range(2):
        for up in range(2):
            for hop in range(GROUP - 1):
                unit = z_at - hop if up else z_at + hop
                pl.when((unit >= 0) & (unit < GROUP) & z_open[up])(
                    functools.partial(gone, all_size(group, 1, 2), z_send.at[group, up, hop], z_next[up])
                )
        gone(all_size(group, GROUP, 2), y_send.at[group], y_peers[0])
        gone(all_size(group, n_dp - 1, 1), x_send.at[group], x_peer)
        gone(all_size(group, n_dp, 3), c_send.at[group], c_peer)


def gather_and_forward(n_dp, n_rep, text_low, image_low, tokens, segments, pictures, text_vectors, image_vectors):
    own, columns = text_low.shape
    images, patches = pictures.shape[0], pictures.shape[1]
    lane_rows = own // LANES
    count = 2 * PARTS
    hbm, vmem = pl.BlockSpec(memory_space=pltpu.HBM), pl.BlockSpec(memory_space=pltpu.VMEM)
    low, full = jnp.bfloat16, jnp.float32
    shape = jax.ShapeDtypeStruct
    gathered = shape((PARTS, n_dp, LANES, lane_rows, PART), low)
    turned = shape((D // GROUP, WORDS), low)
    pairs = GROUP * HEADS // 2
    dma = pltpu.SemaphoreType.DMA
    outs = pl.pallas_call(
        functools.partial(forward_kernel, n_dp, n_rep, patches),
        out_shape=(
            gathered, shape((n_dp * n_rep, images, D), low), shape((PAIR, D), full), shape((8 * GROUP, D), full),
            shape((GROUP, 8, PAIR), full), shape((WORDS, 3 * D), low), shape((pairs, 2 * PAIR, PAIR), full),
            shape((WORDS, D), full), shape((WORDS, FF), full), shape((WORDS, FF), low), turned, turned, turned,
        ),
        in_specs=[hbm] * 4 + [vmem] * 3,
        out_specs=(hbm, vmem, hbm, vmem, vmem) + (hbm,) * 8,
        scratch_shapes=[
            pltpu.VMEM((PARTS, n_dp, LANES, lane_rows, PART), low),
            pltpu.VMEM((PARTS, n_dp, LANES, lane_rows, PART), low),
            pltpu.VMEM((GROUP, PAIR, D), low),
            pltpu.VMEM((GROUP, PAIR, PAIR), full),
            pltpu.VMEM((GROUP, 16, PAIR), low),
            pltpu.VMEM((WORDS, D), low),
            pltpu.VMEM((WORDS, 3 * D), low),
            pltpu.VMEM((WORDS, D), low),
            pltpu.VMEM((WORDS, D), full),
            pltpu.VMEM((WORDS, D), low),
            pltpu.VMEM((WORDS, FF), low),
            pltpu.VMEM((WORDS, FF), full),
            pltpu.VMEM((pairs, 2 * PAIR, PAIR), full),
            pltpu.VMEM((WORDS, D), full),
            pltpu.VMEM((WORDS, TILE), full),
            pltpu.VMEM((3, D, WORDS), low),
            pltpu.VMEM((24, FF), full),
            pltpu.VMEM((images, D), full),
            pltpu.VMEM(pictures.shape, low),
            pltpu.VMEM((images, PAIR // 2, D), low),
            pltpu.VMEM((4, 3, lane_rows, PART), full),
            dma((2, 2, GROUP - 1)), dma((count, GROUP)), dma((2,)), dma((count,)),
            dma((2,)), dma((count,)), dma((2,)), dma((count,)),
            dma((2, 2, GROUP - 1)), dma((2, GROUP)), dma((2,)), dma((count,)), dma((PARTS,)), dma((12,)),
            dma((n_dp * n_rep - 1,)), dma((n_dp * n_rep - 1,)),
        ],
        compiler_params=pltpu.CompilerParams(collective_id=5, has_side_effects=True, vmem_limit_bytes=60 << 20),
        name="gather_and_forward",
    )(
        text_low.reshape(LANES, lane_rows, columns), image_low.reshape(LANES, lane_rows, columns), tokens,
        pictures, segments,
        text_vectors.reshape(1, -1), image_vectors.reshape(1, -1),
    )
    return (outs[0].reshape(PARTS, D, PART),) + tuple(outs[1:])


def backward_kernel(
    n_dp, n_rep,
    wt_ref, nt_ref, at_ref, mt_ref, qkv_ref, chance_ref, mid_ref, slope_ref, act_ref, feed_ref,
    tpool_ref, pic_all, marks_ref, tok_ref, vec_ref, start_ref, flat_ref, moving_ref,
    m_out, input_out, loss_out, left_out, right_out, nvec_out, nvmom_out,
    weight, turned, qkv, chance, middle, slope, active, grad_hidden, grad_mix, low, low_mixed, wide, block, sent, got, sums, dy_ref, e2t, cap_all, rows_out, vector_out,
    factor, factor_rep, factor_dp, basis, tiles, tiles_rep, quarter, tiles_dp, everything,
    load_sem, send, recv, c_send, c_recv, m_sem, g_send, g_recv,
):
    n_inner = n_dp // GROUP
    d_at, r_at = lax.axis_index("dp"), lax.axis_index("rep")
    z_at, y_at = d_at // n_inner, lax.rem(d_at, n_inner)
    peer = (z_at * n_inner + 1 - y_at, r_at)
    own = D // n_dp
    share = 1.0 / GROUP

    barrier = pltpu.get_barrier_semaphore()
    devices = n_dp * n_rep
    near = n_inner * n_rep

    def near_peer(k):
        other = lax.rem(y_at * n_rep + r_at + k, near)
        return z_at * n_inner + other // n_rep, lax.rem(other, n_rep)

    rep_peers = [(d_at, lax.rem(r_at + k, n_rep)) for k in range(1, n_rep)]
    dp_peers = [(lax.rem(d_at + k, n_dp), r_at) for k in range(1, n_dp)]
    far_peers = [
        (lax.rem(z_at + k, GROUP) * n_inner + y, r_at) for k in range(1, GROUP) for y in range(n_inner)
    ]
    met = near - 1 + len(far_peers)
    for other in [near_peer(k) for k in range(1, near)] + far_peers:
        pl.semaphore_signal(barrier, inc=1, device_id=other, device_id_type=MESH)
    loads = {}

    def fetch(name, src, dst):
        copy = pltpu.make_async_copy(src, dst, load_sem.at[len(loads)])
        copy.start()
        loads[name] = copy

    def need(*names):
        for name in names:
            loads[name].wait()

    fetch("act", act_ref, active)
    for part in range(4):
        fetch(("w", 8 + part), wt_ref.at[8 + part], weight.at[8 + part])
    fetch("slope", slope_ref, slope)
    fetch("mt", mt_ref, turned.at[0])
    for part in range(4):
        fetch(("w", 4 + part), wt_ref.at[4 + part], weight.at[4 + part])
    fetch("mid", mid_ref, middle)
    fetch("at", at_ref, turned.at[1])
    fetch(("w", 3), wt_ref.at[3], weight.at[3])
    fetch("qkv", qkv_ref, qkv)
    fetch("chance", chance_ref, chance)
    fetch("nt", nt_ref, turned.at[2])
    for part in range(3):
        fetch(("w", part), wt_ref.at[part], weight.at[part])
    fetch("feed", feed_ref, rows_out)

    def exchange(s):
        return pltpu.make_async_remote_copy(
            src_ref=sent.at[s], dst_ref=got.at[s], send_sem=send.at[s], recv_sem=recv.at[s],
            device_id=peer, device_id_type=MESH,
        )

    own_rows = pl.ds(pl.multiple_of(y_at * own, own), own)
    other_rows = pl.ds(pl.multiple_of((1 - y_at) * own, own), own)

    def exchange_heads(j):
        where = (pl.ds(0, 3), slice(None), pl.ds(j * PAIR, PAIR))
        return pltpu.make_async_remote_copy(
            src_ref=sent.at[where], dst_ref=got.at[where], send_sem=send.at[PARTS + j], recv_sem=recv.at[PARTS + j],
            device_id=peer, device_id_type=MESH,
        )

    def outer(s, left, right_of):
        def body(c):
            block[:, pl.ds(0, TILE)] = dot(left, right_of(c))
            where = pl.ds(pl.multiple_of(s * PART + c * TILE, TILE), TILE)
            rows_out[:, where] = rows_out[:, where] + block[own_rows, pl.ds(0, TILE)]
            sent[s, :, aligned(c, TILE)] = block[other_rows, pl.ds(0, TILE)].astype(jnp.bfloat16)

        loop(PART // TILE, body)
        exchange(s).start()

    ones = jnp.ones((16, WORDS), jnp.bfloat16)

    def put(slot, values):
        for i in range(values.shape[1] // PAIR):
            vector_out[pl.ds(slot // PAIR + i, 1), :] = values[:, i * PAIR : (i + 1) * PAIR]

    def column_sums(values, slot, scale):
        put(slot, dot(ones, values)[0:1, :] * scale)


    def caption_copy(k):
        block_ = cap_all.at[:, y_at * n_rep + r_at]
        return pltpu.make_async_remote_copy(
            src_ref=block_, dst_ref=block_, send_sem=c_send.at[k - 1], recv_sem=c_recv.at[k - 1],
            device_id=near_peer(k), device_id_type=MESH,
        )

    def unit_of(values):
        return values * lax.rsqrt(jnp.sum(values * values, axis=-1, keepdims=True) + LAYER_EPS)

    def contrast():
        group_pairs = GROUP * 8
        for i in range(GROUP):
            cap_all[i, y_at * n_rep + r_at] = unit_of(tpool_ref[pl.ds(i * 8, 8), :]).astype(jnp.bfloat16)
        pl.semaphore_wait(barrier, met)
        for k in range(1, near):
            caption_copy(k).start()
        for k in range(1, near):
            caption_copy(k).wait_recv()
        pairs_ = devices * 8
        pics = pic_all[...].reshape(pairs_, D)
        caps = cap_all[...].reshape(pairs_, D)
        logits = dot_nt(caps, pics) * LOGIT_SCALE
        top = jnp.max(logits, axis=0, keepdims=True)
        image_log = top + jnp.log(jnp.sum(jnp.exp(logits - top), axis=0, keepdims=True))
        top = jnp.max(logits, axis=1, keepdims=True)
        caption_log = top + jnp.log(jnp.sum(jnp.exp(logits - top), axis=1, keepdims=True))
        row = lax.broadcasted_iota(jnp.int32, (pairs_, pairs_), 0)
        column = lax.broadcasted_iota(jnp.int32, (pairs_, pairs_), 1)
        matched = jnp.sum(jnp.where(row == column, logits, 0.0), axis=1, keepdims=True)
        loss = (jnp.sum(image_log) + jnp.sum(caption_log) - 2.0 * jnp.sum(matched)) / (2.0 * pairs_)
        loss_out[0, 0] = loss
        pooled = tpool_ref[...]
        squares = lax.rsqrt(jnp.sum(pooled * pooled, axis=-1, keepdims=True) + LAYER_EPS)
        own_low = (pooled * squares).astype(jnp.bfloat16)
        own_logits = dot_nt(own_low, pics) * LOGIT_SCALE
        top = jnp.max(own_logits, axis=1, keepdims=True)
        own_log = top + jnp.log(jnp.sum(jnp.exp(own_logits - top), axis=1, keepdims=True))
        local = lax.broadcasted_iota(jnp.int32, (group_pairs, pairs_), 0)
        column = lax.broadcasted_iota(jnp.int32, (group_pairs, pairs_), 1)
        wanted = (local // 8) * (near * 8) + (y_at * n_rep + r_at) * 8 + lax.rem(local, 8)
        pick = jnp.where(wanted == column, 1.0, 0.0)
        soft = ((jnp.exp(own_logits - own_log) - pick) * 0.5).astype(jnp.bfloat16)
        across = ((jnp.exp(own_logits - image_log) - pick) * 0.5).astype(jnp.bfloat16)
        grad = LOGIT_SCALE * (dot(soft, pics) + dot(across, pics))
        grad = squares * (
            grad - pooled * (squares * squares) * jnp.sum(grad * pooled, axis=-1, keepdims=True)
        )
        for i in range(GROUP):
            marks = marks_ref[i]
            part = grad[i * 8 : (i + 1) * 8, :] / jnp.sum(marks, axis=1, keepdims=True)
            high, rest = split_two(part)
            rest_low = (part - high.astype(jnp.float32) - rest.astype(jnp.float32)).astype(jnp.bfloat16)
            stacked = jnp.concatenate([high, rest, rest_low], axis=0)
            marks_low = marks.astype(jnp.bfloat16)
            marks_low = jnp.concatenate([marks_low, marks_low, marks_low], axis=0)
            rows = pl.ds(i * PAIR, PAIR)
            words = dot_tn(marks_low, stacked)
            dy_ref[rows, :] = words
            low[rows, :] = words.astype(jnp.bfloat16)
            e2t[:, rows] = dot_tn(stacked, marks_low).astype(jnp.bfloat16)

    contrast()
    need("act", "feed")
    for part in range(4):
        outer(8 + part, e2t[pl.ds(pl.multiple_of(z_at * (D // GROUP), D // GROUP), D // GROUP), :], lambda c: active[:, pl.ds(pl.multiple_of(part * PART + c * TILE, TILE), TILE)])
    need("slope")
    column_sums(low[...], 7 * D, share)
    for part in range(4):
        need(("w", 8 + part))

        def hidden_body(c):
            where = pl.ds(pl.multiple_of(part * PART + c * TILE, TILE), TILE)
            out = dot(low[...], weight[8 + part, :, aligned(c, TILE)])
            grad_hidden[:, where] = (out * slope[:, where]).astype(jnp.bfloat16)

        loop(PART // TILE, hidden_body)
    need("mt")
    for part in range(4):
        outer(
            4 + part, turned[0], lambda c: grad_hidden[:, pl.ds(pl.multiple_of(part * PART + c * TILE, TILE), TILE)]
        )
    for part in range(4):
        need(("w", 4 + part))
    for half in range(2):
        rows = pl.ds(half * (D // 2), D // 2)
        out = dot_nt(grad_hidden[:, pl.ds(0, PART)], weight[4, rows, :])
        for part in range(1, 4):
            out = out + dot_nt(grad_hidden[:, pl.ds(part * PART, PART)], weight[4 + part, rows, :])
        wide[:, rows] = out
    need("mid")

    def norm_back(value, grad, gain):
        center = value - jnp.mean(value, axis=-1, keepdims=True)
        scale = lax.rsqrt(jnp.mean(center * center, axis=-1, keepdims=True) + LAYER_EPS)
        unit = center * scale
        inner = grad * gain
        out = scale * (
            inner - jnp.mean(inner, axis=-1, keepdims=True) - unit * jnp.mean(inner * unit, axis=-1, keepdims=True)
        )
        return out, grad * unit

    def fold(values):
        return jnp.sum(values.reshape(ROWS // 8, 8, D), axis=0)

    sums[...] = jnp.zeros_like(sums)

    def second(i):
        rows = aligned(i, ROWS)
        grad = wide[rows, :]
        out, product = norm_back(middle[rows, :], grad, piece_of(vec_ref, 5))
        sums[0] += fold(product)
        sums[1] += fold(grad)
        out = out + dy_ref[rows, :]
        middle[rows, :] = out
        low[rows, :] = out.astype(jnp.bfloat16)

    loop(WORDS // ROWS, second)
    put(5 * D, jnp.sum(sums[0], axis=0, keepdims=True) * share)
    put(6 * D, jnp.sum(sums[1], axis=0, keepdims=True) * share)
    need("at", ("w", 3))
    outer(3, turned[1], lambda c: low[:, aligned(c, TILE)])
    for half in range(2):
        rows = pl.ds(half * (D // 2), D // 2)
        low_mixed[:, rows] = dot_nt(low[...], weight[3, rows, :]).astype(jnp.bfloat16)
    need("qkv", "chance")
    pairs = HEADS // 2

    def attention(j, i):
        at = i * pairs + j
        rows = pl.ds(i * PAIR, PAIR)
        q_cols = pl.ds(j * PAIR, PAIR)
        k_cols = pl.ds(D + j * PAIR, PAIR)
        v_cols = pl.ds(2 * D + j * PAIR, PAIR)
        query, key, value = qkv[rows, q_cols], qkv[rows, k_cols], qkv[rows, v_cols]
        grad = two_heads(low_mixed[rows, q_cols])
        weight_ = chance[at]
        grad_mix[rows, v_cols] = dot_tn(weight_.astype(jnp.bfloat16), grad).astype(jnp.bfloat16)
        back = dot_nt(grad, value)
        back = weight_ * (back - jnp.sum(weight_ * back, axis=-1, keepdims=True))
        back = back.astype(jnp.bfloat16)
        side = jnp.concatenate([back[:PAIR], back[PAIR:]], axis=1)
        grad_mix[rows, q_cols] = (dot(side, two_heads(key)) * SCORE_SCALE).astype(jnp.bfloat16)
        grad_mix[rows, k_cols] = (dot_tn(back, two_heads(query)) * SCORE_SCALE).astype(jnp.bfloat16)

    need("nt")
    for j in range(pairs):
        for i in range(GROUP):
            attention(j, i)
        for part in range(3):
            value = dot(turned[2], grad_mix[:, pl.ds(part * D + j * PAIR, PAIR)])
            block[:, pl.ds(part * PAIR, PAIR)] = value
            where = pl.ds(part * D + j * PAIR, PAIR)
            rows_out[:, where] = rows_out[:, where] + block[own_rows, pl.ds(part * PAIR, PAIR)]
            sent[part, :, pl.ds(j * PAIR, PAIR)] = block[other_rows, pl.ds(part * PAIR, PAIR)].astype(jnp.bfloat16)
        exchange_heads(j).start()
    column_sums(low[...], 4 * D, share)
    column_sums(grad_hidden[...], 8 * D, share)
    column_sums(grad_mix[:, pl.ds(0, D)], 2 * D, share)
    column_sums(grad_mix[:, pl.ds(2 * D, D)], 3 * D, share)
    for part in range(3):
        need(("w", part))
    mine = aligned(z_at, PAIR)
    for half in range(2):
        rows = pl.ds(half * (D // 2), D // 2)
        out = dot_nt(grad_mix[mine, pl.ds(0, PART)], weight[0, rows, :])
        for part in range(1, 3):
            out = out + dot_nt(grad_mix[mine, pl.ds(part * PART, PART)], weight[part, rows, :])
        wide[pl.ds(0, PAIR), rows] = out
    sums[...] = jnp.zeros_like(sums)

    def first(i):
        rows = aligned(i, ROWS)
        grad = wide[rows, :]
        out, product = norm_back(tok_ref[rows, :].astype(jnp.float32), grad, piece_of(vec_ref, 0))
        sums[0] += fold(product)
        sums[1] += fold(grad)
        input_out[rows, :] = out + middle[pl.ds(pl.multiple_of(z_at * PAIR + i * ROWS, ROWS), ROWS), :]

    loop(PAIR // ROWS, first)
    put(0, jnp.sum(sums[0], axis=0, keepdims=True))
    put(D, jnp.sum(sums[1], axis=0, keepdims=True))

    bounds = matrix_bounds()
    rank = start_ref.shape[0]
    strip = n_dp * OWN_TILES
    sums_of = {}

    def take(s):
        where = pl.ds(s * PART, PART)
        rows_out[:, where] = rows_out[:, where] + got[s].astype(jnp.float32)
        high, rest = split_two(rows_out[:, where])
        start_high, start_low = split_two(start_ref[:, where])
        both = jnp.concatenate([start_high, start_low], axis=0)
        matrix = 0 if s < 3 else 1 if s == 3 else 2 if s < 8 else 3
        out, out_rest = dot_nt(both, high), dot_nt(both, rest)
        out = out[:rank] + out[rank:] + out_rest[:rank]
        sums_of[matrix] = out if matrix not in sums_of else sums_of[matrix] + out

    for s in (8, 9, 10, 11, 4, 5, 6, 7, 3):
        exchange(s).wait_recv()
        take(s)
    for j in range(pairs):
        exchange_heads(j).wait_recv()
    for s in range(3):
        take(s)
    m_copy = pltpu.make_async_copy(rows_out, m_out, m_sem)
    m_copy.start()
    factor[...] = jnp.zeros_like(factor)
    for matrix in range(4):
        factor[pl.ds(matrix * rank, rank), pl.ds(0, own)] = sums_of[matrix]

    def remote(phase, k, src, dst, other):
        return pltpu.make_async_remote_copy(
            src_ref=src, dst_ref=dst, send_sem=g_send.at[phase, k], recv_sem=g_recv.at[phase, k],
            device_id=other, device_id_type=MESH,
        )

    mine = pl.ds(r_at * strip + d_at * OWN_TILES, OWN_TILES)
    strip_mine = pl.ds(r_at * strip, strip)
    phases = [
        [remote(0, k, factor, factor_rep.at[k], other) for k, other in enumerate(rep_peers)],
        [remote(1, k, factor_dp.at[d_at], factor_dp.at[d_at], other) for k, other in enumerate(dp_peers)],
        [
            remote(2, k, tiles.at[pl.ds(other[1] * strip, strip)], tiles_rep.at[k], other)
            for k, other in enumerate(rep_peers)
        ],
        [
            remote(3, k, quarter.at[pl.ds(other[0] * OWN_TILES, OWN_TILES)], tiles_dp.at[k], other)
            for k, other in enumerate(dp_peers)
        ],
        [remote(4, k, everything.at[mine], everything.at[mine], other) for k, other in enumerate(dp_peers)],
        [remote(5, k, everything.at[strip_mine], everything.at[strip_mine], other) for k, other in enumerate(rep_peers)],
    ]

    def begin(phase):
        for copy in phases[phase]:
            copy.start()

    def arrived(phase):
        for copy in phases[phase]:
            copy.wait_recv()

    begin(0)
    arrived(0)
    summed = factor[...]
    for k in range(n_rep - 1):
        summed = summed + factor_rep[k]
    factor_dp[d_at] = summed
    begin(1)
    arrived(1)
    vectors = jnp.concatenate([factor_dp[i] for i in range(n_dp)], axis=1).reshape(4, rank, n_dp * PAIR)
    place = lax.broadcasted_iota(jnp.int32, (4, rank, 1), 1)
    for k in range(rank):
        vector = vectors[:, k : k + 1, :]
        size = jnp.sqrt(jnp.sum(vector * vector, axis=-1, keepdims=True)) + NORM_FLOOR
        vector = vector / size
        along = jnp.sum(vector * vectors, axis=-1, keepdims=True)
        vectors = jnp.where(
            place == k, jnp.broadcast_to(vector, vectors.shape),
            vectors - jnp.where(place > k, along, 0.0) * vector,
        )
    vectors = vectors.reshape(4 * rank, n_dp * PAIR)
    basis[...] = vectors
    left_out[...] = vectors
    basis_high, basis_low = split_two(basis[:, aligned(d_at, PAIR)][:, :own])
    for matrix, (first_col, after_col) in enumerate(bounds):
        where = slice(matrix * rank, (matrix + 1) * rank)
        both = jnp.concatenate([basis_high[where], basis_low[where]], axis=0)

        def project(c):
            high, low = split_two(rows_out[:, pl.ds(pl.multiple_of(first_col + c * TILE, TILE), TILE)])
            out = dot(both, high)
            out = out[:rank] + out[rank:] + dot(both, low)[:rank]
            at = first_col // PAIR + c * (TILE // PAIR)
            for half in range(TILE // PAIR):
                tiles[at + half] = out[:, half * PAIR : (half + 1) * PAIR]

        loop((after_col - first_col) // TILE, project, unroll=3)
    columns = bounds[-1][1] // PAIR
    for i in range(EXTRA):
        tiles[columns + i] = vector_out[pl.ds(i * 8, 8), :]
    for i in range(columns + EXTRA, n_rep * strip):
        tiles[i] = jnp.zeros((8, PAIR), jnp.float32)
    begin(2)
    arrived(2)
    value = tiles[strip_mine]
    for k in range(n_rep - 1):
        value = value + tiles_rep[k]
    quarter[...] = value
    begin(3)
    arrived(3)
    value = quarter[pl.ds(d_at * OWN_TILES, OWN_TILES)]
    for k in range(n_dp - 1):
        value = value + tiles_dp[k]
    everything[mine] = value
    begin(4)
    arrived(4)
    begin(5)
    arrived(5)
    for i in range(columns):
        right_out[:, pl.ds(i * PAIR, PAIR)] = everything[i]
    for i in range(EXTRA):
        at = pl.ds(i * 8, 8)
        moved = MOMENTUM_DECAY * moving_ref[at, :] + everything[columns + i]
        nvmom_out[at, :] = moved
        nvec_out[at, :] = flat_ref[at, :] - STEP_RATE * moved
    m_copy.wait()
    for s in range(3, PARTS):
        exchange(s).wait_send()
    for j in range(pairs):
        exchange_heads(j).wait_send()
    for k in range(1, near):
        caption_copy(k).wait_send()
    for phase in phases:
        for copy in phase:
            copy.wait_send()


def backward(n_dp, n_rep, kept, pooled, pictures, marks, tokens, text_vectors, feedback_rows, start, moving):
    weights, qkv, chance, middle, slope, active, n_turned, a_turned, m_turned = kept
    own = feedback_rows.shape[0]
    hbm, vmem = pl.BlockSpec(memory_space=pltpu.HBM), pl.BlockSpec(memory_space=pltpu.VMEM)
    low, full = jnp.bfloat16, jnp.float32
    shape = jax.ShapeDtypeStruct
    dma = pltpu.SemaphoreType.DMA
    pairs = GROUP * HEADS // 2
    rank = start.shape[0]
    strip = n_dp * OWN_TILES
    flat = (12 * D // PAIR, PAIR)
    return pl.pallas_call(
        functools.partial(backward_kernel, n_dp, n_rep),
        out_shape=(
            shape(feedback_rows.shape, full), shape((PAIR, D), full), shape((1, 1), full),
            shape((4 * rank, n_dp * PAIR), full), shape(start.shape, full), shape(flat, full), shape(flat, full),
        ),
        in_specs=[hbm] * 10 + [vmem] * 8,
        out_specs=(hbm, vmem, pl.BlockSpec(memory_space=pltpu.SMEM)) + (vmem,) * 4,
        scratch_shapes=[
            pltpu.VMEM((PARTS, D, PART), low),
            pltpu.VMEM((3, D // GROUP, WORDS), low),
            pltpu.VMEM((WORDS, 3 * D), low),
            pltpu.VMEM((pairs, 2 * PAIR, PAIR), full),
            pltpu.VMEM((WORDS, D), full),
            pltpu.VMEM((WORDS, FF), full),
            pltpu.VMEM((WORDS, FF), low),
            pltpu.VMEM((WORDS, FF), low),
            pltpu.VMEM((WORDS, 3 * D), low),
            pltpu.VMEM((WORDS, D), low),
            pltpu.VMEM((WORDS, D), low),
            pltpu.VMEM((WORDS, D), full),
            pltpu.VMEM((D // GROUP, 3 * PAIR), full),
            pltpu.VMEM((PARTS, own, PART), low),
            pltpu.VMEM((PARTS, own, PART), low),
            pltpu.VMEM((2, 8, D), full),
            pltpu.VMEM((WORDS, D), full),
            pltpu.VMEM((D, WORDS), low),
            pltpu.VMEM((GROUP, n_dp * n_rep // GROUP, 8, D), low),
            pltpu.VMEM(feedback_rows.shape, full),
            pltpu.VMEM(flat, full),
            pltpu.VMEM((4 * rank, PAIR), full),
            pltpu.VMEM((n_rep - 1, 4 * rank, PAIR), full),
            pltpu.VMEM((n_dp, 4 * rank, PAIR), full),
            pltpu.VMEM((4 * rank, n_dp * PAIR), full),
            pltpu.VMEM((n_rep * strip, 8, PAIR), full),
            pltpu.VMEM((n_rep - 1, strip, 8, PAIR), full),
            pltpu.VMEM((strip, 8, PAIR), full),
            pltpu.VMEM((n_dp - 1, OWN_TILES, 8, PAIR), full),
            pltpu.VMEM((n_rep * strip, 8, PAIR), full),
            dma((24,)), dma((PARTS + 6,)), dma((PARTS + 6,)), dma((8,)), dma((8,)), dma,
            dma((6, n_dp - 1)), dma((6, n_dp - 1)),
        ],
        compiler_params=pltpu.CompilerParams(collective_id=6, has_side_effects=True, vmem_limit_bytes=60 << 20),
        name="backward",
    )(
        weights, n_turned, a_turned, m_turned, qkv, chance, middle, slope, active, feedback_rows,
        pooled, pictures, marks, tokens, text_vectors.reshape(1, -1), start, text_vectors.reshape(flat),
        moving.reshape(flat),
    )


EXTRA = 9
OWN_TILES = 3


def split_two(values):
    high = values.astype(jnp.bfloat16)
    return high, (values - high.astype(jnp.float32)).astype(jnp.bfloat16)


CHUNKS = 4


def finish_kernel(
    n_dp, n_rep,
    rows_ref, mom_ref, wts_ref, words_ref, input_ref, left_ref, right_ref, vec_ref, vmom_ref, loss_ref,
    feed_out, mom_out, wts_out, words_out, input_out, left_out, right_out, vec_out, vmom_out, loss_out,
    rows, mom, wts, change, through, load_sem, store_sem, pass_sem,
):
    own = rows.shape[0]
    piece = own // CHUNKS
    rank = right_ref.shape[0]

    def load(i, j):
        src, dst = ((rows_ref, rows), (mom_ref, mom), (wts_ref, wts))[j]
        span = pl.ds(i * piece, piece)
        return pltpu.make_async_copy(src.at[span], dst.at[span], load_sem.at[i, j])

    def store(i, j):
        src, dst = ((rows, feed_out), (mom, mom_out), (wts, wts_out))[j]
        span = pl.ds(i * piece, piece)
        return pltpu.make_async_copy(src.at[span], dst.at[span], store_sem.at[i, j])

    for i in range(CHUNKS):
        for j in range(3):
            load(i, j).start()
    taken = [
        pltpu.make_async_copy(src, through.at[i], pass_sem.at[i]) for i, src in enumerate((words_ref, input_ref))
    ]
    passed = [
        pltpu.make_async_copy(through.at[i], dst, pass_sem.at[2 + i]) for i, dst in enumerate((words_out, input_out))
    ]
    passed.append(pltpu.make_async_copy(right_ref, right_out, pass_sem.at[4]))
    for copy in taken:
        copy.start()
    passed[2].start()
    vec_out[...] = vec_ref[...]
    vmom_out[...] = vmom_ref[...]
    loss_out[0, 0] = loss_ref[0, 0]
    left_out[...] = jnp.concatenate([left_ref[:, i * PAIR : i * PAIR + own] for i in range(n_dp)], axis=1)
    basis_high, basis_low = split_two(left_ref[:, aligned(lax.axis_index("dp"), PAIR)][:, :own])
    for matrix, (first_col, after_col) in enumerate(matrix_bounds()):
        where = slice(matrix * rank, (matrix + 1) * rank)
        left = jnp.concatenate([basis_high[where], basis_high[where], basis_low[where]], axis=0)

        def approximate(c):
            cols = pl.ds(pl.multiple_of(first_col + c * PART, PART), PART)
            high, low = split_two(right_ref[:, cols])
            change[:, cols] = dot_tn(left, jnp.concatenate([high, low, high], axis=0))

        loop((after_col - first_col) // PART, approximate)
    for i in range(CHUNKS):
        for j in range(3):
            load(i, j).wait()

        def update(c):
            span, cols = pl.ds(i * piece, piece), aligned(c, PART)
            delta = change[span, cols]
            rows[span, cols] = rows[span, cols] - delta * (1.0 / n_rep)
            moved = MOMENTUM_DECAY * mom[span, cols] + delta
            mom[span, cols] = moved
            wts[span, cols] = wts[span, cols] - STEP_RATE * moved

        loop(rows.shape[1] // PART, update)
        for j in range(3):
            store(i, j).start()
        if i == 0:
            for k, copy in enumerate(taken):
                copy.wait()
                passed[k].start()
    for copy in passed:
        copy.wait()
    for i in range(CHUNKS):
        for j in range(3):
            store(i, j).wait()


def finish(n_dp, n_rep, rows, momentum, weights, left, right, words, grad_inputs, vectors, vector_momentum, loss):
    own, columns = rows.shape
    hbm, vmem = pl.BlockSpec(memory_space=pltpu.HBM), pl.BlockSpec(memory_space=pltpu.VMEM)
    smem = pl.BlockSpec(memory_space=pltpu.SMEM)
    full = jnp.float32
    shape = jax.ShapeDtypeStruct
    dma = pltpu.SemaphoreType.DMA
    big = shape(rows.shape, full)
    return pl.pallas_call(
        functools.partial(finish_kernel, n_dp, n_rep),
        out_shape=(
            big, big, big, shape(words.shape, full), shape(grad_inputs.shape, full),
            shape((left.shape[0], n_dp * own), full), shape(right.shape, full), shape(vectors.shape, full),
            shape(vectors.shape, full), shape((1, 1), full),
        ),
        in_specs=[hbm] * 5 + [vmem] * 4 + [smem],
        out_specs=(hbm,) * 5 + (vmem, hbm, vmem, vmem, smem),
        scratch_shapes=[pltpu.VMEM(rows.shape, full)] * 4
        + [pltpu.VMEM((2,) + words.shape, full), dma((CHUNKS, 3)), dma((CHUNKS, 3)), dma((5,))],
        compiler_params=pltpu.CompilerParams(vmem_limit_bytes=60 << 20),
        name="finish",
    )(rows, momentum, weights, words, grad_inputs, left, right, vectors, vector_momentum, loss)


def peer_at(offset, n_dp, n_rep):
    me = lax.axis_index("dp") * n_rep + lax.axis_index("rep")
    other = lax.rem(me + offset, n_dp * n_rep)
    return other, (other // n_rep, lax.rem(other, n_rep))


def meet(n_dp, n_rep):
    total = n_dp * n_rep
    barrier = pltpu.get_barrier_semaphore()

    def hello(offset, carry):
        _, peer = peer_at(offset, n_dp, n_rep)
        pl.semaphore_signal(barrier, inc=1, device_id=peer, device_id_type=MESH)
        return carry

    lax.fori_loop(1, total, hello, 0)
    pl.semaphore_wait(barrier, total - 1)


def spread_kernel(n_dp, n_rep, mine_ref, all_ref, send, recv, own_sem):
    total = n_dp * n_rep
    me = lax.axis_index("dp") * n_rep + lax.axis_index("rep")
    own = pltpu.make_async_copy(mine_ref, all_ref.at[me], own_sem)
    own.start()
    meet(n_dp, n_rep)

    def copy(offset):
        _, peer = peer_at(offset, n_dp, n_rep)
        return pltpu.make_async_remote_copy(
            src_ref=mine_ref, dst_ref=all_ref.at[me], send_sem=send.at[offset - 1],
            recv_sem=recv.at[offset - 1], device_id=peer, device_id_type=MESH,
        )

    def begin(offset, carry):
        copy(offset).start()
        return carry

    def finish(offset, carry):
        copy(offset).wait()
        return carry

    lax.fori_loop(1, total, begin, 0)
    own.wait()
    lax.fori_loop(1, total, finish, 0)


def spread(mine, n_dp, n_rep, collective, name):
    total = n_dp * n_rep
    vmem = pl.BlockSpec(memory_space=pltpu.VMEM)
    dma = pltpu.SemaphoreType.DMA
    return pl.pallas_call(
        functools.partial(spread_kernel, n_dp, n_rep),
        out_shape=jax.ShapeDtypeStruct((total,) + mine.shape, mine.dtype),
        in_specs=[vmem],
        out_specs=vmem,
        scratch_shapes=[dma((total - 1,)), dma((total - 1,)), dma],
        compiler_params=pltpu.CompilerParams(
            collective_id=collective, has_side_effects=True, vmem_limit_bytes=48 << 20
        ),
        name=name,
    )(mine)


def total_kernel(n_dp, n_rep, mine_ref, out_ref, parts, sums, send, recv, send_two, recv_two):
    total = n_dp * n_rep
    me = lax.axis_index("dp") * n_rep + lax.axis_index("rep")
    meet(n_dp, n_rep)

    def scatter(offset):
        other, peer = peer_at(offset, n_dp, n_rep)
        return pltpu.make_async_remote_copy(
            src_ref=mine_ref.at[other], dst_ref=parts.at[offset - 1], send_sem=send.at[offset - 1],
            recv_sem=recv.at[offset - 1], device_id=peer, device_id_type=MESH,
        )

    def share(offset):
        _, peer = peer_at(offset, n_dp, n_rep)
        return pltpu.make_async_remote_copy(
            src_ref=sums, dst_ref=out_ref.at[me], send_sem=send_two.at[offset - 1],
            recv_sem=recv_two.at[offset - 1], device_id=peer, device_id_type=MESH,
        )

    def start_scatter(offset, carry):
        scatter(offset).start()
        return carry

    def add(offset, carry):
        scatter(offset).wait_recv()
        return carry + parts[offset - 1]

    def start_share(offset, carry):
        share(offset).start()
        return carry

    def finish(offset, carry):
        scatter(offset).wait_send()
        share(offset).wait()
        return carry

    lax.fori_loop(1, total, start_scatter, 0)
    result = lax.fori_loop(1, total, add, mine_ref[me])
    sums[...] = result
    lax.fori_loop(1, total, start_share, 0)
    out_ref[me] = result
    lax.fori_loop(1, total, finish, 0)


def total_over_all(flat, n_dp, n_rep, collective, name):
    total = n_dp * n_rep
    count = flat.shape[0]
    chunk = -(-count // (total * 1024)) * 1024
    padded = jnp.pad(flat, (0, total * chunk - count)).reshape(total, chunk // 128, 128)
    vmem = pl.BlockSpec(memory_space=pltpu.VMEM)
    dma = pltpu.SemaphoreType.DMA
    summed = pl.pallas_call(
        functools.partial(total_kernel, n_dp, n_rep),
        out_shape=jax.ShapeDtypeStruct(padded.shape, padded.dtype),
        in_specs=[vmem],
        out_specs=vmem,
        scratch_shapes=[
            pltpu.VMEM((total - 1,) + padded.shape[1:], padded.dtype),
            pltpu.VMEM(padded.shape[1:], padded.dtype),
            dma((total - 1,)), dma((total - 1,)), dma((total - 1,)), dma((total - 1,)),
        ],
        compiler_params=pltpu.CompilerParams(
            collective_id=collective, has_side_effects=True, vmem_limit_bytes=48 << 20
        ),
        name=name,
    )(padded)
    return summed.reshape(-1)[:count]


def masked_scores(query_heads, key_heads, allowed):
    scores = (
        jnp.einsum("rshd,rthd->rhst", query_heads, key_heads, preferred_element_type=jnp.float32)
        * SCORE_SCALE
    )
    return jnp.where(allowed[:, None], scores, MASKED)


def block_forward(inputs, allowed, weights, vector_pieces, pooled_only):
    (
        gain_one, shift_one, bias_query, bias_value, bias_out,
        gain_two, shift_two, bias_shrink, bias_expand,
    ) = vector_pieces
    row_count, seq_tokens = (inputs.shape[0], inputs.shape[1])
    normed = layer_norm(inputs, gain_one, shift_one).astype(jnp.bfloat16)
    mixing = jnp.einsum("rsd,dc->rsc", normed, weights[:, : 3 * D], preferred_element_type=jnp.float32)
    mixing = mixing + jnp.concatenate([bias_query, jnp.zeros_like(bias_query), bias_value])
    head_parts = mixing.astype(jnp.bfloat16).reshape(row_count, seq_tokens, 3, HEADS, HEAD_DIM)
    query_heads, key_heads, value_heads = (head_parts[:, :, 0], head_parts[:, :, 1], head_parts[:, :, 2])
    scores = masked_scores(query_heads, key_heads, allowed)
    highest = jnp.max(scores, axis=-1, keepdims=True)
    log_total = highest + jnp.log(jnp.sum(jnp.exp(scores - highest), axis=-1, keepdims=True))
    attention = jnp.exp(scores - log_total).astype(jnp.bfloat16)
    mixed_heads = jnp.einsum("rhst,rthd->rshd", attention, value_heads, preferred_element_type=jnp.float32)
    mixed_heads = mixed_heads.reshape(row_count, seq_tokens, D).astype(jnp.bfloat16)
    attended = (
        jnp.einsum("rsd,de->rse", mixed_heads, weights[:, 3 * D : 4 * D], preferred_element_type=jnp.float32)
        + bias_out
    )
    middle = inputs + attended
    normed_two = layer_norm(middle, gain_two, shift_two).astype(jnp.bfloat16)
    hidden = (
        jnp.einsum("rsd,df->rsf", normed_two, weights[:, 4 * D : 4 * D + FF], preferred_element_type=jnp.float32)
        + bias_expand
    )
    active = jax.nn.gelu(hidden, approximate=False).astype(jnp.bfloat16)
    shrink = weights[:, 4 * D + FF :]
    if pooled_only:
        mean_active = jnp.mean(active.astype(jnp.float32), axis=1)
        high = mean_active.astype(jnp.bfloat16)
        rest = mean_active - high.astype(jnp.float32)
        low = rest.astype(jnp.bfloat16)
        lower = (rest - low.astype(jnp.float32)).astype(jnp.bfloat16)
        stacked = jnp.concatenate([high, low, lower], axis=0)
        shrunk = jnp.einsum("pf,df->pd", stacked, shrink, preferred_element_type=jnp.float32)
        shrunk = jnp.sum(shrunk.reshape(3, row_count, D), axis=0)
        return jnp.mean(middle, axis=1) + shrunk + bias_shrink
    shrunk = jnp.einsum("rsf,df->rsd", active, shrink, preferred_element_type=jnp.float32) + bias_shrink
    kept = (normed, query_heads, key_heads, value_heads, log_total, mixed_heads, middle, normed_two, hidden, active)
    return (middle + shrunk, kept)


def token_sum(values_low):
    return jnp.sum(values_low.astype(jnp.float32).reshape(-1, values_low.shape[-1]), axis=0)


def block_backward(inputs, allowed, weights, vector_pieces, forward_kept, grad_out, own_group, own_count):
    (gain_one, shift_one, _, _, _, gain_two, shift_two, _, _) = vector_pieces
    (normed, query_heads, key_heads, value_heads, log_total, mixed_heads, middle, normed_two, hidden, active) = forward_kept
    row_count, seq_tokens = (inputs.shape[0], inputs.shape[1])
    grad_shrunk = grad_out.astype(jnp.bfloat16)
    grad_active = jnp.einsum("rsd,df->rsf", grad_shrunk, weights[:, 4 * D + FF :], preferred_element_type=jnp.float32)
    _, gelu_back = jax.vjp(lambda before_gelu: jax.nn.gelu(before_gelu, approximate=False), hidden)
    grad_hidden = gelu_back(grad_active)[0].astype(jnp.bfloat16)
    grad_normed_two = jnp.einsum(
        "rsf,df->rsd", grad_hidden, weights[:, 4 * D : 4 * D + FF], preferred_element_type=jnp.float32
    )
    _, norm_two_back = jax.vjp(layer_norm, middle, gain_two, shift_two)
    grad_middle, grad_gain_two, grad_shift_two = norm_two_back(grad_normed_two)
    grad_middle = grad_middle + grad_out
    grad_attended = grad_middle.astype(jnp.bfloat16)
    grad_mixed = jnp.einsum("rse,de->rsd", grad_attended, weights[:, 3 * D : 4 * D], preferred_element_type=jnp.float32)
    grad_mixed = grad_mixed.astype(jnp.bfloat16).reshape(row_count, seq_tokens, HEADS, HEAD_DIM)
    attention = jnp.exp(masked_scores(query_heads, key_heads, allowed) - log_total)
    grad_values = jnp.einsum("rhst,rshd->rthd", attention.astype(jnp.bfloat16), grad_mixed, preferred_element_type=jnp.float32)
    grad_attention = jnp.einsum("rshd,rthd->rhst", grad_mixed, value_heads, preferred_element_type=jnp.float32)
    grad_scores = attention * (grad_attention - jnp.sum(attention * grad_attention, axis=-1, keepdims=True))
    grad_scores = grad_scores.astype(jnp.bfloat16)
    grad_query = jnp.einsum("rhst,rthd->rshd", grad_scores, key_heads, preferred_element_type=jnp.float32) * SCORE_SCALE
    grad_keys = jnp.einsum("rhst,rshd->rthd", grad_scores, query_heads, preferred_element_type=jnp.float32) * SCORE_SCALE
    grad_mixing = (
        jnp.stack([grad_query, grad_keys, grad_values], axis=2).reshape(row_count, seq_tokens, 3 * D).astype(jnp.bfloat16)
    )

    def mine(values):
        return lax.dynamic_slice_in_dim(values, own_group * own_count, own_count, 0)

    grad_normed = jnp.einsum("rsc,dc->rsd", mine(grad_mixing), weights[:, : 3 * D], preferred_element_type=jnp.float32)
    _, norm_one_back = jax.vjp(layer_norm, mine(inputs), gain_one, shift_one)
    grad_inputs, grad_gain_one, grad_shift_one = norm_one_back(grad_normed)
    grad_inputs = grad_inputs + mine(grad_middle)
    share = 1.0 / GROUP
    vector_grad = jnp.concatenate(
        [
            grad_gain_one, grad_shift_one,
            share * token_sum(grad_mixing[..., :D]), share * token_sum(grad_mixing[..., 2 * D :]),
            share * token_sum(grad_attended), share * grad_gain_two, share * grad_shift_two,
            share * token_sum(grad_shrunk), share * token_sum(grad_hidden),
        ]
    )
    tokens = row_count * seq_tokens
    outer_terms = (
        (normed.reshape(tokens, D), grad_mixing.reshape(tokens, 3 * D)),
        (mixed_heads.reshape(tokens, D), grad_attended.reshape(tokens, D)),
        (normed_two.reshape(tokens, D), grad_hidden.reshape(tokens, FF)),
        (grad_shrunk.reshape(tokens, D), active.reshape(tokens, FF)),
    )
    return (grad_inputs, vector_grad, outer_terms)


def orthonormal(stacked):
    waiting = [stacked[:, column_id] for column_id in range(stacked.shape[1])]
    finished = []
    while waiting:
        vector = waiting.pop(0)
        vector = vector / (jnp.sqrt(jnp.sum(vector * vector, axis=-1, keepdims=True)) + NORM_FLOOR)
        finished.append(vector)
        if waiting:
            later = jnp.stack(waiting, axis=1)
            later = later - jnp.sum(vector[:, None] * later, axis=-1, keepdims=True) * vector[:, None]
            waiting = [later[:, i] for i in range(later.shape[1])]
    return jnp.stack(finished, axis=1)


def rows_factor(start_part, row_block):
    return jnp.einsum("kc,dc->kd", start_part, row_block, precision=PRECISE)


def per_device(
    image_tokens, image_weights, image_vectors, text_tokens, segments, text_weights,
    text_vectors, momentum, vector_momentum, error_feedback, start_factors,
):
    n_rep, n_dp = lax.axis_size("rep"), lax.axis_size("dp")
    n_inner = n_dp // GROUP
    total = n_rep * n_dp
    device_pairs, patches = image_tokens.shape[0], image_tokens.shape[1]
    text_rows, seq_tokens = text_tokens.shape[0], text_tokens.shape[1]
    pair_total = device_pairs * total
    own_rows = text_weights.shape[0]
    d_at, r_at = lax.axis_index("dp"), lax.axis_index("rep")
    z_at, y_at = d_at // n_inner, d_at % n_inner
    row_start = d_at * own_rows
    factor_rank = start_factors.shape[0]
    bounds = matrix_bounds()
    tokens = text_tokens.reshape(text_rows * seq_tokens, D)
    feedback_rows = error_feedback[0]
    fused = (
        own_rows % (16 * LANES) == 0 and n_inner == 2 and n_rep == 4 and device_pairs == 8
        and text_rows * seq_tokens == PAIR and 2 * seq_tokens == PAIR and 2 * patches <= PAIR
        and n_dp == 8 and factor_rank == 8
    )
    if fused:
        outs = gather_and_forward(
            n_dp, n_rep, text_weights, image_weights, tokens, segments, image_tokens, text_vectors, image_vectors
        )
        pictures, words, pooled, marks = outs[1:5]
        kept = (outs[0],) + tuple(outs[5:])
        worker_rows, grad_inputs, loss, left_basis, new_right, new_vectors, new_vector_momentum = backward(
            n_dp, n_rep, kept, pooled, pictures, marks, tokens, text_vectors, feedback_rows, start_factors,
            vector_momentum,
        )
        (
            new_feedback, new_momentum, new_weights, words, grad_inputs, left_basis, new_right,
            new_vectors, new_vector_momentum, loss,
        ) = finish(
            n_dp, n_rep, worker_rows, momentum, text_weights, left_basis, new_right, words, grad_inputs,
            new_vectors, new_vector_momentum, loss,
        )
        return (
            loss.reshape(()), words.reshape(text_rows, seq_tokens, D), grad_inputs.reshape(text_rows, seq_tokens, D),
            new_weights, new_momentum, new_feedback[None], new_vectors.reshape(-1), new_vector_momentum.reshape(-1),
            left_basis, new_right,
        )
    text_low, frozen, token_group, segment_group = gather_weights(
        n_dp, text_weights.astype(jnp.bfloat16), image_weights, tokens, segments
    )
    text_low, frozen = text_low.reshape(D, -1), frozen.reshape(D, -1)
    full_mask = jnp.zeros((device_pairs, patches, patches), jnp.int32) == 0
    image_pooled = block_forward(
        image_tokens.astype(jnp.float32), full_mask, frozen, vector_parts(image_vectors), True
    )
    group_rows = GROUP * text_rows
    text_float = token_group.reshape(group_rows, seq_tokens, D).astype(jnp.float32)
    segment_all = segment_group.reshape(group_rows, seq_tokens)
    allowed = segment_all[:, :, None] == segment_all[:, None, :]
    vector_pieces = vector_parts(text_vectors)
    group_output, forward_kept = block_forward(text_float, allowed, text_low, vector_pieces, False)
    text_output = lax.dynamic_slice_in_dim(group_output, z_at * text_rows, text_rows, 0)
    caption_marks = (
        segment_all[:, None, :] == jnp.arange(PER_ROW, dtype=jnp.int32)[None, :, None]
    ).astype(jnp.float32)
    counts = jnp.sum(caption_marks, axis=-1, keepdims=True)
    pooled = (jnp.einsum("rks,rsd->rkd", caption_marks, group_output, precision=PRECISE) / counts).reshape(-1, D)
    image_emb = unit_rows(image_pooled).astype(jnp.bfloat16)
    text_norm, embed_back = jax.vjp(unit_rows, pooled)
    text_emb = text_norm.astype(jnp.bfloat16)
    own_emb = lax.dynamic_slice_in_dim(text_emb, z_at * device_pairs, device_pairs, 0)
    embeddings = spread(jnp.concatenate([image_emb, own_emb], axis=0), n_dp, n_rep, 2, "spread_embeddings")
    image_all = embeddings[:, :device_pairs].reshape(pair_total, D)
    text_all = embeddings[:, device_pairs:].reshape(pair_total, D)
    own_pairs = (
        ((jnp.arange(GROUP, dtype=jnp.int32) * n_inner + y_at) * n_rep + r_at)[:, None] * device_pairs
        + jnp.arange(device_pairs, dtype=jnp.int32)[None, :]
    ).reshape(-1)
    logits = LOGIT_SCALE * jnp.einsum("pd,bd->pb", image_all, text_all, preferred_element_type=jnp.float32)
    image_top = jnp.max(logits, axis=1)
    image_log_total = image_top + jnp.log(jnp.sum(jnp.exp(logits - image_top[:, None]), axis=1))
    caption_top = jnp.max(logits, axis=0)
    caption_log_total = caption_top + jnp.log(jnp.sum(jnp.exp(logits - caption_top[None, :]), axis=0))
    pair_ids = jnp.arange(pair_total, dtype=jnp.int32)
    matched = jnp.sum(jnp.where(pair_ids[:, None] == pair_ids[None, :], logits, 0.0), axis=1)
    loss_total = (jnp.sum(image_log_total - matched) + jnp.sum(caption_log_total - matched)) / (2.0 * pair_total)
    diagonal_pick = (pair_ids[None, :] == own_pairs[:, None]).astype(jnp.float32)
    text_logits = LOGIT_SCALE * jnp.einsum("pd,bd->pb", text_emb, image_all, preferred_element_type=jnp.float32)
    text_top = jnp.max(text_logits, axis=1, keepdims=True)
    text_log_total = text_top + jnp.log(jnp.sum(jnp.exp(text_logits - text_top), axis=1, keepdims=True))
    text_soft = ((jnp.exp(text_logits - text_log_total) - diagonal_pick) * 0.5).astype(jnp.bfloat16)
    column_soft = ((jnp.exp(text_logits - image_log_total[None, :]) - diagonal_pick) * 0.5).astype(jnp.bfloat16)
    grad_text = LOGIT_SCALE * (
        jnp.einsum("pb,bd->pd", text_soft, image_all, preferred_element_type=jnp.float32)
        + jnp.einsum("pb,bd->pd", column_soft, image_all, preferred_element_type=jnp.float32)
    )
    grad_pooled = embed_back(grad_text)[0]
    grad_pooled = grad_pooled.reshape(-1, PER_ROW, D) / counts
    grad_out = jnp.einsum("rks,rkd->rsd", caption_marks, grad_pooled, precision=PRECISE)
    grad_inputs, vector_grad, outer_terms = block_backward(
        text_float, allowed, text_low, vector_pieces, forward_kept, grad_out, z_at, text_rows
    )
    group_width = n_inner * own_rows
    worker_blocks = []
    for (left_side, right_side), (first_col, after_col) in zip(outer_terms, bounds):
        left_cut = lax.dynamic_slice_in_dim(left_side, z_at * group_width, group_width, 1)
        block = jnp.einsum("tc,tk->ck", left_cut, right_side, preferred_element_type=jnp.float32)
        mine = lax.dynamic_slice_in_dim(block, y_at * own_rows, own_rows, 0)
        for k in range(1, n_inner):
            target = lax.rem(y_at + k, n_inner)
            outgoing = lax.dynamic_slice_in_dim(block, target * own_rows, own_rows, 0).astype(jnp.bfloat16)
            pairs = [
                (z * n_inner + y, z * n_inner + (y + k) % n_inner) for z in range(GROUP) for y in range(n_inner)
            ]
            mine = mine + lax.ppermute(outgoing, "dp", pairs).astype(jnp.float32)
        worker_blocks.append(mine + feedback_rows[:, first_col:after_col])
    factor_rows = jnp.concatenate(
        [
            rows_factor(start_factors[:, first_col:after_col], rows)
            for rows, (first_col, after_col) in zip(worker_blocks, bounds)
        ],
        axis=0,
    )
    gathered_rows = spread(factor_rows, n_dp, n_rep, 3, "spread_factors")
    factor = jnp.sum(gathered_rows.reshape(n_dp, n_rep, 4 * factor_rank, own_rows), axis=1)
    factor = jnp.swapaxes(factor, 0, 1).reshape(4, factor_rank, D)
    left_basis = orthonormal(factor).reshape(4 * factor_rank, D)
    basis_rows = lax.dynamic_slice_in_dim(left_basis, row_start, own_rows, 1)
    basis_parts = [basis_rows[i * factor_rank : (i + 1) * factor_rank] for i in range(4)]
    right_part = jnp.concatenate(
        [jnp.einsum("kd,dc->kc", part, rows, precision=PRECISE) for part, rows in zip(basis_parts, worker_blocks)],
        axis=1,
    )
    summed = total_over_all(
        jnp.concatenate([right_part.reshape(-1), vector_grad]), n_dp, n_rep, 4, "total_right"
    )
    new_right = summed[: right_part.size].reshape(right_part.shape)
    vector_total = summed[right_part.size :]
    approximation = jnp.concatenate(
        [
            jnp.einsum("kd,kc->dc", part, new_right[:, first_col:after_col], precision=PRECISE)
            for part, (first_col, after_col) in zip(basis_parts, bounds)
        ],
        axis=1,
    )
    worker_rows = jnp.concatenate(worker_blocks, axis=1)
    new_feedback = (worker_rows - approximation / n_rep)[None]
    new_momentum = MOMENTUM_DECAY * momentum + approximation
    new_weights = text_weights - STEP_RATE * new_momentum
    new_vector_momentum = MOMENTUM_DECAY * vector_momentum + vector_total
    new_vectors = text_vectors - STEP_RATE * new_vector_momentum
    return (
        loss_total, text_output, grad_inputs, new_weights, new_momentum, new_feedback,
        new_vectors, new_vector_momentum, left_basis, new_right,
    )


def solution(mesh):
    placed = (
        P(("dp", "rep"), None, None), P("dp", None), P(), P(("dp", "rep"), None, None), P(("dp", "rep"), None),
        P("dp", None), P(), P("dp", None), P(), P("rep", "dp", None), P(),
    )
    return jax.shard_map(
        per_device,
        mesh=mesh,
        in_specs=placed,
        out_specs=(
            P(), P(("dp", "rep"), None, None), P(("dp", "rep"), None, None), P("dp", None), P("dp", None),
            P("rep", "dp", None), P(), P(), P(), P(),
        ),
        check_vma=False,
    )
```

```python
import functools

import jax
import jax.numpy as jnp
from jax import lax
from jax.experimental import pallas as pl
from jax.experimental.pallas import tpu as pltpu
from jax.sharding import PartitionSpec as P

D = 768
FF = 3072
HEADS = 12
HEAD_DIM = 64
PER_ROW = 4
GROUP = 4
SECTION = 3072
LANE_COLS = 512

PRECISE = lax.Precision.HIGHEST
LAYER_EPS = 1e-06
SCORE_SCALE = 0.125
LOGIT_SCALE = 50.0
MOMENTUM_DECAY = 0.9
STEP_RATE = 0.08
NORM_FLOOR = 1e-08
MASKED = -1e30
MESH = pl.DeviceIdType.MESH


def layer_norm(values, layer_gain, layer_shift):
    center = values - jnp.mean(values, axis=-1, keepdims=True)
    spread = jnp.mean(center * center, axis=-1, keepdims=True)
    return center * lax.rsqrt(spread + LAYER_EPS) * layer_gain + layer_shift


def unit_rows(values):
    return values * lax.rsqrt(jnp.sum(values * values, axis=-1, keepdims=True) + LAYER_EPS)


def vector_parts(vectors):
    pieces = [vectors[position * D : (position + 1) * D] for position in range(8)]
    return pieces + [vectors[8 * D :]]


def matrix_bounds():
    return ((0, 3 * D), (3 * D, 4 * D), (4 * D, 4 * D + FF), (4 * D + FF, 4 * D + 2 * FF))


def gather_kernel(
    n_dp, text_ref, image_ref, tok_ref, seg_ref, wt_ref, wi_ref, tok_out, seg_out,
    z_send, z_recv, y_send, y_recv, x_send, x_recv, c_send, c_recv, t_send, t_recv, t_own, own_sem,
):
    n_inner = n_dp // GROUP
    d_at, r_at = lax.axis_index("dp"), lax.axis_index("rep")
    z_at, y_at = d_at // n_inner, d_at % n_inner
    x_at, c_at = r_at // 2, r_at % 2
    z_peers = [(lax.rem(z_at + k, GROUP) * n_inner + y_at, r_at) for k in range(1, GROUP)]
    z_from = [lax.rem(z_at + GROUP - k, GROUP) for k in range(1, GROUP)]
    y_peers = [(z_at * n_inner + lax.rem(y_at + k, n_inner), r_at) for k in range(1, n_inner)]
    y_from = [lax.rem(y_at + n_inner - k, n_inner) for k in range(1, n_inner)]
    x_peer = (d_at, (1 - x_at) * 2 + c_at)
    c_peer = (d_at, x_at * 2 + 1 - c_at)

    barrier = pltpu.get_barrier_semaphore()
    everyone = z_peers + y_peers + [x_peer, c_peer]
    for peer in everyone:
        pl.semaphore_signal(barrier, inc=1, device_id=peer, device_id_type=MESH)
    pl.semaphore_wait(barrier, len(everyone))

    def shard_of(z, y):
        return z * n_inner + y

    sections = [(image_ref, wi_ref, 0), (text_ref, wt_ref, 0), (image_ref, wi_ref, 1),
                (text_ref, wt_ref, 1), (image_ref, wi_ref, 2), (text_ref, wt_ref, 2)]

    def cols(section, lane):
        start = sections[section][2] * SECTION + lane * LANE_COLS
        return pl.ds(pl.multiple_of(start, 128), LANE_COLS)

    lane_both = c_at
    lane_mine = 2 + x_at * 2 + c_at
    lane_theirs = 2 + (1 - x_at) * 2 + c_at
    lanes = (lane_both, lane_mine)

    locals_ = [
        pltpu.make_async_copy(tok_ref, tok_out.at[z_at], t_own.at[0]),
        pltpu.make_async_copy(seg_ref, seg_out.at[z_at], t_own.at[1]),
    ]
    for s, (src, full, _) in enumerate(sections):
        for j in range(2):
            column = cols(s, lanes[j])
            locals_.append(pltpu.make_async_copy(src.at[:, column], full.at[d_at, :, column], own_sem.at[s, j]))
    for copy in locals_:
        copy.start()

    def remote(src, dst, send, recv, peer):
        return pltpu.make_async_remote_copy(
            src_ref=src, dst_ref=dst, send_sem=send, recv_sem=recv, device_id=peer, device_id_type=MESH
        )

    def z_copy(s, k, j):
        src, full, _ = sections[s]
        return remote(
            src.at[:, cols(s, lanes[j])], full.at[d_at, :, cols(s, lanes[j])],
            z_send.at[s, k, j], z_recv.at[s, k, j], z_peers[k],
        )

    def y_copy(s, q, zi, j):
        src, full, _ = sections[s]
        column = cols(s, lanes[j])
        if zi == 0:
            shard, source = d_at, src.at[:, column]
        else:
            shard = shard_of(z_from[zi - 1], y_at)
            source = full.at[shard, :, column]
        return remote(source, full.at[shard, :, column], y_send.at[s, q, zi, j], y_recv.at[s, q, zi, j], y_peers[q])

    def x_copy(s):
        full = sections[s][1]
        block = full.at[:, :, cols(s, lane_mine)]
        return remote(block, block, x_send.at[s], x_recv.at[s], x_peer)

    def c_copy(s, j):
        full = sections[s][1]
        block = full.at[:, :, cols(s, (lane_both, lane_mine, lane_theirs)[j])]
        return remote(block, block, c_send.at[s, j], c_recv.at[s, j], c_peer)

    count = len(sections)
    tokens = []
    for k in range(GROUP - 1):
        tokens.append(remote(tok_ref, tok_out.at[z_at], t_send.at[0, k], t_recv.at[0, k], z_peers[k]))
        tokens.append(remote(seg_ref, seg_out.at[z_at], t_send.at[1, k], t_recv.at[1, k], z_peers[k]))

    def begin(s):
        for j in range(2):
            for k in range(GROUP - 1):
                z_copy(s, k, j).start()
            for q in range(n_inner - 1):
                y_copy(s, q, 0, j).start()

    begin(0)
    for copy in tokens:
        copy.start()
    for copy in locals_:
        copy.wait()
    begin(1)
    for step in range(count + 3):
        if step < count:
            for k in range(GROUP - 1):
                for j in range(2):
                    z_copy(step, k, j).wait_recv()
                    for q in range(n_inner - 1):
                        y_copy(step, q, k + 1, j).start()
            if step + 2 < count:
                begin(step + 2)
        s = step - 1
        if 0 <= s < count:
            for q in range(n_inner - 1):
                for zi in range(GROUP):
                    for j in range(2):
                        y_copy(s, q, zi, j).wait_recv()
            x_copy(s).start()
            for j in range(2):
                c_copy(s, j).start()
        s = step - 2
        if 0 <= s < count:
            x_copy(s).wait_recv()
            c_copy(s, 2).start()
        s = step - 3
        if 0 <= s < count:
            for j in range(3):
                c_copy(s, j).wait_recv()
    for copy in tokens:
        copy.wait()
    for s in range(count):
        for j in range(2):
            for k in range(GROUP - 1):
                z_copy(s, k, j).wait_send()
            for q in range(n_inner - 1):
                for zi in range(GROUP):
                    y_copy(s, q, zi, j).wait_send()
        x_copy(s).wait_send()
        for j in range(3):
            c_copy(s, j).wait_send()


def gather_weights(n_dp, text_low, image_low, tokens, segments):
    n_inner = n_dp // GROUP
    full = jax.ShapeDtypeStruct((n_dp,) + text_low.shape, jnp.bfloat16)
    hbm = pl.BlockSpec(memory_space=pltpu.HBM)
    dma = pltpu.SemaphoreType.DMA
    return pl.pallas_call(
        functools.partial(gather_kernel, n_dp),
        out_shape=(
            full,
            full,
            jax.ShapeDtypeStruct((GROUP,) + tokens.shape, jnp.bfloat16),
            jax.ShapeDtypeStruct((GROUP,) + segments.shape, jnp.int32),
        ),
        in_specs=[hbm] * 4,
        out_specs=(hbm,) * 4,
        scratch_shapes=[
            dma((6, GROUP - 1, 2)), dma((6, GROUP - 1, 2)),
            dma((6, n_inner - 1, GROUP, 2)), dma((6, n_inner - 1, GROUP, 2)),
            dma((6,)), dma((6,)), dma((6, 3)), dma((6, 3)),
            dma((2, GROUP - 1)), dma((2, GROUP - 1)), dma((2,)), dma((6, 2)),
        ],
        compiler_params=pltpu.CompilerParams(collective_id=1, has_side_effects=True),
        name="gather_weights",
    )(text_low, image_low, tokens, segments)


TILE = 256
PAIR = 128
ROWS = 32
LANES = 6
PART = 768
PARTS = 12
DEPTH = 8
AHEAD = 2
OWN_AHEAD = 4
TOKENS_AT = 6
STEP_TIME = 4.5
LAG_Z = 1
LAG_Y = 1
LAG_X = 2
LAG_C = 1
AT_Y = 2 * LAG_Z + LAG_Y
AT_X = AT_Y + LAG_X
AT_C = AT_X + LAG_C
WORDS = (GROUP * PAIR)


def piece_of(vec_ref, index, width=D):
    return vec_ref[:, pl.ds(index * D, width)]


def loop(count, body, unroll=1):
    def step(i, carry):
        body(i)
        return carry

    lax.fori_loop(0, count, step, 0, unroll=unroll)


def aligned(i, size):
    return pl.ds(pl.multiple_of(i * size, size), size)


def norm_rows(values):
    center = values - jnp.mean(values, axis=-1, keepdims=True)
    spread_ = jnp.mean(center * center, axis=-1, keepdims=True)
    return center * lax.rsqrt(spread_ + LAYER_EPS)


def dot(left, right):
    return jnp.dot(left, right, preferred_element_type=jnp.float32)


def dot_nt(left, right):
    return lax.dot_general(left, right, (((1,), (1,)), ((), ())), preferred_element_type=jnp.float32)


def dot_tn(left, right):
    return lax.dot_general(left, right, (((0,), (0,)), ((), ())), preferred_element_type=jnp.float32)


def lane_is_first():
    return lax.broadcasted_iota(jnp.int32, (PAIR, PAIR), 1) < HEAD_DIM


def two_heads(block):
    first = lane_is_first()
    zero = jnp.zeros_like(block)
    return jnp.concatenate([jnp.where(first, block, zero), jnp.where(first, zero, block)], axis=0)


def attention_forward(qkv, mixed, chance, allowed_of, first, count):
    pairs = HEADS // 2

    def body(k):
        at = first + k
        i, j = at // pairs, lax.rem(at, pairs)
        rows = aligned(i, PAIR)
        query = qkv[rows, aligned(j, PAIR)]
        key = qkv[rows, pl.ds(pl.multiple_of(D + j * PAIR, PAIR), PAIR)]
        value = qkv[rows, pl.ds(pl.multiple_of(2 * D + j * PAIR, PAIR), PAIR)]
        scores = dot_nt(two_heads(query), key) * SCORE_SCALE
        allowed = allowed_of(i)
        scores = jnp.where(jnp.concatenate([allowed, allowed], axis=0), scores, MASKED)
        scores = jnp.exp(scores - jnp.max(scores, axis=-1, keepdims=True))
        weight = scores / jnp.sum(scores, axis=-1, keepdims=True)
        if chance is not None:
            chance[at] = weight
        low = weight.astype(jnp.bfloat16)
        side = jnp.concatenate([low[:PAIR], low[PAIR:]], axis=1)
        mixed[rows, aligned(j, PAIR)] = dot(side, two_heads(value)).astype(jnp.bfloat16)

    loop(count, body, unroll=2)


def forward_kernel(
    n_dp, n_rep, patches,
    text_ref, image_ref, tok_ref, pic_ref, seg_ref, tvec_ref, ivec_ref,
    wt_out, pic_all, words_out, text_pool_out, marks_out, qkv_out, chance_out, mid_out, slope_out,
    act_out, nt_out, at_out, mt_out,
    wi_ref, wt_vmem, tok, seg_col, seg_row, normed, qkv, mixed, middle, normed_two, active, slope, chance, total, hid, turned, apool, image_pool_out, patches_in, padded, master,
    z_send, z_recv, y_send, y_recv, x_send, x_recv, c_send, c_recv, t_send, t_recv, t_own, own_sem, w_sem, out_sem, p_send, p_recv,
):
    n_inner = n_dp // GROUP
    d_at, r_at = lax.axis_index("dp"), lax.axis_index("rep")
    z_at, y_at = d_at // n_inner, lax.rem(d_at, n_inner)
    x_at, c_at = r_at // 2, lax.rem(r_at, 2)
    z_next = [((z_at - 1) * n_inner + y_at, r_at), ((z_at + 1) * n_inner + y_at, r_at)]
    y_peers = [(z_at * n_inner + 1 - y_at, r_at)]
    x_peer = (d_at, (1 - x_at) * 2 + c_at)
    c_peer = (d_at, x_at * 2 + 1 - c_at)

    devices = n_dp * n_rep
    me = d_at * n_rep + r_at
    z_open = (z_at > 0, z_at < GROUP - 1)
    barrier = pltpu.get_barrier_semaphore()

    def hello(peer):
        pl.semaphore_signal(barrier, inc=1, device_id=peer, device_id_type=MESH)

    for peer in (y_peers[0], x_peer, c_peer):
        hello(peer)
    for up in range(2):
        pl.when(z_open[up])(functools.partial(hello, z_next[up]))

    sections = [(image_ref, wi_ref, k) for k in range(PARTS)] + [(text_ref, wt_vmem, k) for k in range(PARTS)]
    count = len(sections)
    lane_mine = c_at * 3 + 2 * x_at
    lane_theirs = c_at * 3 + 2 * (1 - x_at)
    lanes_two = pl.ds(c_at * 3 + x_at, 2)
    lanes_three = pl.ds(c_at * 3, 3)

    def remote(src, dst, send, recv, peer):
        return pltpu.make_async_remote_copy(
            src_ref=src, dst_ref=dst, send_sem=send, recv_sem=recv, device_id=peer, device_id_type=MESH
        )

    def cols(s):
        return pl.ds(sections[s][2] * PART, PART)

    def set_of(s):
        return s // PARTS

    def size_of(s, shards, lanes_):
        return sections[s][1].at[sections[s][2], pl.ds(0, shards), pl.ds(0, lanes_)]

    def all_size(group, shards, lanes_):
        return sections[group * PARTS][1].at[:, pl.ds(0, shards), pl.ds(0, lanes_)]

    def landed(block, recv, peer):
        remote(block, block, x_send.at[0], recv, peer).wait_recv()

    def gone(block, send, peer):
        remote(block, block, send, x_recv.at[0], peer).wait_send()

    def held(s, shard, lane):
        _, full, k = sections[s]
        return full.at[k, shard, lane]

    def z_copy(s, up, hop):
        unit = z_at - hop if up else z_at + hop
        shard = unit * n_inner + y_at
        return remote(
            held(s, shard, lanes_two), held(s, shard, lanes_two),
            z_send.at[set_of(s), up, hop], z_recv.at[s, unit], z_next[up],
        )

    def y_copy(s, unit):
        shard = unit * n_inner + y_at
        return remote(
            held(s, shard, lanes_two), held(s, shard, lanes_two),
            y_send.at[set_of(s)], y_recv.at[s], y_peers[0],
        )

    def x_copy(s, unit):
        block = held(s, pl.ds(unit * n_inner, n_inner), lane_mine)
        return remote(block, block, x_send.at[set_of(s)], x_recv.at[s], x_peer)

    def x_own_copy(s):
        block = held(s, z_at * n_inner + 1 - y_at, lane_mine)
        return remote(block, block, x_send.at[set_of(s)], x_recv.at[s], x_peer)

    def c_copy(s, j):
        block = held(s, slice(None), (lanes_two, lane_theirs)[j])
        return remote(block, block, c_send.at[set_of(s)], c_recv.at[s], c_peer)

    def store(s):
        return pltpu.make_async_copy(wt_vmem.at[s - PARTS], wt_out.at[s - PARTS], w_sem.at[s - PARTS])

    def own_shard(s):
        src, _, _ = sections[s]
        return pltpu.make_async_copy(
            src.at[lanes_three, :, cols(s)], held(s, d_at, lanes_three) if s < PARTS else master.at[s % 4], own_sem.at[s]
        )

    def own_ready(s):
        own_shard(s).wait()
        if s >= PARTS:
            wt_vmem[s - PARTS, d_at, lanes_three] = master[s % 4].astype(jnp.bfloat16)

    gathered = ((tok_ref, tok), (None, seg_row))
    firsts = [
        pltpu.make_async_copy(tok_ref, tok.at[z_at], t_own.at[0]),
        pltpu.make_async_copy(pic_ref, patches_in, t_own.at[1]),
    ]

    def token_copy(i, up, hop):
        unit = z_at - hop if up else z_at + hop
        block = gathered[i][1].at[unit]
        return remote(block, block, t_send.at[i, up, hop], t_recv.at[i, unit], z_next[up])

    def token_begin():
        firsts[0].wait()
        number = seg_ref[...].astype(jnp.float32)
        number = jnp.concatenate([number[0:1, :], number[1:2, :] + PER_ROW], axis=1)
        seg_row[z_at] = jnp.broadcast_to(number, (16, PAIR)).astype(jnp.bfloat16)
        for i in range(2):
            for up in range(2):
                pl.when(z_open[up])(token_copy(i, up, 0).start)

    def token_arrive(hop):
        for up in range(2):
            unit = z_at - hop if up else z_at + hop

            @pl.when((unit >= 0) & (unit < GROUP))
            def _():
                for i in range(2):
                    block = gathered[i][1].at[0]
                    landed(block, t_recv.at[i, unit], z_next[up])
                    if hop < GROUP - 1:
                        pl.when(z_open[up])(token_copy(i, up, hop).start)

    def token_gone():
        for up in range(2):
            for hop in range(GROUP - 1):
                unit = z_at - hop if up else z_at + hop
                for i in range(2):
                    pl.when((unit >= 0) & (unit < GROUP) & z_open[up])(
                        functools.partial(gone, gathered[i][1].at[0], t_send.at[i, up, hop], z_next[up])
                    )

    def picture_copy(offset):
        _, other = peer_at(offset, n_dp, n_rep)
        return remote(pic_all.at[me], pic_all.at[me], p_send.at[offset - 1], p_recv.at[offset - 1], other)

    def send_pictures():
        values = image_pool_out[...]
        squares = jnp.sum(values * values, axis=-1, keepdims=True)
        pic_all[me] = (values * lax.rsqrt(squares + LAYER_EPS)).astype(jnp.bfloat16)

        def start(offset, carry):
            picture_copy(offset).start()
            return carry

        lax.fori_loop(1, devices, start, 0)

    def end_pictures():
        def end(offset, carry):
            picture_copy(offset).wait()
            return carry

        lax.fori_loop(1, devices, end, 0)

    def begin(s):
        own_ready(s)
        for up in range(2):
            pl.when(z_open[up])(z_copy(s, up, 0).start)
        y_copy(s, z_at).start()

    def arrive(s, hop):
        for up in range(2):
            unit = z_at - hop if up else z_at + hop

            @pl.when((unit >= 0) & (unit < GROUP))
            def _():
                landed(size_of(s, 1, 2), z_recv.at[s, unit], z_next[up])
                if hop < GROUP - 1:
                    pl.when(z_open[up])(z_copy(s, up, hop).start)
                y_copy(s, unit).start()

    def own_start(s):
        own_shard(s).start()

    def stage_y(s):
        landed(size_of(s, GROUP, 2), y_recv.at[s], y_peers[0])
        for unit in range(GROUP):
            pl.when(unit != z_at)(x_copy(s, unit).start)
        x_own_copy(s).start()
        c_copy(s, 0).start()

    def stage_x(s):
        landed(size_of(s, n_dp - 1, 1), x_recv.at[s], x_peer)
        c_copy(s, 1).start()

    def stage_c(s):
        landed(size_of(s, n_dp, 3), c_recv.at[s], c_peer)
        if s >= PARTS:
            store(s).start()

    def carry_on(step):
        moves = []
        if step + OWN_AHEAD < count:
            moves.append(functools.partial(own_start, step + OWN_AHEAD))
        if step + AHEAD < count:
            moves.append(functools.partial(begin, step + AHEAD))
        for hop in range(1, GROUP):
            s = step - (hop - 1) * LAG_Z
            if 0 <= s < count:
                moves.append(functools.partial(arrive, s, hop))
        for lag, stage in ((AT_Y, stage_y), (AT_X, stage_x), (AT_C, stage_c)):
            if 0 <= step - lag < count:
                moves.append(functools.partial(stage, step - lag))
        if step == TOKENS_AT:
            moves.append(token_begin)
        for hop in range(1, GROUP):
            if step == TOKENS_AT + 2 * hop:
                moves.append(functools.partial(token_arrive, hop))
        return moves


    def weight_tile(s, c):
        _, full, k = sections[s]
        return full[k, :, :, :, aligned(c, TILE)].reshape(D, TILE)

    def weight_rows(s, half):
        _, full, k = sections[s]
        return full[k, pl.ds(half * (n_dp // 2), n_dp // 2)].reshape(D // 2, PART)

    def split_loop(total_, pieces, cost, body):
        size = total_ // pieces
        return [
            (cost, functools.partial(loop, size, functools.partial(lambda base, i: body(base + i), p * size)))
            for p in range(pieces)
        ]

    def first_norm(read, vec):
        def body(i):
            rows = aligned(i, ROWS)
            value = norm_rows(read(i).astype(jnp.float32))
            normed[rows, :] = (value * piece_of(vec, 0) + piece_of(vec, 1)).astype(jnp.bfloat16)

        return split_loop(WORDS // ROWS, 4, 0.5, body)

    def project(slot, part, bias):
        def body(c):
            out = dot(normed[...], weight_tile(slot, c))
            if bias is not None:
                out = out + bias[0][:, pl.ds(pl.multiple_of(bias[1] * D + c * TILE, TILE), TILE)]
            qkv[:, pl.ds(pl.multiple_of(part * D + c * TILE, TILE), TILE)] = out.astype(jnp.bfloat16)

        return split_loop(PART // TILE, 3, 0.6, body)

    def attend(slot, read, vec):
        def body(c):
            where = aligned(c, TILE)
            middle[:, where] = dot(mixed[...], weight_tile(slot, c)) + vec[
                :, pl.ds(pl.multiple_of(4 * D + c * TILE, TILE), TILE)
            ]

        def norm(i):
            rows = aligned(i, ROWS)
            value = middle[rows, :] + read(i).astype(jnp.float32)
            middle[rows, :] = value
            normed_two[rows, :] = (norm_rows(value) * piece_of(vec, 5) + piece_of(vec, 6)).astype(jnp.bfloat16)

        return split_loop(PART // TILE, 3, 0.6, body) + split_loop(WORDS // ROWS, 4, 0.6, norm)

    def expand(slot, part, vec, keep):
        def one(c, p):
            start = part * PART + c * TILE
            if p == 0:
                hid[...] = dot(normed_two[...], weight_tile(slot, c)) + vec[:, pl.ds(8 * D + start, TILE)]

            def inner(i):
                rows = aligned(i + p * (WORDS // ROWS // 2), ROWS)
                value = hid[rows, :]
                phi = 0.5 + 0.5 * lax.erf(value * 0.7071067811865476)
                active[rows, pl.ds(start, TILE)] = (value * phi).astype(jnp.bfloat16)
                if keep:
                    slope[rows, pl.ds(start, TILE)] = phi + value * (
                        0.3989422804014327 * jnp.exp(-0.5 * value * value)
                    )

            loop(WORDS // ROWS // 2, inner, unroll=2)

        return [
            (1.2 - 0.4 * p + 0.2 * keep, functools.partial(one, c, p)) for c in range(PART // TILE) for p in range(2)
        ]

    def shrink(slot, part, vec):
        def one(half):
            where = pl.ds(half * (D // 2), D // 2)
            out = dot_nt(active[:, pl.ds(part * PART, PART)], weight_rows(slot, half))
            if part == 0:
                total[:, where] = out + middle[:, where] + vec[:, pl.ds(7 * D + half * (D // 2), D // 2)]
            else:
                total[:, where] += out

        return [(0.8, functools.partial(one, half)) for half in range(2)]

    def attention(chance_, allowed_of):
        pairs_ = GROUP * HEADS // 2
        return [
            (1.2, functools.partial(attention_forward, qkv, mixed, chance_, allowed_of, first, 4))
            for first in range(0, pairs_, 4)
        ]

    def turn(source, slot, out):
        def body(c):
            turned[slot, aligned(c, PAIR), :] = source[:, aligned(c, PAIR)].T

        loop(D // PAIR, body)
        send_out(turned.at[slot, group_rows], out)

    outs = []

    def send_out(src, dst):
        copy = pltpu.make_async_copy(src, dst, out_sem.at[len(outs)])
        copy.start()
        outs.append(copy)

    group_rows = pl.ds(pl.multiple_of(z_at * (D // GROUP), D // GROUP), D // GROUP)

    def text_read(i):
        per = PAIR // ROWS
        return tok[i // per, aligned(lax.rem(i, per), ROWS), :]

    def text_allowed(i):
        row = seg_row[i].astype(jnp.float32)
        return seg_col[i] == row[0:1, :]

    def text_columns():
        for i in range(GROUP):
            row = seg_row[i].astype(jnp.float32)[0:1, :]
            seg_col[i] = jnp.broadcast_to(row, (PAIR, PAIR)).T

    def image_read(i):
        return padded[aligned(i, ROWS), :]

    def picture(axis):
        at = lax.broadcasted_iota(jnp.int32, (PAIR, PAIR), axis)
        number = at // (PAIR // 2)
        return jnp.where(lax.rem(at, PAIR // 2) < patches, number, number + 2)

    def image_allowed(i):
        return picture(0) == picture(1)

    def keep_mark():
        image = lax.broadcasted_iota(jnp.int32, (GROUP * 2, WORDS), 0)
        at = lax.broadcasted_iota(jnp.int32, (GROUP * 2, WORDS), 1)
        inside = (at // (PAIR // 2) == image) & (lax.rem(at, PAIR // 2) < patches)
        return jnp.where(inside, 1.0, 0.0)

    def text_pool():
        send_out(total.at[aligned(z_at, PAIR)], words_out)
        for i in range(GROUP):
            row = seg_row[i].astype(jnp.float32)[0:8, :]
            marks = jnp.where(row == lax.broadcasted_iota(jnp.int32, (8, PAIR), 0).astype(jnp.float32), 1.0, 0.0)
            marks_out[i] = marks
            marks_low = marks.astype(jnp.bfloat16)
            value = total[pl.ds(i * PAIR, PAIR), :]
            high = value.astype(jnp.bfloat16)
            rest = value - high.astype(jnp.float32)
            low = rest.astype(jnp.bfloat16)
            lower = (rest - low.astype(jnp.float32)).astype(jnp.bfloat16)
            sums = dot(
                jnp.concatenate([marks_low] * 3, axis=1), jnp.concatenate([high, low, lower], axis=0)
            )
            text_pool_out[pl.ds(i * 8, 8), :] = sums / jnp.sum(marks, axis=1, keepdims=True)

    def text_part(k):
        slot = k + PARTS
        if k == 0:
            return (
                [(0.3, text_columns)] + first_norm(text_read, tvec_ref) + project(slot, 0, (tvec_ref, 2))
                + [(0.8, lambda: turn(normed, 0, nt_out))]
            )
        if k == 1:
            return project(slot, 1, None)
        if k == 2:
            return (
                project(slot, 2, (tvec_ref, 3)) + [(0.1, lambda: send_out(qkv, qkv_out))]
                + attention(chance, text_allowed)
                + [(0.1, lambda: send_out(chance, chance_out)), (0.8, lambda: turn(mixed, 1, at_out))]
            )
        if k == 3:
            return attend(slot, text_read, tvec_ref) + [
                (0.1, lambda: send_out(middle, mid_out)), (0.8, lambda: turn(normed_two, 2, mt_out))
            ]
        if k < 8:
            return expand(slot, k - 4, tvec_ref, True)
        pieces = shrink(slot, k - 8, tvec_ref)
        if k == 8:
            pieces = [(0.1, lambda: (send_out(active, act_out), send_out(slope, slope_out)))] + pieces
        if k == PARTS - 1:
            pieces = pieces + [(1.0, text_pool)]
        return pieces

    def pool_active(part):
        mark = keep_mark().astype(jnp.bfloat16)
        where = pl.ds(part * PART, PART)
        mean = dot(mark, active[:, where]) * (1.0 / patches)
        high = mean.astype(jnp.bfloat16)
        rest = mean - high.astype(jnp.float32)
        low = rest.astype(jnp.bfloat16)
        apool[0:8, where] = high.astype(jnp.float32)
        apool[8:16, where] = low.astype(jnp.float32)
        apool[16:24, where] = rest - low.astype(jnp.float32)

    def pool_shrink(slot, part):
        for half in range(2):
            where = pl.ds(half * (D // 2), D // 2)
            left = apool[:, pl.ds(part * PART, PART)].astype(jnp.bfloat16)
            out = dot_nt(left, weight_rows(slot, half))
            out = out[0:8] + out[8:16] + out[16:24]
            if part == 0:
                held_ = jnp.concatenate(
                    [
                        jnp.sum(middle[pl.ds(i * (PAIR // 2), patches), where], axis=0, keepdims=True)
                        for i in range(GROUP * 2)
                    ],
                    axis=0,
                )
                image_pool_out[:, where] = (
                    held_ * (1.0 / patches) + ivec_ref[:, pl.ds(7 * D + half * (D // 2), D // 2)] + out
                )
            else:
                image_pool_out[:, where] += out

    def image_part(k):
        slot = k
        if k == 0:
            return first_norm(image_read, ivec_ref) + project(slot, 0, (ivec_ref, 2))
        if k == 1:
            return project(slot, 1, None)
        if k == 2:
            return project(slot, 2, (ivec_ref, 3)) + attention(None, image_allowed)
        if k == 3:
            return attend(slot, image_read, ivec_ref)
        if k < 8:
            return expand(slot, k - 4, ivec_ref, False) + [(0.2, functools.partial(pool_active, k - 4))]
        pieces = [(0.5, functools.partial(pool_shrink, slot, k - 8))]
        if k == PARTS - 1:
            pieces.append((2.0, send_pictures))
        return pieces

    own_start(0)
    for copy in reversed(firsts):
        copy.start()
    for s in range(1, OWN_AHEAD):
        own_start(s)
    firsts[1].wait()
    images = GROUP * 2
    half_row = PAIR // 2
    for quarter_ in range(GROUP):
        row = lax.broadcasted_iota(jnp.int32, (PAIR, patches * images), 0) + quarter_ * PAIR
        source = lax.broadcasted_iota(jnp.int32, (PAIR, patches * images), 1)
        wanted = lax.rem(row, half_row) * images + row // half_row
        move = jnp.where((wanted == source) & (lax.rem(row, half_row) < patches), 1.0, 0.0).astype(jnp.bfloat16)
        padded[pl.ds(quarter_ * PAIR, PAIR), :] = dot(move, patches_in[...]).astype(jnp.bfloat16)
    pl.semaphore_wait(barrier, 5 - jnp.where(z_at == 0, 1, 0) - jnp.where(z_at == GROUP - 1, 1, 0))
    for s in range(AHEAD):
        begin(s)
    moves = [(step, move) for step in range(count + AT_C) for move in carry_on(step)]
    by_step = {}
    for step, move in moves:
        by_step.setdefault(step, []).append(move)
    timed = []
    for step in sorted(by_step):
        for i, move in enumerate(by_step[step]):
            timed.append((STEP_TIME * (step + i / len(by_step[step])), step, move))
    clock, done = 0.0, 0
    for s in range(count):
        pieces = image_part(s) if s < PARTS else text_part(s - PARTS)
        while done < len(timed) and timed[done][1] <= s + AT_C:
            clock = max(clock, timed[done][0])
            timed[done][2]()
            done += 1
        for cost, piece in pieces:
            piece()
            clock += cost
            while done < len(timed) and timed[done][0] <= clock:
                timed[done][2]()
                done += 1
    while done < len(timed):
        timed[done][2]()
        done += 1
    for copy in outs:
        copy.wait()
    for s in range(PARTS, count):
        store(s).wait()
    token_gone()
    end_pictures()
    for group in range(2):
        for up in range(2):
            for hop in range(GROUP - 1):
                unit = z_at - hop if up else z_at + hop
                pl.when((unit >= 0) & (unit < GROUP) & z_open[up])(
                    functools.partial(gone, all_size(group, 1, 2), z_send.at[group, up, hop], z_next[up])
                )
        gone(all_size(group, GROUP, 2), y_send.at[group], y_peers[0])
        gone(all_size(group, n_dp - 1, 1), x_send.at[group], x_peer)
        gone(all_size(group, n_dp, 3), c_send.at[group], c_peer)


def gather_and_forward(n_dp, n_rep, text_low, image_low, tokens, segments, pictures, text_vectors, image_vectors):
    own, columns = text_low.shape
    images, patches = pictures.shape[0], pictures.shape[1]
    lane_rows = own // LANES
    count = 2 * PARTS
    hbm, vmem = pl.BlockSpec(memory_space=pltpu.HBM), pl.BlockSpec(memory_space=pltpu.VMEM)
    low, full = jnp.bfloat16, jnp.float32
    shape = jax.ShapeDtypeStruct
    gathered = shape((PARTS, n_dp, LANES, lane_rows, PART), low)
    turned = shape((D // GROUP, WORDS), low)
    pairs = GROUP * HEADS // 2
    dma = pltpu.SemaphoreType.DMA
    outs = pl.pallas_call(
        functools.partial(forward_kernel, n_dp, n_rep, patches),
        out_shape=(
            gathered, shape((n_dp * n_rep, images, D), low), shape((PAIR, D), full), shape((8 * GROUP, D), full),
            shape((GROUP, 8, PAIR), full), shape((WORDS, 3 * D), low), shape((pairs, 2 * PAIR, PAIR), full),
            shape((WORDS, D), full), shape((WORDS, FF), full), shape((WORDS, FF), low), turned, turned, turned,
        ),
        in_specs=[hbm] * 4 + [vmem] * 3,
        out_specs=(hbm, vmem, hbm, vmem, vmem) + (hbm,) * 8,
        scratch_shapes=[
            pltpu.VMEM((PARTS, n_dp, LANES, lane_rows, PART), low),
            pltpu.VMEM((PARTS, n_dp, LANES, lane_rows, PART), low),
            pltpu.VMEM((GROUP, PAIR, D), low),
            pltpu.VMEM((GROUP, PAIR, PAIR), full),
            pltpu.VMEM((GROUP, 16, PAIR), low),
            pltpu.VMEM((WORDS, D), low),
            pltpu.VMEM((WORDS, 3 * D), low),
            pltpu.VMEM((WORDS, D), low),
            pltpu.VMEM((WORDS, D), full),
            pltpu.VMEM((WORDS, D), low),
            pltpu.VMEM((WORDS, FF), low),
            pltpu.VMEM((WORDS, FF), full),
            pltpu.VMEM((pairs, 2 * PAIR, PAIR), full),
            pltpu.VMEM((WORDS, D), full),
            pltpu.VMEM((WORDS, TILE), full),
            pltpu.VMEM((3, D, WORDS), low),
            pltpu.VMEM((24, FF), full),
            pltpu.VMEM((images, D), full),
            pltpu.VMEM((patches * images, D), low),
            pltpu.VMEM((WORDS, D), low),
            pltpu.VMEM((4, 3, lane_rows, PART), full),
            dma((2, 2, GROUP - 1)), dma((count, GROUP)), dma((2,)), dma((count,)),
            dma((2,)), dma((count,)), dma((2,)), dma((count,)),
            dma((2, 2, GROUP - 1)), dma((2, GROUP)), dma((2,)), dma((count,)), dma((PARTS,)), dma((12,)),
            dma((n_dp * n_rep - 1,)), dma((n_dp * n_rep - 1,)),
        ],
        compiler_params=pltpu.CompilerParams(collective_id=5, has_side_effects=True, vmem_limit_bytes=60 << 20),
        name="gather_and_forward",
    )(
        text_low.reshape(LANES, lane_rows, columns), image_low.reshape(LANES, lane_rows, columns), tokens,
        jnp.swapaxes(pictures, 0, 1).reshape(patches * images, D), segments,
        text_vectors.reshape(1, -1), image_vectors.reshape(1, -1),
    )
    return (outs[0].reshape(PARTS, D, PART),) + tuple(outs[1:])


def backward_kernel(
    n_dp, n_rep,
    wt_ref, nt_ref, at_ref, mt_ref, qkv_ref, chance_ref, mid_ref, slope_ref, act_ref, feed_ref,
    tpool_ref, pic_all, marks_ref, tok_ref, vec_ref, start_ref, flat_ref, moving_ref,
    m_out, input_out, loss_out, left_out, right_out, nvec_out, nvmom_out,
    weight, turned, qkv, chance, middle, slope, active, grad_hidden, grad_mix, low, low_mixed, wide, block, sent, got, sums, dy_ref, e2t, cap_all, rows_out, vector_out,
    factor, factor_rep, factor_dp, basis, tiles, tiles_rep, quarter, tiles_dp, everything,
    load_sem, send, recv, c_send, c_recv, m_sem, g_send, g_recv,
):
    n_inner = n_dp // GROUP
    d_at, r_at = lax.axis_index("dp"), lax.axis_index("rep")
    z_at, y_at = d_at // n_inner, lax.rem(d_at, n_inner)
    peer = (z_at * n_inner + 1 - y_at, r_at)
    own = D // n_dp
    share = 1.0 / GROUP

    barrier = pltpu.get_barrier_semaphore()
    devices = n_dp * n_rep
    near = n_inner * n_rep

    def near_peer(k):
        other = lax.rem(y_at * n_rep + r_at + k, near)
        return z_at * n_inner + other // n_rep, lax.rem(other, n_rep)

    rep_peers = [(d_at, lax.rem(r_at + k, n_rep)) for k in range(1, n_rep)]
    dp_peers = [(lax.rem(d_at + k, n_dp), r_at) for k in range(1, n_dp)]
    far_peers = [
        (lax.rem(z_at + k, GROUP) * n_inner + y, r_at) for k in range(1, GROUP) for y in range(n_inner)
    ]
    met = near - 1 + len(far_peers)
    for other in [near_peer(k) for k in range(1, near)] + far_peers:
        pl.semaphore_signal(barrier, inc=1, device_id=other, device_id_type=MESH)
    loads = {}

    def fetch(name, src, dst):
        copy = pltpu.make_async_copy(src, dst, load_sem.at[len(loads)])
        copy.start()
        loads[name] = copy

    def need(*names):
        for name in names:
            loads[name].wait()

    fetch("act", act_ref, active)
    fetch("feed", feed_ref, rows_out)
    for part in range(4):
        fetch(("w", 8 + part), wt_ref.at[8 + part], weight.at[8 + part])
    fetch("slope", slope_ref, slope)
    fetch("mt", mt_ref, turned.at[0])
    for part in range(4):
        fetch(("w", 4 + part), wt_ref.at[4 + part], weight.at[4 + part])
    fetch("mid", mid_ref, middle)
    fetch("at", at_ref, turned.at[1])
    fetch(("w", 3), wt_ref.at[3], weight.at[3])
    fetch("qkv", qkv_ref, qkv)
    fetch("chance", chance_ref, chance)
    fetch("nt", nt_ref, turned.at[2])
    for part in range(3):
        fetch(("w", part), wt_ref.at[part], weight.at[part])

    def exchange(s):
        return pltpu.make_async_remote_copy(
            src_ref=sent.at[s], dst_ref=got.at[s], send_sem=send.at[s], recv_sem=recv.at[s],
            device_id=peer, device_id_type=MESH,
        )

    own_rows = pl.ds(pl.multiple_of(y_at * own, own), own)
    other_rows = pl.ds(pl.multiple_of((1 - y_at) * own, own), own)

    def exchange_tile(s, where, slot):
        return pltpu.make_async_remote_copy(
            src_ref=sent.at[s, :, where], dst_ref=got.at[s, :, where], send_sem=send.at[slot], recv_sem=recv.at[slot],
            device_id=peer, device_id_type=MESH,
        )

    def exchange_heads(j):
        where = (pl.ds(0, 3), slice(None), pl.ds(j * PAIR, PAIR))
        return pltpu.make_async_remote_copy(
            src_ref=sent.at[where], dst_ref=got.at[where], send_sem=send.at[PARTS + j], recv_sem=recv.at[PARTS + j],
            device_id=peer, device_id_type=MESH,
        )

    def outer(s, left, right_of):
        def body(c):
            block[:, pl.ds(0, TILE)] = dot(left, right_of(c))
            where = pl.ds(pl.multiple_of(s * PART + c * TILE, TILE), TILE)
            rows_out[:, where] = rows_out[:, where] + block[own_rows, pl.ds(0, TILE)]
            sent[s, :, aligned(c, TILE)] = block[other_rows, pl.ds(0, TILE)].astype(jnp.bfloat16)
            exchange_tile(s, aligned(c, TILE), s).start()

        loop(PART // TILE, body, unroll=3)

    ones = jnp.ones((16, WORDS), jnp.bfloat16)

    def put(slot, values):
        for i in range(values.shape[1] // PAIR):
            vector_out[pl.ds(slot // PAIR + i, 1), :] = values[:, i * PAIR : (i + 1) * PAIR]

    def column_sums(values, slot, scale):
        put(slot, dot(ones, values)[0:1, :] * scale)


    def caption_copy(k):
        block_ = cap_all.at[:, y_at * n_rep + r_at]
        return pltpu.make_async_remote_copy(
            src_ref=block_, dst_ref=block_, send_sem=c_send.at[k - 1], recv_sem=c_recv.at[k - 1],
            device_id=near_peer(k), device_id_type=MESH,
        )

    def unit_of(values):
        return values * lax.rsqrt(jnp.sum(values * values, axis=-1, keepdims=True) + LAYER_EPS)

    def contrast():
        group_pairs = GROUP * 8
        for i in range(GROUP):
            cap_all[i, y_at * n_rep + r_at] = unit_of(tpool_ref[pl.ds(i * 8, 8), :]).astype(jnp.bfloat16)
        pl.semaphore_wait(barrier, met)
        for k in range(1, near):
            caption_copy(k).start()
        for k in range(1, near):
            caption_copy(k).wait_recv()
        pairs_ = devices * 8
        pics = pic_all[...].reshape(pairs_, D)
        caps = cap_all[...].reshape(pairs_, D)
        logits = dot_nt(caps, pics) * LOGIT_SCALE
        top = jnp.max(logits, axis=0, keepdims=True)
        image_log = top + jnp.log(jnp.sum(jnp.exp(logits - top), axis=0, keepdims=True))
        top = jnp.max(logits, axis=1, keepdims=True)
        caption_log = top + jnp.log(jnp.sum(jnp.exp(logits - top), axis=1, keepdims=True))
        row = lax.broadcasted_iota(jnp.int32, (pairs_, pairs_), 0)
        column = lax.broadcasted_iota(jnp.int32, (pairs_, pairs_), 1)
        matched = jnp.sum(jnp.where(row == column, logits, 0.0), axis=1, keepdims=True)
        loss = (jnp.sum(image_log) + jnp.sum(caption_log) - 2.0 * jnp.sum(matched)) / (2.0 * pairs_)
        loss_out[0, 0] = loss
        pooled = tpool_ref[...]
        squares = lax.rsqrt(jnp.sum(pooled * pooled, axis=-1, keepdims=True) + LAYER_EPS)
        own_low = (pooled * squares).astype(jnp.bfloat16)
        own_logits = dot_nt(own_low, pics) * LOGIT_SCALE
        top = jnp.max(own_logits, axis=1, keepdims=True)
        own_log = top + jnp.log(jnp.sum(jnp.exp(own_logits - top), axis=1, keepdims=True))
        local = lax.broadcasted_iota(jnp.int32, (group_pairs, pairs_), 0)
        column = lax.broadcasted_iota(jnp.int32, (group_pairs, pairs_), 1)
        wanted = (local // 8) * (near * 8) + (y_at * n_rep + r_at) * 8 + lax.rem(local, 8)
        pick = jnp.where(wanted == column, 1.0, 0.0)
        soft = ((jnp.exp(own_logits - own_log) - pick) * 0.5).astype(jnp.bfloat16)
        across = ((jnp.exp(own_logits - image_log) - pick) * 0.5).astype(jnp.bfloat16)
        grad = LOGIT_SCALE * (dot(soft, pics) + dot(across, pics))
        grad = squares * (
            grad - pooled * (squares * squares) * jnp.sum(grad * pooled, axis=-1, keepdims=True)
        )
        for i in range(GROUP):
            marks = marks_ref[i]
            part = grad[i * 8 : (i + 1) * 8, :] / jnp.sum(marks, axis=1, keepdims=True)
            high, rest = split_two(part)
            rest_low = (part - high.astype(jnp.float32) - rest.astype(jnp.float32)).astype(jnp.bfloat16)
            stacked = jnp.concatenate([high, rest, rest_low], axis=0)
            marks_low = marks.astype(jnp.bfloat16)
            marks_low = jnp.concatenate([marks_low, marks_low, marks_low], axis=0)
            rows = pl.ds(i * PAIR, PAIR)
            words = dot_tn(marks_low, stacked)
            dy_ref[rows, :] = words
            low[rows, :] = words.astype(jnp.bfloat16)
            e2t[:, rows] = dot_tn(stacked, marks_low).astype(jnp.bfloat16)

    contrast()
    need("act", "feed")
    for part in range(4):
        outer(8 + part, e2t[pl.ds(pl.multiple_of(z_at * (D // GROUP), D // GROUP), D // GROUP), :], lambda c: active[:, pl.ds(pl.multiple_of(part * PART + c * TILE, TILE), TILE)])
    need("slope")
    column_sums(low[...], 7 * D, share)
    for part in range(4):
        need(("w", 8 + part))

        def hidden_body(c):
            where = pl.ds(pl.multiple_of(part * PART + c * TILE, TILE), TILE)
            out = dot(low[...], weight[8 + part, :, aligned(c, TILE)])
            grad_hidden[:, where] = (out * slope[:, where]).astype(jnp.bfloat16)

        loop(PART // TILE, hidden_body, unroll=3)
    need("mt")
    for part in range(4):
        outer(
            4 + part, turned[0], lambda c: grad_hidden[:, pl.ds(pl.multiple_of(part * PART + c * TILE, TILE), TILE)]
        )
    for part in range(4):
        need(("w", 4 + part))
    for half in range(2):
        rows = pl.ds(half * (D // 2), D // 2)
        out = dot_nt(grad_hidden[:, pl.ds(0, PART)], weight[4, rows, :])
        for part in range(1, 4):
            out = out + dot_nt(grad_hidden[:, pl.ds(part * PART, PART)], weight[4 + part, rows, :])
        wide[:, rows] = out
    need("mid")

    def norm_back(value, grad, gain):
        center = value - jnp.mean(value, axis=-1, keepdims=True)
        scale = lax.rsqrt(jnp.mean(center * center, axis=-1, keepdims=True) + LAYER_EPS)
        unit = center * scale
        inner = grad * gain
        out = scale * (
            inner - jnp.mean(inner, axis=-1, keepdims=True) - unit * jnp.mean(inner * unit, axis=-1, keepdims=True)
        )
        return out, grad * unit

    def fold(values):
        return jnp.sum(values.reshape(ROWS // 8, 8, D), axis=0)

    sums[...] = jnp.zeros_like(sums)

    def second(i):
        rows = aligned(i, ROWS)
        grad = wide[rows, :]
        out, product = norm_back(middle[rows, :], grad, piece_of(vec_ref, 5))
        sums[0] += fold(product)
        sums[1] += fold(grad)
        out = out + dy_ref[rows, :]
        middle[rows, :] = out
        low[rows, :] = out.astype(jnp.bfloat16)

    loop(WORDS // ROWS, second, unroll=2)
    put(5 * D, jnp.sum(sums[0], axis=0, keepdims=True) * share)
    put(6 * D, jnp.sum(sums[1], axis=0, keepdims=True) * share)
    need("at", ("w", 3))
    outer(3, turned[1], lambda c: low[:, aligned(c, TILE)])
    for half in range(2):
        rows = pl.ds(half * (D // 2), D // 2)
        low_mixed[:, rows] = dot_nt(low[...], weight[3, rows, :]).astype(jnp.bfloat16)
    need("qkv", "chance")
    pairs = HEADS // 2

    def attention(j, i):
        at = i * pairs + j
        rows = pl.ds(i * PAIR, PAIR)
        q_cols = pl.ds(j * PAIR, PAIR)
        k_cols = pl.ds(D + j * PAIR, PAIR)
        v_cols = pl.ds(2 * D + j * PAIR, PAIR)
        query, key, value = qkv[rows, q_cols], qkv[rows, k_cols], qkv[rows, v_cols]
        grad = two_heads(low_mixed[rows, q_cols])
        weight_ = chance[at]
        grad_mix[rows, v_cols] = dot_tn(weight_.astype(jnp.bfloat16), grad).astype(jnp.bfloat16)
        back = dot_nt(grad, value)
        back = weight_ * (back - jnp.sum(weight_ * back, axis=-1, keepdims=True))
        back = back.astype(jnp.bfloat16)
        side = jnp.concatenate([back[:PAIR], back[PAIR:]], axis=1)
        grad_mix[rows, q_cols] = (dot(side, two_heads(key)) * SCORE_SCALE).astype(jnp.bfloat16)
        grad_mix[rows, k_cols] = (dot_tn(back, two_heads(query)) * SCORE_SCALE).astype(jnp.bfloat16)

    need("nt")
    for j in range(pairs):
        for i in range(GROUP):
            attention(j, i)
        for part in range(3):
            value = dot(turned[2], grad_mix[:, pl.ds(part * D + j * PAIR, PAIR)])
            block[:, pl.ds(part * PAIR, PAIR)] = value
            where = pl.ds(part * D + j * PAIR, PAIR)
            rows_out[:, where] = rows_out[:, where] + block[own_rows, pl.ds(part * PAIR, PAIR)]
            sent[part, :, pl.ds(j * PAIR, PAIR)] = block[other_rows, pl.ds(part * PAIR, PAIR)].astype(jnp.bfloat16)
            exchange_tile(part, pl.ds(j * PAIR, PAIR), PARTS + j).start()
    column_sums(low[...], 4 * D, share)
    column_sums(grad_hidden[...], 8 * D, share)
    column_sums(grad_mix[:, pl.ds(0, D)], 2 * D, share)
    column_sums(grad_mix[:, pl.ds(2 * D, D)], 3 * D, share)
    for part in range(3):
        need(("w", part))
    mine = aligned(z_at, PAIR)
    for half in range(2):
        rows = pl.ds(half * (D // 2), D // 2)
        out = dot_nt(grad_mix[mine, pl.ds(0, PART)], weight[0, rows, :])
        for part in range(1, 3):
            out = out + dot_nt(grad_mix[mine, pl.ds(part * PART, PART)], weight[part, rows, :])
        wide[pl.ds(0, PAIR), rows] = out
    sums[...] = jnp.zeros_like(sums)

    def first(i):
        rows = aligned(i, ROWS)
        grad = wide[rows, :]
        out, product = norm_back(tok_ref[rows, :].astype(jnp.float32), grad, piece_of(vec_ref, 0))
        sums[0] += fold(product)
        sums[1] += fold(grad)
        input_out[rows, :] = out + middle[pl.ds(pl.multiple_of(z_at * PAIR + i * ROWS, ROWS), ROWS), :]

    loop(PAIR // ROWS, first)
    put(0, jnp.sum(sums[0], axis=0, keepdims=True))
    put(D, jnp.sum(sums[1], axis=0, keepdims=True))

    bounds = matrix_bounds()
    rank = start_ref.shape[0]
    strip = n_dp * OWN_TILES
    sums_of = {}

    def take(s):
        where = pl.ds(s * PART, PART)
        rows_out[:, where] = rows_out[:, where] + got[s].astype(jnp.float32)
        high, rest = split_two(rows_out[:, where])
        start_high, start_low = split_two(start_ref[:, where])
        both = jnp.concatenate([start_high, start_low], axis=0)
        matrix = 0 if s < 3 else 1 if s == 3 else 2 if s < 8 else 3
        out, out_rest = dot_nt(both, high), dot_nt(both, rest)
        out = out[:rank] + out[rank:] + out_rest[:rank]
        sums_of[matrix] = out if matrix not in sums_of else sums_of[matrix] + out

    for s in (8, 9, 10, 11, 4, 5, 6, 7, 3):
        exchange(s).wait_recv()
        take(s)
    for j in range(pairs):
        exchange_heads(j).wait_recv()
    for s in range(3):
        take(s)
    m_copy = pltpu.make_async_copy(rows_out, m_out, m_sem)
    m_copy.start()
    factor[...] = jnp.zeros_like(factor)
    for matrix in range(4):
        factor[pl.ds(matrix * rank, rank), pl.ds(0, own)] = sums_of[matrix]

    def remote(phase, k, src, dst, other):
        return pltpu.make_async_remote_copy(
            src_ref=src, dst_ref=dst, send_sem=g_send.at[phase, k], recv_sem=g_recv.at[phase, k],
            device_id=other, device_id_type=MESH,
        )

    mine = pl.ds(r_at * strip + d_at * OWN_TILES, OWN_TILES)
    strip_mine = pl.ds(r_at * strip, strip)
    phases = [
        [remote(0, k, factor, factor_rep.at[k], other) for k, other in enumerate(rep_peers)],
        [remote(1, k, factor_dp.at[d_at], factor_dp.at[d_at], other) for k, other in enumerate(dp_peers)],
        [
            remote(2, k, tiles.at[pl.ds(other[1] * strip, strip)], tiles_rep.at[k], other)
            for k, other in enumerate(rep_peers)
        ],
        [
            remote(3, k, quarter.at[pl.ds(other[0] * OWN_TILES, OWN_TILES)], tiles_dp.at[k], other)
            for k, other in enumerate(dp_peers)
        ],
        [remote(4, k, everything.at[mine], everything.at[mine], other) for k, other in enumerate(dp_peers)],
        [remote(5, k, everything.at[strip_mine], everything.at[strip_mine], other) for k, other in enumerate(rep_peers)],
    ]

    def begin(phase):
        for copy in phases[phase]:
            copy.start()

    def arrived(phase):
        for copy in phases[phase]:
            copy.wait_recv()

    begin(0)
    arrived(0)
    summed = factor[...]
    for k in range(n_rep - 1):
        summed = summed + factor_rep[k]
    factor_dp[d_at] = summed
    begin(1)
    arrived(1)
    vectors = jnp.concatenate([factor_dp[i] for i in range(n_dp)], axis=1).reshape(4, rank, n_dp * PAIR)
    place = lax.broadcasted_iota(jnp.int32, (4, rank, 1), 1)
    for k in range(rank):
        vector = vectors[:, k : k + 1, :]
        size = jnp.sqrt(jnp.sum(vector * vector, axis=-1, keepdims=True)) + NORM_FLOOR
        vector = vector / size
        along = jnp.sum(vector * vectors, axis=-1, keepdims=True)
        vectors = jnp.where(
            place == k, jnp.broadcast_to(vector, vectors.shape),
            vectors - jnp.where(place > k, along, 0.0) * vector,
        )
    vectors = vectors.reshape(4 * rank, n_dp * PAIR)
    basis[...] = vectors
    left_out[...] = vectors
    basis_high, basis_low = split_two(basis[:, aligned(d_at, PAIR)][:, :own])
    for matrix, (first_col, after_col) in enumerate(bounds):
        where = slice(matrix * rank, (matrix + 1) * rank)
        both = jnp.concatenate([basis_high[where], basis_low[where]], axis=0)

        def project(c):
            high, low = split_two(rows_out[:, pl.ds(pl.multiple_of(first_col + c * TILE, TILE), TILE)])
            out = dot(both, high)
            out = out[:rank] + out[rank:] + dot(both, low)[:rank]
            at = first_col // PAIR + c * (TILE // PAIR)
            for half in range(TILE // PAIR):
                tiles[at + half] = out[:, half * PAIR : (half + 1) * PAIR]

        loop((after_col - first_col) // TILE, project, unroll=3)
    columns = bounds[-1][1] // PAIR
    for i in range(EXTRA):
        tiles[columns + i] = vector_out[pl.ds(i * 8, 8), :]
    for i in range(columns + EXTRA, n_rep * strip):
        tiles[i] = jnp.zeros((8, PAIR), jnp.float32)
    begin(2)
    arrived(2)
    value = tiles[strip_mine]
    for k in range(n_rep - 1):
        value = value + tiles_rep[k]
    quarter[...] = value
    begin(3)
    arrived(3)
    value = quarter[pl.ds(d_at * OWN_TILES, OWN_TILES)]
    for k in range(n_dp - 1):
        value = value + tiles_dp[k]
    everything[mine] = value
    begin(4)
    arrived(4)
    begin(5)
    arrived(5)
    for i in range(columns):
        right_out[:, pl.ds(i * PAIR, PAIR)] = everything[i]
    for i in range(EXTRA):
        at = pl.ds(i * 8, 8)
        moved = MOMENTUM_DECAY * moving_ref[at, :] + everything[columns + i]
        nvmom_out[at, :] = moved
        nvec_out[at, :] = flat_ref[at, :] - STEP_RATE * moved
    m_copy.wait()
    for s in range(3, PARTS):
        exchange(s).wait_send()
    for j in range(pairs):
        exchange_heads(j).wait_send()
    for k in range(1, near):
        caption_copy(k).wait_send()
    for phase in phases:
        for copy in phase:
            copy.wait_send()


def backward(n_dp, n_rep, kept, pooled, pictures, marks, tokens, text_vectors, feedback_rows, start, moving):
    weights, qkv, chance, middle, slope, active, n_turned, a_turned, m_turned = kept
    own = feedback_rows.shape[0]
    hbm, vmem = pl.BlockSpec(memory_space=pltpu.HBM), pl.BlockSpec(memory_space=pltpu.VMEM)
    low, full = jnp.bfloat16, jnp.float32
    shape = jax.ShapeDtypeStruct
    dma = pltpu.SemaphoreType.DMA
    pairs = GROUP * HEADS // 2
    rank = start.shape[0]
    strip = n_dp * OWN_TILES
    flat = (12 * D // PAIR, PAIR)
    return pl.pallas_call(
        functools.partial(backward_kernel, n_dp, n_rep),
        out_shape=(
            shape(feedback_rows.shape, full), shape((PAIR, D), full), shape((1, 1), full),
            shape((4 * rank, n_dp * PAIR), full), shape(start.shape, full), shape(flat, full), shape(flat, full),
        ),
        in_specs=[hbm] * 10 + [vmem] * 8,
        out_specs=(hbm, vmem, pl.BlockSpec(memory_space=pltpu.SMEM)) + (vmem,) * 4,
        scratch_shapes=[
            pltpu.VMEM((PARTS, D, PART), low),
            pltpu.VMEM((3, D // GROUP, WORDS), low),
            pltpu.VMEM((WORDS, 3 * D), low),
            pltpu.VMEM((pairs, 2 * PAIR, PAIR), full),
            pltpu.VMEM((WORDS, D), full),
            pltpu.VMEM((WORDS, FF), full),
            pltpu.VMEM((WORDS, FF), low),
            pltpu.VMEM((WORDS, FF), low),
            pltpu.VMEM((WORDS, 3 * D), low),
            pltpu.VMEM((WORDS, D), low),
            pltpu.VMEM((WORDS, D), low),
            pltpu.VMEM((WORDS, D), full),
            pltpu.VMEM((D // GROUP, 3 * PAIR), full),
            pltpu.VMEM((PARTS, own, PART), low),
            pltpu.VMEM((PARTS, own, PART), low),
            pltpu.VMEM((2, 8, D), full),
            pltpu.VMEM((WORDS, D), full),
            pltpu.VMEM((D, WORDS), low),
            pltpu.VMEM((GROUP, n_dp * n_rep // GROUP, 8, D), low),
            pltpu.VMEM(feedback_rows.shape, full),
            pltpu.VMEM(flat, full),
            pltpu.VMEM((4 * rank, PAIR), full),
            pltpu.VMEM((n_rep - 1, 4 * rank, PAIR), full),
            pltpu.VMEM((n_dp, 4 * rank, PAIR), full),
            pltpu.VMEM((4 * rank, n_dp * PAIR), full),
            pltpu.VMEM((n_rep * strip, 8, PAIR), full),
            pltpu.VMEM((n_rep - 1, strip, 8, PAIR), full),
            pltpu.VMEM((strip, 8, PAIR), full),
            pltpu.VMEM((n_dp - 1, OWN_TILES, 8, PAIR), full),
            pltpu.VMEM((n_rep * strip, 8, PAIR), full),
            dma((24,)), dma((PARTS + 6,)), dma((PARTS + 6,)), dma((8,)), dma((8,)), dma,
            dma((6, n_dp - 1)), dma((6, n_dp - 1)),
        ],
        compiler_params=pltpu.CompilerParams(collective_id=6, has_side_effects=True, vmem_limit_bytes=60 << 20),
        name="backward",
    )(
        weights, n_turned, a_turned, m_turned, qkv, chance, middle, slope, active, feedback_rows,
        pooled, pictures, marks, tokens, text_vectors.reshape(1, -1), start, text_vectors.reshape(flat),
        moving.reshape(flat),
    )


EXTRA = 9
OWN_TILES = 3


def split_two(values):
    high = values.astype(jnp.bfloat16)
    return high, (values - high.astype(jnp.float32)).astype(jnp.bfloat16)


CHUNKS = 4


def finish_kernel(
    n_dp, n_rep,
    rows_ref, mom_ref, wts_ref, words_ref, input_ref, left_ref, right_ref, vec_ref, vmom_ref, loss_ref,
    feed_out, mom_out, wts_out, words_out, input_out, left_out, right_out, vec_out, vmom_out, loss_out,
    rows, mom, wts, change, through, load_sem, store_sem, pass_sem,
):
    own = rows.shape[0]
    piece = own // CHUNKS
    rank = right_ref.shape[0]

    def load(i, j):
        src, dst = ((rows_ref, rows), (mom_ref, mom), (wts_ref, wts))[j]
        span = pl.ds(i * piece, piece)
        return pltpu.make_async_copy(src.at[span], dst.at[span], load_sem.at[i, j])

    def store(i, j):
        src, dst = ((rows, feed_out), (mom, mom_out), (wts, wts_out))[j]
        span = pl.ds(i * piece, piece)
        return pltpu.make_async_copy(src.at[span], dst.at[span], store_sem.at[i, j])

    for i in range(CHUNKS):
        for j in range(3):
            load(i, j).start()
    taken = [
        pltpu.make_async_copy(src, through.at[i], pass_sem.at[i]) for i, src in enumerate((words_ref, input_ref))
    ]
    passed = [
        pltpu.make_async_copy(through.at[i], dst, pass_sem.at[2 + i]) for i, dst in enumerate((words_out, input_out))
    ]
    passed.append(pltpu.make_async_copy(right_ref, right_out, pass_sem.at[4]))
    for copy in taken:
        copy.start()
    passed[2].start()
    vec_out[...] = vec_ref[...]
    vmom_out[...] = vmom_ref[...]
    loss_out[0, 0] = loss_ref[0, 0]
    left_out[...] = jnp.concatenate([left_ref[:, i * PAIR : i * PAIR + own] for i in range(n_dp)], axis=1)
    basis_high, basis_low = split_two(left_ref[:, aligned(lax.axis_index("dp"), PAIR)][:, :own])
    for matrix, (first_col, after_col) in enumerate(matrix_bounds()):
        where = slice(matrix * rank, (matrix + 1) * rank)
        left = jnp.concatenate([basis_high[where], basis_high[where], basis_low[where]], axis=0)

        def approximate(c):
            cols = pl.ds(pl.multiple_of(first_col + c * PART, PART), PART)
            high, low = split_two(right_ref[:, cols])
            change[:, cols] = dot_tn(left, jnp.concatenate([high, low, high], axis=0))

        loop((after_col - first_col) // PART, approximate)
    for i in range(CHUNKS):
        for j in range(3):
            load(i, j).wait()

        def update(c):
            span, cols = pl.ds(i * piece, piece), aligned(c, PART)
            delta = change[span, cols]
            rows[span, cols] = rows[span, cols] - delta * (1.0 / n_rep)
            moved = MOMENTUM_DECAY * mom[span, cols] + delta
            mom[span, cols] = moved
            wts[span, cols] = wts[span, cols] - STEP_RATE * moved

        loop(rows.shape[1] // PART, update)
        for j in range(3):
            store(i, j).start()
        if i == 0:
            for k, copy in enumerate(taken):
                copy.wait()
                passed[k].start()
    for copy in passed:
        copy.wait()
    for i in range(CHUNKS):
        for j in range(3):
            store(i, j).wait()


def finish(n_dp, n_rep, rows, momentum, weights, left, right, words, grad_inputs, vectors, vector_momentum, loss):
    own, columns = rows.shape
    hbm, vmem = pl.BlockSpec(memory_space=pltpu.HBM), pl.BlockSpec(memory_space=pltpu.VMEM)
    smem = pl.BlockSpec(memory_space=pltpu.SMEM)
    full = jnp.float32
    shape = jax.ShapeDtypeStruct
    dma = pltpu.SemaphoreType.DMA
    big = shape(rows.shape, full)
    return pl.pallas_call(
        functools.partial(finish_kernel, n_dp, n_rep),
        out_shape=(
            big, big, big, shape(words.shape, full), shape(grad_inputs.shape, full),
            shape((left.shape[0], n_dp * own), full), shape(right.shape, full), shape(vectors.shape, full),
            shape(vectors.shape, full), shape((1, 1), full),
        ),
        in_specs=[hbm] * 5 + [vmem] * 4 + [smem],
        out_specs=(hbm,) * 5 + (vmem, hbm, vmem, vmem, smem),
        scratch_shapes=[pltpu.VMEM(rows.shape, full)] * 4
        + [pltpu.VMEM((2,) + words.shape, full), dma((CHUNKS, 3)), dma((CHUNKS, 3)), dma((5,))],
        compiler_params=pltpu.CompilerParams(vmem_limit_bytes=60 << 20),
        name="finish",
    )(rows, momentum, weights, words, grad_inputs, left, right, vectors, vector_momentum, loss)


def peer_at(offset, n_dp, n_rep):
    me = lax.axis_index("dp") * n_rep + lax.axis_index("rep")
    other = lax.rem(me + offset, n_dp * n_rep)
    return other, (other // n_rep, lax.rem(other, n_rep))


def meet(n_dp, n_rep):
    total = n_dp * n_rep
    barrier = pltpu.get_barrier_semaphore()

    def hello(offset, carry):
        _, peer = peer_at(offset, n_dp, n_rep)
        pl.semaphore_signal(barrier, inc=1, device_id=peer, device_id_type=MESH)
        return carry

    lax.fori_loop(1, total, hello, 0)
    pl.semaphore_wait(barrier, total - 1)


def spread_kernel(n_dp, n_rep, mine_ref, all_ref, send, recv, own_sem):
    total = n_dp * n_rep
    me = lax.axis_index("dp") * n_rep + lax.axis_index("rep")
    own = pltpu.make_async_copy(mine_ref, all_ref.at[me], own_sem)
    own.start()
    meet(n_dp, n_rep)

    def copy(offset):
        _, peer = peer_at(offset, n_dp, n_rep)
        return pltpu.make_async_remote_copy(
            src_ref=mine_ref, dst_ref=all_ref.at[me], send_sem=send.at[offset - 1],
            recv_sem=recv.at[offset - 1], device_id=peer, device_id_type=MESH,
        )

    def begin(offset, carry):
        copy(offset).start()
        return carry

    def finish(offset, carry):
        copy(offset).wait()
        return carry

    lax.fori_loop(1, total, begin, 0)
    own.wait()
    lax.fori_loop(1, total, finish, 0)


def spread(mine, n_dp, n_rep, collective, name):
    total = n_dp * n_rep
    vmem = pl.BlockSpec(memory_space=pltpu.VMEM)
    dma = pltpu.SemaphoreType.DMA
    return pl.pallas_call(
        functools.partial(spread_kernel, n_dp, n_rep),
        out_shape=jax.ShapeDtypeStruct((total,) + mine.shape, mine.dtype),
        in_specs=[vmem],
        out_specs=vmem,
        scratch_shapes=[dma((total - 1,)), dma((total - 1,)), dma],
        compiler_params=pltpu.CompilerParams(
            collective_id=collective, has_side_effects=True, vmem_limit_bytes=48 << 20
        ),
        name=name,
    )(mine)


def total_kernel(n_dp, n_rep, mine_ref, out_ref, parts, sums, send, recv, send_two, recv_two):
    total = n_dp * n_rep
    me = lax.axis_index("dp") * n_rep + lax.axis_index("rep")
    meet(n_dp, n_rep)

    def scatter(offset):
        other, peer = peer_at(offset, n_dp, n_rep)
        return pltpu.make_async_remote_copy(
            src_ref=mine_ref.at[other], dst_ref=parts.at[offset - 1], send_sem=send.at[offset - 1],
            recv_sem=recv.at[offset - 1], device_id=peer, device_id_type=MESH,
        )

    def share(offset):
        _, peer = peer_at(offset, n_dp, n_rep)
        return pltpu.make_async_remote_copy(
            src_ref=sums, dst_ref=out_ref.at[me], send_sem=send_two.at[offset - 1],
            recv_sem=recv_two.at[offset - 1], device_id=peer, device_id_type=MESH,
        )

    def start_scatter(offset, carry):
        scatter(offset).start()
        return carry

    def add(offset, carry):
        scatter(offset).wait_recv()
        return carry + parts[offset - 1]

    def start_share(offset, carry):
        share(offset).start()
        return carry

    def finish(offset, carry):
        scatter(offset).wait_send()
        share(offset).wait()
        return carry

    lax.fori_loop(1, total, start_scatter, 0)
    result = lax.fori_loop(1, total, add, mine_ref[me])
    sums[...] = result
    lax.fori_loop(1, total, start_share, 0)
    out_ref[me] = result
    lax.fori_loop(1, total, finish, 0)


def total_over_all(flat, n_dp, n_rep, collective, name):
    total = n_dp * n_rep
    count = flat.shape[0]
    chunk = -(-count // (total * 1024)) * 1024
    padded = jnp.pad(flat, (0, total * chunk - count)).reshape(total, chunk // 128, 128)
    vmem = pl.BlockSpec(memory_space=pltpu.VMEM)
    dma = pltpu.SemaphoreType.DMA
    summed = pl.pallas_call(
        functools.partial(total_kernel, n_dp, n_rep),
        out_shape=jax.ShapeDtypeStruct(padded.shape, padded.dtype),
        in_specs=[vmem],
        out_specs=vmem,
        scratch_shapes=[
            pltpu.VMEM((total - 1,) + padded.shape[1:], padded.dtype),
            pltpu.VMEM(padded.shape[1:], padded.dtype),
            dma((total - 1,)), dma((total - 1,)), dma((total - 1,)), dma((total - 1,)),
        ],
        compiler_params=pltpu.CompilerParams(
            collective_id=collective, has_side_effects=True, vmem_limit_bytes=48 << 20
        ),
        name=name,
    )(padded)
    return summed.reshape(-1)[:count]


def masked_scores(query_heads, key_heads, allowed):
    scores = (
        jnp.einsum("rshd,rthd->rhst", query_heads, key_heads, preferred_element_type=jnp.float32)
        * SCORE_SCALE
    )
    return jnp.where(allowed[:, None], scores, MASKED)


def block_forward(inputs, allowed, weights, vector_pieces, pooled_only):
    (
        gain_one, shift_one, bias_query, bias_value, bias_out,
        gain_two, shift_two, bias_shrink, bias_expand,
    ) = vector_pieces
    row_count, seq_tokens = (inputs.shape[0], inputs.shape[1])
    normed = layer_norm(inputs, gain_one, shift_one).astype(jnp.bfloat16)
    mixing = jnp.einsum("rsd,dc->rsc", normed, weights[:, : 3 * D], preferred_element_type=jnp.float32)
    mixing = mixing + jnp.concatenate([bias_query, jnp.zeros_like(bias_query), bias_value])
    head_parts = mixing.astype(jnp.bfloat16).reshape(row_count, seq_tokens, 3, HEADS, HEAD_DIM)
    query_heads, key_heads, value_heads = (head_parts[:, :, 0], head_parts[:, :, 1], head_parts[:, :, 2])
    scores = masked_scores(query_heads, key_heads, allowed)
    highest = jnp.max(scores, axis=-1, keepdims=True)
    log_total = highest + jnp.log(jnp.sum(jnp.exp(scores - highest), axis=-1, keepdims=True))
    attention = jnp.exp(scores - log_total).astype(jnp.bfloat16)
    mixed_heads = jnp.einsum("rhst,rthd->rshd", attention, value_heads, preferred_element_type=jnp.float32)
    mixed_heads = mixed_heads.reshape(row_count, seq_tokens, D).astype(jnp.bfloat16)
    attended = (
        jnp.einsum("rsd,de->rse", mixed_heads, weights[:, 3 * D : 4 * D], preferred_element_type=jnp.float32)
        + bias_out
    )
    middle = inputs + attended
    normed_two = layer_norm(middle, gain_two, shift_two).astype(jnp.bfloat16)
    hidden = (
        jnp.einsum("rsd,df->rsf", normed_two, weights[:, 4 * D : 4 * D + FF], preferred_element_type=jnp.float32)
        + bias_expand
    )
    active = jax.nn.gelu(hidden, approximate=False).astype(jnp.bfloat16)
    shrink = weights[:, 4 * D + FF :]
    if pooled_only:
        mean_active = jnp.mean(active.astype(jnp.float32), axis=1)
        high = mean_active.astype(jnp.bfloat16)
        rest = mean_active - high.astype(jnp.float32)
        low = rest.astype(jnp.bfloat16)
        lower = (rest - low.astype(jnp.float32)).astype(jnp.bfloat16)
        stacked = jnp.concatenate([high, low, lower], axis=0)
        shrunk = jnp.einsum("pf,df->pd", stacked, shrink, preferred_element_type=jnp.float32)
        shrunk = jnp.sum(shrunk.reshape(3, row_count, D), axis=0)
        return jnp.mean(middle, axis=1) + shrunk + bias_shrink
    shrunk = jnp.einsum("rsf,df->rsd", active, shrink, preferred_element_type=jnp.float32) + bias_shrink
    kept = (normed, query_heads, key_heads, value_heads, log_total, mixed_heads, middle, normed_two, hidden, active)
    return (middle + shrunk, kept)


def token_sum(values_low):
    return jnp.sum(values_low.astype(jnp.float32).reshape(-1, values_low.shape[-1]), axis=0)


def block_backward(inputs, allowed, weights, vector_pieces, forward_kept, grad_out, own_group, own_count):
    (gain_one, shift_one, _, _, _, gain_two, shift_two, _, _) = vector_pieces
    (normed, query_heads, key_heads, value_heads, log_total, mixed_heads, middle, normed_two, hidden, active) = forward_kept
    row_count, seq_tokens = (inputs.shape[0], inputs.shape[1])
    grad_shrunk = grad_out.astype(jnp.bfloat16)
    grad_active = jnp.einsum("rsd,df->rsf", grad_shrunk, weights[:, 4 * D + FF :], preferred_element_type=jnp.float32)
    _, gelu_back = jax.vjp(lambda before_gelu: jax.nn.gelu(before_gelu, approximate=False), hidden)
    grad_hidden = gelu_back(grad_active)[0].astype(jnp.bfloat16)
    grad_normed_two = jnp.einsum(
        "rsf,df->rsd", grad_hidden, weights[:, 4 * D : 4 * D + FF], preferred_element_type=jnp.float32
    )
    _, norm_two_back = jax.vjp(layer_norm, middle, gain_two, shift_two)
    grad_middle, grad_gain_two, grad_shift_two = norm_two_back(grad_normed_two)
    grad_middle = grad_middle + grad_out
    grad_attended = grad_middle.astype(jnp.bfloat16)
    grad_mixed = jnp.einsum("rse,de->rsd", grad_attended, weights[:, 3 * D : 4 * D], preferred_element_type=jnp.float32)
    grad_mixed = grad_mixed.astype(jnp.bfloat16).reshape(row_count, seq_tokens, HEADS, HEAD_DIM)
    attention = jnp.exp(masked_scores(query_heads, key_heads, allowed) - log_total)
    grad_values = jnp.einsum("rhst,rshd->rthd", attention.astype(jnp.bfloat16), grad_mixed, preferred_element_type=jnp.float32)
    grad_attention = jnp.einsum("rshd,rthd->rhst", grad_mixed, value_heads, preferred_element_type=jnp.float32)
    grad_scores = attention * (grad_attention - jnp.sum(attention * grad_attention, axis=-1, keepdims=True))
    grad_scores = grad_scores.astype(jnp.bfloat16)
    grad_query = jnp.einsum("rhst,rthd->rshd", grad_scores, key_heads, preferred_element_type=jnp.float32) * SCORE_SCALE
    grad_keys = jnp.einsum("rhst,rshd->rthd", grad_scores, query_heads, preferred_element_type=jnp.float32) * SCORE_SCALE
    grad_mixing = (
        jnp.stack([grad_query, grad_keys, grad_values], axis=2).reshape(row_count, seq_tokens, 3 * D).astype(jnp.bfloat16)
    )

    def mine(values):
        return lax.dynamic_slice_in_dim(values, own_group * own_count, own_count, 0)

    grad_normed = jnp.einsum("rsc,dc->rsd", mine(grad_mixing), weights[:, : 3 * D], preferred_element_type=jnp.float32)
    _, norm_one_back = jax.vjp(layer_norm, mine(inputs), gain_one, shift_one)
    grad_inputs, grad_gain_one, grad_shift_one = norm_one_back(grad_normed)
    grad_inputs = grad_inputs + mine(grad_middle)
    share = 1.0 / GROUP
    vector_grad = jnp.concatenate(
        [
            grad_gain_one, grad_shift_one,
            share * token_sum(grad_mixing[..., :D]), share * token_sum(grad_mixing[..., 2 * D :]),
            share * token_sum(grad_attended), share * grad_gain_two, share * grad_shift_two,
            share * token_sum(grad_shrunk), share * token_sum(grad_hidden),
        ]
    )
    tokens = row_count * seq_tokens
    outer_terms = (
        (normed.reshape(tokens, D), grad_mixing.reshape(tokens, 3 * D)),
        (mixed_heads.reshape(tokens, D), grad_attended.reshape(tokens, D)),
        (normed_two.reshape(tokens, D), grad_hidden.reshape(tokens, FF)),
        (grad_shrunk.reshape(tokens, D), active.reshape(tokens, FF)),
    )
    return (grad_inputs, vector_grad, outer_terms)


def orthonormal(stacked):
    waiting = [stacked[:, column_id] for column_id in range(stacked.shape[1])]
    finished = []
    while waiting:
        vector = waiting.pop(0)
        vector = vector / (jnp.sqrt(jnp.sum(vector * vector, axis=-1, keepdims=True)) + NORM_FLOOR)
        finished.append(vector)
        if waiting:
            later = jnp.stack(waiting, axis=1)
            later = later - jnp.sum(vector[:, None] * later, axis=-1, keepdims=True) * vector[:, None]
            waiting = [later[:, i] for i in range(later.shape[1])]
    return jnp.stack(finished, axis=1)


def rows_factor(start_part, row_block):
    return jnp.einsum("kc,dc->kd", start_part, row_block, precision=PRECISE)


def per_device(
    image_tokens, image_weights, image_vectors, text_tokens, segments, text_weights,
    text_vectors, momentum, vector_momentum, error_feedback, start_factors,
):
    n_rep, n_dp = lax.axis_size("rep"), lax.axis_size("dp")
    n_inner = n_dp // GROUP
    total = n_rep * n_dp
    device_pairs, patches = image_tokens.shape[0], image_tokens.shape[1]
    text_rows, seq_tokens = text_tokens.shape[0], text_tokens.shape[1]
    pair_total = device_pairs * total
    own_rows = text_weights.shape[0]
    d_at, r_at = lax.axis_index("dp"), lax.axis_index("rep")
    z_at, y_at = d_at // n_inner, d_at % n_inner
    row_start = d_at * own_rows
    factor_rank = start_factors.shape[0]
    bounds = matrix_bounds()
    tokens = text_tokens.reshape(text_rows * seq_tokens, D)
    feedback_rows = error_feedback[0]
    fused = (
        own_rows % (16 * LANES) == 0 and n_inner == 2 and n_rep == 4 and device_pairs == 8
        and text_rows * seq_tokens == PAIR and 2 * seq_tokens == PAIR and 2 * patches <= PAIR
        and n_dp == 8 and factor_rank == 8
    )
    if fused:
        outs = gather_and_forward(
            n_dp, n_rep, text_weights, image_weights, tokens, segments, image_tokens, text_vectors, image_vectors
        )
        pictures, words, pooled, marks = outs[1:5]
        kept = (outs[0],) + tuple(outs[5:])
        worker_rows, grad_inputs, loss, left_basis, new_right, new_vectors, new_vector_momentum = backward(
            n_dp, n_rep, kept, pooled, pictures, marks, tokens, text_vectors, feedback_rows, start_factors,
            vector_momentum,
        )
        (
            new_feedback, new_momentum, new_weights, words, grad_inputs, left_basis, new_right,
            new_vectors, new_vector_momentum, loss,
        ) = finish(
            n_dp, n_rep, worker_rows, momentum, text_weights, left_basis, new_right, words, grad_inputs,
            new_vectors, new_vector_momentum, loss,
        )
        return (
            loss.reshape(()), words.reshape(text_rows, seq_tokens, D), grad_inputs.reshape(text_rows, seq_tokens, D),
            new_weights, new_momentum, new_feedback[None], new_vectors.reshape(-1), new_vector_momentum.reshape(-1),
            left_basis, new_right,
        )
    text_low, frozen, token_group, segment_group = gather_weights(
        n_dp, text_weights.astype(jnp.bfloat16), image_weights, tokens, segments
    )
    text_low, frozen = text_low.reshape(D, -1), frozen.reshape(D, -1)
    full_mask = jnp.zeros((device_pairs, patches, patches), jnp.int32) == 0
    image_pooled = block_forward(
        image_tokens.astype(jnp.float32), full_mask, frozen, vector_parts(image_vectors), True
    )
    group_rows = GROUP * text_rows
    text_float = token_group.reshape(group_rows, seq_tokens, D).astype(jnp.float32)
    segment_all = segment_group.reshape(group_rows, seq_tokens)
    allowed = segment_all[:, :, None] == segment_all[:, None, :]
    vector_pieces = vector_parts(text_vectors)
    group_output, forward_kept = block_forward(text_float, allowed, text_low, vector_pieces, False)
    text_output = lax.dynamic_slice_in_dim(group_output, z_at * text_rows, text_rows, 0)
    caption_marks = (
        segment_all[:, None, :] == jnp.arange(PER_ROW, dtype=jnp.int32)[None, :, None]
    ).astype(jnp.float32)
    counts = jnp.sum(caption_marks, axis=-1, keepdims=True)
    pooled = (jnp.einsum("rks,rsd->rkd", caption_marks, group_output, precision=PRECISE) / counts).reshape(-1, D)
    image_emb = unit_rows(image_pooled).astype(jnp.bfloat16)
    text_norm, embed_back = jax.vjp(unit_rows, pooled)
    text_emb = text_norm.astype(jnp.bfloat16)
    own_emb = lax.dynamic_slice_in_dim(text_emb, z_at * device_pairs, device_pairs, 0)
    embeddings = spread(jnp.concatenate([image_emb, own_emb], axis=0), n_dp, n_rep, 2, "spread_embeddings")
    image_all = embeddings[:, :device_pairs].reshape(pair_total, D)
    text_all = embeddings[:, device_pairs:].reshape(pair_total, D)
    own_pairs = (
        ((jnp.arange(GROUP, dtype=jnp.int32) * n_inner + y_at) * n_rep + r_at)[:, None] * device_pairs
        + jnp.arange(device_pairs, dtype=jnp.int32)[None, :]
    ).reshape(-1)
    logits = LOGIT_SCALE * jnp.einsum("pd,bd->pb", image_all, text_all, preferred_element_type=jnp.float32)
    image_top = jnp.max(logits, axis=1)
    image_log_total = image_top + jnp.log(jnp.sum(jnp.exp(logits - image_top[:, None]), axis=1))
    caption_top = jnp.max(logits, axis=0)
    caption_log_total = caption_top + jnp.log(jnp.sum(jnp.exp(logits - caption_top[None, :]), axis=0))
    pair_ids = jnp.arange(pair_total, dtype=jnp.int32)
    matched = jnp.sum(jnp.where(pair_ids[:, None] == pair_ids[None, :], logits, 0.0), axis=1)
    loss_total = (jnp.sum(image_log_total - matched) + jnp.sum(caption_log_total - matched)) / (2.0 * pair_total)
    diagonal_pick = (pair_ids[None, :] == own_pairs[:, None]).astype(jnp.float32)
    text_logits = LOGIT_SCALE * jnp.einsum("pd,bd->pb", text_emb, image_all, preferred_element_type=jnp.float32)
    text_top = jnp.max(text_logits, axis=1, keepdims=True)
    text_log_total = text_top + jnp.log(jnp.sum(jnp.exp(text_logits - text_top), axis=1, keepdims=True))
    text_soft = ((jnp.exp(text_logits - text_log_total) - diagonal_pick) * 0.5).astype(jnp.bfloat16)
    column_soft = ((jnp.exp(text_logits - image_log_total[None, :]) - diagonal_pick) * 0.5).astype(jnp.bfloat16)
    grad_text = LOGIT_SCALE * (
        jnp.einsum("pb,bd->pd", text_soft, image_all, preferred_element_type=jnp.float32)
        + jnp.einsum("pb,bd->pd", column_soft, image_all, preferred_element_type=jnp.float32)
    )
    grad_pooled = embed_back(grad_text)[0]
    grad_pooled = grad_pooled.reshape(-1, PER_ROW, D) / counts
    grad_out = jnp.einsum("rks,rkd->rsd", caption_marks, grad_pooled, precision=PRECISE)
    grad_inputs, vector_grad, outer_terms = block_backward(
        text_float, allowed, text_low, vector_pieces, forward_kept, grad_out, z_at, text_rows
    )
    group_width = n_inner * own_rows
    worker_blocks = []
    for (left_side, right_side), (first_col, after_col) in zip(outer_terms, bounds):
        left_cut = lax.dynamic_slice_in_dim(left_side, z_at * group_width, group_width, 1)
        block = jnp.einsum("tc,tk->ck", left_cut, right_side, preferred_element_type=jnp.float32)
        mine = lax.dynamic_slice_in_dim(block, y_at * own_rows, own_rows, 0)
        for k in range(1, n_inner):
            target = lax.rem(y_at + k, n_inner)
            outgoing = lax.dynamic_slice_in_dim(block, target * own_rows, own_rows, 0).astype(jnp.bfloat16)
            pairs = [
                (z * n_inner + y, z * n_inner + (y + k) % n_inner) for z in range(GROUP) for y in range(n_inner)
            ]
            mine = mine + lax.ppermute(outgoing, "dp", pairs).astype(jnp.float32)
        worker_blocks.append(mine + feedback_rows[:, first_col:after_col])
    factor_rows = jnp.concatenate(
        [
            rows_factor(start_factors[:, first_col:after_col], rows)
            for rows, (first_col, after_col) in zip(worker_blocks, bounds)
        ],
        axis=0,
    )
    gathered_rows = spread(factor_rows, n_dp, n_rep, 3, "spread_factors")
    factor = jnp.sum(gathered_rows.reshape(n_dp, n_rep, 4 * factor_rank, own_rows), axis=1)
    factor = jnp.swapaxes(factor, 0, 1).reshape(4, factor_rank, D)
    left_basis = orthonormal(factor).reshape(4 * factor_rank, D)
    basis_rows = lax.dynamic_slice_in_dim(left_basis, row_start, own_rows, 1)
    basis_parts = [basis_rows[i * factor_rank : (i + 1) * factor_rank] for i in range(4)]
    right_part = jnp.concatenate(
        [jnp.einsum("kd,dc->kc", part, rows, precision=PRECISE) for part, rows in zip(basis_parts, worker_blocks)],
        axis=1,
    )
    summed = total_over_all(
        jnp.concatenate([right_part.reshape(-1), vector_grad]), n_dp, n_rep, 4, "total_right"
    )
    new_right = summed[: right_part.size].reshape(right_part.shape)
    vector_total = summed[right_part.size :]
    approximation = jnp.concatenate(
        [
            jnp.einsum("kd,kc->dc", part, new_right[:, first_col:after_col], precision=PRECISE)
            for part, (first_col, after_col) in zip(basis_parts, bounds)
        ],
        axis=1,
    )
    worker_rows = jnp.concatenate(worker_blocks, axis=1)
    new_feedback = (worker_rows - approximation / n_rep)[None]
    new_momentum = MOMENTUM_DECAY * momentum + approximation
    new_weights = text_weights - STEP_RATE * new_momentum
    new_vector_momentum = MOMENTUM_DECAY * vector_momentum + vector_total
    new_vectors = text_vectors - STEP_RATE * new_vector_momentum
    return (
        loss_total, text_output, grad_inputs, new_weights, new_momentum, new_feedback,
        new_vectors, new_vector_momentum, left_basis, new_right,
    )


def solution(mesh):
    placed = (
        P(("dp", "rep"), None, None), P("dp", None), P(), P(("dp", "rep"), None, None), P(("dp", "rep"), None),
        P("dp", None), P(), P("dp", None), P(), P("rep", "dp", None), P(),
    )
    return jax.shard_map(
        per_device,
        mesh=mesh,
        in_specs=placed,
        out_specs=(
            P(), P(("dp", "rep"), None, None), P(("dp", "rep"), None, None), P("dp", None), P("dp", None),
            P("rep", "dp", None), P(), P(), P(), P(),
        ),
        check_vma=False,
    )
```

```python
import functools

import jax
import jax.numpy as jnp
from jax import lax
from jax.experimental import pallas as pl
from jax.experimental.pallas import tpu as pltpu
from jax.sharding import PartitionSpec as P

D = 768
FF = 3072
HEADS = 12
HEAD_DIM = 64
PER_ROW = 4
GROUP = 4
SECTION = 3072
LANE_COLS = 512

PRECISE = lax.Precision.HIGHEST
LAYER_EPS = 1e-06
SCORE_SCALE = 0.125
LOGIT_SCALE = 50.0
MOMENTUM_DECAY = 0.9
STEP_RATE = 0.08
NORM_FLOOR = 1e-08
MASKED = -1e30
MESH = pl.DeviceIdType.MESH


def layer_norm(values, layer_gain, layer_shift):
    center = values - jnp.mean(values, axis=-1, keepdims=True)
    spread = jnp.mean(center * center, axis=-1, keepdims=True)
    return center * lax.rsqrt(spread + LAYER_EPS) * layer_gain + layer_shift


def unit_rows(values):
    return values * lax.rsqrt(jnp.sum(values * values, axis=-1, keepdims=True) + LAYER_EPS)


def vector_parts(vectors):
    pieces = [vectors[position * D : (position + 1) * D] for position in range(8)]
    return pieces + [vectors[8 * D :]]


def matrix_bounds():
    return ((0, 3 * D), (3 * D, 4 * D), (4 * D, 4 * D + FF), (4 * D + FF, 4 * D + 2 * FF))


def gather_kernel(
    n_dp, text_ref, image_ref, tok_ref, seg_ref, wt_ref, wi_ref, tok_out, seg_out,
    z_send, z_recv, y_send, y_recv, x_send, x_recv, c_send, c_recv, t_send, t_recv, t_own, own_sem,
):
    n_inner = n_dp // GROUP
    d_at, r_at = lax.axis_index("dp"), lax.axis_index("rep")
    z_at, y_at = d_at // n_inner, d_at % n_inner
    x_at, c_at = r_at // 2, r_at % 2
    z_peers = [(lax.rem(z_at + k, GROUP) * n_inner + y_at, r_at) for k in range(1, GROUP)]
    z_from = [lax.rem(z_at + GROUP - k, GROUP) for k in range(1, GROUP)]
    y_peers = [(z_at * n_inner + lax.rem(y_at + k, n_inner), r_at) for k in range(1, n_inner)]
    y_from = [lax.rem(y_at + n_inner - k, n_inner) for k in range(1, n_inner)]
    x_peer = (d_at, (1 - x_at) * 2 + c_at)
    c_peer = (d_at, x_at * 2 + 1 - c_at)

    barrier = pltpu.get_barrier_semaphore()
    everyone = z_peers + y_peers + [x_peer, c_peer]
    for peer in everyone:
        pl.semaphore_signal(barrier, inc=1, device_id=peer, device_id_type=MESH)
    pl.semaphore_wait(barrier, len(everyone))

    def shard_of(z, y):
        return z * n_inner + y

    sections = [(image_ref, wi_ref, 0), (text_ref, wt_ref, 0), (image_ref, wi_ref, 1),
                (text_ref, wt_ref, 1), (image_ref, wi_ref, 2), (text_ref, wt_ref, 2)]

    def cols(section, lane):
        start = sections[section][2] * SECTION + lane * LANE_COLS
        return pl.ds(pl.multiple_of(start, 128), LANE_COLS)

    lane_both = c_at
    lane_mine = 2 + x_at * 2 + c_at
    lane_theirs = 2 + (1 - x_at) * 2 + c_at
    lanes = (lane_both, lane_mine)

    locals_ = [
        pltpu.make_async_copy(tok_ref, tok_out.at[z_at], t_own.at[0]),
        pltpu.make_async_copy(seg_ref, seg_out.at[z_at], t_own.at[1]),
    ]
    for s, (src, full, _) in enumerate(sections):
        for j in range(2):
            column = cols(s, lanes[j])
            locals_.append(pltpu.make_async_copy(src.at[:, column], full.at[d_at, :, column], own_sem.at[s, j]))
    for copy in locals_:
        copy.start()

    def remote(src, dst, send, recv, peer):
        return pltpu.make_async_remote_copy(
            src_ref=src, dst_ref=dst, send_sem=send, recv_sem=recv, device_id=peer, device_id_type=MESH
        )

    def z_copy(s, k, j):
        src, full, _ = sections[s]
        return remote(
            src.at[:, cols(s, lanes[j])], full.at[d_at, :, cols(s, lanes[j])],
            z_send.at[s, k, j], z_recv.at[s, k, j], z_peers[k],
        )

    def y_copy(s, q, zi, j):
        src, full, _ = sections[s]
        column = cols(s, lanes[j])
        if zi == 0:
            shard, source = d_at, src.at[:, column]
        else:
            shard = shard_of(z_from[zi - 1], y_at)
            source = full.at[shard, :, column]
        return remote(source, full.at[shard, :, column], y_send.at[s, q, zi, j], y_recv.at[s, q, zi, j], y_peers[q])

    def x_copy(s):
        full = sections[s][1]
        block = full.at[:, :, cols(s, lane_mine)]
        return remote(block, block, x_send.at[s], x_recv.at[s], x_peer)

    def c_copy(s, j):
        full = sections[s][1]
        block = full.at[:, :, cols(s, (lane_both, lane_mine, lane_theirs)[j])]
        return remote(block, block, c_send.at[s, j], c_recv.at[s, j], c_peer)

    count = len(sections)
    tokens = []
    for k in range(GROUP - 1):
        tokens.append(remote(tok_ref, tok_out.at[z_at], t_send.at[0, k], t_recv.at[0, k], z_peers[k]))
        tokens.append(remote(seg_ref, seg_out.at[z_at], t_send.at[1, k], t_recv.at[1, k], z_peers[k]))

    def begin(s):
        for j in range(2):
            for k in range(GROUP - 1):
                z_copy(s, k, j).start()
            for q in range(n_inner - 1):
                y_copy(s, q, 0, j).start()

    begin(0)
    for copy in tokens:
        copy.start()
    for copy in locals_:
        copy.wait()
    begin(1)
    for step in range(count + 3):
        if step < count:
            for k in range(GROUP - 1):
                for j in range(2):
                    z_copy(step, k, j).wait_recv()
                    for q in range(n_inner - 1):
                        y_copy(step, q, k + 1, j).start()
            if step + 2 < count:
                begin(step + 2)
        s = step - 1
        if 0 <= s < count:
            for q in range(n_inner - 1):
                for zi in range(GROUP):
                    for j in range(2):
                        y_copy(s, q, zi, j).wait_recv()
            x_copy(s).start()
            for j in range(2):
                c_copy(s, j).start()
        s = step - 2
        if 0 <= s < count:
            x_copy(s).wait_recv()
            c_copy(s, 2).start()
        s = step - 3
        if 0 <= s < count:
            for j in range(3):
                c_copy(s, j).wait_recv()
    for copy in tokens:
        copy.wait()
    for s in range(count):
        for j in range(2):
            for k in range(GROUP - 1):
                z_copy(s, k, j).wait_send()
            for q in range(n_inner - 1):
                for zi in range(GROUP):
                    y_copy(s, q, zi, j).wait_send()
        x_copy(s).wait_send()
        for j in range(3):
            c_copy(s, j).wait_send()


def gather_weights(n_dp, text_low, image_low, tokens, segments):
    n_inner = n_dp // GROUP
    full = jax.ShapeDtypeStruct((n_dp,) + text_low.shape, jnp.bfloat16)
    hbm = pl.BlockSpec(memory_space=pltpu.HBM)
    dma = pltpu.SemaphoreType.DMA
    return pl.pallas_call(
        functools.partial(gather_kernel, n_dp),
        out_shape=(
            full,
            full,
            jax.ShapeDtypeStruct((GROUP,) + tokens.shape, jnp.bfloat16),
            jax.ShapeDtypeStruct((GROUP,) + segments.shape, jnp.int32),
        ),
        in_specs=[hbm] * 4,
        out_specs=(hbm,) * 4,
        scratch_shapes=[
            dma((6, GROUP - 1, 2)), dma((6, GROUP - 1, 2)),
            dma((6, n_inner - 1, GROUP, 2)), dma((6, n_inner - 1, GROUP, 2)),
            dma((6,)), dma((6,)), dma((6, 3)), dma((6, 3)),
            dma((2, GROUP - 1)), dma((2, GROUP - 1)), dma((2,)), dma((6, 2)),
        ],
        compiler_params=pltpu.CompilerParams(collective_id=1, has_side_effects=True),
        name="gather_weights",
    )(text_low, image_low, tokens, segments)


TILE = 256
PAIR = 128
ROWS = 32
LANES = 6
PART = 768
PARTS = 12
DEPTH = 8
AHEAD = 2
OWN_AHEAD = 4
TOKENS_AT = 6
STEP_TIME = 4.5
LAG_Z = 1
LAG_Y = 1
LAG_X = 2
LAG_C = 1
AT_Y = 2 * LAG_Z + LAG_Y
AT_X = AT_Y + LAG_X
AT_C = AT_X + LAG_C
WORDS = (GROUP * PAIR)


def piece_of(vec_ref, index, width=D):
    return vec_ref[:, pl.ds(index * D, width)]


def loop(count, body, unroll=1):
    def step(i, carry):
        body(i)
        return carry

    lax.fori_loop(0, count, step, 0, unroll=unroll)


def aligned(i, size):
    return pl.ds(pl.multiple_of(i * size, size), size)


def norm_rows(values):
    center = values - jnp.mean(values, axis=-1, keepdims=True)
    spread_ = jnp.mean(center * center, axis=-1, keepdims=True)
    return center * lax.rsqrt(spread_ + LAYER_EPS)


def dot(left, right):
    return jnp.dot(left, right, preferred_element_type=jnp.float32)


def dot_nt(left, right):
    return lax.dot_general(left, right, (((1,), (1,)), ((), ())), preferred_element_type=jnp.float32)


def dot_tn(left, right):
    return lax.dot_general(left, right, (((0,), (0,)), ((), ())), preferred_element_type=jnp.float32)


def lane_is_first():
    return lax.broadcasted_iota(jnp.int32, (PAIR, PAIR), 1) < HEAD_DIM


def two_heads(block):
    first = lane_is_first()
    zero = jnp.zeros_like(block)
    return jnp.concatenate([jnp.where(first, block, zero), jnp.where(first, zero, block)], axis=0)


def attention_forward(qkv, mixed, chance, allowed_of, first, count):
    pairs = HEADS // 2

    def body(k):
        at = first + k
        i, j = at // pairs, lax.rem(at, pairs)
        rows = aligned(i, PAIR)
        query = qkv[rows, aligned(j, PAIR)]
        key = qkv[rows, pl.ds(pl.multiple_of(D + j * PAIR, PAIR), PAIR)]
        value = qkv[rows, pl.ds(pl.multiple_of(2 * D + j * PAIR, PAIR), PAIR)]
        scores = dot_nt(two_heads(query), key) * SCORE_SCALE
        allowed = allowed_of(i)
        scores = jnp.where(jnp.concatenate([allowed, allowed], axis=0), scores, MASKED)
        scores = jnp.exp(scores - jnp.max(scores, axis=-1, keepdims=True))
        weight = scores / jnp.sum(scores, axis=-1, keepdims=True)
        if chance is not None:
            chance[at] = weight
        low = weight.astype(jnp.bfloat16)
        side = jnp.concatenate([low[:PAIR], low[PAIR:]], axis=1)
        mixed[rows, aligned(j, PAIR)] = dot(side, two_heads(value)).astype(jnp.bfloat16)

    loop(count, body, unroll=2)


def forward_kernel(
    n_dp, n_rep, patches,
    text_ref, image_ref, tok_ref, pic_ref, seg_ref, tvec_ref, ivec_ref,
    wt_out, pic_all, words_out, text_pool_out, marks_out, qkv_out, chance_out, mid_out, slope_out,
    act_out, nt_out, at_out, mt_out,
    wi_ref, wt_vmem, tok, seg_col, seg_row, normed, qkv, mixed, middle, normed_two, active, slope, chance, total, hid, turned, apool, image_pool_out, patches_in, padded, master,
    z_send, z_recv, y_send, y_recv, x_send, x_recv, c_send, c_recv, t_send, t_recv, t_own, own_sem, w_sem, out_sem, p_send, p_recv,
):
    n_inner = n_dp // GROUP
    d_at, r_at = lax.axis_index("dp"), lax.axis_index("rep")
    z_at, y_at = d_at // n_inner, lax.rem(d_at, n_inner)
    x_at, c_at = r_at // 2, lax.rem(r_at, 2)
    z_next = [((z_at - 1) * n_inner + y_at, r_at), ((z_at + 1) * n_inner + y_at, r_at)]
    y_peers = [(z_at * n_inner + 1 - y_at, r_at)]
    x_peer = (d_at, (1 - x_at) * 2 + c_at)
    c_peer = (d_at, x_at * 2 + 1 - c_at)

    devices = n_dp * n_rep
    me = d_at * n_rep + r_at
    z_open = (z_at > 0, z_at < GROUP - 1)
    barrier = pltpu.get_barrier_semaphore()

    def hello(peer):
        pl.semaphore_signal(barrier, inc=1, device_id=peer, device_id_type=MESH)

    for peer in (y_peers[0], x_peer, c_peer):
        hello(peer)
    for up in range(2):
        pl.when(z_open[up])(functools.partial(hello, z_next[up]))

    sections = [(image_ref, wi_ref, k) for k in range(PARTS)] + [(text_ref, wt_vmem, k) for k in range(PARTS)]
    count = len(sections)
    lane_mine = c_at * 3 + 2 * x_at
    lane_theirs = c_at * 3 + 2 * (1 - x_at)
    lanes_two = pl.ds(c_at * 3 + x_at, 2)
    lanes_three = pl.ds(c_at * 3, 3)

    def remote(src, dst, send, recv, peer):
        return pltpu.make_async_remote_copy(
            src_ref=src, dst_ref=dst, send_sem=send, recv_sem=recv, device_id=peer, device_id_type=MESH
        )

    def cols(s):
        return pl.ds(sections[s][2] * PART, PART)

    def set_of(s):
        return s // PARTS

    def size_of(s, shards, lanes_):
        return sections[s][1].at[sections[s][2], pl.ds(0, shards), pl.ds(0, lanes_)]

    def all_size(group, shards, lanes_):
        return sections[group * PARTS][1].at[:, pl.ds(0, shards), pl.ds(0, lanes_)]

    def landed(block, recv, peer):
        remote(block, block, x_send.at[0], recv, peer).wait_recv()

    def gone(block, send, peer):
        remote(block, block, send, x_recv.at[0], peer).wait_send()

    def held(s, shard, lane):
        _, full, k = sections[s]
        return full.at[k, shard, lane]

    def z_copy(s, up, hop):
        unit = z_at - hop if up else z_at + hop
        shard = unit * n_inner + y_at
        return remote(
            held(s, shard, lanes_two), held(s, shard, lanes_two),
            z_send.at[set_of(s), up, hop], z_recv.at[s, unit], z_next[up],
        )

    def y_copy(s, unit):
        shard = unit * n_inner + y_at
        return remote(
            held(s, shard, lanes_two), held(s, shard, lanes_two),
            y_send.at[set_of(s)], y_recv.at[s], y_peers[0],
        )

    def x_copy(s, unit):
        block = held(s, pl.ds(unit * n_inner, n_inner), lane_mine)
        return remote(block, block, x_send.at[set_of(s)], x_recv.at[s], x_peer)

    def x_own_copy(s):
        block = held(s, z_at * n_inner + 1 - y_at, lane_mine)
        return remote(block, block, x_send.at[set_of(s)], x_recv.at[s], x_peer)

    def c_copy(s, j):
        block = held(s, slice(None), (lanes_two, lane_theirs)[j])
        return remote(block, block, c_send.at[set_of(s)], c_recv.at[s], c_peer)

    def store(s):
        return pltpu.make_async_copy(wt_vmem.at[s - PARTS], wt_out.at[s - PARTS], w_sem.at[s - PARTS])

    def own_shard(s):
        src, _, _ = sections[s]
        return pltpu.make_async_copy(
            src.at[lanes_three, :, cols(s)], held(s, d_at, lanes_three) if s < PARTS else master.at[s % 4], own_sem.at[s]
        )

    def own_ready(s):
        own_shard(s).wait()
        if s >= PARTS:
            wt_vmem[s - PARTS, d_at, lanes_three] = master[s % 4].astype(jnp.bfloat16)

    gathered = ((tok_ref, tok), (None, seg_row))
    firsts = [
        pltpu.make_async_copy(tok_ref, tok.at[z_at], t_own.at[0]),
        pltpu.make_async_copy(pic_ref, patches_in, t_own.at[1]),
    ]

    def token_copy(i, up, hop):
        unit = z_at - hop if up else z_at + hop
        block = gathered[i][1].at[unit]
        return remote(block, block, t_send.at[i, up, hop], t_recv.at[i, unit], z_next[up])

    def token_begin():
        firsts[0].wait()
        number = seg_ref[...].astype(jnp.float32)
        number = jnp.concatenate([number[0:1, :], number[1:2, :] + PER_ROW], axis=1)
        seg_row[z_at] = jnp.broadcast_to(number, (16, PAIR)).astype(jnp.bfloat16)
        for i in range(2):
            for up in range(2):
                pl.when(z_open[up])(token_copy(i, up, 0).start)

    def token_arrive(hop):
        for up in range(2):
            unit = z_at - hop if up else z_at + hop

            @pl.when((unit >= 0) & (unit < GROUP))
            def _():
                for i in range(2):
                    block = gathered[i][1].at[0]
                    landed(block, t_recv.at[i, unit], z_next[up])
                    if hop < GROUP - 1:
                        pl.when(z_open[up])(token_copy(i, up, hop).start)

    def token_gone():
        for up in range(2):
            for hop in range(GROUP - 1):
                unit = z_at - hop if up else z_at + hop
                for i in range(2):
                    pl.when((unit >= 0) & (unit < GROUP) & z_open[up])(
                        functools.partial(gone, gathered[i][1].at[0], t_send.at[i, up, hop], z_next[up])
                    )

    def picture_copy(offset):
        _, other = peer_at(offset, n_dp, n_rep)
        return remote(pic_all.at[me], pic_all.at[me], p_send.at[offset - 1], p_recv.at[offset - 1], other)

    def send_pictures():
        values = image_pool_out[...]
        squares = jnp.sum(values * values, axis=-1, keepdims=True)
        pic_all[me] = (values * lax.rsqrt(squares + LAYER_EPS)).astype(jnp.bfloat16)

        def start(offset, carry):
            picture_copy(offset).start()
            return carry

        lax.fori_loop(1, devices, start, 0)

    def end_pictures():
        def end(offset, carry):
            picture_copy(offset).wait()
            return carry

        lax.fori_loop(1, devices, end, 0)

    def begin(s):
        own_ready(s)
        for up in range(2):
            pl.when(z_open[up])(z_copy(s, up, 0).start)
        y_copy(s, z_at).start()

    def arrive(s, hop):
        for up in range(2):
            unit = z_at - hop if up else z_at + hop

            @pl.when((unit >= 0) & (unit < GROUP))
            def _():
                landed(size_of(s, 1, 2), z_recv.at[s, unit], z_next[up])
                if hop < GROUP - 1:
                    pl.when(z_open[up])(z_copy(s, up, hop).start)
                y_copy(s, unit).start()

    def own_start(s):
        own_shard(s).start()

    def stage_y(s):
        landed(size_of(s, GROUP, 2), y_recv.at[s], y_peers[0])
        for unit in range(GROUP):
            pl.when(unit != z_at)(x_copy(s, unit).start)
        x_own_copy(s).start()
        c_copy(s, 0).start()

    def stage_x(s):
        landed(size_of(s, n_dp - 1, 1), x_recv.at[s], x_peer)
        c_copy(s, 1).start()

    def stage_c(s):
        landed(size_of(s, n_dp, 3), c_recv.at[s], c_peer)
        if s >= PARTS:
            store(s).start()

    def carry_on(step):
        moves = []
        if step + OWN_AHEAD < count:
            moves.append(functools.partial(own_start, step + OWN_AHEAD))
        if step + AHEAD < count:
            moves.append(functools.partial(begin, step + AHEAD))
        for hop in range(1, GROUP):
            s = step - (hop - 1) * LAG_Z
            if 0 <= s < count:
                moves.append(functools.partial(arrive, s, hop))
        for lag, stage in ((AT_Y, stage_y), (AT_X, stage_x), (AT_C, stage_c)):
            if 0 <= step - lag < count:
                moves.append(functools.partial(stage, step - lag))
        if step == TOKENS_AT:
            moves.append(token_begin)
        for hop in range(1, GROUP):
            if step == TOKENS_AT + 2 * hop:
                moves.append(functools.partial(token_arrive, hop))
        return moves


    def weight_tile(s, c):
        _, full, k = sections[s]
        return full[k, :, :, :, aligned(c, TILE)].reshape(D, TILE)

    def weight_rows(s, half):
        _, full, k = sections[s]
        return full[k, pl.ds(half * (n_dp // 2), n_dp // 2)].reshape(D // 2, PART)

    def split_loop(total_, pieces, cost, body):
        size = total_ // pieces
        return [
            (cost, functools.partial(loop, size, functools.partial(lambda base, i: body(base + i), p * size)))
            for p in range(pieces)
        ]

    def first_norm(read, vec):
        def body(i):
            rows = aligned(i, ROWS)
            value = norm_rows(read(i).astype(jnp.float32))
            normed[rows, :] = (value * piece_of(vec, 0) + piece_of(vec, 1)).astype(jnp.bfloat16)

        return split_loop(WORDS // ROWS, 4, 0.5, body)

    def project(slot, part, bias):
        def body(c):
            out = dot(normed[...], weight_tile(slot, c))
            if bias is not None:
                out = out + bias[0][:, pl.ds(pl.multiple_of(bias[1] * D + c * TILE, TILE), TILE)]
            qkv[:, pl.ds(pl.multiple_of(part * D + c * TILE, TILE), TILE)] = out.astype(jnp.bfloat16)

        return split_loop(PART // TILE, 3, 0.6, body)

    def attend(slot, read, vec):
        def body(c):
            where = aligned(c, TILE)
            middle[:, where] = dot(mixed[...], weight_tile(slot, c)) + vec[
                :, pl.ds(pl.multiple_of(4 * D + c * TILE, TILE), TILE)
            ]

        def norm(i):
            rows = aligned(i, ROWS)
            value = middle[rows, :] + read(i).astype(jnp.float32)
            middle[rows, :] = value
            normed_two[rows, :] = (norm_rows(value) * piece_of(vec, 5) + piece_of(vec, 6)).astype(jnp.bfloat16)

        return split_loop(PART // TILE, 3, 0.6, body) + split_loop(WORDS // ROWS, 4, 0.6, norm)

    def expand(slot, part, vec, keep):
        def one(c, p):
            start = part * PART + c * TILE
            if p == 0:
                hid[...] = dot(normed_two[...], weight_tile(slot, c)) + vec[:, pl.ds(8 * D + start, TILE)]

            def inner(i):
                rows = aligned(i + p * (WORDS // ROWS // 2), ROWS)
                value = hid[rows, :]
                phi = 0.5 + 0.5 * lax.erf(value * 0.7071067811865476)
                active[rows, pl.ds(start, TILE)] = (value * phi).astype(jnp.bfloat16)
                if keep:
                    slope[rows, pl.ds(start, TILE)] = phi + value * (
                        0.3989422804014327 * jnp.exp(-0.5 * value * value)
                    )

            loop(WORDS // ROWS // 2, inner, unroll=2)

        return [
            (1.2 - 0.4 * p + 0.2 * keep, functools.partial(one, c, p)) for c in range(PART // TILE) for p in range(2)
        ]

    def shrink(slot, part, vec):
        def one(half):
            where = pl.ds(half * (D // 2), D // 2)
            out = dot_nt(active[:, pl.ds(part * PART, PART)], weight_rows(slot, half))
            if part == 0:
                total[:, where] = out + middle[:, where] + vec[:, pl.ds(7 * D + half * (D // 2), D // 2)]
            else:
                total[:, where] += out

        return [(0.8, functools.partial(one, half)) for half in range(2)]

    def attention(chance_, allowed_of):
        pairs_ = GROUP * HEADS // 2
        return [
            (1.2, functools.partial(attention_forward, qkv, mixed, chance_, allowed_of, first, 4))
            for first in range(0, pairs_, 4)
        ]

    def turn(source, slot, out):
        def body(c):
            turned[slot, aligned(c, PAIR), :] = source[:, aligned(c, PAIR)].T

        loop(D // PAIR, body)
        send_out(turned.at[slot, group_rows], out)

    outs = []

    def send_out(src, dst):
        copy = pltpu.make_async_copy(src, dst, out_sem.at[len(outs)])
        copy.start()
        outs.append(copy)

    group_rows = pl.ds(pl.multiple_of(z_at * (D // GROUP), D // GROUP), D // GROUP)

    def text_read(i):
        per = PAIR // ROWS
        return tok[i // per, aligned(lax.rem(i, per), ROWS), :]

    def text_allowed(i):
        row = seg_row[i].astype(jnp.float32)
        return seg_col[i] == row[0:1, :]

    def text_columns():
        for i in range(GROUP):
            row = seg_row[i].astype(jnp.float32)[0:1, :]
            seg_col[i] = jnp.broadcast_to(row, (PAIR, PAIR)).T

    def image_read(i):
        return padded[aligned(i, ROWS), :]

    def picture(axis):
        at = lax.broadcasted_iota(jnp.int32, (PAIR, PAIR), axis)
        number = at // (PAIR // 2)
        return jnp.where(lax.rem(at, PAIR // 2) < patches, number, number + 2)

    def image_allowed(i):
        return picture(0) == picture(1)

    def keep_mark():
        image = lax.broadcasted_iota(jnp.int32, (GROUP * 2, WORDS), 0)
        at = lax.broadcasted_iota(jnp.int32, (GROUP * 2, WORDS), 1)
        inside = (at // (PAIR // 2) == image) & (lax.rem(at, PAIR // 2) < patches)
        return jnp.where(inside, 1.0, 0.0)

    def text_pool():
        send_out(total.at[aligned(z_at, PAIR)], words_out)
        for i in range(GROUP):
            row = seg_row[i].astype(jnp.float32)[0:8, :]
            marks = jnp.where(row == lax.broadcasted_iota(jnp.int32, (8, PAIR), 0).astype(jnp.float32), 1.0, 0.0)
            marks_out[i] = marks
            marks_low = marks.astype(jnp.bfloat16)
            value = total[pl.ds(i * PAIR, PAIR), :]
            high = value.astype(jnp.bfloat16)
            rest = value - high.astype(jnp.float32)
            low = rest.astype(jnp.bfloat16)
            lower = (rest - low.astype(jnp.float32)).astype(jnp.bfloat16)
            sums = dot(
                jnp.concatenate([marks_low] * 3, axis=1), jnp.concatenate([high, low, lower], axis=0)
            )
            text_pool_out[pl.ds(i * 8, 8), :] = sums / jnp.sum(marks, axis=1, keepdims=True)

    def text_part(k):
        slot = k + PARTS
        if k == 0:
            return (
                [(0.3, text_columns)] + first_norm(text_read, tvec_ref) + project(slot, 0, (tvec_ref, 2))
                + [(0.8, lambda: turn(normed, 0, nt_out))]
            )
        if k == 1:
            return project(slot, 1, None)
        if k == 2:
            return (
                project(slot, 2, (tvec_ref, 3)) + [(0.1, lambda: send_out(qkv, qkv_out))]
                + attention(chance, text_allowed)
                + [(0.1, lambda: send_out(chance, chance_out)), (0.8, lambda: turn(mixed, 1, at_out))]
            )
        if k == 3:
            return attend(slot, text_read, tvec_ref) + [
                (0.1, lambda: send_out(middle, mid_out)), (0.8, lambda: turn(normed_two, 2, mt_out))
            ]
        if k < 8:
            return expand(slot, k - 4, tvec_ref, True)
        pieces = shrink(slot, k - 8, tvec_ref)
        if k == 10:
            pieces = pieces + [(1.0, end_pictures)]
        if k == 8:
            pieces = [(0.1, lambda: (send_out(active, act_out), send_out(slope, slope_out)))] + pieces
        if k == PARTS - 1:
            pieces = pieces + [(1.0, text_pool)]
        return pieces

    def pool_active(part):
        mark = keep_mark().astype(jnp.bfloat16)
        where = pl.ds(part * PART, PART)
        mean = dot(mark, active[:, where]) * (1.0 / patches)
        high = mean.astype(jnp.bfloat16)
        rest = mean - high.astype(jnp.float32)
        low = rest.astype(jnp.bfloat16)
        apool[0:8, where] = high.astype(jnp.float32)
        apool[8:16, where] = low.astype(jnp.float32)
        apool[16:24, where] = rest - low.astype(jnp.float32)

    def pool_shrink(slot, part):
        for half in range(2):
            where = pl.ds(half * (D // 2), D // 2)
            left = apool[:, pl.ds(part * PART, PART)].astype(jnp.bfloat16)
            out = dot_nt(left, weight_rows(slot, half))
            out = out[0:8] + out[8:16] + out[16:24]
            if part == 0:
                held_ = jnp.concatenate(
                    [
                        jnp.sum(middle[pl.ds(i * (PAIR // 2), patches), where], axis=0, keepdims=True)
                        for i in range(GROUP * 2)
                    ],
                    axis=0,
                )
                image_pool_out[:, where] = (
                    held_ * (1.0 / patches) + ivec_ref[:, pl.ds(7 * D + half * (D // 2), D // 2)] + out
                )
            else:
                image_pool_out[:, where] += out

    def image_part(k):
        slot = k
        if k == 0:
            return first_norm(image_read, ivec_ref) + project(slot, 0, (ivec_ref, 2))
        if k == 1:
            return project(slot, 1, None)
        if k == 2:
            return project(slot, 2, (ivec_ref, 3)) + attention(None, image_allowed)
        if k == 3:
            return attend(slot, image_read, ivec_ref)
        if k < 8:
            return expand(slot, k - 4, ivec_ref, False) + [(0.2, functools.partial(pool_active, k - 4))]
        pieces = [(0.5, functools.partial(pool_shrink, slot, k - 8))]
        if k == PARTS - 1:
            pieces.append((2.0, send_pictures))
        return pieces

    own_start(0)
    for copy in reversed(firsts):
        copy.start()
    for s in range(1, OWN_AHEAD):
        own_start(s)
    firsts[1].wait()
    images = GROUP * 2
    half_row = PAIR // 2
    for quarter_ in range(GROUP):
        row = lax.broadcasted_iota(jnp.int32, (PAIR, patches * images), 0) + quarter_ * PAIR
        source = lax.broadcasted_iota(jnp.int32, (PAIR, patches * images), 1)
        wanted = lax.rem(row, half_row) * images + row // half_row
        move = jnp.where((wanted == source) & (lax.rem(row, half_row) < patches), 1.0, 0.0).astype(jnp.bfloat16)
        padded[pl.ds(quarter_ * PAIR, PAIR), :] = dot(move, patches_in[...]).astype(jnp.bfloat16)
    pl.semaphore_wait(barrier, 5 - jnp.where(z_at == 0, 1, 0) - jnp.where(z_at == GROUP - 1, 1, 0))
    for s in range(AHEAD):
        begin(s)
    moves = [(step, move) for step in range(count + AT_C) for move in carry_on(step)]
    by_step = {}
    for step, move in moves:
        by_step.setdefault(step, []).append(move)
    timed = []
    for step in sorted(by_step):
        for i, move in enumerate(by_step[step]):
            timed.append((STEP_TIME * (step + i / len(by_step[step])), step, move))
    clock, done = 0.0, 0
    for s in range(count):
        pieces = image_part(s) if s < PARTS else text_part(s - PARTS)
        while done < len(timed) and timed[done][1] <= s + AT_C:
            clock = max(clock, timed[done][0])
            timed[done][2]()
            done += 1
        for cost, piece in pieces:
            piece()
            clock += cost
            while done < len(timed) and timed[done][0] <= clock:
                timed[done][2]()
                done += 1
    while done < len(timed):
        timed[done][2]()
        done += 1
    for copy in outs:
        copy.wait()
    for s in range(PARTS, count):
        store(s).wait()
    token_gone()
    for group in range(2):
        for up in range(2):
            for hop in range(GROUP - 1):
                unit = z_at - hop if up else z_at + hop
                pl.when((unit >= 0) & (unit < GROUP) & z_open[up])(
                    functools.partial(gone, all_size(group, 1, 2), z_send.at[group, up, hop], z_next[up])
                )
        gone(all_size(group, GROUP, 2), y_send.at[group], y_peers[0])
        gone(all_size(group, n_dp - 1, 1), x_send.at[group], x_peer)
        gone(all_size(group, n_dp, 3), c_send.at[group], c_peer)


def gather_and_forward(n_dp, n_rep, text_low, image_low, tokens, segments, pictures, text_vectors, image_vectors):
    own, columns = text_low.shape
    images, patches = pictures.shape[0], pictures.shape[1]
    lane_rows = own // LANES
    count = 2 * PARTS
    hbm, vmem = pl.BlockSpec(memory_space=pltpu.HBM), pl.BlockSpec(memory_space=pltpu.VMEM)
    low, full = jnp.bfloat16, jnp.float32
    shape = jax.ShapeDtypeStruct
    gathered = shape((PARTS, n_dp, LANES, lane_rows, PART), low)
    turned = shape((D // GROUP, WORDS), low)
    pairs = GROUP * HEADS // 2
    dma = pltpu.SemaphoreType.DMA
    outs = pl.pallas_call(
        functools.partial(forward_kernel, n_dp, n_rep, patches),
        out_shape=(
            gathered, shape((n_dp * n_rep, images, D), low), shape((PAIR, D), full), shape((8 * GROUP, D), full),
            shape((GROUP, 8, PAIR), full), shape((WORDS, 3 * D), low), shape((pairs, 2 * PAIR, PAIR), full),
            shape((WORDS, D), full), shape((WORDS, FF), full), shape((WORDS, FF), low), turned, turned, turned,
        ),
        in_specs=[hbm] * 4 + [vmem] * 3,
        out_specs=(hbm, vmem, hbm, vmem, vmem) + (hbm,) * 8,
        scratch_shapes=[
            pltpu.VMEM((PARTS, n_dp, LANES, lane_rows, PART), low),
            pltpu.VMEM((PARTS, n_dp, LANES, lane_rows, PART), low),
            pltpu.VMEM((GROUP, PAIR, D), low),
            pltpu.VMEM((GROUP, PAIR, PAIR), full),
            pltpu.VMEM((GROUP, 16, PAIR), low),
            pltpu.VMEM((WORDS, D), low),
            pltpu.VMEM((WORDS, 3 * D), low),
            pltpu.VMEM((WORDS, D), low),
            pltpu.VMEM((WORDS, D), full),
            pltpu.VMEM((WORDS, D), low),
            pltpu.VMEM((WORDS, FF), low),
            pltpu.VMEM((WORDS, FF), full),
            pltpu.VMEM((pairs, 2 * PAIR, PAIR), full),
            pltpu.VMEM((WORDS, D), full),
            pltpu.VMEM((WORDS, TILE), full),
            pltpu.VMEM((3, D, WORDS), low),
            pltpu.VMEM((24, FF), full),
            pltpu.VMEM((images, D), full),
            pltpu.VMEM((patches * images, D), low),
            pltpu.VMEM((WORDS, D), low),
            pltpu.VMEM((4, 3, lane_rows, PART), full),
            dma((2, 2, GROUP - 1)), dma((count, GROUP)), dma((2,)), dma((count,)),
            dma((2,)), dma((count,)), dma((2,)), dma((count,)),
            dma((2, 2, GROUP - 1)), dma((2, GROUP)), dma((2,)), dma((count,)), dma((PARTS,)), dma((12,)),
            dma((n_dp * n_rep - 1,)), dma((n_dp * n_rep - 1,)),
        ],
        compiler_params=pltpu.CompilerParams(collective_id=5, has_side_effects=True, vmem_limit_bytes=60 << 20),
        name="gather_and_forward",
    )(
        text_low.reshape(LANES, lane_rows, columns), image_low.reshape(LANES, lane_rows, columns), tokens,
        jnp.swapaxes(pictures, 0, 1).reshape(patches * images, D), segments,
        text_vectors.reshape(1, -1), image_vectors.reshape(1, -1),
    )
    return (outs[0].reshape(PARTS, D, PART),) + tuple(outs[1:])


def backward_kernel(
    n_dp, n_rep,
    wt_ref, nt_ref, at_ref, mt_ref, qkv_ref, chance_ref, mid_ref, slope_ref, act_ref, feed_ref,
    tpool_ref, pic_all, marks_ref, tok_ref, vec_ref, start_ref, flat_ref, moving_ref,
    m_out, input_out, loss_out, left_out, right_out, nvec_out, nvmom_out,
    weight, turned, qkv, chance, middle, slope, active, grad_hidden, grad_mix, low, low_mixed, wide, block, sent, got, sums, dy_ref, e2t, cap_all, rows_out, vector_out,
    factor, factor_rep, factor_dp, basis, tiles, tiles_rep, quarter, tiles_dp, everything,
    load_sem, send, recv, c_send, c_recv, m_sem, g_send, g_recv,
):
    n_inner = n_dp // GROUP
    d_at, r_at = lax.axis_index("dp"), lax.axis_index("rep")
    z_at, y_at = d_at // n_inner, lax.rem(d_at, n_inner)
    peer = (z_at * n_inner + 1 - y_at, r_at)
    own = D // n_dp
    share = 1.0 / GROUP

    barrier = pltpu.get_barrier_semaphore()
    devices = n_dp * n_rep
    near = n_inner * n_rep

    def near_peer(k):
        other = lax.rem(y_at * n_rep + r_at + k, near)
        return z_at * n_inner + other // n_rep, lax.rem(other, n_rep)

    rep_peers = [(d_at, lax.rem(r_at + k, n_rep)) for k in range(1, n_rep)]
    dp_peers = [(lax.rem(d_at + k, n_dp), r_at) for k in range(1, n_dp)]
    far_peers = [
        (lax.rem(z_at + k, GROUP) * n_inner + y, r_at) for k in range(1, GROUP) for y in range(n_inner)
    ]
    met = near - 1 + len(far_peers)
    for other in [near_peer(k) for k in range(1, near)] + far_peers:
        pl.semaphore_signal(barrier, inc=1, device_id=other, device_id_type=MESH)
    loads = {}

    def fetch(name, src, dst):
        copy = pltpu.make_async_copy(src, dst, load_sem.at[len(loads)])
        copy.start()
        loads[name] = copy

    def need(*names):
        for name in names:
            loads[name].wait()

    fetch("act", act_ref, active)
    fetch("feed", feed_ref, rows_out)
    for part in range(4):
        fetch(("w", 8 + part), wt_ref.at[8 + part], weight.at[8 + part])
    fetch("slope", slope_ref, slope)
    fetch("mt", mt_ref, turned.at[0])
    for part in range(4):
        fetch(("w", 4 + part), wt_ref.at[4 + part], weight.at[4 + part])
    fetch("mid", mid_ref, middle)
    fetch("at", at_ref, turned.at[1])
    fetch(("w", 3), wt_ref.at[3], weight.at[3])
    fetch("qkv", qkv_ref, qkv)
    fetch("chance", chance_ref, chance)
    fetch("nt", nt_ref, turned.at[2])
    for part in range(3):
        fetch(("w", part), wt_ref.at[part], weight.at[part])

    def exchange(s):
        return pltpu.make_async_remote_copy(
            src_ref=sent.at[s], dst_ref=got.at[s], send_sem=send.at[s], recv_sem=recv.at[s],
            device_id=peer, device_id_type=MESH,
        )

    own_rows = pl.ds(pl.multiple_of(y_at * own, own), own)
    other_rows = pl.ds(pl.multiple_of((1 - y_at) * own, own), own)

    def exchange_tile(s, where, slot):
        return pltpu.make_async_remote_copy(
            src_ref=sent.at[s, :, where], dst_ref=got.at[s, :, where], send_sem=send.at[slot], recv_sem=recv.at[slot],
            device_id=peer, device_id_type=MESH,
        )

    def exchange_heads(j):
        where = (pl.ds(0, 3), slice(None), pl.ds(j * PAIR, PAIR))
        return pltpu.make_async_remote_copy(
            src_ref=sent.at[where], dst_ref=got.at[where], send_sem=send.at[PARTS + j], recv_sem=recv.at[PARTS + j],
            device_id=peer, device_id_type=MESH,
        )

    def outer(s, left, right_of):
        def body(c):
            block[:, pl.ds(0, TILE)] = dot(left, right_of(c))
            where = pl.ds(pl.multiple_of(s * PART + c * TILE, TILE), TILE)
            rows_out[:, where] = rows_out[:, where] + block[own_rows, pl.ds(0, TILE)]
            sent[s, :, aligned(c, TILE)] = block[other_rows, pl.ds(0, TILE)].astype(jnp.bfloat16)
            exchange_tile(s, aligned(c, TILE), s).start()

        loop(PART // TILE, body, unroll=3)

    ones = jnp.ones((16, WORDS), jnp.bfloat16)

    def put(slot, values):
        for i in range(values.shape[1] // PAIR):
            vector_out[pl.ds(slot // PAIR + i, 1), :] = values[:, i * PAIR : (i + 1) * PAIR]

    def column_sums(values, slot, scale):
        put(slot, dot(ones, values)[0:1, :] * scale)


    def caption_copy(k):
        block_ = cap_all.at[:, y_at * n_rep + r_at]
        return pltpu.make_async_remote_copy(
            src_ref=block_, dst_ref=block_, send_sem=c_send.at[k - 1], recv_sem=c_recv.at[k - 1],
            device_id=near_peer(k), device_id_type=MESH,
        )

    def unit_of(values):
        return values * lax.rsqrt(jnp.sum(values * values, axis=-1, keepdims=True) + LAYER_EPS)

    def contrast():
        group_pairs = GROUP * 8
        for i in range(GROUP):
            cap_all[i, y_at * n_rep + r_at] = unit_of(tpool_ref[pl.ds(i * 8, 8), :]).astype(jnp.bfloat16)
        pl.semaphore_wait(barrier, met)
        for k in range(1, near):
            caption_copy(k).start()
        for k in range(1, near):
            caption_copy(k).wait_recv()
        pairs_ = devices * 8
        pics = pic_all[...].reshape(pairs_, D)
        caps = cap_all[...].reshape(pairs_, D)
        logits = dot_nt(caps, pics) * LOGIT_SCALE
        top = jnp.max(logits, axis=0, keepdims=True)
        image_log = top + jnp.log(jnp.sum(jnp.exp(logits - top), axis=0, keepdims=True))
        top = jnp.max(logits, axis=1, keepdims=True)
        caption_log = top + jnp.log(jnp.sum(jnp.exp(logits - top), axis=1, keepdims=True))
        row = lax.broadcasted_iota(jnp.int32, (pairs_, pairs_), 0)
        column = lax.broadcasted_iota(jnp.int32, (pairs_, pairs_), 1)
        matched = jnp.sum(jnp.where(row == column, logits, 0.0), axis=1, keepdims=True)
        loss = (jnp.sum(image_log) + jnp.sum(caption_log) - 2.0 * jnp.sum(matched)) / (2.0 * pairs_)
        loss_out[0, 0] = loss
        pooled = tpool_ref[...]
        squares = lax.rsqrt(jnp.sum(pooled * pooled, axis=-1, keepdims=True) + LAYER_EPS)
        own_low = (pooled * squares).astype(jnp.bfloat16)
        own_logits = dot_nt(own_low, pics) * LOGIT_SCALE
        top = jnp.max(own_logits, axis=1, keepdims=True)
        own_log = top + jnp.log(jnp.sum(jnp.exp(own_logits - top), axis=1, keepdims=True))
        local = lax.broadcasted_iota(jnp.int32, (group_pairs, pairs_), 0)
        column = lax.broadcasted_iota(jnp.int32, (group_pairs, pairs_), 1)
        wanted = (local // 8) * (near * 8) + (y_at * n_rep + r_at) * 8 + lax.rem(local, 8)
        pick = jnp.where(wanted == column, 1.0, 0.0)
        soft = ((jnp.exp(own_logits - own_log) - pick) * 0.5).astype(jnp.bfloat16)
        across = ((jnp.exp(own_logits - image_log) - pick) * 0.5).astype(jnp.bfloat16)
        grad = LOGIT_SCALE * (dot(soft, pics) + dot(across, pics))
        grad = squares * (
            grad - pooled * (squares * squares) * jnp.sum(grad * pooled, axis=-1, keepdims=True)
        )
        for i in range(GROUP):
            marks = marks_ref[i]
            part = grad[i * 8 : (i + 1) * 8, :] / jnp.sum(marks, axis=1, keepdims=True)
            high, rest = split_two(part)
            rest_low = (part - high.astype(jnp.float32) - rest.astype(jnp.float32)).astype(jnp.bfloat16)
            stacked = jnp.concatenate([high, rest, rest_low], axis=0)
            marks_low = marks.astype(jnp.bfloat16)
            marks_low = jnp.concatenate([marks_low, marks_low, marks_low], axis=0)
            rows = pl.ds(i * PAIR, PAIR)
            words = dot_tn(marks_low, stacked)
            dy_ref[rows, :] = words
            low[rows, :] = words.astype(jnp.bfloat16)
            e2t[:, rows] = dot_tn(stacked, marks_low).astype(jnp.bfloat16)

    contrast()
    need("act", "feed")
    for part in range(4):
        outer(8 + part, e2t[pl.ds(pl.multiple_of(z_at * (D // GROUP), D // GROUP), D // GROUP), :], lambda c: active[:, pl.ds(pl.multiple_of(part * PART + c * TILE, TILE), TILE)])
    need("slope")
    column_sums(low[...], 7 * D, share)
    for part in range(4):
        need(("w", 8 + part))

        def hidden_body(c):
            where = pl.ds(pl.multiple_of(part * PART + c * TILE, TILE), TILE)
            out = dot(low[...], weight[8 + part, :, aligned(c, TILE)])
            grad_hidden[:, where] = (out * slope[:, where]).astype(jnp.bfloat16)

        loop(PART // TILE, hidden_body, unroll=3)
    need("mt")
    for part in range(4):
        outer(
            4 + part, turned[0], lambda c: grad_hidden[:, pl.ds(pl.multiple_of(part * PART + c * TILE, TILE), TILE)]
        )
    for part in range(4):
        need(("w", 4 + part))
    for half in range(2):
        rows = pl.ds(half * (D // 2), D // 2)
        out = dot_nt(grad_hidden[:, pl.ds(0, PART)], weight[4, rows, :])
        for part in range(1, 4):
            out = out + dot_nt(grad_hidden[:, pl.ds(part * PART, PART)], weight[4 + part, rows, :])
        wide[:, rows] = out
    need("mid")

    def norm_back(value, grad, gain):
        center = value - jnp.mean(value, axis=-1, keepdims=True)
        scale = lax.rsqrt(jnp.mean(center * center, axis=-1, keepdims=True) + LAYER_EPS)
        unit = center * scale
        inner = grad * gain
        out = scale * (
            inner - jnp.mean(inner, axis=-1, keepdims=True) - unit * jnp.mean(inner * unit, axis=-1, keepdims=True)
        )
        return out, grad * unit

    def fold(values):
        return jnp.sum(values.reshape(ROWS // 8, 8, D), axis=0)

    sums[...] = jnp.zeros_like(sums)

    def second(i):
        rows = aligned(i, ROWS)
        grad = wide[rows, :]
        out, product = norm_back(middle[rows, :], grad, piece_of(vec_ref, 5))
        sums[0] += fold(product)
        sums[1] += fold(grad)
        out = out + dy_ref[rows, :]
        middle[rows, :] = out
        low[rows, :] = out.astype(jnp.bfloat16)

    loop(WORDS // ROWS, second, unroll=2)
    put(5 * D, jnp.sum(sums[0], axis=0, keepdims=True) * share)
    put(6 * D, jnp.sum(sums[1], axis=0, keepdims=True) * share)
    need("at", ("w", 3))
    outer(3, turned[1], lambda c: low[:, aligned(c, TILE)])
    for half in range(2):
        rows = pl.ds(half * (D // 2), D // 2)
        low_mixed[:, rows] = dot_nt(low[...], weight[3, rows, :]).astype(jnp.bfloat16)
    need("qkv", "chance")
    pairs = HEADS // 2

    def attention(j, i):
        at = i * pairs + j
        rows = pl.ds(i * PAIR, PAIR)
        q_cols = pl.ds(j * PAIR, PAIR)
        k_cols = pl.ds(D + j * PAIR, PAIR)
        v_cols = pl.ds(2 * D + j * PAIR, PAIR)
        query, key, value = qkv[rows, q_cols], qkv[rows, k_cols], qkv[rows, v_cols]
        grad = two_heads(low_mixed[rows, q_cols])
        weight_ = chance[at]
        grad_mix[rows, v_cols] = dot_tn(weight_.astype(jnp.bfloat16), grad).astype(jnp.bfloat16)
        back = dot_nt(grad, value)
        back = weight_ * (back - jnp.sum(weight_ * back, axis=-1, keepdims=True))
        back = back.astype(jnp.bfloat16)
        side = jnp.concatenate([back[:PAIR], back[PAIR:]], axis=1)
        grad_mix[rows, q_cols] = (dot(side, two_heads(key)) * SCORE_SCALE).astype(jnp.bfloat16)
        grad_mix[rows, k_cols] = (dot_tn(back, two_heads(query)) * SCORE_SCALE).astype(jnp.bfloat16)

    need("nt")
    for j in range(pairs):
        for i in range(GROUP):
            attention(j, i)
        for part in range(3):
            value = dot(turned[2], grad_mix[:, pl.ds(part * D + j * PAIR, PAIR)])
            block[:, pl.ds(part * PAIR, PAIR)] = value
            where = pl.ds(part * D + j * PAIR, PAIR)
            rows_out[:, where] = rows_out[:, where] + block[own_rows, pl.ds(part * PAIR, PAIR)]
            sent[part, :, pl.ds(j * PAIR, PAIR)] = block[other_rows, pl.ds(part * PAIR, PAIR)].astype(jnp.bfloat16)
            exchange_tile(part, pl.ds(j * PAIR, PAIR), PARTS + j).start()
    column_sums(low[...], 4 * D, share)
    column_sums(grad_hidden[...], 8 * D, share)
    column_sums(grad_mix[:, pl.ds(0, D)], 2 * D, share)
    column_sums(grad_mix[:, pl.ds(2 * D, D)], 3 * D, share)
    for part in range(3):
        need(("w", part))
    mine = aligned(z_at, PAIR)
    for half in range(2):
        rows = pl.ds(half * (D // 2), D // 2)
        out = dot_nt(grad_mix[mine, pl.ds(0, PART)], weight[0, rows, :])
        for part in range(1, 3):
            out = out + dot_nt(grad_mix[mine, pl.ds(part * PART, PART)], weight[part, rows, :])
        wide[pl.ds(0, PAIR), rows] = out
    sums[...] = jnp.zeros_like(sums)

    def first(i):
        rows = aligned(i, ROWS)
        grad = wide[rows, :]
        out, product = norm_back(tok_ref[rows, :].astype(jnp.float32), grad, piece_of(vec_ref, 0))
        sums[0] += fold(product)
        sums[1] += fold(grad)
        input_out[rows, :] = out + middle[pl.ds(pl.multiple_of(z_at * PAIR + i * ROWS, ROWS), ROWS), :]

    loop(PAIR // ROWS, first)
    put(0, jnp.sum(sums[0], axis=0, keepdims=True))
    put(D, jnp.sum(sums[1], axis=0, keepdims=True))

    bounds = matrix_bounds()
    rank = start_ref.shape[0]
    strip = n_dp * OWN_TILES
    sums_of = {}

    def take(s):
        where = pl.ds(s * PART, PART)
        rows_out[:, where] = rows_out[:, where] + got[s].astype(jnp.float32)
        high, rest = split_two(rows_out[:, where])
        start_high, start_low = split_two(start_ref[:, where])
        both = jnp.concatenate([start_high, start_low], axis=0)
        matrix = 0 if s < 3 else 1 if s == 3 else 2 if s < 8 else 3
        out, out_rest = dot_nt(both, high), dot_nt(both, rest)
        out = out[:rank] + out[rank:] + out_rest[:rank]
        sums_of[matrix] = out if matrix not in sums_of else sums_of[matrix] + out

    for s in (8, 9, 10, 11, 4, 5, 6, 7, 3):
        exchange(s).wait_recv()
        take(s)
    for j in range(pairs):
        exchange_heads(j).wait_recv()
    for s in range(3):
        take(s)
    m_copy = pltpu.make_async_copy(rows_out, m_out, m_sem)
    m_copy.start()
    factor[...] = jnp.zeros_like(factor)
    for matrix in range(4):
        factor[pl.ds(matrix * rank, rank), pl.ds(0, own)] = sums_of[matrix]

    def remote(phase, k, src, dst, other):
        return pltpu.make_async_remote_copy(
            src_ref=src, dst_ref=dst, send_sem=g_send.at[phase, k], recv_sem=g_recv.at[phase, k],
            device_id=other, device_id_type=MESH,
        )

    mine = pl.ds(r_at * strip + d_at * OWN_TILES, OWN_TILES)
    strip_mine = pl.ds(r_at * strip, strip)
    phases = [
        [remote(0, k, factor, factor_rep.at[k], other) for k, other in enumerate(rep_peers)],
        [remote(1, k, factor_dp.at[d_at], factor_dp.at[d_at], other) for k, other in enumerate(dp_peers)],
        [
            remote(2, k, tiles.at[pl.ds(other[1] * strip, strip)], tiles_rep.at[k], other)
            for k, other in enumerate(rep_peers)
        ],
        [
            remote(3, k, quarter.at[pl.ds(other[0] * OWN_TILES, OWN_TILES)], tiles_dp.at[k], other)
            for k, other in enumerate(dp_peers)
        ],
        [remote(4, k, everything.at[mine], everything.at[mine], other) for k, other in enumerate(dp_peers)],
        [remote(5, k, everything.at[strip_mine], everything.at[strip_mine], other) for k, other in enumerate(rep_peers)],
    ]

    def begin(phase):
        for copy in phases[phase]:
            copy.start()

    def arrived(phase):
        for copy in phases[phase]:
            copy.wait_recv()


    def send_strip(j):
        k = lax.rem(j - r_at + 2 * n_rep - 1, n_rep)
        copy = remote(2, k, tiles.at[pl.ds(j * strip, strip)], tiles_rep.at[k], (d_at, j))
        pl.when(r_at != j)(copy.start)

    columns = bounds[-1][1] // PAIR
    for i in range(EXTRA):
        tiles[columns + i] = vector_out[pl.ds(i * 8, 8), :]
    for i in range(columns + EXTRA, n_rep * strip):
        tiles[i] = jnp.zeros((8, PAIR), jnp.float32)
    begin(0)
    send_strip(n_rep - 1)
    arrived(0)
    summed = factor[...]
    for k in range(n_rep - 1):
        summed = summed + factor_rep[k]
    factor_dp[d_at] = summed
    begin(1)
    arrived(1)
    vectors = jnp.concatenate([factor_dp[i] for i in range(n_dp)], axis=1).reshape(4, rank, n_dp * PAIR)
    place = lax.broadcasted_iota(jnp.int32, (4, rank, 1), 1)
    for k in range(rank):
        vector = vectors[:, k : k + 1, :]
        size = jnp.sqrt(jnp.sum(vector * vector, axis=-1, keepdims=True)) + NORM_FLOOR
        vector = vector / size
        along = jnp.sum(vector * vectors, axis=-1, keepdims=True)
        vectors = jnp.where(
            place == k, jnp.broadcast_to(vector, vectors.shape),
            vectors - jnp.where(place > k, along, 0.0) * vector,
        )
    vectors = vectors.reshape(4 * rank, n_dp * PAIR)
    basis[...] = vectors
    left_out[...] = vectors
    basis_high, basis_low = split_two(basis[:, aligned(d_at, PAIR)][:, :own])
    for matrix, (first_col, after_col) in enumerate(bounds):
        where = slice(matrix * rank, (matrix + 1) * rank)
        both = jnp.concatenate([basis_high[where], basis_low[where]], axis=0)

        def project(c):
            high, low = split_two(rows_out[:, pl.ds(pl.multiple_of(first_col + c * TILE, TILE), TILE)])
            out = dot(both, high)
            out = out[:rank] + out[rank:] + dot(both, low)[:rank]
            at = first_col // PAIR + c * (TILE // PAIR)
            for half in range(TILE // PAIR):
                tiles[at + half] = out[:, half * PAIR : (half + 1) * PAIR]

        loop((after_col - first_col) // TILE, project, unroll=3)
        if matrix > 0:
            send_strip(matrix - 1)
    arrived(2)
    value = tiles[strip_mine]
    for k in range(n_rep - 1):
        value = value + tiles_rep[k]
    quarter[...] = value
    begin(3)
    arrived(3)
    value = quarter[pl.ds(d_at * OWN_TILES, OWN_TILES)]
    for k in range(n_dp - 1):
        value = value + tiles_dp[k]
    everything[mine] = value
    begin(4)
    arrived(4)
    begin(5)
    arrived(5)
    for i in range(columns):
        right_out[:, pl.ds(i * PAIR, PAIR)] = everything[i]
    for i in range(EXTRA):
        at = pl.ds(i * 8, 8)
        moved = MOMENTUM_DECAY * moving_ref[at, :] + everything[columns + i]
        nvmom_out[at, :] = moved
        nvec_out[at, :] = flat_ref[at, :] - STEP_RATE * moved
    m_copy.wait()
    for s in range(3, PARTS):
        exchange(s).wait_send()
    for j in range(pairs):
        exchange_heads(j).wait_send()
    for k in range(1, near):
        caption_copy(k).wait_send()
    for phase in phases:
        for copy in phase:
            copy.wait_send()


def backward(n_dp, n_rep, kept, pooled, pictures, marks, tokens, text_vectors, feedback_rows, start, moving):
    weights, qkv, chance, middle, slope, active, n_turned, a_turned, m_turned = kept
    own = feedback_rows.shape[0]
    hbm, vmem = pl.BlockSpec(memory_space=pltpu.HBM), pl.BlockSpec(memory_space=pltpu.VMEM)
    low, full = jnp.bfloat16, jnp.float32
    shape = jax.ShapeDtypeStruct
    dma = pltpu.SemaphoreType.DMA
    pairs = GROUP * HEADS // 2
    rank = start.shape[0]
    strip = n_dp * OWN_TILES
    flat = (12 * D // PAIR, PAIR)
    return pl.pallas_call(
        functools.partial(backward_kernel, n_dp, n_rep),
        out_shape=(
            shape(feedback_rows.shape, full), shape((PAIR, D), full), shape((1, 1), full),
            shape((4 * rank, n_dp * PAIR), full), shape(start.shape, full), shape(flat, full), shape(flat, full),
        ),
        in_specs=[hbm] * 10 + [vmem] * 8,
        out_specs=(hbm, vmem, pl.BlockSpec(memory_space=pltpu.SMEM)) + (vmem,) * 4,
        scratch_shapes=[
            pltpu.VMEM((PARTS, D, PART), low),
            pltpu.VMEM((3, D // GROUP, WORDS), low),
            pltpu.VMEM((WORDS, 3 * D), low),
            pltpu.VMEM((pairs, 2 * PAIR, PAIR), full),
            pltpu.VMEM((WORDS, D), full),
            pltpu.VMEM((WORDS, FF), full),
            pltpu.VMEM((WORDS, FF), low),
            pltpu.VMEM((WORDS, FF), low),
            pltpu.VMEM((WORDS, 3 * D), low),
            pltpu.VMEM((WORDS, D), low),
            pltpu.VMEM((WORDS, D), low),
            pltpu.VMEM((WORDS, D), full),
            pltpu.VMEM((D // GROUP, 3 * PAIR), full),
            pltpu.VMEM((PARTS, own, PART), low),
            pltpu.VMEM((PARTS, own, PART), low),
            pltpu.VMEM((2, 8, D), full),
            pltpu.VMEM((WORDS, D), full),
            pltpu.VMEM((D, WORDS), low),
            pltpu.VMEM((GROUP, n_dp * n_rep // GROUP, 8, D), low),
            pltpu.VMEM(feedback_rows.shape, full),
            pltpu.VMEM(flat, full),
            pltpu.VMEM((4 * rank, PAIR), full),
            pltpu.VMEM((n_rep - 1, 4 * rank, PAIR), full),
            pltpu.VMEM((n_dp, 4 * rank, PAIR), full),
            pltpu.VMEM((4 * rank, n_dp * PAIR), full),
            pltpu.VMEM((n_rep * strip, 8, PAIR), full),
            pltpu.VMEM((n_rep - 1, strip, 8, PAIR), full),
            pltpu.VMEM((strip, 8, PAIR), full),
            pltpu.VMEM((n_dp - 1, OWN_TILES, 8, PAIR), full),
            pltpu.VMEM((n_rep * strip, 8, PAIR), full),
            dma((24,)), dma((PARTS + 6,)), dma((PARTS + 6,)), dma((8,)), dma((8,)), dma,
            dma((6, n_dp - 1)), dma((6, n_dp - 1)),
        ],
        compiler_params=pltpu.CompilerParams(collective_id=6, has_side_effects=True, vmem_limit_bytes=60 << 20),
        name="backward",
    )(
        weights, n_turned, a_turned, m_turned, qkv, chance, middle, slope, active, feedback_rows,
        pooled, pictures, marks, tokens, text_vectors.reshape(1, -1), start, text_vectors.reshape(flat),
        moving.reshape(flat),
    )


EXTRA = 9
OWN_TILES = 3


def split_two(values):
    high = values.astype(jnp.bfloat16)
    return high, (values - high.astype(jnp.float32)).astype(jnp.bfloat16)


CHUNKS = 2


def finish_kernel(
    n_dp, n_rep,
    rows_ref, mom_ref, wts_ref, words_ref, input_ref, left_ref, right_ref, vec_ref, vmom_ref, loss_ref,
    feed_out, mom_out, wts_out, words_out, input_out, left_out, right_out, vec_out, vmom_out, loss_out,
    rows, mom, wts, change, through, load_sem, store_sem, pass_sem,
):
    own = rows.shape[0]
    piece = own // CHUNKS
    rank = right_ref.shape[0]

    def load(i, j):
        src, dst = ((rows_ref, rows), (mom_ref, mom), (wts_ref, wts))[j]
        span = pl.ds(i * piece, piece)
        return pltpu.make_async_copy(src.at[span], dst.at[span], load_sem.at[i, j])

    def store(i, j):
        src, dst = ((rows, feed_out), (mom, mom_out), (wts, wts_out))[j]
        span = pl.ds(i * piece, piece)
        return pltpu.make_async_copy(src.at[span], dst.at[span], store_sem.at[i, j])

    for i in range(CHUNKS):
        for j in range(3):
            load(i, j).start()
    taken = [
        pltpu.make_async_copy(src, through.at[i], pass_sem.at[i]) for i, src in enumerate((words_ref, input_ref))
    ]
    passed = [
        pltpu.make_async_copy(through.at[i], dst, pass_sem.at[2 + i]) for i, dst in enumerate((words_out, input_out))
    ]
    passed.append(pltpu.make_async_copy(right_ref, right_out, pass_sem.at[4]))
    for copy in taken:
        copy.start()
    passed[2].start()
    vec_out[...] = vec_ref[...]
    vmom_out[...] = vmom_ref[...]
    loss_out[0, 0] = loss_ref[0, 0]
    left_out[...] = jnp.concatenate([left_ref[:, i * PAIR : i * PAIR + own] for i in range(n_dp)], axis=1)
    basis_high, basis_low = split_two(left_ref[:, aligned(lax.axis_index("dp"), PAIR)][:, :own])
    for matrix, (first_col, after_col) in enumerate(matrix_bounds()):
        where = slice(matrix * rank, (matrix + 1) * rank)
        left = jnp.concatenate([basis_high[where], basis_high[where], basis_low[where]], axis=0)

        def approximate(c):
            cols = pl.ds(pl.multiple_of(first_col + c * PART, PART), PART)
            high, low = split_two(right_ref[:, cols])
            change[:, cols] = dot_tn(left, jnp.concatenate([high, low, high], axis=0))

        loop((after_col - first_col) // PART, approximate)
    for i in range(CHUNKS):
        for j in range(3):
            load(i, j).wait()

        def update(c):
            span, cols = pl.ds(i * piece, piece), aligned(c, PART)
            delta = change[span, cols]
            rows[span, cols] = rows[span, cols] - delta * (1.0 / n_rep)
            moved = MOMENTUM_DECAY * mom[span, cols] + delta
            mom[span, cols] = moved
            wts[span, cols] = wts[span, cols] - STEP_RATE * moved

        loop(rows.shape[1] // PART, update)
        for j in range(3):
            store(i, j).start()
        if i == 0:
            for k, copy in enumerate(taken):
                copy.wait()
                passed[k].start()
    for copy in passed:
        copy.wait()
    for i in range(CHUNKS):
        for j in range(3):
            store(i, j).wait()


def finish(n_dp, n_rep, rows, momentum, weights, left, right, words, grad_inputs, vectors, vector_momentum, loss):
    own, columns = rows.shape
    hbm, vmem = pl.BlockSpec(memory_space=pltpu.HBM), pl.BlockSpec(memory_space=pltpu.VMEM)
    smem = pl.BlockSpec(memory_space=pltpu.SMEM)
    full = jnp.float32
    shape = jax.ShapeDtypeStruct
    dma = pltpu.SemaphoreType.DMA
    big = shape(rows.shape, full)
    return pl.pallas_call(
        functools.partial(finish_kernel, n_dp, n_rep),
        out_shape=(
            big, big, big, shape(words.shape, full), shape(grad_inputs.shape, full),
            shape((left.shape[0], n_dp * own), full), shape(right.shape, full), shape(vectors.shape, full),
            shape(vectors.shape, full), shape((1, 1), full),
        ),
        in_specs=[hbm] * 5 + [vmem] * 4 + [smem],
        out_specs=(hbm,) * 5 + (vmem, hbm, vmem, vmem, smem),
        scratch_shapes=[pltpu.VMEM(rows.shape, full)] * 4
        + [pltpu.VMEM((2,) + words.shape, full), dma((CHUNKS, 3)), dma((CHUNKS, 3)), dma((5,))],
        compiler_params=pltpu.CompilerParams(vmem_limit_bytes=60 << 20),
        name="finish",
    )(rows, momentum, weights, words, grad_inputs, left, right, vectors, vector_momentum, loss)


def peer_at(offset, n_dp, n_rep):
    me = lax.axis_index("dp") * n_rep + lax.axis_index("rep")
    other = lax.rem(me + offset, n_dp * n_rep)
    return other, (other // n_rep, lax.rem(other, n_rep))


def meet(n_dp, n_rep):
    total = n_dp * n_rep
    barrier = pltpu.get_barrier_semaphore()

    def hello(offset, carry):
        _, peer = peer_at(offset, n_dp, n_rep)
        pl.semaphore_signal(barrier, inc=1, device_id=peer, device_id_type=MESH)
        return carry

    lax.fori_loop(1, total, hello, 0)
    pl.semaphore_wait(barrier, total - 1)


def spread_kernel(n_dp, n_rep, mine_ref, all_ref, send, recv, own_sem):
    total = n_dp * n_rep
    me = lax.axis_index("dp") * n_rep + lax.axis_index("rep")
    own = pltpu.make_async_copy(mine_ref, all_ref.at[me], own_sem)
    own.start()
    meet(n_dp, n_rep)

    def copy(offset):
        _, peer = peer_at(offset, n_dp, n_rep)
        return pltpu.make_async_remote_copy(
            src_ref=mine_ref, dst_ref=all_ref.at[me], send_sem=send.at[offset - 1],
            recv_sem=recv.at[offset - 1], device_id=peer, device_id_type=MESH,
        )

    def begin(offset, carry):
        copy(offset).start()
        return carry

    def finish(offset, carry):
        copy(offset).wait()
        return carry

    lax.fori_loop(1, total, begin, 0)
    own.wait()
    lax.fori_loop(1, total, finish, 0)


def spread(mine, n_dp, n_rep, collective, name):
    total = n_dp * n_rep
    vmem = pl.BlockSpec(memory_space=pltpu.VMEM)
    dma = pltpu.SemaphoreType.DMA
    return pl.pallas_call(
        functools.partial(spread_kernel, n_dp, n_rep),
        out_shape=jax.ShapeDtypeStruct((total,) + mine.shape, mine.dtype),
        in_specs=[vmem],
        out_specs=vmem,
        scratch_shapes=[dma((total - 1,)), dma((total - 1,)), dma],
        compiler_params=pltpu.CompilerParams(
            collective_id=collective, has_side_effects=True, vmem_limit_bytes=48 << 20
        ),
        name=name,
    )(mine)


def total_kernel(n_dp, n_rep, mine_ref, out_ref, parts, sums, send, recv, send_two, recv_two):
    total = n_dp * n_rep
    me = lax.axis_index("dp") * n_rep + lax.axis_index("rep")
    meet(n_dp, n_rep)

    def scatter(offset):
        other, peer = peer_at(offset, n_dp, n_rep)
        return pltpu.make_async_remote_copy(
            src_ref=mine_ref.at[other], dst_ref=parts.at[offset - 1], send_sem=send.at[offset - 1],
            recv_sem=recv.at[offset - 1], device_id=peer, device_id_type=MESH,
        )

    def share(offset):
        _, peer = peer_at(offset, n_dp, n_rep)
        return pltpu.make_async_remote_copy(
            src_ref=sums, dst_ref=out_ref.at[me], send_sem=send_two.at[offset - 1],
            recv_sem=recv_two.at[offset - 1], device_id=peer, device_id_type=MESH,
        )

    def start_scatter(offset, carry):
        scatter(offset).start()
        return carry

    def add(offset, carry):
        scatter(offset).wait_recv()
        return carry + parts[offset - 1]

    def start_share(offset, carry):
        share(offset).start()
        return carry

    def finish(offset, carry):
        scatter(offset).wait_send()
        share(offset).wait()
        return carry

    lax.fori_loop(1, total, start_scatter, 0)
    result = lax.fori_loop(1, total, add, mine_ref[me])
    sums[...] = result
    lax.fori_loop(1, total, start_share, 0)
    out_ref[me] = result
    lax.fori_loop(1, total, finish, 0)


def total_over_all(flat, n_dp, n_rep, collective, name):
    total = n_dp * n_rep
    count = flat.shape[0]
    chunk = -(-count // (total * 1024)) * 1024
    padded = jnp.pad(flat, (0, total * chunk - count)).reshape(total, chunk // 128, 128)
    vmem = pl.BlockSpec(memory_space=pltpu.VMEM)
    dma = pltpu.SemaphoreType.DMA
    summed = pl.pallas_call(
        functools.partial(total_kernel, n_dp, n_rep),
        out_shape=jax.ShapeDtypeStruct(padded.shape, padded.dtype),
        in_specs=[vmem],
        out_specs=vmem,
        scratch_shapes=[
            pltpu.VMEM((total - 1,) + padded.shape[1:], padded.dtype),
            pltpu.VMEM(padded.shape[1:], padded.dtype),
            dma((total - 1,)), dma((total - 1,)), dma((total - 1,)), dma((total - 1,)),
        ],
        compiler_params=pltpu.CompilerParams(
            collective_id=collective, has_side_effects=True, vmem_limit_bytes=48 << 20
        ),
        name=name,
    )(padded)
    return summed.reshape(-1)[:count]


def masked_scores(query_heads, key_heads, allowed):
    scores = (
        jnp.einsum("rshd,rthd->rhst", query_heads, key_heads, preferred_element_type=jnp.float32)
        * SCORE_SCALE
    )
    return jnp.where(allowed[:, None], scores, MASKED)


def block_forward(inputs, allowed, weights, vector_pieces, pooled_only):
    (
        gain_one, shift_one, bias_query, bias_value, bias_out,
        gain_two, shift_two, bias_shrink, bias_expand,
    ) = vector_pieces
    row_count, seq_tokens = (inputs.shape[0], inputs.shape[1])
    normed = layer_norm(inputs, gain_one, shift_one).astype(jnp.bfloat16)
    mixing = jnp.einsum("rsd,dc->rsc", normed, weights[:, : 3 * D], preferred_element_type=jnp.float32)
    mixing = mixing + jnp.concatenate([bias_query, jnp.zeros_like(bias_query), bias_value])
    head_parts = mixing.astype(jnp.bfloat16).reshape(row_count, seq_tokens, 3, HEADS, HEAD_DIM)
    query_heads, key_heads, value_heads = (head_parts[:, :, 0], head_parts[:, :, 1], head_parts[:, :, 2])
    scores = masked_scores(query_heads, key_heads, allowed)
    highest = jnp.max(scores, axis=-1, keepdims=True)
    log_total = highest + jnp.log(jnp.sum(jnp.exp(scores - highest), axis=-1, keepdims=True))
    attention = jnp.exp(scores - log_total).astype(jnp.bfloat16)
    mixed_heads = jnp.einsum("rhst,rthd->rshd", attention, value_heads, preferred_element_type=jnp.float32)
    mixed_heads = mixed_heads.reshape(row_count, seq_tokens, D).astype(jnp.bfloat16)
    attended = (
        jnp.einsum("rsd,de->rse", mixed_heads, weights[:, 3 * D : 4 * D], preferred_element_type=jnp.float32)
        + bias_out
    )
    middle = inputs + attended
    normed_two = layer_norm(middle, gain_two, shift_two).astype(jnp.bfloat16)
    hidden = (
        jnp.einsum("rsd,df->rsf", normed_two, weights[:, 4 * D : 4 * D + FF], preferred_element_type=jnp.float32)
        + bias_expand
    )
    active = jax.nn.gelu(hidden, approximate=False).astype(jnp.bfloat16)
    shrink = weights[:, 4 * D + FF :]
    if pooled_only:
        mean_active = jnp.mean(active.astype(jnp.float32), axis=1)
        high = mean_active.astype(jnp.bfloat16)
        rest = mean_active - high.astype(jnp.float32)
        low = rest.astype(jnp.bfloat16)
        lower = (rest - low.astype(jnp.float32)).astype(jnp.bfloat16)
        stacked = jnp.concatenate([high, low, lower], axis=0)
        shrunk = jnp.einsum("pf,df->pd", stacked, shrink, preferred_element_type=jnp.float32)
        shrunk = jnp.sum(shrunk.reshape(3, row_count, D), axis=0)
        return jnp.mean(middle, axis=1) + shrunk + bias_shrink
    shrunk = jnp.einsum("rsf,df->rsd", active, shrink, preferred_element_type=jnp.float32) + bias_shrink
    kept = (normed, query_heads, key_heads, value_heads, log_total, mixed_heads, middle, normed_two, hidden, active)
    return (middle + shrunk, kept)


def token_sum(values_low):
    return jnp.sum(values_low.astype(jnp.float32).reshape(-1, values_low.shape[-1]), axis=0)


def block_backward(inputs, allowed, weights, vector_pieces, forward_kept, grad_out, own_group, own_count):
    (gain_one, shift_one, _, _, _, gain_two, shift_two, _, _) = vector_pieces
    (normed, query_heads, key_heads, value_heads, log_total, mixed_heads, middle, normed_two, hidden, active) = forward_kept
    row_count, seq_tokens = (inputs.shape[0], inputs.shape[1])
    grad_shrunk = grad_out.astype(jnp.bfloat16)
    grad_active = jnp.einsum("rsd,df->rsf", grad_shrunk, weights[:, 4 * D + FF :], preferred_element_type=jnp.float32)
    _, gelu_back = jax.vjp(lambda before_gelu: jax.nn.gelu(before_gelu, approximate=False), hidden)
    grad_hidden = gelu_back(grad_active)[0].astype(jnp.bfloat16)
    grad_normed_two = jnp.einsum(
        "rsf,df->rsd", grad_hidden, weights[:, 4 * D : 4 * D + FF], preferred_element_type=jnp.float32
    )
    _, norm_two_back = jax.vjp(layer_norm, middle, gain_two, shift_two)
    grad_middle, grad_gain_two, grad_shift_two = norm_two_back(grad_normed_two)
    grad_middle = grad_middle + grad_out
    grad_attended = grad_middle.astype(jnp.bfloat16)
    grad_mixed = jnp.einsum("rse,de->rsd", grad_attended, weights[:, 3 * D : 4 * D], preferred_element_type=jnp.float32)
    grad_mixed = grad_mixed.astype(jnp.bfloat16).reshape(row_count, seq_tokens, HEADS, HEAD_DIM)
    attention = jnp.exp(masked_scores(query_heads, key_heads, allowed) - log_total)
    grad_values = jnp.einsum("rhst,rshd->rthd", attention.astype(jnp.bfloat16), grad_mixed, preferred_element_type=jnp.float32)
    grad_attention = jnp.einsum("rshd,rthd->rhst", grad_mixed, value_heads, preferred_element_type=jnp.float32)
    grad_scores = attention * (grad_attention - jnp.sum(attention * grad_attention, axis=-1, keepdims=True))
    grad_scores = grad_scores.astype(jnp.bfloat16)
    grad_query = jnp.einsum("rhst,rthd->rshd", grad_scores, key_heads, preferred_element_type=jnp.float32) * SCORE_SCALE
    grad_keys = jnp.einsum("rhst,rshd->rthd", grad_scores, query_heads, preferred_element_type=jnp.float32) * SCORE_SCALE
    grad_mixing = (
        jnp.stack([grad_query, grad_keys, grad_values], axis=2).reshape(row_count, seq_tokens, 3 * D).astype(jnp.bfloat16)
    )

    def mine(values):
        return lax.dynamic_slice_in_dim(values, own_group * own_count, own_count, 0)

    grad_normed = jnp.einsum("rsc,dc->rsd", mine(grad_mixing), weights[:, : 3 * D], preferred_element_type=jnp.float32)
    _, norm_one_back = jax.vjp(layer_norm, mine(inputs), gain_one, shift_one)
    grad_inputs, grad_gain_one, grad_shift_one = norm_one_back(grad_normed)
    grad_inputs = grad_inputs + mine(grad_middle)
    share = 1.0 / GROUP
    vector_grad = jnp.concatenate(
        [
            grad_gain_one, grad_shift_one,
            share * token_sum(grad_mixing[..., :D]), share * token_sum(grad_mixing[..., 2 * D :]),
            share * token_sum(grad_attended), share * grad_gain_two, share * grad_shift_two,
            share * token_sum(grad_shrunk), share * token_sum(grad_hidden),
        ]
    )
    tokens = row_count * seq_tokens
    outer_terms = (
        (normed.reshape(tokens, D), grad_mixing.reshape(tokens, 3 * D)),
        (mixed_heads.reshape(tokens, D), grad_attended.reshape(tokens, D)),
        (normed_two.reshape(tokens, D), grad_hidden.reshape(tokens, FF)),
        (grad_shrunk.reshape(tokens, D), active.reshape(tokens, FF)),
    )
    return (grad_inputs, vector_grad, outer_terms)


def orthonormal(stacked):
    waiting = [stacked[:, column_id] for column_id in range(stacked.shape[1])]
    finished = []
    while waiting:
        vector = waiting.pop(0)
        vector = vector / (jnp.sqrt(jnp.sum(vector * vector, axis=-1, keepdims=True)) + NORM_FLOOR)
        finished.append(vector)
        if waiting:
            later = jnp.stack(waiting, axis=1)
            later = later - jnp.sum(vector[:, None] * later, axis=-1, keepdims=True) * vector[:, None]
            waiting = [later[:, i] for i in range(later.shape[1])]
    return jnp.stack(finished, axis=1)


def rows_factor(start_part, row_block):
    return jnp.einsum("kc,dc->kd", start_part, row_block, precision=PRECISE)


def per_device(
    image_tokens, image_weights, image_vectors, text_tokens, segments, text_weights,
    text_vectors, momentum, vector_momentum, error_feedback, start_factors,
):
    n_rep, n_dp = lax.axis_size("rep"), lax.axis_size("dp")
    n_inner = n_dp // GROUP
    total = n_rep * n_dp
    device_pairs, patches = image_tokens.shape[0], image_tokens.shape[1]
    text_rows, seq_tokens = text_tokens.shape[0], text_tokens.shape[1]
    pair_total = device_pairs * total
    own_rows = text_weights.shape[0]
    d_at, r_at = lax.axis_index("dp"), lax.axis_index("rep")
    z_at, y_at = d_at // n_inner, d_at % n_inner
    row_start = d_at * own_rows
    factor_rank = start_factors.shape[0]
    bounds = matrix_bounds()
    tokens = text_tokens.reshape(text_rows * seq_tokens, D)
    feedback_rows = error_feedback[0]
    fused = (
        own_rows % (16 * LANES) == 0 and n_inner == 2 and n_rep == 4 and device_pairs == 8
        and text_rows * seq_tokens == PAIR and 2 * seq_tokens == PAIR and 2 * patches <= PAIR
        and n_dp == 8 and factor_rank == 8
    )
    if fused:
        outs = gather_and_forward(
            n_dp, n_rep, text_weights, image_weights, tokens, segments, image_tokens, text_vectors, image_vectors
        )
        pictures, words, pooled, marks = outs[1:5]
        kept = (outs[0],) + tuple(outs[5:])
        worker_rows, grad_inputs, loss, left_basis, new_right, new_vectors, new_vector_momentum = backward(
            n_dp, n_rep, kept, pooled, pictures, marks, tokens, text_vectors, feedback_rows, start_factors,
            vector_momentum,
        )
        (
            new_feedback, new_momentum, new_weights, words, grad_inputs, left_basis, new_right,
            new_vectors, new_vector_momentum, loss,
        ) = finish(
            n_dp, n_rep, worker_rows, momentum, text_weights, left_basis, new_right, words, grad_inputs,
            new_vectors, new_vector_momentum, loss,
        )
        return (
            loss.reshape(()), words.reshape(text_rows, seq_tokens, D), grad_inputs.reshape(text_rows, seq_tokens, D),
            new_weights, new_momentum, new_feedback[None], new_vectors.reshape(-1), new_vector_momentum.reshape(-1),
            left_basis, new_right,
        )
    text_low, frozen, token_group, segment_group = gather_weights(
        n_dp, text_weights.astype(jnp.bfloat16), image_weights, tokens, segments
    )
    text_low, frozen = text_low.reshape(D, -1), frozen.reshape(D, -1)
    full_mask = jnp.zeros((device_pairs, patches, patches), jnp.int32) == 0
    image_pooled = block_forward(
        image_tokens.astype(jnp.float32), full_mask, frozen, vector_parts(image_vectors), True
    )
    group_rows = GROUP * text_rows
    text_float = token_group.reshape(group_rows, seq_tokens, D).astype(jnp.float32)
    segment_all = segment_group.reshape(group_rows, seq_tokens)
    allowed = segment_all[:, :, None] == segment_all[:, None, :]
    vector_pieces = vector_parts(text_vectors)
    group_output, forward_kept = block_forward(text_float, allowed, text_low, vector_pieces, False)
    text_output = lax.dynamic_slice_in_dim(group_output, z_at * text_rows, text_rows, 0)
    caption_marks = (
        segment_all[:, None, :] == jnp.arange(PER_ROW, dtype=jnp.int32)[None, :, None]
    ).astype(jnp.float32)
    counts = jnp.sum(caption_marks, axis=-1, keepdims=True)
    pooled = (jnp.einsum("rks,rsd->rkd", caption_marks, group_output, precision=PRECISE) / counts).reshape(-1, D)
    image_emb = unit_rows(image_pooled).astype(jnp.bfloat16)
    text_norm, embed_back = jax.vjp(unit_rows, pooled)
    text_emb = text_norm.astype(jnp.bfloat16)
    own_emb = lax.dynamic_slice_in_dim(text_emb, z_at * device_pairs, device_pairs, 0)
    embeddings = spread(jnp.concatenate([image_emb, own_emb], axis=0), n_dp, n_rep, 2, "spread_embeddings")
    image_all = embeddings[:, :device_pairs].reshape(pair_total, D)
    text_all = embeddings[:, device_pairs:].reshape(pair_total, D)
    own_pairs = (
        ((jnp.arange(GROUP, dtype=jnp.int32) * n_inner + y_at) * n_rep + r_at)[:, None] * device_pairs
        + jnp.arange(device_pairs, dtype=jnp.int32)[None, :]
    ).reshape(-1)
    logits = LOGIT_SCALE * jnp.einsum("pd,bd->pb", image_all, text_all, preferred_element_type=jnp.float32)
    image_top = jnp.max(logits, axis=1)
    image_log_total = image_top + jnp.log(jnp.sum(jnp.exp(logits - image_top[:, None]), axis=1))
    caption_top = jnp.max(logits, axis=0)
    caption_log_total = caption_top + jnp.log(jnp.sum(jnp.exp(logits - caption_top[None, :]), axis=0))
    pair_ids = jnp.arange(pair_total, dtype=jnp.int32)
    matched = jnp.sum(jnp.where(pair_ids[:, None] == pair_ids[None, :], logits, 0.0), axis=1)
    loss_total = (jnp.sum(image_log_total - matched) + jnp.sum(caption_log_total - matched)) / (2.0 * pair_total)
    diagonal_pick = (pair_ids[None, :] == own_pairs[:, None]).astype(jnp.float32)
    text_logits = LOGIT_SCALE * jnp.einsum("pd,bd->pb", text_emb, image_all, preferred_element_type=jnp.float32)
    text_top = jnp.max(text_logits, axis=1, keepdims=True)
    text_log_total = text_top + jnp.log(jnp.sum(jnp.exp(text_logits - text_top), axis=1, keepdims=True))
    text_soft = ((jnp.exp(text_logits - text_log_total) - diagonal_pick) * 0.5).astype(jnp.bfloat16)
    column_soft = ((jnp.exp(text_logits - image_log_total[None, :]) - diagonal_pick) * 0.5).astype(jnp.bfloat16)
    grad_text = LOGIT_SCALE * (
        jnp.einsum("pb,bd->pd", text_soft, image_all, preferred_element_type=jnp.float32)
        + jnp.einsum("pb,bd->pd", column_soft, image_all, preferred_element_type=jnp.float32)
    )
    grad_pooled = embed_back(grad_text)[0]
    grad_pooled = grad_pooled.reshape(-1, PER_ROW, D) / counts
    grad_out = jnp.einsum("rks,rkd->rsd", caption_marks, grad_pooled, precision=PRECISE)
    grad_inputs, vector_grad, outer_terms = block_backward(
        text_float, allowed, text_low, vector_pieces, forward_kept, grad_out, z_at, text_rows
    )
    group_width = n_inner * own_rows
    worker_blocks = []
    for (left_side, right_side), (first_col, after_col) in zip(outer_terms, bounds):
        left_cut = lax.dynamic_slice_in_dim(left_side, z_at * group_width, group_width, 1)
        block = jnp.einsum("tc,tk->ck", left_cut, right_side, preferred_element_type=jnp.float32)
        mine = lax.dynamic_slice_in_dim(block, y_at * own_rows, own_rows, 0)
        for k in range(1, n_inner):
            target = lax.rem(y_at + k, n_inner)
            outgoing = lax.dynamic_slice_in_dim(block, target * own_rows, own_rows, 0).astype(jnp.bfloat16)
            pairs = [
                (z * n_inner + y, z * n_inner + (y + k) % n_inner) for z in range(GROUP) for y in range(n_inner)
            ]
            mine = mine + lax.ppermute(outgoing, "dp", pairs).astype(jnp.float32)
        worker_blocks.append(mine + feedback_rows[:, first_col:after_col])
    factor_rows = jnp.concatenate(
        [
            rows_factor(start_factors[:, first_col:after_col], rows)
            for rows, (first_col, after_col) in zip(worker_blocks, bounds)
        ],
        axis=0,
    )
    gathered_rows = spread(factor_rows, n_dp, n_rep, 3, "spread_factors")
    factor = jnp.sum(gathered_rows.reshape(n_dp, n_rep, 4 * factor_rank, own_rows), axis=1)
    factor = jnp.swapaxes(factor, 0, 1).reshape(4, factor_rank, D)
    left_basis = orthonormal(factor).reshape(4 * factor_rank, D)
    basis_rows = lax.dynamic_slice_in_dim(left_basis, row_start, own_rows, 1)
    basis_parts = [basis_rows[i * factor_rank : (i + 1) * factor_rank] for i in range(4)]
    right_part = jnp.concatenate(
        [jnp.einsum("kd,dc->kc", part, rows, precision=PRECISE) for part, rows in zip(basis_parts, worker_blocks)],
        axis=1,
    )
    summed = total_over_all(
        jnp.concatenate([right_part.reshape(-1), vector_grad]), n_dp, n_rep, 4, "total_right"
    )
    new_right = summed[: right_part.size].reshape(right_part.shape)
    vector_total = summed[right_part.size :]
    approximation = jnp.concatenate(
        [
            jnp.einsum("kd,kc->dc", part, new_right[:, first_col:after_col], precision=PRECISE)
            for part, (first_col, after_col) in zip(basis_parts, bounds)
        ],
        axis=1,
    )
    worker_rows = jnp.concatenate(worker_blocks, axis=1)
    new_feedback = (worker_rows - approximation / n_rep)[None]
    new_momentum = MOMENTUM_DECAY * momentum + approximation
    new_weights = text_weights - STEP_RATE * new_momentum
    new_vector_momentum = MOMENTUM_DECAY * vector_momentum + vector_total
    new_vectors = text_vectors - STEP_RATE * new_vector_momentum
    return (
        loss_total, text_output, grad_inputs, new_weights, new_momentum, new_feedback,
        new_vectors, new_vector_momentum, left_basis, new_right,
    )


def solution(mesh):
    placed = (
        P(("dp", "rep"), None, None), P("dp", None), P(), P(("dp", "rep"), None, None), P(("dp", "rep"), None),
        P("dp", None), P(), P("dp", None), P(), P("rep", "dp", None), P(),
    )
    return jax.shard_map(
        per_device,
        mesh=mesh,
        in_specs=placed,
        out_specs=(
            P(), P(("dp", "rep"), None, None), P(("dp", "rep"), None, None), P("dp", None), P("dp", None),
            P("rep", "dp", None), P(), P(), P(), P(),
        ),
        check_vma=False,
    )
```

```python
import functools

import jax
import jax.numpy as jnp
from jax import lax
from jax.experimental import pallas as pl
from jax.experimental.pallas import tpu as pltpu
from jax.sharding import PartitionSpec as P

D = 768
FF = 3072
HEADS = 12
HEAD_DIM = 64
PER_ROW = 4
GROUP = 4
SECTION = 3072
LANE_COLS = 512

PRECISE = lax.Precision.HIGHEST
LAYER_EPS = 1e-06
SCORE_SCALE = 0.125
LOGIT_SCALE = 50.0
MOMENTUM_DECAY = 0.9
STEP_RATE = 0.08
NORM_FLOOR = 1e-08
MASKED = -1e30
MESH = pl.DeviceIdType.MESH


def layer_norm(values, layer_gain, layer_shift):
    center = values - jnp.mean(values, axis=-1, keepdims=True)
    spread = jnp.mean(center * center, axis=-1, keepdims=True)
    return center * lax.rsqrt(spread + LAYER_EPS) * layer_gain + layer_shift


def unit_rows(values):
    return values * lax.rsqrt(jnp.sum(values * values, axis=-1, keepdims=True) + LAYER_EPS)


def vector_parts(vectors):
    pieces = [vectors[position * D : (position + 1) * D] for position in range(8)]
    return pieces + [vectors[8 * D :]]


def matrix_bounds():
    return ((0, 3 * D), (3 * D, 4 * D), (4 * D, 4 * D + FF), (4 * D + FF, 4 * D + 2 * FF))


def gather_kernel(
    n_dp, text_ref, image_ref, tok_ref, seg_ref, wt_ref, wi_ref, tok_out, seg_out,
    z_send, z_recv, y_send, y_recv, x_send, x_recv, c_send, c_recv, t_send, t_recv, t_own, own_sem,
):
    n_inner = n_dp // GROUP
    d_at, r_at = lax.axis_index("dp"), lax.axis_index("rep")
    z_at, y_at = d_at // n_inner, d_at % n_inner
    x_at, c_at = r_at // 2, r_at % 2
    z_peers = [(lax.rem(z_at + k, GROUP) * n_inner + y_at, r_at) for k in range(1, GROUP)]
    z_from = [lax.rem(z_at + GROUP - k, GROUP) for k in range(1, GROUP)]
    y_peers = [(z_at * n_inner + lax.rem(y_at + k, n_inner), r_at) for k in range(1, n_inner)]
    y_from = [lax.rem(y_at + n_inner - k, n_inner) for k in range(1, n_inner)]
    x_peer = (d_at, (1 - x_at) * 2 + c_at)
    c_peer = (d_at, x_at * 2 + 1 - c_at)

    barrier = pltpu.get_barrier_semaphore()
    everyone = z_peers + y_peers + [x_peer, c_peer]
    for peer in everyone:
        pl.semaphore_signal(barrier, inc=1, device_id=peer, device_id_type=MESH)
    pl.semaphore_wait(barrier, len(everyone))

    def shard_of(z, y):
        return z * n_inner + y

    sections = [(image_ref, wi_ref, 0), (text_ref, wt_ref, 0), (image_ref, wi_ref, 1),
                (text_ref, wt_ref, 1), (image_ref, wi_ref, 2), (text_ref, wt_ref, 2)]

    def cols(section, lane):
        start = sections[section][2] * SECTION + lane * LANE_COLS
        return pl.ds(pl.multiple_of(start, 128), LANE_COLS)

    lane_both = c_at
    lane_mine = 2 + x_at * 2 + c_at
    lane_theirs = 2 + (1 - x_at) * 2 + c_at
    lanes = (lane_both, lane_mine)

    locals_ = [
        pltpu.make_async_copy(tok_ref, tok_out.at[z_at], t_own.at[0]),
        pltpu.make_async_copy(seg_ref, seg_out.at[z_at], t_own.at[1]),
    ]
    for s, (src, full, _) in enumerate(sections):
        for j in range(2):
            column = cols(s, lanes[j])
            locals_.append(pltpu.make_async_copy(src.at[:, column], full.at[d_at, :, column], own_sem.at[s, j]))
    for copy in locals_:
        copy.start()

    def remote(src, dst, send, recv, peer):
        return pltpu.make_async_remote_copy(
            src_ref=src, dst_ref=dst, send_sem=send, recv_sem=recv, device_id=peer, device_id_type=MESH
        )

    def z_copy(s, k, j):
        src, full, _ = sections[s]
        return remote(
            src.at[:, cols(s, lanes[j])], full.at[d_at, :, cols(s, lanes[j])],
            z_send.at[s, k, j], z_recv.at[s, k, j], z_peers[k],
        )

    def y_copy(s, q, zi, j):
        src, full, _ = sections[s]
        column = cols(s, lanes[j])
        if zi == 0:
            shard, source = d_at, src.at[:, column]
        else:
            shard = shard_of(z_from[zi - 1], y_at)
            source = full.at[shard, :, column]
        return remote(source, full.at[shard, :, column], y_send.at[s, q, zi, j], y_recv.at[s, q, zi, j], y_peers[q])

    def x_copy(s):
        full = sections[s][1]
        block = full.at[:, :, cols(s, lane_mine)]
        return remote(block, block, x_send.at[s], x_recv.at[s], x_peer)

    def c_copy(s, j):
        full = sections[s][1]
        block = full.at[:, :, cols(s, (lane_both, lane_mine, lane_theirs)[j])]
        return remote(block, block, c_send.at[s, j], c_recv.at[s, j], c_peer)

    count = len(sections)
    tokens = []
    for k in range(GROUP - 1):
        tokens.append(remote(tok_ref, tok_out.at[z_at], t_send.at[0, k], t_recv.at[0, k], z_peers[k]))
        tokens.append(remote(seg_ref, seg_out.at[z_at], t_send.at[1, k], t_recv.at[1, k], z_peers[k]))

    def begin(s):
        for j in range(2):
            for k in range(GROUP - 1):
                z_copy(s, k, j).start()
            for q in range(n_inner - 1):
                y_copy(s, q, 0, j).start()

    begin(0)
    for copy in tokens:
        copy.start()
    for copy in locals_:
        copy.wait()
    begin(1)
    for step in range(count + 3):
        if step < count:
            for k in range(GROUP - 1):
                for j in range(2):
                    z_copy(step, k, j).wait_recv()
                    for q in range(n_inner - 1):
                        y_copy(step, q, k + 1, j).start()
            if step + 2 < count:
                begin(step + 2)
        s = step - 1
        if 0 <= s < count:
            for q in range(n_inner - 1):
                for zi in range(GROUP):
                    for j in range(2):
                        y_copy(s, q, zi, j).wait_recv()
            x_copy(s).start()
            for j in range(2):
                c_copy(s, j).start()
        s = step - 2
        if 0 <= s < count:
            x_copy(s).wait_recv()
            c_copy(s, 2).start()
        s = step - 3
        if 0 <= s < count:
            for j in range(3):
                c_copy(s, j).wait_recv()
    for copy in tokens:
        copy.wait()
    for s in range(count):
        for j in range(2):
            for k in range(GROUP - 1):
                z_copy(s, k, j).wait_send()
            for q in range(n_inner - 1):
                for zi in range(GROUP):
                    y_copy(s, q, zi, j).wait_send()
        x_copy(s).wait_send()
        for j in range(3):
            c_copy(s, j).wait_send()


def gather_weights(n_dp, text_low, image_low, tokens, segments):
    n_inner = n_dp // GROUP
    full = jax.ShapeDtypeStruct((n_dp,) + text_low.shape, jnp.bfloat16)
    hbm = pl.BlockSpec(memory_space=pltpu.HBM)
    dma = pltpu.SemaphoreType.DMA
    return pl.pallas_call(
        functools.partial(gather_kernel, n_dp),
        out_shape=(
            full,
            full,
            jax.ShapeDtypeStruct((GROUP,) + tokens.shape, jnp.bfloat16),
            jax.ShapeDtypeStruct((GROUP,) + segments.shape, jnp.int32),
        ),
        in_specs=[hbm] * 4,
        out_specs=(hbm,) * 4,
        scratch_shapes=[
            dma((6, GROUP - 1, 2)), dma((6, GROUP - 1, 2)),
            dma((6, n_inner - 1, GROUP, 2)), dma((6, n_inner - 1, GROUP, 2)),
            dma((6,)), dma((6,)), dma((6, 3)), dma((6, 3)),
            dma((2, GROUP - 1)), dma((2, GROUP - 1)), dma((2,)), dma((6, 2)),
        ],
        compiler_params=pltpu.CompilerParams(collective_id=1, has_side_effects=True),
        name="gather_weights",
    )(text_low, image_low, tokens, segments)


TILE = 256
PAIR = 128
ROWS = 32
LANES = 6
PART = 768
PARTS = 12
DEPTH = 8
AHEAD = 2
OWN_AHEAD = 4
TOKENS_AT = 6
STEP_TIME = 4.5
LAG_Z = 1
LAG_Y = 1
LAG_X = 2
LAG_C = 1
AT_Y = 2 * LAG_Z + LAG_Y
AT_X = AT_Y + LAG_X
AT_C = AT_X + LAG_C
WORDS = (GROUP * PAIR)


def piece_of(vec_ref, index, width=D):
    return vec_ref[:, pl.ds(index * D, width)]


def loop(count, body, unroll=1):
    def step(i, carry):
        body(i)
        return carry

    lax.fori_loop(0, count, step, 0, unroll=unroll)


def aligned(i, size):
    return pl.ds(pl.multiple_of(i * size, size), size)


def norm_rows(values):
    center = values - jnp.mean(values, axis=-1, keepdims=True)
    spread_ = jnp.mean(center * center, axis=-1, keepdims=True)
    return center * lax.rsqrt(spread_ + LAYER_EPS)


def dot(left, right):
    return jnp.dot(left, right, preferred_element_type=jnp.float32)


def dot_nt(left, right):
    return lax.dot_general(left, right, (((1,), (1,)), ((), ())), preferred_element_type=jnp.float32)


def dot_tn(left, right):
    return lax.dot_general(left, right, (((0,), (0,)), ((), ())), preferred_element_type=jnp.float32)


def lane_is_first():
    return lax.broadcasted_iota(jnp.int32, (PAIR, PAIR), 1) < HEAD_DIM


def two_heads(block):
    first = lane_is_first()
    zero = jnp.zeros_like(block)
    return jnp.concatenate([jnp.where(first, block, zero), jnp.where(first, zero, block)], axis=0)


def attention_forward(qkv, mixed, chance, allowed_of, first, count):
    pairs = HEADS // 2

    def body(k):
        at = first + k
        i, j = at // pairs, lax.rem(at, pairs)
        rows = aligned(i, PAIR)
        query = qkv[rows, aligned(j, PAIR)]
        key = qkv[rows, pl.ds(pl.multiple_of(D + j * PAIR, PAIR), PAIR)]
        value = qkv[rows, pl.ds(pl.multiple_of(2 * D + j * PAIR, PAIR), PAIR)]
        scores = dot_nt(two_heads(query), key) * SCORE_SCALE
        allowed = allowed_of(i)
        scores = jnp.where(jnp.concatenate([allowed, allowed], axis=0), scores, MASKED)
        scores = jnp.exp(scores - jnp.max(scores, axis=-1, keepdims=True))
        weight = scores / jnp.sum(scores, axis=-1, keepdims=True)
        if chance is not None:
            chance[at] = weight
        low = weight.astype(jnp.bfloat16)
        side = jnp.concatenate([low[:PAIR], low[PAIR:]], axis=1)
        mixed[rows, aligned(j, PAIR)] = dot(side, two_heads(value)).astype(jnp.bfloat16)

    loop(count, body, unroll=2)


def forward_kernel(
    n_dp, n_rep, patches,
    text_ref, image_ref, tok_ref, pic_ref, seg_ref, tvec_ref, ivec_ref,
    wt_out, pic_all, cap_all, words_out, text_pool_out, marks_out, qkv_out, chance_out, mid_out, slope_out,
    act_out, nt_out, at_out, mt_out,
    wi_ref, wt_vmem, tok, seg_col, seg_row, normed, qkv, mixed, middle, normed_two, active, slope, chance, total, hid, turned, apool, image_pool_out, patches_in, padded, master,
    z_send, z_recv, y_send, y_recv, x_send, x_recv, c_send, c_recv, t_send, t_recv, t_own, own_sem, w_sem, out_sem, p_send, p_recv, g_send, g_recv,
):
    n_inner = n_dp // GROUP
    d_at, r_at = lax.axis_index("dp"), lax.axis_index("rep")
    z_at, y_at = d_at // n_inner, lax.rem(d_at, n_inner)
    x_at, c_at = r_at // 2, lax.rem(r_at, 2)
    z_next = [((z_at - 1) * n_inner + y_at, r_at), ((z_at + 1) * n_inner + y_at, r_at)]
    y_peers = [(z_at * n_inner + 1 - y_at, r_at)]
    x_peer = (d_at, (1 - x_at) * 2 + c_at)
    c_peer = (d_at, x_at * 2 + 1 - c_at)

    devices = n_dp * n_rep
    me = d_at * n_rep + r_at
    z_open = (z_at > 0, z_at < GROUP - 1)
    barrier = pltpu.get_barrier_semaphore()

    def hello(peer):
        pl.semaphore_signal(barrier, inc=1, device_id=peer, device_id_type=MESH)

    for peer in (y_peers[0], x_peer, c_peer):
        hello(peer)
    for up in range(2):
        pl.when(z_open[up])(functools.partial(hello, z_next[up]))

    sections = [(image_ref, wi_ref, k) for k in range(PARTS)] + [(text_ref, wt_vmem, k) for k in range(PARTS)]
    count = len(sections)
    lane_mine = c_at * 3 + 2 * x_at
    lane_theirs = c_at * 3 + 2 * (1 - x_at)
    lanes_two = pl.ds(c_at * 3 + x_at, 2)
    lanes_three = pl.ds(c_at * 3, 3)

    def remote(src, dst, send, recv, peer):
        return pltpu.make_async_remote_copy(
            src_ref=src, dst_ref=dst, send_sem=send, recv_sem=recv, device_id=peer, device_id_type=MESH
        )

    def cols(s):
        return pl.ds(sections[s][2] * PART, PART)

    def set_of(s):
        return s // PARTS

    def size_of(s, shards, lanes_):
        return sections[s][1].at[sections[s][2], pl.ds(0, shards), pl.ds(0, lanes_)]

    def all_size(group, shards, lanes_):
        return sections[group * PARTS][1].at[:, pl.ds(0, shards), pl.ds(0, lanes_)]

    def landed(block, recv, peer):
        remote(block, block, x_send.at[0], recv, peer).wait_recv()

    def gone(block, send, peer):
        remote(block, block, send, x_recv.at[0], peer).wait_send()

    def held(s, shard, lane):
        _, full, k = sections[s]
        return full.at[k, shard, lane]

    def z_copy(s, up, hop):
        unit = z_at - hop if up else z_at + hop
        shard = unit * n_inner + y_at
        return remote(
            held(s, shard, lanes_two), held(s, shard, lanes_two),
            z_send.at[set_of(s), up, hop], z_recv.at[s, unit], z_next[up],
        )

    def y_copy(s, unit):
        shard = unit * n_inner + y_at
        return remote(
            held(s, shard, lanes_two), held(s, shard, lanes_two),
            y_send.at[set_of(s)], y_recv.at[s], y_peers[0],
        )

    def x_copy(s, unit):
        block = held(s, pl.ds(unit * n_inner, n_inner), lane_mine)
        return remote(block, block, x_send.at[set_of(s)], x_recv.at[s], x_peer)

    def x_own_copy(s):
        block = held(s, z_at * n_inner + 1 - y_at, lane_mine)
        return remote(block, block, x_send.at[set_of(s)], x_recv.at[s], x_peer)

    def c_copy(s, j):
        block = held(s, slice(None), (lanes_two, lane_theirs)[j])
        return remote(block, block, c_send.at[set_of(s)], c_recv.at[s], c_peer)

    def store(s):
        return pltpu.make_async_copy(wt_vmem.at[s - PARTS], wt_out.at[s - PARTS], w_sem.at[s - PARTS])

    def own_shard(s):
        src, _, _ = sections[s]
        return pltpu.make_async_copy(
            src.at[lanes_three, :, cols(s)], held(s, d_at, lanes_three) if s < PARTS else master.at[s % 4], own_sem.at[s]
        )

    def own_ready(s):
        own_shard(s).wait()
        if s >= PARTS:
            wt_vmem[s - PARTS, d_at, lanes_three] = master[s % 4].astype(jnp.bfloat16)

    gathered = ((tok_ref, tok), (None, seg_row))
    firsts = [
        pltpu.make_async_copy(tok_ref, tok.at[z_at], t_own.at[0]),
        pltpu.make_async_copy(pic_ref, patches_in, t_own.at[1]),
    ]

    def token_copy(i, up, hop):
        unit = z_at - hop if up else z_at + hop
        block = gathered[i][1].at[unit]
        return remote(block, block, t_send.at[i, up, hop], t_recv.at[i, unit], z_next[up])

    def token_begin():
        firsts[0].wait()
        number = seg_ref[...].astype(jnp.float32)
        number = jnp.concatenate([number[0:1, :], number[1:2, :] + PER_ROW], axis=1)
        seg_row[z_at] = jnp.broadcast_to(number, (16, PAIR)).astype(jnp.bfloat16)
        for i in range(2):
            for up in range(2):
                pl.when(z_open[up])(token_copy(i, up, 0).start)

    def token_arrive(hop):
        for up in range(2):
            unit = z_at - hop if up else z_at + hop

            @pl.when((unit >= 0) & (unit < GROUP))
            def _():
                for i in range(2):
                    block = gathered[i][1].at[0]
                    landed(block, t_recv.at[i, unit], z_next[up])
                    if hop < GROUP - 1:
                        pl.when(z_open[up])(token_copy(i, up, hop).start)

    def token_gone():
        for up in range(2):
            for hop in range(GROUP - 1):
                unit = z_at - hop if up else z_at + hop
                for i in range(2):
                    pl.when((unit >= 0) & (unit < GROUP) & z_open[up])(
                        functools.partial(gone, gathered[i][1].at[0], t_send.at[i, up, hop], z_next[up])
                    )

    def picture_copy(offset):
        _, other = peer_at(offset, n_dp, n_rep)
        return remote(pic_all.at[me], pic_all.at[me], p_send.at[offset - 1], p_recv.at[offset - 1], other)

    def send_pictures():
        values = image_pool_out[...]
        squares = jnp.sum(values * values, axis=-1, keepdims=True)
        pic_all[me] = (values * lax.rsqrt(squares + LAYER_EPS)).astype(jnp.bfloat16)

        def start(offset, carry):
            picture_copy(offset).start()
            return carry

        lax.fori_loop(1, devices, start, 0)

    near = n_inner * n_rep

    def caption_copy(k):
        other = lax.rem(y_at * n_rep + r_at + k, near)
        block = cap_all.at[:, y_at * n_rep + r_at]
        peer_ = (z_at * n_inner + other // n_rep, lax.rem(other, n_rep))
        return remote(block, block, g_send.at[k - 1], g_recv.at[k - 1], peer_)

    def send_captions():
        for i in range(GROUP):
            values = text_pool_out[pl.ds(i * 8, 8), :]
            squares = jnp.sum(values * values, axis=-1, keepdims=True)
            cap_all[i, y_at * n_rep + r_at] = (values * lax.rsqrt(squares + LAYER_EPS)).astype(jnp.bfloat16)
        for k in range(1, near):
            caption_copy(k).start()

    def end_pictures():
        def end(offset, carry):
            picture_copy(offset).wait()
            return carry

        lax.fori_loop(1, devices, end, 0)

    def begin(s):
        own_ready(s)
        for up in range(2):
            pl.when(z_open[up])(z_copy(s, up, 0).start)
        y_copy(s, z_at).start()

    def arrive(s, hop):
        for up in range(2):
            unit = z_at - hop if up else z_at + hop

            @pl.when((unit >= 0) & (unit < GROUP))
            def _():
                landed(size_of(s, 1, 2), z_recv.at[s, unit], z_next[up])
                if hop < GROUP - 1:
                    pl.when(z_open[up])(z_copy(s, up, hop).start)
                y_copy(s, unit).start()

    def own_start(s):
        own_shard(s).start()

    def stage_y(s):
        landed(size_of(s, GROUP, 2), y_recv.at[s], y_peers[0])
        for unit in range(GROUP):
            pl.when(unit != z_at)(x_copy(s, unit).start)
        x_own_copy(s).start()
        c_copy(s, 0).start()

    def stage_x(s):
        landed(size_of(s, n_dp - 1, 1), x_recv.at[s], x_peer)
        c_copy(s, 1).start()

    def stage_c(s):
        landed(size_of(s, n_dp, 3), c_recv.at[s], c_peer)
        if s >= PARTS:
            store(s).start()

    def carry_on(step):
        moves = []
        if step + OWN_AHEAD < count:
            moves.append(functools.partial(own_start, step + OWN_AHEAD))
        if step + AHEAD < count:
            moves.append(functools.partial(begin, step + AHEAD))
        for hop in range(1, GROUP):
            s = step - (hop - 1) * LAG_Z
            if 0 <= s < count:
                moves.append(functools.partial(arrive, s, hop))
        for lag, stage in ((AT_Y, stage_y), (AT_X, stage_x), (AT_C, stage_c)):
            if 0 <= step - lag < count:
                moves.append(functools.partial(stage, step - lag))
        if step == TOKENS_AT:
            moves.append(token_begin)
        for hop in range(1, GROUP):
            if step == TOKENS_AT + 2 * hop:
                moves.append(functools.partial(token_arrive, hop))
        return moves


    def weight_tile(s, c):
        _, full, k = sections[s]
        return full[k, :, :, :, aligned(c, TILE)].reshape(D, TILE)

    def weight_rows(s, half):
        _, full, k = sections[s]
        return full[k, pl.ds(half * (n_dp // 2), n_dp // 2)].reshape(D // 2, PART)

    def split_loop(total_, pieces, cost, body):
        size = total_ // pieces
        return [
            (cost, functools.partial(loop, size, functools.partial(lambda base, i: body(base + i), p * size)))
            for p in range(pieces)
        ]

    def first_norm(read, vec):
        def body(i):
            rows = aligned(i, ROWS)
            value = norm_rows(read(i).astype(jnp.float32))
            normed[rows, :] = (value * piece_of(vec, 0) + piece_of(vec, 1)).astype(jnp.bfloat16)

        return split_loop(WORDS // ROWS, 4, 0.5, body)

    def project(slot, part, bias):
        def body(c):
            out = dot(normed[...], weight_tile(slot, c))
            if bias is not None:
                out = out + bias[0][:, pl.ds(pl.multiple_of(bias[1] * D + c * TILE, TILE), TILE)]
            qkv[:, pl.ds(pl.multiple_of(part * D + c * TILE, TILE), TILE)] = out.astype(jnp.bfloat16)

        return split_loop(PART // TILE, 3, 0.6, body)

    def attend(slot, read, vec):
        def body(c):
            where = aligned(c, TILE)
            middle[:, where] = dot(mixed[...], weight_tile(slot, c)) + vec[
                :, pl.ds(pl.multiple_of(4 * D + c * TILE, TILE), TILE)
            ]

        def norm(i):
            rows = aligned(i, ROWS)
            value = middle[rows, :] + read(i).astype(jnp.float32)
            middle[rows, :] = value
            normed_two[rows, :] = (norm_rows(value) * piece_of(vec, 5) + piece_of(vec, 6)).astype(jnp.bfloat16)

        return split_loop(PART // TILE, 3, 0.6, body) + split_loop(WORDS // ROWS, 4, 0.6, norm)

    def expand(slot, part, vec, keep):
        def one(c, p):
            start = part * PART + c * TILE
            if p == 0:
                hid[...] = dot(normed_two[...], weight_tile(slot, c)) + vec[:, pl.ds(8 * D + start, TILE)]

            def inner(i):
                rows = aligned(i + p * (WORDS // ROWS // 2), ROWS)
                value = hid[rows, :]
                phi = 0.5 + 0.5 * lax.erf(value * 0.7071067811865476)
                active[rows, pl.ds(start, TILE)] = (value * phi).astype(jnp.bfloat16)
                if keep:
                    slope[rows, pl.ds(start, TILE)] = phi + value * (
                        0.3989422804014327 * jnp.exp(-0.5 * value * value)
                    )

            loop(WORDS // ROWS // 2, inner, unroll=2)

        return [
            (1.2 - 0.4 * p + 0.2 * keep, functools.partial(one, c, p)) for c in range(PART // TILE) for p in range(2)
        ]

    def shrink(slot, part, vec):
        def one(half):
            where = pl.ds(half * (D // 2), D // 2)
            out = dot_nt(active[:, pl.ds(part * PART, PART)], weight_rows(slot, half))
            if part == 0:
                total[:, where] = out + middle[:, where] + vec[:, pl.ds(7 * D + half * (D // 2), D // 2)]
            else:
                total[:, where] += out

        return [(0.8, functools.partial(one, half)) for half in range(2)]

    def attention(chance_, allowed_of):
        pairs_ = GROUP * HEADS // 2
        return [
            (1.2, functools.partial(attention_forward, qkv, mixed, chance_, allowed_of, first, 4))
            for first in range(0, pairs_, 4)
        ]

    def turn(source, slot, out):
        def body(c):
            turned[slot, aligned(c, PAIR), :] = source[:, aligned(c, PAIR)].T

        loop(D // PAIR, body)
        send_out(turned.at[slot, group_rows], out)

    outs = []

    def send_out(src, dst):
        copy = pltpu.make_async_copy(src, dst, out_sem.at[len(outs)])
        copy.start()
        outs.append(copy)

    group_rows = pl.ds(pl.multiple_of(z_at * (D // GROUP), D // GROUP), D // GROUP)

    def text_read(i):
        per = PAIR // ROWS
        return tok[i // per, aligned(lax.rem(i, per), ROWS), :]

    def text_allowed(i):
        row = seg_row[i].astype(jnp.float32)
        return seg_col[i] == row[0:1, :]

    def text_columns():
        for i in range(GROUP):
            row = seg_row[i].astype(jnp.float32)[0:1, :]
            seg_col[i] = jnp.broadcast_to(row, (PAIR, PAIR)).T

    def image_read(i):
        return padded[aligned(i, ROWS), :]

    def picture(axis):
        at = lax.broadcasted_iota(jnp.int32, (PAIR, PAIR), axis)
        number = at // (PAIR // 2)
        return jnp.where(lax.rem(at, PAIR // 2) < patches, number, number + 2)

    def image_allowed(i):
        return picture(0) == picture(1)

    def keep_mark():
        image = lax.broadcasted_iota(jnp.int32, (GROUP * 2, WORDS), 0)
        at = lax.broadcasted_iota(jnp.int32, (GROUP * 2, WORDS), 1)
        inside = (at // (PAIR // 2) == image) & (lax.rem(at, PAIR // 2) < patches)
        return jnp.where(inside, 1.0, 0.0)

    def text_pool():
        send_out(total.at[aligned(z_at, PAIR)], words_out)
        for i in range(GROUP):
            row = seg_row[i].astype(jnp.float32)[0:8, :]
            marks = jnp.where(row == lax.broadcasted_iota(jnp.int32, (8, PAIR), 0).astype(jnp.float32), 1.0, 0.0)
            marks_out[i] = marks
            marks_low = marks.astype(jnp.bfloat16)
            value = total[pl.ds(i * PAIR, PAIR), :]
            high = value.astype(jnp.bfloat16)
            rest = value - high.astype(jnp.float32)
            low = rest.astype(jnp.bfloat16)
            lower = (rest - low.astype(jnp.float32)).astype(jnp.bfloat16)
            sums = dot(
                jnp.concatenate([marks_low] * 3, axis=1), jnp.concatenate([high, low, lower], axis=0)
            )
            text_pool_out[pl.ds(i * 8, 8), :] = sums / jnp.sum(marks, axis=1, keepdims=True)

    def text_part(k):
        slot = k + PARTS
        if k == 0:
            return (
                [(0.3, text_columns)] + first_norm(text_read, tvec_ref) + project(slot, 0, (tvec_ref, 2))
                + [(0.8, lambda: turn(normed, 0, nt_out))]
            )
        if k == 1:
            return project(slot, 1, None)
        if k == 2:
            return (
                project(slot, 2, (tvec_ref, 3)) + [(0.1, lambda: send_out(qkv, qkv_out))]
                + attention(chance, text_allowed)
                + [(0.1, lambda: send_out(chance, chance_out)), (0.8, lambda: turn(mixed, 1, at_out))]
            )
        if k == 3:
            return attend(slot, text_read, tvec_ref) + [
                (0.1, lambda: send_out(middle, mid_out)), (0.8, lambda: turn(normed_two, 2, mt_out))
            ]
        if k < 8:
            return expand(slot, k - 4, tvec_ref, True)
        pieces = shrink(slot, k - 8, tvec_ref)
        if k == 10:
            pieces = pieces + [(1.0, end_pictures)]
        if k == 8:
            pieces = [(0.1, lambda: (send_out(active, act_out), send_out(slope, slope_out)))] + pieces
        if k == PARTS - 1:
            pieces = pieces + [(1.0, text_pool), (0.5, send_captions)]
        return pieces

    def pool_active(part):
        mark = keep_mark().astype(jnp.bfloat16)
        where = pl.ds(part * PART, PART)
        mean = dot(mark, active[:, where]) * (1.0 / patches)
        high = mean.astype(jnp.bfloat16)
        rest = mean - high.astype(jnp.float32)
        low = rest.astype(jnp.bfloat16)
        apool[0:8, where] = high.astype(jnp.float32)
        apool[8:16, where] = low.astype(jnp.float32)
        apool[16:24, where] = rest - low.astype(jnp.float32)

    def pool_shrink(slot, part):
        for half in range(2):
            where = pl.ds(half * (D // 2), D // 2)
            left = apool[:, pl.ds(part * PART, PART)].astype(jnp.bfloat16)
            out = dot_nt(left, weight_rows(slot, half))
            out = out[0:8] + out[8:16] + out[16:24]
            if part == 0:
                held_ = jnp.concatenate(
                    [
                        jnp.sum(middle[pl.ds(i * (PAIR // 2), patches), where], axis=0, keepdims=True)
                        for i in range(GROUP * 2)
                    ],
                    axis=0,
                )
                image_pool_out[:, where] = (
                    held_ * (1.0 / patches) + ivec_ref[:, pl.ds(7 * D + half * (D // 2), D // 2)] + out
                )
            else:
                image_pool_out[:, where] += out

    def image_part(k):
        slot = k
        if k == 0:
            return first_norm(image_read, ivec_ref) + project(slot, 0, (ivec_ref, 2))
        if k == 1:
            return project(slot, 1, None)
        if k == 2:
            return project(slot, 2, (ivec_ref, 3)) + attention(None, image_allowed)
        if k == 3:
            return attend(slot, image_read, ivec_ref)
        if k < 8:
            return expand(slot, k - 4, ivec_ref, False) + [(0.2, functools.partial(pool_active, k - 4))]
        pieces = [(0.5, functools.partial(pool_shrink, slot, k - 8))]
        if k == PARTS - 1:
            pieces.append((2.0, send_pictures))
        return pieces

    own_start(0)
    for copy in reversed(firsts):
        copy.start()
    for s in range(1, OWN_AHEAD):
        own_start(s)
    firsts[1].wait()
    images = GROUP * 2
    half_row = PAIR // 2
    for quarter_ in range(GROUP):
        row = lax.broadcasted_iota(jnp.int32, (PAIR, patches * images), 0) + quarter_ * PAIR
        source = lax.broadcasted_iota(jnp.int32, (PAIR, patches * images), 1)
        wanted = lax.rem(row, half_row) * images + row // half_row
        move = jnp.where((wanted == source) & (lax.rem(row, half_row) < patches), 1.0, 0.0).astype(jnp.bfloat16)
        padded[pl.ds(quarter_ * PAIR, PAIR), :] = dot(move, patches_in[...]).astype(jnp.bfloat16)
    pl.semaphore_wait(barrier, 5 - jnp.where(z_at == 0, 1, 0) - jnp.where(z_at == GROUP - 1, 1, 0))
    for s in range(AHEAD):
        begin(s)
    moves = [(step, move) for step in range(count + AT_C) for move in carry_on(step)]
    by_step = {}
    for step, move in moves:
        by_step.setdefault(step, []).append(move)
    timed = []
    for step in sorted(by_step):
        for i, move in enumerate(by_step[step]):
            timed.append((STEP_TIME * (step + i / len(by_step[step])), step, move))
    clock, done = 0.0, 0
    for s in range(count):
        pieces = image_part(s) if s < PARTS else text_part(s - PARTS)
        while done < len(timed) and timed[done][1] <= s + AT_C:
            clock = max(clock, timed[done][0])
            timed[done][2]()
            done += 1
        for cost, piece in pieces:
            piece()
            clock += cost
            while done < len(timed) and timed[done][0] <= clock:
                timed[done][2]()
                done += 1
    while done < len(timed):
        timed[done][2]()
        done += 1
    for copy in outs:
        copy.wait()
    for s in range(PARTS, count):
        store(s).wait()
    token_gone()
    for group in range(2):
        for up in range(2):
            for hop in range(GROUP - 1):
                unit = z_at - hop if up else z_at + hop
                pl.when((unit >= 0) & (unit < GROUP) & z_open[up])(
                    functools.partial(gone, all_size(group, 1, 2), z_send.at[group, up, hop], z_next[up])
                )
        gone(all_size(group, GROUP, 2), y_send.at[group], y_peers[0])
        gone(all_size(group, n_dp - 1, 1), x_send.at[group], x_peer)
        gone(all_size(group, n_dp, 3), c_send.at[group], c_peer)
    for k in range(1, near):
        caption_copy(k).wait()


def gather_and_forward(n_dp, n_rep, text_low, image_low, tokens, segments, pictures, text_vectors, image_vectors):
    own, columns = text_low.shape
    images, patches = pictures.shape[0], pictures.shape[1]
    lane_rows = own // LANES
    count = 2 * PARTS
    hbm, vmem = pl.BlockSpec(memory_space=pltpu.HBM), pl.BlockSpec(memory_space=pltpu.VMEM)
    low, full = jnp.bfloat16, jnp.float32
    shape = jax.ShapeDtypeStruct
    gathered = shape((PARTS, n_dp, LANES, lane_rows, PART), low)
    turned = shape((D // GROUP, WORDS), low)
    pairs = GROUP * HEADS // 2
    dma = pltpu.SemaphoreType.DMA
    outs = pl.pallas_call(
        functools.partial(forward_kernel, n_dp, n_rep, patches),
        out_shape=(
            gathered, shape((n_dp * n_rep, images, D), low), shape((GROUP, n_dp * n_rep // GROUP, 8, D), low),
            shape((PAIR, D), full), shape((8 * GROUP, D), full),
            shape((GROUP, 8, PAIR), full), shape((WORDS, 3 * D), low), shape((pairs, 2 * PAIR, PAIR), full),
            shape((WORDS, D), full), shape((WORDS, FF), full), shape((WORDS, FF), low), turned, turned, turned,
        ),
        in_specs=[hbm] * 4 + [vmem] * 3,
        out_specs=(hbm, vmem, vmem, hbm, vmem, vmem) + (hbm,) * 8,
        scratch_shapes=[
            pltpu.VMEM((PARTS, n_dp, LANES, lane_rows, PART), low),
            pltpu.VMEM((PARTS, n_dp, LANES, lane_rows, PART), low),
            pltpu.VMEM((GROUP, PAIR, D), low),
            pltpu.VMEM((GROUP, PAIR, PAIR), full),
            pltpu.VMEM((GROUP, 16, PAIR), low),
            pltpu.VMEM((WORDS, D), low),
            pltpu.VMEM((WORDS, 3 * D), low),
            pltpu.VMEM((WORDS, D), low),
            pltpu.VMEM((WORDS, D), full),
            pltpu.VMEM((WORDS, D), low),
            pltpu.VMEM((WORDS, FF), low),
            pltpu.VMEM((WORDS, FF), full),
            pltpu.VMEM((pairs, 2 * PAIR, PAIR), full),
            pltpu.VMEM((WORDS, D), full),
            pltpu.VMEM((WORDS, TILE), full),
            pltpu.VMEM((3, D, WORDS), low),
            pltpu.VMEM((24, FF), full),
            pltpu.VMEM((images, D), full),
            pltpu.VMEM((patches * images, D), low),
            pltpu.VMEM((WORDS, D), low),
            pltpu.VMEM((4, 3, lane_rows, PART), full),
            dma((2, 2, GROUP - 1)), dma((count, GROUP)), dma((2,)), dma((count,)),
            dma((2,)), dma((count,)), dma((2,)), dma((count,)),
            dma((2, 2, GROUP - 1)), dma((2, GROUP)), dma((2,)), dma((count,)), dma((PARTS,)), dma((12,)),
            dma((n_dp * n_rep - 1,)), dma((n_dp * n_rep - 1,)), dma((8,)), dma((8,)),
        ],
        compiler_params=pltpu.CompilerParams(collective_id=5, has_side_effects=True, vmem_limit_bytes=60 << 20),
        name="gather_and_forward",
    )(
        text_low.reshape(LANES, lane_rows, columns), image_low.reshape(LANES, lane_rows, columns), tokens,
        jnp.swapaxes(pictures, 0, 1).reshape(patches * images, D), segments,
        text_vectors.reshape(1, -1), image_vectors.reshape(1, -1),
    )
    return (outs[0].reshape(PARTS, D, PART),) + tuple(outs[1:])


def backward_kernel(
    n_dp, n_rep,
    wt_ref, nt_ref, at_ref, mt_ref, qkv_ref, chance_ref, mid_ref, slope_ref, act_ref, feed_ref,
    tpool_ref, pic_all, cap_all, marks_ref, tok_ref, vec_ref, start_ref, flat_ref, moving_ref,
    m_out, input_out, loss_out, left_out, right_out, nvec_out, nvmom_out,
    weight, turned, qkv, chance, middle, slope, active, grad_hidden, grad_mix, low, low_mixed, wide, block, sent, got, sums, dy_ref, e2t, rows_out, vector_out,
    factor, factor_rep, factor_dp, basis, tiles, tiles_rep, quarter, tiles_dp, everything,
    load_sem, send, recv, m_sem, g_send, g_recv,
):
    n_inner = n_dp // GROUP
    d_at, r_at = lax.axis_index("dp"), lax.axis_index("rep")
    z_at, y_at = d_at // n_inner, lax.rem(d_at, n_inner)
    peer = (z_at * n_inner + 1 - y_at, r_at)
    own = D // n_dp
    share = 1.0 / GROUP

    barrier = pltpu.get_barrier_semaphore()
    devices = n_dp * n_rep
    near = n_inner * n_rep

    def near_peer(k):
        other = lax.rem(y_at * n_rep + r_at + k, near)
        return z_at * n_inner + other // n_rep, lax.rem(other, n_rep)

    rep_peers = [(d_at, lax.rem(r_at + k, n_rep)) for k in range(1, n_rep)]
    dp_peers = [(lax.rem(d_at + k, n_dp), r_at) for k in range(1, n_dp)]
    far_peers = [
        (lax.rem(z_at + k, GROUP) * n_inner + y, r_at) for k in range(1, GROUP) for y in range(n_inner)
    ]
    met = near - 1 + len(far_peers)
    for other in [near_peer(k) for k in range(1, near)] + far_peers:
        pl.semaphore_signal(barrier, inc=1, device_id=other, device_id_type=MESH)
    loads = {}

    def fetch(name, src, dst):
        copy = pltpu.make_async_copy(src, dst, load_sem.at[len(loads)])
        copy.start()
        loads[name] = copy

    def need(*names):
        for name in names:
            loads[name].wait()

    fetch("act", act_ref, active)
    fetch("feed", feed_ref, rows_out)
    for part in range(4):
        fetch(("w", 8 + part), wt_ref.at[8 + part], weight.at[8 + part])
    fetch("slope", slope_ref, slope)
    fetch("mt", mt_ref, turned.at[0])
    for part in range(4):
        fetch(("w", 4 + part), wt_ref.at[4 + part], weight.at[4 + part])
    fetch("mid", mid_ref, middle)
    fetch("at", at_ref, turned.at[1])
    fetch(("w", 3), wt_ref.at[3], weight.at[3])
    fetch("qkv", qkv_ref, qkv)
    fetch("chance", chance_ref, chance)
    fetch("nt", nt_ref, turned.at[2])
    for part in range(3):
        fetch(("w", part), wt_ref.at[part], weight.at[part])

    def exchange(s):
        return pltpu.make_async_remote_copy(
            src_ref=sent.at[s], dst_ref=got.at[s], send_sem=send.at[s], recv_sem=recv.at[s],
            device_id=peer, device_id_type=MESH,
        )

    own_rows = pl.ds(pl.multiple_of(y_at * own, own), own)
    other_rows = pl.ds(pl.multiple_of((1 - y_at) * own, own), own)

    def exchange_tile(s, where, slot):
        return pltpu.make_async_remote_copy(
            src_ref=sent.at[s, :, where], dst_ref=got.at[s, :, where], send_sem=send.at[slot], recv_sem=recv.at[slot],
            device_id=peer, device_id_type=MESH,
        )

    def exchange_heads(j):
        where = (pl.ds(0, 3), slice(None), pl.ds(j * PAIR, PAIR))
        return pltpu.make_async_remote_copy(
            src_ref=sent.at[where], dst_ref=got.at[where], send_sem=send.at[PARTS + j], recv_sem=recv.at[PARTS + j],
            device_id=peer, device_id_type=MESH,
        )

    def outer(s, left, right_of):
        def body(c):
            block[:, pl.ds(0, TILE)] = dot(left, right_of(c))
            where = pl.ds(pl.multiple_of(s * PART + c * TILE, TILE), TILE)
            rows_out[:, where] = rows_out[:, where] + block[own_rows, pl.ds(0, TILE)]
            sent[s, :, aligned(c, TILE)] = block[other_rows, pl.ds(0, TILE)].astype(jnp.bfloat16)
            exchange_tile(s, aligned(c, TILE), s).start()

        loop(PART // TILE, body, unroll=3)

    ones = jnp.ones((16, WORDS), jnp.bfloat16)

    def put(slot, values):
        for i in range(values.shape[1] // PAIR):
            vector_out[pl.ds(slot // PAIR + i, 1), :] = values[:, i * PAIR : (i + 1) * PAIR]

    def column_sums(values, slot, scale):
        put(slot, dot(ones, values)[0:1, :] * scale)


    def contrast():
        group_pairs = GROUP * 8
        pairs_ = devices * 8
        pics = pic_all[...].reshape(pairs_, D)
        caps = cap_all[...].reshape(pairs_, D)
        logits = dot_nt(caps, pics) * LOGIT_SCALE
        top = jnp.max(logits, axis=0, keepdims=True)
        image_log = top + jnp.log(jnp.sum(jnp.exp(logits - top), axis=0, keepdims=True))
        top = jnp.max(logits, axis=1, keepdims=True)
        caption_log = top + jnp.log(jnp.sum(jnp.exp(logits - top), axis=1, keepdims=True))
        row = lax.broadcasted_iota(jnp.int32, (pairs_, pairs_), 0)
        column = lax.broadcasted_iota(jnp.int32, (pairs_, pairs_), 1)
        matched = jnp.sum(jnp.where(row == column, logits, 0.0), axis=1, keepdims=True)
        loss = (jnp.sum(image_log) + jnp.sum(caption_log) - 2.0 * jnp.sum(matched)) / (2.0 * pairs_)
        loss_out[0, 0] = loss
        pooled = tpool_ref[...]
        squares = lax.rsqrt(jnp.sum(pooled * pooled, axis=-1, keepdims=True) + LAYER_EPS)
        own_low = (pooled * squares).astype(jnp.bfloat16)
        own_logits = dot_nt(own_low, pics) * LOGIT_SCALE
        top = jnp.max(own_logits, axis=1, keepdims=True)
        own_log = top + jnp.log(jnp.sum(jnp.exp(own_logits - top), axis=1, keepdims=True))
        local = lax.broadcasted_iota(jnp.int32, (group_pairs, pairs_), 0)
        column = lax.broadcasted_iota(jnp.int32, (group_pairs, pairs_), 1)
        wanted = (local // 8) * (near * 8) + (y_at * n_rep + r_at) * 8 + lax.rem(local, 8)
        pick = jnp.where(wanted == column, 1.0, 0.0)
        soft = ((jnp.exp(own_logits - own_log) - pick) * 0.5).astype(jnp.bfloat16)
        across = ((jnp.exp(own_logits - image_log) - pick) * 0.5).astype(jnp.bfloat16)
        grad = LOGIT_SCALE * (dot(soft, pics) + dot(across, pics))
        grad = squares * (
            grad - pooled * (squares * squares) * jnp.sum(grad * pooled, axis=-1, keepdims=True)
        )
        for i in range(GROUP):
            marks = marks_ref[i]
            part = grad[i * 8 : (i + 1) * 8, :] / jnp.sum(marks, axis=1, keepdims=True)
            high, rest = split_two(part)
            rest_low = (part - high.astype(jnp.float32) - rest.astype(jnp.float32)).astype(jnp.bfloat16)
            stacked = jnp.concatenate([high, rest, rest_low], axis=0)
            marks_low = marks.astype(jnp.bfloat16)
            marks_low = jnp.concatenate([marks_low, marks_low, marks_low], axis=0)
            rows = pl.ds(i * PAIR, PAIR)
            words = dot_tn(marks_low, stacked)
            dy_ref[rows, :] = words
            low[rows, :] = words.astype(jnp.bfloat16)
            e2t[:, rows] = dot_tn(stacked, marks_low).astype(jnp.bfloat16)

    contrast()
    pl.semaphore_wait(barrier, met)
    need("act", "feed")
    for part in range(4):
        outer(8 + part, e2t[pl.ds(pl.multiple_of(z_at * (D // GROUP), D // GROUP), D // GROUP), :], lambda c: active[:, pl.ds(pl.multiple_of(part * PART + c * TILE, TILE), TILE)])
    need("slope")
    column_sums(low[...], 7 * D, share)
    for part in range(4):
        need(("w", 8 + part))

        def hidden_body(c):
            where = pl.ds(pl.multiple_of(part * PART + c * TILE, TILE), TILE)
            out = dot(low[...], weight[8 + part, :, aligned(c, TILE)])
            grad_hidden[:, where] = (out * slope[:, where]).astype(jnp.bfloat16)

        loop(PART // TILE, hidden_body, unroll=3)
    need("mt")
    for part in range(4):
        outer(
            4 + part, turned[0], lambda c: grad_hidden[:, pl.ds(pl.multiple_of(part * PART + c * TILE, TILE), TILE)]
        )
    for part in range(4):
        need(("w", 4 + part))
    for half in range(2):
        rows = pl.ds(half * (D // 2), D // 2)
        out = dot_nt(grad_hidden[:, pl.ds(0, PART)], weight[4, rows, :])
        for part in range(1, 4):
            out = out + dot_nt(grad_hidden[:, pl.ds(part * PART, PART)], weight[4 + part, rows, :])
        wide[:, rows] = out
    need("mid")

    def norm_back(value, grad, gain):
        center = value - jnp.mean(value, axis=-1, keepdims=True)
        scale = lax.rsqrt(jnp.mean(center * center, axis=-1, keepdims=True) + LAYER_EPS)
        unit = center * scale
        inner = grad * gain
        out = scale * (
            inner - jnp.mean(inner, axis=-1, keepdims=True) - unit * jnp.mean(inner * unit, axis=-1, keepdims=True)
        )
        return out, grad * unit

    def fold(values):
        return jnp.sum(values.reshape(ROWS // 8, 8, D), axis=0)

    sums[...] = jnp.zeros_like(sums)

    def second(i):
        rows = aligned(i, ROWS)
        grad = wide[rows, :]
        out, product = norm_back(middle[rows, :], grad, piece_of(vec_ref, 5))
        sums[0] += fold(product)
        sums[1] += fold(grad)
        out = out + dy_ref[rows, :]
        middle[rows, :] = out
        low[rows, :] = out.astype(jnp.bfloat16)

    loop(WORDS // ROWS, second, unroll=2)
    put(5 * D, jnp.sum(sums[0], axis=0, keepdims=True) * share)
    put(6 * D, jnp.sum(sums[1], axis=0, keepdims=True) * share)
    need("at", ("w", 3))
    outer(3, turned[1], lambda c: low[:, aligned(c, TILE)])
    for half in range(2):
        rows = pl.ds(half * (D // 2), D // 2)
        low_mixed[:, rows] = dot_nt(low[...], weight[3, rows, :]).astype(jnp.bfloat16)
    need("qkv", "chance")
    pairs = HEADS // 2

    def attention(j, i):
        at = i * pairs + j
        rows = pl.ds(i * PAIR, PAIR)
        q_cols = pl.ds(j * PAIR, PAIR)
        k_cols = pl.ds(D + j * PAIR, PAIR)
        v_cols = pl.ds(2 * D + j * PAIR, PAIR)
        query, key, value = qkv[rows, q_cols], qkv[rows, k_cols], qkv[rows, v_cols]
        grad = two_heads(low_mixed[rows, q_cols])
        weight_ = chance[at]
        grad_mix[rows, v_cols] = dot_tn(weight_.astype(jnp.bfloat16), grad).astype(jnp.bfloat16)
        back = dot_nt(grad, value)
        back = weight_ * (back - jnp.sum(weight_ * back, axis=-1, keepdims=True))
        back = back.astype(jnp.bfloat16)
        side = jnp.concatenate([back[:PAIR], back[PAIR:]], axis=1)
        grad_mix[rows, q_cols] = (dot(side, two_heads(key)) * SCORE_SCALE).astype(jnp.bfloat16)
        grad_mix[rows, k_cols] = (dot_tn(back, two_heads(query)) * SCORE_SCALE).astype(jnp.bfloat16)

    need("nt")
    for j in range(pairs):
        for i in range(GROUP):
            attention(j, i)
        for part in range(3):
            value = dot(turned[2], grad_mix[:, pl.ds(part * D + j * PAIR, PAIR)])
            block[:, pl.ds(part * PAIR, PAIR)] = value
            where = pl.ds(part * D + j * PAIR, PAIR)
            rows_out[:, where] = rows_out[:, where] + block[own_rows, pl.ds(part * PAIR, PAIR)]
            sent[part, :, pl.ds(j * PAIR, PAIR)] = block[other_rows, pl.ds(part * PAIR, PAIR)].astype(jnp.bfloat16)
            exchange_tile(part, pl.ds(j * PAIR, PAIR), PARTS + j).start()
    column_sums(low[...], 4 * D, share)
    column_sums(grad_hidden[...], 8 * D, share)
    column_sums(grad_mix[:, pl.ds(0, D)], 2 * D, share)
    column_sums(grad_mix[:, pl.ds(2 * D, D)], 3 * D, share)
    for part in range(3):
        need(("w", part))
    mine = aligned(z_at, PAIR)
    for half in range(2):
        rows = pl.ds(half * (D // 2), D // 2)
        out = dot_nt(grad_mix[mine, pl.ds(0, PART)], weight[0, rows, :])
        for part in range(1, 3):
            out = out + dot_nt(grad_mix[mine, pl.ds(part * PART, PART)], weight[part, rows, :])
        wide[pl.ds(0, PAIR), rows] = out
    sums[...] = jnp.zeros_like(sums)

    def first(i):
        rows = aligned(i, ROWS)
        grad = wide[rows, :]
        out, product = norm_back(tok_ref[rows, :].astype(jnp.float32), grad, piece_of(vec_ref, 0))
        sums[0] += fold(product)
        sums[1] += fold(grad)
        input_out[rows, :] = out + middle[pl.ds(pl.multiple_of(z_at * PAIR + i * ROWS, ROWS), ROWS), :]

    loop(PAIR // ROWS, first)
    put(0, jnp.sum(sums[0], axis=0, keepdims=True))
    put(D, jnp.sum(sums[1], axis=0, keepdims=True))

    bounds = matrix_bounds()
    rank = start_ref.shape[0]
    strip = n_dp * OWN_TILES
    sums_of = {}

    def take(s):
        where = pl.ds(s * PART, PART)
        rows_out[:, where] = rows_out[:, where] + got[s].astype(jnp.float32)
        high, rest = split_two(rows_out[:, where])
        start_high, start_low = split_two(start_ref[:, where])
        both = jnp.concatenate([start_high, start_low], axis=0)
        matrix = 0 if s < 3 else 1 if s == 3 else 2 if s < 8 else 3
        out, out_rest = dot_nt(both, high), dot_nt(both, rest)
        out = out[:rank] + out[rank:] + out_rest[:rank]
        sums_of[matrix] = out if matrix not in sums_of else sums_of[matrix] + out

    for s in (8, 9, 10, 11, 4, 5, 6, 7, 3):
        exchange(s).wait_recv()
        take(s)
    for j in range(pairs):
        exchange_heads(j).wait_recv()
    for s in range(3):
        take(s)
    m_copy = pltpu.make_async_copy(rows_out, m_out, m_sem)
    m_copy.start()
    factor[...] = jnp.zeros_like(factor)
    for matrix in range(4):
        factor[pl.ds(matrix * rank, rank), pl.ds(0, own)] = sums_of[matrix]

    def remote(phase, k, src, dst, other):
        return pltpu.make_async_remote_copy(
            src_ref=src, dst_ref=dst, send_sem=g_send.at[phase, k], recv_sem=g_recv.at[phase, k],
            device_id=other, device_id_type=MESH,
        )

    mine = pl.ds(r_at * strip + d_at * OWN_TILES, OWN_TILES)
    strip_mine = pl.ds(r_at * strip, strip)
    phases = [
        [remote(0, k, factor, factor_rep.at[k], other) for k, other in enumerate(rep_peers)],
        [remote(1, k, factor_dp.at[d_at], factor_dp.at[d_at], other) for k, other in enumerate(dp_peers)],
        [
            remote(2, k, tiles.at[pl.ds(other[1] * strip, strip)], tiles_rep.at[k], other)
            for k, other in enumerate(rep_peers)
        ],
        [
            remote(3, k, quarter.at[pl.ds(other[0] * OWN_TILES, OWN_TILES)], tiles_dp.at[k], other)
            for k, other in enumerate(dp_peers)
        ],
        [remote(4, k, everything.at[mine], everything.at[mine], other) for k, other in enumerate(dp_peers)],
        [remote(5, k, everything.at[strip_mine], everything.at[strip_mine], other) for k, other in enumerate(rep_peers)],
    ]

    def begin(phase):
        for copy in phases[phase]:
            copy.start()

    def arrived(phase):
        for copy in phases[phase]:
            copy.wait_recv()


    def send_strip(j):
        k = lax.rem(j - r_at + 2 * n_rep - 1, n_rep)
        copy = remote(2, k, tiles.at[pl.ds(j * strip, strip)], tiles_rep.at[k], (d_at, j))
        pl.when(r_at != j)(copy.start)

    columns = bounds[-1][1] // PAIR
    for i in range(EXTRA):
        tiles[columns + i] = vector_out[pl.ds(i * 8, 8), :]
    for i in range(columns + EXTRA, n_rep * strip):
        tiles[i] = jnp.zeros((8, PAIR), jnp.float32)
    begin(0)
    send_strip(n_rep - 1)
    arrived(0)
    summed = factor[...]
    for k in range(n_rep - 1):
        summed = summed + factor_rep[k]
    factor_dp[d_at] = summed
    begin(1)
    arrived(1)
    vectors = jnp.concatenate([factor_dp[i] for i in range(n_dp)], axis=1).reshape(4, rank, n_dp * PAIR)
    place = lax.broadcasted_iota(jnp.int32, (4, rank, 1), 1)
    for k in range(rank):
        vector = vectors[:, k : k + 1, :]
        size = jnp.sqrt(jnp.sum(vector * vector, axis=-1, keepdims=True)) + NORM_FLOOR
        vector = vector / size
        along = jnp.sum(vector * vectors, axis=-1, keepdims=True)
        vectors = jnp.where(
            place == k, jnp.broadcast_to(vector, vectors.shape),
            vectors - jnp.where(place > k, along, 0.0) * vector,
        )
    vectors = vectors.reshape(4 * rank, n_dp * PAIR)
    basis[...] = vectors
    left_out[...] = vectors
    basis_high, basis_low = split_two(basis[:, aligned(d_at, PAIR)][:, :own])
    for matrix, (first_col, after_col) in enumerate(bounds):
        where = slice(matrix * rank, (matrix + 1) * rank)
        both = jnp.concatenate([basis_high[where], basis_low[where]], axis=0)

        def project(c):
            high, low = split_two(rows_out[:, pl.ds(pl.multiple_of(first_col + c * TILE, TILE), TILE)])
            out = dot(both, high)
            out = out[:rank] + out[rank:] + dot(both, low)[:rank]
            at = first_col // PAIR + c * (TILE // PAIR)
            for half in range(TILE // PAIR):
                tiles[at + half] = out[:, half * PAIR : (half + 1) * PAIR]

        loop((after_col - first_col) // TILE, project, unroll=3)
        if matrix > 0:
            send_strip(matrix - 1)
    arrived(2)
    value = tiles[strip_mine]
    for k in range(n_rep - 1):
        value = value + tiles_rep[k]
    quarter[...] = value
    begin(3)
    arrived(3)
    value = quarter[pl.ds(d_at * OWN_TILES, OWN_TILES)]
    for k in range(n_dp - 1):
        value = value + tiles_dp[k]
    everything[mine] = value
    begin(4)
    arrived(4)
    begin(5)
    arrived(5)
    for i in range(columns):
        right_out[:, pl.ds(i * PAIR, PAIR)] = everything[i]
    for i in range(EXTRA):
        at = pl.ds(i * 8, 8)
        moved = MOMENTUM_DECAY * moving_ref[at, :] + everything[columns + i]
        nvmom_out[at, :] = moved
        nvec_out[at, :] = flat_ref[at, :] - STEP_RATE * moved
    m_copy.wait()
    for s in range(3, PARTS):
        exchange(s).wait_send()
    for j in range(pairs):
        exchange_heads(j).wait_send()
    for phase in phases:
        for copy in phase:
            copy.wait_send()


def backward(n_dp, n_rep, kept, pooled, pictures, captions, marks, tokens, text_vectors, feedback_rows, start, moving):
    weights, qkv, chance, middle, slope, active, n_turned, a_turned, m_turned = kept
    own = feedback_rows.shape[0]
    hbm, vmem = pl.BlockSpec(memory_space=pltpu.HBM), pl.BlockSpec(memory_space=pltpu.VMEM)
    low, full = jnp.bfloat16, jnp.float32
    shape = jax.ShapeDtypeStruct
    dma = pltpu.SemaphoreType.DMA
    pairs = GROUP * HEADS // 2
    rank = start.shape[0]
    strip = n_dp * OWN_TILES
    flat = (12 * D // PAIR, PAIR)
    return pl.pallas_call(
        functools.partial(backward_kernel, n_dp, n_rep),
        out_shape=(
            shape(feedback_rows.shape, full), shape((PAIR, D), full), shape((1, 1), full),
            shape((4 * rank, n_dp * PAIR), full), shape(start.shape, full), shape(flat, full), shape(flat, full),
        ),
        in_specs=[hbm] * 10 + [vmem] * 9,
        out_specs=(hbm, vmem, pl.BlockSpec(memory_space=pltpu.SMEM)) + (vmem,) * 4,
        scratch_shapes=[
            pltpu.VMEM((PARTS, D, PART), low),
            pltpu.VMEM((3, D // GROUP, WORDS), low),
            pltpu.VMEM((WORDS, 3 * D), low),
            pltpu.VMEM((pairs, 2 * PAIR, PAIR), full),
            pltpu.VMEM((WORDS, D), full),
            pltpu.VMEM((WORDS, FF), full),
            pltpu.VMEM((WORDS, FF), low),
            pltpu.VMEM((WORDS, FF), low),
            pltpu.VMEM((WORDS, 3 * D), low),
            pltpu.VMEM((WORDS, D), low),
            pltpu.VMEM((WORDS, D), low),
            pltpu.VMEM((WORDS, D), full),
            pltpu.VMEM((D // GROUP, 3 * PAIR), full),
            pltpu.VMEM((PARTS, own, PART), low),
            pltpu.VMEM((PARTS, own, PART), low),
            pltpu.VMEM((2, 8, D), full),
            pltpu.VMEM((WORDS, D), full),
            pltpu.VMEM((D, WORDS), low),
            pltpu.VMEM(feedback_rows.shape, full),
            pltpu.VMEM(flat, full),
            pltpu.VMEM((4 * rank, PAIR), full),
            pltpu.VMEM((n_rep - 1, 4 * rank, PAIR), full),
            pltpu.VMEM((n_dp, 4 * rank, PAIR), full),
            pltpu.VMEM((4 * rank, n_dp * PAIR), full),
            pltpu.VMEM((n_rep * strip, 8, PAIR), full),
            pltpu.VMEM((n_rep - 1, strip, 8, PAIR), full),
            pltpu.VMEM((strip, 8, PAIR), full),
            pltpu.VMEM((n_dp - 1, OWN_TILES, 8, PAIR), full),
            pltpu.VMEM((n_rep * strip, 8, PAIR), full),
            dma((24,)), dma((PARTS + 6,)), dma((PARTS + 6,)), dma,
            dma((6, n_dp - 1)), dma((6, n_dp - 1)),
        ],
        compiler_params=pltpu.CompilerParams(collective_id=6, has_side_effects=True, vmem_limit_bytes=60 << 20),
        name="backward",
    )(
        weights, n_turned, a_turned, m_turned, qkv, chance, middle, slope, active, feedback_rows,
        pooled, pictures, captions, marks, tokens, text_vectors.reshape(1, -1), start, text_vectors.reshape(flat),
        moving.reshape(flat),
    )


EXTRA = 9
OWN_TILES = 3


def split_two(values):
    high = values.astype(jnp.bfloat16)
    return high, (values - high.astype(jnp.float32)).astype(jnp.bfloat16)


CHUNKS = 2


def finish_kernel(
    n_dp, n_rep,
    rows_ref, mom_ref, wts_ref, words_ref, input_ref, left_ref, right_ref, vec_ref, vmom_ref, loss_ref,
    feed_out, mom_out, wts_out, words_out, input_out, left_out, right_out, vec_out, vmom_out, loss_out,
    rows, mom, wts, change, through, load_sem, store_sem, pass_sem,
):
    own = rows.shape[0]
    piece = own // CHUNKS
    rank = right_ref.shape[0]

    def load(i, j):
        src, dst = ((rows_ref, rows), (mom_ref, mom), (wts_ref, wts))[j]
        span = pl.ds(i * piece, piece)
        return pltpu.make_async_copy(src.at[span], dst.at[span], load_sem.at[i, j])

    def store(i, j):
        src, dst = ((rows, feed_out), (mom, mom_out), (wts, wts_out))[j]
        span = pl.ds(i * piece, piece)
        return pltpu.make_async_copy(src.at[span], dst.at[span], store_sem.at[i, j])

    for i in range(CHUNKS):
        for j in range(3):
            load(i, j).start()
    taken = [
        pltpu.make_async_copy(src, through.at[i], pass_sem.at[i]) for i, src in enumerate((words_ref, input_ref))
    ]
    passed = [
        pltpu.make_async_copy(through.at[i], dst, pass_sem.at[2 + i]) for i, dst in enumerate((words_out, input_out))
    ]
    passed.append(pltpu.make_async_copy(right_ref, right_out, pass_sem.at[4]))
    for copy in taken:
        copy.start()
    passed[2].start()
    vec_out[...] = vec_ref[...]
    vmom_out[...] = vmom_ref[...]
    loss_out[0, 0] = loss_ref[0, 0]
    left_out[...] = jnp.concatenate([left_ref[:, i * PAIR : i * PAIR + own] for i in range(n_dp)], axis=1)
    basis_high, basis_low = split_two(left_ref[:, aligned(lax.axis_index("dp"), PAIR)][:, :own])
    for matrix, (first_col, after_col) in enumerate(matrix_bounds()):
        where = slice(matrix * rank, (matrix + 1) * rank)
        left = jnp.concatenate([basis_high[where], basis_high[where], basis_low[where]], axis=0)

        def approximate(c):
            cols = pl.ds(pl.multiple_of(first_col + c * PART, PART), PART)
            high, low = split_two(right_ref[:, cols])
            change[:, cols] = dot_tn(left, jnp.concatenate([high, low, high], axis=0))

        loop((after_col - first_col) // PART, approximate)
    for i in range(CHUNKS):
        for j in range(3):
            load(i, j).wait()

        def update(c):
            span, cols = pl.ds(i * piece, piece), aligned(c, PART)
            delta = change[span, cols]
            rows[span, cols] = rows[span, cols] - delta * (1.0 / n_rep)
            moved = MOMENTUM_DECAY * mom[span, cols] + delta
            mom[span, cols] = moved
            wts[span, cols] = wts[span, cols] - STEP_RATE * moved

        loop(rows.shape[1] // PART, update)
        for j in range(3):
            store(i, j).start()
        if i == 0:
            for k, copy in enumerate(taken):
                copy.wait()
                passed[k].start()
    for copy in passed:
        copy.wait()
    for i in range(CHUNKS):
        for j in range(3):
            store(i, j).wait()


def finish(n_dp, n_rep, rows, momentum, weights, left, right, words, grad_inputs, vectors, vector_momentum, loss):
    own, columns = rows.shape
    hbm, vmem = pl.BlockSpec(memory_space=pltpu.HBM), pl.BlockSpec(memory_space=pltpu.VMEM)
    smem = pl.BlockSpec(memory_space=pltpu.SMEM)
    full = jnp.float32
    shape = jax.ShapeDtypeStruct
    dma = pltpu.SemaphoreType.DMA
    big = shape(rows.shape, full)
    return pl.pallas_call(
        functools.partial(finish_kernel, n_dp, n_rep),
        out_shape=(
            big, big, big, shape(words.shape, full), shape(grad_inputs.shape, full),
            shape((left.shape[0], n_dp * own), full), shape(right.shape, full), shape(vectors.shape, full),
            shape(vectors.shape, full), shape((1, 1), full),
        ),
        in_specs=[hbm] * 5 + [vmem] * 4 + [smem],
        out_specs=(hbm,) * 5 + (vmem, hbm, vmem, vmem, smem),
        scratch_shapes=[pltpu.VMEM(rows.shape, full)] * 4
        + [pltpu.VMEM((2,) + words.shape, full), dma((CHUNKS, 3)), dma((CHUNKS, 3)), dma((5,))],
        compiler_params=pltpu.CompilerParams(vmem_limit_bytes=60 << 20),
        name="finish",
    )(rows, momentum, weights, words, grad_inputs, left, right, vectors, vector_momentum, loss)


def peer_at(offset, n_dp, n_rep):
    me = lax.axis_index("dp") * n_rep + lax.axis_index("rep")
    other = lax.rem(me + offset, n_dp * n_rep)
    return other, (other // n_rep, lax.rem(other, n_rep))


def meet(n_dp, n_rep):
    total = n_dp * n_rep
    barrier = pltpu.get_barrier_semaphore()

    def hello(offset, carry):
        _, peer = peer_at(offset, n_dp, n_rep)
        pl.semaphore_signal(barrier, inc=1, device_id=peer, device_id_type=MESH)
        return carry

    lax.fori_loop(1, total, hello, 0)
    pl.semaphore_wait(barrier, total - 1)


def spread_kernel(n_dp, n_rep, mine_ref, all_ref, send, recv, own_sem):
    total = n_dp * n_rep
    me = lax.axis_index("dp") * n_rep + lax.axis_index("rep")
    own = pltpu.make_async_copy(mine_ref, all_ref.at[me], own_sem)
    own.start()
    meet(n_dp, n_rep)

    def copy(offset):
        _, peer = peer_at(offset, n_dp, n_rep)
        return pltpu.make_async_remote_copy(
            src_ref=mine_ref, dst_ref=all_ref.at[me], send_sem=send.at[offset - 1],
            recv_sem=recv.at[offset - 1], device_id=peer, device_id_type=MESH,
        )

    def begin(offset, carry):
        copy(offset).start()
        return carry

    def finish(offset, carry):
        copy(offset).wait()
        return carry

    lax.fori_loop(1, total, begin, 0)
    own.wait()
    lax.fori_loop(1, total, finish, 0)


def spread(mine, n_dp, n_rep, collective, name):
    total = n_dp * n_rep
    vmem = pl.BlockSpec(memory_space=pltpu.VMEM)
    dma = pltpu.SemaphoreType.DMA
    return pl.pallas_call(
        functools.partial(spread_kernel, n_dp, n_rep),
        out_shape=jax.ShapeDtypeStruct((total,) + mine.shape, mine.dtype),
        in_specs=[vmem],
        out_specs=vmem,
        scratch_shapes=[dma((total - 1,)), dma((total - 1,)), dma],
        compiler_params=pltpu.CompilerParams(
            collective_id=collective, has_side_effects=True, vmem_limit_bytes=48 << 20
        ),
        name=name,
    )(mine)


def total_kernel(n_dp, n_rep, mine_ref, out_ref, parts, sums, send, recv, send_two, recv_two):
    total = n_dp * n_rep
    me = lax.axis_index("dp") * n_rep + lax.axis_index("rep")
    meet(n_dp, n_rep)

    def scatter(offset):
        other, peer = peer_at(offset, n_dp, n_rep)
        return pltpu.make_async_remote_copy(
            src_ref=mine_ref.at[other], dst_ref=parts.at[offset - 1], send_sem=send.at[offset - 1],
            recv_sem=recv.at[offset - 1], device_id=peer, device_id_type=MESH,
        )

    def share(offset):
        _, peer = peer_at(offset, n_dp, n_rep)
        return pltpu.make_async_remote_copy(
            src_ref=sums, dst_ref=out_ref.at[me], send_sem=send_two.at[offset - 1],
            recv_sem=recv_two.at[offset - 1], device_id=peer, device_id_type=MESH,
        )

    def start_scatter(offset, carry):
        scatter(offset).start()
        return carry

    def add(offset, carry):
        scatter(offset).wait_recv()
        return carry + parts[offset - 1]

    def start_share(offset, carry):
        share(offset).start()
        return carry

    def finish(offset, carry):
        scatter(offset).wait_send()
        share(offset).wait()
        return carry

    lax.fori_loop(1, total, start_scatter, 0)
    result = lax.fori_loop(1, total, add, mine_ref[me])
    sums[...] = result
    lax.fori_loop(1, total, start_share, 0)
    out_ref[me] = result
    lax.fori_loop(1, total, finish, 0)


def total_over_all(flat, n_dp, n_rep, collective, name):
    total = n_dp * n_rep
    count = flat.shape[0]
    chunk = -(-count // (total * 1024)) * 1024
    padded = jnp.pad(flat, (0, total * chunk - count)).reshape(total, chunk // 128, 128)
    vmem = pl.BlockSpec(memory_space=pltpu.VMEM)
    dma = pltpu.SemaphoreType.DMA
    summed = pl.pallas_call(
        functools.partial(total_kernel, n_dp, n_rep),
        out_shape=jax.ShapeDtypeStruct(padded.shape, padded.dtype),
        in_specs=[vmem],
        out_specs=vmem,
        scratch_shapes=[
            pltpu.VMEM((total - 1,) + padded.shape[1:], padded.dtype),
            pltpu.VMEM(padded.shape[1:], padded.dtype),
            dma((total - 1,)), dma((total - 1,)), dma((total - 1,)), dma((total - 1,)),
        ],
        compiler_params=pltpu.CompilerParams(
            collective_id=collective, has_side_effects=True, vmem_limit_bytes=48 << 20
        ),
        name=name,
    )(padded)
    return summed.reshape(-1)[:count]


def masked_scores(query_heads, key_heads, allowed):
    scores = (
        jnp.einsum("rshd,rthd->rhst", query_heads, key_heads, preferred_element_type=jnp.float32)
        * SCORE_SCALE
    )
    return jnp.where(allowed[:, None], scores, MASKED)


def block_forward(inputs, allowed, weights, vector_pieces, pooled_only):
    (
        gain_one, shift_one, bias_query, bias_value, bias_out,
        gain_two, shift_two, bias_shrink, bias_expand,
    ) = vector_pieces
    row_count, seq_tokens = (inputs.shape[0], inputs.shape[1])
    normed = layer_norm(inputs, gain_one, shift_one).astype(jnp.bfloat16)
    mixing = jnp.einsum("rsd,dc->rsc", normed, weights[:, : 3 * D], preferred_element_type=jnp.float32)
    mixing = mixing + jnp.concatenate([bias_query, jnp.zeros_like(bias_query), bias_value])
    head_parts = mixing.astype(jnp.bfloat16).reshape(row_count, seq_tokens, 3, HEADS, HEAD_DIM)
    query_heads, key_heads, value_heads = (head_parts[:, :, 0], head_parts[:, :, 1], head_parts[:, :, 2])
    scores = masked_scores(query_heads, key_heads, allowed)
    highest = jnp.max(scores, axis=-1, keepdims=True)
    log_total = highest + jnp.log(jnp.sum(jnp.exp(scores - highest), axis=-1, keepdims=True))
    attention = jnp.exp(scores - log_total).astype(jnp.bfloat16)
    mixed_heads = jnp.einsum("rhst,rthd->rshd", attention, value_heads, preferred_element_type=jnp.float32)
    mixed_heads = mixed_heads.reshape(row_count, seq_tokens, D).astype(jnp.bfloat16)
    attended = (
        jnp.einsum("rsd,de->rse", mixed_heads, weights[:, 3 * D : 4 * D], preferred_element_type=jnp.float32)
        + bias_out
    )
    middle = inputs + attended
    normed_two = layer_norm(middle, gain_two, shift_two).astype(jnp.bfloat16)
    hidden = (
        jnp.einsum("rsd,df->rsf", normed_two, weights[:, 4 * D : 4 * D + FF], preferred_element_type=jnp.float32)
        + bias_expand
    )
    active = jax.nn.gelu(hidden, approximate=False).astype(jnp.bfloat16)
    shrink = weights[:, 4 * D + FF :]
    if pooled_only:
        mean_active = jnp.mean(active.astype(jnp.float32), axis=1)
        high = mean_active.astype(jnp.bfloat16)
        rest = mean_active - high.astype(jnp.float32)
        low = rest.astype(jnp.bfloat16)
        lower = (rest - low.astype(jnp.float32)).astype(jnp.bfloat16)
        stacked = jnp.concatenate([high, low, lower], axis=0)
        shrunk = jnp.einsum("pf,df->pd", stacked, shrink, preferred_element_type=jnp.float32)
        shrunk = jnp.sum(shrunk.reshape(3, row_count, D), axis=0)
        return jnp.mean(middle, axis=1) + shrunk + bias_shrink
    shrunk = jnp.einsum("rsf,df->rsd", active, shrink, preferred_element_type=jnp.float32) + bias_shrink
    kept = (normed, query_heads, key_heads, value_heads, log_total, mixed_heads, middle, normed_two, hidden, active)
    return (middle + shrunk, kept)


def token_sum(values_low):
    return jnp.sum(values_low.astype(jnp.float32).reshape(-1, values_low.shape[-1]), axis=0)


def block_backward(inputs, allowed, weights, vector_pieces, forward_kept, grad_out, own_group, own_count):
    (gain_one, shift_one, _, _, _, gain_two, shift_two, _, _) = vector_pieces
    (normed, query_heads, key_heads, value_heads, log_total, mixed_heads, middle, normed_two, hidden, active) = forward_kept
    row_count, seq_tokens = (inputs.shape[0], inputs.shape[1])
    grad_shrunk = grad_out.astype(jnp.bfloat16)
    grad_active = jnp.einsum("rsd,df->rsf", grad_shrunk, weights[:, 4 * D + FF :], preferred_element_type=jnp.float32)
    _, gelu_back = jax.vjp(lambda before_gelu: jax.nn.gelu(before_gelu, approximate=False), hidden)
    grad_hidden = gelu_back(grad_active)[0].astype(jnp.bfloat16)
    grad_normed_two = jnp.einsum(
        "rsf,df->rsd", grad_hidden, weights[:, 4 * D : 4 * D + FF], preferred_element_type=jnp.float32
    )
    _, norm_two_back = jax.vjp(layer_norm, middle, gain_two, shift_two)
    grad_middle, grad_gain_two, grad_shift_two = norm_two_back(grad_normed_two)
    grad_middle = grad_middle + grad_out
    grad_attended = grad_middle.astype(jnp.bfloat16)
    grad_mixed = jnp.einsum("rse,de->rsd", grad_attended, weights[:, 3 * D : 4 * D], preferred_element_type=jnp.float32)
    grad_mixed = grad_mixed.astype(jnp.bfloat16).reshape(row_count, seq_tokens, HEADS, HEAD_DIM)
    attention = jnp.exp(masked_scores(query_heads, key_heads, allowed) - log_total)
    grad_values = jnp.einsum("rhst,rshd->rthd", attention.astype(jnp.bfloat16), grad_mixed, preferred_element_type=jnp.float32)
    grad_attention = jnp.einsum("rshd,rthd->rhst", grad_mixed, value_heads, preferred_element_type=jnp.float32)
    grad_scores = attention * (grad_attention - jnp.sum(attention * grad_attention, axis=-1, keepdims=True))
    grad_scores = grad_scores.astype(jnp.bfloat16)
    grad_query = jnp.einsum("rhst,rthd->rshd", grad_scores, key_heads, preferred_element_type=jnp.float32) * SCORE_SCALE
    grad_keys = jnp.einsum("rhst,rshd->rthd", grad_scores, query_heads, preferred_element_type=jnp.float32) * SCORE_SCALE
    grad_mixing = (
        jnp.stack([grad_query, grad_keys, grad_values], axis=2).reshape(row_count, seq_tokens, 3 * D).astype(jnp.bfloat16)
    )

    def mine(values):
        return lax.dynamic_slice_in_dim(values, own_group * own_count, own_count, 0)

    grad_normed = jnp.einsum("rsc,dc->rsd", mine(grad_mixing), weights[:, : 3 * D], preferred_element_type=jnp.float32)
    _, norm_one_back = jax.vjp(layer_norm, mine(inputs), gain_one, shift_one)
    grad_inputs, grad_gain_one, grad_shift_one = norm_one_back(grad_normed)
    grad_inputs = grad_inputs + mine(grad_middle)
    share = 1.0 / GROUP
    vector_grad = jnp.concatenate(
        [
            grad_gain_one, grad_shift_one,
            share * token_sum(grad_mixing[..., :D]), share * token_sum(grad_mixing[..., 2 * D :]),
            share * token_sum(grad_attended), share * grad_gain_two, share * grad_shift_two,
            share * token_sum(grad_shrunk), share * token_sum(grad_hidden),
        ]
    )
    tokens = row_count * seq_tokens
    outer_terms = (
        (normed.reshape(tokens, D), grad_mixing.reshape(tokens, 3 * D)),
        (mixed_heads.reshape(tokens, D), grad_attended.reshape(tokens, D)),
        (normed_two.reshape(tokens, D), grad_hidden.reshape(tokens, FF)),
        (grad_shrunk.reshape(tokens, D), active.reshape(tokens, FF)),
    )
    return (grad_inputs, vector_grad, outer_terms)


def orthonormal(stacked):
    waiting = [stacked[:, column_id] for column_id in range(stacked.shape[1])]
    finished = []
    while waiting:
        vector = waiting.pop(0)
        vector = vector / (jnp.sqrt(jnp.sum(vector * vector, axis=-1, keepdims=True)) + NORM_FLOOR)
        finished.append(vector)
        if waiting:
            later = jnp.stack(waiting, axis=1)
            later = later - jnp.sum(vector[:, None] * later, axis=-1, keepdims=True) * vector[:, None]
            waiting = [later[:, i] for i in range(later.shape[1])]
    return jnp.stack(finished, axis=1)


def rows_factor(start_part, row_block):
    return jnp.einsum("kc,dc->kd", start_part, row_block, precision=PRECISE)


def per_device(
    image_tokens, image_weights, image_vectors, text_tokens, segments, text_weights,
    text_vectors, momentum, vector_momentum, error_feedback, start_factors,
):
    n_rep, n_dp = lax.axis_size("rep"), lax.axis_size("dp")
    n_inner = n_dp // GROUP
    total = n_rep * n_dp
    device_pairs, patches = image_tokens.shape[0], image_tokens.shape[1]
    text_rows, seq_tokens = text_tokens.shape[0], text_tokens.shape[1]
    pair_total = device_pairs * total
    own_rows = text_weights.shape[0]
    d_at, r_at = lax.axis_index("dp"), lax.axis_index("rep")
    z_at, y_at = d_at // n_inner, d_at % n_inner
    row_start = d_at * own_rows
    factor_rank = start_factors.shape[0]
    bounds = matrix_bounds()
    tokens = text_tokens.reshape(text_rows * seq_tokens, D)
    feedback_rows = error_feedback[0]
    fused = (
        own_rows % (16 * LANES) == 0 and n_inner == 2 and n_rep == 4 and device_pairs == 8
        and text_rows * seq_tokens == PAIR and 2 * seq_tokens == PAIR and 2 * patches <= PAIR
        and n_dp == 8 and factor_rank == 8
    )
    if fused:
        outs = gather_and_forward(
            n_dp, n_rep, text_weights, image_weights, tokens, segments, image_tokens, text_vectors, image_vectors
        )
        pictures, captions, words, pooled, marks = outs[1:6]
        kept = (outs[0],) + tuple(outs[6:])
        worker_rows, grad_inputs, loss, left_basis, new_right, new_vectors, new_vector_momentum = backward(
            n_dp, n_rep, kept, pooled, pictures, captions, marks, tokens, text_vectors, feedback_rows, start_factors,
            vector_momentum,
        )
        (
            new_feedback, new_momentum, new_weights, words, grad_inputs, left_basis, new_right,
            new_vectors, new_vector_momentum, loss,
        ) = finish(
            n_dp, n_rep, worker_rows, momentum, text_weights, left_basis, new_right, words, grad_inputs,
            new_vectors, new_vector_momentum, loss,
        )
        return (
            loss.reshape(()), words.reshape(text_rows, seq_tokens, D), grad_inputs.reshape(text_rows, seq_tokens, D),
            new_weights, new_momentum, new_feedback[None], new_vectors.reshape(-1), new_vector_momentum.reshape(-1),
            left_basis, new_right,
        )
    text_low, frozen, token_group, segment_group = gather_weights(
        n_dp, text_weights.astype(jnp.bfloat16), image_weights, tokens, segments
    )
    text_low, frozen = text_low.reshape(D, -1), frozen.reshape(D, -1)
    full_mask = jnp.zeros((device_pairs, patches, patches), jnp.int32) == 0
    image_pooled = block_forward(
        image_tokens.astype(jnp.float32), full_mask, frozen, vector_parts(image_vectors), True
    )
    group_rows = GROUP * text_rows
    text_float = token_group.reshape(group_rows, seq_tokens, D).astype(jnp.float32)
    segment_all = segment_group.reshape(group_rows, seq_tokens)
    allowed = segment_all[:, :, None] == segment_all[:, None, :]
    vector_pieces = vector_parts(text_vectors)
    group_output, forward_kept = block_forward(text_float, allowed, text_low, vector_pieces, False)
    text_output = lax.dynamic_slice_in_dim(group_output, z_at * text_rows, text_rows, 0)
    caption_marks = (
        segment_all[:, None, :] == jnp.arange(PER_ROW, dtype=jnp.int32)[None, :, None]
    ).astype(jnp.float32)
    counts = jnp.sum(caption_marks, axis=-1, keepdims=True)
    pooled = (jnp.einsum("rks,rsd->rkd", caption_marks, group_output, precision=PRECISE) / counts).reshape(-1, D)
    image_emb = unit_rows(image_pooled).astype(jnp.bfloat16)
    text_norm, embed_back = jax.vjp(unit_rows, pooled)
    text_emb = text_norm.astype(jnp.bfloat16)
    own_emb = lax.dynamic_slice_in_dim(text_emb, z_at * device_pairs, device_pairs, 0)
    embeddings = spread(jnp.concatenate([image_emb, own_emb], axis=0), n_dp, n_rep, 2, "spread_embeddings")
    image_all = embeddings[:, :device_pairs].reshape(pair_total, D)
    text_all = embeddings[:, device_pairs:].reshape(pair_total, D)
    own_pairs = (
        ((jnp.arange(GROUP, dtype=jnp.int32) * n_inner + y_at) * n_rep + r_at)[:, None] * device_pairs
        + jnp.arange(device_pairs, dtype=jnp.int32)[None, :]
    ).reshape(-1)
    logits = LOGIT_SCALE * jnp.einsum("pd,bd->pb", image_all, text_all, preferred_element_type=jnp.float32)
    image_top = jnp.max(logits, axis=1)
    image_log_total = image_top + jnp.log(jnp.sum(jnp.exp(logits - image_top[:, None]), axis=1))
    caption_top = jnp.max(logits, axis=0)
    caption_log_total = caption_top + jnp.log(jnp.sum(jnp.exp(logits - caption_top[None, :]), axis=0))
    pair_ids = jnp.arange(pair_total, dtype=jnp.int32)
    matched = jnp.sum(jnp.where(pair_ids[:, None] == pair_ids[None, :], logits, 0.0), axis=1)
    loss_total = (jnp.sum(image_log_total - matched) + jnp.sum(caption_log_total - matched)) / (2.0 * pair_total)
    diagonal_pick = (pair_ids[None, :] == own_pairs[:, None]).astype(jnp.float32)
    text_logits = LOGIT_SCALE * jnp.einsum("pd,bd->pb", text_emb, image_all, preferred_element_type=jnp.float32)
    text_top = jnp.max(text_logits, axis=1, keepdims=True)
    text_log_total = text_top + jnp.log(jnp.sum(jnp.exp(text_logits - text_top), axis=1, keepdims=True))
    text_soft = ((jnp.exp(text_logits - text_log_total) - diagonal_pick) * 0.5).astype(jnp.bfloat16)
    column_soft = ((jnp.exp(text_logits - image_log_total[None, :]) - diagonal_pick) * 0.5).astype(jnp.bfloat16)
    grad_text = LOGIT_SCALE * (
        jnp.einsum("pb,bd->pd", text_soft, image_all, preferred_element_type=jnp.float32)
        + jnp.einsum("pb,bd->pd", column_soft, image_all, preferred_element_type=jnp.float32)
    )
    grad_pooled = embed_back(grad_text)[0]
    grad_pooled = grad_pooled.reshape(-1, PER_ROW, D) / counts
    grad_out = jnp.einsum("rks,rkd->rsd", caption_marks, grad_pooled, precision=PRECISE)
    grad_inputs, vector_grad, outer_terms = block_backward(
        text_float, allowed, text_low, vector_pieces, forward_kept, grad_out, z_at, text_rows
    )
    group_width = n_inner * own_rows
    worker_blocks = []
    for (left_side, right_side), (first_col, after_col) in zip(outer_terms, bounds):
        left_cut = lax.dynamic_slice_in_dim(left_side, z_at * group_width, group_width, 1)
        block = jnp.einsum("tc,tk->ck", left_cut, right_side, preferred_element_type=jnp.float32)
        mine = lax.dynamic_slice_in_dim(block, y_at * own_rows, own_rows, 0)
        for k in range(1, n_inner):
            target = lax.rem(y_at + k, n_inner)
            outgoing = lax.dynamic_slice_in_dim(block, target * own_rows, own_rows, 0).astype(jnp.bfloat16)
            pairs = [
                (z * n_inner + y, z * n_inner + (y + k) % n_inner) for z in range(GROUP) for y in range(n_inner)
            ]
            mine = mine + lax.ppermute(outgoing, "dp", pairs).astype(jnp.float32)
        worker_blocks.append(mine + feedback_rows[:, first_col:after_col])
    factor_rows = jnp.concatenate(
        [
            rows_factor(start_factors[:, first_col:after_col], rows)
            for rows, (first_col, after_col) in zip(worker_blocks, bounds)
        ],
        axis=0,
    )
    gathered_rows = spread(factor_rows, n_dp, n_rep, 3, "spread_factors")
    factor = jnp.sum(gathered_rows.reshape(n_dp, n_rep, 4 * factor_rank, own_rows), axis=1)
    factor = jnp.swapaxes(factor, 0, 1).reshape(4, factor_rank, D)
    left_basis = orthonormal(factor).reshape(4 * factor_rank, D)
    basis_rows = lax.dynamic_slice_in_dim(left_basis, row_start, own_rows, 1)
    basis_parts = [basis_rows[i * factor_rank : (i + 1) * factor_rank] for i in range(4)]
    right_part = jnp.concatenate(
        [jnp.einsum("kd,dc->kc", part, rows, precision=PRECISE) for part, rows in zip(basis_parts, worker_blocks)],
        axis=1,
    )
    summed = total_over_all(
        jnp.concatenate([right_part.reshape(-1), vector_grad]), n_dp, n_rep, 4, "total_right"
    )
    new_right = summed[: right_part.size].reshape(right_part.shape)
    vector_total = summed[right_part.size :]
    approximation = jnp.concatenate(
        [
            jnp.einsum("kd,kc->dc", part, new_right[:, first_col:after_col], precision=PRECISE)
            for part, (first_col, after_col) in zip(basis_parts, bounds)
        ],
        axis=1,
    )
    worker_rows = jnp.concatenate(worker_blocks, axis=1)
    new_feedback = (worker_rows - approximation / n_rep)[None]
    new_momentum = MOMENTUM_DECAY * momentum + approximation
    new_weights = text_weights - STEP_RATE * new_momentum
    new_vector_momentum = MOMENTUM_DECAY * vector_momentum + vector_total
    new_vectors = text_vectors - STEP_RATE * new_vector_momentum
    return (
        loss_total, text_output, grad_inputs, new_weights, new_momentum, new_feedback,
        new_vectors, new_vector_momentum, left_basis, new_right,
    )


def solution(mesh):
    placed = (
        P(("dp", "rep"), None, None), P("dp", None), P(), P(("dp", "rep"), None, None), P(("dp", "rep"), None),
        P("dp", None), P(), P("dp", None), P(), P("rep", "dp", None), P(),
    )
    return jax.shard_map(
        per_device,
        mesh=mesh,
        in_specs=placed,
        out_specs=(
            P(), P(("dp", "rep"), None, None), P(("dp", "rep"), None, None), P("dp", None), P("dp", None),
            P("rep", "dp", None), P(), P(), P(), P(),
        ),
        check_vma=False,
    )
```

```python
import functools

import jax
import jax.numpy as jnp
from jax import lax
from jax.experimental import pallas as pl
from jax.experimental.pallas import tpu as pltpu
from jax.sharding import PartitionSpec as P

D = 768
FF = 3072
HEADS = 12
HEAD_DIM = 64
PER_ROW = 4
GROUP = 4
SECTION = 3072
LANE_COLS = 512

PRECISE = lax.Precision.HIGHEST
LAYER_EPS = 1e-06
SCORE_SCALE = 0.125
LOGIT_SCALE = 50.0
MOMENTUM_DECAY = 0.9
STEP_RATE = 0.08
NORM_FLOOR = 1e-08
MASKED = -1e30
MESH = pl.DeviceIdType.MESH


def layer_norm(values, layer_gain, layer_shift):
    center = values - jnp.mean(values, axis=-1, keepdims=True)
    spread = jnp.mean(center * center, axis=-1, keepdims=True)
    return center * lax.rsqrt(spread + LAYER_EPS) * layer_gain + layer_shift


def unit_rows(values):
    return values * lax.rsqrt(jnp.sum(values * values, axis=-1, keepdims=True) + LAYER_EPS)


def vector_parts(vectors):
    pieces = [vectors[position * D : (position + 1) * D] for position in range(8)]
    return pieces + [vectors[8 * D :]]


def matrix_bounds():
    return ((0, 3 * D), (3 * D, 4 * D), (4 * D, 4 * D + FF), (4 * D + FF, 4 * D + 2 * FF))


def gather_kernel(
    n_dp, text_ref, image_ref, tok_ref, seg_ref, wt_ref, wi_ref, tok_out, seg_out,
    z_send, z_recv, y_send, y_recv, x_send, x_recv, c_send, c_recv, t_send, t_recv, t_own, own_sem,
):
    n_inner = n_dp // GROUP
    d_at, r_at = lax.axis_index("dp"), lax.axis_index("rep")
    z_at, y_at = d_at // n_inner, d_at % n_inner
    x_at, c_at = r_at // 2, r_at % 2
    z_peers = [(lax.rem(z_at + k, GROUP) * n_inner + y_at, r_at) for k in range(1, GROUP)]
    z_from = [lax.rem(z_at + GROUP - k, GROUP) for k in range(1, GROUP)]
    y_peers = [(z_at * n_inner + lax.rem(y_at + k, n_inner), r_at) for k in range(1, n_inner)]
    y_from = [lax.rem(y_at + n_inner - k, n_inner) for k in range(1, n_inner)]
    x_peer = (d_at, (1 - x_at) * 2 + c_at)
    c_peer = (d_at, x_at * 2 + 1 - c_at)

    barrier = pltpu.get_barrier_semaphore()
    everyone = z_peers + y_peers + [x_peer, c_peer]
    for peer in everyone:
        pl.semaphore_signal(barrier, inc=1, device_id=peer, device_id_type=MESH)
    pl.semaphore_wait(barrier, len(everyone))

    def shard_of(z, y):
        return z * n_inner + y

    sections = [(image_ref, wi_ref, 0), (text_ref, wt_ref, 0), (image_ref, wi_ref, 1),
                (text_ref, wt_ref, 1), (image_ref, wi_ref, 2), (text_ref, wt_ref, 2)]

    def cols(section, lane):
        start = sections[section][2] * SECTION + lane * LANE_COLS
        return pl.ds(pl.multiple_of(start, 128), LANE_COLS)

    lane_both = c_at
    lane_mine = 2 + x_at * 2 + c_at
    lane_theirs = 2 + (1 - x_at) * 2 + c_at
    lanes = (lane_both, lane_mine)

    locals_ = [
        pltpu.make_async_copy(tok_ref, tok_out.at[z_at], t_own.at[0]),
        pltpu.make_async_copy(seg_ref, seg_out.at[z_at], t_own.at[1]),
    ]
    for s, (src, full, _) in enumerate(sections):
        for j in range(2):
            column = cols(s, lanes[j])
            locals_.append(pltpu.make_async_copy(src.at[:, column], full.at[d_at, :, column], own_sem.at[s, j]))
    for copy in locals_:
        copy.start()

    def remote(src, dst, send, recv, peer):
        return pltpu.make_async_remote_copy(
            src_ref=src, dst_ref=dst, send_sem=send, recv_sem=recv, device_id=peer, device_id_type=MESH
        )

    def z_copy(s, k, j):
        src, full, _ = sections[s]
        return remote(
            src.at[:, cols(s, lanes[j])], full.at[d_at, :, cols(s, lanes[j])],
            z_send.at[s, k, j], z_recv.at[s, k, j], z_peers[k],
        )

    def y_copy(s, q, zi, j):
        src, full, _ = sections[s]
        column = cols(s, lanes[j])
        if zi == 0:
            shard, source = d_at, src.at[:, column]
        else:
            shard = shard_of(z_from[zi - 1], y_at)
            source = full.at[shard, :, column]
        return remote(source, full.at[shard, :, column], y_send.at[s, q, zi, j], y_recv.at[s, q, zi, j], y_peers[q])

    def x_copy(s):
        full = sections[s][1]
        block = full.at[:, :, cols(s, lane_mine)]
        return remote(block, block, x_send.at[s], x_recv.at[s], x_peer)

    def c_copy(s, j):
        full = sections[s][1]
        block = full.at[:, :, cols(s, (lane_both, lane_mine, lane_theirs)[j])]
        return remote(block, block, c_send.at[s, j], c_recv.at[s, j], c_peer)

    count = len(sections)
    tokens = []
    for k in range(GROUP - 1):
        tokens.append(remote(tok_ref, tok_out.at[z_at], t_send.at[0, k], t_recv.at[0, k], z_peers[k]))
        tokens.append(remote(seg_ref, seg_out.at[z_at], t_send.at[1, k], t_recv.at[1, k], z_peers[k]))

    def begin(s):
        for j in range(2):
            for k in range(GROUP - 1):
                z_copy(s, k, j).start()
            for q in range(n_inner - 1):
                y_copy(s, q, 0, j).start()

    begin(0)
    for copy in tokens:
        copy.start()
    for copy in locals_:
        copy.wait()
    begin(1)
    for step in range(count + 3):
        if step < count:
            for k in range(GROUP - 1):
                for j in range(2):
                    z_copy(step, k, j).wait_recv()
                    for q in range(n_inner - 1):
                        y_copy(step, q, k + 1, j).start()
            if step + 2 < count:
                begin(step + 2)
        s = step - 1
        if 0 <= s < count:
            for q in range(n_inner - 1):
                for zi in range(GROUP):
                    for j in range(2):
                        y_copy(s, q, zi, j).wait_recv()
            x_copy(s).start()
            for j in range(2):
                c_copy(s, j).start()
        s = step - 2
        if 0 <= s < count:
            x_copy(s).wait_recv()
            c_copy(s, 2).start()
        s = step - 3
        if 0 <= s < count:
            for j in range(3):
                c_copy(s, j).wait_recv()
    for copy in tokens:
        copy.wait()
    for s in range(count):
        for j in range(2):
            for k in range(GROUP - 1):
                z_copy(s, k, j).wait_send()
            for q in range(n_inner - 1):
                for zi in range(GROUP):
                    y_copy(s, q, zi, j).wait_send()
        x_copy(s).wait_send()
        for j in range(3):
            c_copy(s, j).wait_send()


def gather_weights(n_dp, text_low, image_low, tokens, segments):
    n_inner = n_dp // GROUP
    full = jax.ShapeDtypeStruct((n_dp,) + text_low.shape, jnp.bfloat16)
    hbm = pl.BlockSpec(memory_space=pltpu.HBM)
    dma = pltpu.SemaphoreType.DMA
    return pl.pallas_call(
        functools.partial(gather_kernel, n_dp),
        out_shape=(
            full,
            full,
            jax.ShapeDtypeStruct((GROUP,) + tokens.shape, jnp.bfloat16),
            jax.ShapeDtypeStruct((GROUP,) + segments.shape, jnp.int32),
        ),
        in_specs=[hbm] * 4,
        out_specs=(hbm,) * 4,
        scratch_shapes=[
            dma((6, GROUP - 1, 2)), dma((6, GROUP - 1, 2)),
            dma((6, n_inner - 1, GROUP, 2)), dma((6, n_inner - 1, GROUP, 2)),
            dma((6,)), dma((6,)), dma((6, 3)), dma((6, 3)),
            dma((2, GROUP - 1)), dma((2, GROUP - 1)), dma((2,)), dma((6, 2)),
        ],
        compiler_params=pltpu.CompilerParams(collective_id=1, has_side_effects=True),
        name="gather_weights",
    )(text_low, image_low, tokens, segments)


TILE = 256
PAIR = 128
ROWS = 32
LANES = 6
PART = 768
PARTS = 12
DEPTH = 8
AHEAD = 2
OWN_AHEAD = 4
TOKENS_AT = 6
STEP_TIME = 4.6
LAG_Z = 1
LAG_Y = 1
LAG_X = 2
LAG_C = 1
AT_Y = 2 * LAG_Z + LAG_Y
AT_X = AT_Y + LAG_X
AT_C = AT_X + LAG_C
WORDS = (GROUP * PAIR)


def piece_of(vec_ref, index, width=D):
    return vec_ref[:, pl.ds(index * D, width)]


def loop(count, body, unroll=1):
    def step(i, carry):
        body(i)
        return carry

    lax.fori_loop(0, count, step, 0, unroll=unroll)


def aligned(i, size):
    return pl.ds(pl.multiple_of(i * size, size), size)


def norm_rows(values):
    center = values - jnp.mean(values, axis=-1, keepdims=True)
    spread_ = jnp.mean(center * center, axis=-1, keepdims=True)
    return center * lax.rsqrt(spread_ + LAYER_EPS)


def dot(left, right):
    return jnp.dot(left, right, preferred_element_type=jnp.float32)


def dot_nt(left, right):
    return lax.dot_general(left, right, (((1,), (1,)), ((), ())), preferred_element_type=jnp.float32)


def dot_tn(left, right):
    return lax.dot_general(left, right, (((0,), (0,)), ((), ())), preferred_element_type=jnp.float32)


def lane_is_first():
    return lax.broadcasted_iota(jnp.int32, (PAIR, PAIR), 1) < HEAD_DIM


def two_heads(block):
    first = lane_is_first()
    zero = jnp.zeros_like(block)
    return jnp.concatenate([jnp.where(first, block, zero), jnp.where(first, zero, block)], axis=0)


def attention_forward(qkv, mixed, chance, allowed_of, first, count):
    pairs = HEADS // 2

    def body(k):
        at = first + k
        i, j = at // pairs, lax.rem(at, pairs)
        rows = aligned(i, PAIR)
        query = qkv[rows, aligned(j, PAIR)]
        key = qkv[rows, pl.ds(pl.multiple_of(D + j * PAIR, PAIR), PAIR)]
        value = qkv[rows, pl.ds(pl.multiple_of(2 * D + j * PAIR, PAIR), PAIR)]
        scores = dot_nt(two_heads(query), key) * SCORE_SCALE
        allowed = allowed_of(i)
        scores = jnp.where(jnp.concatenate([allowed, allowed], axis=0), scores, MASKED)
        scores = jnp.exp(scores - jnp.max(scores, axis=-1, keepdims=True))
        weight = scores / jnp.sum(scores, axis=-1, keepdims=True)
        if chance is not None:
            chance[at] = weight
        low = weight.astype(jnp.bfloat16)
        side = jnp.concatenate([low[:PAIR], low[PAIR:]], axis=1)
        mixed[rows, aligned(j, PAIR)] = dot(side, two_heads(value)).astype(jnp.bfloat16)

    loop(count, body, unroll=2)


def forward_kernel(
    n_dp, n_rep, patches,
    text_ref, image_ref, tok_ref, pic_ref, seg_ref, tvec_ref, ivec_ref,
    wt_out, pic_all, cap_all, words_out, text_pool_out, marks_out, qkv_out, chance_out, mid_out, slope_out,
    act_out, nt_out, at_out, mt_out,
    wi_ref, wt_vmem, tok, seg_col, seg_row, normed, qkv, mixed, middle, normed_two, active, slope, chance, total, hid, turned, apool, image_pool_out, patches_in, padded, master,
    z_send, z_recv, y_send, y_recv, x_send, x_recv, c_send, c_recv, t_send, t_recv, t_own, own_sem, w_sem, out_sem, p_send, p_recv, g_send, g_recv,
):
    n_inner = n_dp // GROUP
    d_at, r_at = lax.axis_index("dp"), lax.axis_index("rep")
    z_at, y_at = d_at // n_inner, lax.rem(d_at, n_inner)
    x_at, c_at = r_at // 2, lax.rem(r_at, 2)
    z_next = [((z_at - 1) * n_inner + y_at, r_at), ((z_at + 1) * n_inner + y_at, r_at)]
    y_peers = [(z_at * n_inner + 1 - y_at, r_at)]
    x_peer = (d_at, (1 - x_at) * 2 + c_at)
    c_peer = (d_at, x_at * 2 + 1 - c_at)

    devices = n_dp * n_rep
    me = d_at * n_rep + r_at
    z_open = (z_at > 0, z_at < GROUP - 1)
    barrier = pltpu.get_barrier_semaphore()

    def hello(peer):
        pl.semaphore_signal(barrier, inc=1, device_id=peer, device_id_type=MESH)

    for peer in (y_peers[0], x_peer, c_peer):
        hello(peer)
    for up in range(2):
        pl.when(z_open[up])(functools.partial(hello, z_next[up]))

    sections = [(image_ref, wi_ref, k) for k in range(PARTS)] + [(text_ref, wt_vmem, k) for k in range(PARTS)]
    count = len(sections)
    lane_mine = c_at * 3 + 2 * x_at
    lane_theirs = c_at * 3 + 2 * (1 - x_at)
    lanes_two = pl.ds(c_at * 3 + x_at, 2)
    lanes_three = pl.ds(c_at * 3, 3)

    def remote(src, dst, send, recv, peer):
        return pltpu.make_async_remote_copy(
            src_ref=src, dst_ref=dst, send_sem=send, recv_sem=recv, device_id=peer, device_id_type=MESH
        )

    def cols(s):
        return pl.ds(sections[s][2] * PART, PART)

    def set_of(s):
        return s // PARTS

    def size_of(s, shards, lanes_):
        return sections[s][1].at[sections[s][2], pl.ds(0, shards), pl.ds(0, lanes_)]

    def all_size(group, shards, lanes_):
        return sections[group * PARTS][1].at[:, pl.ds(0, shards), pl.ds(0, lanes_)]

    def landed(block, recv, peer):
        remote(block, block, x_send.at[0], recv, peer).wait_recv()

    def gone(block, send, peer):
        remote(block, block, send, x_recv.at[0], peer).wait_send()

    def held(s, shard, lane):
        _, full, k = sections[s]
        return full.at[k, shard, lane]

    def z_copy(s, up, hop):
        unit = z_at - hop if up else z_at + hop
        shard = unit * n_inner + y_at
        return remote(
            held(s, shard, lanes_two), held(s, shard, lanes_two),
            z_send.at[set_of(s), up, hop], z_recv.at[s, unit], z_next[up],
        )

    def y_copy(s, unit):
        shard = unit * n_inner + y_at
        return remote(
            held(s, shard, lanes_two), held(s, shard, lanes_two),
            y_send.at[set_of(s)], y_recv.at[s], y_peers[0],
        )

    def x_copy(s, unit):
        block = held(s, pl.ds(unit * n_inner, n_inner), lane_mine)
        return remote(block, block, x_send.at[set_of(s)], x_recv.at[s], x_peer)

    def x_own_copy(s):
        block = held(s, z_at * n_inner + 1 - y_at, lane_mine)
        return remote(block, block, x_send.at[set_of(s)], x_recv.at[s], x_peer)

    def c_copy(s, j):
        block = held(s, slice(None), (lanes_two, lane_theirs)[j])
        return remote(block, block, c_send.at[set_of(s)], c_recv.at[s], c_peer)

    def store(s):
        return pltpu.make_async_copy(wt_vmem.at[s - PARTS], wt_out.at[s - PARTS], w_sem.at[s - PARTS])

    def own_shard(s):
        src, _, _ = sections[s]
        return pltpu.make_async_copy(
            src.at[lanes_three, :, cols(s)], held(s, d_at, lanes_three) if s < PARTS else master.at[s % 4], own_sem.at[s]
        )

    def own_ready(s):
        own_shard(s).wait()
        if s >= PARTS:
            wt_vmem[s - PARTS, d_at, lanes_three] = master[s % 4].astype(jnp.bfloat16)

    gathered = ((tok_ref, tok), (None, seg_row))
    firsts = [
        pltpu.make_async_copy(tok_ref, tok.at[z_at], t_own.at[0]),
        pltpu.make_async_copy(pic_ref, patches_in, t_own.at[1]),
    ]

    def token_copy(i, up, hop):
        unit = z_at - hop if up else z_at + hop
        block = gathered[i][1].at[unit]
        return remote(block, block, t_send.at[i, up, hop], t_recv.at[i, unit], z_next[up])

    def token_begin():
        firsts[0].wait()
        number = seg_ref[...].astype(jnp.float32)
        number = jnp.concatenate([number[0:1, :], number[1:2, :] + PER_ROW], axis=1)
        seg_row[z_at] = jnp.broadcast_to(number, (16, PAIR)).astype(jnp.bfloat16)
        for i in range(2):
            for up in range(2):
                pl.when(z_open[up])(token_copy(i, up, 0).start)

    def token_arrive(hop):
        for up in range(2):
            unit = z_at - hop if up else z_at + hop

            @pl.when((unit >= 0) & (unit < GROUP))
            def _():
                for i in range(2):
                    block = gathered[i][1].at[0]
                    landed(block, t_recv.at[i, unit], z_next[up])
                    if hop < GROUP - 1:
                        pl.when(z_open[up])(token_copy(i, up, hop).start)

    def token_gone():
        for up in range(2):
            for hop in range(GROUP - 1):
                unit = z_at - hop if up else z_at + hop
                for i in range(2):
                    pl.when((unit >= 0) & (unit < GROUP) & z_open[up])(
                        functools.partial(gone, gathered[i][1].at[0], t_send.at[i, up, hop], z_next[up])
                    )

    def picture_copy(offset):
        _, other = peer_at(offset, n_dp, n_rep)
        return remote(pic_all.at[me], pic_all.at[me], p_send.at[offset - 1], p_recv.at[offset - 1], other)

    def send_pictures():
        values = image_pool_out[...]
        squares = jnp.sum(values * values, axis=-1, keepdims=True)
        pic_all[me] = (values * lax.rsqrt(squares + LAYER_EPS)).astype(jnp.bfloat16)

        def start(offset, carry):
            picture_copy(offset).start()
            return carry

        lax.fori_loop(1, devices, start, 0)

    near = n_inner * n_rep

    def caption_copy(k):
        other = lax.rem(y_at * n_rep + r_at + k, near)
        block = cap_all.at[:, y_at * n_rep + r_at]
        peer_ = (z_at * n_inner + other // n_rep, lax.rem(other, n_rep))
        return remote(block, block, g_send.at[k - 1], g_recv.at[k - 1], peer_)

    def send_captions():
        for i in range(GROUP):
            values = text_pool_out[pl.ds(i * 8, 8), :]
            squares = jnp.sum(values * values, axis=-1, keepdims=True)
            cap_all[i, y_at * n_rep + r_at] = (values * lax.rsqrt(squares + LAYER_EPS)).astype(jnp.bfloat16)
        for k in range(1, near):
            caption_copy(k).start()

    def end_pictures():
        def end(offset, carry):
            picture_copy(offset).wait()
            return carry

        lax.fori_loop(1, devices, end, 0)

    def begin(s):
        own_ready(s)
        for up in range(2):
            pl.when(z_open[up])(z_copy(s, up, 0).start)
        y_copy(s, z_at).start()

    def arrive(s, hop):
        for up in range(2):
            unit = z_at - hop if up else z_at + hop

            @pl.when((unit >= 0) & (unit < GROUP))
            def _():
                landed(size_of(s, 1, 2), z_recv.at[s, unit], z_next[up])
                if hop < GROUP - 1:
                    pl.when(z_open[up])(z_copy(s, up, hop).start)
                y_copy(s, unit).start()

    def own_start(s):
        own_shard(s).start()

    def stage_y(s):
        landed(size_of(s, GROUP, 2), y_recv.at[s], y_peers[0])
        for unit in range(GROUP):
            pl.when(unit != z_at)(x_copy(s, unit).start)
        x_own_copy(s).start()
        c_copy(s, 0).start()

    def stage_x(s):
        landed(size_of(s, n_dp - 1, 1), x_recv.at[s], x_peer)
        c_copy(s, 1).start()

    def stage_c(s):
        landed(size_of(s, n_dp, 3), c_recv.at[s], c_peer)
        if s >= PARTS:
            store(s).start()

    def carry_on(step):
        moves = []
        if step + OWN_AHEAD < count:
            moves.append(functools.partial(own_start, step + OWN_AHEAD))
        if step + AHEAD < count:
            moves.append(functools.partial(begin, step + AHEAD))
        for hop in range(1, GROUP):
            s = step - (hop - 1) * LAG_Z
            if 0 <= s < count:
                moves.append(functools.partial(arrive, s, hop))
        for lag, stage in ((AT_Y, stage_y), (AT_X, stage_x), (AT_C, stage_c)):
            if 0 <= step - lag < count:
                moves.append(functools.partial(stage, step - lag))
        if step == TOKENS_AT:
            moves.append(token_begin)
        for hop in range(1, GROUP):
            if step == TOKENS_AT + 2 * hop:
                moves.append(functools.partial(token_arrive, hop))
        return moves


    def weight_tile(s, c):
        _, full, k = sections[s]
        return full[k, :, :, :, aligned(c, TILE)].reshape(D, TILE)

    def weight_rows(s, half):
        _, full, k = sections[s]
        return full[k, pl.ds(half * (n_dp // 2), n_dp // 2)].reshape(D // 2, PART)

    def split_loop(total_, pieces, cost, body):
        size = total_ // pieces
        return [
            (cost, functools.partial(loop, size, functools.partial(lambda base, i: body(base + i), p * size)))
            for p in range(pieces)
        ]

    def first_norm(read, vec):
        def body(i):
            rows = aligned(i, ROWS)
            value = norm_rows(read(i).astype(jnp.float32))
            normed[rows, :] = (value * piece_of(vec, 0) + piece_of(vec, 1)).astype(jnp.bfloat16)

        return split_loop(WORDS // ROWS, 4, 0.5, body)

    def project(slot, part, bias):
        def body(c):
            out = dot(normed[...], weight_tile(slot, c))
            if bias is not None:
                out = out + bias[0][:, pl.ds(pl.multiple_of(bias[1] * D + c * TILE, TILE), TILE)]
            qkv[:, pl.ds(pl.multiple_of(part * D + c * TILE, TILE), TILE)] = out.astype(jnp.bfloat16)

        return split_loop(PART // TILE, 3, 0.6, body)

    def attend(slot, read, vec):
        def body(c):
            where = aligned(c, TILE)
            middle[:, where] = dot(mixed[...], weight_tile(slot, c)) + vec[
                :, pl.ds(pl.multiple_of(4 * D + c * TILE, TILE), TILE)
            ]

        def norm(i):
            rows = aligned(i, ROWS)
            value = middle[rows, :] + read(i).astype(jnp.float32)
            middle[rows, :] = value
            normed_two[rows, :] = (norm_rows(value) * piece_of(vec, 5) + piece_of(vec, 6)).astype(jnp.bfloat16)

        return split_loop(PART // TILE, 3, 0.6, body) + split_loop(WORDS // ROWS, 4, 0.6, norm)

    def expand(slot, part, vec, keep):
        def one(c, p):
            start = part * PART + c * TILE
            if p == 0:
                hid[...] = dot(normed_two[...], weight_tile(slot, c)) + vec[:, pl.ds(8 * D + start, TILE)]

            def inner(i):
                rows = aligned(i + p * (WORDS // ROWS // 2), ROWS)
                value = hid[rows, :]
                phi = 0.5 + 0.5 * lax.erf(value * 0.7071067811865476)
                active[rows, pl.ds(start, TILE)] = (value * phi).astype(jnp.bfloat16)
                if keep:
                    slope[rows, pl.ds(start, TILE)] = phi + value * (
                        0.3989422804014327 * jnp.exp(-0.5 * value * value)
                    )

            loop(WORDS // ROWS // 2, inner, unroll=2)

        return [
            (1.2 - 0.4 * p + 0.2 * keep, functools.partial(one, c, p)) for c in range(PART // TILE) for p in range(2)
        ]

    def shrink(slot, part, vec):
        def one(half):
            where = pl.ds(half * (D // 2), D // 2)
            out = dot_nt(active[:, pl.ds(part * PART, PART)], weight_rows(slot, half))
            if part == 0:
                total[:, where] = out + middle[:, where] + vec[:, pl.ds(7 * D + half * (D // 2), D // 2)]
            else:
                total[:, where] += out

        return [(0.8, functools.partial(one, half)) for half in range(2)]

    def attention(chance_, allowed_of):
        pairs_ = GROUP * HEADS // 2
        return [
            (1.2, functools.partial(attention_forward, qkv, mixed, chance_, allowed_of, first, 4))
            for first in range(0, pairs_, 4)
        ]

    def turn(source, slot, out):
        def body(c):
            turned[slot, aligned(c, PAIR), :] = source[:, aligned(c, PAIR)].T

        loop(D // PAIR, body)
        send_out(turned.at[slot, group_rows], out)

    outs = []

    def send_out(src, dst):
        copy = pltpu.make_async_copy(src, dst, out_sem.at[len(outs)])
        copy.start()
        outs.append(copy)

    group_rows = pl.ds(pl.multiple_of(z_at * (D // GROUP), D // GROUP), D // GROUP)

    def text_read(i):
        per = PAIR // ROWS
        return tok[i // per, aligned(lax.rem(i, per), ROWS), :]

    def text_allowed(i):
        row = seg_row[i].astype(jnp.float32)
        return seg_col[i] == row[0:1, :]

    def text_columns():
        for i in range(GROUP):
            row = seg_row[i].astype(jnp.float32)[0:1, :]
            seg_col[i] = jnp.broadcast_to(row, (PAIR, PAIR)).T

    def image_read(i):
        return padded[aligned(i, ROWS), :]

    def picture(axis):
        at = lax.broadcasted_iota(jnp.int32, (PAIR, PAIR), axis)
        number = at // (PAIR // 2)
        return jnp.where(lax.rem(at, PAIR // 2) < patches, number, number + 2)

    def image_allowed(i):
        return picture(0) == picture(1)

    def keep_mark():
        image = lax.broadcasted_iota(jnp.int32, (GROUP * 2, WORDS), 0)
        at = lax.broadcasted_iota(jnp.int32, (GROUP * 2, WORDS), 1)
        inside = (at // (PAIR // 2) == image) & (lax.rem(at, PAIR // 2) < patches)
        return jnp.where(inside, 1.0, 0.0)

    def text_pool():
        send_out(total.at[aligned(z_at, PAIR)], words_out)
        for i in range(GROUP):
            row = seg_row[i].astype(jnp.float32)[0:8, :]
            marks = jnp.where(row == lax.broadcasted_iota(jnp.int32, (8, PAIR), 0).astype(jnp.float32), 1.0, 0.0)
            marks_out[i] = marks
            marks_low = marks.astype(jnp.bfloat16)
            value = total[pl.ds(i * PAIR, PAIR), :]
            high = value.astype(jnp.bfloat16)
            rest = value - high.astype(jnp.float32)
            low = rest.astype(jnp.bfloat16)
            lower = (rest - low.astype(jnp.float32)).astype(jnp.bfloat16)
            sums = dot(
                jnp.concatenate([marks_low] * 3, axis=1), jnp.concatenate([high, low, lower], axis=0)
            )
            text_pool_out[pl.ds(i * 8, 8), :] = sums / jnp.sum(marks, axis=1, keepdims=True)

    def text_part(k):
        slot = k + PARTS
        if k == 0:
            return (
                [(0.3, text_columns)] + first_norm(text_read, tvec_ref) + project(slot, 0, (tvec_ref, 2))
                + [(0.8, lambda: turn(normed, 0, nt_out))]
            )
        if k == 1:
            return project(slot, 1, None)
        if k == 2:
            return (
                project(slot, 2, (tvec_ref, 3)) + [(0.1, lambda: send_out(qkv, qkv_out))]
                + attention(chance, text_allowed)
                + [(0.1, lambda: send_out(chance, chance_out)), (0.8, lambda: turn(mixed, 1, at_out))]
            )
        if k == 3:
            return attend(slot, text_read, tvec_ref) + [
                (0.1, lambda: send_out(middle, mid_out)), (0.8, lambda: turn(normed_two, 2, mt_out))
            ]
        if k < 8:
            return expand(slot, k - 4, tvec_ref, True)
        pieces = shrink(slot, k - 8, tvec_ref)
        if k == 10:
            pieces = pieces + [(1.0, end_pictures)]
        if k == 8:
            pieces = [(0.1, lambda: (send_out(active, act_out), send_out(slope, slope_out)))] + pieces
        if k == PARTS - 1:
            pieces = pieces + [(1.0, text_pool), (0.5, send_captions)]
        return pieces

    def pool_active(part):
        mark = keep_mark().astype(jnp.bfloat16)
        where = pl.ds(part * PART, PART)
        mean = dot(mark, active[:, where]) * (1.0 / patches)
        high = mean.astype(jnp.bfloat16)
        rest = mean - high.astype(jnp.float32)
        low = rest.astype(jnp.bfloat16)
        apool[0:8, where] = high.astype(jnp.float32)
        apool[8:16, where] = low.astype(jnp.float32)
        apool[16:24, where] = rest - low.astype(jnp.float32)

    def pool_shrink(slot, part):
        for half in range(2):
            where = pl.ds(half * (D // 2), D // 2)
            left = apool[:, pl.ds(part * PART, PART)].astype(jnp.bfloat16)
            out = dot_nt(left, weight_rows(slot, half))
            out = out[0:8] + out[8:16] + out[16:24]
            if part == 0:
                held_ = jnp.concatenate(
                    [
                        jnp.sum(middle[pl.ds(i * (PAIR // 2), patches), where], axis=0, keepdims=True)
                        for i in range(GROUP * 2)
                    ],
                    axis=0,
                )
                image_pool_out[:, where] = (
                    held_ * (1.0 / patches) + ivec_ref[:, pl.ds(7 * D + half * (D // 2), D // 2)] + out
                )
            else:
                image_pool_out[:, where] += out

    def image_part(k):
        slot = k
        if k == 0:
            return first_norm(image_read, ivec_ref) + project(slot, 0, (ivec_ref, 2))
        if k == 1:
            return project(slot, 1, None)
        if k == 2:
            return project(slot, 2, (ivec_ref, 3)) + attention(None, image_allowed)
        if k == 3:
            return attend(slot, image_read, ivec_ref)
        if k < 8:
            return expand(slot, k - 4, ivec_ref, False) + [(0.2, functools.partial(pool_active, k - 4))]
        pieces = [(0.5, functools.partial(pool_shrink, slot, k - 8))]
        if k == PARTS - 1:
            pieces.append((2.0, send_pictures))
        return pieces

    own_start(0)
    for copy in reversed(firsts):
        copy.start()
    for s in range(1, OWN_AHEAD):
        own_start(s)
    firsts[1].wait()
    images = GROUP * 2
    half_row = PAIR // 2
    for quarter_ in range(GROUP):
        row = lax.broadcasted_iota(jnp.int32, (PAIR, patches * images), 0) + quarter_ * PAIR
        source = lax.broadcasted_iota(jnp.int32, (PAIR, patches * images), 1)
        wanted = lax.rem(row, half_row) * images + row // half_row
        move = jnp.where((wanted == source) & (lax.rem(row, half_row) < patches), 1.0, 0.0).astype(jnp.bfloat16)
        padded[pl.ds(quarter_ * PAIR, PAIR), :] = dot(move, patches_in[...]).astype(jnp.bfloat16)
    pl.semaphore_wait(barrier, 5 - jnp.where(z_at == 0, 1, 0) - jnp.where(z_at == GROUP - 1, 1, 0))
    for s in range(AHEAD):
        begin(s)
    moves = [(step, move) for step in range(count + AT_C) for move in carry_on(step)]
    by_step = {}
    for step, move in moves:
        by_step.setdefault(step, []).append(move)
    timed = []
    for step in sorted(by_step):
        for i, move in enumerate(by_step[step]):
            timed.append((STEP_TIME * (step + i / len(by_step[step])), step, move))
    clock, done = 0.0, 0
    for s in range(count):
        pieces = image_part(s) if s < PARTS else text_part(s - PARTS)
        while done < len(timed) and timed[done][1] <= s + AT_C:
            clock = max(clock, timed[done][0])
            timed[done][2]()
            done += 1
        for cost, piece in pieces:
            piece()
            clock += cost
            while done < len(timed) and timed[done][0] <= clock:
                timed[done][2]()
                done += 1
    while done < len(timed):
        timed[done][2]()
        done += 1
    for copy in outs:
        copy.wait()
    for s in range(PARTS, count):
        store(s).wait()
    token_gone()
    for group in range(2):
        for up in range(2):
            for hop in range(GROUP - 1):
                unit = z_at - hop if up else z_at + hop
                pl.when((unit >= 0) & (unit < GROUP) & z_open[up])(
                    functools.partial(gone, all_size(group, 1, 2), z_send.at[group, up, hop], z_next[up])
                )
        gone(all_size(group, GROUP, 2), y_send.at[group], y_peers[0])
        gone(all_size(group, n_dp - 1, 1), x_send.at[group], x_peer)
        gone(all_size(group, n_dp, 3), c_send.at[group], c_peer)
    for k in range(1, near):
        caption_copy(k).wait()


def gather_and_forward(n_dp, n_rep, text_low, image_low, tokens, segments, pictures, text_vectors, image_vectors):
    own, columns = text_low.shape
    images, patches = pictures.shape[0], pictures.shape[1]
    lane_rows = own // LANES
    count = 2 * PARTS
    hbm, vmem = pl.BlockSpec(memory_space=pltpu.HBM), pl.BlockSpec(memory_space=pltpu.VMEM)
    low, full = jnp.bfloat16, jnp.float32
    shape = jax.ShapeDtypeStruct
    gathered = shape((PARTS, n_dp, LANES, lane_rows, PART), low)
    turned = shape((D // GROUP, WORDS), low)
    pairs = GROUP * HEADS // 2
    dma = pltpu.SemaphoreType.DMA
    outs = pl.pallas_call(
        functools.partial(forward_kernel, n_dp, n_rep, patches),
        out_shape=(
            gathered, shape((n_dp * n_rep, images, D), low), shape((GROUP, n_dp * n_rep // GROUP, 8, D), low),
            shape((PAIR, D), full), shape((8 * GROUP, D), full),
            shape((GROUP, 8, PAIR), full), shape((WORDS, 3 * D), low), shape((pairs, 2 * PAIR, PAIR), full),
            shape((WORDS, D), full), shape((WORDS, FF), full), shape((WORDS, FF), low), turned, turned, turned,
        ),
        in_specs=[hbm] * 4 + [vmem] * 3,
        out_specs=(hbm, vmem, vmem, hbm, vmem, vmem) + (hbm,) * 8,
        scratch_shapes=[
            pltpu.VMEM((PARTS, n_dp, LANES, lane_rows, PART), low),
            pltpu.VMEM((PARTS, n_dp, LANES, lane_rows, PART), low),
            pltpu.VMEM((GROUP, PAIR, D), low),
            pltpu.VMEM((GROUP, PAIR, PAIR), full),
            pltpu.VMEM((GROUP, 16, PAIR), low),
            pltpu.VMEM((WORDS, D), low),
            pltpu.VMEM((WORDS, 3 * D), low),
            pltpu.VMEM((WORDS, D), low),
            pltpu.VMEM((WORDS, D), full),
            pltpu.VMEM((WORDS, D), low),
            pltpu.VMEM((WORDS, FF), low),
            pltpu.VMEM((WORDS, FF), full),
            pltpu.VMEM((pairs, 2 * PAIR, PAIR), full),
            pltpu.VMEM((WORDS, D), full),
            pltpu.VMEM((WORDS, TILE), full),
            pltpu.VMEM((3, D, WORDS), low),
            pltpu.VMEM((24, FF), full),
            pltpu.VMEM((images, D), full),
            pltpu.VMEM((patches * images, D), low),
            pltpu.VMEM((WORDS, D), low),
            pltpu.VMEM((4, 3, lane_rows, PART), full),
            dma((2, 2, GROUP - 1)), dma((count, GROUP)), dma((2,)), dma((count,)),
            dma((2,)), dma((count,)), dma((2,)), dma((count,)),
            dma((2, 2, GROUP - 1)), dma((2, GROUP)), dma((2,)), dma((count,)), dma((PARTS,)), dma((12,)),
            dma((n_dp * n_rep - 1,)), dma((n_dp * n_rep - 1,)), dma((8,)), dma((8,)),
        ],
        compiler_params=pltpu.CompilerParams(collective_id=5, has_side_effects=True, vmem_limit_bytes=60 << 20),
        name="gather_and_forward",
    )(
        text_low.reshape(LANES, lane_rows, columns), image_low.reshape(LANES, lane_rows, columns), tokens,
        jnp.swapaxes(pictures, 0, 1).reshape(patches * images, D), segments,
        text_vectors.reshape(1, -1), image_vectors.reshape(1, -1),
    )
    return (outs[0].reshape(PARTS, D, PART),) + tuple(outs[1:])


def backward_kernel(
    n_dp, n_rep,
    wt_ref, nt_ref, at_ref, mt_ref, qkv_ref, chance_ref, mid_ref, slope_ref, act_ref, feed_ref,
    tpool_ref, pic_all, cap_all, marks_ref, tok_ref, vec_ref, start_ref, flat_ref, moving_ref,
    m_out, input_out, loss_out, left_out, right_out, nvec_out, nvmom_out,
    weight, turned, qkv, chance, middle, slope, active, grad_hidden, grad_mix, low, low_mixed, wide, block, sent, got, sums, dy_ref, e2t, rows_out, vector_out,
    factor, factor_rep, factor_dp, basis, tiles, tiles_rep, quarter, tiles_dp, everything,
    load_sem, send, recv, m_sem, g_send, g_recv,
):
    n_inner = n_dp // GROUP
    d_at, r_at = lax.axis_index("dp"), lax.axis_index("rep")
    z_at, y_at = d_at // n_inner, lax.rem(d_at, n_inner)
    peer = (z_at * n_inner + 1 - y_at, r_at)
    own = D // n_dp
    share = 1.0 / GROUP

    barrier = pltpu.get_barrier_semaphore()
    devices = n_dp * n_rep
    near = n_inner * n_rep

    def near_peer(k):
        other = lax.rem(y_at * n_rep + r_at + k, near)
        return z_at * n_inner + other // n_rep, lax.rem(other, n_rep)

    rep_peers = [(d_at, lax.rem(r_at + k, n_rep)) for k in range(1, n_rep)]
    dp_peers = [(lax.rem(d_at + k, n_dp), r_at) for k in range(1, n_dp)]
    far_peers = [
        (lax.rem(z_at + k, GROUP) * n_inner + y, r_at) for k in range(1, GROUP) for y in range(n_inner)
    ]
    met = near - 1 + len(far_peers)
    for other in [near_peer(k) for k in range(1, near)] + far_peers:
        pl.semaphore_signal(barrier, inc=1, device_id=other, device_id_type=MESH)
    loads = {}

    def fetch(name, src, dst):
        copy = pltpu.make_async_copy(src, dst, load_sem.at[len(loads)])
        copy.start()
        loads[name] = copy

    def need(*names):
        for name in names:
            loads[name].wait()

    fetch("act", act_ref, active)
    fetch("feed", feed_ref, rows_out)
    for part in range(4):
        fetch(("w", 8 + part), wt_ref.at[8 + part], weight.at[8 + part])
    fetch("slope", slope_ref, slope)
    fetch("mt", mt_ref, turned.at[0])
    for part in range(4):
        fetch(("w", 4 + part), wt_ref.at[4 + part], weight.at[4 + part])
    fetch("mid", mid_ref, middle)
    fetch("at", at_ref, turned.at[1])
    fetch(("w", 3), wt_ref.at[3], weight.at[3])
    fetch("qkv", qkv_ref, qkv)
    fetch("chance", chance_ref, chance)
    fetch("nt", nt_ref, turned.at[2])
    for part in range(3):
        fetch(("w", part), wt_ref.at[part], weight.at[part])

    def exchange(s):
        return pltpu.make_async_remote_copy(
            src_ref=sent.at[s], dst_ref=got.at[s], send_sem=send.at[s], recv_sem=recv.at[s],
            device_id=peer, device_id_type=MESH,
        )

    own_rows = pl.ds(pl.multiple_of(y_at * own, own), own)
    other_rows = pl.ds(pl.multiple_of((1 - y_at) * own, own), own)

    def exchange_tile(s, where, slot):
        return pltpu.make_async_remote_copy(
            src_ref=sent.at[s, :, where], dst_ref=got.at[s, :, where], send_sem=send.at[slot], recv_sem=recv.at[slot],
            device_id=peer, device_id_type=MESH,
        )

    def exchange_heads(j):
        where = (pl.ds(0, 3), slice(None), pl.ds(j * PAIR, PAIR))
        return pltpu.make_async_remote_copy(
            src_ref=sent.at[where], dst_ref=got.at[where], send_sem=send.at[PARTS + j], recv_sem=recv.at[PARTS + j],
            device_id=peer, device_id_type=MESH,
        )

    def outer(s, left, right_of):
        def body(c):
            block[:, pl.ds(0, TILE)] = dot(left, right_of(c))
            where = pl.ds(pl.multiple_of(s * PART + c * TILE, TILE), TILE)
            rows_out[:, where] = rows_out[:, where] + block[own_rows, pl.ds(0, TILE)]
            sent[s, :, aligned(c, TILE)] = block[other_rows, pl.ds(0, TILE)].astype(jnp.bfloat16)
            exchange_tile(s, aligned(c, TILE), s).start()

        loop(PART // TILE, body, unroll=3)

    ones = jnp.ones((16, WORDS), jnp.bfloat16)

    def put(slot, values):
        for i in range(values.shape[1] // PAIR):
            vector_out[pl.ds(slot // PAIR + i, 1), :] = values[:, i * PAIR : (i + 1) * PAIR]

    def column_sums(values, slot, scale):
        put(slot, dot(ones, values)[0:1, :] * scale)


    def contrast():
        group_pairs = GROUP * 8
        pairs_ = devices * 8
        pics = pic_all[...].reshape(pairs_, D)
        caps = cap_all[...].reshape(pairs_, D)
        logits = dot_nt(caps, pics) * LOGIT_SCALE
        top = jnp.max(logits, axis=0, keepdims=True)
        image_log = top + jnp.log(jnp.sum(jnp.exp(logits - top), axis=0, keepdims=True))
        top = jnp.max(logits, axis=1, keepdims=True)
        caption_log = top + jnp.log(jnp.sum(jnp.exp(logits - top), axis=1, keepdims=True))
        row = lax.broadcasted_iota(jnp.int32, (pairs_, pairs_), 0)
        column = lax.broadcasted_iota(jnp.int32, (pairs_, pairs_), 1)
        matched = jnp.sum(jnp.where(row == column, logits, 0.0), axis=1, keepdims=True)
        loss = (jnp.sum(image_log) + jnp.sum(caption_log) - 2.0 * jnp.sum(matched)) / (2.0 * pairs_)
        loss_out[0, 0] = loss
        pooled = tpool_ref[...]
        squares = lax.rsqrt(jnp.sum(pooled * pooled, axis=-1, keepdims=True) + LAYER_EPS)
        own_low = (pooled * squares).astype(jnp.bfloat16)
        own_logits = dot_nt(own_low, pics) * LOGIT_SCALE
        top = jnp.max(own_logits, axis=1, keepdims=True)
        own_log = top + jnp.log(jnp.sum(jnp.exp(own_logits - top), axis=1, keepdims=True))
        local = lax.broadcasted_iota(jnp.int32, (group_pairs, pairs_), 0)
        column = lax.broadcasted_iota(jnp.int32, (group_pairs, pairs_), 1)
        wanted = (local // 8) * (near * 8) + (y_at * n_rep + r_at) * 8 + lax.rem(local, 8)
        pick = jnp.where(wanted == column, 1.0, 0.0)
        soft = ((jnp.exp(own_logits - own_log) - pick) * 0.5).astype(jnp.bfloat16)
        across = ((jnp.exp(own_logits - image_log) - pick) * 0.5).astype(jnp.bfloat16)
        grad = LOGIT_SCALE * (dot(soft, pics) + dot(across, pics))
        grad = squares * (
            grad - pooled * (squares * squares) * jnp.sum(grad * pooled, axis=-1, keepdims=True)
        )
        for i in range(GROUP):
            marks = marks_ref[i]
            part = grad[i * 8 : (i + 1) * 8, :] / jnp.sum(marks, axis=1, keepdims=True)
            high, rest = split_two(part)
            rest_low = (part - high.astype(jnp.float32) - rest.astype(jnp.float32)).astype(jnp.bfloat16)
            stacked = jnp.concatenate([high, rest, rest_low], axis=0)
            marks_low = marks.astype(jnp.bfloat16)
            marks_low = jnp.concatenate([marks_low, marks_low, marks_low], axis=0)
            rows = pl.ds(i * PAIR, PAIR)
            words = dot_tn(marks_low, stacked)
            dy_ref[rows, :] = words
            low[rows, :] = words.astype(jnp.bfloat16)
            e2t[:, rows] = dot_tn(stacked, marks_low).astype(jnp.bfloat16)

    contrast()
    pl.semaphore_wait(barrier, met)
    need("act", "feed")
    for part in range(4):
        outer(8 + part, e2t[pl.ds(pl.multiple_of(z_at * (D // GROUP), D // GROUP), D // GROUP), :], lambda c: active[:, pl.ds(pl.multiple_of(part * PART + c * TILE, TILE), TILE)])
    need("slope")
    column_sums(low[...], 7 * D, share)
    for part in range(4):
        need(("w", 8 + part))

        def hidden_body(c):
            where = pl.ds(pl.multiple_of(part * PART + c * TILE, TILE), TILE)
            out = dot(low[...], weight[8 + part, :, aligned(c, TILE)])
            grad_hidden[:, where] = (out * slope[:, where]).astype(jnp.bfloat16)

        loop(PART // TILE, hidden_body, unroll=3)
    need("mt")
    for part in range(4):
        outer(
            4 + part, turned[0], lambda c: grad_hidden[:, pl.ds(pl.multiple_of(part * PART + c * TILE, TILE), TILE)]
        )
    for part in range(4):
        need(("w", 4 + part))
    for half in range(2):
        rows = pl.ds(half * (D // 2), D // 2)
        out = dot_nt(grad_hidden[:, pl.ds(0, PART)], weight[4, rows, :])
        for part in range(1, 4):
            out = out + dot_nt(grad_hidden[:, pl.ds(part * PART, PART)], weight[4 + part, rows, :])
        wide[:, rows] = out
    need("mid")

    def norm_back(value, grad, gain):
        center = value - jnp.mean(value, axis=-1, keepdims=True)
        scale = lax.rsqrt(jnp.mean(center * center, axis=-1, keepdims=True) + LAYER_EPS)
        unit = center * scale
        inner = grad * gain
        out = scale * (
            inner - jnp.mean(inner, axis=-1, keepdims=True) - unit * jnp.mean(inner * unit, axis=-1, keepdims=True)
        )
        return out, grad * unit

    def fold(values):
        return jnp.sum(values.reshape(ROWS // 8, 8, D), axis=0)

    sums[...] = jnp.zeros_like(sums)

    def second(i):
        rows = aligned(i, ROWS)
        grad = wide[rows, :]
        out, product = norm_back(middle[rows, :], grad, piece_of(vec_ref, 5))
        sums[0] += fold(product)
        sums[1] += fold(grad)
        out = out + dy_ref[rows, :]
        middle[rows, :] = out
        low[rows, :] = out.astype(jnp.bfloat16)

    loop(WORDS // ROWS, second, unroll=2)
    put(5 * D, jnp.sum(sums[0], axis=0, keepdims=True) * share)
    put(6 * D, jnp.sum(sums[1], axis=0, keepdims=True) * share)
    need("at", ("w", 3))
    outer(3, turned[1], lambda c: low[:, aligned(c, TILE)])
    for half in range(2):
        rows = pl.ds(half * (D // 2), D // 2)
        low_mixed[:, rows] = dot_nt(low[...], weight[3, rows, :]).astype(jnp.bfloat16)
    need("qkv", "chance")
    pairs = HEADS // 2

    def attention(j, i):
        at = i * pairs + j
        rows = pl.ds(i * PAIR, PAIR)
        q_cols = pl.ds(j * PAIR, PAIR)
        k_cols = pl.ds(D + j * PAIR, PAIR)
        v_cols = pl.ds(2 * D + j * PAIR, PAIR)
        query, key, value = qkv[rows, q_cols], qkv[rows, k_cols], qkv[rows, v_cols]
        grad = two_heads(low_mixed[rows, q_cols])
        weight_ = chance[at]
        grad_mix[rows, v_cols] = dot_tn(weight_.astype(jnp.bfloat16), grad).astype(jnp.bfloat16)
        back = dot_nt(grad, value)
        back = weight_ * (back - jnp.sum(weight_ * back, axis=-1, keepdims=True))
        back = back.astype(jnp.bfloat16)
        side = jnp.concatenate([back[:PAIR], back[PAIR:]], axis=1)
        grad_mix[rows, q_cols] = (dot(side, two_heads(key)) * SCORE_SCALE).astype(jnp.bfloat16)
        grad_mix[rows, k_cols] = (dot_tn(back, two_heads(query)) * SCORE_SCALE).astype(jnp.bfloat16)

    need("nt")
    for j in range(pairs):
        for i in range(GROUP):
            attention(j, i)
        for part in range(3):
            value = dot(turned[2], grad_mix[:, pl.ds(part * D + j * PAIR, PAIR)])
            block[:, pl.ds(part * PAIR, PAIR)] = value
            where = pl.ds(part * D + j * PAIR, PAIR)
            rows_out[:, where] = rows_out[:, where] + block[own_rows, pl.ds(part * PAIR, PAIR)]
            sent[part, :, pl.ds(j * PAIR, PAIR)] = block[other_rows, pl.ds(part * PAIR, PAIR)].astype(jnp.bfloat16)
            exchange_tile(part, pl.ds(j * PAIR, PAIR), PARTS + j).start()
    column_sums(low[...], 4 * D, share)
    column_sums(grad_hidden[...], 8 * D, share)
    column_sums(grad_mix[:, pl.ds(0, D)], 2 * D, share)
    column_sums(grad_mix[:, pl.ds(2 * D, D)], 3 * D, share)
    for part in range(3):
        need(("w", part))
    mine = aligned(z_at, PAIR)
    for half in range(2):
        rows = pl.ds(half * (D // 2), D // 2)
        out = dot_nt(grad_mix[mine, pl.ds(0, PART)], weight[0, rows, :])
        for part in range(1, 3):
            out = out + dot_nt(grad_mix[mine, pl.ds(part * PART, PART)], weight[part, rows, :])
        wide[pl.ds(0, PAIR), rows] = out
    sums[...] = jnp.zeros_like(sums)

    def first(i):
        rows = aligned(i, ROWS)
        grad = wide[rows, :]
        out, product = norm_back(tok_ref[rows, :].astype(jnp.float32), grad, piece_of(vec_ref, 0))
        sums[0] += fold(product)
        sums[1] += fold(grad)
        input_out[rows, :] = out + middle[pl.ds(pl.multiple_of(z_at * PAIR + i * ROWS, ROWS), ROWS), :]

    loop(PAIR // ROWS, first)
    put(0, jnp.sum(sums[0], axis=0, keepdims=True))
    put(D, jnp.sum(sums[1], axis=0, keepdims=True))

    bounds = matrix_bounds()
    rank = start_ref.shape[0]
    strip = n_dp * OWN_TILES
    sums_of = {}

    def take(s):
        where = pl.ds(s * PART, PART)
        rows_out[:, where] = rows_out[:, where] + got[s].astype(jnp.float32)
        high, rest = split_two(rows_out[:, where])
        start_high, start_low = split_two(start_ref[:, where])
        both = jnp.concatenate([start_high, start_low], axis=0)
        matrix = 0 if s < 3 else 1 if s == 3 else 2 if s < 8 else 3
        out, out_rest = dot_nt(both, high), dot_nt(both, rest)
        out = out[:rank] + out[rank:] + out_rest[:rank]
        sums_of[matrix] = out if matrix not in sums_of else sums_of[matrix] + out

    for s in (8, 9, 10, 11, 4, 5, 6, 7, 3):
        exchange(s).wait_recv()
        take(s)
    for j in range(pairs):
        exchange_heads(j).wait_recv()
    for s in range(3):
        take(s)
    m_copy = pltpu.make_async_copy(rows_out, m_out, m_sem)
    m_copy.start()
    factor[...] = jnp.zeros_like(factor)
    for matrix in range(4):
        factor[pl.ds(matrix * rank, rank), pl.ds(0, own)] = sums_of[matrix]

    def remote(phase, k, src, dst, other):
        return pltpu.make_async_remote_copy(
            src_ref=src, dst_ref=dst, send_sem=g_send.at[phase, k], recv_sem=g_recv.at[phase, k],
            device_id=other, device_id_type=MESH,
        )

    mine = pl.ds(r_at * strip + d_at * OWN_TILES, OWN_TILES)
    strip_mine = pl.ds(r_at * strip, strip)
    phases = [
        [remote(0, k, factor, factor_rep.at[k], other) for k, other in enumerate(rep_peers)],
        [remote(1, k, factor_dp.at[d_at], factor_dp.at[d_at], other) for k, other in enumerate(dp_peers)],
        [
            remote(2, k, tiles.at[pl.ds(other[1] * strip, strip)], tiles_rep.at[k], other)
            for k, other in enumerate(rep_peers)
        ],
        [
            remote(3, k, quarter.at[pl.ds(other[0] * OWN_TILES, OWN_TILES)], tiles_dp.at[k], other)
            for k, other in enumerate(dp_peers)
        ],
        [remote(4, k, everything.at[mine], everything.at[mine], other) for k, other in enumerate(dp_peers)],
        [remote(5, k, everything.at[strip_mine], everything.at[strip_mine], other) for k, other in enumerate(rep_peers)],
    ]

    def begin(phase):
        for copy in phases[phase]:
            copy.start()

    def arrived(phase):
        for copy in phases[phase]:
            copy.wait_recv()


    def send_strip(j):
        k = lax.rem(j - r_at + 2 * n_rep - 1, n_rep)
        copy = remote(2, k, tiles.at[pl.ds(j * strip, strip)], tiles_rep.at[k], (d_at, j))
        pl.when(r_at != j)(copy.start)

    columns = bounds[-1][1] // PAIR
    for i in range(EXTRA):
        tiles[columns + i] = vector_out[pl.ds(i * 8, 8), :]
    for i in range(columns + EXTRA, n_rep * strip):
        tiles[i] = jnp.zeros((8, PAIR), jnp.float32)
    begin(0)
    send_strip(n_rep - 1)
    arrived(0)
    summed = factor[...]
    for k in range(n_rep - 1):
        summed = summed + factor_rep[k]
    factor_dp[d_at] = summed
    begin(1)
    arrived(1)
    vectors = jnp.concatenate([factor_dp[i] for i in range(n_dp)], axis=1).reshape(4, rank, n_dp * PAIR)
    place = lax.broadcasted_iota(jnp.int32, (4, rank, 1), 1)
    for k in range(rank):
        vector = vectors[:, k : k + 1, :]
        size = jnp.sqrt(jnp.sum(vector * vector, axis=-1, keepdims=True)) + NORM_FLOOR
        vector = vector / size
        along = jnp.sum(vector * vectors, axis=-1, keepdims=True)
        vectors = jnp.where(
            place == k, jnp.broadcast_to(vector, vectors.shape),
            vectors - jnp.where(place > k, along, 0.0) * vector,
        )
    vectors = vectors.reshape(4 * rank, n_dp * PAIR)
    basis[...] = vectors
    left_out[...] = vectors
    basis_high, basis_low = split_two(basis[:, aligned(d_at, PAIR)][:, :own])
    for matrix, (first_col, after_col) in enumerate(bounds):
        where = slice(matrix * rank, (matrix + 1) * rank)
        both = jnp.concatenate([basis_high[where], basis_low[where]], axis=0)

        def project(c):
            high, low = split_two(rows_out[:, pl.ds(pl.multiple_of(first_col + c * TILE, TILE), TILE)])
            out = dot(both, high)
            out = out[:rank] + out[rank:] + dot(both, low)[:rank]
            at = first_col // PAIR + c * (TILE // PAIR)
            for half in range(TILE // PAIR):
                tiles[at + half] = out[:, half * PAIR : (half + 1) * PAIR]

        loop((after_col - first_col) // TILE, project, unroll=3)
        if matrix > 0:
            send_strip(matrix - 1)
    arrived(2)
    value = tiles[strip_mine]
    for k in range(n_rep - 1):
        value = value + tiles_rep[k]
    quarter[...] = value
    begin(3)
    arrived(3)
    value = quarter[pl.ds(d_at * OWN_TILES, OWN_TILES)]
    for k in range(n_dp - 1):
        value = value + tiles_dp[k]
    everything[mine] = value
    begin(4)
    arrived(4)
    begin(5)
    arrived(5)
    for i in range(columns):
        right_out[:, pl.ds(i * PAIR, PAIR)] = everything[i]
    for i in range(EXTRA):
        at = pl.ds(i * 8, 8)
        moved = MOMENTUM_DECAY * moving_ref[at, :] + everything[columns + i]
        nvmom_out[at, :] = moved
        nvec_out[at, :] = flat_ref[at, :] - STEP_RATE * moved
    m_copy.wait()
    for s in range(3, PARTS):
        exchange(s).wait_send()
    for j in range(pairs):
        exchange_heads(j).wait_send()
    for phase in phases:
        for copy in phase:
            copy.wait_send()


def backward(n_dp, n_rep, kept, pooled, pictures, captions, marks, tokens, text_vectors, feedback_rows, start, moving):
    weights, qkv, chance, middle, slope, active, n_turned, a_turned, m_turned = kept
    own = feedback_rows.shape[0]
    hbm, vmem = pl.BlockSpec(memory_space=pltpu.HBM), pl.BlockSpec(memory_space=pltpu.VMEM)
    low, full = jnp.bfloat16, jnp.float32
    shape = jax.ShapeDtypeStruct
    dma = pltpu.SemaphoreType.DMA
    pairs = GROUP * HEADS // 2
    rank = start.shape[0]
    strip = n_dp * OWN_TILES
    flat = (12 * D // PAIR, PAIR)
    return pl.pallas_call(
        functools.partial(backward_kernel, n_dp, n_rep),
        out_shape=(
            shape(feedback_rows.shape, full), shape((PAIR, D), full), shape((1, 1), full),
            shape((4 * rank, n_dp * PAIR), full), shape(start.shape, full), shape(flat, full), shape(flat, full),
        ),
        in_specs=[hbm] * 10 + [vmem] * 9,
        out_specs=(hbm, vmem, pl.BlockSpec(memory_space=pltpu.SMEM)) + (vmem,) * 4,
        scratch_shapes=[
            pltpu.VMEM((PARTS, D, PART), low),
            pltpu.VMEM((3, D // GROUP, WORDS), low),
            pltpu.VMEM((WORDS, 3 * D), low),
            pltpu.VMEM((pairs, 2 * PAIR, PAIR), full),
            pltpu.VMEM((WORDS, D), full),
            pltpu.VMEM((WORDS, FF), full),
            pltpu.VMEM((WORDS, FF), low),
            pltpu.VMEM((WORDS, FF), low),
            pltpu.VMEM((WORDS, 3 * D), low),
            pltpu.VMEM((WORDS, D), low),
            pltpu.VMEM((WORDS, D), low),
            pltpu.VMEM((WORDS, D), full),
            pltpu.VMEM((D // GROUP, 3 * PAIR), full),
            pltpu.VMEM((PARTS, own, PART), low),
            pltpu.VMEM((PARTS, own, PART), low),
            pltpu.VMEM((2, 8, D), full),
            pltpu.VMEM((WORDS, D), full),
            pltpu.VMEM((D, WORDS), low),
            pltpu.VMEM(feedback_rows.shape, full),
            pltpu.VMEM(flat, full),
            pltpu.VMEM((4 * rank, PAIR), full),
            pltpu.VMEM((n_rep - 1, 4 * rank, PAIR), full),
            pltpu.VMEM((n_dp, 4 * rank, PAIR), full),
            pltpu.VMEM((4 * rank, n_dp * PAIR), full),
            pltpu.VMEM((n_rep * strip, 8, PAIR), full),
            pltpu.VMEM((n_rep - 1, strip, 8, PAIR), full),
            pltpu.VMEM((strip, 8, PAIR), full),
            pltpu.VMEM((n_dp - 1, OWN_TILES, 8, PAIR), full),
            pltpu.VMEM((n_rep * strip, 8, PAIR), full),
            dma((24,)), dma((PARTS + 6,)), dma((PARTS + 6,)), dma,
            dma((6, n_dp - 1)), dma((6, n_dp - 1)),
        ],
        compiler_params=pltpu.CompilerParams(collective_id=6, has_side_effects=True, vmem_limit_bytes=60 << 20),
        name="backward",
    )(
        weights, n_turned, a_turned, m_turned, qkv, chance, middle, slope, active, feedback_rows,
        pooled, pictures, captions, marks, tokens, text_vectors.reshape(1, -1), start, text_vectors.reshape(flat),
        moving.reshape(flat),
    )


EXTRA = 9
OWN_TILES = 3


def split_two(values):
    high = values.astype(jnp.bfloat16)
    return high, (values - high.astype(jnp.float32)).astype(jnp.bfloat16)


CHUNKS = 2


def finish_kernel(
    n_dp, n_rep,
    rows_ref, mom_ref, wts_ref, words_ref, input_ref, left_ref, right_ref, vec_ref, vmom_ref, loss_ref,
    feed_out, mom_out, wts_out, words_out, input_out, left_out, right_out, vec_out, vmom_out, loss_out,
    rows, mom, wts, change, through, load_sem, store_sem, pass_sem,
):
    own = rows.shape[0]
    piece = own // CHUNKS
    rank = right_ref.shape[0]

    def load(i, j):
        src, dst = ((rows_ref, rows), (mom_ref, mom), (wts_ref, wts))[j]
        span = pl.ds(i * piece, piece)
        return pltpu.make_async_copy(src.at[span], dst.at[span], load_sem.at[i, j])

    def store(i, j):
        src, dst = ((rows, feed_out), (mom, mom_out), (wts, wts_out))[j]
        span = pl.ds(i * piece, piece)
        return pltpu.make_async_copy(src.at[span], dst.at[span], store_sem.at[i, j])

    for i in range(CHUNKS):
        for j in range(3):
            load(i, j).start()
    taken = [
        pltpu.make_async_copy(src, through.at[i], pass_sem.at[i]) for i, src in enumerate((words_ref, input_ref))
    ]
    passed = [
        pltpu.make_async_copy(through.at[i], dst, pass_sem.at[2 + i]) for i, dst in enumerate((words_out, input_out))
    ]
    passed.append(pltpu.make_async_copy(right_ref, right_out, pass_sem.at[4]))
    for copy in taken:
        copy.start()
    passed[2].start()
    vec_out[...] = vec_ref[...]
    vmom_out[...] = vmom_ref[...]
    loss_out[0, 0] = loss_ref[0, 0]
    left_out[...] = jnp.concatenate([left_ref[:, i * PAIR : i * PAIR + own] for i in range(n_dp)], axis=1)
    basis_high, basis_low = split_two(left_ref[:, aligned(lax.axis_index("dp"), PAIR)][:, :own])
    for matrix, (first_col, after_col) in enumerate(matrix_bounds()):
        where = slice(matrix * rank, (matrix + 1) * rank)
        left = jnp.concatenate([basis_high[where], basis_high[where], basis_low[where]], axis=0)

        def approximate(c):
            cols = pl.ds(pl.multiple_of(first_col + c * PART, PART), PART)
            high, low = split_two(right_ref[:, cols])
            change[:, cols] = dot_tn(left, jnp.concatenate([high, low, high], axis=0))

        loop((after_col - first_col) // PART, approximate)
    for i in range(CHUNKS):
        for j in range(3):
            load(i, j).wait()

        def update(c):
            span, cols = pl.ds(i * piece, piece), aligned(c, PART)
            delta = change[span, cols]
            rows[span, cols] = rows[span, cols] - delta * (1.0 / n_rep)
            moved = MOMENTUM_DECAY * mom[span, cols] + delta
            mom[span, cols] = moved
            wts[span, cols] = wts[span, cols] - STEP_RATE * moved

        loop(rows.shape[1] // PART, update)
        for j in range(3):
            store(i, j).start()
        if i == 0:
            for k, copy in enumerate(taken):
                copy.wait()
                passed[k].start()
    for copy in passed:
        copy.wait()
    for i in range(CHUNKS):
        for j in range(3):
            store(i, j).wait()


def finish(n_dp, n_rep, rows, momentum, weights, left, right, words, grad_inputs, vectors, vector_momentum, loss):
    own, columns = rows.shape
    hbm, vmem = pl.BlockSpec(memory_space=pltpu.HBM), pl.BlockSpec(memory_space=pltpu.VMEM)
    smem = pl.BlockSpec(memory_space=pltpu.SMEM)
    full = jnp.float32
    shape = jax.ShapeDtypeStruct
    dma = pltpu.SemaphoreType.DMA
    big = shape(rows.shape, full)
    return pl.pallas_call(
        functools.partial(finish_kernel, n_dp, n_rep),
        out_shape=(
            big, big, big, shape(words.shape, full), shape(grad_inputs.shape, full),
            shape((left.shape[0], n_dp * own), full), shape(right.shape, full), shape(vectors.shape, full),
            shape(vectors.shape, full), shape((1, 1), full),
        ),
        in_specs=[hbm] * 5 + [vmem] * 4 + [smem],
        out_specs=(hbm,) * 5 + (vmem, hbm, vmem, vmem, smem),
        scratch_shapes=[pltpu.VMEM(rows.shape, full)] * 4
        + [pltpu.VMEM((2,) + words.shape, full), dma((CHUNKS, 3)), dma((CHUNKS, 3)), dma((5,))],
        compiler_params=pltpu.CompilerParams(vmem_limit_bytes=60 << 20),
        name="finish",
    )(rows, momentum, weights, words, grad_inputs, left, right, vectors, vector_momentum, loss)


def peer_at(offset, n_dp, n_rep):
    me = lax.axis_index("dp") * n_rep + lax.axis_index("rep")
    other = lax.rem(me + offset, n_dp * n_rep)
    return other, (other // n_rep, lax.rem(other, n_rep))


def meet(n_dp, n_rep):
    total = n_dp * n_rep
    barrier = pltpu.get_barrier_semaphore()

    def hello(offset, carry):
        _, peer = peer_at(offset, n_dp, n_rep)
        pl.semaphore_signal(barrier, inc=1, device_id=peer, device_id_type=MESH)
        return carry

    lax.fori_loop(1, total, hello, 0)
    pl.semaphore_wait(barrier, total - 1)


def spread_kernel(n_dp, n_rep, mine_ref, all_ref, send, recv, own_sem):
    total = n_dp * n_rep
    me = lax.axis_index("dp") * n_rep + lax.axis_index("rep")
    own = pltpu.make_async_copy(mine_ref, all_ref.at[me], own_sem)
    own.start()
    meet(n_dp, n_rep)

    def copy(offset):
        _, peer = peer_at(offset, n_dp, n_rep)
        return pltpu.make_async_remote_copy(
            src_ref=mine_ref, dst_ref=all_ref.at[me], send_sem=send.at[offset - 1],
            recv_sem=recv.at[offset - 1], device_id=peer, device_id_type=MESH,
        )

    def begin(offset, carry):
        copy(offset).start()
        return carry

    def finish(offset, carry):
        copy(offset).wait()
        return carry

    lax.fori_loop(1, total, begin, 0)
    own.wait()
    lax.fori_loop(1, total, finish, 0)


def spread(mine, n_dp, n_rep, collective, name):
    total = n_dp * n_rep
    vmem = pl.BlockSpec(memory_space=pltpu.VMEM)
    dma = pltpu.SemaphoreType.DMA
    return pl.pallas_call(
        functools.partial(spread_kernel, n_dp, n_rep),
        out_shape=jax.ShapeDtypeStruct((total,) + mine.shape, mine.dtype),
        in_specs=[vmem],
        out_specs=vmem,
        scratch_shapes=[dma((total - 1,)), dma((total - 1,)), dma],
        compiler_params=pltpu.CompilerParams(
            collective_id=collective, has_side_effects=True, vmem_limit_bytes=48 << 20
        ),
        name=name,
    )(mine)


def total_kernel(n_dp, n_rep, mine_ref, out_ref, parts, sums, send, recv, send_two, recv_two):
    total = n_dp * n_rep
    me = lax.axis_index("dp") * n_rep + lax.axis_index("rep")
    meet(n_dp, n_rep)

    def scatter(offset):
        other, peer = peer_at(offset, n_dp, n_rep)
        return pltpu.make_async_remote_copy(
            src_ref=mine_ref.at[other], dst_ref=parts.at[offset - 1], send_sem=send.at[offset - 1],
            recv_sem=recv.at[offset - 1], device_id=peer, device_id_type=MESH,
        )

    def share(offset):
        _, peer = peer_at(offset, n_dp, n_rep)
        return pltpu.make_async_remote_copy(
            src_ref=sums, dst_ref=out_ref.at[me], send_sem=send_two.at[offset - 1],
            recv_sem=recv_two.at[offset - 1], device_id=peer, device_id_type=MESH,
        )

    def start_scatter(offset, carry):
        scatter(offset).start()
        return carry

    def add(offset, carry):
        scatter(offset).wait_recv()
        return carry + parts[offset - 1]

    def start_share(offset, carry):
        share(offset).start()
        return carry

    def finish(offset, carry):
        scatter(offset).wait_send()
        share(offset).wait()
        return carry

    lax.fori_loop(1, total, start_scatter, 0)
    result = lax.fori_loop(1, total, add, mine_ref[me])
    sums[...] = result
    lax.fori_loop(1, total, start_share, 0)
    out_ref[me] = result
    lax.fori_loop(1, total, finish, 0)


def total_over_all(flat, n_dp, n_rep, collective, name):
    total = n_dp * n_rep
    count = flat.shape[0]
    chunk = -(-count // (total * 1024)) * 1024
    padded = jnp.pad(flat, (0, total * chunk - count)).reshape(total, chunk // 128, 128)
    vmem = pl.BlockSpec(memory_space=pltpu.VMEM)
    dma = pltpu.SemaphoreType.DMA
    summed = pl.pallas_call(
        functools.partial(total_kernel, n_dp, n_rep),
        out_shape=jax.ShapeDtypeStruct(padded.shape, padded.dtype),
        in_specs=[vmem],
        out_specs=vmem,
        scratch_shapes=[
            pltpu.VMEM((total - 1,) + padded.shape[1:], padded.dtype),
            pltpu.VMEM(padded.shape[1:], padded.dtype),
            dma((total - 1,)), dma((total - 1,)), dma((total - 1,)), dma((total - 1,)),
        ],
        compiler_params=pltpu.CompilerParams(
            collective_id=collective, has_side_effects=True, vmem_limit_bytes=48 << 20
        ),
        name=name,
    )(padded)
    return summed.reshape(-1)[:count]


def masked_scores(query_heads, key_heads, allowed):
    scores = (
        jnp.einsum("rshd,rthd->rhst", query_heads, key_heads, preferred_element_type=jnp.float32)
        * SCORE_SCALE
    )
    return jnp.where(allowed[:, None], scores, MASKED)


def block_forward(inputs, allowed, weights, vector_pieces, pooled_only):
    (
        gain_one, shift_one, bias_query, bias_value, bias_out,
        gain_two, shift_two, bias_shrink, bias_expand,
    ) = vector_pieces
    row_count, seq_tokens = (inputs.shape[0], inputs.shape[1])
    normed = layer_norm(inputs, gain_one, shift_one).astype(jnp.bfloat16)
    mixing = jnp.einsum("rsd,dc->rsc", normed, weights[:, : 3 * D], preferred_element_type=jnp.float32)
    mixing = mixing + jnp.concatenate([bias_query, jnp.zeros_like(bias_query), bias_value])
    head_parts = mixing.astype(jnp.bfloat16).reshape(row_count, seq_tokens, 3, HEADS, HEAD_DIM)
    query_heads, key_heads, value_heads = (head_parts[:, :, 0], head_parts[:, :, 1], head_parts[:, :, 2])
    scores = masked_scores(query_heads, key_heads, allowed)
    highest = jnp.max(scores, axis=-1, keepdims=True)
    log_total = highest + jnp.log(jnp.sum(jnp.exp(scores - highest), axis=-1, keepdims=True))
    attention = jnp.exp(scores - log_total).astype(jnp.bfloat16)
    mixed_heads = jnp.einsum("rhst,rthd->rshd", attention, value_heads, preferred_element_type=jnp.float32)
    mixed_heads = mixed_heads.reshape(row_count, seq_tokens, D).astype(jnp.bfloat16)
    attended = (
        jnp.einsum("rsd,de->rse", mixed_heads, weights[:, 3 * D : 4 * D], preferred_element_type=jnp.float32)
        + bias_out
    )
    middle = inputs + attended
    normed_two = layer_norm(middle, gain_two, shift_two).astype(jnp.bfloat16)
    hidden = (
        jnp.einsum("rsd,df->rsf", normed_two, weights[:, 4 * D : 4 * D + FF], preferred_element_type=jnp.float32)
        + bias_expand
    )
    active = jax.nn.gelu(hidden, approximate=False).astype(jnp.bfloat16)
    shrink = weights[:, 4 * D + FF :]
    if pooled_only:
        mean_active = jnp.mean(active.astype(jnp.float32), axis=1)
        high = mean_active.astype(jnp.bfloat16)
        rest = mean_active - high.astype(jnp.float32)
        low = rest.astype(jnp.bfloat16)
        lower = (rest - low.astype(jnp.float32)).astype(jnp.bfloat16)
        stacked = jnp.concatenate([high, low, lower], axis=0)
        shrunk = jnp.einsum("pf,df->pd", stacked, shrink, preferred_element_type=jnp.float32)
        shrunk = jnp.sum(shrunk.reshape(3, row_count, D), axis=0)
        return jnp.mean(middle, axis=1) + shrunk + bias_shrink
    shrunk = jnp.einsum("rsf,df->rsd", active, shrink, preferred_element_type=jnp.float32) + bias_shrink
    kept = (normed, query_heads, key_heads, value_heads, log_total, mixed_heads, middle, normed_two, hidden, active)
    return (middle + shrunk, kept)


def token_sum(values_low):
    return jnp.sum(values_low.astype(jnp.float32).reshape(-1, values_low.shape[-1]), axis=0)


def block_backward(inputs, allowed, weights, vector_pieces, forward_kept, grad_out, own_group, own_count):
    (gain_one, shift_one, _, _, _, gain_two, shift_two, _, _) = vector_pieces
    (normed, query_heads, key_heads, value_heads, log_total, mixed_heads, middle, normed_two, hidden, active) = forward_kept
    row_count, seq_tokens = (inputs.shape[0], inputs.shape[1])
    grad_shrunk = grad_out.astype(jnp.bfloat16)
    grad_active = jnp.einsum("rsd,df->rsf", grad_shrunk, weights[:, 4 * D + FF :], preferred_element_type=jnp.float32)
    _, gelu_back = jax.vjp(lambda before_gelu: jax.nn.gelu(before_gelu, approximate=False), hidden)
    grad_hidden = gelu_back(grad_active)[0].astype(jnp.bfloat16)
    grad_normed_two = jnp.einsum(
        "rsf,df->rsd", grad_hidden, weights[:, 4 * D : 4 * D + FF], preferred_element_type=jnp.float32
    )
    _, norm_two_back = jax.vjp(layer_norm, middle, gain_two, shift_two)
    grad_middle, grad_gain_two, grad_shift_two = norm_two_back(grad_normed_two)
    grad_middle = grad_middle + grad_out
    grad_attended = grad_middle.astype(jnp.bfloat16)
    grad_mixed = jnp.einsum("rse,de->rsd", grad_attended, weights[:, 3 * D : 4 * D], preferred_element_type=jnp.float32)
    grad_mixed = grad_mixed.astype(jnp.bfloat16).reshape(row_count, seq_tokens, HEADS, HEAD_DIM)
    attention = jnp.exp(masked_scores(query_heads, key_heads, allowed) - log_total)
    grad_values = jnp.einsum("rhst,rshd->rthd", attention.astype(jnp.bfloat16), grad_mixed, preferred_element_type=jnp.float32)
    grad_attention = jnp.einsum("rshd,rthd->rhst", grad_mixed, value_heads, preferred_element_type=jnp.float32)
    grad_scores = attention * (grad_attention - jnp.sum(attention * grad_attention, axis=-1, keepdims=True))
    grad_scores = grad_scores.astype(jnp.bfloat16)
    grad_query = jnp.einsum("rhst,rthd->rshd", grad_scores, key_heads, preferred_element_type=jnp.float32) * SCORE_SCALE
    grad_keys = jnp.einsum("rhst,rshd->rthd", grad_scores, query_heads, preferred_element_type=jnp.float32) * SCORE_SCALE
    grad_mixing = (
        jnp.stack([grad_query, grad_keys, grad_values], axis=2).reshape(row_count, seq_tokens, 3 * D).astype(jnp.bfloat16)
    )

    def mine(values):
        return lax.dynamic_slice_in_dim(values, own_group * own_count, own_count, 0)

    grad_normed = jnp.einsum("rsc,dc->rsd", mine(grad_mixing), weights[:, : 3 * D], preferred_element_type=jnp.float32)
    _, norm_one_back = jax.vjp(layer_norm, mine(inputs), gain_one, shift_one)
    grad_inputs, grad_gain_one, grad_shift_one = norm_one_back(grad_normed)
    grad_inputs = grad_inputs + mine(grad_middle)
    share = 1.0 / GROUP
    vector_grad = jnp.concatenate(
        [
            grad_gain_one, grad_shift_one,
            share * token_sum(grad_mixing[..., :D]), share * token_sum(grad_mixing[..., 2 * D :]),
            share * token_sum(grad_attended), share * grad_gain_two, share * grad_shift_two,
            share * token_sum(grad_shrunk), share * token_sum(grad_hidden),
        ]
    )
    tokens = row_count * seq_tokens
    outer_terms = (
        (normed.reshape(tokens, D), grad_mixing.reshape(tokens, 3 * D)),
        (mixed_heads.reshape(tokens, D), grad_attended.reshape(tokens, D)),
        (normed_two.reshape(tokens, D), grad_hidden.reshape(tokens, FF)),
        (grad_shrunk.reshape(tokens, D), active.reshape(tokens, FF)),
    )
    return (grad_inputs, vector_grad, outer_terms)


def orthonormal(stacked):
    waiting = [stacked[:, column_id] for column_id in range(stacked.shape[1])]
    finished = []
    while waiting:
        vector = waiting.pop(0)
        vector = vector / (jnp.sqrt(jnp.sum(vector * vector, axis=-1, keepdims=True)) + NORM_FLOOR)
        finished.append(vector)
        if waiting:
            later = jnp.stack(waiting, axis=1)
            later = later - jnp.sum(vector[:, None] * later, axis=-1, keepdims=True) * vector[:, None]
            waiting = [later[:, i] for i in range(later.shape[1])]
    return jnp.stack(finished, axis=1)


def rows_factor(start_part, row_block):
    return jnp.einsum("kc,dc->kd", start_part, row_block, precision=PRECISE)


def per_device(
    image_tokens, image_weights, image_vectors, text_tokens, segments, text_weights,
    text_vectors, momentum, vector_momentum, error_feedback, start_factors,
):
    n_rep, n_dp = lax.axis_size("rep"), lax.axis_size("dp")
    n_inner = n_dp // GROUP
    total = n_rep * n_dp
    device_pairs, patches = image_tokens.shape[0], image_tokens.shape[1]
    text_rows, seq_tokens = text_tokens.shape[0], text_tokens.shape[1]
    pair_total = device_pairs * total
    own_rows = text_weights.shape[0]
    d_at, r_at = lax.axis_index("dp"), lax.axis_index("rep")
    z_at, y_at = d_at // n_inner, d_at % n_inner
    row_start = d_at * own_rows
    factor_rank = start_factors.shape[0]
    bounds = matrix_bounds()
    tokens = text_tokens.reshape(text_rows * seq_tokens, D)
    feedback_rows = error_feedback[0]
    fused = (
        own_rows % (16 * LANES) == 0 and n_inner == 2 and n_rep == 4 and device_pairs == 8
        and text_rows * seq_tokens == PAIR and 2 * seq_tokens == PAIR and 2 * patches <= PAIR
        and n_dp == 8 and factor_rank == 8
    )
    if fused:
        outs = gather_and_forward(
            n_dp, n_rep, text_weights, image_weights, tokens, segments, image_tokens, text_vectors, image_vectors
        )
        pictures, captions, words, pooled, marks = outs[1:6]
        kept = (outs[0],) + tuple(outs[6:])
        worker_rows, grad_inputs, loss, left_basis, new_right, new_vectors, new_vector_momentum = backward(
            n_dp, n_rep, kept, pooled, pictures, captions, marks, tokens, text_vectors, feedback_rows, start_factors,
            vector_momentum,
        )
        (
            new_feedback, new_momentum, new_weights, words, grad_inputs, left_basis, new_right,
            new_vectors, new_vector_momentum, loss,
        ) = finish(
            n_dp, n_rep, worker_rows, momentum, text_weights, left_basis, new_right, words, grad_inputs,
            new_vectors, new_vector_momentum, loss,
        )
        return (
            loss.reshape(()), words.reshape(text_rows, seq_tokens, D), grad_inputs.reshape(text_rows, seq_tokens, D),
            new_weights, new_momentum, new_feedback[None], new_vectors.reshape(-1), new_vector_momentum.reshape(-1),
            left_basis, new_right,
        )
    text_low, frozen, token_group, segment_group = gather_weights(
        n_dp, text_weights.astype(jnp.bfloat16), image_weights, tokens, segments
    )
    text_low, frozen = text_low.reshape(D, -1), frozen.reshape(D, -1)
    full_mask = jnp.zeros((device_pairs, patches, patches), jnp.int32) == 0
    image_pooled = block_forward(
        image_tokens.astype(jnp.float32), full_mask, frozen, vector_parts(image_vectors), True
    )
    group_rows = GROUP * text_rows
    text_float = token_group.reshape(group_rows, seq_tokens, D).astype(jnp.float32)
    segment_all = segment_group.reshape(group_rows, seq_tokens)
    allowed = segment_all[:, :, None] == segment_all[:, None, :]
    vector_pieces = vector_parts(text_vectors)
    group_output, forward_kept = block_forward(text_float, allowed, text_low, vector_pieces, False)
    text_output = lax.dynamic_slice_in_dim(group_output, z_at * text_rows, text_rows, 0)
    caption_marks = (
        segment_all[:, None, :] == jnp.arange(PER_ROW, dtype=jnp.int32)[None, :, None]
    ).astype(jnp.float32)
    counts = jnp.sum(caption_marks, axis=-1, keepdims=True)
    pooled = (jnp.einsum("rks,rsd->rkd", caption_marks, group_output, precision=PRECISE) / counts).reshape(-1, D)
    image_emb = unit_rows(image_pooled).astype(jnp.bfloat16)
    text_norm, embed_back = jax.vjp(unit_rows, pooled)
    text_emb = text_norm.astype(jnp.bfloat16)
    own_emb = lax.dynamic_slice_in_dim(text_emb, z_at * device_pairs, device_pairs, 0)
    embeddings = spread(jnp.concatenate([image_emb, own_emb], axis=0), n_dp, n_rep, 2, "spread_embeddings")
    image_all = embeddings[:, :device_pairs].reshape(pair_total, D)
    text_all = embeddings[:, device_pairs:].reshape(pair_total, D)
    own_pairs = (
        ((jnp.arange(GROUP, dtype=jnp.int32) * n_inner + y_at) * n_rep + r_at)[:, None] * device_pairs
        + jnp.arange(device_pairs, dtype=jnp.int32)[None, :]
    ).reshape(-1)
    logits = LOGIT_SCALE * jnp.einsum("pd,bd->pb", image_all, text_all, preferred_element_type=jnp.float32)
    image_top = jnp.max(logits, axis=1)
    image_log_total = image_top + jnp.log(jnp.sum(jnp.exp(logits - image_top[:, None]), axis=1))
    caption_top = jnp.max(logits, axis=0)
    caption_log_total = caption_top + jnp.log(jnp.sum(jnp.exp(logits - caption_top[None, :]), axis=0))
    pair_ids = jnp.arange(pair_total, dtype=jnp.int32)
    matched = jnp.sum(jnp.where(pair_ids[:, None] == pair_ids[None, :], logits, 0.0), axis=1)
    loss_total = (jnp.sum(image_log_total - matched) + jnp.sum(caption_log_total - matched)) / (2.0 * pair_total)
    diagonal_pick = (pair_ids[None, :] == own_pairs[:, None]).astype(jnp.float32)
    text_logits = LOGIT_SCALE * jnp.einsum("pd,bd->pb", text_emb, image_all, preferred_element_type=jnp.float32)
    text_top = jnp.max(text_logits, axis=1, keepdims=True)
    text_log_total = text_top + jnp.log(jnp.sum(jnp.exp(text_logits - text_top), axis=1, keepdims=True))
    text_soft = ((jnp.exp(text_logits - text_log_total) - diagonal_pick) * 0.5).astype(jnp.bfloat16)
    column_soft = ((jnp.exp(text_logits - image_log_total[None, :]) - diagonal_pick) * 0.5).astype(jnp.bfloat16)
    grad_text = LOGIT_SCALE * (
        jnp.einsum("pb,bd->pd", text_soft, image_all, preferred_element_type=jnp.float32)
        + jnp.einsum("pb,bd->pd", column_soft, image_all, preferred_element_type=jnp.float32)
    )
    grad_pooled = embed_back(grad_text)[0]
    grad_pooled = grad_pooled.reshape(-1, PER_ROW, D) / counts
    grad_out = jnp.einsum("rks,rkd->rsd", caption_marks, grad_pooled, precision=PRECISE)
    grad_inputs, vector_grad, outer_terms = block_backward(
        text_float, allowed, text_low, vector_pieces, forward_kept, grad_out, z_at, text_rows
    )
    group_width = n_inner * own_rows
    worker_blocks = []
    for (left_side, right_side), (first_col, after_col) in zip(outer_terms, bounds):
        left_cut = lax.dynamic_slice_in_dim(left_side, z_at * group_width, group_width, 1)
        block = jnp.einsum("tc,tk->ck", left_cut, right_side, preferred_element_type=jnp.float32)
        mine = lax.dynamic_slice_in_dim(block, y_at * own_rows, own_rows, 0)
        for k in range(1, n_inner):
            target = lax.rem(y_at + k, n_inner)
            outgoing = lax.dynamic_slice_in_dim(block, target * own_rows, own_rows, 0).astype(jnp.bfloat16)
            pairs = [
                (z * n_inner + y, z * n_inner + (y + k) % n_inner) for z in range(GROUP) for y in range(n_inner)
            ]
            mine = mine + lax.ppermute(outgoing, "dp", pairs).astype(jnp.float32)
        worker_blocks.append(mine + feedback_rows[:, first_col:after_col])
    factor_rows = jnp.concatenate(
        [
            rows_factor(start_factors[:, first_col:after_col], rows)
            for rows, (first_col, after_col) in zip(worker_blocks, bounds)
        ],
        axis=0,
    )
    gathered_rows = spread(factor_rows, n_dp, n_rep, 3, "spread_factors")
    factor = jnp.sum(gathered_rows.reshape(n_dp, n_rep, 4 * factor_rank, own_rows), axis=1)
    factor = jnp.swapaxes(factor, 0, 1).reshape(4, factor_rank, D)
    left_basis = orthonormal(factor).reshape(4 * factor_rank, D)
    basis_rows = lax.dynamic_slice_in_dim(left_basis, row_start, own_rows, 1)
    basis_parts = [basis_rows[i * factor_rank : (i + 1) * factor_rank] for i in range(4)]
    right_part = jnp.concatenate(
        [jnp.einsum("kd,dc->kc", part, rows, precision=PRECISE) for part, rows in zip(basis_parts, worker_blocks)],
        axis=1,
    )
    summed = total_over_all(
        jnp.concatenate([right_part.reshape(-1), vector_grad]), n_dp, n_rep, 4, "total_right"
    )
    new_right = summed[: right_part.size].reshape(right_part.shape)
    vector_total = summed[right_part.size :]
    approximation = jnp.concatenate(
        [
            jnp.einsum("kd,kc->dc", part, new_right[:, first_col:after_col], precision=PRECISE)
            for part, (first_col, after_col) in zip(basis_parts, bounds)
        ],
        axis=1,
    )
    worker_rows = jnp.concatenate(worker_blocks, axis=1)
    new_feedback = (worker_rows - approximation / n_rep)[None]
    new_momentum = MOMENTUM_DECAY * momentum + approximation
    new_weights = text_weights - STEP_RATE * new_momentum
    new_vector_momentum = MOMENTUM_DECAY * vector_momentum + vector_total
    new_vectors = text_vectors - STEP_RATE * new_vector_momentum
    return (
        loss_total, text_output, grad_inputs, new_weights, new_momentum, new_feedback,
        new_vectors, new_vector_momentum, left_basis, new_right,
    )


def solution(mesh):
    placed = (
        P(("dp", "rep"), None, None), P("dp", None), P(), P(("dp", "rep"), None, None), P(("dp", "rep"), None),
        P("dp", None), P(), P("dp", None), P(), P("rep", "dp", None), P(),
    )
    return jax.shard_map(
        per_device,
        mesh=mesh,
        in_specs=placed,
        out_specs=(
            P(), P(("dp", "rep"), None, None), P(("dp", "rep"), None, None), P("dp", None), P("dp", None),
            P("rep", "dp", None), P(), P(), P(), P(),
        ),
        check_vma=False,
    )
```

```python
import functools

import jax
import jax.numpy as jnp
from jax import lax
from jax.experimental import pallas as pl
from jax.experimental.pallas import tpu as pltpu
from jax.sharding import PartitionSpec as P

D = 768
FF = 3072
HEADS = 12
HEAD_DIM = 64
PER_ROW = 4
GROUP = 4
SECTION = 3072
LANE_COLS = 512

PRECISE = lax.Precision.HIGHEST
LAYER_EPS = 1e-06
SCORE_SCALE = 0.125
LOGIT_SCALE = 50.0
MOMENTUM_DECAY = 0.9
STEP_RATE = 0.08
NORM_FLOOR = 1e-08
MASKED = -1e30
MESH = pl.DeviceIdType.MESH


def layer_norm(values, layer_gain, layer_shift):
    center = values - jnp.mean(values, axis=-1, keepdims=True)
    spread = jnp.mean(center * center, axis=-1, keepdims=True)
    return center * lax.rsqrt(spread + LAYER_EPS) * layer_gain + layer_shift


def unit_rows(values):
    return values * lax.rsqrt(jnp.sum(values * values, axis=-1, keepdims=True) + LAYER_EPS)


def vector_parts(vectors):
    pieces = [vectors[position * D : (position + 1) * D] for position in range(8)]
    return pieces + [vectors[8 * D :]]


def matrix_bounds():
    return ((0, 3 * D), (3 * D, 4 * D), (4 * D, 4 * D + FF), (4 * D + FF, 4 * D + 2 * FF))


def gather_kernel(
    n_dp, text_ref, image_ref, tok_ref, seg_ref, wt_ref, wi_ref, tok_out, seg_out,
    z_send, z_recv, y_send, y_recv, x_send, x_recv, c_send, c_recv, t_send, t_recv, t_own, own_sem,
):
    n_inner = n_dp // GROUP
    d_at, r_at = lax.axis_index("dp"), lax.axis_index("rep")
    z_at, y_at = d_at // n_inner, d_at % n_inner
    x_at, c_at = r_at // 2, r_at % 2
    z_peers = [(lax.rem(z_at + k, GROUP) * n_inner + y_at, r_at) for k in range(1, GROUP)]
    z_from = [lax.rem(z_at + GROUP - k, GROUP) for k in range(1, GROUP)]
    y_peers = [(z_at * n_inner + lax.rem(y_at + k, n_inner), r_at) for k in range(1, n_inner)]
    y_from = [lax.rem(y_at + n_inner - k, n_inner) for k in range(1, n_inner)]
    x_peer = (d_at, (1 - x_at) * 2 + c_at)
    c_peer = (d_at, x_at * 2 + 1 - c_at)

    barrier = pltpu.get_barrier_semaphore()
    everyone = z_peers + y_peers + [x_peer, c_peer]
    for peer in everyone:
        pl.semaphore_signal(barrier, inc=1, device_id=peer, device_id_type=MESH)
    pl.semaphore_wait(barrier, len(everyone))

    def shard_of(z, y):
        return z * n_inner + y

    sections = [(image_ref, wi_ref, 0), (text_ref, wt_ref, 0), (image_ref, wi_ref, 1),
                (text_ref, wt_ref, 1), (image_ref, wi_ref, 2), (text_ref, wt_ref, 2)]

    def cols(section, lane):
        start = sections[section][2] * SECTION + lane * LANE_COLS
        return pl.ds(pl.multiple_of(start, 128), LANE_COLS)

    lane_both = c_at
    lane_mine = 2 + x_at * 2 + c_at
    lane_theirs = 2 + (1 - x_at) * 2 + c_at
    lanes = (lane_both, lane_mine)

    locals_ = [
        pltpu.make_async_copy(tok_ref, tok_out.at[z_at], t_own.at[0]),
        pltpu.make_async_copy(seg_ref, seg_out.at[z_at], t_own.at[1]),
    ]
    for s, (src, full, _) in enumerate(sections):
        for j in range(2):
            column = cols(s, lanes[j])
            locals_.append(pltpu.make_async_copy(src.at[:, column], full.at[d_at, :, column], own_sem.at[s, j]))
    for copy in locals_:
        copy.start()

    def remote(src, dst, send, recv, peer):
        return pltpu.make_async_remote_copy(
            src_ref=src, dst_ref=dst, send_sem=send, recv_sem=recv, device_id=peer, device_id_type=MESH
        )

    def z_copy(s, k, j):
        src, full, _ = sections[s]
        return remote(
            src.at[:, cols(s, lanes[j])], full.at[d_at, :, cols(s, lanes[j])],
            z_send.at[s, k, j], z_recv.at[s, k, j], z_peers[k],
        )

    def y_copy(s, q, zi, j):
        src, full, _ = sections[s]
        column = cols(s, lanes[j])
        if zi == 0:
            shard, source = d_at, src.at[:, column]
        else:
            shard = shard_of(z_from[zi - 1], y_at)
            source = full.at[shard, :, column]
        return remote(source, full.at[shard, :, column], y_send.at[s, q, zi, j], y_recv.at[s, q, zi, j], y_peers[q])

    def x_copy(s):
        full = sections[s][1]
        block = full.at[:, :, cols(s, lane_mine)]
        return remote(block, block, x_send.at[s], x_recv.at[s], x_peer)

    def c_copy(s, j):
        full = sections[s][1]
        block = full.at[:, :, cols(s, (lane_both, lane_mine, lane_theirs)[j])]
        return remote(block, block, c_send.at[s, j], c_recv.at[s, j], c_peer)

    count = len(sections)
    tokens = []
    for k in range(GROUP - 1):
        tokens.append(remote(tok_ref, tok_out.at[z_at], t_send.at[0, k], t_recv.at[0, k], z_peers[k]))
        tokens.append(remote(seg_ref, seg_out.at[z_at], t_send.at[1, k], t_recv.at[1, k], z_peers[k]))

    def begin(s):
        for j in range(2):
            for k in range(GROUP - 1):
                z_copy(s, k, j).start()
            for q in range(n_inner - 1):
                y_copy(s, q, 0, j).start()

    begin(0)
    for copy in tokens:
        copy.start()
    for copy in locals_:
        copy.wait()
    begin(1)
    for step in range(count + 3):
        if step < count:
            for k in range(GROUP - 1):
                for j in range(2):
                    z_copy(step, k, j).wait_recv()
                    for q in range(n_inner - 1):
                        y_copy(step, q, k + 1, j).start()
            if step + 2 < count:
                begin(step + 2)
        s = step - 1
        if 0 <= s < count:
            for q in range(n_inner - 1):
                for zi in range(GROUP):
                    for j in range(2):
                        y_copy(s, q, zi, j).wait_recv()
            x_copy(s).start()
            for j in range(2):
                c_copy(s, j).start()
        s = step - 2
        if 0 <= s < count:
            x_copy(s).wait_recv()
            c_copy(s, 2).start()
        s = step - 3
        if 0 <= s < count:
            for j in range(3):
                c_copy(s, j).wait_recv()
    for copy in tokens:
        copy.wait()
    for s in range(count):
        for j in range(2):
            for k in range(GROUP - 1):
                z_copy(s, k, j).wait_send()
            for q in range(n_inner - 1):
                for zi in range(GROUP):
                    y_copy(s, q, zi, j).wait_send()
        x_copy(s).wait_send()
        for j in range(3):
            c_copy(s, j).wait_send()


def gather_weights(n_dp, text_low, image_low, tokens, segments):
    n_inner = n_dp // GROUP
    full = jax.ShapeDtypeStruct((n_dp,) + text_low.shape, jnp.bfloat16)
    hbm = pl.BlockSpec(memory_space=pltpu.HBM)
    dma = pltpu.SemaphoreType.DMA
    return pl.pallas_call(
        functools.partial(gather_kernel, n_dp),
        out_shape=(
            full,
            full,
            jax.ShapeDtypeStruct((GROUP,) + tokens.shape, jnp.bfloat16),
            jax.ShapeDtypeStruct((GROUP,) + segments.shape, jnp.int32),
        ),
        in_specs=[hbm] * 4,
        out_specs=(hbm,) * 4,
        scratch_shapes=[
            dma((6, GROUP - 1, 2)), dma((6, GROUP - 1, 2)),
            dma((6, n_inner - 1, GROUP, 2)), dma((6, n_inner - 1, GROUP, 2)),
            dma((6,)), dma((6,)), dma((6, 3)), dma((6, 3)),
            dma((2, GROUP - 1)), dma((2, GROUP - 1)), dma((2,)), dma((6, 2)),
        ],
        compiler_params=pltpu.CompilerParams(collective_id=1, has_side_effects=True),
        name="gather_weights",
    )(text_low, image_low, tokens, segments)


TILE = 256
PAIR = 128
ROWS = 32
LANES = 6
PART = 768
PARTS = 12
DEPTH = 8
AHEAD = 2
OWN_AHEAD = 4
TOKENS_AT = 6
STEP_TIME = 4.6
LAG_Z = 1
LAG_Y = 1
LAG_X = 2
LAG_C = 1
AT_Y = 2 * LAG_Z + LAG_Y
AT_X = AT_Y + LAG_X
AT_C = AT_X + LAG_C
WORDS = (GROUP * PAIR)


def piece_of(vec_ref, index, width=D):
    return vec_ref[:, pl.ds(index * D, width)]


def loop(count, body, unroll=1):
    def step(i, carry):
        body(i)
        return carry

    lax.fori_loop(0, count, step, 0, unroll=unroll)


def aligned(i, size):
    return pl.ds(pl.multiple_of(i * size, size), size)


def norm_rows(values):
    center = values - jnp.mean(values, axis=-1, keepdims=True)
    spread_ = jnp.mean(center * center, axis=-1, keepdims=True)
    return center * lax.rsqrt(spread_ + LAYER_EPS)


def dot(left, right):
    return jnp.dot(left, right, preferred_element_type=jnp.float32)


def dot_nt(left, right):
    return lax.dot_general(left, right, (((1,), (1,)), ((), ())), preferred_element_type=jnp.float32)


def dot_tn(left, right):
    return lax.dot_general(left, right, (((0,), (0,)), ((), ())), preferred_element_type=jnp.float32)


def lane_is_first():
    return lax.broadcasted_iota(jnp.int32, (PAIR, PAIR), 1) < HEAD_DIM


def two_heads(block):
    first = lane_is_first()
    zero = jnp.zeros_like(block)
    return jnp.concatenate([jnp.where(first, block, zero), jnp.where(first, zero, block)], axis=0)


def attention_forward(qkv, mixed, chance, allowed_of, first, count):
    pairs = HEADS // 2

    def body(k):
        at = first + k
        i, j = at // pairs, lax.rem(at, pairs)
        rows = aligned(i, PAIR)
        query = qkv[rows, aligned(j, PAIR)]
        key = qkv[rows, pl.ds(pl.multiple_of(D + j * PAIR, PAIR), PAIR)]
        value = qkv[rows, pl.ds(pl.multiple_of(2 * D + j * PAIR, PAIR), PAIR)]
        scores = dot_nt(two_heads(query), key) * SCORE_SCALE
        allowed = allowed_of(i)
        scores = jnp.where(jnp.concatenate([allowed, allowed], axis=0), scores, MASKED)
        scores = jnp.exp(scores - jnp.max(scores, axis=-1, keepdims=True))
        weight = scores / jnp.sum(scores, axis=-1, keepdims=True)
        if chance is not None:
            chance[at] = weight
        low = weight.astype(jnp.bfloat16)
        side = jnp.concatenate([low[:PAIR], low[PAIR:]], axis=1)
        mixed[rows, aligned(j, PAIR)] = dot(side, two_heads(value)).astype(jnp.bfloat16)

    loop(count, body, unroll=2)


def forward_kernel(
    n_dp, n_rep, patches,
    text_ref, image_ref, tok_ref, pic_ref, seg_ref, tvec_ref, ivec_ref,
    wt_out, pic_all, cap_all, words_out, text_pool_out, marks_out, qkv_out, chance_out, mid_out, slope_out,
    act_out, nt_out, at_out, mt_out,
    wi_ref, wt_vmem, tok, seg_col, seg_row, normed, qkv, mixed, middle, normed_two, active, slope, chance, total, hid, turned, apool, image_pool_out, patches_in, padded, master,
    z_send, z_recv, y_send, y_recv, x_send, x_recv, c_send, c_recv, t_send, t_recv, t_own, own_sem, w_sem, out_sem, p_send, p_recv, g_send, g_recv,
):
    n_inner = n_dp // GROUP
    d_at, r_at = lax.axis_index("dp"), lax.axis_index("rep")
    z_at, y_at = d_at // n_inner, lax.rem(d_at, n_inner)
    x_at, c_at = r_at // 2, lax.rem(r_at, 2)
    z_next = [((z_at - 1) * n_inner + y_at, r_at), ((z_at + 1) * n_inner + y_at, r_at)]
    y_peers = [(z_at * n_inner + 1 - y_at, r_at)]
    x_peer = (d_at, (1 - x_at) * 2 + c_at)
    c_peer = (d_at, x_at * 2 + 1 - c_at)

    devices = n_dp * n_rep
    me = d_at * n_rep + r_at
    z_open = (z_at > 0, z_at < GROUP - 1)
    barrier = pltpu.get_barrier_semaphore()

    def hello(peer):
        pl.semaphore_signal(barrier, inc=1, device_id=peer, device_id_type=MESH)

    for peer in (y_peers[0], x_peer, c_peer):
        hello(peer)
    for up in range(2):
        pl.when(z_open[up])(functools.partial(hello, z_next[up]))

    sections = [(image_ref, wi_ref, k) for k in range(PARTS)] + [(text_ref, wt_vmem, k) for k in range(PARTS)]
    count = len(sections)
    lane_mine = c_at * 3 + 2 * x_at
    lane_theirs = c_at * 3 + 2 * (1 - x_at)
    lanes_two = pl.ds(c_at * 3 + x_at, 2)
    lanes_three = pl.ds(c_at * 3, 3)

    def remote(src, dst, send, recv, peer):
        return pltpu.make_async_remote_copy(
            src_ref=src, dst_ref=dst, send_sem=send, recv_sem=recv, device_id=peer, device_id_type=MESH
        )

    def cols(s):
        return pl.ds(sections[s][2] * PART, PART)

    def set_of(s):
        return s // PARTS

    def size_of(s, shards, lanes_):
        return sections[s][1].at[sections[s][2], pl.ds(0, shards), pl.ds(0, lanes_)]

    def all_size(group, shards, lanes_):
        return sections[group * PARTS][1].at[:, pl.ds(0, shards), pl.ds(0, lanes_)]

    def landed(block, recv, peer):
        remote(block, block, x_send.at[0], recv, peer).wait_recv()

    def gone(block, send, peer):
        remote(block, block, send, x_recv.at[0], peer).wait_send()

    def held(s, shard, lane):
        _, full, k = sections[s]
        return full.at[k, shard, lane]

    def z_copy(s, up, hop):
        unit = z_at - hop if up else z_at + hop
        shard = unit * n_inner + y_at
        return remote(
            held(s, shard, lanes_two), held(s, shard, lanes_two),
            z_send.at[set_of(s), up, hop], z_recv.at[s, unit], z_next[up],
        )

    def y_copy(s, unit):
        shard = unit * n_inner + y_at
        return remote(
            held(s, shard, lanes_two), held(s, shard, lanes_two),
            y_send.at[set_of(s)], y_recv.at[s], y_peers[0],
        )

    def x_copy(s, unit):
        block = held(s, pl.ds(unit * n_inner, n_inner), lane_mine)
        return remote(block, block, x_send.at[set_of(s)], x_recv.at[s], x_peer)

    def x_own_copy(s):
        block = held(s, z_at * n_inner + 1 - y_at, lane_mine)
        return remote(block, block, x_send.at[set_of(s)], x_recv.at[s], x_peer)

    def c_copy(s, j):
        block = held(s, slice(None), (lanes_two, lane_theirs)[j])
        return remote(block, block, c_send.at[set_of(s)], c_recv.at[s], c_peer)

    def store(s):
        return pltpu.make_async_copy(wt_vmem.at[s - PARTS], wt_out.at[s - PARTS], w_sem.at[s - PARTS])

    def own_shard(s):
        src, _, _ = sections[s]
        return pltpu.make_async_copy(
            src.at[lanes_three, :, cols(s)], held(s, d_at, lanes_three) if s < PARTS else master.at[s % 4], own_sem.at[s]
        )

    def own_ready(s):
        own_shard(s).wait()
        if s >= PARTS:
            wt_vmem[s - PARTS, d_at, lanes_three] = master[s % 4].astype(jnp.bfloat16)

    gathered = ((tok_ref, tok), (None, seg_row))
    firsts = [
        pltpu.make_async_copy(tok_ref, tok.at[z_at], t_own.at[0]),
        pltpu.make_async_copy(pic_ref, patches_in, t_own.at[1]),
    ]

    def token_copy(i, up, hop):
        unit = z_at - hop if up else z_at + hop
        block = gathered[i][1].at[unit]
        return remote(block, block, t_send.at[i, up, hop], t_recv.at[i, unit], z_next[up])

    def token_begin():
        firsts[0].wait()
        number = seg_ref[...].astype(jnp.float32)
        number = jnp.concatenate([number[0:1, :], number[1:2, :] + PER_ROW], axis=1)
        seg_row[z_at] = jnp.broadcast_to(number, (16, PAIR)).astype(jnp.bfloat16)
        for i in range(2):
            for up in range(2):
                pl.when(z_open[up])(token_copy(i, up, 0).start)

    def token_arrive(hop):
        for up in range(2):
            unit = z_at - hop if up else z_at + hop

            @pl.when((unit >= 0) & (unit < GROUP))
            def _():
                for i in range(2):
                    block = gathered[i][1].at[0]
                    landed(block, t_recv.at[i, unit], z_next[up])
                    if hop < GROUP - 1:
                        pl.when(z_open[up])(token_copy(i, up, hop).start)

    def token_gone():
        for up in range(2):
            for hop in range(GROUP - 1):
                unit = z_at - hop if up else z_at + hop
                for i in range(2):
                    pl.when((unit >= 0) & (unit < GROUP) & z_open[up])(
                        functools.partial(gone, gathered[i][1].at[0], t_send.at[i, up, hop], z_next[up])
                    )

    def picture_copy(offset):
        _, other = peer_at(offset, n_dp, n_rep)
        return remote(pic_all.at[me], pic_all.at[me], p_send.at[offset - 1], p_recv.at[offset - 1], other)

    def send_pictures():
        values = image_pool_out[...]
        squares = jnp.sum(values * values, axis=-1, keepdims=True)
        pic_all[me] = (values * lax.rsqrt(squares + LAYER_EPS)).astype(jnp.bfloat16)

        def start(offset, carry):
            picture_copy(offset).start()
            return carry

        lax.fori_loop(1, devices, start, 0)

    near = n_inner * n_rep

    def caption_copy(k):
        other = lax.rem(y_at * n_rep + r_at + k, near)
        block = cap_all.at[:, y_at * n_rep + r_at]
        peer_ = (z_at * n_inner + other // n_rep, lax.rem(other, n_rep))
        return remote(block, block, g_send.at[k - 1], g_recv.at[k - 1], peer_)

    def send_captions():
        for i in range(GROUP):
            values = text_pool_out[pl.ds(i * 8, 8), :]
            squares = jnp.sum(values * values, axis=-1, keepdims=True)
            cap_all[i, y_at * n_rep + r_at] = (values * lax.rsqrt(squares + LAYER_EPS)).astype(jnp.bfloat16)
        for k in range(1, near):
            caption_copy(k).start()

    def end_pictures():
        def end(offset, carry):
            picture_copy(offset).wait()
            return carry

        lax.fori_loop(1, devices, end, 0)

    def begin(s):
        own_ready(s)
        for up in range(2):
            pl.when(z_open[up])(z_copy(s, up, 0).start)
        y_copy(s, z_at).start()

    def arrive(s, hop):
        for up in range(2):
            unit = z_at - hop if up else z_at + hop

            @pl.when((unit >= 0) & (unit < GROUP))
            def _():
                landed(size_of(s, 1, 2), z_recv.at[s, unit], z_next[up])
                if hop < GROUP - 1:
                    pl.when(z_open[up])(z_copy(s, up, hop).start)
                y_copy(s, unit).start()

    def own_start(s):
        own_shard(s).start()

    def stage_y(s):
        landed(size_of(s, GROUP, 2), y_recv.at[s], y_peers[0])
        for unit in range(GROUP):
            pl.when(unit != z_at)(x_copy(s, unit).start)
        x_own_copy(s).start()
        c_copy(s, 0).start()

    def stage_x(s):
        landed(size_of(s, n_dp - 1, 1), x_recv.at[s], x_peer)
        c_copy(s, 1).start()

    def stage_c(s):
        landed(size_of(s, n_dp, 3), c_recv.at[s], c_peer)
        if s >= PARTS:
            store(s).start()

    def carry_on(step):
        moves = []
        if step + OWN_AHEAD < count:
            moves.append(functools.partial(own_start, step + OWN_AHEAD))
        if step + AHEAD < count:
            moves.append(functools.partial(begin, step + AHEAD))
        for hop in range(1, GROUP):
            s = step - (hop - 1) * LAG_Z
            if 0 <= s < count:
                moves.append(functools.partial(arrive, s, hop))
        for lag, stage in ((AT_Y, stage_y), (AT_X, stage_x), (AT_C, stage_c)):
            if 0 <= step - lag < count:
                moves.append(functools.partial(stage, step - lag))
        if step == TOKENS_AT:
            moves.append(token_begin)
        for hop in range(1, GROUP):
            if step == TOKENS_AT + 2 * hop:
                moves.append(functools.partial(token_arrive, hop))
        return moves


    def weight_tile(s, c):
        _, full, k = sections[s]
        return full[k, :, :, :, aligned(c, TILE)].reshape(D, TILE)

    def weight_rows(s, half):
        _, full, k = sections[s]
        return full[k, pl.ds(half * (n_dp // 2), n_dp // 2)].reshape(D // 2, PART)

    def split_loop(total_, pieces, cost, body):
        size = total_ // pieces
        return [
            (cost, functools.partial(loop, size, functools.partial(lambda base, i: body(base + i), p * size)))
            for p in range(pieces)
        ]

    def first_norm(read, vec):
        def body(i):
            rows = aligned(i, ROWS)
            value = norm_rows(read(i).astype(jnp.float32))
            normed[rows, :] = (value * piece_of(vec, 0) + piece_of(vec, 1)).astype(jnp.bfloat16)

        return split_loop(WORDS // ROWS, 4, 0.5, body)

    def project(slot, part, bias):
        def body(c):
            out = dot(normed[...], weight_tile(slot, c))
            if bias is not None:
                out = out + bias[0][:, pl.ds(pl.multiple_of(bias[1] * D + c * TILE, TILE), TILE)]
            qkv[:, pl.ds(pl.multiple_of(part * D + c * TILE, TILE), TILE)] = out.astype(jnp.bfloat16)

        return split_loop(PART // TILE, 3, 0.6, body)

    def attend(slot, read, vec):
        def body(c):
            where = aligned(c, TILE)
            middle[:, where] = dot(mixed[...], weight_tile(slot, c)) + vec[
                :, pl.ds(pl.multiple_of(4 * D + c * TILE, TILE), TILE)
            ]

        def norm(i):
            rows = aligned(i, ROWS)
            value = middle[rows, :] + read(i).astype(jnp.float32)
            middle[rows, :] = value
            normed_two[rows, :] = (norm_rows(value) * piece_of(vec, 5) + piece_of(vec, 6)).astype(jnp.bfloat16)

        return split_loop(PART // TILE, 3, 0.6, body) + split_loop(WORDS // ROWS, 4, 0.6, norm)

    def expand(slot, part, vec, keep):
        def one(c, p):
            start = part * PART + c * TILE
            if p == 0:
                hid[...] = dot(normed_two[...], weight_tile(slot, c)) + vec[:, pl.ds(8 * D + start, TILE)]

            def inner(i):
                rows = aligned(i + p * (WORDS // ROWS // 2), ROWS)
                value = hid[rows, :]
                phi = 0.5 + 0.5 * lax.erf(value * 0.7071067811865476)
                active[rows, pl.ds(start, TILE)] = (value * phi).astype(jnp.bfloat16)
                if keep:
                    slope[rows, pl.ds(start, TILE)] = phi + value * (
                        0.3989422804014327 * jnp.exp(-0.5 * value * value)
                    )

            loop(WORDS // ROWS // 2, inner, unroll=2)

        return [
            (1.2 - 0.4 * p + 0.2 * keep, functools.partial(one, c, p)) for c in range(PART // TILE) for p in range(2)
        ]

    def shrink(slot, part, vec):
        def one(half):
            where = pl.ds(half * (D // 2), D // 2)
            out = dot_nt(active[:, pl.ds(part * PART, PART)], weight_rows(slot, half))
            if part == 0:
                total[:, where] = out + middle[:, where] + vec[:, pl.ds(7 * D + half * (D // 2), D // 2)]
            else:
                total[:, where] += out

        return [(0.8, functools.partial(one, half)) for half in range(2)]

    def attention(chance_, allowed_of):
        pairs_ = GROUP * HEADS // 2
        return [
            (1.2, functools.partial(attention_forward, qkv, mixed, chance_, allowed_of, first, 4))
            for first in range(0, pairs_, 4)
        ]

    def turn(source, slot, out):
        def body(c):
            turned[slot, aligned(c, PAIR), :] = source[:, aligned(c, PAIR)].T

        loop(D // PAIR, body)
        send_out(turned.at[slot, group_rows], out)

    outs = []

    def send_out(src, dst):
        copy = pltpu.make_async_copy(src, dst, out_sem.at[len(outs)])
        copy.start()
        outs.append(copy)

    group_rows = pl.ds(pl.multiple_of(z_at * (D // GROUP), D // GROUP), D // GROUP)

    def text_read(i):
        per = PAIR // ROWS
        return tok[i // per, aligned(lax.rem(i, per), ROWS), :]

    def text_allowed(i):
        row = seg_row[i].astype(jnp.float32)
        return seg_col[i] == row[0:1, :]

    def text_columns():
        for i in range(GROUP):
            row = seg_row[i].astype(jnp.float32)[0:1, :]
            seg_col[i] = jnp.broadcast_to(row, (PAIR, PAIR)).T

    def image_read(i):
        return padded[aligned(i, ROWS), :]

    def picture(axis):
        at = lax.broadcasted_iota(jnp.int32, (PAIR, PAIR), axis)
        number = at // (PAIR // 2)
        return jnp.where(lax.rem(at, PAIR // 2) < patches, number, number + 2)

    def image_allowed(i):
        return picture(0) == picture(1)

    def keep_mark():
        image = lax.broadcasted_iota(jnp.int32, (GROUP * 2, WORDS), 0)
        at = lax.broadcasted_iota(jnp.int32, (GROUP * 2, WORDS), 1)
        inside = (at // (PAIR // 2) == image) & (lax.rem(at, PAIR // 2) < patches)
        return jnp.where(inside, 1.0, 0.0)

    def text_pool():
        send_out(total.at[aligned(z_at, PAIR)], words_out)
        for i in range(GROUP):
            row = seg_row[i].astype(jnp.float32)[0:8, :]
            marks = jnp.where(row == lax.broadcasted_iota(jnp.int32, (8, PAIR), 0).astype(jnp.float32), 1.0, 0.0)
            marks_out[i] = marks
            marks_low = marks.astype(jnp.bfloat16)
            value = total[pl.ds(i * PAIR, PAIR), :]
            high = value.astype(jnp.bfloat16)
            rest = value - high.astype(jnp.float32)
            low = rest.astype(jnp.bfloat16)
            lower = (rest - low.astype(jnp.float32)).astype(jnp.bfloat16)
            sums = dot(
                jnp.concatenate([marks_low] * 3, axis=1), jnp.concatenate([high, low, lower], axis=0)
            )
            text_pool_out[pl.ds(i * 8, 8), :] = sums / jnp.sum(marks, axis=1, keepdims=True)

    def text_part(k):
        slot = k + PARTS
        if k == 0:
            return (
                [(0.3, text_columns)] + first_norm(text_read, tvec_ref) + project(slot, 0, (tvec_ref, 2))
                + [(0.8, lambda: turn(normed, 0, nt_out))]
            )
        if k == 1:
            return project(slot, 1, None)
        if k == 2:
            return (
                project(slot, 2, (tvec_ref, 3)) + [(0.1, lambda: send_out(qkv, qkv_out))]
                + attention(chance, text_allowed)
                + [(0.1, lambda: send_out(chance, chance_out)), (0.8, lambda: turn(mixed, 1, at_out))]
            )
        if k == 3:
            return attend(slot, text_read, tvec_ref) + [
                (0.1, lambda: send_out(middle, mid_out)), (0.8, lambda: turn(normed_two, 2, mt_out))
            ]
        if k < 8:
            return expand(slot, k - 4, tvec_ref, True)
        pieces = shrink(slot, k - 8, tvec_ref)
        if k == 10:
            pieces = pieces + [(1.0, end_pictures)]
        if k == 8:
            pieces = [(0.1, lambda: (send_out(active, act_out), send_out(slope, slope_out)))] + pieces
        if k == PARTS - 1:
            pieces = pieces + [(1.0, text_pool), (0.5, send_captions)]
        return pieces

    def pool_active(part):
        mark = keep_mark().astype(jnp.bfloat16)
        where = pl.ds(part * PART, PART)
        mean = dot(mark, active[:, where]) * (1.0 / patches)
        high = mean.astype(jnp.bfloat16)
        rest = mean - high.astype(jnp.float32)
        low = rest.astype(jnp.bfloat16)
        apool[0:8, where] = high.astype(jnp.float32)
        apool[8:16, where] = low.astype(jnp.float32)
        apool[16:24, where] = rest - low.astype(jnp.float32)

    def pool_shrink(slot, part):
        for half in range(2):
            where = pl.ds(half * (D // 2), D // 2)
            left = apool[:, pl.ds(part * PART, PART)].astype(jnp.bfloat16)
            out = dot_nt(left, weight_rows(slot, half))
            out = out[0:8] + out[8:16] + out[16:24]
            if part == 0:
                held_ = jnp.concatenate(
                    [
                        jnp.sum(middle[pl.ds(i * (PAIR // 2), patches), where], axis=0, keepdims=True)
                        for i in range(GROUP * 2)
                    ],
                    axis=0,
                )
                image_pool_out[:, where] = (
                    held_ * (1.0 / patches) + ivec_ref[:, pl.ds(7 * D + half * (D // 2), D // 2)] + out
                )
            else:
                image_pool_out[:, where] += out

    def image_part(k):
        slot = k
        if k == 0:
            return first_norm(image_read, ivec_ref) + project(slot, 0, (ivec_ref, 2))
        if k == 1:
            return project(slot, 1, None)
        if k == 2:
            return project(slot, 2, (ivec_ref, 3)) + attention(None, image_allowed)
        if k == 3:
            return attend(slot, image_read, ivec_ref)
        if k < 8:
            return expand(slot, k - 4, ivec_ref, False) + [(0.2, functools.partial(pool_active, k - 4))]
        pieces = [(0.5, functools.partial(pool_shrink, slot, k - 8))]
        if k == PARTS - 1:
            pieces.append((2.0, send_pictures))
        return pieces

    own_start(0)
    for copy in reversed(firsts):
        copy.start()
    for s in range(1, OWN_AHEAD):
        own_start(s)
    firsts[1].wait()
    images = GROUP * 2
    half_row = PAIR // 2
    for quarter_ in range(GROUP):
        row = lax.broadcasted_iota(jnp.int32, (PAIR, patches * images), 0) + quarter_ * PAIR
        source = lax.broadcasted_iota(jnp.int32, (PAIR, patches * images), 1)
        wanted = lax.rem(row, half_row) * images + row // half_row
        move = jnp.where((wanted == source) & (lax.rem(row, half_row) < patches), 1.0, 0.0).astype(jnp.bfloat16)
        padded[pl.ds(quarter_ * PAIR, PAIR), :] = dot(move, patches_in[...]).astype(jnp.bfloat16)
    pl.semaphore_wait(barrier, 5 - jnp.where(z_at == 0, 1, 0) - jnp.where(z_at == GROUP - 1, 1, 0))
    for s in range(AHEAD):
        begin(s)
    moves = [(step, move) for step in range(count + AT_C) for move in carry_on(step)]
    by_step = {}
    for step, move in moves:
        by_step.setdefault(step, []).append(move)
    timed = []
    for step in sorted(by_step):
        for i, move in enumerate(by_step[step]):
            timed.append((STEP_TIME * (step + i / len(by_step[step])), step, move))
    clock, done = 0.0, 0
    for s in range(count):
        pieces = image_part(s) if s < PARTS else text_part(s - PARTS)
        while done < len(timed) and timed[done][1] <= s + AT_C:
            clock = max(clock, timed[done][0])
            timed[done][2]()
            done += 1
        for cost, piece in pieces:
            piece()
            clock += cost
            while done < len(timed) and timed[done][0] <= clock:
                timed[done][2]()
                done += 1
    while done < len(timed):
        timed[done][2]()
        done += 1
    for copy in outs:
        copy.wait()
    for s in range(PARTS, count):
        store(s).wait()
    token_gone()
    for group in range(2):
        for up in range(2):
            for hop in range(GROUP - 1):
                unit = z_at - hop if up else z_at + hop
                pl.when((unit >= 0) & (unit < GROUP) & z_open[up])(
                    functools.partial(gone, all_size(group, 1, 2), z_send.at[group, up, hop], z_next[up])
                )
        gone(all_size(group, GROUP, 2), y_send.at[group], y_peers[0])
        gone(all_size(group, n_dp - 1, 1), x_send.at[group], x_peer)
        gone(all_size(group, n_dp, 3), c_send.at[group], c_peer)
    for k in range(1, near):
        caption_copy(k).wait()


def gather_and_forward(n_dp, n_rep, text_low, image_low, tokens, segments, pictures, text_vectors, image_vectors):
    own, columns = text_low.shape
    images, patches = pictures.shape[0], pictures.shape[1]
    lane_rows = own // LANES
    count = 2 * PARTS
    hbm, vmem = pl.BlockSpec(memory_space=pltpu.HBM), pl.BlockSpec(memory_space=pltpu.VMEM)
    low, full = jnp.bfloat16, jnp.float32
    shape = jax.ShapeDtypeStruct
    gathered = shape((PARTS, n_dp, LANES, lane_rows, PART), low)
    turned = shape((D // GROUP, WORDS), low)
    pairs = GROUP * HEADS // 2
    dma = pltpu.SemaphoreType.DMA
    outs = pl.pallas_call(
        functools.partial(forward_kernel, n_dp, n_rep, patches),
        out_shape=(
            gathered, shape((n_dp * n_rep, images, D), low), shape((GROUP, n_dp * n_rep // GROUP, 8, D), low),
            shape((PAIR, D), full), shape((8 * GROUP, D), full),
            shape((GROUP, 8, PAIR), full), shape((WORDS, 3 * D), low), shape((pairs, 2 * PAIR, PAIR), full),
            shape((WORDS, D), full), shape((WORDS, FF), full), shape((WORDS, FF), low), turned, turned, turned,
        ),
        in_specs=[hbm] * 4 + [vmem] * 3,
        out_specs=(hbm, vmem, vmem, hbm, vmem, vmem) + (hbm,) * 8,
        scratch_shapes=[
            pltpu.VMEM((PARTS, n_dp, LANES, lane_rows, PART), low),
            pltpu.VMEM((PARTS, n_dp, LANES, lane_rows, PART), low),
            pltpu.VMEM((GROUP, PAIR, D), low),
            pltpu.VMEM((GROUP, PAIR, PAIR), full),
            pltpu.VMEM((GROUP, 16, PAIR), low),
            pltpu.VMEM((WORDS, D), low),
            pltpu.VMEM((WORDS, 3 * D), low),
            pltpu.VMEM((WORDS, D), low),
            pltpu.VMEM((WORDS, D), full),
            pltpu.VMEM((WORDS, D), low),
            pltpu.VMEM((WORDS, FF), low),
            pltpu.VMEM((WORDS, FF), full),
            pltpu.VMEM((pairs, 2 * PAIR, PAIR), full),
            pltpu.VMEM((WORDS, D), full),
            pltpu.VMEM((WORDS, TILE), full),
            pltpu.VMEM((3, D, WORDS), low),
            pltpu.VMEM((24, FF), full),
            pltpu.VMEM((images, D), full),
            pltpu.VMEM((patches * images, D), low),
            pltpu.VMEM((WORDS, D), low),
            pltpu.VMEM((4, 3, lane_rows, PART), full),
            dma((2, 2, GROUP - 1)), dma((count, GROUP)), dma((2,)), dma((count,)),
            dma((2,)), dma((count,)), dma((2,)), dma((count,)),
            dma((2, 2, GROUP - 1)), dma((2, GROUP)), dma((2,)), dma((count,)), dma((PARTS,)), dma((12,)),
            dma((n_dp * n_rep - 1,)), dma((n_dp * n_rep - 1,)), dma((8,)), dma((8,)),
        ],
        compiler_params=pltpu.CompilerParams(collective_id=5, has_side_effects=True, vmem_limit_bytes=60 << 20),
        name="gather_and_forward",
    )(
        text_low.reshape(LANES, lane_rows, columns), image_low.reshape(LANES, lane_rows, columns), tokens,
        jnp.swapaxes(pictures, 0, 1).reshape(patches * images, D), segments,
        text_vectors.reshape(1, -1), image_vectors.reshape(1, -1),
    )
    return (outs[0].reshape(PARTS, D, PART),) + tuple(outs[1:])


def backward_kernel(
    n_dp, n_rep,
    wt_ref, nt_ref, at_ref, mt_ref, qkv_ref, chance_ref, mid_ref, slope_ref, act_ref, feed_ref,
    tpool_ref, pic_all, cap_all, marks_ref, tok_ref, vec_ref, start_ref, flat_ref, moving_ref,
    m_out, input_out, loss_out, left_out, right_out, nvec_out, nvmom_out,
    weight, turned, qkv, chance, middle, slope, active, grad_hidden, grad_mix, low, low_mixed, wide, block, sent, got, sums, dy_ref, e2t, rows_out, vector_out,
    factor, factor_rep, factor_dp, basis, tiles, tiles_rep, quarter, tiles_dp, everything,
    load_sem, send, recv, m_sem, g_send, g_recv,
):
    n_inner = n_dp // GROUP
    d_at, r_at = lax.axis_index("dp"), lax.axis_index("rep")
    z_at, y_at = d_at // n_inner, lax.rem(d_at, n_inner)
    peer = (z_at * n_inner + 1 - y_at, r_at)
    own = D // n_dp
    share = 1.0 / GROUP

    barrier = pltpu.get_barrier_semaphore()
    devices = n_dp * n_rep
    near = n_inner * n_rep

    def near_peer(k):
        other = lax.rem(y_at * n_rep + r_at + k, near)
        return z_at * n_inner + other // n_rep, lax.rem(other, n_rep)

    rep_peers = [(d_at, lax.rem(r_at + k, n_rep)) for k in range(1, n_rep)]
    dp_peers = [(lax.rem(d_at + k, n_dp), r_at) for k in range(1, n_dp)]
    far_peers = [
        (lax.rem(z_at + k, GROUP) * n_inner + y, r_at) for k in range(1, GROUP) for y in range(n_inner)
    ]
    met = near - 1 + len(far_peers)
    for other in [near_peer(k) for k in range(1, near)] + far_peers:
        pl.semaphore_signal(barrier, inc=1, device_id=other, device_id_type=MESH)
    loads = {}

    def fetch(name, src, dst):
        copy = pltpu.make_async_copy(src, dst, load_sem.at[len(loads)])
        copy.start()
        loads[name] = copy

    def need(*names):
        for name in names:
            loads[name].wait()

    fetch("act", act_ref, active)
    fetch("feed", feed_ref, rows_out)
    for part in range(4):
        fetch(("w", 8 + part), wt_ref.at[8 + part], weight.at[8 + part])
    fetch("slope", slope_ref, slope)
    fetch("mt", mt_ref, turned.at[0])
    for part in range(4):
        fetch(("w", 4 + part), wt_ref.at[4 + part], weight.at[4 + part])
    fetch("mid", mid_ref, middle)
    fetch("at", at_ref, turned.at[1])
    fetch(("w", 3), wt_ref.at[3], weight.at[3])
    fetch("qkv", qkv_ref, qkv)
    fetch("chance", chance_ref, chance)
    fetch("nt", nt_ref, turned.at[2])
    for part in range(3):
        fetch(("w", part), wt_ref.at[part], weight.at[part])

    def exchange(s):
        return pltpu.make_async_remote_copy(
            src_ref=sent.at[s], dst_ref=got.at[s], send_sem=send.at[s], recv_sem=recv.at[s],
            device_id=peer, device_id_type=MESH,
        )

    own_rows = pl.ds(pl.multiple_of(y_at * own, own), own)
    other_rows = pl.ds(pl.multiple_of((1 - y_at) * own, own), own)

    def exchange_tile(s, where, slot):
        return pltpu.make_async_remote_copy(
            src_ref=sent.at[s, :, where], dst_ref=got.at[s, :, where], send_sem=send.at[slot], recv_sem=recv.at[slot],
            device_id=peer, device_id_type=MESH,
        )

    def exchange_heads(j):
        where = (pl.ds(0, 3), slice(None), pl.ds(j * PAIR, PAIR))
        return pltpu.make_async_remote_copy(
            src_ref=sent.at[where], dst_ref=got.at[where], send_sem=send.at[PARTS + j], recv_sem=recv.at[PARTS + j],
            device_id=peer, device_id_type=MESH,
        )

    def outer(s, left, right_of):
        def body(c):
            block[:, pl.ds(0, TILE)] = dot(left, right_of(c))
            where = pl.ds(pl.multiple_of(s * PART + c * TILE, TILE), TILE)
            rows_out[:, where] = rows_out[:, where] + block[own_rows, pl.ds(0, TILE)]
            sent[s, :, aligned(c, TILE)] = block[other_rows, pl.ds(0, TILE)].astype(jnp.bfloat16)
            exchange_tile(s, aligned(c, TILE), s).start()

        loop(PART // TILE, body, unroll=3)

    ones = jnp.ones((16, WORDS), jnp.bfloat16)

    def put(slot, values):
        for i in range(values.shape[1] // PAIR):
            vector_out[pl.ds(slot // PAIR + i, 1), :] = values[:, i * PAIR : (i + 1) * PAIR]

    def column_sums(values, slot, scale):
        put(slot, dot(ones, values)[0:1, :] * scale)


    def contrast():
        group_pairs = GROUP * 8
        pairs_ = devices * 8
        pics = pic_all[...].reshape(pairs_, D)
        caps = cap_all[...].reshape(pairs_, D)
        logits = dot_nt(caps, pics) * LOGIT_SCALE
        top = jnp.max(logits, axis=0, keepdims=True)
        image_log = top + jnp.log(jnp.sum(jnp.exp(logits - top), axis=0, keepdims=True))
        top = jnp.max(logits, axis=1, keepdims=True)
        caption_log = top + jnp.log(jnp.sum(jnp.exp(logits - top), axis=1, keepdims=True))
        row = lax.broadcasted_iota(jnp.int32, (pairs_, pairs_), 0)
        column = lax.broadcasted_iota(jnp.int32, (pairs_, pairs_), 1)
        matched = jnp.sum(jnp.where(row == column, logits, 0.0), axis=1, keepdims=True)
        loss = (jnp.sum(image_log) + jnp.sum(caption_log) - 2.0 * jnp.sum(matched)) / (2.0 * pairs_)
        loss_out[0, 0] = loss
        pooled = tpool_ref[...]
        squares = lax.rsqrt(jnp.sum(pooled * pooled, axis=-1, keepdims=True) + LAYER_EPS)
        own_low = (pooled * squares).astype(jnp.bfloat16)
        own_logits = dot_nt(own_low, pics) * LOGIT_SCALE
        top = jnp.max(own_logits, axis=1, keepdims=True)
        own_log = top + jnp.log(jnp.sum(jnp.exp(own_logits - top), axis=1, keepdims=True))
        local = lax.broadcasted_iota(jnp.int32, (group_pairs, pairs_), 0)
        column = lax.broadcasted_iota(jnp.int32, (group_pairs, pairs_), 1)
        wanted = (local // 8) * (near * 8) + (y_at * n_rep + r_at) * 8 + lax.rem(local, 8)
        pick = jnp.where(wanted == column, 1.0, 0.0)
        soft = ((jnp.exp(own_logits - own_log) - pick) * 0.5).astype(jnp.bfloat16)
        across = ((jnp.exp(own_logits - image_log) - pick) * 0.5).astype(jnp.bfloat16)
        grad = LOGIT_SCALE * (dot(soft, pics) + dot(across, pics))
        grad = squares * (
            grad - pooled * (squares * squares) * jnp.sum(grad * pooled, axis=-1, keepdims=True)
        )
        for i in range(GROUP):
            marks = marks_ref[i]
            part = grad[i * 8 : (i + 1) * 8, :] / jnp.sum(marks, axis=1, keepdims=True)
            high, rest = split_two(part)
            rest_low = (part - high.astype(jnp.float32) - rest.astype(jnp.float32)).astype(jnp.bfloat16)
            stacked = jnp.concatenate([high, rest, rest_low], axis=0)
            marks_low = marks.astype(jnp.bfloat16)
            marks_low = jnp.concatenate([marks_low, marks_low, marks_low], axis=0)
            rows = pl.ds(i * PAIR, PAIR)
            words = dot_tn(marks_low, stacked)
            dy_ref[rows, :] = words
            low[rows, :] = words.astype(jnp.bfloat16)
            e2t[:, rows] = dot_tn(stacked, marks_low).astype(jnp.bfloat16)

    contrast()
    pl.semaphore_wait(barrier, met)
    need("act", "feed")
    for part in range(4):
        outer(8 + part, e2t[pl.ds(pl.multiple_of(z_at * (D // GROUP), D // GROUP), D // GROUP), :], lambda c: active[:, pl.ds(pl.multiple_of(part * PART + c * TILE, TILE), TILE)])
    need("slope")
    column_sums(low[...], 7 * D, share)
    for part in range(4):
        need(("w", 8 + part))

        def hidden_body(c):
            where = pl.ds(pl.multiple_of(part * PART + c * TILE, TILE), TILE)
            out = dot(low[...], weight[8 + part, :, aligned(c, TILE)])
            grad_hidden[:, where] = (out * slope[:, where]).astype(jnp.bfloat16)

        loop(PART // TILE, hidden_body, unroll=3)
    need("mt")
    for part in range(4):
        outer(
            4 + part, turned[0], lambda c: grad_hidden[:, pl.ds(pl.multiple_of(part * PART + c * TILE, TILE), TILE)]
        )
    for part in range(4):
        need(("w", 4 + part))
    for half in range(2):
        rows = pl.ds(half * (D // 2), D // 2)
        out = dot_nt(grad_hidden[:, pl.ds(0, PART)], weight[4, rows, :])
        for part in range(1, 4):
            out = out + dot_nt(grad_hidden[:, pl.ds(part * PART, PART)], weight[4 + part, rows, :])
        wide[:, rows] = out
    need("mid")

    def norm_back(value, grad, gain):
        center = value - jnp.mean(value, axis=-1, keepdims=True)
        scale = lax.rsqrt(jnp.mean(center * center, axis=-1, keepdims=True) + LAYER_EPS)
        unit = center * scale
        inner = grad * gain
        out = scale * (
            inner - jnp.mean(inner, axis=-1, keepdims=True) - unit * jnp.mean(inner * unit, axis=-1, keepdims=True)
        )
        return out, grad * unit

    def fold(values):
        return jnp.sum(values.reshape(ROWS // 8, 8, D), axis=0)

    sums[...] = jnp.zeros_like(sums)

    def second(i):
        rows = aligned(i, ROWS)
        grad = wide[rows, :]
        out, product = norm_back(middle[rows, :], grad, piece_of(vec_ref, 5))
        sums[0] += fold(product)
        sums[1] += fold(grad)
        out = out + dy_ref[rows, :]
        middle[rows, :] = out
        low[rows, :] = out.astype(jnp.bfloat16)

    loop(WORDS // ROWS, second, unroll=2)
    put(5 * D, jnp.sum(sums[0], axis=0, keepdims=True) * share)
    put(6 * D, jnp.sum(sums[1], axis=0, keepdims=True) * share)
    need("at", ("w", 3))
    outer(3, turned[1], lambda c: low[:, aligned(c, TILE)])
    for half in range(2):
        rows = pl.ds(half * (D // 2), D // 2)
        low_mixed[:, rows] = dot_nt(low[...], weight[3, rows, :]).astype(jnp.bfloat16)
    need("qkv", "chance")
    pairs = HEADS // 2

    def attention(j, i):
        at = i * pairs + j
        rows = pl.ds(i * PAIR, PAIR)
        q_cols = pl.ds(j * PAIR, PAIR)
        k_cols = pl.ds(D + j * PAIR, PAIR)
        v_cols = pl.ds(2 * D + j * PAIR, PAIR)
        query, key, value = qkv[rows, q_cols], qkv[rows, k_cols], qkv[rows, v_cols]
        grad = two_heads(low_mixed[rows, q_cols])
        weight_ = chance[at]
        grad_mix[rows, v_cols] = dot_tn(weight_.astype(jnp.bfloat16), grad).astype(jnp.bfloat16)
        back = dot_nt(grad, value)
        back = weight_ * (back - jnp.sum(weight_ * back, axis=-1, keepdims=True))
        back = back.astype(jnp.bfloat16)
        side = jnp.concatenate([back[:PAIR], back[PAIR:]], axis=1)
        grad_mix[rows, q_cols] = (dot(side, two_heads(key)) * SCORE_SCALE).astype(jnp.bfloat16)
        grad_mix[rows, k_cols] = (dot_tn(back, two_heads(query)) * SCORE_SCALE).astype(jnp.bfloat16)

    need("nt")
    for j in range(pairs):
        for i in range(GROUP):
            attention(j, i)
        sides = [grad_mix[:, pl.ds(part * D + j * PAIR, PAIR)] for part in range(3)]
        block[...] = dot(turned[2], jnp.concatenate(sides, axis=1))
        for part in range(3):
            where = pl.ds(part * D + j * PAIR, PAIR)
            rows_out[:, where] = rows_out[:, where] + block[own_rows, pl.ds(part * PAIR, PAIR)]
            sent[part, :, pl.ds(j * PAIR, PAIR)] = block[other_rows, pl.ds(part * PAIR, PAIR)].astype(jnp.bfloat16)
            exchange_tile(part, pl.ds(j * PAIR, PAIR), PARTS + j).start()
    column_sums(low[...], 4 * D, share)
    column_sums(grad_hidden[...], 8 * D, share)
    column_sums(grad_mix[:, pl.ds(0, D)], 2 * D, share)
    column_sums(grad_mix[:, pl.ds(2 * D, D)], 3 * D, share)
    for part in range(3):
        need(("w", part))
    mine = aligned(z_at, PAIR)
    for half in range(2):
        rows = pl.ds(half * (D // 2), D // 2)
        out = dot_nt(grad_mix[mine, pl.ds(0, PART)], weight[0, rows, :])
        for part in range(1, 3):
            out = out + dot_nt(grad_mix[mine, pl.ds(part * PART, PART)], weight[part, rows, :])
        wide[pl.ds(0, PAIR), rows] = out
    sums[...] = jnp.zeros_like(sums)

    def first(i):
        rows = aligned(i, ROWS)
        grad = wide[rows, :]
        out, product = norm_back(tok_ref[rows, :].astype(jnp.float32), grad, piece_of(vec_ref, 0))
        sums[0] += fold(product)
        sums[1] += fold(grad)
        input_out[rows, :] = out + middle[pl.ds(pl.multiple_of(z_at * PAIR + i * ROWS, ROWS), ROWS), :]

    loop(PAIR // ROWS, first)
    put(0, jnp.sum(sums[0], axis=0, keepdims=True))
    put(D, jnp.sum(sums[1], axis=0, keepdims=True))

    bounds = matrix_bounds()
    rank = start_ref.shape[0]
    strip = n_dp * OWN_TILES
    sums_of = {}

    def take(s):
        where = pl.ds(s * PART, PART)
        rows_out[:, where] = rows_out[:, where] + got[s].astype(jnp.float32)
        high, rest = split_two(rows_out[:, where])
        start_high, start_low = split_two(start_ref[:, where])
        both = jnp.concatenate([start_high, start_low], axis=0)
        matrix = 0 if s < 3 else 1 if s == 3 else 2 if s < 8 else 3
        out, out_rest = dot_nt(both, high), dot_nt(both, rest)
        out = out[:rank] + out[rank:] + out_rest[:rank]
        sums_of[matrix] = out if matrix not in sums_of else sums_of[matrix] + out

    for s in (8, 9, 10, 11, 4, 5, 6, 7, 3):
        exchange(s).wait_recv()
        take(s)
    for j in range(pairs):
        exchange_heads(j).wait_recv()
    for s in range(3):
        take(s)
    m_copy = pltpu.make_async_copy(rows_out, m_out, m_sem)
    m_copy.start()
    factor[...] = jnp.zeros_like(factor)
    for matrix in range(4):
        factor[pl.ds(matrix * rank, rank), pl.ds(0, own)] = sums_of[matrix]

    def remote(phase, k, src, dst, other):
        return pltpu.make_async_remote_copy(
            src_ref=src, dst_ref=dst, send_sem=g_send.at[phase, k], recv_sem=g_recv.at[phase, k],
            device_id=other, device_id_type=MESH,
        )

    mine = pl.ds(r_at * strip + d_at * OWN_TILES, OWN_TILES)
    strip_mine = pl.ds(r_at * strip, strip)
    phases = [
        [remote(0, k, factor, factor_rep.at[k], other) for k, other in enumerate(rep_peers)],
        [remote(1, k, factor_dp.at[d_at], factor_dp.at[d_at], other) for k, other in enumerate(dp_peers)],
        [
            remote(2, k, tiles.at[pl.ds(other[1] * strip, strip)], tiles_rep.at[k], other)
            for k, other in enumerate(rep_peers)
        ],
        [
            remote(3, k, quarter.at[pl.ds(other[0] * OWN_TILES, OWN_TILES)], tiles_dp.at[k], other)
            for k, other in enumerate(dp_peers)
        ],
        [remote(4, k, everything.at[mine], everything.at[mine], other) for k, other in enumerate(dp_peers)],
        [remote(5, k, everything.at[strip_mine], everything.at[strip_mine], other) for k, other in enumerate(rep_peers)],
    ]

    def begin(phase):
        for copy in phases[phase]:
            copy.start()

    def arrived(phase):
        for copy in phases[phase]:
            copy.wait_recv()


    def send_strip(j):
        k = lax.rem(j - r_at + 2 * n_rep - 1, n_rep)
        copy = remote(2, k, tiles.at[pl.ds(j * strip, strip)], tiles_rep.at[k], (d_at, j))
        pl.when(r_at != j)(copy.start)

    columns = bounds[-1][1] // PAIR
    for i in range(EXTRA):
        tiles[columns + i] = vector_out[pl.ds(i * 8, 8), :]
    for i in range(columns + EXTRA, n_rep * strip):
        tiles[i] = jnp.zeros((8, PAIR), jnp.float32)
    begin(0)
    send_strip(n_rep - 1)
    arrived(0)
    summed = factor[...]
    for k in range(n_rep - 1):
        summed = summed + factor_rep[k]
    factor_dp[d_at] = summed
    begin(1)
    arrived(1)
    vectors = jnp.concatenate([factor_dp[i] for i in range(n_dp)], axis=1).reshape(4, rank, n_dp * PAIR)
    place = lax.broadcasted_iota(jnp.int32, (4, rank, 1), 1)
    for k in range(rank):
        vector = vectors[:, k : k + 1, :]
        size = jnp.sqrt(jnp.sum(vector * vector, axis=-1, keepdims=True)) + NORM_FLOOR
        vector = vector / size
        along = jnp.sum(vector * vectors, axis=-1, keepdims=True)
        vectors = jnp.where(
            place == k, jnp.broadcast_to(vector, vectors.shape),
            vectors - jnp.where(place > k, along, 0.0) * vector,
        )
    vectors = vectors.reshape(4 * rank, n_dp * PAIR)
    basis[...] = vectors
    left_out[...] = vectors
    basis_high, basis_low = split_two(basis[:, aligned(d_at, PAIR)][:, :own])
    for matrix, (first_col, after_col) in enumerate(bounds):
        where = slice(matrix * rank, (matrix + 1) * rank)
        both = jnp.concatenate([basis_high[where], basis_low[where]], axis=0)

        def project(c):
            high, low = split_two(rows_out[:, pl.ds(pl.multiple_of(first_col + c * TILE, TILE), TILE)])
            out = dot(both, high)
            out = out[:rank] + out[rank:] + dot(both, low)[:rank]
            at = first_col // PAIR + c * (TILE // PAIR)
            for half in range(TILE // PAIR):
                tiles[at + half] = out[:, half * PAIR : (half + 1) * PAIR]

        loop((after_col - first_col) // TILE, project, unroll=3)
        if matrix > 0:
            send_strip(matrix - 1)
    arrived(2)
    value = tiles[strip_mine]
    for k in range(n_rep - 1):
        value = value + tiles_rep[k]
    quarter[...] = value
    begin(3)
    arrived(3)
    value = quarter[pl.ds(d_at * OWN_TILES, OWN_TILES)]
    for k in range(n_dp - 1):
        value = value + tiles_dp[k]
    everything[mine] = value
    begin(4)
    arrived(4)
    begin(5)
    arrived(5)
    for i in range(columns):
        right_out[:, pl.ds(i * PAIR, PAIR)] = everything[i]
    for i in range(EXTRA):
        at = pl.ds(i * 8, 8)
        moved = MOMENTUM_DECAY * moving_ref[at, :] + everything[columns + i]
        nvmom_out[at, :] = moved
        nvec_out[at, :] = flat_ref[at, :] - STEP_RATE * moved
    m_copy.wait()
    for s in range(3, PARTS):
        exchange(s).wait_send()
    for j in range(pairs):
        exchange_heads(j).wait_send()
    for phase in phases:
        for copy in phase:
            copy.wait_send()


def backward(n_dp, n_rep, kept, pooled, pictures, captions, marks, tokens, text_vectors, feedback_rows, start, moving):
    weights, qkv, chance, middle, slope, active, n_turned, a_turned, m_turned = kept
    own = feedback_rows.shape[0]
    hbm, vmem = pl.BlockSpec(memory_space=pltpu.HBM), pl.BlockSpec(memory_space=pltpu.VMEM)
    low, full = jnp.bfloat16, jnp.float32
    shape = jax.ShapeDtypeStruct
    dma = pltpu.SemaphoreType.DMA
    pairs = GROUP * HEADS // 2
    rank = start.shape[0]
    strip = n_dp * OWN_TILES
    flat = (12 * D // PAIR, PAIR)
    return pl.pallas_call(
        functools.partial(backward_kernel, n_dp, n_rep),
        out_shape=(
            shape(feedback_rows.shape, full), shape((PAIR, D), full), shape((1, 1), full),
            shape((4 * rank, n_dp * PAIR), full), shape(start.shape, full), shape(flat, full), shape(flat, full),
        ),
        in_specs=[hbm] * 10 + [vmem] * 9,
        out_specs=(hbm, vmem, pl.BlockSpec(memory_space=pltpu.SMEM)) + (vmem,) * 4,
        scratch_shapes=[
            pltpu.VMEM((PARTS, D, PART), low),
            pltpu.VMEM((3, D // GROUP, WORDS), low),
            pltpu.VMEM((WORDS, 3 * D), low),
            pltpu.VMEM((pairs, 2 * PAIR, PAIR), full),
            pltpu.VMEM((WORDS, D), full),
            pltpu.VMEM((WORDS, FF), full),
            pltpu.VMEM((WORDS, FF), low),
            pltpu.VMEM((WORDS, FF), low),
            pltpu.VMEM((WORDS, 3 * D), low),
            pltpu.VMEM((WORDS, D), low),
            pltpu.VMEM((WORDS, D), low),
            pltpu.VMEM((WORDS, D), full),
            pltpu.VMEM((D // GROUP, 3 * PAIR), full),
            pltpu.VMEM((PARTS, own, PART), low),
            pltpu.VMEM((PARTS, own, PART), low),
            pltpu.VMEM((2, 8, D), full),
            pltpu.VMEM((WORDS, D), full),
            pltpu.VMEM((D, WORDS), low),
            pltpu.VMEM(feedback_rows.shape, full),
            pltpu.VMEM(flat, full),
            pltpu.VMEM((4 * rank, PAIR), full),
            pltpu.VMEM((n_rep - 1, 4 * rank, PAIR), full),
            pltpu.VMEM((n_dp, 4 * rank, PAIR), full),
            pltpu.VMEM((4 * rank, n_dp * PAIR), full),
            pltpu.VMEM((n_rep * strip, 8, PAIR), full),
            pltpu.VMEM((n_rep - 1, strip, 8, PAIR), full),
            pltpu.VMEM((strip, 8, PAIR), full),
            pltpu.VMEM((n_dp - 1, OWN_TILES, 8, PAIR), full),
            pltpu.VMEM((n_rep * strip, 8, PAIR), full),
            dma((24,)), dma((PARTS + 6,)), dma((PARTS + 6,)), dma,
            dma((6, n_dp - 1)), dma((6, n_dp - 1)),
        ],
        compiler_params=pltpu.CompilerParams(collective_id=6, has_side_effects=True, vmem_limit_bytes=60 << 20),
        name="backward",
    )(
        weights, n_turned, a_turned, m_turned, qkv, chance, middle, slope, active, feedback_rows,
        pooled, pictures, captions, marks, tokens, text_vectors.reshape(1, -1), start, text_vectors.reshape(flat),
        moving.reshape(flat),
    )


EXTRA = 9
OWN_TILES = 3


def split_two(values):
    high = values.astype(jnp.bfloat16)
    return high, (values - high.astype(jnp.float32)).astype(jnp.bfloat16)


CHUNKS = 2


def finish_kernel(
    n_dp, n_rep,
    rows_ref, mom_ref, wts_ref, words_ref, input_ref, left_ref, right_ref, vec_ref, vmom_ref, loss_ref,
    feed_out, mom_out, wts_out, words_out, input_out, left_out, right_out, vec_out, vmom_out, loss_out,
    rows, mom, wts, change, through, load_sem, store_sem, pass_sem,
):
    own = rows.shape[0]
    piece = own // CHUNKS
    rank = right_ref.shape[0]

    def load(i, j):
        src, dst = ((rows_ref, rows), (mom_ref, mom), (wts_ref, wts))[j]
        span = pl.ds(i * piece, piece)
        return pltpu.make_async_copy(src.at[span], dst.at[span], load_sem.at[i, j])

    def store(i, j):
        src, dst = ((rows, feed_out), (mom, mom_out), (wts, wts_out))[j]
        span = pl.ds(i * piece, piece)
        return pltpu.make_async_copy(src.at[span], dst.at[span], store_sem.at[i, j])

    for i in range(CHUNKS):
        for j in range(3):
            load(i, j).start()
    taken = [
        pltpu.make_async_copy(src, through.at[i], pass_sem.at[i]) for i, src in enumerate((words_ref, input_ref))
    ]
    passed = [
        pltpu.make_async_copy(through.at[i], dst, pass_sem.at[2 + i]) for i, dst in enumerate((words_out, input_out))
    ]
    passed.append(pltpu.make_async_copy(right_ref, right_out, pass_sem.at[4]))
    for copy in taken:
        copy.start()
    passed[2].start()
    vec_out[...] = vec_ref[...]
    vmom_out[...] = vmom_ref[...]
    loss_out[0, 0] = loss_ref[0, 0]
    left_out[...] = jnp.concatenate([left_ref[:, i * PAIR : i * PAIR + own] for i in range(n_dp)], axis=1)
    basis_high, basis_low = split_two(left_ref[:, aligned(lax.axis_index("dp"), PAIR)][:, :own])
    for matrix, (first_col, after_col) in enumerate(matrix_bounds()):
        where = slice(matrix * rank, (matrix + 1) * rank)
        left = jnp.concatenate([basis_high[where], basis_high[where], basis_low[where]], axis=0)

        def approximate(c):
            cols = pl.ds(pl.multiple_of(first_col + c * PART, PART), PART)
            high, low = split_two(right_ref[:, cols])
            change[:, cols] = dot_tn(left, jnp.concatenate([high, low, high], axis=0))

        loop((after_col - first_col) // PART, approximate)
    for i in range(CHUNKS):
        for j in range(3):
            load(i, j).wait()

        def update(c):
            span, cols = pl.ds(i * piece, piece), aligned(c, PART)
            delta = change[span, cols]
            rows[span, cols] = rows[span, cols] - delta * (1.0 / n_rep)
            moved = MOMENTUM_DECAY * mom[span, cols] + delta
            mom[span, cols] = moved
            wts[span, cols] = wts[span, cols] - STEP_RATE * moved

        loop(rows.shape[1] // PART, update)
        for j in range(3):
            store(i, j).start()
        if i == 0:
            for k, copy in enumerate(taken):
                copy.wait()
                passed[k].start()
    for copy in passed:
        copy.wait()
    for i in range(CHUNKS):
        for j in range(3):
            store(i, j).wait()


def finish(n_dp, n_rep, rows, momentum, weights, left, right, words, grad_inputs, vectors, vector_momentum, loss):
    own, columns = rows.shape
    hbm, vmem = pl.BlockSpec(memory_space=pltpu.HBM), pl.BlockSpec(memory_space=pltpu.VMEM)
    smem = pl.BlockSpec(memory_space=pltpu.SMEM)
    full = jnp.float32
    shape = jax.ShapeDtypeStruct
    dma = pltpu.SemaphoreType.DMA
    big = shape(rows.shape, full)
    return pl.pallas_call(
        functools.partial(finish_kernel, n_dp, n_rep),
        out_shape=(
            big, big, big, shape(words.shape, full), shape(grad_inputs.shape, full),
            shape((left.shape[0], n_dp * own), full), shape(right.shape, full), shape(vectors.shape, full),
            shape(vectors.shape, full), shape((1, 1), full),
        ),
        in_specs=[hbm] * 5 + [vmem] * 4 + [smem],
        out_specs=(hbm,) * 5 + (vmem, hbm, vmem, vmem, smem),
        scratch_shapes=[pltpu.VMEM(rows.shape, full)] * 4
        + [pltpu.VMEM((2,) + words.shape, full), dma((CHUNKS, 3)), dma((CHUNKS, 3)), dma((5,))],
        compiler_params=pltpu.CompilerParams(vmem_limit_bytes=60 << 20),
        name="finish",
    )(rows, momentum, weights, words, grad_inputs, left, right, vectors, vector_momentum, loss)


def peer_at(offset, n_dp, n_rep):
    me = lax.axis_index("dp") * n_rep + lax.axis_index("rep")
    other = lax.rem(me + offset, n_dp * n_rep)
    return other, (other // n_rep, lax.rem(other, n_rep))


def meet(n_dp, n_rep):
    total = n_dp * n_rep
    barrier = pltpu.get_barrier_semaphore()

    def hello(offset, carry):
        _, peer = peer_at(offset, n_dp, n_rep)
        pl.semaphore_signal(barrier, inc=1, device_id=peer, device_id_type=MESH)
        return carry

    lax.fori_loop(1, total, hello, 0)
    pl.semaphore_wait(barrier, total - 1)


def spread_kernel(n_dp, n_rep, mine_ref, all_ref, send, recv, own_sem):
    total = n_dp * n_rep
    me = lax.axis_index("dp") * n_rep + lax.axis_index("rep")
    own = pltpu.make_async_copy(mine_ref, all_ref.at[me], own_sem)
    own.start()
    meet(n_dp, n_rep)

    def copy(offset):
        _, peer = peer_at(offset, n_dp, n_rep)
        return pltpu.make_async_remote_copy(
            src_ref=mine_ref, dst_ref=all_ref.at[me], send_sem=send.at[offset - 1],
            recv_sem=recv.at[offset - 1], device_id=peer, device_id_type=MESH,
        )

    def begin(offset, carry):
        copy(offset).start()
        return carry

    def finish(offset, carry):
        copy(offset).wait()
        return carry

    lax.fori_loop(1, total, begin, 0)
    own.wait()
    lax.fori_loop(1, total, finish, 0)


def spread(mine, n_dp, n_rep, collective, name):
    total = n_dp * n_rep
    vmem = pl.BlockSpec(memory_space=pltpu.VMEM)
    dma = pltpu.SemaphoreType.DMA
    return pl.pallas_call(
        functools.partial(spread_kernel, n_dp, n_rep),
        out_shape=jax.ShapeDtypeStruct((total,) + mine.shape, mine.dtype),
        in_specs=[vmem],
        out_specs=vmem,
        scratch_shapes=[dma((total - 1,)), dma((total - 1,)), dma],
        compiler_params=pltpu.CompilerParams(
            collective_id=collective, has_side_effects=True, vmem_limit_bytes=48 << 20
        ),
        name=name,
    )(mine)


def total_kernel(n_dp, n_rep, mine_ref, out_ref, parts, sums, send, recv, send_two, recv_two):
    total = n_dp * n_rep
    me = lax.axis_index("dp") * n_rep + lax.axis_index("rep")
    meet(n_dp, n_rep)

    def scatter(offset):
        other, peer = peer_at(offset, n_dp, n_rep)
        return pltpu.make_async_remote_copy(
            src_ref=mine_ref.at[other], dst_ref=parts.at[offset - 1], send_sem=send.at[offset - 1],
            recv_sem=recv.at[offset - 1], device_id=peer, device_id_type=MESH,
        )

    def share(offset):
        _, peer = peer_at(offset, n_dp, n_rep)
        return pltpu.make_async_remote_copy(
            src_ref=sums, dst_ref=out_ref.at[me], send_sem=send_two.at[offset - 1],
            recv_sem=recv_two.at[offset - 1], device_id=peer, device_id_type=MESH,
        )

    def start_scatter(offset, carry):
        scatter(offset).start()
        return carry

    def add(offset, carry):
        scatter(offset).wait_recv()
        return carry + parts[offset - 1]

    def start_share(offset, carry):
        share(offset).start()
        return carry

    def finish(offset, carry):
        scatter(offset).wait_send()
        share(offset).wait()
        return carry

    lax.fori_loop(1, total, start_scatter, 0)
    result = lax.fori_loop(1, total, add, mine_ref[me])
    sums[...] = result
    lax.fori_loop(1, total, start_share, 0)
    out_ref[me] = result
    lax.fori_loop(1, total, finish, 0)


def total_over_all(flat, n_dp, n_rep, collective, name):
    total = n_dp * n_rep
    count = flat.shape[0]
    chunk = -(-count // (total * 1024)) * 1024
    padded = jnp.pad(flat, (0, total * chunk - count)).reshape(total, chunk // 128, 128)
    vmem = pl.BlockSpec(memory_space=pltpu.VMEM)
    dma = pltpu.SemaphoreType.DMA
    summed = pl.pallas_call(
        functools.partial(total_kernel, n_dp, n_rep),
        out_shape=jax.ShapeDtypeStruct(padded.shape, padded.dtype),
        in_specs=[vmem],
        out_specs=vmem,
        scratch_shapes=[
            pltpu.VMEM((total - 1,) + padded.shape[1:], padded.dtype),
            pltpu.VMEM(padded.shape[1:], padded.dtype),
            dma((total - 1,)), dma((total - 1,)), dma((total - 1,)), dma((total - 1,)),
        ],
        compiler_params=pltpu.CompilerParams(
            collective_id=collective, has_side_effects=True, vmem_limit_bytes=48 << 20
        ),
        name=name,
    )(padded)
    return summed.reshape(-1)[:count]


def masked_scores(query_heads, key_heads, allowed):
    scores = (
        jnp.einsum("rshd,rthd->rhst", query_heads, key_heads, preferred_element_type=jnp.float32)
        * SCORE_SCALE
    )
    return jnp.where(allowed[:, None], scores, MASKED)


def block_forward(inputs, allowed, weights, vector_pieces, pooled_only):
    (
        gain_one, shift_one, bias_query, bias_value, bias_out,
        gain_two, shift_two, bias_shrink, bias_expand,
    ) = vector_pieces
    row_count, seq_tokens = (inputs.shape[0], inputs.shape[1])
    normed = layer_norm(inputs, gain_one, shift_one).astype(jnp.bfloat16)
    mixing = jnp.einsum("rsd,dc->rsc", normed, weights[:, : 3 * D], preferred_element_type=jnp.float32)
    mixing = mixing + jnp.concatenate([bias_query, jnp.zeros_like(bias_query), bias_value])
    head_parts = mixing.astype(jnp.bfloat16).reshape(row_count, seq_tokens, 3, HEADS, HEAD_DIM)
    query_heads, key_heads, value_heads = (head_parts[:, :, 0], head_parts[:, :, 1], head_parts[:, :, 2])
    scores = masked_scores(query_heads, key_heads, allowed)
    highest = jnp.max(scores, axis=-1, keepdims=True)
    log_total = highest + jnp.log(jnp.sum(jnp.exp(scores - highest), axis=-1, keepdims=True))
    attention = jnp.exp(scores - log_total).astype(jnp.bfloat16)
    mixed_heads = jnp.einsum("rhst,rthd->rshd", attention, value_heads, preferred_element_type=jnp.float32)
    mixed_heads = mixed_heads.reshape(row_count, seq_tokens, D).astype(jnp.bfloat16)
    attended = (
        jnp.einsum("rsd,de->rse", mixed_heads, weights[:, 3 * D : 4 * D], preferred_element_type=jnp.float32)
        + bias_out
    )
    middle = inputs + attended
    normed_two = layer_norm(middle, gain_two, shift_two).astype(jnp.bfloat16)
    hidden = (
        jnp.einsum("rsd,df->rsf", normed_two, weights[:, 4 * D : 4 * D + FF], preferred_element_type=jnp.float32)
        + bias_expand
    )
    active = jax.nn.gelu(hidden, approximate=False).astype(jnp.bfloat16)
    shrink = weights[:, 4 * D + FF :]
    if pooled_only:
        mean_active = jnp.mean(active.astype(jnp.float32), axis=1)
        high = mean_active.astype(jnp.bfloat16)
        rest = mean_active - high.astype(jnp.float32)
        low = rest.astype(jnp.bfloat16)
        lower = (rest - low.astype(jnp.float32)).astype(jnp.bfloat16)
        stacked = jnp.concatenate([high, low, lower], axis=0)
        shrunk = jnp.einsum("pf,df->pd", stacked, shrink, preferred_element_type=jnp.float32)
        shrunk = jnp.sum(shrunk.reshape(3, row_count, D), axis=0)
        return jnp.mean(middle, axis=1) + shrunk + bias_shrink
    shrunk = jnp.einsum("rsf,df->rsd", active, shrink, preferred_element_type=jnp.float32) + bias_shrink
    kept = (normed, query_heads, key_heads, value_heads, log_total, mixed_heads, middle, normed_two, hidden, active)
    return (middle + shrunk, kept)


def token_sum(values_low):
    return jnp.sum(values_low.astype(jnp.float32).reshape(-1, values_low.shape[-1]), axis=0)


def block_backward(inputs, allowed, weights, vector_pieces, forward_kept, grad_out, own_group, own_count):
    (gain_one, shift_one, _, _, _, gain_two, shift_two, _, _) = vector_pieces
    (normed, query_heads, key_heads, value_heads, log_total, mixed_heads, middle, normed_two, hidden, active) = forward_kept
    row_count, seq_tokens = (inputs.shape[0], inputs.shape[1])
    grad_shrunk = grad_out.astype(jnp.bfloat16)
    grad_active = jnp.einsum("rsd,df->rsf", grad_shrunk, weights[:, 4 * D + FF :], preferred_element_type=jnp.float32)
    _, gelu_back = jax.vjp(lambda before_gelu: jax.nn.gelu(before_gelu, approximate=False), hidden)
    grad_hidden = gelu_back(grad_active)[0].astype(jnp.bfloat16)
    grad_normed_two = jnp.einsum(
        "rsf,df->rsd", grad_hidden, weights[:, 4 * D : 4 * D + FF], preferred_element_type=jnp.float32
    )
    _, norm_two_back = jax.vjp(layer_norm, middle, gain_two, shift_two)
    grad_middle, grad_gain_two, grad_shift_two = norm_two_back(grad_normed_two)
    grad_middle = grad_middle + grad_out
    grad_attended = grad_middle.astype(jnp.bfloat16)
    grad_mixed = jnp.einsum("rse,de->rsd", grad_attended, weights[:, 3 * D : 4 * D], preferred_element_type=jnp.float32)
    grad_mixed = grad_mixed.astype(jnp.bfloat16).reshape(row_count, seq_tokens, HEADS, HEAD_DIM)
    attention = jnp.exp(masked_scores(query_heads, key_heads, allowed) - log_total)
    grad_values = jnp.einsum("rhst,rshd->rthd", attention.astype(jnp.bfloat16), grad_mixed, preferred_element_type=jnp.float32)
    grad_attention = jnp.einsum("rshd,rthd->rhst", grad_mixed, value_heads, preferred_element_type=jnp.float32)
    grad_scores = attention * (grad_attention - jnp.sum(attention * grad_attention, axis=-1, keepdims=True))
    grad_scores = grad_scores.astype(jnp.bfloat16)
    grad_query = jnp.einsum("rhst,rthd->rshd", grad_scores, key_heads, preferred_element_type=jnp.float32) * SCORE_SCALE
    grad_keys = jnp.einsum("rhst,rshd->rthd", grad_scores, query_heads, preferred_element_type=jnp.float32) * SCORE_SCALE
    grad_mixing = (
        jnp.stack([grad_query, grad_keys, grad_values], axis=2).reshape(row_count, seq_tokens, 3 * D).astype(jnp.bfloat16)
    )

    def mine(values):
        return lax.dynamic_slice_in_dim(values, own_group * own_count, own_count, 0)

    grad_normed = jnp.einsum("rsc,dc->rsd", mine(grad_mixing), weights[:, : 3 * D], preferred_element_type=jnp.float32)
    _, norm_one_back = jax.vjp(layer_norm, mine(inputs), gain_one, shift_one)
    grad_inputs, grad_gain_one, grad_shift_one = norm_one_back(grad_normed)
    grad_inputs = grad_inputs + mine(grad_middle)
    share = 1.0 / GROUP
    vector_grad = jnp.concatenate(
        [
            grad_gain_one, grad_shift_one,
            share * token_sum(grad_mixing[..., :D]), share * token_sum(grad_mixing[..., 2 * D :]),
            share * token_sum(grad_attended), share * grad_gain_two, share * grad_shift_two,
            share * token_sum(grad_shrunk), share * token_sum(grad_hidden),
        ]
    )
    tokens = row_count * seq_tokens
    outer_terms = (
        (normed.reshape(tokens, D), grad_mixing.reshape(tokens, 3 * D)),
        (mixed_heads.reshape(tokens, D), grad_attended.reshape(tokens, D)),
        (normed_two.reshape(tokens, D), grad_hidden.reshape(tokens, FF)),
        (grad_shrunk.reshape(tokens, D), active.reshape(tokens, FF)),
    )
    return (grad_inputs, vector_grad, outer_terms)


def orthonormal(stacked):
    waiting = [stacked[:, column_id] for column_id in range(stacked.shape[1])]
    finished = []
    while waiting:
        vector = waiting.pop(0)
        vector = vector / (jnp.sqrt(jnp.sum(vector * vector, axis=-1, keepdims=True)) + NORM_FLOOR)
        finished.append(vector)
        if waiting:
            later = jnp.stack(waiting, axis=1)
            later = later - jnp.sum(vector[:, None] * later, axis=-1, keepdims=True) * vector[:, None]
            waiting = [later[:, i] for i in range(later.shape[1])]
    return jnp.stack(finished, axis=1)


def rows_factor(start_part, row_block):
    return jnp.einsum("kc,dc->kd", start_part, row_block, precision=PRECISE)


def per_device(
    image_tokens, image_weights, image_vectors, text_tokens, segments, text_weights,
    text_vectors, momentum, vector_momentum, error_feedback, start_factors,
):
    n_rep, n_dp = lax.axis_size("rep"), lax.axis_size("dp")
    n_inner = n_dp // GROUP
    total = n_rep * n_dp
    device_pairs, patches = image_tokens.shape[0], image_tokens.shape[1]
    text_rows, seq_tokens = text_tokens.shape[0], text_tokens.shape[1]
    pair_total = device_pairs * total
    own_rows = text_weights.shape[0]
    d_at, r_at = lax.axis_index("dp"), lax.axis_index("rep")
    z_at, y_at = d_at // n_inner, d_at % n_inner
    row_start = d_at * own_rows
    factor_rank = start_factors.shape[0]
    bounds = matrix_bounds()
    tokens = text_tokens.reshape(text_rows * seq_tokens, D)
    feedback_rows = error_feedback[0]
    fused = (
        own_rows % (16 * LANES) == 0 and n_inner == 2 and n_rep == 4 and device_pairs == 8
        and text_rows * seq_tokens == PAIR and 2 * seq_tokens == PAIR and 2 * patches <= PAIR
        and n_dp == 8 and factor_rank == 8
    )
    if fused:
        outs = gather_and_forward(
            n_dp, n_rep, text_weights, image_weights, tokens, segments, image_tokens, text_vectors, image_vectors
        )
        pictures, captions, words, pooled, marks = outs[1:6]
        kept = (outs[0],) + tuple(outs[6:])
        worker_rows, grad_inputs, loss, left_basis, new_right, new_vectors, new_vector_momentum = backward(
            n_dp, n_rep, kept, pooled, pictures, captions, marks, tokens, text_vectors, feedback_rows, start_factors,
            vector_momentum,
        )
        (
            new_feedback, new_momentum, new_weights, words, grad_inputs, left_basis, new_right,
            new_vectors, new_vector_momentum, loss,
        ) = finish(
            n_dp, n_rep, worker_rows, momentum, text_weights, left_basis, new_right, words, grad_inputs,
            new_vectors, new_vector_momentum, loss,
        )
        return (
            loss.reshape(()), words.reshape(text_rows, seq_tokens, D), grad_inputs.reshape(text_rows, seq_tokens, D),
            new_weights, new_momentum, new_feedback[None], new_vectors.reshape(-1), new_vector_momentum.reshape(-1),
            left_basis, new_right,
        )
    text_low, frozen, token_group, segment_group = gather_weights(
        n_dp, text_weights.astype(jnp.bfloat16), image_weights, tokens, segments
    )
    text_low, frozen = text_low.reshape(D, -1), frozen.reshape(D, -1)
    full_mask = jnp.zeros((device_pairs, patches, patches), jnp.int32) == 0
    image_pooled = block_forward(
        image_tokens.astype(jnp.float32), full_mask, frozen, vector_parts(image_vectors), True
    )
    group_rows = GROUP * text_rows
    text_float = token_group.reshape(group_rows, seq_tokens, D).astype(jnp.float32)
    segment_all = segment_group.reshape(group_rows, seq_tokens)
    allowed = segment_all[:, :, None] == segment_all[:, None, :]
    vector_pieces = vector_parts(text_vectors)
    group_output, forward_kept = block_forward(text_float, allowed, text_low, vector_pieces, False)
    text_output = lax.dynamic_slice_in_dim(group_output, z_at * text_rows, text_rows, 0)
    caption_marks = (
        segment_all[:, None, :] == jnp.arange(PER_ROW, dtype=jnp.int32)[None, :, None]
    ).astype(jnp.float32)
    counts = jnp.sum(caption_marks, axis=-1, keepdims=True)
    pooled = (jnp.einsum("rks,rsd->rkd", caption_marks, group_output, precision=PRECISE) / counts).reshape(-1, D)
    image_emb = unit_rows(image_pooled).astype(jnp.bfloat16)
    text_norm, embed_back = jax.vjp(unit_rows, pooled)
    text_emb = text_norm.astype(jnp.bfloat16)
    own_emb = lax.dynamic_slice_in_dim(text_emb, z_at * device_pairs, device_pairs, 0)
    embeddings = spread(jnp.concatenate([image_emb, own_emb], axis=0), n_dp, n_rep, 2, "spread_embeddings")
    image_all = embeddings[:, :device_pairs].reshape(pair_total, D)
    text_all = embeddings[:, device_pairs:].reshape(pair_total, D)
    own_pairs = (
        ((jnp.arange(GROUP, dtype=jnp.int32) * n_inner + y_at) * n_rep + r_at)[:, None] * device_pairs
        + jnp.arange(device_pairs, dtype=jnp.int32)[None, :]
    ).reshape(-1)
    logits = LOGIT_SCALE * jnp.einsum("pd,bd->pb", image_all, text_all, preferred_element_type=jnp.float32)
    image_top = jnp.max(logits, axis=1)
    image_log_total = image_top + jnp.log(jnp.sum(jnp.exp(logits - image_top[:, None]), axis=1))
    caption_top = jnp.max(logits, axis=0)
    caption_log_total = caption_top + jnp.log(jnp.sum(jnp.exp(logits - caption_top[None, :]), axis=0))
    pair_ids = jnp.arange(pair_total, dtype=jnp.int32)
    matched = jnp.sum(jnp.where(pair_ids[:, None] == pair_ids[None, :], logits, 0.0), axis=1)
    loss_total = (jnp.sum(image_log_total - matched) + jnp.sum(caption_log_total - matched)) / (2.0 * pair_total)
    diagonal_pick = (pair_ids[None, :] == own_pairs[:, None]).astype(jnp.float32)
    text_logits = LOGIT_SCALE * jnp.einsum("pd,bd->pb", text_emb, image_all, preferred_element_type=jnp.float32)
    text_top = jnp.max(text_logits, axis=1, keepdims=True)
    text_log_total = text_top + jnp.log(jnp.sum(jnp.exp(text_logits - text_top), axis=1, keepdims=True))
    text_soft = ((jnp.exp(text_logits - text_log_total) - diagonal_pick) * 0.5).astype(jnp.bfloat16)
    column_soft = ((jnp.exp(text_logits - image_log_total[None, :]) - diagonal_pick) * 0.5).astype(jnp.bfloat16)
    grad_text = LOGIT_SCALE * (
        jnp.einsum("pb,bd->pd", text_soft, image_all, preferred_element_type=jnp.float32)
        + jnp.einsum("pb,bd->pd", column_soft, image_all, preferred_element_type=jnp.float32)
    )
    grad_pooled = embed_back(grad_text)[0]
    grad_pooled = grad_pooled.reshape(-1, PER_ROW, D) / counts
    grad_out = jnp.einsum("rks,rkd->rsd", caption_marks, grad_pooled, precision=PRECISE)
    grad_inputs, vector_grad, outer_terms = block_backward(
        text_float, allowed, text_low, vector_pieces, forward_kept, grad_out, z_at, text_rows
    )
    group_width = n_inner * own_rows
    worker_blocks = []
    for (left_side, right_side), (first_col, after_col) in zip(outer_terms, bounds):
        left_cut = lax.dynamic_slice_in_dim(left_side, z_at * group_width, group_width, 1)
        block = jnp.einsum("tc,tk->ck", left_cut, right_side, preferred_element_type=jnp.float32)
        mine = lax.dynamic_slice_in_dim(block, y_at * own_rows, own_rows, 0)
        for k in range(1, n_inner):
            target = lax.rem(y_at + k, n_inner)
            outgoing = lax.dynamic_slice_in_dim(block, target * own_rows, own_rows, 0).astype(jnp.bfloat16)
            pairs = [
                (z * n_inner + y, z * n_inner + (y + k) % n_inner) for z in range(GROUP) for y in range(n_inner)
            ]
            mine = mine + lax.ppermute(outgoing, "dp", pairs).astype(jnp.float32)
        worker_blocks.append(mine + feedback_rows[:, first_col:after_col])
    factor_rows = jnp.concatenate(
        [
            rows_factor(start_factors[:, first_col:after_col], rows)
            for rows, (first_col, after_col) in zip(worker_blocks, bounds)
        ],
        axis=0,
    )
    gathered_rows = spread(factor_rows, n_dp, n_rep, 3, "spread_factors")
    factor = jnp.sum(gathered_rows.reshape(n_dp, n_rep, 4 * factor_rank, own_rows), axis=1)
    factor = jnp.swapaxes(factor, 0, 1).reshape(4, factor_rank, D)
    left_basis = orthonormal(factor).reshape(4 * factor_rank, D)
    basis_rows = lax.dynamic_slice_in_dim(left_basis, row_start, own_rows, 1)
    basis_parts = [basis_rows[i * factor_rank : (i + 1) * factor_rank] for i in range(4)]
    right_part = jnp.concatenate(
        [jnp.einsum("kd,dc->kc", part, rows, precision=PRECISE) for part, rows in zip(basis_parts, worker_blocks)],
        axis=1,
    )
    summed = total_over_all(
        jnp.concatenate([right_part.reshape(-1), vector_grad]), n_dp, n_rep, 4, "total_right"
    )
    new_right = summed[: right_part.size].reshape(right_part.shape)
    vector_total = summed[right_part.size :]
    approximation = jnp.concatenate(
        [
            jnp.einsum("kd,kc->dc", part, new_right[:, first_col:after_col], precision=PRECISE)
            for part, (first_col, after_col) in zip(basis_parts, bounds)
        ],
        axis=1,
    )
    worker_rows = jnp.concatenate(worker_blocks, axis=1)
    new_feedback = (worker_rows - approximation / n_rep)[None]
    new_momentum = MOMENTUM_DECAY * momentum + approximation
    new_weights = text_weights - STEP_RATE * new_momentum
    new_vector_momentum = MOMENTUM_DECAY * vector_momentum + vector_total
    new_vectors = text_vectors - STEP_RATE * new_vector_momentum
    return (
        loss_total, text_output, grad_inputs, new_weights, new_momentum, new_feedback,
        new_vectors, new_vector_momentum, left_basis, new_right,
    )


def solution(mesh):
    placed = (
        P(("dp", "rep"), None, None), P("dp", None), P(), P(("dp", "rep"), None, None), P(("dp", "rep"), None),
        P("dp", None), P(), P("dp", None), P(), P("rep", "dp", None), P(),
    )
    return jax.shard_map(
        per_device,
        mesh=mesh,
        in_specs=placed,
        out_specs=(
            P(), P(("dp", "rep"), None, None), P(("dp", "rep"), None, None), P("dp", None), P("dp", None),
            P("rep", "dp", None), P(), P(), P(), P(),
        ),
        check_vma=False,
    )
```
